32 devices in a mesh: seq: 8 (over z, x), fsdp: 4 (over y, core).
Axes of the slice: x: 2, y: 2, z: 4, core: 2. Of those that a mesh axis runs over, the one named last changes fastest.
Arguments:
- layer_in: bfloat16 [4, 2048, 1024], P('fsdp', 'seq'), may hold values from -6 to 6
- encoder: bfloat16 [4, 512, 1024], P('fsdp', 'seq'), may hold values from -6 to 6
- decoder_ids: int32 [4, 2048], P('fsdp', 'seq'), may hold values from 0 to 3, never falling along the last dimension, each value on 1 to 1024 neighbouring positions
- encoder_ids: int32 [4, 512], P('fsdp', 'seq'), may hold values from 0 to 3, never falling along the last dimension, each value on 1 to 256 neighbouring positions
- rel_buckets: int32 [2048], replicated, may hold values from 0 to 31, as said below
- norm_self: bfloat16 [1024], P('fsdp'), may hold values from 0.5 to 1.5
- self_qkv: bfloat16 [1024, 16, 192], P('fsdp'), may hold values from -0.0625 to 0.0625
- self_out: bfloat16 [1024, 1024], P('fsdp'), may hold values from -1.5 to 1.5
- rel_table: bfloat16 [32, 16], P(None, 'fsdp'), may hold values from -4 to 4
- norm_cross: bfloat16 [1024], P('fsdp'), may hold values from 0.5 to 1.5
- cross_q: bfloat16 [1024, 1024], P('fsdp'), may hold values from -0.0625 to 0.0625
- cross_kv: bfloat16 [1024, 16, 128], P('fsdp'), may hold values from -0.0625 to 0.0625
- cross_out: bfloat16 [1024, 1024], P('fsdp'), may hold values from -1.5 to 1.5
- norm_ff: bfloat16 [1024], P('fsdp'), may hold values from 0.5 to 1.5
- ff_in: bfloat16 [1024, 5632], P('fsdp'), may hold values from -0.1875 to 0.1875
- ff_out: bfloat16 [2816, 1024], P('fsdp'), may hold values from -0.109375 to 0.109375
- cotangent: bfloat16 [4, 2048, 1024], P('fsdp', 'seq'), may hold values from -6 to 6
Outputs:
- layer_out: bfloat16 [4, 2048, 1024], P('fsdp', 'seq')
- grad_layer_in: float32 [4, 2048, 1024], P('fsdp', 'seq')
- grad_encoder: float32 [4, 512, 1024], P('fsdp', 'seq')
- grad_norm_self: float32 [1024], P('fsdp')
- grad_self_qkv: float32 [1024, 16, 192], P('fsdp')
- grad_self_out: float32 [1024, 1024], P('fsdp')
- grad_rel_table: float32 [32, 16], P(None, 'fsdp')
- grad_norm_cross: float32 [1024], P('fsdp')
- grad_cross_q: float32 [1024, 1024], P('fsdp')
- grad_cross_kv: float32 [1024, 16, 128], P('fsdp')
- grad_cross_out: float32 [1024, 1024], P('fsdp')
- grad_norm_ff: float32 [1024], P('fsdp')
- grad_ff_in: float32 [1024, 5632], P('fsdp')
- grad_ff_out: float32 [2816, 1024], P('fsdp')
The draws below stay inside these ranges and needn't reach their ends.
Inputs may be any that keep to these rules, and one draw needn't show every extreme that they name: `rel_buckets`: the bucket of a query-key distance, in tokens, in the self-attention. Never falls along a sequence; every number from 0 to 3 occurs in each sequence, in decoder_ids and encoder_ids alike. `encoder_ids`: never falls along a sequence; every number from 0 to 3 occurs in each sequence.
All inputs are finite; a program needn't handle non-finite values.
Results may differ from the reference program's by a relative error of at most 0.024.
Values may be sent and summed in bfloat16 or wider, within the bound.
A program may use at most 192 MiB of HBM per device.

```python
import math
import jax
import jax.numpy as jnp
import numpy as np
from jax import lax

D = 1024
H = 16
DH = 64
FF = 2816
NB = 32
LENGTH = 2048
ENC_LEN = 512
SEQS = 4


def draw_rel_buckets(key, part):
    distance = jnp.arange(LENGTH, dtype=jnp.int32)
    exact = NB // 2
    breaks = jax.random.permutation(key, LENGTH - exact - 1)[:NB - exact - 1].astype(jnp.int32) + exact + 1
    passed = jnp.sum((breaks[None, :] <= distance[:, None]).astype(jnp.int32), axis=1)
    return jnp.where(distance < exact, distance, exact + passed).astype(jnp.int32)


def block_scale(key, shape, cuts, least, top_value):
    def one(axis_at, shards_of):
        steps = jax.random.uniform(jax.random.fold_in(jax.random.fold_in(key, 6), axis_at), (shards_of,), jnp.float32, least / len(cuts), top_value / len(cuts))
        return jnp.repeat(jnp.exp(steps), shape[axis_at] // shards_of).reshape((-1,) + (1,) * (len(shape) - axis_at - 1))

    level = one(*cuts[0])
    for cut in cuts[1:]:
        level = level * one(*cut)
    return level


def split_up(number_of, total, reach, lean):
    weights = [(1 << 20) // math.isqrt(standing ** lean) + 1 for standing in range(2, number_of + 1)]
    rest, holding = total - reach - (number_of - 1), [1] * (number_of - 1)
    while rest > 0:
        free = [i for i in range(number_of - 1) if holding[i] < reach]
        mass, budget = sum([weights[i] for i in free]), rest
        for i in free:
            addition = min(reach - holding[i], max(1, budget * weights[i] // mass), rest)
            holding[i] = holding[i] + addition
            rest = rest - addition
    return np.array([reach] + holding)


def ragged_sizes(stream_key, amount, total, limit, lean):
    if amount == 2:
        one = jax.random.randint(stream_key, (), max(1, total - limit), min(limit, total - 1) + 1)
        return jnp.stack([one, total - one])
    tallies = jnp.asarray(split_up(amount, total, limit, lean), jnp.int32)
    twos = (amount - 1) // 2
    giver, sink = tallies[1:1 + 2 * twos:2], tallies[2:2 + 2 * twos:2]
    room = jnp.minimum(giver - 1, limit - sink)
    moved = jax.random.randint(jax.random.fold_in(stream_key, 1), (twos,), 0, 1 << 20) % (room + 1)
    tallies = tallies.at[1:1 + 2 * twos:2].set(giver - moved).at[2:2 + 2 * twos:2].set(sink + moved)
    return tallies[jax.random.permutation(jax.random.fold_in(stream_key, 2), amount)]


def noise(stream_key, shape, scale, limit, shards=(), held_as=jnp.bfloat16):
    entries = scale * jax.random.normal(stream_key, shape, jnp.float32)
    if shards:
        entries = entries * block_scale(stream_key, shape, shards, -0.22, 0.18)
    return jnp.clip(entries, -limit, limit).astype(held_as)


def setup_inputs(seed: int = 0) -> dict:
    key_list = jax.random.split(jax.random.key(seed), 18)
    return {
        "layer_in": noise(key_list[0], (SEQS, LENGTH, D), 1.0, 6.0, ((0, 4), (1, 8))),
        "encoder": noise(key_list[1], (SEQS, ENC_LEN, D), 1.0, 6.0, ((0, 4), (1, 8))),
        "decoder_ids": jax.vmap(lambda own: jnp.searchsorted(jnp.cumsum(ragged_sizes(own, 4, LENGTH, LENGTH // 2, 0)), jnp.arange(LENGTH), side="right"))(jax.random.split(key_list[2], SEQS)).reshape((SEQS, LENGTH)).astype(jnp.int32),
        "encoder_ids": jax.vmap(lambda own: jnp.searchsorted(jnp.cumsum(ragged_sizes(own, 4, ENC_LEN, ENC_LEN // 2, 0)), jnp.arange(ENC_LEN), side="right"))(jax.random.split(key_list[3], SEQS)).reshape((SEQS, ENC_LEN)).astype(jnp.int32),
        "rel_buckets": draw_rel_buckets(jax.random.fold_in(key_list[17], 71), 0),
        "norm_self": jnp.clip(1.0 + 0.1 * jax.random.normal(key_list[5], (D,), jnp.float32), 0.5, 1.5).astype(jnp.bfloat16),
        "self_qkv": noise(key_list[6], (D, H, 3 * DH), (7 * D) ** -0.5, 0.0625, ((0, 4),)),
        "self_out": noise(key_list[7], (D, D), (D // 64) ** -0.5, 1.5, ((0, 4),)),
        "rel_table": noise(key_list[8], (NB, H), 1.0, 4.0, ((1, 4),)),
        "norm_cross": jnp.clip(1.0 + 0.1 * jax.random.normal(key_list[9], (D,), jnp.float32), 0.5, 1.5).astype(jnp.bfloat16),
        "cross_q": noise(key_list[10], (D, D), (7 * D) ** -0.5, 0.0625, ((0, 4),)),
        "cross_kv": noise(key_list[11], (D, H, 2 * DH), (7 * D) ** -0.5, 0.0625, ((0, 4),)),
        "cross_out": noise(key_list[12], (D, D), (D // 64) ** -0.5, 1.5, ((0, 4),)),
        "norm_ff": jnp.clip(1.0 + 0.1 * jax.random.normal(key_list[13], (D,), jnp.float32), 0.5, 1.5).astype(jnp.bfloat16),
        "ff_in": noise(key_list[14], (D, 2 * FF), D ** -0.5, 0.1875, ((0, 4),)),
        "ff_out": noise(key_list[15], (FF, D), FF ** -0.5, 0.109375, ((0, 4),)),
        "cotangent": noise(key_list[16], (SEQS, LENGTH, D), 1.0, 6.0, ((0, 4), (1, 8))),
    }


@jax.custom_vjp
def low(v):
    return lax.optimization_barrier(v.astype(jnp.bfloat16)).astype(jnp.float32)

@jax.custom_vjp
def low_back(v):
    return v

def low_keep(v):
    return (low(v), None)

def low_pass(kept, grad):
    return (grad,)

def back_keep(v):
    return (v, None)

def back_low(kept, grad):
    return (low(grad),)
low.defvjp(low_keep, low_pass)
low_back.defvjp(back_keep, back_low)
EPS = 1e-06
HIGH = lax.Precision.HIGHEST
MASKED = -1e+30

def norm_apply(value, gain):
    return value * lax.rsqrt(lax.optimization_barrier(jnp.mean(value * value, axis=-1, keepdims=True)) + EPS) * gain

def attend(query, key, value, ids_query, ids_key, table, buckets):
    length = query.shape[0]
    block = min(512, length)
    count = length // block

    def one(index):
        start = index * block
        query_rows = lax.dynamic_slice_in_dim(query, start, block, 0)
        ids_rows = lax.dynamic_slice_in_dim(ids_query, start, block, 0)
        score = jnp.einsum('qhd,khd->hqk', query_rows, key, precision=HIGH)
        allowed = ids_rows[:, None] == ids_key[None, :]
        if table is not None:
            position = start + jnp.arange(block, dtype=jnp.int32)
            column = jnp.arange(key.shape[0], dtype=jnp.int32)
            allowed = allowed & (column[None, :] <= position[:, None])
            distance = jnp.maximum(position[:, None] - column[None, :], 0)
            score = score + jnp.transpose(table[buckets[distance]], (2, 0, 1))
        score = low_back(jnp.where(allowed[None], score, MASKED))
        maximum = lax.optimization_barrier(jnp.max(score, axis=-1, keepdims=True))
        exponent = jnp.exp(score - maximum)
        probability = low(exponent / lax.optimization_barrier(jnp.sum(exponent, axis=-1, keepdims=True)))
        return jnp.einsum('hqk,khd->qhd', probability, value, precision=HIGH)
    pieces = lax.map(jax.checkpoint(one), jnp.arange(count, dtype=jnp.int32))
    return pieces.reshape(length, query.shape[1], query.shape[2])

def layer(stream, states, ids, enc_ids, buckets, weights):
    gain_first, qkv_w, mix_self, table, gain_second, query_w, pairs_w, mix_cross, gain_third, inner_w, outer_w = weights
    length, width = stream.shape
    heads = qkv_w.shape[1]
    head_dim = qkv_w.shape[2] // 3
    normed_first = low(norm_apply(stream, gain_first))
    qkv = low_back(low(jnp.einsum('td,dhe->the', normed_first, qkv_w, precision=HIGH)))
    out_self = low_back(low(attend(qkv[..., :head_dim], qkv[..., head_dim:2 * head_dim], qkv[..., 2 * head_dim:], ids, ids, table, buckets)))
    after_self = stream + low_back(jnp.dot(out_self.reshape(length, width), mix_self, precision=HIGH))
    normed_second = low(norm_apply(after_self, gain_second))
    query_cross = low_back(low(jnp.dot(normed_second, query_w, precision=HIGH))).reshape(length, heads, head_dim)
    pairs = low_back(low(jnp.einsum('td,dhe->the', states, pairs_w, precision=HIGH)))
    out_cross = low_back(low(attend(query_cross, pairs[..., :head_dim], pairs[..., head_dim:], ids, enc_ids, None, None)))
    after_cross = after_self + low_back(jnp.dot(out_cross.reshape(length, width), mix_cross, precision=HIGH))
    normed_third = low(norm_apply(after_cross, gain_third))
    gate_up = low_back(jnp.dot(normed_third, inner_w, precision=HIGH))
    inner = gate_up.shape[1] // 2
    hidden = low(jax.nn.gelu(gate_up[:, :inner], approximate=True) * gate_up[:, inner:])
    return after_cross + low_back(jnp.dot(hidden, outer_w, precision=HIGH))

def reference(layer_in, encoder, decoder_ids, encoder_ids, rel_buckets, norm_self, self_qkv, self_out, rel_table, norm_cross, cross_q, cross_kv, cross_out, norm_ff, ff_in, ff_out, cotangent):
    weights = tuple((array.astype(jnp.float32) for array in (norm_self, self_qkv, self_out, rel_table, norm_cross, cross_q, cross_kv, cross_out, norm_ff, ff_in, ff_out)))

    def step(totals, item):
        stream, states, ids, enc_ids, grad_out = item

        def forward(stream_in, states_in, weight_set):
            return layer(stream_in, states_in, ids, enc_ids, rel_buckets, weight_set)
        result, pull = jax.vjp(forward, stream, states, weights)
        grad_stream, grad_states, grad_weights = pull(grad_out)
        return (jax.tree.map(jnp.add, totals, grad_weights), (result.astype(jnp.bfloat16), grad_stream, grad_states))
    zeros = jax.tree.map(jnp.zeros_like, weights)
    items = (layer_in.astype(jnp.float32), encoder.astype(jnp.float32), decoder_ids, encoder_ids, cotangent.astype(jnp.float32))
    totals, outputs = lax.scan(step, zeros, items)
    layer_out, grad_layer_in, grad_encoder = outputs
    grad_norm_self, grad_self_qkv, grad_self_out, grad_rel_table, grad_norm_cross, grad_cross_q, grad_cross_kv, grad_cross_out, grad_norm_ff, grad_ff_in, grad_ff_out = totals
    return (layer_out, grad_layer_in, grad_encoder, grad_norm_self, grad_self_qkv, grad_self_out, grad_rel_table, grad_norm_cross, grad_cross_q, grad_cross_kv, grad_cross_out, grad_norm_ff, grad_ff_in, grad_ff_out)
```

```python
import functools

import jax
import jax.numpy as jnp
from jax import lax
from jax.experimental import pallas as pl
from jax.experimental.pallas import tpu as pltpu
from jax.sharding import PartitionSpec as P

EPS = 1e-06
HIGH = lax.Precision.HIGHEST
MASKED = -1e30
DOCS = 4

BQ = 256
REACH = 1024


def blk(index, size):
    return pl.ds(pl.multiple_of(index * size, size), size)


def turn(value):
    return jnp.transpose(value.astype(jnp.float32), (1, 0))


def bias_tiles(ext_ref, tile_ref, own, bk):
    span = BQ + bk
    for h in range(own):
        for t in range(tile_ref.shape[1]):
            first = t * bk
            line = jnp.broadcast_to(ext_ref[h : h + 1, first : first + span], (bk, span))
            tile_ref[h, t] = pltpu.roll(line, 0, 1, stride=1, stride_axis=0)[:, bk:]


def tile_count(bk):
    return BQ // bk + REACH // bk


def unpack(ref, own, width, picks, flips, base):
    block = 256

    def one(b, _):
        rows = blk(b, block)
        value = ref[rows, :]
        if flips:
            flat = turn(value).astype(jnp.bfloat16)
            for target, piece in flips:
                for h in range(own):
                    at = h * width + piece * 64
                    target[base + h, :, rows] = flat[at : at + 64]
        for target, piece in picks:
            for h in range(own):
                at = h * width + piece * 64
                target[base + h, rows, :] = value[:, at : at + 64]
        return 0

    lax.fori_loop(0, ref.shape[0] // block, one, 0)


def dot(a, b):
    return jnp.dot(a, b, preferred_element_type=jnp.float32)


def score(own_index, key_tile, query_t, tile_ref, t, low, high, first_key):
    value = dot(key_tile, query_t)
    place = lax.broadcasted_iota(jnp.int32, value.shape, 0)
    keep = place >= low - first_key
    if high is not None:
        keep = keep & (place < high - first_key)
    else:
        value = value + tile_ref[own_index, t]
    return jnp.where(keep, value, MASKED)


def forward_body(own, bk, causal, lim_ref, rows_ref, q_t, k_rows, v_t, tile_ref, o_ref, ot_ref, lse_ref):
    length = o_ref.shape[0]

    def q_block(i, _):
        cols = blk(i, BQ)
        queries = [q_t[h, :, cols] for h in range(own)]
        low = rows_ref[0:1, cols]
        high = None if causal else rows_ref[1:2, cols]

        def k_block(j, carry):
            keys = blk(j, bk)
            t = i * (BQ // bk) - j + (BQ // bk - 1)
            out = []
            for h in range(own):
                top, total, acc = carry[h]
                s = score(h, k_rows[h, keys, :], queries[h], tile_ref, t, low, high, j * bk)
                new_top = jnp.maximum(top, jnp.max(s, axis=0, keepdims=True))
                p = jnp.exp(s - new_top)
                scale = jnp.exp(top - new_top)
                total = total * scale + jnp.sum(p, axis=0, keepdims=True)
                acc = acc * scale + dot(v_t[h, :, keys], p.astype(jnp.bfloat16))
                out.append((new_top, total, acc))
            return tuple(out)

        start = tuple(
            (
                jnp.full((1, BQ), MASKED, jnp.float32),
                jnp.zeros((1, BQ), jnp.float32),
                jnp.zeros((64, BQ), jnp.float32),
            )
            for _ in range(own)
        )
        ends = lax.fori_loop(lim_ref[0, i], lim_ref[1, i], k_block, start)
        for h in range(own):
            top, total, acc = ends[h]
            ot_ref[h * 64 : h * 64 + 64, cols] = acc / total
            lse_ref[h : h + 1, cols] = top + jnp.log(total)
        o_ref[cols, :] = turn(ot_ref[:, cols]).astype(jnp.bfloat16)
        return 0

    lax.fori_loop(0, length // BQ, q_block, 0)


def self_forward_kernel(own, bk, lim_ref, rows_ref, ext_ref, x_ref, o_ref, ot_ref, lse_ref, q_t, k_rows, v_t, tile_ref):
    bias_tiles(ext_ref, tile_ref, own, bk)
    unpack(x_ref, own, 192, [(k_rows, 1)], [(q_t, 0), (v_t, 2)], 0)
    forward_body(own, bk, True, lim_ref, rows_ref, q_t, k_rows, v_t, tile_ref, o_ref, ot_ref, lse_ref)


def cross_forward_kernel(own, bk, lim_ref, rows_ref, q_ref, kv_ref, o_ref, ot_ref, lse_ref, q_t, k_rows, v_t):
    unpack(q_ref, own, 64, [], [(q_t, 0)], 0)
    unpack(kv_ref, own, 128, [(k_rows, 0)], [(v_t, 1)], 0)
    forward_body(own, bk, False, lim_ref, rows_ref, q_t, k_rows, v_t, None, o_ref, ot_ref, lse_ref)


def backward_body(
    own, bk, causal, lim_ref, rows_ref, do_ref, ot_ref, lse_ref,
    q_t, q_rows, k_t, k_rows, v_rows, do_t, do_rows, tile_ref, sum_ref, dq_t, dk, dv,
):
    length = do_ref.shape[0]
    dk[...] = jnp.zeros_like(dk)
    dv[...] = jnp.zeros_like(dv)
    if causal:
        sum_ref[...] = jnp.zeros_like(sum_ref)

    def q_block(i, _):
        cols = blk(i, BQ)
        low = rows_ref[0:1, cols]
        high = None if causal else rows_ref[1:2, cols]
        per_head = []
        for h in range(own):
            grad_t = do_t[h, :, cols]
            delta = jnp.sum(
                grad_t.astype(jnp.float32) * ot_ref[h * 64 : h * 64 + 64, cols], axis=0, keepdims=True
            )
            per_head.append((q_t[h, :, cols], grad_t, delta, lse_ref[h : h + 1, cols]))

        def k_block(j, carry):
            keys = blk(j, bk)
            t = i * (BQ // bk) - j + (BQ // bk - 1)
            out = []
            for h in range(own):
                query_t, grad_t, delta, lse = per_head[h]
                s = score(h, k_rows[h, keys, :], query_t, tile_ref, t, low, high, j * bk)
                p = jnp.exp(s - lse)
                dp = dot(v_rows[h, keys, :], grad_t)
                ds = (p * (dp - delta)).astype(jnp.bfloat16)
                dv[h, keys, :] += dot(p.astype(jnp.bfloat16), do_rows[h, cols, :])
                dk[h, keys, :] += dot(ds, q_rows[h, cols, :])
                if causal:
                    sum_ref[h, t] += ds.astype(jnp.float32)
                out.append(carry[h] + dot(k_t[h, :, keys], ds))
            return tuple(out)

        ends = lax.fori_loop(
            lim_ref[0, i],
            lim_ref[1, i],
            k_block,
            tuple(jnp.zeros((64, BQ), jnp.float32) for _ in range(own)),
        )
        for h in range(own):
            dq_t[h * 64 : h * 64 + 64, cols] = ends[h]
        return 0

    lax.fori_loop(0, length // BQ, q_block, 0)


def diagonal_sums(sum_ref, u_ref, own, bk):
    flip = (
        lax.broadcasted_iota(jnp.int32, (bk, bk), 0) + lax.broadcasted_iota(jnp.int32, (bk, bk), 1) == bk - 1
    ).astype(jnp.float32)
    for h in range(own):
        for t in range(sum_ref.shape[1]):
            upside = jnp.dot(flip, sum_ref[h, t], precision=HIGH, preferred_element_type=jnp.float32)
            wide = jnp.concatenate([upside, jnp.zeros((bk, bk), jnp.float32)], axis=1)
            aligned = pltpu.roll(wide, 0, 1, stride=1, stride_axis=0)
            u_ref[h, t : t + 1, :] = jnp.sum(aligned, axis=0, keepdims=True)


def self_backward_kernel(
    own, bk, lim_ref, rows_ref, ext_ref, x_ref, do_ref, ot_ref, lse_ref, dx_ref, u_ref,
    q_t, q_rows, k_t, k_rows, v_rows, do_t, do_rows, tile_ref, sum_ref, dq_t, dk, dv,
):
    bias_tiles(ext_ref, tile_ref, own, bk)
    unpack(x_ref, own, 192, [(q_rows, 0), (k_rows, 1), (v_rows, 2)], [(q_t, 0), (k_t, 1)], 0)
    unpack(do_ref, own, 64, [(do_rows, 0)], [(do_t, 0)], 0)
    backward_body(
        own, bk, True, lim_ref, rows_ref, do_ref, ot_ref, lse_ref,
        q_t, q_rows, k_t, k_rows, v_rows, do_t, do_rows, tile_ref, sum_ref, dq_t, dk, dv,
    )
    diagonal_sums(sum_ref, u_ref, own, bk)

    def pack(b, _):
        rows = blk(b, 256)
        dq = turn(dq_t[:, rows])
        pieces = []
        for h in range(own):
            pieces += [dq[:, h * 64 : h * 64 + 64], dk[h, rows, :], dv[h, rows, :]]
        dx_ref[rows, :] = jnp.concatenate(pieces, axis=1).astype(jnp.bfloat16)
        return 0

    lax.fori_loop(0, x_ref.shape[0] // 256, pack, 0)


def cross_backward_kernel(
    own, bk, lim_ref, rows_ref, q_ref, kv_ref, do_ref, ot_ref, lse_ref, dq_ref, dkv_ref,
    q_t, q_rows, k_t, k_rows, v_rows, do_t, do_rows, dq_t, dk, dv,
):
    unpack(q_ref, own, 64, [(q_rows, 0)], [(q_t, 0)], 0)
    unpack(kv_ref, own, 128, [(k_rows, 0), (v_rows, 1)], [(k_t, 0)], 0)
    unpack(do_ref, own, 64, [(do_rows, 0)], [(do_t, 0)], 0)
    backward_body(
        own, bk, False, lim_ref, rows_ref, do_ref, ot_ref, lse_ref,
        q_t, q_rows, k_t, k_rows, v_rows, do_t, do_rows, None, None, dq_t, dk, dv,
    )

    def pack_q(b, _):
        rows = blk(b, 256)
        dq_ref[rows, :] = turn(dq_t[:, rows]).astype(jnp.bfloat16)
        return 0

    def pack_kv(b, _):
        rows = blk(b, 256)
        pieces = []
        for h in range(own):
            pieces += [dk[h, rows, :], dv[h, rows, :]]
        dkv_ref[rows, :] = jnp.concatenate(pieces, axis=1).astype(jnp.bfloat16)
        return 0

    lax.fori_loop(0, q_ref.shape[0] // 256, pack_q, 0)
    lax.fori_loop(0, kv_ref.shape[0] // 256, pack_kv, 0)


SMEM = pl.BlockSpec(memory_space=pltpu.SMEM)
VMEM = pl.BlockSpec(memory_space=pltpu.VMEM)
bf16, f32 = jnp.bfloat16, jnp.float32


def call(body, name, operands, outs, scratch, flops):
    size = sum(v.size * v.dtype.itemsize for v in operands)
    return pl.pallas_call(
        body,
        name=name,
        out_shape=[jax.ShapeDtypeStruct(s, d) for s, d in outs],
        in_specs=[SMEM] + [VMEM] * (len(operands) - 1),
        out_specs=[VMEM] * len(outs),
        scratch_shapes=[pltpu.VMEM(s, d) for s, d in scratch],
        compiler_params=pltpu.CompilerParams(vmem_limit_bytes=40 << 20),
        cost_estimate=pl.CostEstimate(flops=flops, bytes_accessed=2 * size, transcendentals=flops // 256),
    )(*operands)


def self_forward(limits, rows, ext, x, bk=256):
    length, own = x.shape[0], x.shape[1] // 192
    return call(
        functools.partial(self_forward_kernel, own, bk),
        "self_forward",
        [limits, rows, ext, x],
        [((length, own * 64), bf16), ((own * 64, length), f32), ((own, length), f32)],
        [
            ((own, 64, length), bf16),
            ((own, length, 64), bf16),
            ((own, 64, length), bf16),
            ((own, tile_count(bk), bk, BQ), f32),
        ],
        length * length * own * 64,
    )


def cross_forward(limits, rows, q, kv, bk=256):
    length, own, keys = q.shape[0], q.shape[1] // 64, kv.shape[0]
    return call(
        functools.partial(cross_forward_kernel, own, bk),
        "cross_forward",
        [limits, rows, q, kv],
        [((length, own * 64), bf16), ((own * 64, length), f32), ((own, length), f32)],
        [((own, 64, length), bf16), ((own, keys, 64), bf16), ((own, 64, keys), bf16)],
        length * keys * own * 128,
    )


def self_backward(limits, rows, ext, x, grad, o_t, lse, bk=256):
    length, own = x.shape[0], x.shape[1] // 192
    return call(
        functools.partial(self_backward_kernel, own, bk),
        "self_backward",
        [limits, rows, ext, x, grad, o_t, lse],
        [((length, own * 192), bf16), ((own, tile_count(bk), BQ + bk), f32)],
        [
            ((own, 64, length), bf16),
            ((own, length, 64), bf16),
            ((own, 64, length), bf16),
            ((own, length, 64), bf16),
            ((own, length, 64), bf16),
            ((own, 64, length), bf16),
            ((own, length, 64), bf16),
            ((own, tile_count(bk), bk, BQ), f32),
            ((own, tile_count(bk), bk, BQ), f32),
            ((own * 64, length), f32),
            ((own, length, 64), f32),
            ((own, length, 64), f32),
        ],
        length * length * own * 160,
    )


def cross_backward(limits, rows, q, kv, grad, o_t, lse, bk=256):
    length, own, keys = q.shape[0], q.shape[1] // 64, kv.shape[0]
    return call(
        functools.partial(cross_backward_kernel, own, bk),
        "cross_backward",
        [limits, rows, q, kv, grad, o_t, lse],
        [((length, own * 64), bf16), ((keys, own * 128), bf16)],
        [
            ((own, 64, length), bf16),
            ((own, length, 64), bf16),
            ((own, 64, keys), bf16),
            ((own, keys, 64), bf16),
            ((own, keys, 64), bf16),
            ((own, 64, length), bf16),
            ((own, length, 64), bf16),
            ((own * 64, length), f32),
            ((own, keys, 64), f32),
            ((own, keys, 64), f32),
        ],
        length * keys * own * 320,
    )


def norm_apply(value, gain):
    return value * lax.rsqrt(jnp.mean(value * value, axis=-1, keepdims=True) + EPS) * gain


def norm_back(value, gain, grad):
    _, pull = jax.vjp(norm_apply, value, gain)
    return pull(grad)


def gate_mix(gate_up):
    inner = gate_up.shape[1] // 2
    return jax.nn.gelu(gate_up[:, :inner], approximate=True) * gate_up[:, inner:]


def counts_below(ids, values):
    total = jnp.zeros_like(values)
    for doc in range(DOCS):
        total = total + jnp.where(values > doc, jnp.sum((ids == doc).astype(jnp.int32)), 0)
    return total


def swap(blocks):
    return lax.all_to_all(blocks, "seq", split_axis=0, concat_axis=0, tiled=True)


def shards(
    layer_in, encoder, decoder_ids, encoder_ids, rel_buckets,
    norm_self, self_qkv, self_out, rel_table, norm_cross, cross_q, cross_kv, cross_out, norm_ff, ff_in, ff_out,
    cotangent,
):
    seqs, local, width = layer_in.shape
    enc_local = encoder.shape[1]
    parts = lax.axis_size("seq")
    heads = self_qkv.shape[1]
    dh = self_qkv.shape[2] // 3
    own = heads // parts
    rows = seqs * local
    buckets, table_own = rel_table.shape
    length, keys = local * parts, enc_local * parts
    gather = lambda v: lax.all_gather(v, "fsdp", axis=0, tiled=True)

    qkv_w = gather(self_qkv).reshape(width, parts, own * 3 * dh)
    pairs_w = gather(cross_kv).reshape(width, parts, own * 2 * dh)
    mix_self = gather(self_out).reshape(parts, own * dh, width)
    query_w = gather(cross_q).reshape(width, parts, own * dh)
    mix_cross = gather(cross_out).reshape(parts, own * dh, width)
    inner_w = gather(ff_in)
    outer_w = gather(ff_out)
    small = jnp.concatenate([norm_self, norm_cross, norm_ff, rel_table.reshape(-1)])
    small = lax.all_gather(small, "fsdp", axis=0, tiled=False)
    part = norm_self.shape[0]
    gain_first, gain_second, gain_third = (
        small[:, i * part : (i + 1) * part].reshape(width).astype(f32) for i in range(3)
    )
    table = jnp.transpose(small[:, 3 * part :].reshape(-1, buckets, table_own), (1, 0, 2)).reshape(buckets, heads)
    both_ids = jnp.concatenate([decoder_ids.reshape(-1), encoder_ids.reshape(-1)])
    both_ids = lax.all_gather(both_ids, "seq", axis=0, tiled=False)
    ids = both_ids[:, :local].reshape(length)
    enc_ids = both_ids[:, local:].reshape(keys)

    first_seen = counts_below(ids, ids)
    enc_first = counts_below(enc_ids, ids)
    enc_last = counts_below(enc_ids, ids + 1)
    blocks = length // BQ
    bk = 256
    self_rows = jnp.broadcast_to(first_seen[None], (8, length))
    cross_rows = jnp.concatenate([enc_first[None], enc_last[None], jnp.zeros((6, length), jnp.int32)])
    self_limits = jnp.stack(
        [first_seen[::BQ] // bk, (jnp.arange(blocks, dtype=jnp.int32) + 1) * (BQ // bk)]
    )
    cross_limits = jnp.stack([enc_first[::BQ] // bk, (enc_last[BQ - 1 :: BQ] + bk - 1) // bk])

    first_head = lax.axis_index("seq") * own
    table_mine = lax.dynamic_slice_in_dim(table.astype(f32), first_head, own, 1)
    near = rel_buckets[:REACH]
    onehot = (near[:, None] == jnp.arange(buckets, dtype=jnp.int32)[None, :]).astype(f32)
    bias = jnp.einsum("ln,ng->gl", onehot, table_mine, precision=HIGH)
    ext = jnp.concatenate(
        [jnp.full((own, BQ), MASKED, f32), bias, jnp.zeros((own, BQ), f32)], axis=1
    )

    stream = layer_in.astype(f32).reshape(rows, width)
    normed_first = norm_apply(stream, gain_first).astype(bf16)
    qkv_tok = jnp.einsum("td,dge->gte", normed_first, qkv_w, preferred_element_type=f32).astype(bf16)
    qkv = swap(qkv_tok).reshape(length, own * 3 * dh)
    out_self, self_t, self_lse = self_forward(self_limits, self_rows, ext, qkv)
    self_tok = swap(out_self.reshape(parts, local, own * dh))
    after_self = stream + jnp.einsum("gtc,gcd->td", self_tok, mix_self, preferred_element_type=f32)
    normed_second = norm_apply(after_self, gain_second).astype(bf16)
    query_tok = jnp.einsum("td,dgc->gtc", normed_second, query_w, preferred_element_type=f32).astype(bf16)
    enc_flat = encoder.reshape(seqs * enc_local, width)
    pairs_tok = jnp.einsum("td,dge->gte", enc_flat, pairs_w, preferred_element_type=f32).astype(bf16)
    query_cross = swap(query_tok).reshape(length, own * dh)
    pairs = swap(pairs_tok).reshape(keys, own * 2 * dh)
    out_cross, cross_t, cross_lse = cross_forward(cross_limits, cross_rows, query_cross, pairs)
    cross_tok = swap(out_cross.reshape(parts, local, own * dh))
    after_cross = after_self + jnp.einsum("gtc,gcd->td", cross_tok, mix_cross, preferred_element_type=f32)
    normed_third = norm_apply(after_cross, gain_third).astype(bf16)
    gate_up = jnp.dot(normed_third, inner_w, preferred_element_type=f32)
    hidden = gate_mix(gate_up).astype(bf16)
    layer_out = (
        (after_cross + jnp.dot(hidden, outer_w, preferred_element_type=f32)).astype(bf16).reshape(seqs, local, width)
    )

    grad_low = cotangent.reshape(rows, width)
    grad_outer = jnp.einsum("tf,td->fd", hidden, grad_low, preferred_element_type=f32)
    grad_hidden = jnp.einsum("td,fd->tf", grad_low, outer_w, preferred_element_type=f32)
    _, pull_mix = jax.vjp(gate_mix, gate_up)
    grad_gate_up = pull_mix(grad_hidden)[0].astype(bf16)
    grad_inner = jnp.einsum("td,tf->df", normed_third, grad_gate_up, preferred_element_type=f32)
    grad_third_in = jnp.einsum("tf,df->td", grad_gate_up, inner_w, preferred_element_type=f32)
    grad_from_third, grad_gain_third = norm_back(after_cross, gain_third, grad_third_in)
    grad_middle = grad_low.astype(f32) + grad_from_third
    middle_low = grad_middle.astype(bf16)
    grad_mix_cross = jnp.einsum("gtc,td->gcd", cross_tok, middle_low, preferred_element_type=f32)
    grad_cross_tok = jnp.einsum("td,gcd->gtc", middle_low, mix_cross, preferred_element_type=f32).astype(bf16)
    grad_cross = swap(grad_cross_tok).reshape(length, own * dh)
    grad_query, grad_pairs = cross_backward(
        cross_limits, cross_rows, query_cross, pairs, grad_cross, cross_t, cross_lse
    )
    grad_query_tok = swap(grad_query.reshape(parts, local, own * dh))
    grad_pairs_tok = swap(grad_pairs.reshape(parts, enc_local, own * 2 * dh))
    grad_query_w = jnp.einsum("td,gtc->dgc", normed_second, grad_query_tok, preferred_element_type=f32)
    grad_second_in = jnp.einsum("gtc,dgc->td", grad_query_tok, query_w, preferred_element_type=f32)
    grad_pairs_w = jnp.einsum("td,gte->dge", enc_flat, grad_pairs_tok, preferred_element_type=f32)
    grad_encoder = jnp.einsum("gte,dge->td", grad_pairs_tok, pairs_w, preferred_element_type=f32).reshape(
        seqs, enc_local, width
    )
    grad_from_second, grad_gain_second = norm_back(after_self, gain_second, grad_second_in)
    grad_upper = grad_middle + grad_from_second
    upper_low = grad_upper.astype(bf16)
    grad_mix_self = jnp.einsum("gtc,td->gcd", self_tok, upper_low, preferred_element_type=f32)
    grad_self_tok = jnp.einsum("td,gcd->gtc", upper_low, mix_self, preferred_element_type=f32).astype(bf16)
    grad_self = swap(grad_self_tok).reshape(length, own * dh)
    grad_qkv, tile_sums = self_backward(self_limits, self_rows, ext, qkv, grad_self, self_t, self_lse)
    grad_qkv_tok = swap(grad_qkv.reshape(parts, local, own * 3 * dh))
    grad_qkv_w = jnp.einsum("td,gte->dge", normed_first, grad_qkv_tok, preferred_element_type=f32)
    grad_first_in = jnp.einsum("gte,dge->td", grad_qkv_tok, qkv_w, preferred_element_type=f32)
    grad_from_first, grad_gain_first = norm_back(stream, gain_first, grad_first_in)
    grad_layer_in = (grad_upper + grad_from_first).reshape(seqs, local, width)

    bucket_line = jnp.concatenate(
        [jnp.full((BQ,), -1, jnp.int32), near, jnp.full((BQ + bk,), -1, jnp.int32)]
    )
    by_tile = jnp.stack([bucket_line[t * bk + 1 : t * bk + 1 + BQ + bk] for t in range(tile_count(bk))])
    in_bucket = (by_tile[:, :, None] == jnp.arange(buckets, dtype=jnp.int32)).astype(f32)
    by_bucket = jnp.einsum("twn,gtw->ng", in_bucket, tile_sums, precision=HIGH)
    grad_table = lax.dynamic_update_slice_in_dim(jnp.zeros((buckets, heads), f32), by_bucket, first_head, 1)

    def reduce(grad):
        mine = lax.psum_scatter(grad.astype(bf16), "fsdp", scatter_dimension=0, tiled=True)
        return lax.psum(mine, "seq").astype(f32)

    total_qkv = reduce(grad_qkv_w.reshape(width, heads, 3 * dh))
    total_pairs = reduce(grad_pairs_w.reshape(width, heads, 2 * dh))
    total_mix_self = reduce(grad_mix_self.reshape(width, width))
    total_query = reduce(grad_query_w.reshape(width, width))
    total_mix_cross = reduce(grad_mix_cross.reshape(width, width))
    total_inner = reduce(grad_inner)
    total_outer = reduce(grad_outer)
    gains = jnp.concatenate(
        [g.reshape(-1, part) for g in (grad_gain_first, grad_gain_second, grad_gain_third)], axis=1
    )
    tables = jnp.transpose(grad_table.reshape(buckets, -1, table_own), (1, 0, 2)).reshape(-1, buckets * table_own)
    small_grads = jnp.concatenate([gains, tables], axis=1).astype(bf16)
    small_total = lax.psum(small_grads, ("seq", "fsdp")).astype(f32)
    mine = lax.dynamic_index_in_dim(small_total, lax.axis_index("fsdp"), 0, False)
    total_gain_first, total_gain_second, total_gain_third = (mine[i * part : (i + 1) * part] for i in range(3))
    total_table = mine[3 * part :].reshape(buckets, table_own)
    return (
        layer_out, grad_layer_in, grad_encoder, total_gain_first, total_qkv, total_mix_self, total_table,
        total_gain_second, total_query, total_pairs, total_mix_cross, total_gain_third, total_inner, total_outer,
    )


def solution(mesh):
    in_specs = (
        P("fsdp", "seq", None), P("fsdp", "seq", None), P("fsdp", "seq"), P("fsdp", "seq"), P(),
        P("fsdp"), P("fsdp", None, None), P("fsdp", None), P(None, "fsdp"), P("fsdp"), P("fsdp", None),
        P("fsdp", None, None), P("fsdp", None), P("fsdp"), P("fsdp", None), P("fsdp", None),
        P("fsdp", "seq", None),
    )
    out_specs = (
        P("fsdp", "seq", None), P("fsdp", "seq", None), P("fsdp", "seq", None), P("fsdp"), P("fsdp", None, None),
        P("fsdp", None), P(None, "fsdp"), P("fsdp"), P("fsdp", None), P("fsdp", None, None), P("fsdp", None),
        P("fsdp"), P("fsdp", None), P("fsdp", None),
    )
    return jax.shard_map(shards, mesh=mesh, in_specs=in_specs, out_specs=out_specs, check_vma=False)
```

```python
import functools

import jax
import jax.numpy as jnp
from jax import lax
from jax.experimental import pallas as pl
from jax.experimental.pallas import tpu as pltpu
from jax.sharding import PartitionSpec as P

EPS = 1e-06
HIGH = lax.Precision.HIGHEST
MASKED = -1e30
DOCS = 4

BQ = 256
REACH = 1024


def blk(index, size):
    return pl.ds(pl.multiple_of(index * size, size), size)


def turn(value):
    return jnp.transpose(value.astype(jnp.float32), (1, 0))


def bias_tiles(ext_ref, tile_ref, own, bk):
    span = BQ + bk
    for h in range(own):
        for t in range(tile_ref.shape[1]):
            first = t * bk
            line = jnp.broadcast_to(ext_ref[h : h + 1, first : first + span], (bk, span))
            tile_ref[h, t] = pltpu.roll(line, 0, 1, stride=1, stride_axis=0)[:, bk:]


def tile_count(bk):
    return BQ // bk + REACH // bk


def unpack(ref, own, width, picks, flips, base):
    block = 256

    def one(b, _):
        rows = blk(b, block)
        value = ref[rows, :]
        if flips:
            flat = turn(value).astype(jnp.bfloat16)
            for target, piece in flips:
                for h in range(own):
                    at = h * width + piece * 64
                    target[base + h, :, rows] = flat[at : at + 64]
        for target, piece in picks:
            for h in range(own):
                at = h * width + piece * 64
                target[base + h, rows, :] = value[:, at : at + 64]
        return 0

    lax.fori_loop(0, ref.shape[0] // block, one, 0)


def dot(a, b):
    return jnp.dot(a, b, preferred_element_type=jnp.float32)


def score(own_index, key_tile, query_t, tile_ref, t, low, high, first_key):
    value = dot(key_tile, query_t)
    place = lax.broadcasted_iota(jnp.int32, value.shape, 0)
    keep = place >= low - first_key
    if high is not None:
        keep = keep & (place < high - first_key)
    else:
        value = value + tile_ref[own_index, t]
    return jnp.where(keep, value, MASKED)


def forward_body(own, bk, causal, lim_ref, rows_ref, q_t, k_rows, v_t, tile_ref, o_ref, ot_ref, lse_ref):
    length = o_ref.shape[0]

    def q_block(i, _):
        cols = blk(i, BQ)
        queries = [q_t[h, :, cols] for h in range(own)]
        low = rows_ref[0:1, cols]
        high = None if causal else rows_ref[1:2, cols]

        def k_block(j, carry):
            keys = blk(j, bk)
            t = i * (BQ // bk) - j + (BQ // bk - 1)
            out = []
            for h in range(own):
                top, total, acc = carry[h]
                s = score(h, k_rows[h, keys, :], queries[h], tile_ref, t, low, high, j * bk)
                new_top = jnp.maximum(top, jnp.max(s, axis=0, keepdims=True))
                p = jnp.exp(s - new_top)
                scale = jnp.exp(top - new_top)
                total = total * scale + jnp.sum(p, axis=0, keepdims=True)
                acc = acc * scale + dot(v_t[h, :, keys], p.astype(jnp.bfloat16))
                out.append((new_top, total, acc))
            return tuple(out)

        start = tuple(
            (
                jnp.full((1, BQ), MASKED, jnp.float32),
                jnp.zeros((1, BQ), jnp.float32),
                jnp.zeros((64, BQ), jnp.float32),
            )
            for _ in range(own)
        )
        ends = lax.fori_loop(lim_ref[0, i], lim_ref[1, i], k_block, start)
        for h in range(own):
            top, total, acc = ends[h]
            ot_ref[h * 64 : h * 64 + 64, cols] = acc / total
            lse_ref[h : h + 1, cols] = top + jnp.log(total)
        o_ref[cols, :] = turn(ot_ref[:, cols]).astype(jnp.bfloat16)
        return 0

    lax.fori_loop(0, length // BQ, q_block, 0)


def self_forward_kernel(own, bk, lim_ref, rows_ref, ext_ref, x_ref, o_ref, ot_ref, lse_ref, q_t, k_rows, v_t, tile_ref):
    bias_tiles(ext_ref, tile_ref, own, bk)
    unpack(x_ref, own, 192, [(k_rows, 1)], [(q_t, 0), (v_t, 2)], 0)
    forward_body(own, bk, True, lim_ref, rows_ref, q_t, k_rows, v_t, tile_ref, o_ref, ot_ref, lse_ref)


def cross_forward_kernel(own, bk, lim_ref, rows_ref, q_ref, kv_ref, o_ref, ot_ref, lse_ref, q_t, k_rows, v_t):
    unpack(q_ref, own, 64, [], [(q_t, 0)], 0)
    unpack(kv_ref, own, 128, [(k_rows, 0)], [(v_t, 1)], 0)
    forward_body(own, bk, False, lim_ref, rows_ref, q_t, k_rows, v_t, None, o_ref, ot_ref, lse_ref)


def backward_body(
    own, bk, causal, lim_ref, rows_ref, do_ref, ot_ref, lse_ref,
    q_t, q_rows, k_t, k_rows, v_rows, do_t, do_rows, tile_ref, sum_ref, dq_t, dk, dv,
):
    length = do_ref.shape[0]
    dk[...] = jnp.zeros_like(dk)
    dv[...] = jnp.zeros_like(dv)
    if causal:
        sum_ref[...] = jnp.zeros_like(sum_ref)

    def q_block(i, _):
        cols = blk(i, BQ)
        low = rows_ref[0:1, cols]
        high = None if causal else rows_ref[1:2, cols]
        per_head = []
        for h in range(own):
            grad_t = do_t[h, :, cols]
            delta = jnp.sum(
                grad_t.astype(jnp.float32) * ot_ref[h * 64 : h * 64 + 64, cols], axis=0, keepdims=True
            )
            per_head.append((q_t[h, :, cols], grad_t, delta, lse_ref[h : h + 1, cols]))

        def k_block(j, carry):
            keys = blk(j, bk)
            t = i * (BQ // bk) - j + (BQ // bk - 1)
            out = []
            for h in range(own):
                query_t, grad_t, delta, lse = per_head[h]
                s = score(h, k_rows[h, keys, :], query_t, tile_ref, t, low, high, j * bk)
                p = jnp.exp(s - lse)
                dp = dot(v_rows[h, keys, :], grad_t)
                ds = (p * (dp - delta)).astype(jnp.bfloat16)
                dv[h, keys, :] += dot(p.astype(jnp.bfloat16), do_rows[h, cols, :])
                dk[h, keys, :] += dot(ds, q_rows[h, cols, :])
                if causal:
                    sum_ref[h, t] += ds.astype(jnp.float32)
                out.append(carry[h] + dot(k_t[h, :, keys], ds))
            return tuple(out)

        ends = lax.fori_loop(
            lim_ref[0, i],
            lim_ref[1, i],
            k_block,
            tuple(jnp.zeros((64, BQ), jnp.float32) for _ in range(own)),
        )
        for h in range(own):
            dq_t[h * 64 : h * 64 + 64, cols] = ends[h]
        return 0

    lax.fori_loop(0, length // BQ, q_block, 0)


def diagonal_sums(sum_ref, u_ref, own, bk):
    flip = (
        lax.broadcasted_iota(jnp.int32, (bk, bk), 0) + lax.broadcasted_iota(jnp.int32, (bk, bk), 1) == bk - 1
    ).astype(jnp.float32)
    for h in range(own):
        for t in range(sum_ref.shape[1]):
            upside = jnp.dot(flip, sum_ref[h, t], precision=HIGH, preferred_element_type=jnp.float32)
            wide = jnp.concatenate([upside, jnp.zeros((bk, bk), jnp.float32)], axis=1)
            aligned = pltpu.roll(wide, 0, 1, stride=1, stride_axis=0)
            u_ref[h, t : t + 1, :] = jnp.sum(aligned, axis=0, keepdims=True)


def self_backward_kernel(
    own, bk, lim_ref, rows_ref, ext_ref, x_ref, do_ref, ot_ref, lse_ref, dx_ref, u_ref,
    q_t, q_rows, k_t, k_rows, v_rows, do_t, do_rows, tile_ref, sum_ref, dq_t, dk, dv,
):
    bias_tiles(ext_ref, tile_ref, own, bk)
    unpack(x_ref, own, 192, [(q_rows, 0), (k_rows, 1), (v_rows, 2)], [(q_t, 0), (k_t, 1)], 0)
    unpack(do_ref, own, 64, [(do_rows, 0)], [(do_t, 0)], 0)
    backward_body(
        own, bk, True, lim_ref, rows_ref, do_ref, ot_ref, lse_ref,
        q_t, q_rows, k_t, k_rows, v_rows, do_t, do_rows, tile_ref, sum_ref, dq_t, dk, dv,
    )
    diagonal_sums(sum_ref, u_ref, own, bk)

    def pack(b, _):
        rows = blk(b, 256)
        dq = turn(dq_t[:, rows])
        pieces = []
        for h in range(own):
            pieces += [dq[:, h * 64 : h * 64 + 64], dk[h, rows, :], dv[h, rows, :]]
        dx_ref[rows, :] = jnp.concatenate(pieces, axis=1).astype(jnp.bfloat16)
        return 0

    lax.fori_loop(0, x_ref.shape[0] // 256, pack, 0)


def cross_backward_kernel(
    own, bk, lim_ref, rows_ref, q_ref, kv_ref, do_ref, ot_ref, lse_ref, dq_ref, dkv_ref,
    q_t, q_rows, k_t, k_rows, v_rows, do_t, do_rows, dq_t, dk, dv,
):
    unpack(q_ref, own, 64, [(q_rows, 0)], [(q_t, 0)], 0)
    unpack(kv_ref, own, 128, [(k_rows, 0), (v_rows, 1)], [(k_t, 0)], 0)
    unpack(do_ref, own, 64, [(do_rows, 0)], [(do_t, 0)], 0)
    backward_body(
        own, bk, False, lim_ref, rows_ref, do_ref, ot_ref, lse_ref,
        q_t, q_rows, k_t, k_rows, v_rows, do_t, do_rows, None, None, dq_t, dk, dv,
    )

    def pack_q(b, _):
        rows = blk(b, 256)
        dq_ref[rows, :] = turn(dq_t[:, rows]).astype(jnp.bfloat16)
        return 0

    def pack_kv(b, _):
        rows = blk(b, 256)
        pieces = []
        for h in range(own):
            pieces += [dk[h, rows, :], dv[h, rows, :]]
        dkv_ref[rows, :] = jnp.concatenate(pieces, axis=1).astype(jnp.bfloat16)
        return 0

    lax.fori_loop(0, q_ref.shape[0] // 256, pack_q, 0)
    lax.fori_loop(0, kv_ref.shape[0] // 256, pack_kv, 0)


SMEM = pl.BlockSpec(memory_space=pltpu.SMEM)
VMEM = pl.BlockSpec(memory_space=pltpu.VMEM)
bf16, f32 = jnp.bfloat16, jnp.float32


def call(body, name, operands, outs, scratch, flops):
    size = sum(v.size * v.dtype.itemsize for v in operands)
    return pl.pallas_call(
        body,
        name=name,
        out_shape=[jax.ShapeDtypeStruct(s, d) for s, d in outs],
        in_specs=[SMEM] + [VMEM] * (len(operands) - 1),
        out_specs=[VMEM] * len(outs),
        scratch_shapes=[pltpu.VMEM(s, d) for s, d in scratch],
        compiler_params=pltpu.CompilerParams(vmem_limit_bytes=40 << 20),
        cost_estimate=pl.CostEstimate(flops=flops, bytes_accessed=2 * size, transcendentals=flops // 256),
    )(*operands)


def self_forward(limits, rows, ext, x, bk=256):
    length, own = x.shape[0], x.shape[1] // 192
    return call(
        functools.partial(self_forward_kernel, own, bk),
        "self_forward",
        [limits, rows, ext, x],
        [((length, own * 64), bf16), ((own * 64, length), f32), ((own, length), f32)],
        [
            ((own, 64, length), bf16),
            ((own, length, 64), bf16),
            ((own, 64, length), bf16),
            ((own, tile_count(bk), bk, BQ), f32),
        ],
        length * length * own * 64,
    )


def cross_forward(limits, rows, q, kv, bk=256):
    length, own, keys = q.shape[0], q.shape[1] // 64, kv.shape[0]
    return call(
        functools.partial(cross_forward_kernel, own, bk),
        "cross_forward",
        [limits, rows, q, kv],
        [((length, own * 64), bf16), ((own * 64, length), f32), ((own, length), f32)],
        [((own, 64, length), bf16), ((own, keys, 64), bf16), ((own, 64, keys), bf16)],
        length * keys * own * 128,
    )


def self_backward(limits, rows, ext, x, grad, o_t, lse, bk=256):
    length, own = x.shape[0], x.shape[1] // 192
    return call(
        functools.partial(self_backward_kernel, own, bk),
        "self_backward",
        [limits, rows, ext, x, grad, o_t, lse],
        [((length, own * 192), bf16), ((own, tile_count(bk), BQ + bk), f32)],
        [
            ((own, 64, length), bf16),
            ((own, length, 64), bf16),
            ((own, 64, length), bf16),
            ((own, length, 64), bf16),
            ((own, length, 64), bf16),
            ((own, 64, length), bf16),
            ((own, length, 64), bf16),
            ((own, tile_count(bk), bk, BQ), f32),
            ((own, tile_count(bk), bk, BQ), f32),
            ((own * 64, length), f32),
            ((own, length, 64), f32),
            ((own, length, 64), f32),
        ],
        length * length * own * 160,
    )


def cross_backward(limits, rows, q, kv, grad, o_t, lse, bk=256):
    length, own, keys = q.shape[0], q.shape[1] // 64, kv.shape[0]
    return call(
        functools.partial(cross_backward_kernel, own, bk),
        "cross_backward",
        [limits, rows, q, kv, grad, o_t, lse],
        [((length, own * 64), bf16), ((keys, own * 128), bf16)],
        [
            ((own, 64, length), bf16),
            ((own, length, 64), bf16),
            ((own, 64, keys), bf16),
            ((own, keys, 64), bf16),
            ((own, keys, 64), bf16),
            ((own, 64, length), bf16),
            ((own, length, 64), bf16),
            ((own * 64, length), f32),
            ((own, keys, 64), f32),
            ((own, keys, 64), f32),
        ],
        length * keys * own * 320,
    )


MESH = pl.DeviceIdType.MESH


def ring_place(index, n):
    z, x = index // 2, index % 2
    return z + x * (n - 1 - 2 * z)


def ring_index(place, n):
    x = place // (n // 2)
    z = place + x * (n - 1 - 2 * place)
    return 2 * z + x


def ring_kernel(n, splits, *refs):
    count = len(splits)
    x_refs, y_refs, slots = refs[:count], refs[count : 2 * count], refs[2 * count : 3 * count]
    send_sem, recv_sem = refs[3 * count :]
    place = ring_place(lax.axis_index("seq"), n)
    right = ring_index((place + 1) % n, n)
    left = ring_index((place + n - 1) % n, n)
    barrier = pltpu.get_barrier_semaphore()
    for neighbour in (left, right):
        pl.semaphore_signal(barrier, inc=1, device_id={"seq": neighbour}, device_id_type=MESH)
    pl.semaphore_wait(barrier, 2)

    streams = []
    for k in range(count):
        for piece in range(splits[k]):
            streams.append((k, piece, piece % 2))

    def view(ref, k, piece, chunk):
        rows = x_refs[k].shape[0] // n
        cols = x_refs[k].shape[1] // splits[k]
        return ref.at[pl.ds(pl.multiple_of(chunk * rows, 8), rows), pl.ds(piece * cols, cols)]

    def slot(k, piece, step):
        rows = x_refs[k].shape[0] // n
        cols = x_refs[k].shape[1] // splits[k]
        return slots[k].at[pl.ds(step * rows, rows), pl.ds(piece * cols, cols)]

    def copy(number, step, src, dst, down):
        return pltpu.make_async_remote_copy(
            src_ref=src,
            dst_ref=dst,
            send_sem=send_sem.at[number, step],
            recv_sem=recv_sem.at[number, step],
            device_id={"seq": left if down else right},
            device_id_type=MESH,
        )

    def chunk_at(down, step):
        return (place + 1 + step) % n if down else (place + 2 * n - 1 - step) % n

    copies = {}

    def start(number, step, src, dst, down):
        copies[number, step] = copy(number, step, src, dst, down)
        copies[number, step].start()

    for number, (k, piece, down) in enumerate(streams):
        start(number, 0, view(x_refs[k], k, piece, place), slot(k, piece, 0), down)
    for step in range(n - 1):
        for number, (k, piece, down) in enumerate(streams):
            copies[number, step].wait_recv()
            chunk = chunk_at(down, step)
            mine = view(x_refs[k], k, piece, chunk)
            landed = slot(k, piece, step)
            total = landed[...].astype(jnp.float32) + mine[...].astype(jnp.float32)
            if step < n - 2:
                landed[...] = total.astype(jnp.bfloat16)
                start(number, step + 1, landed, slot(k, piece, step + 1), down)
            else:
                done = view(y_refs[k], k, piece, chunk)
                done[...] = total.astype(jnp.bfloat16)
                start(number, n - 1, done, done, down)
    for step in range(n - 1):
        for number, (k, piece, down) in enumerate(streams):
            copies[number, n - 1 + step].wait_recv()
            if step < n - 2:
                chunk = chunk_at(down, n - 1 + step)
                done = view(y_refs[k], k, piece, chunk)
                start(number, n + step, done, done, down)
    for one in copies.values():
        one.wait_send()


def ring_total(arrays, splits, ident):
    n = lax.axis_size("seq")
    size = sum(v.size * 2 for v in arrays)
    return pl.pallas_call(
        functools.partial(ring_kernel, n, splits),
        name="ring_total",
        out_shape=[jax.ShapeDtypeStruct(v.shape, jnp.bfloat16) for v in arrays],
        in_specs=[pl.BlockSpec(memory_space=pltpu.VMEM)] * len(arrays),
        out_specs=[pl.BlockSpec(memory_space=pltpu.VMEM)] * len(arrays),
        scratch_shapes=[pltpu.VMEM((v.shape[0] // n * (n - 1), v.shape[1]), jnp.bfloat16) for v in arrays]
        + [pltpu.SemaphoreType.DMA((sum(splits), 2 * n - 2)), pltpu.SemaphoreType.DMA((sum(splits), 2 * n - 2))],
        compiler_params=pltpu.CompilerParams(
            collective_id=ident, has_side_effects=True, vmem_limit_bytes=48 << 20
        ),
        cost_estimate=pl.CostEstimate(flops=size, bytes_accessed=60 * size, transcendentals=0),
    )(*arrays)


def norm_apply(value, gain):
    return value * lax.rsqrt(jnp.mean(value * value, axis=-1, keepdims=True) + EPS) * gain


def norm_back(value, gain, grad):
    _, pull = jax.vjp(norm_apply, value, gain)
    return pull(grad)


def gate_mix(gate_up):
    inner = gate_up.shape[1] // 2
    return jax.nn.gelu(gate_up[:, :inner], approximate=True) * gate_up[:, inner:]


def counts_below(ids, values):
    total = jnp.zeros_like(values)
    for doc in range(DOCS):
        total = total + jnp.where(values > doc, jnp.sum((ids == doc).astype(jnp.int32)), 0)
    return total


def swap(blocks):
    return lax.all_to_all(blocks, "seq", split_axis=0, concat_axis=0, tiled=True)


def scatter(grad):
    return lax.psum_scatter(grad, "fsdp", scatter_dimension=0, tiled=True)


def over_seq(arrays, splits, ident):
    n = lax.axis_size("seq")
    if all(v.shape[0] % (8 * n) == 0 and v.shape[1] % (128 * s) == 0 for v, s in zip(arrays, splits)):
        return ring_total(arrays, splits, ident)
    return [lax.psum(v, "seq") for v in arrays]


def shards(
    layer_in, encoder, decoder_ids, encoder_ids, rel_buckets,
    norm_self, self_qkv, self_out, rel_table, norm_cross, cross_q, cross_kv, cross_out, norm_ff, ff_in, ff_out,
    cotangent,
):
    seqs, local, width = layer_in.shape
    enc_local = encoder.shape[1]
    parts = lax.axis_size("seq")
    heads = self_qkv.shape[1]
    dh = self_qkv.shape[2] // 3
    own = heads // parts
    rows = seqs * local
    buckets, table_own = rel_table.shape
    length, keys = local * parts, enc_local * parts
    gather = lambda v: lax.all_gather(v, "fsdp", axis=0, tiled=True)

    qkv_w = gather(self_qkv).reshape(width, parts, own * 3 * dh)
    middle = gather(jnp.concatenate([self_out, cross_q, cross_out], axis=1))
    pairs_w = gather(cross_kv).reshape(width, parts, own * 2 * dh)
    mix_self = middle[:, :width].reshape(parts, own * dh, width)
    query_w = middle[:, width : 2 * width].reshape(width, parts, own * dh)
    mix_cross = middle[:, 2 * width :].reshape(parts, own * dh, width)
    inner_w = gather(ff_in)
    outer_w = gather(ff_out)
    small = jnp.concatenate([norm_self, norm_cross, norm_ff, rel_table.reshape(-1)])
    small = lax.all_gather(small, "fsdp", axis=0, tiled=False)
    part = norm_self.shape[0]
    gain_first, gain_second, gain_third = (
        small[:, i * part : (i + 1) * part].reshape(width).astype(f32) for i in range(3)
    )
    table = jnp.transpose(small[:, 3 * part :].reshape(-1, buckets, table_own), (1, 0, 2)).reshape(buckets, heads)
    both_ids = jnp.concatenate([decoder_ids.reshape(-1), encoder_ids.reshape(-1)])
    both_ids = lax.all_gather(both_ids, "seq", axis=0, tiled=False)
    ids = both_ids[:, :local].reshape(length)
    enc_ids = both_ids[:, local:].reshape(keys)

    first_seen = counts_below(ids, ids)
    enc_first = counts_below(enc_ids, ids)
    enc_last = counts_below(enc_ids, ids + 1)
    blocks = length // BQ
    bk = 256
    self_rows = jnp.broadcast_to(first_seen[None], (8, length))
    cross_rows = jnp.concatenate([enc_first[None], enc_last[None], jnp.zeros((6, length), jnp.int32)])
    self_limits = jnp.stack(
        [first_seen[::BQ] // bk, (jnp.arange(blocks, dtype=jnp.int32) + 1) * (BQ // bk)]
    )
    cross_limits = jnp.stack([enc_first[::BQ] // bk, (enc_last[BQ - 1 :: BQ] + bk - 1) // bk])

    first_head = lax.axis_index("seq") * own
    table_mine = lax.dynamic_slice_in_dim(table.astype(f32), first_head, own, 1)
    near = rel_buckets[:REACH]
    onehot = (near[:, None] == jnp.arange(buckets, dtype=jnp.int32)[None, :]).astype(f32)
    bias = jnp.einsum("ln,ng->gl", onehot, table_mine, precision=HIGH)
    ext = jnp.concatenate(
        [jnp.full((own, BQ), MASKED, f32), bias, jnp.zeros((own, BQ), f32)], axis=1
    )

    stream = layer_in.astype(f32).reshape(rows, width)
    normed_first = norm_apply(stream, gain_first).astype(bf16)
    qkv_tok = jnp.einsum("td,dge->gte", normed_first, qkv_w, preferred_element_type=f32).astype(bf16)
    qkv = swap(qkv_tok).reshape(length, own * 3 * dh)
    out_self, self_t, self_lse = self_forward(self_limits, self_rows, ext, qkv)
    self_tok = swap(out_self.reshape(parts, local, own * dh))
    after_self = stream + jnp.einsum("gtc,gcd->td", self_tok, mix_self, preferred_element_type=f32)
    normed_second = norm_apply(after_self, gain_second).astype(bf16)
    query_tok = jnp.einsum("td,dgc->gtc", normed_second, query_w, preferred_element_type=f32).astype(bf16)
    enc_flat = encoder.reshape(seqs * enc_local, width)
    pairs_tok = jnp.einsum("td,dge->gte", enc_flat, pairs_w, preferred_element_type=f32).astype(bf16)
    query_cross = swap(query_tok).reshape(length, own * dh)
    pairs = swap(pairs_tok).reshape(keys, own * 2 * dh)
    out_cross, cross_t, cross_lse = cross_forward(cross_limits, cross_rows, query_cross, pairs)
    cross_tok = swap(out_cross.reshape(parts, local, own * dh))
    after_cross = after_self + jnp.einsum("gtc,gcd->td", cross_tok, mix_cross, preferred_element_type=f32)
    normed_third = norm_apply(after_cross, gain_third).astype(bf16)
    gate_up = jnp.dot(normed_third, inner_w, preferred_element_type=f32)
    hidden = gate_mix(gate_up).astype(bf16)
    layer_out = (
        (after_cross + jnp.dot(hidden, outer_w, preferred_element_type=f32)).astype(bf16).reshape(seqs, local, width)
    )

    grad_low = cotangent.reshape(rows, width)
    grad_outer = jnp.einsum("tf,td->fd", hidden, grad_low, preferred_element_type=f32)
    grad_hidden = jnp.einsum("td,fd->tf", grad_low, outer_w, preferred_element_type=f32)
    _, pull_mix = jax.vjp(gate_mix, gate_up)
    grad_gate_up = pull_mix(grad_hidden)[0].astype(bf16)
    grad_inner = jnp.einsum("td,tf->df", normed_third, grad_gate_up, preferred_element_type=f32)
    grad_third_in = jnp.einsum("tf,df->td", grad_gate_up, inner_w, preferred_element_type=f32)
    grad_from_third, grad_gain_third = norm_back(after_cross, gain_third, grad_third_in)
    grad_middle = grad_low.astype(f32) + grad_from_third
    middle_low, grad_inner, grad_outer = lax.optimization_barrier(
        (grad_middle.astype(bf16), grad_inner.astype(bf16), grad_outer.astype(bf16))
    )
    part_inner, part_outer = scatter(grad_inner), scatter(grad_outer)
    grad_mix_cross = jnp.einsum("gtc,td->gcd", cross_tok, middle_low, preferred_element_type=f32)
    grad_cross_tok = jnp.einsum("td,gcd->gtc", middle_low, mix_cross, preferred_element_type=f32).astype(bf16)
    grad_cross = swap(grad_cross_tok).reshape(length, own * dh)
    grad_query, grad_pairs = cross_backward(
        cross_limits, cross_rows, query_cross, pairs, grad_cross, cross_t, cross_lse
    )
    grad_query_tok = swap(grad_query.reshape(parts, local, own * dh))
    grad_pairs_tok = swap(grad_pairs.reshape(parts, enc_local, own * 2 * dh))
    grad_query_w = jnp.einsum("td,gtc->dgc", normed_second, grad_query_tok, preferred_element_type=f32)
    grad_second_in = jnp.einsum("gtc,dgc->td", grad_query_tok, query_w, preferred_element_type=f32)
    grad_pairs_w = jnp.einsum("td,gte->dge", enc_flat, grad_pairs_tok, preferred_element_type=f32)
    grad_encoder = jnp.einsum("gte,dge->td", grad_pairs_tok, pairs_w, preferred_element_type=f32).reshape(
        seqs, enc_local, width
    )
    grad_from_second, grad_gain_second = norm_back(after_self, gain_second, grad_second_in)
    grad_upper = grad_middle + grad_from_second
    upper_low = grad_upper.astype(bf16)
    grad_mix_self = jnp.einsum("gtc,td->gcd", self_tok, upper_low, preferred_element_type=f32)
    grad_self_tok = jnp.einsum("td,gcd->gtc", upper_low, mix_self, preferred_element_type=f32).astype(bf16)
    grad_self = swap(grad_self_tok).reshape(length, own * dh)
    grad_qkv, tile_sums = self_backward(self_limits, self_rows, ext, qkv, grad_self, self_t, self_lse)
    grad_qkv_tok = swap(grad_qkv.reshape(parts, local, own * 3 * dh))
    grad_qkv_w = jnp.einsum("td,gte->dge", normed_first, grad_qkv_tok, preferred_element_type=f32)
    grad_first_in = jnp.einsum("gte,dge->td", grad_qkv_tok, qkv_w, preferred_element_type=f32)
    grad_from_first, grad_gain_first = norm_back(stream, gain_first, grad_first_in)
    grad_layer_in = (grad_upper + grad_from_first).reshape(seqs, local, width)

    bucket_line = jnp.concatenate(
        [jnp.full((BQ,), -1, jnp.int32), near, jnp.full((BQ + bk,), -1, jnp.int32)]
    )
    by_tile = jnp.stack([bucket_line[t * bk + 1 : t * bk + 1 + BQ + bk] for t in range(tile_count(bk))])
    in_bucket = (by_tile[:, :, None] == jnp.arange(buckets, dtype=jnp.int32)).astype(f32)
    by_bucket = jnp.einsum("twn,gtw->ng", in_bucket, tile_sums, precision=HIGH)
    grad_table = lax.dynamic_update_slice_in_dim(jnp.zeros((buckets, heads), f32), by_bucket, first_head, 1)

    grad_mid = jnp.concatenate(
        [
            grad_mix_self.reshape(width, width).astype(bf16),
            grad_query_w.reshape(width, width).astype(bf16),
            grad_pairs_w.reshape(width, 2 * width).astype(bf16),
            grad_mix_cross.reshape(width, width).astype(bf16),
        ],
        axis=1,
    )
    part_mid = scatter(grad_mid)
    gains = jnp.concatenate(
        [g.reshape(-1, part) for g in (grad_gain_first, grad_gain_second, grad_gain_third)], axis=1
    )
    tables = jnp.transpose(grad_table.reshape(buckets, -1, table_own), (1, 0, 2)).reshape(-1, buckets * table_own)
    small_grads = lax.psum(jnp.concatenate([gains, tables], axis=1).astype(bf16), "fsdp")
    small_grads = lax.dynamic_index_in_dim(small_grads, lax.axis_index("fsdp"), 0, False)
    small_size = small_grads.shape[0]
    small_grads = jnp.pad(small_grads, (0, parts * 1024 - small_size)).reshape(parts * 8, 128)
    grad_qkv_w, part_inner, part_outer = lax.optimization_barrier(
        (grad_qkv_w.reshape(width, 3 * width).astype(bf16), part_inner, part_outer)
    )
    part_qkv = scatter(grad_qkv_w)
    total_inner, total_outer = over_seq([part_inner, part_outer], (2, 2), 0)
    total_inner, part_mid = lax.optimization_barrier((total_inner, part_mid))
    (total_mid,) = over_seq([part_mid], (4,), 1)
    part_qkv, small_grads, total_mid = lax.optimization_barrier((part_qkv, small_grads, total_mid))
    total_qkv, small_total = over_seq([part_qkv, small_grads], (4, 1), 2)
    total_qkv = total_qkv.astype(f32).reshape(-1, heads, 3 * dh)
    total_inner, total_outer, total_mid = (v.astype(f32) for v in (total_inner, total_outer, total_mid))
    total_mix_self, total_query = total_mid[:, :width], total_mid[:, width : 2 * width]
    total_pairs = total_mid[:, 2 * width : 4 * width].reshape(-1, heads, 2 * dh)
    total_mix_cross = total_mid[:, 4 * width :]
    mine = small_total.reshape(-1)[:small_size].astype(f32)
    total_gain_first, total_gain_second, total_gain_third = (mine[i * part : (i + 1) * part] for i in range(3))
    total_table = mine[3 * part :].reshape(buckets, table_own)
    return (
        layer_out, grad_layer_in, grad_encoder, total_gain_first, total_qkv, total_mix_self, total_table,
        total_gain_second, total_query, total_pairs, total_mix_cross, total_gain_third, total_inner, total_outer,
    )


def solution(mesh):
    in_specs = (
        P("fsdp", "seq", None), P("fsdp", "seq", None), P("fsdp", "seq"), P("fsdp", "seq"), P(),
        P("fsdp"), P("fsdp", None, None), P("fsdp", None), P(None, "fsdp"), P("fsdp"), P("fsdp", None),
        P("fsdp", None, None), P("fsdp", None), P("fsdp"), P("fsdp", None), P("fsdp", None),
        P("fsdp", "seq", None),
    )
    out_specs = (
        P("fsdp", "seq", None), P("fsdp", "seq", None), P("fsdp", "seq", None), P("fsdp"), P("fsdp", None, None),
        P("fsdp", None), P(None, "fsdp"), P("fsdp"), P("fsdp", None), P("fsdp", None, None), P("fsdp", None),
        P("fsdp"), P("fsdp", None), P("fsdp", None),
    )
    return jax.shard_map(shards, mesh=mesh, in_specs=in_specs, out_specs=out_specs, check_vma=False)
```

```python
import functools

import jax
import jax.numpy as jnp
from jax import lax
from jax.experimental import pallas as pl
from jax.experimental.pallas import tpu as pltpu
from jax.sharding import PartitionSpec as P

EPS = 1e-06
HIGH = lax.Precision.HIGHEST
MASKED = -1e30
DOCS = 4

BQ = 256
REACH = 1024


def blk(index, size):
    return pl.ds(pl.multiple_of(index * size, size), size)


def turn(value):
    return jnp.transpose(value.astype(jnp.float32), (1, 0))


def bias_tiles(ext_ref, tile_ref, own, bk):
    span = BQ + bk
    for h in range(own):
        for t in range(tile_ref.shape[1]):
            first = t * bk
            line = jnp.broadcast_to(ext_ref[h : h + 1, first : first + span], (bk, span))
            tile_ref[h, t] = pltpu.roll(line, 0, 1, stride=1, stride_axis=0)[:, bk:]


def tile_count(bk):
    return BQ // bk + REACH // bk


def unpack(ref, own, width, picks, flips, base):
    block = 256

    def one(b, _):
        rows = blk(b, block)
        value = ref[rows, :]
        if flips:
            flat = turn(value).astype(jnp.bfloat16)
            for target, piece in flips:
                for h in range(own):
                    at = h * width + piece * 64
                    target[base + h, :, rows] = flat[at : at + 64]
        for target, piece in picks:
            for h in range(own):
                at = h * width + piece * 64
                target[base + h, rows, :] = value[:, at : at + 64]
        return 0

    lax.fori_loop(0, ref.shape[0] // block, one, 0)


def dot(a, b):
    return jnp.dot(a, b, preferred_element_type=jnp.float32)


def score(own_index, key_tile, query_t, tile_ref, t, low, high, first_key):
    value = dot(key_tile, query_t)
    place = lax.broadcasted_iota(jnp.int32, value.shape, 0)
    keep = place >= low - first_key
    if high is not None:
        keep = keep & (place < high - first_key)
    else:
        value = value + tile_ref[own_index, t]
    return jnp.where(keep, value, MASKED)


def forward_body(own, bk, causal, lim_ref, rows_ref, q_t, k_rows, v_t, tile_ref, o_ref, ot_ref, lse_ref):
    length = o_ref.shape[0]

    def q_block(i, _):
        cols = blk(i, BQ)
        queries = [q_t[h, :, cols] for h in range(own)]
        low = rows_ref[0:1, cols]
        high = None if causal else rows_ref[1:2, cols]

        def k_block(j, carry):
            keys = blk(j, bk)
            t = i * (BQ // bk) - j + (BQ // bk - 1)
            out = []
            for h in range(own):
                top, total, acc = carry[h]
                s = score(h, k_rows[h, keys, :], queries[h], tile_ref, t, low, high, j * bk)
                new_top = jnp.maximum(top, jnp.max(s, axis=0, keepdims=True))
                p = jnp.exp(s - new_top)
                scale = jnp.exp(top - new_top)
                total = total * scale + jnp.sum(p, axis=0, keepdims=True)
                acc = acc * scale + dot(v_t[h, :, keys], p.astype(jnp.bfloat16))
                out.append((new_top, total, acc))
            return tuple(out)

        start = tuple(
            (
                jnp.full((1, BQ), MASKED, jnp.float32),
                jnp.zeros((1, BQ), jnp.float32),
                jnp.zeros((64, BQ), jnp.float32),
            )
            for _ in range(own)
        )
        ends = lax.fori_loop(lim_ref[0, i], lim_ref[1, i], k_block, start)
        for h in range(own):
            top, total, acc = ends[h]
            ot_ref[h * 64 : h * 64 + 64, cols] = acc / total
            lse_ref[h : h + 1, cols] = top + jnp.log(total)
        o_ref[cols, :] = turn(ot_ref[:, cols]).astype(jnp.bfloat16)
        return 0

    lax.fori_loop(0, length // BQ, q_block, 0)


def self_forward_kernel(own, bk, lim_ref, rows_ref, ext_ref, x_ref, o_ref, ot_ref, lse_ref, q_t, k_rows, v_t, tile_ref):
    bias_tiles(ext_ref, tile_ref, own, bk)
    unpack(x_ref, own, 192, [(k_rows, 1)], [(q_t, 0), (v_t, 2)], 0)
    forward_body(own, bk, True, lim_ref, rows_ref, q_t, k_rows, v_t, tile_ref, o_ref, ot_ref, lse_ref)


def cross_forward_kernel(own, bk, lim_ref, rows_ref, q_ref, kv_ref, o_ref, ot_ref, lse_ref, q_t, k_rows, v_t):
    unpack(q_ref, own, 64, [], [(q_t, 0)], 0)
    unpack(kv_ref, own, 128, [(k_rows, 0)], [(v_t, 1)], 0)
    forward_body(own, bk, False, lim_ref, rows_ref, q_t, k_rows, v_t, None, o_ref, ot_ref, lse_ref)


def backward_body(
    own, bk, causal, lim_ref, rows_ref, do_ref, ot_ref, lse_ref,
    q_t, q_rows, k_t, k_rows, v_rows, do_t, do_rows, tile_ref, sum_ref, dq_t, dk, dv,
):
    length = do_ref.shape[0]
    dk[...] = jnp.zeros_like(dk)
    dv[...] = jnp.zeros_like(dv)
    if causal:
        sum_ref[...] = jnp.zeros_like(sum_ref)

    def q_block(i, _):
        cols = blk(i, BQ)
        low = rows_ref[0:1, cols]
        high = None if causal else rows_ref[1:2, cols]
        per_head = []
        for h in range(own):
            grad_t = do_t[h, :, cols]
            delta = jnp.sum(
                grad_t.astype(jnp.float32) * ot_ref[h * 64 : h * 64 + 64, cols], axis=0, keepdims=True
            )
            per_head.append((q_t[h, :, cols], grad_t, delta, lse_ref[h : h + 1, cols]))

        def k_block(j, carry):
            keys = blk(j, bk)
            t = i * (BQ // bk) - j + (BQ // bk - 1)
            out = []
            for h in range(own):
                query_t, grad_t, delta, lse = per_head[h]
                s = score(h, k_rows[h, keys, :], query_t, tile_ref, t, low, high, j * bk)
                p = jnp.exp(s - lse)
                dp = dot(v_rows[h, keys, :], grad_t)
                ds = (p * (dp - delta)).astype(jnp.bfloat16)
                dv[h, keys, :] += dot(p.astype(jnp.bfloat16), do_rows[h, cols, :])
                dk[h, keys, :] += dot(ds, q_rows[h, cols, :])
                if causal:
                    sum_ref[h, t] += ds.astype(jnp.float32)
                out.append(carry[h] + dot(k_t[h, :, keys], ds))
            return tuple(out)

        ends = lax.fori_loop(
            lim_ref[0, i],
            lim_ref[1, i],
            k_block,
            tuple(jnp.zeros((64, BQ), jnp.float32) for _ in range(own)),
        )
        for h in range(own):
            dq_t[h * 64 : h * 64 + 64, cols] = ends[h]
        return 0

    lax.fori_loop(0, length // BQ, q_block, 0)


def diagonal_sums(sum_ref, u_ref, own, bk):
    flip = (
        lax.broadcasted_iota(jnp.int32, (bk, bk), 0) + lax.broadcasted_iota(jnp.int32, (bk, bk), 1) == bk - 1
    ).astype(jnp.float32)
    for h in range(own):
        for t in range(sum_ref.shape[1]):
            upside = jnp.dot(flip, sum_ref[h, t], precision=HIGH, preferred_element_type=jnp.float32)
            wide = jnp.concatenate([upside, jnp.zeros((bk, bk), jnp.float32)], axis=1)
            aligned = pltpu.roll(wide, 0, 1, stride=1, stride_axis=0)
            u_ref[h, t : t + 1, :] = jnp.sum(aligned, axis=0, keepdims=True)


def self_backward_kernel(
    own, bk, lim_ref, rows_ref, ext_ref, x_ref, do_ref, ot_ref, lse_ref, dx_ref, u_ref,
    q_t, q_rows, k_t, k_rows, v_rows, do_t, do_rows, tile_ref, sum_ref, dq_t, dk, dv,
):
    bias_tiles(ext_ref, tile_ref, own, bk)
    unpack(x_ref, own, 192, [(q_rows, 0), (k_rows, 1), (v_rows, 2)], [(q_t, 0), (k_t, 1)], 0)
    unpack(do_ref, own, 64, [(do_rows, 0)], [(do_t, 0)], 0)
    backward_body(
        own, bk, True, lim_ref, rows_ref, do_ref, ot_ref, lse_ref,
        q_t, q_rows, k_t, k_rows, v_rows, do_t, do_rows, tile_ref, sum_ref, dq_t, dk, dv,
    )
    diagonal_sums(sum_ref, u_ref, own, bk)

    def pack(b, _):
        rows = blk(b, 256)
        dq = turn(dq_t[:, rows])
        pieces = []
        for h in range(own):
            pieces += [dq[:, h * 64 : h * 64 + 64], dk[h, rows, :], dv[h, rows, :]]
        dx_ref[rows, :] = jnp.concatenate(pieces, axis=1).astype(jnp.bfloat16)
        return 0

    lax.fori_loop(0, x_ref.shape[0] // 256, pack, 0)


def cross_backward_kernel(
    own, bk, lim_ref, rows_ref, q_ref, kv_ref, do_ref, ot_ref, lse_ref, dq_ref, dkv_ref,
    q_t, q_rows, k_t, k_rows, v_rows, do_t, do_rows, dq_t, dk, dv,
):
    unpack(q_ref, own, 64, [(q_rows, 0)], [(q_t, 0)], 0)
    unpack(kv_ref, own, 128, [(k_rows, 0), (v_rows, 1)], [(k_t, 0)], 0)
    unpack(do_ref, own, 64, [(do_rows, 0)], [(do_t, 0)], 0)
    backward_body(
        own, bk, False, lim_ref, rows_ref, do_ref, ot_ref, lse_ref,
        q_t, q_rows, k_t, k_rows, v_rows, do_t, do_rows, None, None, dq_t, dk, dv,
    )

    def pack_q(b, _):
        rows = blk(b, 256)
        dq_ref[rows, :] = turn(dq_t[:, rows]).astype(jnp.bfloat16)
        return 0

    def pack_kv(b, _):
        rows = blk(b, 256)
        pieces = []
        for h in range(own):
            pieces += [dk[h, rows, :], dv[h, rows, :]]
        dkv_ref[rows, :] = jnp.concatenate(pieces, axis=1).astype(jnp.bfloat16)
        return 0

    lax.fori_loop(0, q_ref.shape[0] // 256, pack_q, 0)
    lax.fori_loop(0, kv_ref.shape[0] // 256, pack_kv, 0)


SMEM = pl.BlockSpec(memory_space=pltpu.SMEM)
VMEM = pl.BlockSpec(memory_space=pltpu.VMEM)
bf16, f32 = jnp.bfloat16, jnp.float32


def call(body, name, operands, outs, scratch, flops):
    size = sum(v.size * v.dtype.itemsize for v in operands)
    return pl.pallas_call(
        body,
        name=name,
        out_shape=[jax.ShapeDtypeStruct(s, d) for s, d in outs],
        in_specs=[SMEM] + [VMEM] * (len(operands) - 1),
        out_specs=[VMEM] * len(outs),
        scratch_shapes=[pltpu.VMEM(s, d) for s, d in scratch],
        compiler_params=pltpu.CompilerParams(vmem_limit_bytes=40 << 20),
        cost_estimate=pl.CostEstimate(flops=flops, bytes_accessed=2 * size, transcendentals=flops // 256),
    )(*operands)


def self_forward(limits, rows, ext, x, bk=256):
    length, own = x.shape[0], x.shape[1] // 192
    return call(
        functools.partial(self_forward_kernel, own, bk),
        "self_forward",
        [limits, rows, ext, x],
        [((length, own * 64), bf16), ((own * 64, length), f32), ((own, length), f32)],
        [
            ((own, 64, length), bf16),
            ((own, length, 64), bf16),
            ((own, 64, length), bf16),
            ((own, tile_count(bk), bk, BQ), f32),
        ],
        length * length * own * 64,
    )


def cross_forward(limits, rows, q, kv, bk=256):
    length, own, keys = q.shape[0], q.shape[1] // 64, kv.shape[0]
    return call(
        functools.partial(cross_forward_kernel, own, bk),
        "cross_forward",
        [limits, rows, q, kv],
        [((length, own * 64), bf16), ((own * 64, length), f32), ((own, length), f32)],
        [((own, 64, length), bf16), ((own, keys, 64), bf16), ((own, 64, keys), bf16)],
        length * keys * own * 128,
    )


def self_backward(limits, rows, ext, x, grad, o_t, lse, bk=256):
    length, own = x.shape[0], x.shape[1] // 192
    return call(
        functools.partial(self_backward_kernel, own, bk),
        "self_backward",
        [limits, rows, ext, x, grad, o_t, lse],
        [((length, own * 192), bf16), ((own, tile_count(bk), BQ + bk), f32)],
        [
            ((own, 64, length), bf16),
            ((own, length, 64), bf16),
            ((own, 64, length), bf16),
            ((own, length, 64), bf16),
            ((own, length, 64), bf16),
            ((own, 64, length), bf16),
            ((own, length, 64), bf16),
            ((own, tile_count(bk), bk, BQ), f32),
            ((own, tile_count(bk), bk, BQ), f32),
            ((own * 64, length), f32),
            ((own, length, 64), f32),
            ((own, length, 64), f32),
        ],
        length * length * own * 160,
    )


def cross_backward(limits, rows, q, kv, grad, o_t, lse, bk=256):
    length, own, keys = q.shape[0], q.shape[1] // 64, kv.shape[0]
    return call(
        functools.partial(cross_backward_kernel, own, bk),
        "cross_backward",
        [limits, rows, q, kv, grad, o_t, lse],
        [((length, own * 64), bf16), ((keys, own * 128), bf16)],
        [
            ((own, 64, length), bf16),
            ((own, length, 64), bf16),
            ((own, 64, keys), bf16),
            ((own, keys, 64), bf16),
            ((own, keys, 64), bf16),
            ((own, 64, length), bf16),
            ((own, length, 64), bf16),
            ((own * 64, length), f32),
            ((own, keys, 64), f32),
            ((own, keys, 64), f32),
        ],
        length * keys * own * 320,
    )


MESH = pl.DeviceIdType.MESH


def ring_place(index, n):
    z, x = index // 2, index % 2
    return z + x * (n - 1 - 2 * z)


def ring_index(place, n):
    x = place // (n // 2)
    z = place + x * (n - 1 - 2 * place)
    return 2 * z + x


def ring_cut(shape, split, n):
    rows, cols = shape[0] // n, shape[1]
    return (rows, cols // split) if split > 0 else (rows // -split, cols)


def ring_kernel(n, splits, *refs):
    count = len(splits)
    x_refs, y_refs, slots = refs[:count], refs[count : 2 * count], refs[2 * count : 3 * count]
    send_sem, recv_sem = refs[3 * count :]
    place = ring_place(lax.axis_index("seq"), n)
    right = ring_index((place + 1) % n, n)
    left = ring_index((place + n - 1) % n, n)
    barrier = pltpu.get_barrier_semaphore()
    for neighbour in (left, right):
        pl.semaphore_signal(barrier, inc=1, device_id={"seq": neighbour}, device_id_type=MESH)
    pl.semaphore_wait(barrier, 2)

    streams = []
    for k in range(count):
        for piece in range(abs(splits[k])):
            streams.append((k, piece, piece % 2))

    def window(ref, k, piece, chunk):
        whole = x_refs[k].shape[0] // n
        rows, cols = ring_cut(x_refs[k].shape, splits[k], n)
        if splits[k] > 0:
            return ref.at[pl.ds(chunk * whole, rows), pl.ds(piece * cols, cols)]
        return ref.at[pl.ds(chunk * whole + piece * rows, rows), :]

    def copy(number, step, src, dst, down):
        return pltpu.make_async_remote_copy(
            src_ref=src,
            dst_ref=dst,
            send_sem=send_sem.at[number, step],
            recv_sem=recv_sem.at[number, step],
            device_id={"seq": left if down else right},
            device_id_type=MESH,
        )

    def chunk_at(down, step):
        return (place + 1 + step) % n if down else (place + 2 * n - 1 - step) % n

    copies = {}

    def start(number, step, src, dst, down):
        copies[number, step] = copy(number, step, src, dst, down)
        copies[number, step].start()

    for number, (k, piece, down) in enumerate(streams):
        start(number, 0, window(x_refs[k], k, piece, place), window(slots[k], k, piece, 0), down)
    for step in range(n - 1):
        for number, (k, piece, down) in enumerate(streams):
            copies[number, step].wait_recv()
            chunk = chunk_at(down, step)
            mine = window(x_refs[k], k, piece, chunk)
            landed = window(slots[k], k, piece, step)
            total = landed[...].astype(jnp.float32) + mine[...].astype(jnp.float32)
            if step < n - 2:
                landed[...] = total.astype(jnp.bfloat16)
                start(number, step + 1, landed, window(slots[k], k, piece, step + 1), down)
            else:
                done = window(y_refs[k], k, piece, chunk)
                done[...] = total.astype(jnp.bfloat16)
                start(number, n - 1, done, done, down)
    for step in range(n - 1):
        for number, (k, piece, down) in enumerate(streams):
            copies[number, n - 1 + step].wait_recv()
            if step < n - 2:
                chunk = chunk_at(down, n - 1 + step)
                done = window(y_refs[k], k, piece, chunk)
                start(number, n + step, done, done, down)
    for one in copies.values():
        one.wait_send()


def ring_total(arrays, splits, ident):
    n = lax.axis_size("seq")
    size = sum(v.size * 2 for v in arrays)
    streams = sum(abs(s) for s in splits)
    return pl.pallas_call(
        functools.partial(ring_kernel, n, splits),
        name="ring_total",
        out_shape=[jax.ShapeDtypeStruct(v.shape, jnp.bfloat16) for v in arrays],
        in_specs=[pl.BlockSpec(memory_space=pltpu.VMEM)] * len(arrays),
        out_specs=[pl.BlockSpec(memory_space=pltpu.VMEM)] * len(arrays),
        scratch_shapes=[pltpu.VMEM((v.shape[0] // n * (n - 1), v.shape[1]), jnp.bfloat16) for v in arrays]
        + [pltpu.SemaphoreType.DMA((streams, 2 * n - 2)), pltpu.SemaphoreType.DMA((streams, 2 * n - 2))],
        compiler_params=pltpu.CompilerParams(
            collective_id=ident, has_side_effects=True, vmem_limit_bytes=48 << 20
        ),
        cost_estimate=pl.CostEstimate(flops=size, bytes_accessed=60 * size, transcendentals=0),
    )(*arrays)


def team(n):
    s, f = lax.axis_index("seq"), lax.axis_index("fsdp")
    half = s // (n // 2)
    away = (half + f) % 2
    return f // 2, half, (s + away * (n // 2)) % n


def swap_kernel(n, count, *refs):
    x_refs, y_refs = refs[:count], refs[count : 2 * count]
    send_sem, recv_sem, own_sem = refs[2 * count :]
    pair, half, rank = team(n)

    def device(other):
        away = (other // (n // 2) + half) % 2
        return {"seq": (other + away * (n // 2)) % n, "fsdp": 2 * pair + (half + away) % 2}

    barrier = pltpu.get_barrier_semaphore()
    for j in range(1, n):
        pl.semaphore_signal(barrier, inc=1, device_id=device((rank + j) % n), device_id_type=MESH)
    pl.semaphore_wait(barrier, n - 1)
    copies = []
    for k in range(count):
        for j in range(1, n):
            other = (rank + j) % n
            one = pltpu.make_async_remote_copy(
                src_ref=x_refs[k].at[other],
                dst_ref=y_refs[k].at[rank],
                send_sem=send_sem.at[k, j],
                recv_sem=recv_sem.at[k, j],
                device_id=device(other),
                device_id_type=MESH,
            )
            one.start()
            copies.append(one)
    own = [
        pltpu.make_async_copy(x_refs[k].at[rank], y_refs[k].at[rank], own_sem.at[k]) for k in range(count)
    ]
    for one in own:
        one.start()
    for one in copies + own:
        one.wait()


def swap(arrays, ident):
    n = lax.axis_size("seq")
    count = len(arrays)
    size = sum(v.size * 2 for v in arrays)
    return pl.pallas_call(
        functools.partial(swap_kernel, n, count),
        name="swap",
        out_shape=[jax.ShapeDtypeStruct(v.shape, v.dtype) for v in arrays],
        in_specs=[pl.BlockSpec(memory_space=pl.ANY)] * count,
        out_specs=[pl.BlockSpec(memory_space=pl.ANY)] * count,
        scratch_shapes=[
            pltpu.SemaphoreType.DMA((count, n)),
            pltpu.SemaphoreType.DMA((count, n)),
            pltpu.SemaphoreType.DMA((count,)),
        ],
        compiler_params=pltpu.CompilerParams(collective_id=ident, has_side_effects=True),
        cost_estimate=pl.CostEstimate(flops=0, bytes_accessed=30 * size, transcendentals=0),
    )(*arrays)


def norm_apply(value, gain):
    return value * lax.rsqrt(jnp.mean(value * value, axis=-1, keepdims=True) + EPS) * gain


def norm_back(value, gain, grad):
    _, pull = jax.vjp(norm_apply, value, gain)
    return pull(grad)


def gate_mix(gate, up):
    return jax.nn.gelu(gate, approximate=True) * up


def counts_below(ids, values):
    total = jnp.zeros_like(values)
    for doc in range(DOCS):
        total = total + jnp.where(values > doc, jnp.sum((ids == doc).astype(jnp.int32)), 0)
    return total


def change_home(value):
    n, fan = lax.axis_size("seq"), lax.axis_size("fsdp")
    pairs = []
    for s in range(n):
        for f in range(fan):
            away = (s // (n // 2) + f) % 2
            target = ((s + n // 2) % n, f ^ 1) if away else (s, f)
            pairs.append((s * fan + f, target[0] * fan + target[1]))
    return lax.ppermute(value, ("seq", "fsdp"), pairs)


def spread(blocks):
    return lax.all_to_all(blocks, "fsdp", split_axis=0, concat_axis=0, tiled=True)


def scatter(grad):
    return lax.psum_scatter(grad, "fsdp", scatter_dimension=0, tiled=True)


def over_seq(arrays, splits, ident):
    n = lax.axis_size("seq")
    if all(v.shape[0] % (8 * n) == 0 and v.shape[1] % (128 * s) == 0 for v, s in zip(arrays, splits)):
        return ring_total(arrays, splits, ident)
    return [lax.psum(v, "seq") for v in arrays]


def shards(
    layer_in, encoder, decoder_ids, encoder_ids, rel_buckets,
    norm_self, self_qkv, self_out, rel_table, norm_cross, cross_q, cross_kv, cross_out, norm_ff, ff_in, ff_out,
    cotangent,
):
    seqs, local, width = layer_in.shape
    enc_local = encoder.shape[1]
    parts = lax.axis_size("seq")
    heads = self_qkv.shape[1]
    dh = self_qkv.shape[2] // 3
    own = heads // parts
    rows = seqs * local
    buckets, table_own = rel_table.shape
    length, keys = local * parts, enc_local * parts
    gather = lambda v: lax.all_gather(v, "fsdp", axis=0, tiled=True)

    qkv_w = gather(self_qkv).reshape(width, parts, own * 3 * dh)
    middle = gather(jnp.concatenate([self_out, cross_q, cross_out], axis=1))
    pairs_w = gather(cross_kv).reshape(width, parts, own * 2 * dh)
    fan = lax.axis_size("fsdp")
    units = ff_in.shape[1] // (2 * fan)
    inner_mine = spread(jnp.transpose(ff_in.reshape(-1, 2, fan, units), (2, 1, 0, 3)))
    gate_w, up_w = (inner_mine[:, i].reshape(width, units) for i in range(2))
    mix_self = middle[:, :width].reshape(parts, own * dh, width)
    query_w = middle[:, width : 2 * width].reshape(width, parts, own * dh)
    mix_cross = middle[:, 2 * width :].reshape(parts, own * dh, width)
    small = jnp.concatenate([norm_self, norm_cross, norm_ff, rel_table.reshape(-1)])
    small = lax.all_gather(small, "fsdp", axis=0, tiled=False)
    part = norm_self.shape[0]
    gain_first, gain_second, gain_third = (
        small[:, i * part : (i + 1) * part].reshape(width).astype(f32) for i in range(3)
    )
    table = jnp.transpose(small[:, 3 * part :].reshape(-1, buckets, table_own), (1, 0, 2)).reshape(buckets, heads)
    both_ids = jnp.concatenate([decoder_ids.reshape(-1), encoder_ids.reshape(-1)])
    both_ids = lax.all_gather(both_ids, ("seq", "fsdp"), axis=0, tiled=False).reshape(parts, fan, -1)
    pair, half, rank = team(parts)
    both_ids = lax.dynamic_index_in_dim(both_ids, 2 * pair + half, 1, False)
    qkv_w, both_ids, small = lax.optimization_barrier((qkv_w, both_ids, small))
    ids = both_ids[:, :local].reshape(length)
    enc_ids = both_ids[:, local:].reshape(keys)

    first_seen = counts_below(ids, ids)
    enc_first = counts_below(enc_ids, ids)
    enc_last = counts_below(enc_ids, ids + 1)
    blocks = length // BQ
    bk = 256
    self_rows = jnp.broadcast_to(first_seen[None], (8, length))
    cross_rows = jnp.concatenate([enc_first[None], enc_last[None], jnp.zeros((6, length), jnp.int32)])
    self_limits = jnp.stack(
        [first_seen[::BQ] // bk, (jnp.arange(blocks, dtype=jnp.int32) + 1) * (BQ // bk)]
    )
    cross_limits = jnp.stack([enc_first[::BQ] // bk, (enc_last[BQ - 1 :: BQ] + bk - 1) // bk])

    first_head = rank * own
    table_mine = lax.dynamic_slice_in_dim(table.astype(f32), first_head, own, 1)
    near = rel_buckets[:REACH]
    onehot = (near[:, None] == jnp.arange(buckets, dtype=jnp.int32)[None, :]).astype(f32)
    bias = jnp.einsum("ln,ng->gl", onehot, table_mine, precision=HIGH)
    ext = jnp.concatenate(
        [jnp.full((own, BQ), MASKED, f32), bias, jnp.zeros((own, BQ), f32)], axis=1
    )

    stream = change_home(layer_in.reshape(rows, width)).astype(f32)
    others = change_home(jnp.concatenate([cotangent.reshape(rows, width), encoder.reshape(-1, width)]))
    grad_low, enc_flat = others[:rows], others[rows:]
    normed_first = norm_apply(stream, gain_first).astype(bf16)
    qkv_tok = jnp.einsum("td,dge->gte", normed_first, qkv_w, preferred_element_type=f32).astype(bf16)
    (qkv,) = swap([qkv_tok], 10)
    qkv = qkv.reshape(length, own * 3 * dh)
    out_self, self_t, self_lse = self_forward(self_limits, self_rows, ext, qkv)
    (self_tok,) = swap([out_self.reshape(parts, local, own * dh)], 11)
    after_self = stream + jnp.einsum("gtc,gcd->td", self_tok, mix_self, preferred_element_type=f32)
    normed_second = norm_apply(after_self, gain_second).astype(bf16)
    query_tok = jnp.einsum("td,dgc->gtc", normed_second, query_w, preferred_element_type=f32).astype(bf16)
    pairs_tok = jnp.einsum("td,dge->gte", enc_flat, pairs_w, preferred_element_type=f32).astype(bf16)
    query_cross, pairs = swap([query_tok, pairs_tok], 12)
    query_cross, pairs = query_cross.reshape(length, own * dh), pairs.reshape(keys, own * 2 * dh)
    out_cross, cross_t, cross_lse = cross_forward(cross_limits, cross_rows, query_cross, pairs)
    (cross_tok,) = swap([out_cross.reshape(parts, local, own * dh)], 11)
    after_cross = after_self + jnp.einsum("gtc,gcd->td", cross_tok, mix_cross, preferred_element_type=f32)
    normed_third = norm_apply(after_cross, gain_third).astype(bf16)
    normed_group = gather(normed_third)
    gate = jnp.dot(normed_group, gate_w, preferred_element_type=f32)
    up = jnp.dot(normed_group, up_w, preferred_element_type=f32)
    hidden = gate_mix(gate, up).astype(bf16)
    outer_part = jnp.dot(hidden, ff_out, preferred_element_type=f32).astype(bf16)
    layer_out = (after_cross + scatter(outer_part).astype(f32)).astype(bf16)
    layer_out = change_home(layer_out).reshape(seqs, local, width)

    grad_group = gather(grad_low)
    part_outer = jnp.einsum("tf,td->fd", hidden, grad_group, preferred_element_type=f32).astype(bf16)
    grad_hidden = jnp.einsum("td,fd->tf", grad_group, ff_out, preferred_element_type=f32)
    _, pull_mix = jax.vjp(gate_mix, gate, up)
    grad_gate, grad_up = (g.astype(bf16) for g in pull_mix(grad_hidden))
    grad_third_in = jnp.einsum("tf,df->td", grad_gate, gate_w, preferred_element_type=f32) + jnp.einsum(
        "tf,df->td", grad_up, up_w, preferred_element_type=f32
    )
    grad_third_in = scatter(grad_third_in.astype(bf16))
    grad_inner = [
        jnp.einsum("td,tf->df", normed_group, g, preferred_element_type=f32).astype(bf16).reshape(fan, -1, units)
        for g in (grad_gate, grad_up)
    ]
    grad_third_in, grad_inner, part_outer = lax.optimization_barrier(
        (grad_third_in, jnp.stack(grad_inner, axis=1), part_outer)
    )
    part_inner = jnp.transpose(spread(grad_inner), (2, 1, 0, 3)).reshape(-1, 2 * fan * units)
    grad_third_in = grad_third_in.astype(f32)
    grad_from_third, grad_gain_third = norm_back(after_cross, gain_third, grad_third_in)
    grad_middle = grad_low.astype(f32) + grad_from_third
    middle_low = grad_middle.astype(bf16)
    grad_mix_cross = jnp.einsum("gtc,td->gcd", cross_tok, middle_low, preferred_element_type=f32)
    grad_cross_tok = jnp.einsum("td,gcd->gtc", middle_low, mix_cross, preferred_element_type=f32).astype(bf16)
    (grad_cross,) = swap([grad_cross_tok], 11)
    grad_cross = grad_cross.reshape(length, own * dh)
    grad_query, grad_pairs = cross_backward(
        cross_limits, cross_rows, query_cross, pairs, grad_cross, cross_t, cross_lse
    )
    grad_query_tok, grad_pairs_tok = swap(
        [grad_query.reshape(parts, local, own * dh), grad_pairs.reshape(parts, enc_local, own * 2 * dh)], 12
    )
    grad_query_w = jnp.einsum("td,gtc->dgc", normed_second, grad_query_tok, preferred_element_type=f32)
    grad_second_in = jnp.einsum("gtc,dgc->td", grad_query_tok, query_w, preferred_element_type=f32)
    grad_pairs_w = jnp.einsum("td,gte->dge", enc_flat, grad_pairs_tok, preferred_element_type=f32)
    grad_encoder = jnp.einsum("gte,dge->td", grad_pairs_tok, pairs_w, preferred_element_type=f32)
    grad_encoder = change_home(grad_encoder.astype(bf16)).astype(f32).reshape(seqs, enc_local, width)
    grad_from_second, grad_gain_second = norm_back(after_self, gain_second, grad_second_in)
    grad_upper = grad_middle + grad_from_second
    upper_low = grad_upper.astype(bf16)
    grad_mix_self = jnp.einsum("gtc,td->gcd", self_tok, upper_low, preferred_element_type=f32)
    grad_self_tok = jnp.einsum("td,gcd->gtc", upper_low, mix_self, preferred_element_type=f32).astype(bf16)
    (grad_self,) = swap([grad_self_tok], 11)
    grad_self = grad_self.reshape(length, own * dh)
    grad_qkv, tile_sums = self_backward(self_limits, self_rows, ext, qkv, grad_self, self_t, self_lse)
    (grad_qkv_tok,) = swap([grad_qkv.reshape(parts, local, own * 3 * dh)], 10)
    grad_qkv_w = jnp.einsum("td,gte->dge", normed_first, grad_qkv_tok, preferred_element_type=f32)
    grad_first_in = jnp.einsum("gte,dge->td", grad_qkv_tok, qkv_w, preferred_element_type=f32)
    grad_from_first, grad_gain_first = norm_back(stream, gain_first, grad_first_in)
    grad_layer_in = change_home((grad_upper + grad_from_first).astype(bf16)).astype(f32)
    grad_layer_in = grad_layer_in.reshape(seqs, local, width)

    bucket_line = jnp.concatenate(
        [jnp.full((BQ,), -1, jnp.int32), near, jnp.full((BQ + bk,), -1, jnp.int32)]
    )
    by_tile = jnp.stack([bucket_line[t * bk + 1 : t * bk + 1 + BQ + bk] for t in range(tile_count(bk))])
    in_bucket = (by_tile[:, :, None] == jnp.arange(buckets, dtype=jnp.int32)).astype(f32)
    by_bucket = jnp.einsum("twn,gtw->ng", in_bucket, tile_sums, precision=HIGH)
    grad_table = lax.dynamic_update_slice_in_dim(jnp.zeros((buckets, heads), f32), by_bucket, first_head, 1)

    grad_mid = jnp.concatenate(
        [
            grad_mix_self.reshape(width, width).astype(bf16),
            grad_query_w.reshape(width, width).astype(bf16),
            grad_pairs_w.reshape(width, 2 * width).astype(bf16),
            grad_mix_cross.reshape(width, width).astype(bf16),
        ],
        axis=1,
    )
    part_mid = scatter(grad_mid)
    gains = jnp.concatenate(
        [g.reshape(-1, part) for g in (grad_gain_first, grad_gain_second, grad_gain_third)], axis=1
    )
    tables = jnp.transpose(grad_table.reshape(buckets, -1, table_own), (1, 0, 2)).reshape(-1, buckets * table_own)
    small_grads = lax.psum(jnp.concatenate([gains, tables], axis=1).astype(bf16), "fsdp")
    small_grads = lax.dynamic_index_in_dim(small_grads, lax.axis_index("fsdp"), 0, False)
    small_size = small_grads.shape[0]
    small_grads = jnp.pad(small_grads, (0, parts * 1024 - small_size)).reshape(parts * 8, 128)
    grad_qkv_w, part_inner, part_outer = lax.optimization_barrier(
        (grad_qkv_w.reshape(width, 3 * width).astype(bf16), part_inner, part_outer)
    )
    part_qkv = scatter(grad_qkv_w)
    total_inner, total_outer = over_seq([part_inner, part_outer], (2, 2), 0)
    total_inner, part_mid = lax.optimization_barrier((total_inner, part_mid))
    (total_mid,) = over_seq([part_mid], (4,), 1)
    part_qkv, small_grads, total_mid = lax.optimization_barrier((part_qkv, small_grads, total_mid))
    total_qkv, small_total = over_seq([part_qkv, small_grads], (4, 1), 2)
    total_qkv = total_qkv.astype(f32).reshape(-1, heads, 3 * dh)
    total_inner, total_outer, total_mid = (v.astype(f32) for v in (total_inner, total_outer, total_mid))
    total_mix_self, total_query = total_mid[:, :width], total_mid[:, width : 2 * width]
    total_pairs = total_mid[:, 2 * width : 4 * width].reshape(-1, heads, 2 * dh)
    total_mix_cross = total_mid[:, 4 * width :]
    mine = small_total.reshape(-1)[:small_size].astype(f32)
    total_gain_first, total_gain_second, total_gain_third = (mine[i * part : (i + 1) * part] for i in range(3))
    total_table = mine[3 * part :].reshape(buckets, table_own)
    return (
        layer_out, grad_layer_in, grad_encoder, total_gain_first, total_qkv, total_mix_self, total_table,
        total_gain_second, total_query, total_pairs, total_mix_cross, total_gain_third, total_inner, total_outer,
    )


def solution(mesh):
    in_specs = (
        P("fsdp", "seq", None), P("fsdp", "seq", None), P("fsdp", "seq"), P("fsdp", "seq"), P(),
        P("fsdp"), P("fsdp", None, None), P("fsdp", None), P(None, "fsdp"), P("fsdp"), P("fsdp", None),
        P("fsdp", None, None), P("fsdp", None), P("fsdp"), P("fsdp", None), P("fsdp", None),
        P("fsdp", "seq", None),
    )
    out_specs = (
        P("fsdp", "seq", None), P("fsdp", "seq", None), P("fsdp", "seq", None), P("fsdp"), P("fsdp", None, None),
        P("fsdp", None), P(None, "fsdp"), P("fsdp"), P("fsdp", None), P("fsdp", None, None), P("fsdp", None),
        P("fsdp"), P("fsdp", None), P("fsdp", None),
    )
    return jax.shard_map(shards, mesh=mesh, in_specs=in_specs, out_specs=out_specs, check_vma=False)
```

```python
import functools

import jax
import jax.numpy as jnp
from jax import lax
from jax.experimental import pallas as pl
from jax.experimental.layout import Layout, with_layout_constraint
from jax.experimental.pallas import tpu as pltpu
from jax.sharding import PartitionSpec as P

EPS = 1e-06
HIGH = lax.Precision.HIGHEST
MASKED = -1e30
DOCS = 4

BQ = 256
REACH = 1024


def blk(index, size):
    return pl.ds(pl.multiple_of(index * size, size), size)


def turn(value):
    return jnp.transpose(value.astype(jnp.float32), (1, 0))


def bias_tiles(ext_ref, tile_ref, own, bk):
    span = BQ + bk
    for h in range(own):
        for t in range(tile_ref.shape[1]):
            first = t * bk
            line = jnp.broadcast_to(ext_ref[h : h + 1, first : first + span], (bk, span))
            tile_ref[h, t] = pltpu.roll(line, 0, 1, stride=1, stride_axis=0)[:, bk:]


def tile_count(bk):
    return BQ // bk + REACH // bk


def unpack(ref, own, width, picks, flips, base):
    block = 256

    def one(b, _):
        rows = blk(b, block)
        value = ref[rows, :]
        if flips:
            flat = turn(value).astype(jnp.bfloat16)
            for target, piece in flips:
                for h in range(own):
                    at = h * width + piece * 64
                    target[base + h, :, rows] = flat[at : at + 64]
        for target, piece in picks:
            for h in range(own):
                at = h * width + piece * 64
                target[base + h, rows, :] = value[:, at : at + 64]
        return 0

    lax.fori_loop(0, ref.shape[0] // block, one, 0)


def dot(a, b):
    return jnp.dot(a, b, preferred_element_type=jnp.float32)


def score(own_index, key_tile, query_t, tile_ref, t, low, high, first_key):
    value = dot(key_tile, query_t)
    place = lax.broadcasted_iota(jnp.int32, value.shape, 0)
    keep = place >= low - first_key
    if high is not None:
        keep = keep & (place < high - first_key)
    else:
        value = value + tile_ref[own_index, t]
    return jnp.where(keep, value, MASKED)


def forward_body(own, bk, causal, lim_ref, rows_ref, q_t, k_rows, v_t, tile_ref, o_ref, ot_ref, lse_ref):
    length = o_ref.shape[0]

    def q_block(i, _):
        cols = blk(i, BQ)
        queries = [q_t[h, :, cols] for h in range(own)]
        low = rows_ref[0:1, cols]
        high = None if causal else rows_ref[1:2, cols]

        def k_block(j, carry):
            keys = blk(j, bk)
            t = i * (BQ // bk) - j + (BQ // bk - 1)
            out = []
            for h in range(own):
                top, total, acc = carry[h]
                s = score(h, k_rows[h, keys, :], queries[h], tile_ref, t, low, high, j * bk)
                new_top = jnp.maximum(top, jnp.max(s, axis=0, keepdims=True))
                p = jnp.exp(s - new_top)
                scale = jnp.exp(top - new_top)
                total = total * scale + jnp.sum(p, axis=0, keepdims=True)
                acc = acc * scale + dot(v_t[h, :, keys], p.astype(jnp.bfloat16))
                out.append((new_top, total, acc))
            return tuple(out)

        start = tuple(
            (
                jnp.full((1, BQ), MASKED, jnp.float32),
                jnp.zeros((1, BQ), jnp.float32),
                jnp.zeros((64, BQ), jnp.float32),
            )
            for _ in range(own)
        )
        ends = lax.fori_loop(lim_ref[0, i], lim_ref[1, i], k_block, start)
        for h in range(own):
            top, total, acc = ends[h]
            ot_ref[h * 64 : h * 64 + 64, cols] = acc / total
            lse_ref[h : h + 1, cols] = top + jnp.log(total)
        o_ref[cols, :] = turn(ot_ref[:, cols]).astype(jnp.bfloat16)
        return 0

    lax.fori_loop(0, length // BQ, q_block, 0)


def self_forward_kernel(own, bk, lim_ref, rows_ref, ext_ref, x_ref, o_ref, ot_ref, lse_ref, q_t, k_rows, v_t, tile_ref):
    bias_tiles(ext_ref, tile_ref, own, bk)
    unpack(x_ref, own, 192, [(k_rows, 1)], [(q_t, 0), (v_t, 2)], 0)
    forward_body(own, bk, True, lim_ref, rows_ref, q_t, k_rows, v_t, tile_ref, o_ref, ot_ref, lse_ref)


def cross_forward_kernel(own, bk, lim_ref, rows_ref, q_ref, kv_ref, o_ref, ot_ref, lse_ref, q_t, k_rows, v_t):
    unpack(q_ref, own, 64, [], [(q_t, 0)], 0)
    unpack(kv_ref, own, 128, [(k_rows, 0)], [(v_t, 1)], 0)
    forward_body(own, bk, False, lim_ref, rows_ref, q_t, k_rows, v_t, None, o_ref, ot_ref, lse_ref)


def backward_body(
    own, bk, causal, lim_ref, rows_ref, do_ref, ot_ref, lse_ref,
    q_t, q_rows, k_t, k_rows, v_rows, do_t, do_rows, tile_ref, sum_ref, dq_t, dk, dv,
):
    length = do_ref.shape[0]
    dk[...] = jnp.zeros_like(dk)
    dv[...] = jnp.zeros_like(dv)
    if causal:
        sum_ref[...] = jnp.zeros_like(sum_ref)

    def q_block(i, _):
        cols = blk(i, BQ)
        low = rows_ref[0:1, cols]
        high = None if causal else rows_ref[1:2, cols]
        per_head = []
        for h in range(own):
            grad_t = do_t[h, :, cols]
            delta = jnp.sum(
                grad_t.astype(jnp.float32) * ot_ref[h * 64 : h * 64 + 64, cols], axis=0, keepdims=True
            )
            per_head.append((q_t[h, :, cols], grad_t, delta, lse_ref[h : h + 1, cols]))

        def k_block(j, carry):
            keys = blk(j, bk)
            t = i * (BQ // bk) - j + (BQ // bk - 1)
            out = []
            for h in range(own):
                query_t, grad_t, delta, lse = per_head[h]
                s = score(h, k_rows[h, keys, :], query_t, tile_ref, t, low, high, j * bk)
                p = jnp.exp(s - lse)
                dp = dot(v_rows[h, keys, :], grad_t)
                ds = (p * (dp - delta)).astype(jnp.bfloat16)
                dv[h, keys, :] += dot(p.astype(jnp.bfloat16), do_rows[h, cols, :])
                dk[h, keys, :] += dot(ds, q_rows[h, cols, :])
                if causal:
                    sum_ref[h, t] += ds.astype(jnp.float32)
                out.append(carry[h] + dot(k_t[h, :, keys], ds))
            return tuple(out)

        ends = lax.fori_loop(
            lim_ref[0, i],
            lim_ref[1, i],
            k_block,
            tuple(jnp.zeros((64, BQ), jnp.float32) for _ in range(own)),
        )
        for h in range(own):
            dq_t[h * 64 : h * 64 + 64, cols] = ends[h]
        return 0

    lax.fori_loop(0, length // BQ, q_block, 0)


def diagonal_sums(sum_ref, u_ref, own, bk):
    flip = (
        lax.broadcasted_iota(jnp.int32, (bk, bk), 0) + lax.broadcasted_iota(jnp.int32, (bk, bk), 1) == bk - 1
    ).astype(jnp.float32)
    for h in range(own):
        for t in range(sum_ref.shape[1]):
            upside = jnp.dot(flip, sum_ref[h, t], precision=HIGH, preferred_element_type=jnp.float32)
            wide = jnp.concatenate([upside, jnp.zeros((bk, bk), jnp.float32)], axis=1)
            aligned = pltpu.roll(wide, 0, 1, stride=1, stride_axis=0)
            u_ref[h, t : t + 1, :] = jnp.sum(aligned, axis=0, keepdims=True)


def self_backward_kernel(
    own, bk, lim_ref, rows_ref, ext_ref, x_ref, do_ref, ot_ref, lse_ref, dx_ref, u_ref,
    q_t, q_rows, k_t, k_rows, v_rows, do_t, do_rows, tile_ref, sum_ref, dq_t, dk, dv,
):
    bias_tiles(ext_ref, tile_ref, own, bk)
    unpack(x_ref, own, 192, [(q_rows, 0), (k_rows, 1), (v_rows, 2)], [(q_t, 0), (k_t, 1)], 0)
    unpack(do_ref, own, 64, [(do_rows, 0)], [(do_t, 0)], 0)
    backward_body(
        own, bk, True, lim_ref, rows_ref, do_ref, ot_ref, lse_ref,
        q_t, q_rows, k_t, k_rows, v_rows, do_t, do_rows, tile_ref, sum_ref, dq_t, dk, dv,
    )
    diagonal_sums(sum_ref, u_ref, own, bk)

    def pack(b, _):
        rows = blk(b, 256)
        dq = turn(dq_t[:, rows])
        pieces = []
        for h in range(own):
            pieces += [dq[:, h * 64 : h * 64 + 64], dk[h, rows, :], dv[h, rows, :]]
        dx_ref[rows, :] = jnp.concatenate(pieces, axis=1).astype(jnp.bfloat16)
        return 0

    lax.fori_loop(0, x_ref.shape[0] // 256, pack, 0)


def cross_backward_kernel(
    own, bk, lim_ref, rows_ref, q_ref, kv_ref, do_ref, ot_ref, lse_ref, dq_ref, dkv_ref,
    q_t, q_rows, k_t, k_rows, v_rows, do_t, do_rows, dq_t, dk, dv,
):
    unpack(q_ref, own, 64, [(q_rows, 0)], [(q_t, 0)], 0)
    unpack(kv_ref, own, 128, [(k_rows, 0), (v_rows, 1)], [(k_t, 0)], 0)
    unpack(do_ref, own, 64, [(do_rows, 0)], [(do_t, 0)], 0)
    backward_body(
        own, bk, False, lim_ref, rows_ref, do_ref, ot_ref, lse_ref,
        q_t, q_rows, k_t, k_rows, v_rows, do_t, do_rows, None, None, dq_t, dk, dv,
    )

    def pack_q(b, _):
        rows = blk(b, 256)
        dq_ref[rows, :] = turn(dq_t[:, rows]).astype(jnp.bfloat16)
        return 0

    def pack_kv(b, _):
        rows = blk(b, 256)
        pieces = []
        for h in range(own):
            pieces += [dk[h, rows, :], dv[h, rows, :]]
        dkv_ref[rows, :] = jnp.concatenate(pieces, axis=1).astype(jnp.bfloat16)
        return 0

    lax.fori_loop(0, q_ref.shape[0] // 256, pack_q, 0)
    lax.fori_loop(0, kv_ref.shape[0] // 256, pack_kv, 0)


SMEM = pl.BlockSpec(memory_space=pltpu.SMEM)
VMEM = pl.BlockSpec(memory_space=pltpu.VMEM)
bf16, f32 = jnp.bfloat16, jnp.float32


def call(body, name, operands, outs, scratch, flops):
    size = sum(v.size * v.dtype.itemsize for v in operands)
    return pl.pallas_call(
        body,
        name=name,
        out_shape=[jax.ShapeDtypeStruct(s, d) for s, d in outs],
        in_specs=[SMEM] + [VMEM] * (len(operands) - 1),
        out_specs=[VMEM] * len(outs),
        scratch_shapes=[pltpu.VMEM(s, d) for s, d in scratch],
        compiler_params=pltpu.CompilerParams(vmem_limit_bytes=40 << 20),
        cost_estimate=pl.CostEstimate(flops=flops, bytes_accessed=2 * size, transcendentals=flops // 256),
    )(*operands)


def self_forward(limits, rows, ext, x, bk=256):
    length, own = x.shape[0], x.shape[1] // 192
    return call(
        functools.partial(self_forward_kernel, own, bk),
        "self_forward",
        [limits, rows, ext, x],
        [((length, own * 64), bf16), ((own * 64, length), f32), ((own, length), f32)],
        [
            ((own, 64, length), bf16),
            ((own, length, 64), bf16),
            ((own, 64, length), bf16),
            ((own, tile_count(bk), bk, BQ), f32),
        ],
        length * length * own * 64,
    )


def cross_forward(limits, rows, q, kv, bk=256):
    length, own, keys = q.shape[0], q.shape[1] // 64, kv.shape[0]
    return call(
        functools.partial(cross_forward_kernel, own, bk),
        "cross_forward",
        [limits, rows, q, kv],
        [((length, own * 64), bf16), ((own * 64, length), f32), ((own, length), f32)],
        [((own, 64, length), bf16), ((own, keys, 64), bf16), ((own, 64, keys), bf16)],
        length * keys * own * 128,
    )


def self_backward(limits, rows, ext, x, grad, o_t, lse, bk=256):
    length, own = x.shape[0], x.shape[1] // 192
    return call(
        functools.partial(self_backward_kernel, own, bk),
        "self_backward",
        [limits, rows, ext, x, grad, o_t, lse],
        [((length, own * 192), bf16), ((own, tile_count(bk), BQ + bk), f32)],
        [
            ((own, 64, length), bf16),
            ((own, length, 64), bf16),
            ((own, 64, length), bf16),
            ((own, length, 64), bf16),
            ((own, length, 64), bf16),
            ((own, 64, length), bf16),
            ((own, length, 64), bf16),
            ((own, tile_count(bk), bk, BQ), f32),
            ((own, tile_count(bk), bk, BQ), f32),
            ((own * 64, length), f32),
            ((own, length, 64), f32),
            ((own, length, 64), f32),
        ],
        length * length * own * 160,
    )


def cross_backward(limits, rows, q, kv, grad, o_t, lse, bk=256):
    length, own, keys = q.shape[0], q.shape[1] // 64, kv.shape[0]
    return call(
        functools.partial(cross_backward_kernel, own, bk),
        "cross_backward",
        [limits, rows, q, kv, grad, o_t, lse],
        [((length, own * 64), bf16), ((keys, own * 128), bf16)],
        [
            ((own, 64, length), bf16),
            ((own, length, 64), bf16),
            ((own, 64, keys), bf16),
            ((own, keys, 64), bf16),
            ((own, keys, 64), bf16),
            ((own, 64, length), bf16),
            ((own, length, 64), bf16),
            ((own * 64, length), f32),
            ((own, keys, 64), f32),
            ((own, keys, 64), f32),
        ],
        length * keys * own * 320,
    )


MESH = pl.DeviceIdType.MESH


def ring_place(index, n):
    z, x = index // 2, index % 2
    return z + x * (n - 1 - 2 * z)


def ring_index(place, n):
    x = place // (n // 2)
    z = place + x * (n - 1 - 2 * place)
    return 2 * z + x


def ring_cut(shape, split, n):
    rows, cols = shape[0] // n, shape[1]
    return (rows, cols // split) if split > 0 else (rows // -split, cols)


def ring_kernel(n, splits, *refs):
    count = len(splits)
    x_refs, y_refs, slots = refs[:count], refs[count : 2 * count], refs[2 * count : 3 * count]
    send_sem, recv_sem = refs[3 * count :]
    place = ring_place(lax.axis_index("seq"), n)
    right = ring_index((place + 1) % n, n)
    left = ring_index((place + n - 1) % n, n)
    barrier = pltpu.get_barrier_semaphore()
    for neighbour in (left, right):
        pl.semaphore_signal(barrier, inc=1, device_id={"seq": neighbour}, device_id_type=MESH)
    pl.semaphore_wait(barrier, 2)

    streams = []
    for k in range(count):
        for piece in range(abs(splits[k])):
            streams.append((k, piece, piece % 2))

    def window(ref, k, piece, chunk):
        whole = x_refs[k].shape[0] // n
        rows, cols = ring_cut(x_refs[k].shape, splits[k], n)
        if splits[k] > 0:
            return ref.at[pl.ds(chunk * whole, rows), pl.ds(piece * cols, cols)]
        return ref.at[pl.ds(chunk * whole + piece * rows, rows), :]

    def copy(number, step, src, dst, down):
        return pltpu.make_async_remote_copy(
            src_ref=src,
            dst_ref=dst,
            send_sem=send_sem.at[number, step],
            recv_sem=recv_sem.at[number, step],
            device_id={"seq": left if down else right},
            device_id_type=MESH,
        )

    def chunk_at(down, step):
        return (place + 1 + step) % n if down else (place + 2 * n - 1 - step) % n

    copies = {}

    def start(number, step, src, dst, down):
        copies[number, step] = copy(number, step, src, dst, down)
        copies[number, step].start()

    for number, (k, piece, down) in enumerate(streams):
        start(number, 0, window(x_refs[k], k, piece, place), window(slots[k], k, piece, 0), down)
    for step in range(n - 1):
        for number, (k, piece, down) in enumerate(streams):
            copies[number, step].wait_recv()
            chunk = chunk_at(down, step)
            mine = window(x_refs[k], k, piece, chunk)
            landed = window(slots[k], k, piece, step)
            total = landed[...].astype(jnp.float32) + mine[...].astype(jnp.float32)
            if step < n - 2:
                landed[...] = total.astype(jnp.bfloat16)
                start(number, step + 1, landed, window(slots[k], k, piece, step + 1), down)
            else:
                done = window(y_refs[k], k, piece, chunk)
                done[...] = total.astype(jnp.bfloat16)
                start(number, n - 1, done, done, down)
    for step in range(n - 1):
        for number, (k, piece, down) in enumerate(streams):
            copies[number, n - 1 + step].wait_recv()
            if step < n - 2:
                chunk = chunk_at(down, n - 1 + step)
                done = window(y_refs[k], k, piece, chunk)
                start(number, n + step, done, done, down)
    for one in copies.values():
        one.wait_send()


def ring_total(arrays, splits, ident):
    n = lax.axis_size("seq")
    size = sum(v.size * 2 for v in arrays)
    streams = sum(abs(s) for s in splits)
    return pl.pallas_call(
        functools.partial(ring_kernel, n, splits),
        name="ring_total",
        out_shape=[jax.ShapeDtypeStruct(v.shape, jnp.bfloat16) for v in arrays],
        in_specs=[pl.BlockSpec(memory_space=pltpu.VMEM)] * len(arrays),
        out_specs=[pl.BlockSpec(memory_space=pltpu.VMEM)] * len(arrays),
        scratch_shapes=[pltpu.VMEM((v.shape[0] // n * (n - 1), v.shape[1]), jnp.bfloat16) for v in arrays]
        + [pltpu.SemaphoreType.DMA((streams, 2 * n - 2)), pltpu.SemaphoreType.DMA((streams, 2 * n - 2))],
        compiler_params=pltpu.CompilerParams(
            collective_id=ident, has_side_effects=True, vmem_limit_bytes=48 << 20
        ),
        cost_estimate=pl.CostEstimate(flops=size, bytes_accessed=60 * size, transcendentals=0),
    )(*arrays)


def team(n):
    s, f = lax.axis_index("seq"), lax.axis_index("fsdp")
    half = s // (n // 2)
    away = (half + f) % 2
    return f // 2, half, (s + away * (n // 2)) % n


def swap_kernel(n, count, *refs):
    x_refs, y_refs = refs[:count], refs[count : 2 * count]
    send_sem, recv_sem, own_sem = refs[2 * count :]
    pair, half, rank = team(n)

    def device(other):
        away = (other // (n // 2) + half) % 2
        return {"seq": (other + away * (n // 2)) % n, "fsdp": 2 * pair + (half + away) % 2}

    barrier = pltpu.get_barrier_semaphore()
    for j in range(1, n):
        pl.semaphore_signal(barrier, inc=1, device_id=device((rank + j) % n), device_id_type=MESH)
    pl.semaphore_wait(barrier, n - 1)
    copies = []
    for k in range(count):
        for j in range(1, n):
            other = (rank + j) % n
            one = pltpu.make_async_remote_copy(
                src_ref=x_refs[k].at[other],
                dst_ref=y_refs[k].at[rank],
                send_sem=send_sem.at[k, j],
                recv_sem=recv_sem.at[k, j],
                device_id=device(other),
                device_id_type=MESH,
            )
            one.start()
            copies.append(one)
    own = [
        pltpu.make_async_copy(x_refs[k].at[rank], y_refs[k].at[rank], own_sem.at[k]) for k in range(count)
    ]
    for one in own:
        one.start()
    for one in copies + own:
        one.wait()


def swap(arrays, ident):
    n = lax.axis_size("seq")
    count = len(arrays)
    size = sum(v.size * 2 for v in arrays)
    return pl.pallas_call(
        functools.partial(swap_kernel, n, count),
        name="swap",
        out_shape=[jax.ShapeDtypeStruct(v.shape, v.dtype) for v in arrays],
        in_specs=[pl.BlockSpec(memory_space=pl.ANY)] * count,
        out_specs=[pl.BlockSpec(memory_space=pl.ANY)] * count,
        scratch_shapes=[
            pltpu.SemaphoreType.DMA((count, n)),
            pltpu.SemaphoreType.DMA((count, n)),
            pltpu.SemaphoreType.DMA((count,)),
        ],
        compiler_params=pltpu.CompilerParams(collective_id=ident, has_side_effects=True),
        cost_estimate=pl.CostEstimate(flops=0, bytes_accessed=30 * size, transcendentals=0),
    )(*arrays)


def norm_apply(value, gain):
    return value * lax.rsqrt(jnp.mean(value * value, axis=-1, keepdims=True) + EPS) * gain


def norm_back(value, gain, grad):
    _, pull = jax.vjp(norm_apply, value, gain)
    return pull(grad)


def gate_mix(gate, up):
    return jax.nn.gelu(gate, approximate=True) * up


def counts_below(ids, values):
    total = jnp.zeros_like(values)
    for doc in range(DOCS):
        total = total + jnp.where(values > doc, jnp.sum((ids == doc).astype(jnp.int32)), 0)
    return total


def change_home(value):
    n, fan = lax.axis_size("seq"), lax.axis_size("fsdp")
    pairs = []
    for s in range(n):
        for f in range(fan):
            away = (s // (n // 2) + f) % 2
            target = ((s + n // 2) % n, f ^ 1) if away else (s, f)
            pairs.append((s * fan + f, target[0] * fan + target[1]))
    return lax.ppermute(value, ("seq", "fsdp"), pairs)


def spread(blocks):
    fan, me = lax.axis_size("fsdp"), lax.axis_index("fsdp")
    result = blocks
    for far in range(1, fan):
        block = lax.dynamic_index_in_dim(blocks, (me + far) % fan, 0, True)
        block = lax.ppermute(block, "fsdp", [(f, (f + far) % fan) for f in range(fan)])
        result = lax.dynamic_update_slice_in_dim(result, block, (me - far) % fan, 0)
    return result


def flat(blocks):
    return jnp.transpose(blocks, (1, 0, 2)).reshape(blocks.shape[1], -1)


def by_rows(value):
    return with_layout_constraint(value, Layout(major_to_minor=tuple(range(value.ndim))))


def scatter(grad):
    return lax.psum_scatter(grad, "fsdp", scatter_dimension=0, tiled=True)


def over_seq(arrays, splits, ident):
    n = lax.axis_size("seq")
    if all(
        v.shape[0] % (8 * n) == 0
        and ring_cut(v.shape, s, n)[0] % 8 == 0
        and v.shape[1] % (128 * max(s, 1)) == 0
        for v, s in zip(arrays, splits)
    ):
        return ring_total(arrays, splits, ident)
    return [lax.psum(v, "seq") for v in arrays]


def shards(
    layer_in, encoder, decoder_ids, encoder_ids, rel_buckets,
    norm_self, self_qkv, self_out, rel_table, norm_cross, cross_q, cross_kv, cross_out, norm_ff, ff_in, ff_out,
    cotangent,
):
    seqs, local, width = layer_in.shape
    enc_local = encoder.shape[1]
    parts = lax.axis_size("seq")
    heads = self_qkv.shape[1]
    dh = self_qkv.shape[2] // 3
    own = heads // parts
    rows = seqs * local
    buckets, table_own = rel_table.shape
    length, keys = local * parts, enc_local * parts
    gather = lambda v: lax.all_gather(v, "fsdp", axis=0, tiled=True)

    fan = lax.axis_size("fsdp")
    units = ff_in.shape[1] // (2 * fan)
    part = norm_self.shape[0]
    pair, half, rank = team(parts)

    qkv_w = gather(self_qkv)
    small = jnp.concatenate([norm_self, norm_cross, norm_ff, rel_table.reshape(-1)])
    small = lax.all_gather(small, "fsdp", axis=0, tiled=False)
    qkv_w, small, first_batch, cross_out = lax.optimization_barrier(
        (qkv_w, small, jnp.concatenate([self_out, cross_q, cross_kv.reshape(-1, 2 * width)], axis=1), cross_out)
    )
    qkv_w = qkv_w.reshape(width, parts, own * 3 * dh)
    first_batch = by_rows(gather(by_rows(first_batch)))
    inner_t = jnp.transpose(ff_in.T.reshape(2, fan, units, -1), (1, 0, 2, 3))
    first_batch, cross_out, inner_t = lax.optimization_barrier((first_batch, cross_out, inner_t))
    mix_self = first_batch[:, :width].reshape(parts, own * dh, width)
    query_w = first_batch[:, width : 2 * width].reshape(width, parts, own * dh)
    pairs_w = first_batch[:, 2 * width :].reshape(width, parts, own * 2 * dh)
    mix_cross = gather(cross_out)
    inner_t = spread(inner_t)
    gate_t, up_t = (jnp.transpose(inner_t[:, i], (1, 0, 2)).reshape(units, width) for i in range(2))

    gain_first, gain_second, gain_third = (
        small[:, i * part : (i + 1) * part].reshape(width).astype(f32) for i in range(3)
    )
    table = jnp.transpose(small[:, 3 * part :].reshape(-1, buckets, table_own), (1, 0, 2)).reshape(buckets, heads)
    both_ids = jnp.concatenate([decoder_ids.reshape(-1), encoder_ids.reshape(-1)])
    both_ids = change_home(jnp.pad(both_ids, (0, 1024 - local - enc_local)).reshape(8, 128))
    (both_ids,) = swap([jnp.broadcast_to(both_ids[None], (parts, 8, 128))], 13)
    both_ids = both_ids.reshape(parts, 1024)
    ids = both_ids[:, :local].reshape(length)
    enc_ids = both_ids[:, local : local + enc_local].reshape(keys)

    first_seen = counts_below(ids, ids)
    enc_first = counts_below(enc_ids, ids)
    enc_last = counts_below(enc_ids, ids + 1)
    blocks = length // BQ
    bk = 256
    self_rows = jnp.broadcast_to(first_seen[None], (8, length))
    cross_rows = jnp.concatenate([enc_first[None], enc_last[None], jnp.zeros((6, length), jnp.int32)])
    self_limits = jnp.stack(
        [first_seen[::BQ] // bk, (jnp.arange(blocks, dtype=jnp.int32) + 1) * (BQ // bk)]
    )
    cross_limits = jnp.stack([enc_first[::BQ] // bk, (enc_last[BQ - 1 :: BQ] + bk - 1) // bk])

    first_head = rank * own
    table_mine = lax.dynamic_slice_in_dim(table.astype(f32), first_head, own, 1)
    near = rel_buckets[:REACH]
    onehot = (near[:, None] == jnp.arange(buckets, dtype=jnp.int32)[None, :]).astype(f32)
    bias = jnp.einsum("ln,ng->gl", onehot, table_mine, precision=HIGH)
    ext = jnp.concatenate(
        [jnp.full((own, BQ), MASKED, f32), bias, jnp.zeros((own, BQ), f32)], axis=1
    )

    stream = change_home(layer_in.reshape(rows, width)).astype(f32)
    others = change_home(jnp.concatenate([cotangent.reshape(rows, width), encoder.reshape(-1, width)]))
    grad_low, enc_flat = others[:rows], others[rows:]
    mix_cross, grad_low = lax.optimization_barrier((mix_cross, grad_low))
    mix_cross = mix_cross.reshape(parts, own * dh, width)
    grad_group = gather(grad_low)
    normed_first = norm_apply(stream, gain_first).astype(bf16)
    qkv_tok = jnp.einsum("td,dge->gte", normed_first, qkv_w, preferred_element_type=f32).astype(bf16)
    (qkv,) = swap([qkv_tok], 10)
    qkv = qkv.reshape(length, own * 3 * dh)
    out_self, self_t, self_lse = self_forward(self_limits, self_rows, ext, qkv)
    (self_tok,) = swap([out_self.reshape(parts, local, own * dh)], 11)
    after_self = stream + jnp.einsum("gtc,gcd->td", self_tok, mix_self, preferred_element_type=f32)
    normed_second = norm_apply(after_self, gain_second).astype(bf16)
    query_tok = jnp.einsum("td,dgc->gtc", normed_second, query_w, preferred_element_type=f32).astype(bf16)
    pairs_tok = jnp.einsum("td,dge->gte", enc_flat, pairs_w, preferred_element_type=f32).astype(bf16)
    query_cross, pairs = swap([query_tok, pairs_tok], 12)
    query_cross, pairs = query_cross.reshape(length, own * dh), pairs.reshape(keys, own * 2 * dh)
    out_cross, cross_t, cross_lse = cross_forward(cross_limits, cross_rows, query_cross, pairs)
    (cross_tok,) = swap([out_cross.reshape(parts, local, own * dh)], 11)
    after_cross = after_self + jnp.einsum("gtc,gcd->td", cross_tok, mix_cross, preferred_element_type=f32)
    normed_third = norm_apply(after_cross, gain_third).astype(bf16)
    normed_group = gather(normed_third)
    gate = jnp.einsum("td,fd->tf", normed_group, gate_t, preferred_element_type=f32)
    up = jnp.einsum("td,fd->tf", normed_group, up_t, preferred_element_type=f32)
    hidden = gate_mix(gate, up).astype(bf16)

    grad_hidden = jnp.einsum("td,fd->tf", grad_group, ff_out, preferred_element_type=f32)
    _, pull_mix = jax.vjp(gate_mix, gate, up)
    grad_gate, grad_up = (g.astype(bf16) for g in pull_mix(grad_hidden))
    grad_third_in = jnp.dot(grad_gate, gate_t, preferred_element_type=f32) + jnp.dot(
        grad_up, up_t, preferred_element_type=f32
    )
    grad_third_in = scatter(grad_third_in.astype(bf16))
    outer_part = jnp.dot(hidden, ff_out, preferred_element_type=f32).astype(bf16)
    part_outer = jnp.einsum("tf,td->fd", hidden, grad_group, preferred_element_type=f32).astype(bf16)
    grad_inner = [
        jnp.einsum("tf,td->fd", g, normed_group, preferred_element_type=f32).astype(bf16)
        for g in (grad_gate, grad_up)
    ]
    grad_inner = jnp.transpose(jnp.stack(grad_inner).reshape(2, units, fan, -1), (2, 0, 1, 3))
    grad_third_in, outer_part, part_outer, grad_inner = lax.optimization_barrier(
        (grad_third_in, outer_part, part_outer, grad_inner)
    )
    outer_part = scatter(outer_part)
    part_inner = spread(grad_inner).reshape(2 * fan * units, -1)
    grad_third_in = grad_third_in.astype(f32)
    grad_from_third, grad_gain_third = norm_back(after_cross, gain_third, grad_third_in)
    grad_middle = grad_low.astype(f32) + grad_from_third
    middle_low = grad_middle.astype(bf16)
    grad_mix_cross = jnp.einsum("gtc,td->gcd", cross_tok, middle_low, preferred_element_type=f32)
    grad_cross_tok = jnp.einsum("td,gcd->gtc", middle_low, mix_cross, preferred_element_type=f32).astype(bf16)
    (grad_cross,) = swap([grad_cross_tok], 11)
    grad_cross = grad_cross.reshape(length, own * dh)
    grad_query, grad_pairs = cross_backward(
        cross_limits, cross_rows, query_cross, pairs, grad_cross, cross_t, cross_lse
    )
    grad_query_tok, grad_pairs_tok = swap(
        [grad_query.reshape(parts, local, own * dh), grad_pairs.reshape(parts, enc_local, own * 2 * dh)], 12
    )
    grad_query_tok, grad_pairs_tok = flat(grad_query_tok), flat(grad_pairs_tok)
    grad_query_w = jnp.einsum("td,te->de", normed_second, grad_query_tok, preferred_element_type=f32)
    grad_second_in = jnp.einsum("te,de->td", grad_query_tok, query_w.reshape(width, -1), preferred_element_type=f32)
    grad_pairs_w = jnp.einsum("td,te->de", enc_flat, grad_pairs_tok, preferred_element_type=f32)
    grad_encoder = jnp.einsum("te,de->td", grad_pairs_tok, pairs_w.reshape(width, -1), preferred_element_type=f32)
    grad_encoder = change_home(grad_encoder.astype(bf16)).astype(f32).reshape(seqs, enc_local, width)
    grad_from_second, grad_gain_second = norm_back(after_self, gain_second, grad_second_in)
    grad_upper = grad_middle + grad_from_second
    upper_low = grad_upper.astype(bf16)
    grad_mix_self = jnp.einsum("gtc,td->gcd", self_tok, upper_low, preferred_element_type=f32)
    grad_self_tok = jnp.einsum("td,gcd->gtc", upper_low, mix_self, preferred_element_type=f32).astype(bf16)
    grad_mid = jnp.concatenate(
        [
            grad_query_w.astype(bf16),
            grad_pairs_w.astype(bf16),
            grad_mix_cross.reshape(width, width).astype(bf16),
        ],
        axis=1,
    )
    grad_self_tok, grad_mid = lax.optimization_barrier((grad_self_tok, grad_mid))
    part_mid = scatter(grad_mid)
    (grad_self,) = swap([grad_self_tok], 11)
    grad_self = grad_self.reshape(length, own * dh)
    grad_qkv, tile_sums = self_backward(self_limits, self_rows, ext, qkv, grad_self, self_t, self_lse)
    (grad_qkv_tok,) = swap([grad_qkv.reshape(parts, local, own * 3 * dh)], 10)
    grad_qkv_tok = flat(grad_qkv_tok)
    grad_qkv_w = jnp.einsum("td,te->de", normed_first, grad_qkv_tok, preferred_element_type=f32)
    grad_last = jnp.concatenate([grad_mix_self.reshape(width, width).astype(bf16), grad_qkv_w.astype(bf16)], axis=1)
    grad_last, part_mid, part_inner, part_outer, outer_part = lax.optimization_barrier(
        (grad_last, part_mid, part_inner, part_outer, outer_part)
    )
    part_last = scatter(grad_last)
    layer_out = (after_cross + outer_part.astype(f32)).astype(bf16)
    layer_out = change_home(layer_out).reshape(seqs, local, width)
    grad_first_in = jnp.einsum("te,de->td", grad_qkv_tok, qkv_w.reshape(width, -1), preferred_element_type=f32)
    grad_from_first, grad_gain_first = norm_back(stream, gain_first, grad_first_in)
    grad_layer_in = change_home((grad_upper + grad_from_first).astype(bf16)).astype(f32)
    grad_layer_in = grad_layer_in.reshape(seqs, local, width)

    bucket_line = jnp.concatenate(
        [jnp.full((BQ,), -1, jnp.int32), near, jnp.full((BQ + bk,), -1, jnp.int32)]
    )
    by_tile = jnp.stack([bucket_line[t * bk + 1 : t * bk + 1 + BQ + bk] for t in range(tile_count(bk))])
    in_bucket = (by_tile[:, :, None] == jnp.arange(buckets, dtype=jnp.int32)).astype(f32)
    by_bucket = jnp.einsum("twn,gtw->ng", in_bucket, tile_sums, precision=HIGH)
    grad_table = lax.dynamic_update_slice_in_dim(jnp.zeros((buckets, heads), f32), by_bucket, first_head, 1)

    gains = jnp.concatenate(
        [g.reshape(-1, part) for g in (grad_gain_first, grad_gain_second, grad_gain_third)], axis=1
    )
    tables = jnp.transpose(grad_table.reshape(buckets, -1, table_own), (1, 0, 2)).reshape(-1, buckets * table_own)
    small_grads = lax.psum(jnp.concatenate([gains, tables], axis=1).astype(bf16), "fsdp")
    small_grads = lax.dynamic_index_in_dim(small_grads, lax.axis_index("fsdp"), 0, False)
    small_size = small_grads.shape[0]
    small_grads = jnp.pad(small_grads, (0, parts * 1024 - small_size)).reshape(parts * 8, 128)
    total_inner, total_outer = over_seq([part_inner, part_outer], (-2, 2), 0)
    total_inner, part_mid, part_last = lax.optimization_barrier((total_inner, part_mid, part_last))
    total_mid, total_last, small_total = over_seq([part_mid, part_last, small_grads], (2, 2, 1), 1)
    total_outer, total_mid, total_last = (v.astype(f32) for v in (total_outer, total_mid, total_last))
    total_inner = jnp.transpose(total_inner.reshape(fan, 2, units, -1), (3, 1, 0, 2)).reshape(-1, 2 * fan * units)
    total_inner = total_inner.astype(f32)
    total_query, total_mix_cross = total_mid[:, :width], total_mid[:, 3 * width :]
    total_pairs = total_mid[:, width : 3 * width].reshape(-1, heads, 2 * dh)
    total_mix_self, total_qkv = total_last[:, :width], total_last[:, width:].reshape(-1, heads, 3 * dh)
    mine = small_total.reshape(-1)[:small_size].astype(f32)
    total_gain_first, total_gain_second, total_gain_third = (mine[i * part : (i + 1) * part] for i in range(3))
    total_table = mine[3 * part :].reshape(buckets, table_own)
    return (
        layer_out, grad_layer_in, grad_encoder, total_gain_first, total_qkv, total_mix_self, total_table,
        total_gain_second, total_query, total_pairs, total_mix_cross, total_gain_third, total_inner, total_outer,
    )


def solution(mesh):
    in_specs = (
        P("fsdp", "seq", None), P("fsdp", "seq", None), P("fsdp", "seq"), P("fsdp", "seq"), P(),
        P("fsdp"), P("fsdp", None, None), P("fsdp", None), P(None, "fsdp"), P("fsdp"), P("fsdp", None),
        P("fsdp", None, None), P("fsdp", None), P("fsdp"), P("fsdp", None), P("fsdp", None),
        P("fsdp", "seq", None),
    )
    out_specs = (
        P("fsdp", "seq", None), P("fsdp", "seq", None), P("fsdp", "seq", None), P("fsdp"), P("fsdp", None, None),
        P("fsdp", None), P(None, "fsdp"), P("fsdp"), P("fsdp", None), P("fsdp", None, None), P("fsdp", None),
        P("fsdp"), P("fsdp", None), P("fsdp", None),
    )
    return jax.shard_map(shards, mesh=mesh, in_specs=in_specs, out_specs=out_specs, check_vma=False)
```

```python
import functools

import jax
import jax.numpy as jnp
from jax import lax
from jax.experimental import pallas as pl
from jax.experimental.layout import Layout, with_layout_constraint
from jax.experimental.pallas import tpu as pltpu
from jax.sharding import PartitionSpec as P

EPS = 1e-06
HIGH = lax.Precision.HIGHEST
MASKED = -1e30
DOCS = 4

BQ = 256
REACH = 1024


def blk(index, size):
    return pl.ds(pl.multiple_of(index * size, size), size)


def turn(value):
    return jnp.transpose(value.astype(jnp.float32), (1, 0))


def bias_tiles(ext_ref, tile_ref, own, bk):
    span = BQ + bk
    for h in range(own):
        for t in range(tile_ref.shape[1]):
            first = t * bk
            line = jnp.broadcast_to(ext_ref[h : h + 1, first : first + span], (bk, span))
            tile_ref[h, t] = pltpu.roll(line, 0, 1, stride=1, stride_axis=0)[:, bk:]


def tile_count(bk):
    return BQ // bk + REACH // bk


def unpack(ref, own, width, picks, flips, base):
    block = 256

    def one(b, _):
        rows = blk(b, block)
        value = ref[rows, :]
        if flips:
            flat = turn(value).astype(jnp.bfloat16)
            for target, piece in flips:
                for h in range(own):
                    at = h * width + piece * 64
                    target[base + h, :, rows] = flat[at : at + 64]
        for target, piece in picks:
            for h in range(own):
                at = h * width + piece * 64
                target[base + h, rows, :] = value[:, at : at + 64]
        return 0

    lax.fori_loop(0, ref.shape[0] // block, one, 0)


def dot(a, b):
    return jnp.dot(a, b, preferred_element_type=jnp.float32)


def score(own_index, key_tile, query_t, tile_ref, t, low, high, first_key):
    value = dot(key_tile, query_t)
    place = lax.broadcasted_iota(jnp.int32, value.shape, 0)
    keep = place >= low - first_key
    if high is not None:
        keep = keep & (place < high - first_key)
    else:
        value = value + tile_ref[own_index, t]
    return jnp.where(keep, value, MASKED)


def forward_body(own, bk, causal, lim_ref, rows_ref, q_t, k_rows, v_t, tile_ref, o_ref, ot_ref, lse_ref):
    length = o_ref.shape[0]

    def q_block(i, _):
        cols = blk(i, BQ)
        queries = [q_t[h, :, cols] for h in range(own)]
        low = rows_ref[0:1, cols]
        high = None if causal else rows_ref[1:2, cols]

        def k_block(j, carry):
            keys = blk(j, bk)
            t = i * (BQ // bk) - j + (BQ // bk - 1)
            out = []
            for h in range(own):
                top, total, acc = carry[h]
                s = score(h, k_rows[h, keys, :], queries[h], tile_ref, t, low, high, j * bk)
                new_top = jnp.maximum(top, jnp.max(s, axis=0, keepdims=True))
                p = jnp.exp(s - new_top)
                scale = jnp.exp(top - new_top)
                total = total * scale + jnp.sum(p, axis=0, keepdims=True)
                acc = acc * scale + dot(v_t[h, :, keys], p.astype(jnp.bfloat16))
                out.append((new_top, total, acc))
            return tuple(out)

        start = tuple(
            (
                jnp.full((1, BQ), MASKED, jnp.float32),
                jnp.zeros((1, BQ), jnp.float32),
                jnp.zeros((64, BQ), jnp.float32),
            )
            for _ in range(own)
        )
        ends = lax.fori_loop(lim_ref[0, i], lim_ref[1, i], k_block, start)
        for h in range(own):
            top, total, acc = ends[h]
            ot_ref[h * 64 : h * 64 + 64, cols] = acc / total
            lse_ref[h : h + 1, cols] = top + jnp.log(total)
        o_ref[cols, :] = turn(ot_ref[:, cols]).astype(jnp.bfloat16)
        return 0

    lax.fori_loop(0, length // BQ, q_block, 0)


def self_forward_kernel(own, bk, lim_ref, rows_ref, ext_ref, x_ref, o_ref, ot_ref, lse_ref, q_t, k_rows, v_t, tile_ref):
    bias_tiles(ext_ref, tile_ref, own, bk)
    unpack(x_ref, own, 192, [(k_rows, 1)], [(q_t, 0), (v_t, 2)], 0)
    forward_body(own, bk, True, lim_ref, rows_ref, q_t, k_rows, v_t, tile_ref, o_ref, ot_ref, lse_ref)


def cross_forward_kernel(own, bk, lim_ref, rows_ref, q_ref, kv_ref, o_ref, ot_ref, lse_ref, q_t, k_rows, v_t):
    unpack(q_ref, own, 64, [], [(q_t, 0)], 0)
    unpack(kv_ref, own, 128, [(k_rows, 0)], [(v_t, 1)], 0)
    forward_body(own, bk, False, lim_ref, rows_ref, q_t, k_rows, v_t, None, o_ref, ot_ref, lse_ref)


def backward_body(
    own, bk, causal, lim_ref, rows_ref, do_ref, ot_ref, lse_ref,
    q_t, q_rows, k_t, k_rows, v_rows, do_t, do_rows, tile_ref, sum_ref, dq_t, dk, dv,
):
    length = do_ref.shape[0]
    dk[...] = jnp.zeros_like(dk)
    dv[...] = jnp.zeros_like(dv)
    if causal:
        sum_ref[...] = jnp.zeros_like(sum_ref)

    def q_block(i, _):
        cols = blk(i, BQ)
        low = rows_ref[0:1, cols]
        high = None if causal else rows_ref[1:2, cols]
        per_head = []
        for h in range(own):
            grad_t = do_t[h, :, cols]
            delta = jnp.sum(
                grad_t.astype(jnp.float32) * ot_ref[h * 64 : h * 64 + 64, cols], axis=0, keepdims=True
            )
            per_head.append((q_t[h, :, cols], grad_t, delta, lse_ref[h : h + 1, cols]))

        def k_block(j, carry):
            keys = blk(j, bk)
            t = i * (BQ // bk) - j + (BQ // bk - 1)
            out = []
            for h in range(own):
                query_t, grad_t, delta, lse = per_head[h]
                s = score(h, k_rows[h, keys, :], query_t, tile_ref, t, low, high, j * bk)
                p = jnp.exp(s - lse)
                dp = dot(v_rows[h, keys, :], grad_t)
                ds = (p * (dp - delta)).astype(jnp.bfloat16)
                dv[h, keys, :] += dot(p.astype(jnp.bfloat16), do_rows[h, cols, :])
                dk[h, keys, :] += dot(ds, q_rows[h, cols, :])
                if causal:
                    sum_ref[h, t] += ds.astype(jnp.float32)
                out.append(carry[h] + dot(k_t[h, :, keys], ds))
            return tuple(out)

        ends = lax.fori_loop(
            lim_ref[0, i],
            lim_ref[1, i],
            k_block,
            tuple(jnp.zeros((64, BQ), jnp.float32) for _ in range(own)),
        )
        for h in range(own):
            dq_t[h * 64 : h * 64 + 64, cols] = ends[h]
        return 0

    lax.fori_loop(0, length // BQ, q_block, 0)


def diagonal_sums(sum_ref, u_ref, own, bk):
    flip = (
        lax.broadcasted_iota(jnp.int32, (bk, bk), 0) + lax.broadcasted_iota(jnp.int32, (bk, bk), 1) == bk - 1
    ).astype(jnp.float32)
    for h in range(own):
        for t in range(sum_ref.shape[1]):
            upside = jnp.dot(flip, sum_ref[h, t], precision=HIGH, preferred_element_type=jnp.float32)
            wide = jnp.concatenate([upside, jnp.zeros((bk, bk), jnp.float32)], axis=1)
            aligned = pltpu.roll(wide, 0, 1, stride=1, stride_axis=0)
            u_ref[h, t : t + 1, :] = jnp.sum(aligned, axis=0, keepdims=True)


def self_backward_kernel(
    own, bk, lim_ref, rows_ref, ext_ref, x_ref, do_ref, ot_ref, lse_ref, dx_ref, u_ref,
    q_t, q_rows, k_t, k_rows, v_rows, do_t, do_rows, tile_ref, sum_ref, dq_t, dk, dv,
):
    bias_tiles(ext_ref, tile_ref, own, bk)
    unpack(x_ref, own, 192, [(q_rows, 0), (k_rows, 1), (v_rows, 2)], [(q_t, 0), (k_t, 1)], 0)
    unpack(do_ref, own, 64, [(do_rows, 0)], [(do_t, 0)], 0)
    backward_body(
        own, bk, True, lim_ref, rows_ref, do_ref, ot_ref, lse_ref,
        q_t, q_rows, k_t, k_rows, v_rows, do_t, do_rows, tile_ref, sum_ref, dq_t, dk, dv,
    )
    diagonal_sums(sum_ref, u_ref, own, bk)

    def pack(b, _):
        rows = blk(b, 256)
        dq = turn(dq_t[:, rows])
        pieces = []
        for h in range(own):
            pieces += [dq[:, h * 64 : h * 64 + 64], dk[h, rows, :], dv[h, rows, :]]
        dx_ref[rows, :] = jnp.concatenate(pieces, axis=1).astype(jnp.bfloat16)
        return 0

    lax.fori_loop(0, x_ref.shape[0] // 256, pack, 0)


def cross_backward_kernel(
    own, bk, lim_ref, rows_ref, q_ref, kv_ref, do_ref, ot_ref, lse_ref, dq_ref, dkv_ref,
    q_t, q_rows, k_t, k_rows, v_rows, do_t, do_rows, dq_t, dk, dv,
):
    unpack(q_ref, own, 64, [(q_rows, 0)], [(q_t, 0)], 0)
    unpack(kv_ref, own, 128, [(k_rows, 0), (v_rows, 1)], [(k_t, 0)], 0)
    unpack(do_ref, own, 64, [(do_rows, 0)], [(do_t, 0)], 0)
    backward_body(
        own, bk, False, lim_ref, rows_ref, do_ref, ot_ref, lse_ref,
        q_t, q_rows, k_t, k_rows, v_rows, do_t, do_rows, None, None, dq_t, dk, dv,
    )

    def pack_q(b, _):
        rows = blk(b, 256)
        dq_ref[rows, :] = turn(dq_t[:, rows]).astype(jnp.bfloat16)
        return 0

    def pack_kv(b, _):
        rows = blk(b, 256)
        pieces = []
        for h in range(own):
            pieces += [dk[h, rows, :], dv[h, rows, :]]
        dkv_ref[rows, :] = jnp.concatenate(pieces, axis=1).astype(jnp.bfloat16)
        return 0

    lax.fori_loop(0, q_ref.shape[0] // 256, pack_q, 0)
    lax.fori_loop(0, kv_ref.shape[0] // 256, pack_kv, 0)


SMEM = pl.BlockSpec(memory_space=pltpu.SMEM)
VMEM = pl.BlockSpec(memory_space=pltpu.VMEM)
bf16, f32 = jnp.bfloat16, jnp.float32


def call(body, name, operands, outs, scratch, flops):
    size = sum(v.size * v.dtype.itemsize for v in operands)
    return pl.pallas_call(
        body,
        name=name,
        out_shape=[jax.ShapeDtypeStruct(s, d) for s, d in outs],
        in_specs=[SMEM] + [VMEM] * (len(operands) - 1),
        out_specs=[VMEM] * len(outs),
        scratch_shapes=[pltpu.VMEM(s, d) for s, d in scratch],
        compiler_params=pltpu.CompilerParams(vmem_limit_bytes=40 << 20),
        cost_estimate=pl.CostEstimate(flops=0, bytes_accessed=size, transcendentals=0),
    )(*operands)


def self_forward(limits, rows, ext, x, bk=256):
    length, own = x.shape[0], x.shape[1] // 192
    return call(
        functools.partial(self_forward_kernel, own, bk),
        "self_forward",
        [limits, rows, ext, x],
        [((length, own * 64), bf16), ((own * 64, length), f32), ((own, length), f32)],
        [
            ((own, 64, length), bf16),
            ((own, length, 64), bf16),
            ((own, 64, length), bf16),
            ((own, tile_count(bk), bk, BQ), f32),
        ],
        length * length * own * 64,
    )


def cross_forward(limits, rows, q, kv, bk=256):
    length, own, keys = q.shape[0], q.shape[1] // 64, kv.shape[0]
    return call(
        functools.partial(cross_forward_kernel, own, bk),
        "cross_forward",
        [limits, rows, q, kv],
        [((length, own * 64), bf16), ((own * 64, length), f32), ((own, length), f32)],
        [((own, 64, length), bf16), ((own, keys, 64), bf16), ((own, 64, keys), bf16)],
        length * keys * own * 128,
    )


def self_backward(limits, rows, ext, x, grad, o_t, lse, bk=256):
    length, own = x.shape[0], x.shape[1] // 192
    return call(
        functools.partial(self_backward_kernel, own, bk),
        "self_backward",
        [limits, rows, ext, x, grad, o_t, lse],
        [((length, own * 192), bf16), ((own, tile_count(bk), BQ + bk), f32)],
        [
            ((own, 64, length), bf16),
            ((own, length, 64), bf16),
            ((own, 64, length), bf16),
            ((own, length, 64), bf16),
            ((own, length, 64), bf16),
            ((own, 64, length), bf16),
            ((own, length, 64), bf16),
            ((own, tile_count(bk), bk, BQ), f32),
            ((own, tile_count(bk), bk, BQ), f32),
            ((own * 64, length), f32),
            ((own, length, 64), f32),
            ((own, length, 64), f32),
        ],
        length * length * own * 160,
    )


def cross_backward(limits, rows, q, kv, grad, o_t, lse, bk=256):
    length, own, keys = q.shape[0], q.shape[1] // 64, kv.shape[0]
    return call(
        functools.partial(cross_backward_kernel, own, bk),
        "cross_backward",
        [limits, rows, q, kv, grad, o_t, lse],
        [((length, own * 64), bf16), ((keys, own * 128), bf16)],
        [
            ((own, 64, length), bf16),
            ((own, length, 64), bf16),
            ((own, 64, keys), bf16),
            ((own, keys, 64), bf16),
            ((own, keys, 64), bf16),
            ((own, 64, length), bf16),
            ((own, length, 64), bf16),
            ((own * 64, length), f32),
            ((own, keys, 64), f32),
            ((own, keys, 64), f32),
        ],
        length * keys * own * 320,
    )


MESH = pl.DeviceIdType.MESH


def ring_place(index, n):
    z, x = index // 2, index % 2
    return z + x * (n - 1 - 2 * z)


def ring_index(place, n):
    x = place // (n // 2)
    z = place + x * (n - 1 - 2 * place)
    return 2 * z + x


def ring_greet(n, others):
    place = ring_place(lax.axis_index("seq"), n)
    right = ring_index((place + 1) % n, n)
    left = ring_index((place + n - 1) % n, n)
    barrier = pltpu.get_barrier_semaphore()
    for neighbour in (left, right):
        pl.semaphore_signal(barrier, inc=1, device_id={"seq": neighbour}, device_id_type=MESH)
    for other in others:
        pl.semaphore_signal(barrier, inc=1, device_id={"fsdp": other}, device_id_type=MESH)
    pl.semaphore_wait(barrier, 2 + len(others))
    return place, right, left


def ring_cut(shape, split, n):
    rows, cols = shape[0] // n, shape[1]
    return (rows, cols // split) if split > 0 else (rows // -split, cols)


def ring_window(ref, shape, split, n, piece, chunk):
    whole = shape[0] // n
    rows, cols = ring_cut(shape, split, n)
    if split > 0:
        return ref.at[pl.ds(chunk * whole, rows), pl.ds(piece * cols, cols)]
    return ref.at[pl.ds(chunk * whole + piece * rows, rows), :]


def ring_kernel(n, splits, *refs):
    count = len(splits)
    x_refs, y_refs, slots = refs[:count], refs[count : 2 * count], refs[2 * count : 3 * count]
    send_sem, recv_sem = refs[3 * count :]
    place, right, left = ring_greet(n, [])
    streams = [(k, piece, piece % 2) for k in range(count) for piece in range(abs(splits[k]))]

    def window(ref, k, piece, chunk):
        return ring_window(ref, x_refs[k].shape, splits[k], n, piece, chunk)

    def chunk_at(down, step):
        return (place + 1 + step) % n if down else (place + 2 * n - 1 - step) % n

    copies = {}

    def start(number, step, src, dst, down):
        copies[number, step] = pltpu.make_async_remote_copy(
            src_ref=src,
            dst_ref=dst,
            send_sem=send_sem.at[number, step],
            recv_sem=recv_sem.at[number, step],
            device_id={"seq": left if down else right},
            device_id_type=MESH,
        )
        copies[number, step].start()

    for number, (k, piece, down) in enumerate(streams):
        start(number, 0, window(x_refs[k], k, piece, place), window(slots[k], k, piece, 0), down)
    for step in range(n - 1):
        for number, (k, piece, down) in enumerate(streams):
            copies[number, step].wait_recv()
            chunk = chunk_at(down, step)
            mine = window(x_refs[k], k, piece, chunk)
            landed = window(slots[k], k, piece, step)
            total = landed[...].astype(jnp.float32) + mine[...].astype(jnp.float32)
            if step < n - 2:
                landed[...] = total.astype(jnp.bfloat16)
                start(number, step + 1, landed, window(slots[k], k, piece, step + 1), down)
            else:
                done = window(y_refs[k], k, piece, chunk)
                done[...] = total.astype(jnp.bfloat16)
                start(number, n - 1, done, done, down)
    for step in range(n - 1):
        for number, (k, piece, down) in enumerate(streams):
            copies[number, n - 1 + step].wait_recv()
            if step < n - 2:
                done = window(y_refs[k], k, piece, chunk_at(down, n - 1 + step))
                start(number, n + step, done, done, down)
    for one in copies.values():
        one.wait_send()


def ring_call(body, name, arrays, outs, scratch, ident):
    size = sum(v.size * 2 for v in arrays)
    return pl.pallas_call(
        body,
        name=name,
        out_shape=[jax.ShapeDtypeStruct(s, jnp.bfloat16) for s in outs],
        in_specs=[pl.BlockSpec(memory_space=pltpu.VMEM)] * len(arrays),
        out_specs=[pl.BlockSpec(memory_space=pltpu.VMEM)] * len(outs),
        scratch_shapes=scratch,
        compiler_params=pltpu.CompilerParams(
            collective_id=ident, has_side_effects=True, vmem_limit_bytes=48 << 20
        ),
        cost_estimate=pl.CostEstimate(flops=0, bytes_accessed=size, transcendentals=0),
    )(*arrays)


def ring_total(arrays, splits, ident):
    n = lax.axis_size("seq")
    streams = sum(abs(s) for s in splits)
    return ring_call(
        functools.partial(ring_kernel, n, splits),
        "ring_total",
        arrays,
        [v.shape for v in arrays],
        [pltpu.VMEM((v.shape[0] // n * (n - 1), v.shape[1]), jnp.bfloat16) for v in arrays]
        + [pltpu.SemaphoreType.DMA((streams, 2 * n - 2))] * 2,
        ident,
    )


def units_kernel(n, fan, x_ref, inner_ref, outer_ref, swap_send, swap_recv, own_sem, send_sem, recv_sem):
    s, me = lax.axis_index("seq"), lax.axis_index("fsdp")
    rows, width = x_ref.shape[0] // 3, x_ref.shape[1]
    cols = width // fan
    block = 2 * fan * rows
    place, right, left = ring_greet(n, [(me + far) % fan for far in range(1, fan)])
    moves = []
    for far in range(fan):
        target = (me + far) % fan
        for half in range(2):
            src = x_ref.at[pl.ds(half * rows, rows), pl.ds(pl.multiple_of(target * cols, 128), cols)]
            dst = inner_ref.at[pl.ds(s * block + (me * 2 + half) * rows, rows), :]
            if far:
                one = pltpu.make_async_remote_copy(
                    src_ref=src,
                    dst_ref=dst,
                    send_sem=swap_send.at[far, half],
                    recv_sem=swap_recv.at[far, half],
                    device_id={"fsdp": target},
                    device_id_type=MESH,
                )
            else:
                one = pltpu.make_async_copy(src, dst, own_sem.at[half])
            one.start()
            moves.append(one)
    mine = pltpu.make_async_copy(
        x_ref.at[pl.ds(2 * rows, rows), :], outer_ref.at[pl.ds(s * rows, rows), :], own_sem.at[2]
    )
    mine.start()
    copies = {}
    outs = ((outer_ref, (n * rows, width), 2), (inner_ref, (n * block, cols), -2))

    def start(k, piece, step):
        ref, shape, split = outs[k]
        chunk = ring_index((place + step) % n if piece else (place + n - step) % n, n)
        view = ring_window(ref, shape, split, n, piece, chunk)
        copies[k, piece, step] = pltpu.make_async_remote_copy(
            src_ref=view,
            dst_ref=view,
            send_sem=send_sem.at[2 * k + piece, step],
            recv_sem=recv_sem.at[2 * k + piece, step],
            device_id={"seq": left if piece else right},
            device_id_type=MESH,
        )
        copies[k, piece, step].start()

    mine.wait()
    start(0, 0, 0)
    start(0, 1, 0)
    for one in moves:
        one.wait()
    start(1, 0, 0)
    start(1, 1, 0)
    for step in range(n - 1):
        for k in range(2):
            for piece in range(2):
                copies[k, piece, step].wait_recv()
                if step < n - 2:
                    start(k, piece, step + 1)
    for one in copies.values():
        one.wait_send()


def units_total(part, ident):
    n, fan = lax.axis_size("seq"), lax.axis_size("fsdp")
    rows, width = part.shape[0] // 3, part.shape[1]
    sems = lambda *shape: pltpu.SemaphoreType.DMA(shape)
    return ring_call(
        functools.partial(units_kernel, n, fan),
        "units_total",
        [part],
        [(n * 2 * fan * rows, width // fan), (n * rows, width)],
        [sems(fan, 2), sems(fan, 2), sems(3), sems(4, n - 1), sems(4, n - 1)],
        ident,
    )


def team(n):
    s, f = lax.axis_index("seq"), lax.axis_index("fsdp")
    half = s // (n // 2)
    away = (half + f) % 2
    return f // 2, half, (s + away * (n // 2)) % n


def swap_kernel(n, fan, count, fars, fresh, *refs):
    given = count + (len(fars) > 0) + (0 if fresh else 2)
    x_refs, y_refs = refs[:count], refs[given : given + count]
    sems = refs[given + count + (2 if fars else 0) :]
    send_sem, recv_sem, own_sem = sems[:3]
    pair, half, rank = team(n)
    me = lax.axis_index("fsdp")

    def device(other):
        away = (other // (n // 2) + half) % 2
        return {"seq": (other + away * (n // 2)) % n, "fsdp": 2 * pair + (half + away) % 2}

    barrier = pltpu.get_barrier_semaphore()
    for j in range(1, n):
        pl.semaphore_signal(barrier, inc=1, device_id=device((rank + j) % n), device_id_type=MESH)
    travel = [far for far in fars if far]
    for far in travel:
        pl.semaphore_signal(barrier, inc=1, device_id={"fsdp": (me + fan - far) % fan}, device_id_type=MESH)
    pl.semaphore_wait(barrier, n - 1 + len(travel))
    copies = []
    for k in range(count):
        for j in range(1, n):
            other = (rank + j) % n
            one = pltpu.make_async_remote_copy(
                src_ref=x_refs[k].at[other],
                dst_ref=y_refs[k].at[rank],
                send_sem=send_sem.at[k, j],
                recv_sem=recv_sem.at[k, j],
                device_id=device(other),
                device_id_type=MESH,
            )
            one.start()
            copies.append(one)
    for k in range(count):
        one = pltpu.make_async_copy(x_refs[k].at[rank], y_refs[k].at[rank], own_sem.at[k])
        one.start()
        copies.append(one)
    if fars:
        w_ref, halves = refs[count], refs[given + count : given + count + 2]
        far_send, far_recv, far_own = sems[3:]
        units, cols = halves[0].shape[0], w_ref.shape[1]
        for i, far in enumerate(fars):
            target = (me + far) % fan
            for part in range(2):
                src = w_ref.at[pl.ds((part * fan + target) * units, units), :]
                dst = halves[part].at[:, pl.ds(pl.multiple_of(me * cols, 128), cols)]
                if far:
                    one = pltpu.make_async_remote_copy(
                        src_ref=src,
                        dst_ref=dst,
                        send_sem=far_send.at[i, part],
                        recv_sem=far_recv.at[i, part],
                        device_id={"fsdp": target},
                        device_id_type=MESH,
                    )
                else:
                    one = pltpu.make_async_copy(src, dst, far_own.at[part])
                one.start()
                copies.append(one)
    for one in copies:
        one.wait()


def swap(arrays, ident, fars=(), given=None, halves=None):
    n, fan = lax.axis_size("seq"), lax.axis_size("fsdp")
    count = len(arrays)
    size = sum(v.size * 2 for v in arrays)
    operands, outs, alias = list(arrays), [jax.ShapeDtypeStruct(v.shape, v.dtype) for v in arrays], {}
    scratch = [
        pltpu.SemaphoreType.DMA((count, n)),
        pltpu.SemaphoreType.DMA((count, n)),
        pltpu.SemaphoreType.DMA((count,)),
    ]
    if fars:
        operands.append(given)
        shape = (given.shape[0] // (2 * fan), given.shape[1] * fan)
        outs += [jax.ShapeDtypeStruct(shape, given.dtype)] * 2
        scratch += [pltpu.SemaphoreType.DMA((len(fars), 2))] * 2 + [pltpu.SemaphoreType.DMA((2,))]
        if halves is not None:
            operands += list(halves)
            alias = {count + 1: count, count + 2: count + 1}
    return pl.pallas_call(
        functools.partial(swap_kernel, n, fan, count, fars, not fars or halves is None),
        name="swap",
        out_shape=outs,
        in_specs=[pl.BlockSpec(memory_space=pl.ANY)] * len(operands),
        out_specs=[pl.BlockSpec(memory_space=pl.ANY)] * len(outs),
        scratch_shapes=scratch,
        input_output_aliases=alias,
        compiler_params=pltpu.CompilerParams(collective_id=ident, has_side_effects=True),
        cost_estimate=pl.CostEstimate(flops=0, bytes_accessed=size, transcendentals=0),
    )(*operands)


def norm_apply(value, gain):
    return value * lax.rsqrt(jnp.mean(value * value, axis=-1, keepdims=True) + EPS) * gain


def norm_back(value, gain, grad):
    _, pull = jax.vjp(norm_apply, value, gain)
    return pull(grad)


def gate_mix(gate, up):
    return jax.nn.gelu(gate, approximate=True) * up


def counts_below(ids, values):
    total = jnp.zeros_like(values)
    for doc in range(DOCS):
        total = total + jnp.where(values > doc, jnp.sum((ids == doc).astype(jnp.int32)), 0)
    return total


def change_home(value):
    n, fan = lax.axis_size("seq"), lax.axis_size("fsdp")
    pairs = []
    for s in range(n):
        for f in range(fan):
            away = (s // (n // 2) + f) % 2
            target = ((s + n // 2) % n, f ^ 1) if away else (s, f)
            pairs.append((s * fan + f, target[0] * fan + target[1]))
    return lax.ppermute(value, ("seq", "fsdp"), pairs)


def spread(blocks):
    fan, me = lax.axis_size("fsdp"), lax.axis_index("fsdp")
    result = blocks
    for far in range(1, fan):
        block = lax.dynamic_index_in_dim(blocks, (me + far) % fan, 0, True)
        block = lax.ppermute(block, "fsdp", [(f, (f + far) % fan) for f in range(fan)])
        result = lax.dynamic_update_slice_in_dim(result, block, (me - far) % fan, 0)
    return result


def flat(blocks):
    return jnp.transpose(blocks, (1, 0, 2)).reshape(blocks.shape[1], -1)


def by_rows(value):
    return with_layout_constraint(value, Layout(major_to_minor=tuple(range(value.ndim))))


def scatter(grad):
    return lax.psum_scatter(grad, "fsdp", scatter_dimension=0, tiled=True)


def over_seq(arrays, splits, ident):
    n = lax.axis_size("seq")
    if all(
        v.shape[0] % (8 * n) == 0
        and ring_cut(v.shape, s, n)[0] % 8 == 0
        and v.shape[1] % (128 * max(s, 1)) == 0
        for v, s in zip(arrays, splits)
    ):
        return ring_total(arrays, splits, ident)
    return [lax.psum(v, "seq") for v in arrays]


def shards(
    layer_in, encoder, decoder_ids, encoder_ids, rel_buckets,
    norm_self, self_qkv, self_out, rel_table, norm_cross, cross_q, cross_kv, cross_out, norm_ff, ff_in, ff_out,
    cotangent,
):
    seqs, local, width = layer_in.shape
    enc_local = encoder.shape[1]
    parts = lax.axis_size("seq")
    heads = self_qkv.shape[1]
    dh = self_qkv.shape[2] // 3
    own = heads // parts
    rows = seqs * local
    buckets, table_own = rel_table.shape
    length, keys = local * parts, enc_local * parts
    gather = lambda v: lax.all_gather(v, "fsdp", axis=0, tiled=True)

    fan = lax.axis_size("fsdp")
    units = ff_in.shape[1] // (2 * fan)
    part = norm_self.shape[0]
    pair, half, rank = team(parts)

    qkv_w = gather(self_qkv)
    small = jnp.concatenate([norm_self, norm_cross, norm_ff, rel_table.reshape(-1)])
    small = lax.all_gather(small, "fsdp", axis=0, tiled=False)
    early = jnp.stack([self_out, cross_q, *jnp.split(cross_kv.reshape(-1, 2 * width), 2, axis=1)])
    small, early = lax.optimization_barrier((small, early))
    early = lax.all_gather(early, "fsdp", axis=1, tiled=True)
    both_ids = jnp.concatenate([decoder_ids.reshape(-1), encoder_ids.reshape(-1)])
    both_ids = change_home(jnp.pad(both_ids, (0, 1024 - local - enc_local)).reshape(8, 128))
    (both_ids,) = swap([jnp.broadcast_to(both_ids[None], (parts, 8, 128))], 13)
    home = change_home(layer_in.reshape(rows, width))
    inner_t = ff_in.T
    qkv_w, small, both_ids, home, inner_t = lax.optimization_barrier((qkv_w, small, both_ids, home, inner_t))
    qkv_w = qkv_w.reshape(width, parts, own * 3 * dh)
    mix_self = early[0].reshape(parts, own * dh, width)
    query_w = early[1].reshape(width, parts, own * dh)
    pairs_w = early[2:]

    gain_first, gain_second, gain_third = (
        small[:, i * part : (i + 1) * part].reshape(width).astype(f32) for i in range(3)
    )
    table = jnp.transpose(small[:, 3 * part :].reshape(-1, buckets, table_own), (1, 0, 2)).reshape(buckets, heads)
    both_ids = both_ids.reshape(parts, 1024)
    ids = both_ids[:, :local].reshape(length)
    enc_ids = both_ids[:, local : local + enc_local].reshape(keys)

    first_seen = counts_below(ids, ids)
    enc_first = counts_below(enc_ids, ids)
    enc_last = counts_below(enc_ids, ids + 1)
    blocks = length // BQ
    bk = 256
    self_rows = jnp.broadcast_to(first_seen[None], (8, length))
    cross_rows = jnp.concatenate([enc_first[None], enc_last[None], jnp.zeros((6, length), jnp.int32)])
    self_limits = jnp.stack(
        [first_seen[::BQ] // bk, (jnp.arange(blocks, dtype=jnp.int32) + 1) * (BQ // bk)]
    )
    cross_limits = jnp.stack([enc_first[::BQ] // bk, (enc_last[BQ - 1 :: BQ] + bk - 1) // bk])

    first_head = rank * own
    table_mine = lax.dynamic_slice_in_dim(table.astype(f32), first_head, own, 1)
    near = rel_buckets[:REACH]
    onehot = (near[:, None] == jnp.arange(buckets, dtype=jnp.int32)[None, :]).astype(f32)
    bias = jnp.einsum("ln,ng->gl", onehot, table_mine, precision=HIGH)
    ext = jnp.concatenate(
        [jnp.full((own, BQ), MASKED, f32), bias, jnp.zeros((own, BQ), f32)], axis=1
    )

    stream = home.astype(f32)
    normed_first = norm_apply(stream, gain_first).astype(bf16)
    qkv_tok = jnp.einsum("td,dge->gte", normed_first, qkv_w, preferred_element_type=f32).astype(bf16)
    qkv_tok, cross_out, cotangent, encoder = lax.optimization_barrier((qkv_tok, cross_out, cotangent, encoder))
    mix_cross = gather(cross_out).reshape(parts, own * dh, width)
    others = change_home(jnp.concatenate([cotangent.reshape(rows, width), encoder.reshape(-1, width)]))
    grad_low, enc_flat = others[:rows], others[rows:]
    (qkv,) = swap([qkv_tok], 10)
    qkv = qkv.reshape(length, own * 3 * dh)
    out_self, self_t, self_lse = self_forward(self_limits, self_rows, ext, qkv)
    out_self, grad_low = lax.optimization_barrier((out_self, grad_low))
    grad_group = gather(grad_low)
    by_kernel = (width // fan) % 128 == 0
    fars = [tuple(far for far in range(fan) if (far + 2) % 3 == i) if by_kernel else () for i in range(3)]
    self_tok, *halves = swap([out_self.reshape(parts, local, own * dh)], 14, fars[0], inner_t)
    after_self = stream + jnp.einsum("gtc,gcd->td", self_tok, mix_self, preferred_element_type=f32)
    normed_second = norm_apply(after_self, gain_second).astype(bf16)
    query_tok = jnp.einsum("td,dgc->gtc", normed_second, query_w, preferred_element_type=f32).astype(bf16)
    pairs_tok = jnp.einsum(
        "td,sdge->sgte", enc_flat, pairs_w.reshape(2, width, parts // 2, -1), preferred_element_type=f32
    )
    pairs_tok = pairs_tok.astype(bf16).reshape(parts, enc_local, -1)
    query_cross, pairs, *halves = swap([query_tok, pairs_tok], 15, fars[1], inner_t, halves)
    query_cross, pairs = query_cross.reshape(length, own * dh), pairs.reshape(keys, own * 2 * dh)
    out_cross, cross_t, cross_lse = cross_forward(cross_limits, cross_rows, query_cross, pairs)
    cross_tok, *halves = swap([out_cross.reshape(parts, local, own * dh)], 16, fars[2], inner_t, halves)
    if not by_kernel:
        halves = spread(jnp.transpose(inner_t.reshape(2, fan, units, -1), (1, 0, 2, 3)))
        halves = [jnp.transpose(halves[:, i], (1, 0, 2)).reshape(units, width) for i in range(2)]
    gate_t, up_t = halves
    after_cross = after_self + jnp.einsum("gtc,gcd->td", cross_tok, mix_cross, preferred_element_type=f32)
    normed_third = norm_apply(after_cross, gain_third).astype(bf16)
    normed_group = gather(normed_third)
    gate = jnp.einsum("td,fd->tf", normed_group, gate_t, preferred_element_type=f32)
    up = jnp.einsum("td,fd->tf", normed_group, up_t, preferred_element_type=f32)
    hidden = gate_mix(gate, up).astype(bf16)

    grad_hidden = jnp.einsum("td,fd->tf", grad_group, ff_out, preferred_element_type=f32)
    _, pull_mix = jax.vjp(gate_mix, gate, up)
    grad_gate, grad_up = (g.astype(bf16) for g in pull_mix(grad_hidden))
    grad_third_in = jnp.dot(grad_gate, gate_t, preferred_element_type=f32) + jnp.dot(
        grad_up, up_t, preferred_element_type=f32
    )
    grad_third_in = scatter(grad_third_in.astype(bf16))
    outer_part = jnp.dot(hidden, ff_out, preferred_element_type=f32).astype(bf16)
    grad_units = [
        jnp.einsum("tf,td->fd", g, y, preferred_element_type=f32).astype(bf16)
        for g, y in ((grad_gate, normed_group), (grad_up, normed_group), (hidden, grad_group))
    ]
    grad_third_in, outer_part, grad_units = lax.optimization_barrier((grad_third_in, outer_part, grad_units))
    if by_kernel:
        grad_units = jnp.stack([g.reshape(parts, units // parts, width) for g in grad_units], axis=1)
        part_units = lax.psum_scatter(
            grad_units.reshape(3 * units, width), "seq", scatter_dimension=0, tiled=True
        )
    grad_third_in = grad_third_in.astype(f32)
    grad_from_third, grad_gain_third = norm_back(after_cross, gain_third, grad_third_in)
    grad_middle = grad_low.astype(f32) + grad_from_third
    middle_low = grad_middle.astype(bf16)
    grad_mix_cross = jnp.einsum("gtc,td->gcd", cross_tok, middle_low, preferred_element_type=f32)
    grad_cross_tok = jnp.einsum("td,gcd->gtc", middle_low, mix_cross, preferred_element_type=f32).astype(bf16)
    (grad_cross,) = swap([grad_cross_tok], 11)
    grad_cross = grad_cross.reshape(length, own * dh)
    grad_query, grad_pairs = cross_backward(
        cross_limits, cross_rows, query_cross, pairs, grad_cross, cross_t, cross_lse
    )
    grad_query_tok, grad_pairs_tok = swap(
        [grad_query.reshape(parts, local, own * dh), grad_pairs.reshape(parts, enc_local, own * 2 * dh)], 12
    )
    grad_query_tok, grad_pairs_tok = flat(grad_query_tok), flat(grad_pairs_tok)
    grad_query_w = jnp.einsum("td,te->de", normed_second, grad_query_tok, preferred_element_type=f32)
    grad_second_in = jnp.einsum("te,de->td", grad_query_tok, query_w.reshape(width, -1), preferred_element_type=f32)
    grad_pairs_w = jnp.einsum("td,te->de", enc_flat, grad_pairs_tok, preferred_element_type=f32)
    grad_encoder = sum(
        jnp.einsum("te,de->td", grad_pairs_tok[:, i * width : (i + 1) * width], pairs_w[i], preferred_element_type=f32)
        for i in range(2)
    )
    grad_encoder = change_home(grad_encoder.astype(bf16)).astype(f32).reshape(seqs, enc_local, width)
    grad_from_second, grad_gain_second = norm_back(after_self, gain_second, grad_second_in)
    grad_upper = grad_middle + grad_from_second
    upper_low = grad_upper.astype(bf16)
    grad_mix_self = jnp.einsum("gtc,td->gcd", self_tok, upper_low, preferred_element_type=f32)
    grad_self_tok = jnp.einsum("td,gcd->gtc", upper_low, mix_self, preferred_element_type=f32).astype(bf16)
    grad_mid = jnp.concatenate(
        [
            grad_query_w.astype(bf16),
            grad_pairs_w.astype(bf16),
            grad_mix_cross.reshape(width, width).astype(bf16),
            grad_mix_self.reshape(width, width).astype(bf16),
        ],
        axis=1,
    )
    if by_kernel:
        grad_self_tok, grad_mid, part_units = lax.optimization_barrier((grad_self_tok, grad_mid, part_units))
    part_mid = scatter(grad_mid)
    (grad_self,) = swap([grad_self_tok], 11)
    grad_self = grad_self.reshape(length, own * dh)
    grad_qkv, tile_sums = self_backward(self_limits, self_rows, ext, qkv, grad_self, self_t, self_lse)
    (grad_qkv_tok,) = swap([grad_qkv.reshape(parts, local, own * 3 * dh)], 10)
    grad_qkv_tok = flat(grad_qkv_tok)
    grad_qkv_w = jnp.einsum("td,te->de", normed_first, grad_qkv_tok, preferred_element_type=f32)
    grad_last, part_mid = lax.optimization_barrier((grad_qkv_w.astype(bf16), part_mid))
    part_last = scatter(grad_last)
    grad_first_in = jnp.einsum("te,de->td", grad_qkv_tok, qkv_w.reshape(width, -1), preferred_element_type=f32)
    grad_from_first, grad_gain_first = norm_back(stream, gain_first, grad_first_in)
    grad_gain_first, outer_part = lax.optimization_barrier((grad_gain_first, outer_part))
    outer_part = scatter(outer_part)
    grad_layer_in = change_home((grad_upper + grad_from_first).astype(bf16)).astype(f32)
    grad_layer_in = grad_layer_in.reshape(seqs, local, width)

    bucket_line = jnp.concatenate(
        [jnp.full((BQ,), -1, jnp.int32), near, jnp.full((BQ + bk,), -1, jnp.int32)]
    )
    by_tile = jnp.stack([bucket_line[t * bk + 1 : t * bk + 1 + BQ + bk] for t in range(tile_count(bk))])
    in_bucket = (by_tile[:, :, None] == jnp.arange(buckets, dtype=jnp.int32)).astype(f32)
    by_bucket = jnp.einsum("twn,gtw->ng", in_bucket, tile_sums, precision=HIGH)
    grad_table = lax.dynamic_update_slice_in_dim(jnp.zeros((buckets, heads), f32), by_bucket, first_head, 1)

    gains = jnp.concatenate(
        [g.reshape(-1, part) for g in (grad_gain_first, grad_gain_second, grad_gain_third)], axis=1
    )
    tables = jnp.transpose(grad_table.reshape(buckets, -1, table_own), (1, 0, 2)).reshape(-1, buckets * table_own)
    small_grads = lax.psum(jnp.concatenate([gains, tables], axis=1).astype(bf16), "fsdp")
    small_grads = lax.dynamic_index_in_dim(small_grads, lax.axis_index("fsdp"), 0, False)
    small_size = small_grads.shape[0]
    small_grads = jnp.pad(small_grads, (0, parts * 1024 - small_size)).reshape(parts * 8, 128)
    grad_layer_in, small_grads, part_last = lax.optimization_barrier((grad_layer_in, small_grads, part_last))
    if by_kernel:
        total_inner, total_outer = units_total(part_units, 0)
        total_inner = jnp.transpose(total_inner.reshape(parts, fan, 2, units // parts, -1), (4, 2, 1, 0, 3))
    else:
        grad_units = [lax.psum(g, "seq") for g in grad_units]
        total_inner = spread(jnp.transpose(jnp.stack(grad_units[:2]).reshape(2, units, fan, -1), (2, 0, 1, 3)))
        total_inner, total_outer = jnp.transpose(total_inner, (3, 1, 0, 2)), grad_units[2]
    total_inner = total_inner.astype(f32).reshape(-1, 2 * fan * units)
    total_outer, part_last = lax.optimization_barrier((total_outer, part_last))
    total_mid, total_qkv, small_total = over_seq([part_mid, part_last, small_grads], (2, 2, 1), 1)
    layer_out = (after_cross + outer_part.astype(f32)).astype(bf16)
    layer_out = change_home(layer_out).reshape(seqs, local, width)
    total_outer, total_mid, total_qkv = (v.astype(f32) for v in (total_outer, total_mid, total_qkv))
    total_query, total_mix_cross = total_mid[:, :width], total_mid[:, 3 * width : 4 * width]
    total_pairs = total_mid[:, width : 3 * width].reshape(-1, heads, 2 * dh)
    total_mix_self, total_qkv = total_mid[:, 4 * width :], total_qkv.reshape(-1, heads, 3 * dh)
    mine = small_total.reshape(-1)[:small_size].astype(f32)
    total_gain_first, total_gain_second, total_gain_third = (mine[i * part : (i + 1) * part] for i in range(3))
    total_table = mine[3 * part :].reshape(buckets, table_own)
    return (
        layer_out, grad_layer_in, grad_encoder, total_gain_first, total_qkv, total_mix_self, total_table,
        total_gain_second, total_query, total_pairs, total_mix_cross, total_gain_third, total_inner, total_outer,
    )


def solution(mesh):
    in_specs = (
        P("fsdp", "seq", None), P("fsdp", "seq", None), P("fsdp", "seq"), P("fsdp", "seq"), P(),
        P("fsdp"), P("fsdp", None, None), P("fsdp", None), P(None, "fsdp"), P("fsdp"), P("fsdp", None),
        P("fsdp", None, None), P("fsdp", None), P("fsdp"), P("fsdp", None), P("fsdp", None),
        P("fsdp", "seq", None),
    )
    out_specs = (
        P("fsdp", "seq", None), P("fsdp", "seq", None), P("fsdp", "seq", None), P("fsdp"), P("fsdp", None, None),
        P("fsdp", None), P(None, "fsdp"), P("fsdp"), P("fsdp", None), P("fsdp", None, None), P("fsdp", None),
        P("fsdp"), P("fsdp", None), P("fsdp", None),
    )
    return jax.shard_map(shards, mesh=mesh, in_specs=in_specs, out_specs=out_specs, check_vma=False)
```

```python
import functools

import jax
import jax.numpy as jnp
from jax import lax
from jax.experimental import pallas as pl
from jax.experimental.layout import Layout, with_layout_constraint
from jax.experimental.pallas import tpu as pltpu
from jax.sharding import PartitionSpec as P

EPS = 1e-06
HIGH = lax.Precision.HIGHEST
MASKED = -1e30
DOCS = 4

BQ = 256
REACH = 1024


def blk(index, size):
    return pl.ds(pl.multiple_of(index * size, size), size)


def turn(value):
    return jnp.transpose(value.astype(jnp.float32), (1, 0))


def bias_tiles(ext_ref, tile_ref, own, bk):
    span = BQ + bk
    for h in range(own):
        for t in range(tile_ref.shape[1]):
            first = t * bk
            line = jnp.broadcast_to(ext_ref[h : h + 1, first : first + span], (bk, span))
            tile_ref[h, t] = pltpu.roll(line, 0, 1, stride=1, stride_axis=0)[:, bk:]


def tile_count(bk):
    return BQ // bk + REACH // bk


def unpack(ref, own, width, picks, flips, base):
    block = 256

    def one(b, _):
        rows = blk(b, block)
        value = ref[rows, :]
        if flips:
            flat = turn(value).astype(jnp.bfloat16)
            for target, piece in flips:
                for h in range(own):
                    at = h * width + piece * 64
                    target[base + h, :, rows] = flat[at : at + 64]
        for target, piece in picks:
            for h in range(own):
                at = h * width + piece * 64
                target[base + h, rows, :] = value[:, at : at + 64]
        return 0

    lax.fori_loop(0, ref.shape[0] // block, one, 0)


def dot(a, b):
    return jnp.dot(a, b, preferred_element_type=jnp.float32)


def score(own_index, key_tile, query_t, tile_ref, t, low, high, first_key):
    value = dot(key_tile, query_t)
    place = lax.broadcasted_iota(jnp.int32, value.shape, 0)
    keep = place >= low - first_key
    if high is not None:
        keep = keep & (place < high - first_key)
    else:
        value = value + tile_ref[own_index, t]
    return jnp.where(keep, value, MASKED)


def forward_body(own, bk, causal, lim_ref, rows_ref, q_t, k_rows, v_t, tile_ref, o_ref, ot_ref, lse_ref):
    length = o_ref.shape[0]

    def q_block(i, _):
        cols = blk(i, BQ)
        queries = [q_t[h, :, cols] for h in range(own)]
        low = rows_ref[0:1, cols]
        high = None if causal else rows_ref[1:2, cols]

        def k_block(j, carry):
            keys = blk(j, bk)
            t = i * (BQ // bk) - j + (BQ // bk - 1)
            out = []
            for h in range(own):
                top, total, acc = carry[h]
                s = score(h, k_rows[h, keys, :], queries[h], tile_ref, t, low, high, j * bk)
                new_top = jnp.maximum(top, jnp.max(s, axis=0, keepdims=True))
                p = jnp.exp(s - new_top)
                scale = jnp.exp(top - new_top)
                total = total * scale + jnp.sum(p, axis=0, keepdims=True)
                acc = acc * scale + dot(v_t[h, :, keys], p.astype(jnp.bfloat16))
                out.append((new_top, total, acc))
            return tuple(out)

        start = tuple(
            (
                jnp.full((1, BQ), MASKED, jnp.float32),
                jnp.zeros((1, BQ), jnp.float32),
                jnp.zeros((64, BQ), jnp.float32),
            )
            for _ in range(own)
        )
        ends = lax.fori_loop(lim_ref[0, i], lim_ref[1, i], k_block, start)
        for h in range(own):
            top, total, acc = ends[h]
            ot_ref[h * 64 : h * 64 + 64, cols] = acc / total
            lse_ref[h : h + 1, cols] = top + jnp.log(total)
        o_ref[cols, :] = turn(ot_ref[:, cols]).astype(jnp.bfloat16)
        return 0

    lax.fori_loop(0, length // BQ, q_block, 0)


def self_forward_kernel(own, bk, lim_ref, rows_ref, ext_ref, x_ref, o_ref, ot_ref, lse_ref, q_t, k_rows, v_t, tile_ref):
    bias_tiles(ext_ref, tile_ref, own, bk)
    unpack(x_ref, own, 192, [(k_rows, 1)], [(q_t, 0), (v_t, 2)], 0)
    forward_body(own, bk, True, lim_ref, rows_ref, q_t, k_rows, v_t, tile_ref, o_ref, ot_ref, lse_ref)


def cross_forward_kernel(own, bk, lim_ref, rows_ref, q_ref, kv_ref, o_ref, ot_ref, lse_ref, q_t, k_rows, v_t):
    unpack(q_ref, own, 64, [], [(q_t, 0)], 0)
    unpack(kv_ref, own, 128, [(k_rows, 0)], [(v_t, 1)], 0)
    forward_body(own, bk, False, lim_ref, rows_ref, q_t, k_rows, v_t, None, o_ref, ot_ref, lse_ref)


def backward_body(
    own, bk, causal, lim_ref, rows_ref, do_ref, ot_ref, lse_ref,
    q_t, q_rows, k_t, k_rows, v_rows, do_t, do_rows, tile_ref, sum_ref, dq_t, dk, dv,
):
    length = do_ref.shape[0]
    dk[...] = jnp.zeros_like(dk)
    dv[...] = jnp.zeros_like(dv)
    if causal:
        sum_ref[...] = jnp.zeros_like(sum_ref)

    def q_block(i, _):
        cols = blk(i, BQ)
        low = rows_ref[0:1, cols]
        high = None if causal else rows_ref[1:2, cols]
        per_head = []
        for h in range(own):
            grad_t = do_t[h, :, cols]
            delta = jnp.sum(
                grad_t.astype(jnp.float32) * ot_ref[h * 64 : h * 64 + 64, cols], axis=0, keepdims=True
            )
            per_head.append((q_t[h, :, cols], grad_t, delta, lse_ref[h : h + 1, cols]))

        def k_block(j, carry):
            keys = blk(j, bk)
            t = i * (BQ // bk) - j + (BQ // bk - 1)
            out = []
            for h in range(own):
                query_t, grad_t, delta, lse = per_head[h]
                s = score(h, k_rows[h, keys, :], query_t, tile_ref, t, low, high, j * bk)
                p = jnp.exp(s - lse)
                dp = dot(v_rows[h, keys, :], grad_t)
                ds = (p * (dp - delta)).astype(jnp.bfloat16)
                dv[h, keys, :] += dot(p.astype(jnp.bfloat16), do_rows[h, cols, :])
                dk[h, keys, :] += dot(ds, q_rows[h, cols, :])
                if causal:
                    sum_ref[h, t] += ds.astype(jnp.float32)
                out.append(carry[h] + dot(k_t[h, :, keys], ds))
            return tuple(out)

        ends = lax.fori_loop(
            lim_ref[0, i],
            lim_ref[1, i],
            k_block,
            tuple(jnp.zeros((64, BQ), jnp.float32) for _ in range(own)),
        )
        for h in range(own):
            dq_t[h * 64 : h * 64 + 64, cols] = ends[h]
        return 0

    lax.fori_loop(0, length // BQ, q_block, 0)


def diagonal_sums(sum_ref, u_ref, own, bk):
    flip = (
        lax.broadcasted_iota(jnp.int32, (bk, bk), 0) + lax.broadcasted_iota(jnp.int32, (bk, bk), 1) == bk - 1
    ).astype(jnp.float32)
    for h in range(own):
        for t in range(sum_ref.shape[1]):
            upside = jnp.dot(flip, sum_ref[h, t], precision=HIGH, preferred_element_type=jnp.float32)
            wide = jnp.concatenate([upside, jnp.zeros((bk, bk), jnp.float32)], axis=1)
            aligned = pltpu.roll(wide, 0, 1, stride=1, stride_axis=0)
            u_ref[h, t : t + 1, :] = jnp.sum(aligned, axis=0, keepdims=True)


def self_backward_kernel(
    own, bk, lim_ref, rows_ref, ext_ref, x_ref, do_ref, ot_ref, lse_ref, dx_ref, u_ref,
    q_t, q_rows, k_t, k_rows, v_rows, do_t, do_rows, tile_ref, sum_ref, dq_t, dk, dv,
):
    bias_tiles(ext_ref, tile_ref, own, bk)
    unpack(x_ref, own, 192, [(q_rows, 0), (k_rows, 1), (v_rows, 2)], [(q_t, 0), (k_t, 1)], 0)
    unpack(do_ref, own, 64, [(do_rows, 0)], [(do_t, 0)], 0)
    backward_body(
        own, bk, True, lim_ref, rows_ref, do_ref, ot_ref, lse_ref,
        q_t, q_rows, k_t, k_rows, v_rows, do_t, do_rows, tile_ref, sum_ref, dq_t, dk, dv,
    )
    diagonal_sums(sum_ref, u_ref, own, bk)

    def pack(b, _):
        rows = blk(b, 256)
        dq = turn(dq_t[:, rows])
        pieces = []
        for h in range(own):
            pieces += [dq[:, h * 64 : h * 64 + 64], dk[h, rows, :], dv[h, rows, :]]
        dx_ref[rows, :] = jnp.concatenate(pieces, axis=1).astype(jnp.bfloat16)
        return 0

    lax.fori_loop(0, x_ref.shape[0] // 256, pack, 0)


def cross_backward_kernel(
    own, bk, lim_ref, rows_ref, q_ref, kv_ref, do_ref, ot_ref, lse_ref, dq_ref, dkv_ref,
    q_t, q_rows, k_t, k_rows, v_rows, do_t, do_rows, dq_t, dk, dv,
):
    unpack(q_ref, own, 64, [(q_rows, 0)], [(q_t, 0)], 0)
    unpack(kv_ref, own, 128, [(k_rows, 0), (v_rows, 1)], [(k_t, 0)], 0)
    unpack(do_ref, own, 64, [(do_rows, 0)], [(do_t, 0)], 0)
    backward_body(
        own, bk, False, lim_ref, rows_ref, do_ref, ot_ref, lse_ref,
        q_t, q_rows, k_t, k_rows, v_rows, do_t, do_rows, None, None, dq_t, dk, dv,
    )

    def pack_q(b, _):
        rows = blk(b, 256)
        dq_ref[rows, :] = turn(dq_t[:, rows]).astype(jnp.bfloat16)
        return 0

    def pack_kv(b, _):
        rows = blk(b, 256)
        pieces = []
        for h in range(own):
            pieces += [dk[h, rows, :], dv[h, rows, :]]
        dkv_ref[rows, :] = jnp.concatenate(pieces, axis=1).astype(jnp.bfloat16)
        return 0

    lax.fori_loop(0, q_ref.shape[0] // 256, pack_q, 0)
    lax.fori_loop(0, kv_ref.shape[0] // 256, pack_kv, 0)


SMEM = pl.BlockSpec(memory_space=pltpu.SMEM)
VMEM = pl.BlockSpec(memory_space=pltpu.VMEM)
bf16, f32 = jnp.bfloat16, jnp.float32


def call(body, name, operands, outs, scratch, flops):
    size = sum(v.size * v.dtype.itemsize for v in operands)
    return pl.pallas_call(
        body,
        name=name,
        out_shape=[jax.ShapeDtypeStruct(s, d) for s, d in outs],
        in_specs=[SMEM] + [VMEM] * (len(operands) - 1),
        out_specs=[VMEM] * len(outs),
        scratch_shapes=[pltpu.VMEM(s, d) for s, d in scratch],
        compiler_params=pltpu.CompilerParams(vmem_limit_bytes=40 << 20),
        cost_estimate=pl.CostEstimate(flops=0, bytes_accessed=size, transcendentals=0),
    )(*operands)


def self_forward(limits, rows, ext, x, bk=256):
    length, own = x.shape[0], x.shape[1] // 192
    return call(
        functools.partial(self_forward_kernel, own, bk),
        "self_forward",
        [limits, rows, ext, x],
        [((length, own * 64), bf16), ((own * 64, length), f32), ((own, length), f32)],
        [
            ((own, 64, length), bf16),
            ((own, length, 64), bf16),
            ((own, 64, length), bf16),
            ((own, tile_count(bk), bk, BQ), f32),
        ],
        length * length * own * 64,
    )


def cross_forward(limits, rows, q, kv, bk=256):
    length, own, keys = q.shape[0], q.shape[1] // 64, kv.shape[0]
    return call(
        functools.partial(cross_forward_kernel, own, bk),
        "cross_forward",
        [limits, rows, q, kv],
        [((length, own * 64), bf16), ((own * 64, length), f32), ((own, length), f32)],
        [((own, 64, length), bf16), ((own, keys, 64), bf16), ((own, 64, keys), bf16)],
        length * keys * own * 128,
    )


def self_backward(limits, rows, ext, x, grad, o_t, lse, bk=256):
    length, own = x.shape[0], x.shape[1] // 192
    return call(
        functools.partial(self_backward_kernel, own, bk),
        "self_backward",
        [limits, rows, ext, x, grad, o_t, lse],
        [((length, own * 192), bf16), ((own, tile_count(bk), BQ + bk), f32)],
        [
            ((own, 64, length), bf16),
            ((own, length, 64), bf16),
            ((own, 64, length), bf16),
            ((own, length, 64), bf16),
            ((own, length, 64), bf16),
            ((own, 64, length), bf16),
            ((own, length, 64), bf16),
            ((own, tile_count(bk), bk, BQ), f32),
            ((own, tile_count(bk), bk, BQ), f32),
            ((own * 64, length), f32),
            ((own, length, 64), f32),
            ((own, length, 64), f32),
        ],
        length * length * own * 160,
    )


def cross_backward(limits, rows, q, kv, grad, o_t, lse, bk=256):
    length, own, keys = q.shape[0], q.shape[1] // 64, kv.shape[0]
    return call(
        functools.partial(cross_backward_kernel, own, bk),
        "cross_backward",
        [limits, rows, q, kv, grad, o_t, lse],
        [((length, own * 64), bf16), ((keys, own * 128), bf16)],
        [
            ((own, 64, length), bf16),
            ((own, length, 64), bf16),
            ((own, 64, keys), bf16),
            ((own, keys, 64), bf16),
            ((own, keys, 64), bf16),
            ((own, 64, length), bf16),
            ((own, length, 64), bf16),
            ((own * 64, length), f32),
            ((own, keys, 64), f32),
            ((own, keys, 64), f32),
        ],
        length * keys * own * 320,
    )


MESH = pl.DeviceIdType.MESH


def ring_place(index, n):
    z, x = index // 2, index % 2
    return z + x * (n - 1 - 2 * z)


def ring_index(place, n):
    x = place // (n // 2)
    z = place + x * (n - 1 - 2 * place)
    return 2 * z + x


def ring_greet(n, others):
    place = ring_place(lax.axis_index("seq"), n)
    right = ring_index((place + 1) % n, n)
    left = ring_index((place + n - 1) % n, n)
    barrier = pltpu.get_barrier_semaphore()
    for neighbour in (left, right):
        pl.semaphore_signal(barrier, inc=1, device_id={"seq": neighbour}, device_id_type=MESH)
    for other in others:
        pl.semaphore_signal(barrier, inc=1, device_id={"fsdp": other}, device_id_type=MESH)
    pl.semaphore_wait(barrier, 2 + len(others))
    return place, right, left


def ring_cut(shape, split, n):
    rows, cols = shape[0] // n, shape[1]
    return (rows, cols // split) if split > 0 else (rows // -split, cols)


def ring_window(ref, shape, split, n, piece, chunk):
    whole = shape[0] // n
    rows, cols = ring_cut(shape, split, n)
    if split > 0:
        return ref.at[pl.ds(chunk * whole, rows), pl.ds(piece * cols, cols)]
    return ref.at[pl.ds(chunk * whole + piece * rows, rows), :]


def ring_kernel(n, splits, *refs):
    count = len(splits)
    x_refs, y_refs, slots = refs[:count], refs[count : 2 * count], refs[2 * count : 3 * count]
    send_sem, recv_sem = refs[3 * count :]
    place, right, left = ring_greet(n, [])
    streams = [(k, piece, piece % 2) for k in range(count) for piece in range(abs(splits[k]))]

    def window(ref, k, piece, chunk):
        return ring_window(ref, x_refs[k].shape, splits[k], n, piece, chunk)

    def chunk_at(down, step):
        return (place + 1 + step) % n if down else (place + 2 * n - 1 - step) % n

    copies = {}

    def start(number, step, src, dst, down):
        copies[number, step] = pltpu.make_async_remote_copy(
            src_ref=src,
            dst_ref=dst,
            send_sem=send_sem.at[number, step],
            recv_sem=recv_sem.at[number, step],
            device_id={"seq": left if down else right},
            device_id_type=MESH,
        )
        copies[number, step].start()

    for number, (k, piece, down) in enumerate(streams):
        start(number, 0, window(x_refs[k], k, piece, place), window(slots[k], k, piece, 0), down)
    for step in range(n - 1):
        for number, (k, piece, down) in enumerate(streams):
            copies[number, step].wait_recv()
            chunk = chunk_at(down, step)
            mine = window(x_refs[k], k, piece, chunk)
            landed = window(slots[k], k, piece, step)
            total = landed[...].astype(jnp.float32) + mine[...].astype(jnp.float32)
            if step < n - 2:
                landed[...] = total.astype(jnp.bfloat16)
                start(number, step + 1, landed, window(slots[k], k, piece, step + 1), down)
            else:
                done = window(y_refs[k], k, piece, chunk)
                done[...] = total.astype(jnp.bfloat16)
                start(number, n - 1, done, done, down)
    for step in range(n - 1):
        for number, (k, piece, down) in enumerate(streams):
            copies[number, n - 1 + step].wait_recv()
            if step < n - 2:
                done = window(y_refs[k], k, piece, chunk_at(down, n - 1 + step))
                start(number, n + step, done, done, down)
    for one in copies.values():
        one.wait_send()


def ring_call(body, name, arrays, outs, scratch, ident):
    size = sum(v.size * 2 for v in arrays)
    return pl.pallas_call(
        body,
        name=name,
        out_shape=[jax.ShapeDtypeStruct(s, d) for s, d in outs],
        in_specs=[pl.BlockSpec(memory_space=pltpu.VMEM)] * len(arrays),
        out_specs=[pl.BlockSpec(memory_space=pltpu.VMEM)] * len(outs),
        scratch_shapes=scratch,
        compiler_params=pltpu.CompilerParams(
            collective_id=ident, has_side_effects=True, vmem_limit_bytes=48 << 20
        ),
        cost_estimate=pl.CostEstimate(flops=0, bytes_accessed=60 * size, transcendentals=0),
    )(*arrays)


def ring_total(arrays, splits, ident):
    n = lax.axis_size("seq")
    streams = sum(abs(s) for s in splits)
    return ring_call(
        functools.partial(ring_kernel, n, splits),
        "ring_total",
        arrays,
        [(v.shape, jnp.bfloat16) for v in arrays],
        [pltpu.VMEM((v.shape[0] // n * (n - 1), v.shape[1]), jnp.bfloat16) for v in arrays]
        + [pltpu.SemaphoreType.DMA((streams, 2 * n - 2))] * 2,
        ident,
    )


def units_kernel(
    n, fan, x_ref, part_ref, inner_ref, outer_ref, sum_ref, landed,
    swap_send, swap_recv, own_sem, send_sem, recv_sem, part_send, part_recv,
):
    s, me = lax.axis_index("seq"), lax.axis_index("fsdp")
    rows, width = x_ref.shape[0] // 3, x_ref.shape[1]
    cols = width // fan
    block = 2 * fan * rows
    place, right, left = ring_greet(n, [(me + far) % fan for far in range(1, fan)])
    moves = []
    for far in range(fan):
        target = (me + far) % fan
        for half in range(2):
            src = x_ref.at[pl.ds(half * rows, rows), pl.ds(pl.multiple_of(target * cols, 128), cols)]
            dst = inner_ref.at[pl.ds(s * block + (me * 2 + half) * rows, rows), :]
            if far:
                one = pltpu.make_async_remote_copy(
                    src_ref=src,
                    dst_ref=dst,
                    send_sem=swap_send.at[far, half],
                    recv_sem=swap_recv.at[far, half],
                    device_id={"fsdp": target},
                    device_id_type=MESH,
                )
            else:
                one = pltpu.make_async_copy(src, dst, own_sem.at[half])
            one.start()
            moves.append(one)
    mine = pltpu.make_async_copy(
        x_ref.at[pl.ds(2 * rows, rows), :], outer_ref.at[pl.ds(s * rows, rows), :], own_sem.at[2]
    )
    mine.start()
    copies = {}
    outs = ((outer_ref, (n * rows, width), 2), (inner_ref, (n * block, cols), -2))

    def start(k, piece, step):
        ref, shape, split = outs[k]
        chunk = ring_index((place + step) % n if piece else (place + n - step) % n, n)
        view = ring_window(ref, shape, split, n, piece, chunk)
        copies[k, piece, step] = pltpu.make_async_remote_copy(
            src_ref=view,
            dst_ref=view,
            send_sem=send_sem.at[2 * k + piece, step],
            recv_sem=recv_sem.at[2 * k + piece, step],
            device_id={"seq": left if piece else right},
            device_id_type=MESH,
        )
        copies[k, piece, step].start()

    tokens = sum_ref.shape[0]
    parts = []
    for far in range(1, fan):
        target = (me + far) % fan
        one = pltpu.make_async_remote_copy(
            src_ref=part_ref.at[pl.ds(target * tokens, tokens), :],
            dst_ref=landed.at[far],
            send_sem=part_send.at[far],
            recv_sem=part_recv.at[far],
            device_id={"fsdp": target},
            device_id_type=MESH,
        )
        one.start()
        parts.append(one)
    mine.wait()
    start(0, 0, 0)
    start(0, 1, 0)
    for one in moves:
        one.wait()
    start(1, 0, 0)
    start(1, 1, 0)
    for step in range(n - 1):
        for k in range(2):
            for piece in range(2):
                copies[k, piece, step].wait_recv()
                if step < n - 2:
                    start(k, piece, step + 1)
    total = part_ref[pl.ds(pl.multiple_of(me * tokens, tokens), tokens), :].astype(jnp.float32)
    for far in range(1, fan):
        parts[far - 1].wait()
        total = total + landed[far].astype(jnp.float32)
    sum_ref[...] = total
    for one in copies.values():
        one.wait_send()


def units_total(grads, part, ident):
    n, fan = lax.axis_size("seq"), lax.axis_size("fsdp")
    rows, width = grads.shape[0] // 3, grads.shape[1]
    tokens = part.shape[0] // fan
    sems = lambda *shape: pltpu.SemaphoreType.DMA(shape)
    return ring_call(
        functools.partial(units_kernel, n, fan),
        "units_total",
        [grads, part],
        [
            ((n * 2 * fan * rows, width // fan), jnp.bfloat16),
            ((n * rows, width), jnp.bfloat16),
            ((tokens, part.shape[1]), jnp.float32),
        ],
        [pltpu.VMEM((fan, tokens, part.shape[1]), jnp.bfloat16), sems(fan, 2), sems(fan, 2), sems(3)]
        + [sems(4, n - 1), sems(4, n - 1), sems(fan), sems(fan)],
        ident,
    )


def team(n):
    s, f = lax.axis_index("seq"), lax.axis_index("fsdp")
    half = s // (n // 2)
    away = (half + f) % 2
    return f // 2, half, (s + away * (n // 2)) % n


def swap_kernel(n, fan, count, fars, fresh, *refs):
    given = count + (len(fars) > 0) + (0 if fresh else 2)
    x_refs, y_refs = refs[:count], refs[given : given + count]
    sems = refs[given + count + (2 if fars else 0) :]
    send_sem, recv_sem, own_sem = sems[:3]
    pair, half, rank = team(n)
    me = lax.axis_index("fsdp")

    def device(other):
        away = (other // (n // 2) + half) % 2
        return {"seq": (other + away * (n // 2)) % n, "fsdp": 2 * pair + (half + away) % 2}

    barrier = pltpu.get_barrier_semaphore()
    for j in range(1, n):
        pl.semaphore_signal(barrier, inc=1, device_id=device((rank + j) % n), device_id_type=MESH)
    travel = [far for far in fars if far]
    for far in travel:
        pl.semaphore_signal(barrier, inc=1, device_id={"fsdp": (me + fan - far) % fan}, device_id_type=MESH)
    pl.semaphore_wait(barrier, n - 1 + len(travel))
    copies = []
    for k in range(count):
        for j in range(1, n):
            other = (rank + j) % n
            one = pltpu.make_async_remote_copy(
                src_ref=x_refs[k].at[other],
                dst_ref=y_refs[k].at[rank],
                send_sem=send_sem.at[k, j],
                recv_sem=recv_sem.at[k, j],
                device_id=device(other),
                device_id_type=MESH,
            )
            one.start()
            copies.append(one)
    for k in range(count):
        one = pltpu.make_async_copy(x_refs[k].at[rank], y_refs[k].at[rank], own_sem.at[k])
        one.start()
        copies.append(one)
    if fars:
        w_ref, halves = refs[count], refs[given + count : given + count + 2]
        far_send, far_recv, far_own, stage = sems[3:]
        rest = []
        units, cols = halves[0].shape[0], w_ref.shape[1]
        for i, far in enumerate(fars):
            target = (me + far) % fan
            for part in range(2):
                src = w_ref.at[pl.ds((part * fan + target) * units, units), :]
                dst = halves[part].at[:, pl.ds(pl.multiple_of(me * cols, 128), cols)]
                if far:
                    one = pltpu.make_async_remote_copy(
                        src_ref=src,
                        dst_ref=dst,
                        send_sem=far_send.at[i, part],
                        recv_sem=far_recv.at[i, part],
                        device_id={"fsdp": target},
                        device_id_type=MESH,
                    )
                else:
                    one = pltpu.make_async_copy(src, stage.at[part], far_own.at[0, part])
                    rest.append((one, pltpu.make_async_copy(stage.at[part], dst, far_own.at[1, part])))
                one.start()
                if far:
                    copies.append(one)
        for inward, outward in rest:
            inward.wait()
            outward.start()
            copies.append(outward)
    for one in copies:
        one.wait()


def swap(arrays, ident, fars=(), given=None, halves=None):
    n, fan = lax.axis_size("seq"), lax.axis_size("fsdp")
    count = len(arrays)
    size = sum(v.size * 2 for v in arrays)
    operands, outs, alias = list(arrays), [jax.ShapeDtypeStruct(v.shape, v.dtype) for v in arrays], {}
    scratch = [
        pltpu.SemaphoreType.DMA((count, n)),
        pltpu.SemaphoreType.DMA((count, n)),
        pltpu.SemaphoreType.DMA((count,)),
    ]
    if fars:
        operands.append(given)
        shape = (given.shape[0] // (2 * fan), given.shape[1] * fan)
        outs += [jax.ShapeDtypeStruct(shape, given.dtype)] * 2
        scratch += [pltpu.SemaphoreType.DMA((len(fars), 2))] * 2 + [
            pltpu.SemaphoreType.DMA((2, 2)),
            pltpu.VMEM((2, given.shape[0] // (2 * fan), given.shape[1]), given.dtype),
        ]
        if halves is not None:
            operands += list(halves)
            alias = {count + 1: count, count + 2: count + 1}
    return pl.pallas_call(
        functools.partial(swap_kernel, n, fan, count, fars, not fars or halves is None),
        name="swap",
        out_shape=outs,
        in_specs=[pl.BlockSpec(memory_space=pl.ANY)] * len(operands),
        out_specs=[pl.BlockSpec(memory_space=pl.ANY)] * len(outs),
        scratch_shapes=scratch,
        input_output_aliases=alias,
        compiler_params=pltpu.CompilerParams(collective_id=ident, has_side_effects=True),
        cost_estimate=pl.CostEstimate(flops=0, bytes_accessed=size, transcendentals=0),
    )(*operands)


def norm_apply(value, gain):
    return value * lax.rsqrt(jnp.mean(value * value, axis=-1, keepdims=True) + EPS) * gain


def norm_back(value, gain, grad):
    _, pull = jax.vjp(norm_apply, value, gain)
    return pull(grad)


def gate_mix(gate, up):
    return jax.nn.gelu(gate, approximate=True) * up


def counts_below(ids, values):
    total = jnp.zeros_like(values)
    for doc in range(DOCS):
        total = total + jnp.where(values > doc, jnp.sum((ids == doc).astype(jnp.int32)), 0)
    return total


def change_home(value):
    n, fan = lax.axis_size("seq"), lax.axis_size("fsdp")
    pairs = []
    for s in range(n):
        for f in range(fan):
            away = (s // (n // 2) + f) % 2
            target = ((s + n // 2) % n, f ^ 1) if away else (s, f)
            pairs.append((s * fan + f, target[0] * fan + target[1]))
    return lax.ppermute(value, ("seq", "fsdp"), pairs)


def spread(blocks):
    fan, me = lax.axis_size("fsdp"), lax.axis_index("fsdp")
    result = blocks
    for far in range(1, fan):
        block = lax.dynamic_index_in_dim(blocks, (me + far) % fan, 0, True)
        block = lax.ppermute(block, "fsdp", [(f, (f + far) % fan) for f in range(fan)])
        result = lax.dynamic_update_slice_in_dim(result, block, (me - far) % fan, 0)
    return result


def flat(blocks):
    return jnp.transpose(blocks, (1, 0, 2)).reshape(blocks.shape[1], -1)


def by_rows(value):
    return with_layout_constraint(value, Layout(major_to_minor=tuple(range(value.ndim))))


def scatter(grad):
    return lax.psum_scatter(grad, "fsdp", scatter_dimension=0, tiled=True)


def over_seq(arrays, splits, ident):
    n = lax.axis_size("seq")
    if all(
        v.shape[0] % (8 * n) == 0
        and ring_cut(v.shape, s, n)[0] % 8 == 0
        and v.shape[1] % (128 * max(s, 1)) == 0
        for v, s in zip(arrays, splits)
    ):
        return ring_total(arrays, splits, ident)
    return [lax.psum(v, "seq") for v in arrays]


def shards(
    layer_in, encoder, decoder_ids, encoder_ids, rel_buckets,
    norm_self, self_qkv, self_out, rel_table, norm_cross, cross_q, cross_kv, cross_out, norm_ff, ff_in, ff_out,
    cotangent,
):
    seqs, local, width = layer_in.shape
    enc_local = encoder.shape[1]
    parts = lax.axis_size("seq")
    heads = self_qkv.shape[1]
    dh = self_qkv.shape[2] // 3
    own = heads // parts
    rows = seqs * local
    buckets, table_own = rel_table.shape
    length, keys = local * parts, enc_local * parts
    gather = lambda v: lax.all_gather(v, "fsdp", axis=0, tiled=True)

    fan = lax.axis_size("fsdp")
    units = ff_in.shape[1] // (2 * fan)
    part = norm_self.shape[0]
    pair, half, rank = team(parts)

    qkv_w = gather(self_qkv)
    small = jnp.concatenate([norm_self, norm_cross, norm_ff, rel_table.reshape(-1)])
    small = lax.all_gather(small, "fsdp", axis=0, tiled=False)
    early = by_rows(jnp.stack([self_out, cross_q, *jnp.split(cross_kv.reshape(-1, 2 * width), 2, axis=1)]))
    small, early = lax.optimization_barrier((small, early))
    early = lax.all_gather(early, "fsdp", axis=1, tiled=True)
    both_ids = jnp.concatenate([decoder_ids.reshape(-1), encoder_ids.reshape(-1)])
    both_ids = change_home(jnp.pad(both_ids, (0, 1024 - local - enc_local)).reshape(8, 128))
    (both_ids,) = swap([jnp.broadcast_to(both_ids[None], (parts, 8, 128))], 13)
    home = change_home(layer_in.reshape(rows, width))
    inner_t = ff_in.T
    early = by_rows(early)
    mix_self = early[0].reshape(parts, own * dh, width)
    query_w = early[1].reshape(width, parts, own * dh)
    pairs_w = early[2:]

    gain_first, gain_second, gain_third = (
        small[:, i * part : (i + 1) * part].reshape(width).astype(f32) for i in range(3)
    )
    table = jnp.transpose(small[:, 3 * part :].reshape(-1, buckets, table_own), (1, 0, 2)).reshape(buckets, heads)
    both_ids = both_ids.reshape(parts, 1024)
    ids = both_ids[:, :local].reshape(length)
    enc_ids = both_ids[:, local : local + enc_local].reshape(keys)

    first_seen = counts_below(ids, ids)
    enc_first = counts_below(enc_ids, ids)
    enc_last = counts_below(enc_ids, ids + 1)
    blocks = length // BQ
    bk = 256
    self_rows = jnp.broadcast_to(first_seen[None], (8, length))
    cross_rows = jnp.concatenate([enc_first[None], enc_last[None], jnp.zeros((6, length), jnp.int32)])
    self_limits = jnp.stack(
        [first_seen[::BQ] // bk, (jnp.arange(blocks, dtype=jnp.int32) + 1) * (BQ // bk)]
    )
    cross_limits = jnp.stack([enc_first[::BQ] // bk, (enc_last[BQ - 1 :: BQ] + bk - 1) // bk])

    first_head = rank * own
    table_mine = lax.dynamic_slice_in_dim(table.astype(f32), first_head, own, 1)
    near = rel_buckets[:REACH]
    onehot = (near[:, None] == jnp.arange(buckets, dtype=jnp.int32)[None, :]).astype(f32)
    bias = jnp.einsum("ln,ng->gl", onehot, table_mine, precision=HIGH)
    ext = jnp.concatenate(
        [jnp.full((own, BQ), MASKED, f32), bias, jnp.zeros((own, BQ), f32)], axis=1
    )

    qkv_w, home, inner_t, ext, self_rows, cross_rows, self_limits, cross_limits = lax.optimization_barrier(
        (qkv_w, home, inner_t, ext, self_rows, cross_rows, self_limits, cross_limits)
    )
    qkv_w = qkv_w.reshape(width, parts, own * 3 * dh)

    stream = home.astype(f32)
    normed_first = norm_apply(stream, gain_first).astype(bf16)
    qkv_tok = jnp.einsum("td,dge->gte", normed_first, qkv_w, preferred_element_type=f32).astype(bf16)
    qkv_tok, cross_out, cotangent, encoder = lax.optimization_barrier((qkv_tok, cross_out, cotangent, encoder))
    mix_cross = gather(cross_out).reshape(parts, own * dh, width)
    others = change_home(jnp.concatenate([cotangent.reshape(rows, width), encoder.reshape(-1, width)]))
    grad_low, enc_flat = others[:rows], others[rows:]
    (qkv,) = swap([qkv_tok], 10)
    qkv = qkv.reshape(length, own * 3 * dh)
    out_self, self_t, self_lse = self_forward(self_limits, self_rows, ext, qkv)
    out_self, grad_low = lax.optimization_barrier((out_self, grad_low))
    grad_group = gather(grad_low)
    by_kernel = (width // fan) % 128 == 0
    fars = [tuple(far for far in range(fan) if (far + 2) % 3 == i) if by_kernel else () for i in range(3)]
    self_tok, *halves = swap([out_self.reshape(parts, local, own * dh)], 14, fars[0], inner_t)
    after_self = stream + jnp.einsum("gtc,gcd->td", self_tok, mix_self, preferred_element_type=f32)
    normed_second = norm_apply(after_self, gain_second).astype(bf16)
    query_tok = jnp.einsum("td,dgc->gtc", normed_second, query_w, preferred_element_type=f32).astype(bf16)
    pairs_tok = jnp.einsum(
        "td,sdge->sgte", enc_flat, pairs_w.reshape(2, width, parts // 2, -1), preferred_element_type=f32
    )
    pairs_tok = pairs_tok.astype(bf16).reshape(parts, enc_local, -1)
    query_cross, pairs, *halves = swap([query_tok, pairs_tok], 15, fars[1], inner_t, halves)
    query_cross, pairs = query_cross.reshape(length, own * dh), pairs.reshape(keys, own * 2 * dh)
    out_cross, cross_t, cross_lse = cross_forward(cross_limits, cross_rows, query_cross, pairs)
    cross_tok, *halves = swap([out_cross.reshape(parts, local, own * dh)], 16, fars[2], inner_t, halves)
    if not by_kernel:
        halves = spread(jnp.transpose(inner_t.reshape(2, fan, units, -1), (1, 0, 2, 3)))
        halves = [jnp.transpose(halves[:, i], (1, 0, 2)).reshape(units, width) for i in range(2)]
    gate_t, up_t = halves
    after_cross = after_self + jnp.einsum("gtc,gcd->td", cross_tok, mix_cross, preferred_element_type=f32)
    normed_third = norm_apply(after_cross, gain_third).astype(bf16)
    normed_group = gather(normed_third)
    gate = jnp.einsum("td,fd->tf", normed_group, gate_t, preferred_element_type=f32)
    up = jnp.einsum("td,fd->tf", normed_group, up_t, preferred_element_type=f32)
    hidden = gate_mix(gate, up).astype(bf16)

    grad_hidden = jnp.einsum("td,fd->tf", grad_group, ff_out, preferred_element_type=f32)
    _, pull_mix = jax.vjp(gate_mix, gate, up)
    grad_gate, grad_up = (g.astype(bf16) for g in pull_mix(grad_hidden))
    grad_third_in = jnp.dot(grad_gate, gate_t, preferred_element_type=f32) + jnp.dot(
        grad_up, up_t, preferred_element_type=f32
    )
    grad_third_in = scatter(grad_third_in.astype(bf16))
    outer_part = jnp.dot(hidden, ff_out, preferred_element_type=f32).astype(bf16)
    grad_units = [
        jnp.einsum("tf,td->fd", g, y, preferred_element_type=f32).astype(bf16)
        for g, y in ((grad_gate, normed_group), (grad_up, normed_group), (hidden, grad_group))
    ]
    grad_third_in, outer_part, grad_units = lax.optimization_barrier((grad_third_in, outer_part, grad_units))
    if by_kernel:
        grad_units = jnp.stack([g.reshape(parts, units // parts, width) for g in grad_units], axis=1)
        part_units = lax.psum_scatter(
            grad_units.reshape(3 * units, width), "seq", scatter_dimension=0, tiled=True
        )
    grad_third_in = grad_third_in.astype(f32)
    grad_from_third, grad_gain_third = norm_back(after_cross, gain_third, grad_third_in)
    grad_middle = grad_low.astype(f32) + grad_from_third
    middle_low = grad_middle.astype(bf16)
    grad_mix_cross = jnp.einsum("gtc,td->gcd", cross_tok, middle_low, preferred_element_type=f32)
    grad_cross_tok = jnp.einsum("td,gcd->gtc", middle_low, mix_cross, preferred_element_type=f32).astype(bf16)
    (grad_cross,) = swap([grad_cross_tok], 11)
    grad_cross = grad_cross.reshape(length, own * dh)
    grad_query, grad_pairs = cross_backward(
        cross_limits, cross_rows, query_cross, pairs, grad_cross, cross_t, cross_lse
    )
    grad_query_tok, grad_pairs_tok = swap(
        [grad_query.reshape(parts, local, own * dh), grad_pairs.reshape(parts, enc_local, own * 2 * dh)], 12
    )
    grad_query_tok, grad_pairs_tok = flat(grad_query_tok), flat(grad_pairs_tok)
    grad_query_w = jnp.einsum("td,te->de", normed_second, grad_query_tok, preferred_element_type=f32)
    grad_second_in = jnp.einsum("te,de->td", grad_query_tok, query_w.reshape(width, -1), preferred_element_type=f32)
    grad_pairs_w = jnp.einsum("td,te->de", enc_flat, grad_pairs_tok, preferred_element_type=f32)
    grad_encoder = sum(
        jnp.einsum("te,de->td", grad_pairs_tok[:, i * width : (i + 1) * width], pairs_w[i], preferred_element_type=f32)
        for i in range(2)
    )
    grad_from_second, grad_gain_second = norm_back(after_self, gain_second, grad_second_in)
    grad_upper = grad_middle + grad_from_second
    upper_low = grad_upper.astype(bf16)
    grad_mix_self = jnp.einsum("gtc,td->gcd", self_tok, upper_low, preferred_element_type=f32)
    grad_self_tok = jnp.einsum("td,gcd->gtc", upper_low, mix_self, preferred_element_type=f32).astype(bf16)
    grad_mid = jnp.concatenate(
        [
            grad_query_w.astype(bf16),
            grad_pairs_w.astype(bf16),
            grad_mix_cross.reshape(width, width).astype(bf16),
            grad_mix_self.reshape(width, width).astype(bf16),
        ],
        axis=1,
    )
    grad_self_tok, grad_mid = lax.optimization_barrier((grad_self_tok, grad_mid))
    part_mid = scatter(grad_mid)
    (grad_self,) = swap([grad_self_tok], 11)
    grad_self = grad_self.reshape(length, own * dh)
    grad_qkv, tile_sums = self_backward(self_limits, self_rows, ext, qkv, grad_self, self_t, self_lse)
    (grad_qkv_tok,) = swap([grad_qkv.reshape(parts, local, own * 3 * dh)], 10)
    grad_qkv_tok = flat(grad_qkv_tok)
    grad_qkv_w = jnp.einsum("td,te->de", normed_first, grad_qkv_tok, preferred_element_type=f32)
    grad_first_in = jnp.einsum("te,de->td", grad_qkv_tok, qkv_w.reshape(width, -1), preferred_element_type=f32)
    grad_from_first, grad_gain_first = norm_back(stream, gain_first, grad_first_in)
    grad_layer_in = (grad_upper + grad_from_first).astype(bf16)
    if not by_kernel:
        part_units = grad_units
    bucket_line = jnp.concatenate(
        [jnp.full((BQ,), -1, jnp.int32), near, jnp.full((BQ + bk,), -1, jnp.int32)]
    )
    by_tile = jnp.stack([bucket_line[t * bk + 1 : t * bk + 1 + BQ + bk] for t in range(tile_count(bk))])
    in_bucket = (by_tile[:, :, None] == jnp.arange(buckets, dtype=jnp.int32)).astype(f32)
    by_bucket = jnp.einsum("twn,gtw->ng", in_bucket, tile_sums, precision=HIGH)
    grad_table = lax.dynamic_update_slice_in_dim(jnp.zeros((buckets, heads), f32), by_bucket, first_head, 1)

    gains = jnp.concatenate(
        [g.reshape(-1, part) for g in (grad_gain_first, grad_gain_second, grad_gain_third)], axis=1
    )
    tables = jnp.transpose(grad_table.reshape(buckets, -1, table_own), (1, 0, 2)).reshape(-1, buckets * table_own)
    small_grads = lax.psum(jnp.concatenate([gains, tables], axis=1).astype(bf16), "fsdp")
    small_grads = lax.dynamic_index_in_dim(small_grads, lax.axis_index("fsdp"), 0, False)
    small_size = small_grads.shape[0]
    small_grads = jnp.pad(small_grads, (0, parts * 1024 - small_size)).reshape(parts * 8, 128)
    going_home = jnp.concatenate([grad_layer_in, grad_encoder.astype(bf16)])
    going_home, small_grads, grad_qkv_w, part_units, part_mid = lax.optimization_barrier(
        (going_home, small_grads, grad_qkv_w.astype(bf16), part_units, part_mid)
    )
    part_last = scatter(grad_qkv_w)
    going_home = change_home(going_home)
    if by_kernel:
        total_inner, total_outer, outer_sum = units_total(part_units, outer_part, 0)
    else:
        grad_units = [lax.psum(g, "seq") for g in grad_units]
        total_inner = spread(jnp.transpose(jnp.stack(grad_units[:2]).reshape(2, units, fan, -1), (2, 0, 1, 3)))
        total_outer, outer_sum = grad_units[2], scatter(outer_part).astype(f32)
    total_mid, total_qkv, small_total = over_seq([part_mid, part_last, small_grads], (2, 2, 1), 1)
    layer_out = (after_cross + outer_sum).astype(bf16)
    layer_out, total_inner, total_outer, total_mid, total_qkv, going_home = lax.optimization_barrier(
        (layer_out, total_inner, total_outer, total_mid, total_qkv, going_home)
    )
    layer_out = change_home(layer_out).reshape(seqs, local, width)
    grad_layer_in = going_home[:rows].astype(f32).reshape(seqs, local, width)
    grad_encoder = going_home[rows:].astype(f32).reshape(seqs, enc_local, width)
    if by_kernel:
        total_inner = jnp.transpose(total_inner.reshape(parts, fan, 2, units // parts, -1), (4, 2, 1, 0, 3))
    else:
        total_inner = jnp.transpose(total_inner, (3, 1, 0, 2))
    total_inner = total_inner.reshape(-1, 2 * fan * units).astype(f32)
    total_outer, total_mid, total_qkv = (v.astype(f32) for v in (total_outer, total_mid, total_qkv))
    total_query, total_mix_cross = total_mid[:, :width], total_mid[:, 3 * width : 4 * width]
    total_pairs = total_mid[:, width : 3 * width].reshape(-1, heads, 2 * dh)
    total_mix_self, total_qkv = total_mid[:, 4 * width :], total_qkv.reshape(-1, heads, 3 * dh)
    mine = small_total.reshape(-1)[:small_size].astype(f32)
    total_gain_first, total_gain_second, total_gain_third = (mine[i * part : (i + 1) * part] for i in range(3))
    total_table = mine[3 * part :].reshape(buckets, table_own)
    return (
        layer_out, grad_layer_in, grad_encoder, total_gain_first, total_qkv, total_mix_self, total_table,
        total_gain_second, total_query, total_pairs, total_mix_cross, total_gain_third, total_inner, total_outer,
    )


def solution(mesh):
    in_specs = (
        P("fsdp", "seq", None), P("fsdp", "seq", None), P("fsdp", "seq"), P("fsdp", "seq"), P(),
        P("fsdp"), P("fsdp", None, None), P("fsdp", None), P(None, "fsdp"), P("fsdp"), P("fsdp", None),
        P("fsdp", None, None), P("fsdp", None), P("fsdp"), P("fsdp", None), P("fsdp", None),
        P("fsdp", "seq", None),
    )
    out_specs = (
        P("fsdp", "seq", None), P("fsdp", "seq", None), P("fsdp", "seq", None), P("fsdp"), P("fsdp", None, None),
        P("fsdp", None), P(None, "fsdp"), P("fsdp"), P("fsdp", None), P("fsdp", None, None), P("fsdp", None),
        P("fsdp"), P("fsdp", None), P("fsdp", None),
    )
    return jax.shard_map(shards, mesh=mesh, in_specs=in_specs, out_specs=out_specs, check_vma=False)
```

```python
import functools

import jax
import jax.numpy as jnp
from jax import lax
from jax.experimental import pallas as pl
from jax.experimental.layout import Layout, with_layout_constraint
from jax.experimental.pallas import tpu as pltpu
from jax.sharding import PartitionSpec as P

EPS = 1e-06
HIGH = lax.Precision.HIGHEST
MASKED = -1e30
DOCS = 4

BQ = 256
REACH = 1024


def blk(index, size):
    return pl.ds(pl.multiple_of(index * size, size), size)


def turn(value):
    return jnp.transpose(value.astype(jnp.float32), (1, 0))


def bias_tiles(ext_ref, tile_ref, own, bk):
    span = BQ + bk
    for h in range(own):
        for t in range(tile_ref.shape[1]):
            first = t * bk
            line = jnp.broadcast_to(ext_ref[h : h + 1, first : first + span], (bk, span))
            tile_ref[h, t] = pltpu.roll(line, 0, 1, stride=1, stride_axis=0)[:, bk:]


def tile_count(bk):
    return BQ // bk + REACH // bk


def unpack(ref, own, width, picks, flips, base):
    block = 256

    def one(b, _):
        rows = blk(b, block)
        value = ref[rows, :]
        if flips:
            flat = turn(value).astype(jnp.bfloat16)
            for target, piece in flips:
                for h in range(own):
                    at = h * width + piece * 64
                    target[base + h, :, rows] = flat[at : at + 64]
        for target, piece in picks:
            for h in range(own):
                at = h * width + piece * 64
                target[base + h, rows, :] = value[:, at : at + 64]
        return 0

    lax.fori_loop(0, ref.shape[0] // block, one, 0)


def dot(a, b):
    return jnp.dot(a, b, preferred_element_type=jnp.float32)


def score(own_index, key_tile, query_t, tile_ref, t, low, high, first_key):
    value = dot(key_tile, query_t)
    place = lax.broadcasted_iota(jnp.int32, value.shape, 0)
    keep = place >= low - first_key
    if high is not None:
        keep = keep & (place < high - first_key)
    else:
        value = value + tile_ref[own_index, t]
    return jnp.where(keep, value, MASKED)


def forward_body(own, bk, causal, lim_ref, rows_ref, q_t, k_rows, v_t, tile_ref, o_ref, ot_ref, lse_ref):
    length = o_ref.shape[0]

    def q_block(i, _):
        cols = blk(i, BQ)
        queries = [q_t[h, :, cols] for h in range(own)]
        low = rows_ref[0:1, cols]
        high = None if causal else rows_ref[1:2, cols]

        def k_block(j, carry):
            keys = blk(j, bk)
            t = i * (BQ // bk) - j + (BQ // bk - 1)
            out = []
            for h in range(own):
                top, total, acc = carry[h]
                s = score(h, k_rows[h, keys, :], queries[h], tile_ref, t, low, high, j * bk)
                new_top = jnp.maximum(top, jnp.max(s, axis=0, keepdims=True))
                p = jnp.exp(s - new_top)
                scale = jnp.exp(top - new_top)
                total = total * scale + jnp.sum(p, axis=0, keepdims=True)
                acc = acc * scale + dot(v_t[h, :, keys], p.astype(jnp.bfloat16))
                out.append((new_top, total, acc))
            return tuple(out)

        start = tuple(
            (
                jnp.full((1, BQ), MASKED, jnp.float32),
                jnp.zeros((1, BQ), jnp.float32),
                jnp.zeros((64, BQ), jnp.float32),
            )
            for _ in range(own)
        )
        ends = lax.fori_loop(lim_ref[0, i], lim_ref[1, i], k_block, start)
        for h in range(own):
            top, total, acc = ends[h]
            ot_ref[h * 64 : h * 64 + 64, cols] = acc / total
            lse_ref[h : h + 1, cols] = top + jnp.log(total)
        o_ref[cols, :] = turn(ot_ref[:, cols]).astype(jnp.bfloat16)
        return 0

    lax.fori_loop(0, length // BQ, q_block, 0)


def self_forward_kernel(own, bk, lim_ref, rows_ref, ext_ref, x_ref, o_ref, ot_ref, lse_ref, q_t, k_rows, v_t, tile_ref):
    bias_tiles(ext_ref, tile_ref, own, bk)
    unpack(x_ref, own, 192, [(k_rows, 1)], [(q_t, 0), (v_t, 2)], 0)
    forward_body(own, bk, True, lim_ref, rows_ref, q_t, k_rows, v_t, tile_ref, o_ref, ot_ref, lse_ref)


def cross_forward_kernel(own, bk, lim_ref, rows_ref, q_ref, kv_ref, o_ref, ot_ref, lse_ref, q_t, k_rows, v_t):
    unpack(q_ref, own, 64, [], [(q_t, 0)], 0)
    unpack(kv_ref, own, 128, [(k_rows, 0)], [(v_t, 1)], 0)
    forward_body(own, bk, False, lim_ref, rows_ref, q_t, k_rows, v_t, None, o_ref, ot_ref, lse_ref)


def backward_body(
    own, bk, causal, lim_ref, rows_ref, do_ref, ot_ref, lse_ref,
    q_t, q_rows, k_t, k_rows, v_rows, do_t, do_rows, tile_ref, sum_ref, dq_t, dk, dv,
):
    length = do_ref.shape[0]
    dk[...] = jnp.zeros_like(dk)
    dv[...] = jnp.zeros_like(dv)
    if causal:
        sum_ref[...] = jnp.zeros_like(sum_ref)

    def q_block(i, _):
        cols = blk(i, BQ)
        low = rows_ref[0:1, cols]
        high = None if causal else rows_ref[1:2, cols]
        per_head = []
        for h in range(own):
            grad_t = do_t[h, :, cols]
            delta = jnp.sum(
                grad_t.astype(jnp.float32) * ot_ref[h * 64 : h * 64 + 64, cols], axis=0, keepdims=True
            )
            per_head.append((q_t[h, :, cols], grad_t, delta, lse_ref[h : h + 1, cols]))

        def k_block(j, carry):
            keys = blk(j, bk)
            t = i * (BQ // bk) - j + (BQ // bk - 1)
            out = []
            for h in range(own):
                query_t, grad_t, delta, lse = per_head[h]
                s = score(h, k_rows[h, keys, :], query_t, tile_ref, t, low, high, j * bk)
                p = jnp.exp(s - lse)
                dp = dot(v_rows[h, keys, :], grad_t)
                ds = (p * (dp - delta)).astype(jnp.bfloat16)
                dv[h, keys, :] += dot(p.astype(jnp.bfloat16), do_rows[h, cols, :])
                dk[h, keys, :] += dot(ds, q_rows[h, cols, :])
                if causal:
                    sum_ref[h, t] += ds.astype(jnp.float32)
                out.append(carry[h] + dot(k_t[h, :, keys], ds))
            return tuple(out)

        ends = lax.fori_loop(
            lim_ref[0, i],
            lim_ref[1, i],
            k_block,
            tuple(jnp.zeros((64, BQ), jnp.float32) for _ in range(own)),
        )
        for h in range(own):
            dq_t[h * 64 : h * 64 + 64, cols] = ends[h]
        return 0

    lax.fori_loop(0, length // BQ, q_block, 0)


def diagonal_sums(sum_ref, u_ref, own, bk):
    flip = (
        lax.broadcasted_iota(jnp.int32, (bk, bk), 0) + lax.broadcasted_iota(jnp.int32, (bk, bk), 1) == bk - 1
    ).astype(jnp.float32)
    for h in range(own):
        for t in range(sum_ref.shape[1]):
            upside = jnp.dot(flip, sum_ref[h, t], precision=HIGH, preferred_element_type=jnp.float32)
            wide = jnp.concatenate([upside, jnp.zeros((bk, bk), jnp.float32)], axis=1)
            aligned = pltpu.roll(wide, 0, 1, stride=1, stride_axis=0)
            u_ref[h, t : t + 1, :] = jnp.sum(aligned, axis=0, keepdims=True)


def self_backward_kernel(
    own, bk, lim_ref, rows_ref, ext_ref, x_ref, do_ref, ot_ref, lse_ref, dx_ref, u_ref,
    q_t, q_rows, k_t, k_rows, v_rows, do_t, do_rows, tile_ref, sum_ref, dq_t, dk, dv,
):
    bias_tiles(ext_ref, tile_ref, own, bk)
    unpack(x_ref, own, 192, [(q_rows, 0), (k_rows, 1), (v_rows, 2)], [(q_t, 0), (k_t, 1)], 0)
    unpack(do_ref, own, 64, [(do_rows, 0)], [(do_t, 0)], 0)
    backward_body(
        own, bk, True, lim_ref, rows_ref, do_ref, ot_ref, lse_ref,
        q_t, q_rows, k_t, k_rows, v_rows, do_t, do_rows, tile_ref, sum_ref, dq_t, dk, dv,
    )
    diagonal_sums(sum_ref, u_ref, own, bk)

    def pack(b, _):
        rows = blk(b, 256)
        dq = turn(dq_t[:, rows])
        pieces = []
        for h in range(own):
            pieces += [dq[:, h * 64 : h * 64 + 64], dk[h, rows, :], dv[h, rows, :]]
        dx_ref[rows, :] = jnp.concatenate(pieces, axis=1).astype(jnp.bfloat16)
        return 0

    lax.fori_loop(0, x_ref.shape[0] // 256, pack, 0)


def cross_backward_kernel(
    own, bk, lim_ref, rows_ref, q_ref, kv_ref, do_ref, ot_ref, lse_ref, dq_ref, dkv_ref,
    q_t, q_rows, k_t, k_rows, v_rows, do_t, do_rows, dq_t, dk, dv,
):
    unpack(q_ref, own, 64, [(q_rows, 0)], [(q_t, 0)], 0)
    unpack(kv_ref, own, 128, [(k_rows, 0), (v_rows, 1)], [(k_t, 0)], 0)
    unpack(do_ref, own, 64, [(do_rows, 0)], [(do_t, 0)], 0)
    backward_body(
        own, bk, False, lim_ref, rows_ref, do_ref, ot_ref, lse_ref,
        q_t, q_rows, k_t, k_rows, v_rows, do_t, do_rows, None, None, dq_t, dk, dv,
    )

    def pack_q(b, _):
        rows = blk(b, 256)
        dq_ref[rows, :] = turn(dq_t[:, rows]).astype(jnp.bfloat16)
        return 0

    def pack_kv(b, _):
        rows = blk(b, 256)
        pieces = []
        for h in range(own):
            pieces += [dk[h, rows, :], dv[h, rows, :]]
        dkv_ref[rows, :] = jnp.concatenate(pieces, axis=1).astype(jnp.bfloat16)
        return 0

    lax.fori_loop(0, q_ref.shape[0] // 256, pack_q, 0)
    lax.fori_loop(0, kv_ref.shape[0] // 256, pack_kv, 0)


SMEM = pl.BlockSpec(memory_space=pltpu.SMEM)
VMEM = pl.BlockSpec(memory_space=pltpu.VMEM)
bf16, f32 = jnp.bfloat16, jnp.float32


def call(body, name, operands, outs, scratch, flops):
    size = sum(v.size * v.dtype.itemsize for v in operands)
    return pl.pallas_call(
        body,
        name=name,
        out_shape=[jax.ShapeDtypeStruct(s, d) for s, d in outs],
        in_specs=[SMEM] + [VMEM] * (len(operands) - 1),
        out_specs=[VMEM] * len(outs),
        scratch_shapes=[pltpu.VMEM(s, d) for s, d in scratch],
        compiler_params=pltpu.CompilerParams(vmem_limit_bytes=40 << 20),
        cost_estimate=pl.CostEstimate(flops=0, bytes_accessed=size, transcendentals=0),
    )(*operands)


def self_forward(limits, rows, ext, x, bk=256):
    length, own = x.shape[0], x.shape[1] // 192
    return call(
        functools.partial(self_forward_kernel, own, bk),
        "self_forward",
        [limits, rows, ext, x],
        [((length, own * 64), bf16), ((own * 64, length), f32), ((own, length), f32)],
        [
            ((own, 64, length), bf16),
            ((own, length, 64), bf16),
            ((own, 64, length), bf16),
            ((own, tile_count(bk), bk, BQ), f32),
        ],
        length * length * own * 64,
    )


def cross_forward(limits, rows, q, kv, bk=256):
    length, own, keys = q.shape[0], q.shape[1] // 64, kv.shape[0]
    return call(
        functools.partial(cross_forward_kernel, own, bk),
        "cross_forward",
        [limits, rows, q, kv],
        [((length, own * 64), bf16), ((own * 64, length), f32), ((own, length), f32)],
        [((own, 64, length), bf16), ((own, keys, 64), bf16), ((own, 64, keys), bf16)],
        length * keys * own * 128,
    )


def self_backward(limits, rows, ext, x, grad, o_t, lse, bk=256):
    length, own = x.shape[0], x.shape[1] // 192
    return call(
        functools.partial(self_backward_kernel, own, bk),
        "self_backward",
        [limits, rows, ext, x, grad, o_t, lse],
        [((length, own * 192), bf16), ((own, tile_count(bk), BQ + bk), f32)],
        [
            ((own, 64, length), bf16),
            ((own, length, 64), bf16),
            ((own, 64, length), bf16),
            ((own, length, 64), bf16),
            ((own, length, 64), bf16),
            ((own, 64, length), bf16),
            ((own, length, 64), bf16),
            ((own, tile_count(bk), bk, BQ), f32),
            ((own, tile_count(bk), bk, BQ), f32),
            ((own * 64, length), f32),
            ((own, length, 64), f32),
            ((own, length, 64), f32),
        ],
        length * length * own * 160,
    )


def cross_backward(limits, rows, q, kv, grad, o_t, lse, bk=256):
    length, own, keys = q.shape[0], q.shape[1] // 64, kv.shape[0]
    return call(
        functools.partial(cross_backward_kernel, own, bk),
        "cross_backward",
        [limits, rows, q, kv, grad, o_t, lse],
        [((length, own * 64), bf16), ((keys, own * 128), bf16)],
        [
            ((own, 64, length), bf16),
            ((own, length, 64), bf16),
            ((own, 64, keys), bf16),
            ((own, keys, 64), bf16),
            ((own, keys, 64), bf16),
            ((own, 64, length), bf16),
            ((own, length, 64), bf16),
            ((own * 64, length), f32),
            ((own, keys, 64), f32),
            ((own, keys, 64), f32),
        ],
        length * keys * own * 320,
    )


MESH = pl.DeviceIdType.MESH


def ring_place(index, n):
    z, x = index // 2, index % 2
    return z + x * (n - 1 - 2 * z)


def ring_index(place, n):
    x = place // (n // 2)
    z = place + x * (n - 1 - 2 * place)
    return 2 * z + x


def ring_greet(n, others):
    place = ring_place(lax.axis_index("seq"), n)
    right = ring_index((place + 1) % n, n)
    left = ring_index((place + n - 1) % n, n)
    barrier = pltpu.get_barrier_semaphore()
    for neighbour in (left, right):
        pl.semaphore_signal(barrier, inc=1, device_id={"seq": neighbour}, device_id_type=MESH)
    for other in others:
        pl.semaphore_signal(barrier, inc=1, device_id={"fsdp": other}, device_id_type=MESH)
    pl.semaphore_wait(barrier, 2 + len(others))
    return place, right, left


def ring_cut(shape, split, n):
    rows, cols = shape[0] // n, shape[1]
    return (rows, cols // split) if split > 0 else (rows // -split, cols)


def ring_window(ref, shape, split, n, piece, chunk):
    whole = shape[0] // n
    rows, cols = ring_cut(shape, split, n)
    if split > 0:
        return ref.at[pl.ds(chunk * whole, rows), pl.ds(piece * cols, cols)]
    return ref.at[pl.ds(chunk * whole + piece * rows, rows), :]


def ring_kernel(n, splits, *refs):
    count = len(splits)
    x_refs, y_refs, slots = refs[:count], refs[count : 2 * count], refs[2 * count : 3 * count]
    send_sem, recv_sem = refs[3 * count :]
    place, right, left = ring_greet(n, [])
    streams = [(k, piece, piece % 2) for k in range(count) for piece in range(abs(splits[k]))]

    def window(ref, k, piece, chunk):
        return ring_window(ref, x_refs[k].shape, splits[k], n, piece, chunk)

    def chunk_at(down, step):
        return (place + 1 + step) % n if down else (place + 2 * n - 1 - step) % n

    copies = {}

    def start(number, step, src, dst, down):
        copies[number, step] = pltpu.make_async_remote_copy(
            src_ref=src,
            dst_ref=dst,
            send_sem=send_sem.at[number, step],
            recv_sem=recv_sem.at[number, step],
            device_id={"seq": left if down else right},
            device_id_type=MESH,
        )
        copies[number, step].start()

    for number, (k, piece, down) in enumerate(streams):
        start(number, 0, window(x_refs[k], k, piece, place), window(slots[k], k, piece, 0), down)
    for step in range(n - 1):
        for number, (k, piece, down) in enumerate(streams):
            copies[number, step].wait_recv()
            chunk = chunk_at(down, step)
            mine = window(x_refs[k], k, piece, chunk)
            landed = window(slots[k], k, piece, step)
            total = landed[...].astype(jnp.float32) + mine[...].astype(jnp.float32)
            if step < n - 2:
                landed[...] = total.astype(jnp.bfloat16)
                start(number, step + 1, landed, window(slots[k], k, piece, step + 1), down)
            else:
                done = window(y_refs[k], k, piece, chunk)
                done[...] = total.astype(jnp.bfloat16)
                start(number, n - 1, done, done, down)
    for step in range(n - 1):
        for number, (k, piece, down) in enumerate(streams):
            copies[number, n - 1 + step].wait_recv()
            if step < n - 2:
                done = window(y_refs[k], k, piece, chunk_at(down, n - 1 + step))
                start(number, n + step, done, done, down)
    for one in copies.values():
        one.wait_send()


def ring_call(body, name, arrays, outs, scratch, ident):
    size = sum(v.size * 2 for v in arrays)
    return pl.pallas_call(
        body,
        name=name,
        out_shape=[jax.ShapeDtypeStruct(s, d) for s, d in outs],
        in_specs=[pl.BlockSpec(memory_space=pltpu.VMEM)] * len(arrays),
        out_specs=[pl.BlockSpec(memory_space=pltpu.VMEM)] * len(outs),
        scratch_shapes=scratch,
        compiler_params=pltpu.CompilerParams(
            collective_id=ident, has_side_effects=True, vmem_limit_bytes=48 << 20
        ),
        cost_estimate=pl.CostEstimate(flops=0, bytes_accessed=size, transcendentals=0),
    )(*arrays)


def ring_total(arrays, splits, ident):
    n = lax.axis_size("seq")
    streams = sum(abs(s) for s in splits)
    return ring_call(
        functools.partial(ring_kernel, n, splits),
        "ring_total",
        arrays,
        [(v.shape, jnp.bfloat16) for v in arrays],
        [pltpu.VMEM((v.shape[0] // n * (n - 1), v.shape[1]), jnp.bfloat16) for v in arrays]
        + [pltpu.SemaphoreType.DMA((streams, 2 * n - 2))] * 2,
        ident,
    )


def units_kernel(
    n, fan, x_ref, part_ref, inner_ref, outer_ref, sum_ref, landed,
    swap_send, swap_recv, own_sem, send_sem, recv_sem, part_send, part_recv,
):
    s, me = lax.axis_index("seq"), lax.axis_index("fsdp")
    rows, width = x_ref.shape[0] // 3, x_ref.shape[1]
    cols = width // fan
    block = 2 * fan * rows
    place, right, left = ring_greet(n, [(me + far) % fan for far in range(1, fan)])
    moves = []
    for far in range(fan):
        target = (me + far) % fan
        for half in range(2):
            src = x_ref.at[pl.ds(half * rows, rows), pl.ds(pl.multiple_of(target * cols, 128), cols)]
            dst = inner_ref.at[pl.ds(s * block + (me * 2 + half) * rows, rows), :]
            if far:
                one = pltpu.make_async_remote_copy(
                    src_ref=src,
                    dst_ref=dst,
                    send_sem=swap_send.at[far, half],
                    recv_sem=swap_recv.at[far, half],
                    device_id={"fsdp": target},
                    device_id_type=MESH,
                )
            else:
                one = pltpu.make_async_copy(src, dst, own_sem.at[half])
            one.start()
            moves.append(one)
    mine = pltpu.make_async_copy(
        x_ref.at[pl.ds(2 * rows, rows), :], outer_ref.at[pl.ds(s * rows, rows), :], own_sem.at[2]
    )
    mine.start()
    copies = {}
    outs = ((outer_ref, (n * rows, width), 2), (inner_ref, (n * block, cols), -2))

    def start(k, piece, step):
        ref, shape, split = outs[k]
        chunk = ring_index((place + step) % n if piece else (place + n - step) % n, n)
        view = ring_window(ref, shape, split, n, piece, chunk)
        copies[k, piece, step] = pltpu.make_async_remote_copy(
            src_ref=view,
            dst_ref=view,
            send_sem=send_sem.at[2 * k + piece, step],
            recv_sem=recv_sem.at[2 * k + piece, step],
            device_id={"seq": left if piece else right},
            device_id_type=MESH,
        )
        copies[k, piece, step].start()

    tokens = sum_ref.shape[0]
    parts = []
    for far in range(1, fan):
        target = (me + far) % fan
        one = pltpu.make_async_remote_copy(
            src_ref=part_ref.at[pl.ds(target * tokens, tokens), :],
            dst_ref=landed.at[far],
            send_sem=part_send.at[far],
            recv_sem=part_recv.at[far],
            device_id={"fsdp": target},
            device_id_type=MESH,
        )
        one.start()
        parts.append(one)
    mine.wait()
    start(0, 0, 0)
    start(0, 1, 0)
    for one in moves:
        one.wait()
    start(1, 0, 0)
    start(1, 1, 0)
    for step in range(n - 1):
        for k in range(2):
            for piece in range(2):
                copies[k, piece, step].wait_recv()
                if step < n - 2:
                    start(k, piece, step + 1)
    total = part_ref[pl.ds(pl.multiple_of(me * tokens, tokens), tokens), :].astype(jnp.float32)
    for far in range(1, fan):
        parts[far - 1].wait()
        total = total + landed[far].astype(jnp.float32)
    sum_ref[...] = total
    for one in copies.values():
        one.wait_send()


def units_total(grads, part, ident):
    n, fan = lax.axis_size("seq"), lax.axis_size("fsdp")
    rows, width = grads.shape[0] // 3, grads.shape[1]
    tokens = part.shape[0] // fan
    sems = lambda *shape: pltpu.SemaphoreType.DMA(shape)
    return ring_call(
        functools.partial(units_kernel, n, fan),
        "units_total",
        [grads, part],
        [
            ((n * 2 * fan * rows, width // fan), jnp.bfloat16),
            ((n * rows, width), jnp.bfloat16),
            ((tokens, part.shape[1]), jnp.float32),
        ],
        [pltpu.VMEM((fan, tokens, part.shape[1]), jnp.bfloat16), sems(fan, 2), sems(fan, 2), sems(3)]
        + [sems(4, n - 1), sems(4, n - 1), sems(fan), sems(fan)],
        ident,
    )


def team(n):
    s, f = lax.axis_index("seq"), lax.axis_index("fsdp")
    half = s // (n // 2)
    away = (half + f) % 2
    return f // 2, half, (s + away * (n // 2)) % n


def swap_kernel(n, fan, count, fars, fresh, *refs):
    given = count + (len(fars) > 0) + (0 if fresh else 2)
    x_refs, y_refs = refs[:count], refs[given : given + count]
    sems = refs[given + count + (2 if fars else 0) :]
    send_sem, recv_sem, own_sem = sems[:3]
    pair, half, rank = team(n)
    me = lax.axis_index("fsdp")

    def device(other):
        away = (other // (n // 2) + half) % 2
        return {"seq": (other + away * (n // 2)) % n, "fsdp": 2 * pair + (half + away) % 2}

    barrier = pltpu.get_barrier_semaphore()
    for j in range(1, n):
        pl.semaphore_signal(barrier, inc=1, device_id=device((rank + j) % n), device_id_type=MESH)
    travel = [far for far in fars if far]
    for far in travel:
        pl.semaphore_signal(barrier, inc=1, device_id={"fsdp": (me + fan - far) % fan}, device_id_type=MESH)
    pl.semaphore_wait(barrier, n - 1 + len(travel))
    copies = []
    for k in range(count):
        for j in range(1, n):
            other = (rank + j) % n
            one = pltpu.make_async_remote_copy(
                src_ref=x_refs[k].at[other],
                dst_ref=y_refs[k].at[rank],
                send_sem=send_sem.at[k, j],
                recv_sem=recv_sem.at[k, j],
                device_id=device(other),
                device_id_type=MESH,
            )
            one.start()
            copies.append(one)
    for k in range(count):
        one = pltpu.make_async_copy(x_refs[k].at[rank], y_refs[k].at[rank], own_sem.at[k])
        one.start()
        copies.append(one)
    if fars:
        w_ref, halves = refs[count], refs[given + count : given + count + 2]
        far_send, far_recv, far_own, stage = sems[3:]
        rest = []
        units, cols = halves[0].shape[0], w_ref.shape[1]
        for i, far in enumerate(fars):
            target = (me + far) % fan
            for part in range(2):
                src = w_ref.at[pl.ds((part * fan + target) * units, units), :]
                dst = halves[part].at[:, pl.ds(pl.multiple_of(me * cols, 128), cols)]
                if far:
                    one = pltpu.make_async_remote_copy(
                        src_ref=src,
                        dst_ref=dst,
                        send_sem=far_send.at[i, part],
                        recv_sem=far_recv.at[i, part],
                        device_id={"fsdp": target},
                        device_id_type=MESH,
                    )
                else:
                    one = pltpu.make_async_copy(src, stage.at[part], far_own.at[0, part])
                    rest.append((one, pltpu.make_async_copy(stage.at[part], dst, far_own.at[1, part])))
                one.start()
                if far:
                    copies.append(one)
        for inward, outward in rest:
            inward.wait()
            outward.start()
            copies.append(outward)
    for one in copies:
        one.wait()


def swap(arrays, ident, fars=(), given=None, halves=None):
    n, fan = lax.axis_size("seq"), lax.axis_size("fsdp")
    count = len(arrays)
    size = sum(v.size * 2 for v in arrays)
    operands, outs, alias = list(arrays), [jax.ShapeDtypeStruct(v.shape, v.dtype) for v in arrays], {}
    scratch = [
        pltpu.SemaphoreType.DMA((count, n)),
        pltpu.SemaphoreType.DMA((count, n)),
        pltpu.SemaphoreType.DMA((count,)),
    ]
    if fars:
        operands.append(given)
        shape = (given.shape[0] // (2 * fan), given.shape[1] * fan)
        outs += [jax.ShapeDtypeStruct(shape, given.dtype)] * 2
        scratch += [pltpu.SemaphoreType.DMA((len(fars), 2))] * 2 + [
            pltpu.SemaphoreType.DMA((2, 2)),
            pltpu.VMEM((2, given.shape[0] // (2 * fan), given.shape[1]), given.dtype),
        ]
        if halves is not None:
            operands += list(halves)
            alias = {count + 1: count, count + 2: count + 1}
    return pl.pallas_call(
        functools.partial(swap_kernel, n, fan, count, fars, not fars or halves is None),
        name="swap",
        out_shape=outs,
        in_specs=[pl.BlockSpec(memory_space=pl.ANY)] * len(operands),
        out_specs=[pl.BlockSpec(memory_space=pl.ANY)] * len(outs),
        scratch_shapes=scratch,
        input_output_aliases=alias,
        compiler_params=pltpu.CompilerParams(collective_id=ident, has_side_effects=True),
        cost_estimate=pl.CostEstimate(flops=0, bytes_accessed=size, transcendentals=0),
    )(*operands)


def norm_apply(value, gain):
    return value * lax.rsqrt(jnp.mean(value * value, axis=-1, keepdims=True) + EPS) * gain


def norm_back(value, gain, grad):
    _, pull = jax.vjp(norm_apply, value, gain)
    return pull(grad)


def gate_mix(gate, up):
    return jax.nn.gelu(gate, approximate=True) * up


def counts_below(ids, values):
    total = jnp.zeros_like(values)
    for doc in range(DOCS):
        total = total + jnp.where(values > doc, jnp.sum((ids == doc).astype(jnp.int32)), 0)
    return total


def change_home(value):
    n, fan = lax.axis_size("seq"), lax.axis_size("fsdp")
    pairs = []
    for s in range(n):
        for f in range(fan):
            away = (s // (n // 2) + f) % 2
            target = ((s + n // 2) % n, f ^ 1) if away else (s, f)
            pairs.append((s * fan + f, target[0] * fan + target[1]))
    return lax.ppermute(value, ("seq", "fsdp"), pairs)


def spread(blocks):
    fan, me = lax.axis_size("fsdp"), lax.axis_index("fsdp")
    result = blocks
    for far in range(1, fan):
        block = lax.dynamic_index_in_dim(blocks, (me + far) % fan, 0, True)
        block = lax.ppermute(block, "fsdp", [(f, (f + far) % fan) for f in range(fan)])
        result = lax.dynamic_update_slice_in_dim(result, block, (me - far) % fan, 0)
    return result


def flat(blocks):
    return jnp.transpose(blocks, (1, 0, 2)).reshape(blocks.shape[1], -1)


def by_rows(value):
    return with_layout_constraint(value, Layout(major_to_minor=tuple(range(value.ndim))))


def scatter(grad):
    return lax.psum_scatter(grad, "fsdp", scatter_dimension=0, tiled=True)


def over_seq(arrays, splits, ident):
    n = lax.axis_size("seq")
    if all(
        v.shape[0] % (8 * n) == 0
        and ring_cut(v.shape, s, n)[0] % 8 == 0
        and v.shape[1] % (128 * max(s, 1)) == 0
        for v, s in zip(arrays, splits)
    ):
        return ring_total(arrays, splits, ident)
    return [lax.psum(v, "seq") for v in arrays]


def shards(
    layer_in, encoder, decoder_ids, encoder_ids, rel_buckets,
    norm_self, self_qkv, self_out, rel_table, norm_cross, cross_q, cross_kv, cross_out, norm_ff, ff_in, ff_out,
    cotangent,
):
    seqs, local, width = layer_in.shape
    enc_local = encoder.shape[1]
    parts = lax.axis_size("seq")
    heads = self_qkv.shape[1]
    dh = self_qkv.shape[2] // 3
    own = heads // parts
    rows = seqs * local
    buckets, table_own = rel_table.shape
    length, keys = local * parts, enc_local * parts
    gather = lambda v: lax.all_gather(v, "fsdp", axis=0, tiled=True)

    fan = lax.axis_size("fsdp")
    units = ff_in.shape[1] // (2 * fan)
    part = norm_self.shape[0]
    pair, half, rank = team(parts)

    qkv_w = gather(self_qkv)
    small = jnp.concatenate([norm_self, norm_cross, norm_ff, rel_table.reshape(-1)])
    small = lax.all_gather(small, "fsdp", axis=0, tiled=False)
    small, self_out = lax.optimization_barrier((small, self_out))
    mix_self = gather(self_out).reshape(parts, own * dh, width)
    both_ids = jnp.concatenate([decoder_ids.reshape(-1), encoder_ids.reshape(-1)])
    both_ids = change_home(jnp.pad(both_ids, (0, 1024 - local - enc_local)).reshape(8, 128))
    (both_ids,) = swap([jnp.broadcast_to(both_ids[None], (parts, 8, 128))], 13)
    both_ids, cross_q = lax.optimization_barrier((both_ids, cross_q))
    query_w = gather(cross_q)
    home = change_home(layer_in.reshape(rows, width))
    inner_t = ff_in.T
    gain_first, gain_second, gain_third = (
        small[:, i * part : (i + 1) * part].reshape(width).astype(f32) for i in range(3)
    )
    table = jnp.transpose(small[:, 3 * part :].reshape(-1, buckets, table_own), (1, 0, 2)).reshape(buckets, heads)
    both_ids = both_ids.reshape(parts, 1024)
    ids = both_ids[:, :local].reshape(length)
    enc_ids = both_ids[:, local : local + enc_local].reshape(keys)

    first_seen = counts_below(ids, ids)
    enc_first = counts_below(enc_ids, ids)
    enc_last = counts_below(enc_ids, ids + 1)
    blocks = length // BQ
    bk = 256
    self_rows = jnp.broadcast_to(first_seen[None], (8, length))
    cross_rows = jnp.concatenate([enc_first[None], enc_last[None], jnp.zeros((6, length), jnp.int32)])
    self_limits = jnp.stack(
        [first_seen[::BQ] // bk, (jnp.arange(blocks, dtype=jnp.int32) + 1) * (BQ // bk)]
    )
    cross_limits = jnp.stack([enc_first[::BQ] // bk, (enc_last[BQ - 1 :: BQ] + bk - 1) // bk])

    first_head = rank * own
    table_mine = lax.dynamic_slice_in_dim(table.astype(f32), first_head, own, 1)
    near = rel_buckets[:REACH]
    onehot = (near[:, None] == jnp.arange(buckets, dtype=jnp.int32)[None, :]).astype(f32)
    bias = jnp.einsum("ln,ng->gl", onehot, table_mine, precision=HIGH)
    ext = jnp.concatenate(
        [jnp.full((own, BQ), MASKED, f32), bias, jnp.zeros((own, BQ), f32)], axis=1
    )

    pairs_t = jnp.transpose(cross_kv, (1, 2, 0))
    qkv_w, home, inner_t, pairs_t, ext, self_rows, cross_rows, self_limits, cross_limits = lax.optimization_barrier(
        (qkv_w, home, inner_t, pairs_t, ext, self_rows, cross_rows, self_limits, cross_limits)
    )
    qkv_w = qkv_w.reshape(width, parts, own * 3 * dh)

    stream = home.astype(f32)
    normed_first = norm_apply(stream, gain_first).astype(bf16)
    qkv_tok = jnp.einsum("td,dge->gte", normed_first, qkv_w, preferred_element_type=f32).astype(bf16)
    qkv_tok, pairs_t, cotangent, encoder = lax.optimization_barrier((qkv_tok, pairs_t, cotangent, encoder))
    pairs_t = lax.all_gather(pairs_t, "fsdp", axis=2, tiled=True).reshape(parts, own * 2 * dh, width)
    others = change_home(jnp.concatenate([cotangent.reshape(rows, width), encoder.reshape(-1, width)]))
    grad_low, enc_flat = others[:rows], others[rows:]
    (qkv,) = swap([qkv_tok], 10)
    qkv, cross_out, grad_low = lax.optimization_barrier((qkv, cross_out, grad_low))
    if rows == cross_out.shape[0]:
        mix_cross, grad_group = lax.all_gather(jnp.stack([cross_out, grad_low]), "fsdp", axis=1, tiled=True)
    else:
        mix_cross, grad_group = gather(cross_out), gather(grad_low)
    mix_cross = mix_cross.reshape(parts, own * dh, width)
    qkv = qkv.reshape(length, own * 3 * dh)
    out_self, self_t, self_lse = self_forward(self_limits, self_rows, ext, qkv)
    by_kernel = (width // fan) % 128 == 0
    fars = [tuple(far for far in range(fan) if (far + 2) % 3 == i) if by_kernel else () for i in range(3)]
    self_tok, *halves = swap([out_self.reshape(parts, local, own * dh)], 14, fars[0], inner_t)
    after_self = stream + jnp.einsum("gtc,gcd->td", self_tok, mix_self, preferred_element_type=f32)
    normed_second = norm_apply(after_self, gain_second).astype(bf16)
    query_tok = jnp.dot(normed_second, query_w, preferred_element_type=f32).astype(bf16)
    query_tok = jnp.transpose(query_tok.reshape(rows, parts, own * dh), (1, 0, 2))
    pairs_tok = jnp.einsum("td,ged->gte", enc_flat, pairs_t, preferred_element_type=f32).astype(bf16)
    query_cross, pairs, *halves = swap([query_tok, pairs_tok], 15, fars[1], inner_t, halves)
    query_cross, pairs = query_cross.reshape(length, own * dh), pairs.reshape(keys, own * 2 * dh)
    out_cross, cross_t, cross_lse = cross_forward(cross_limits, cross_rows, query_cross, pairs)
    cross_tok, *halves = swap([out_cross.reshape(parts, local, own * dh)], 16, fars[2], inner_t, halves)
    if not by_kernel:
        halves = spread(jnp.transpose(inner_t.reshape(2, fan, units, -1), (1, 0, 2, 3)))
        halves = [jnp.transpose(halves[:, i], (1, 0, 2)).reshape(units, width) for i in range(2)]
    gate_t, up_t = halves
    after_cross = after_self + jnp.einsum("gtc,gcd->td", cross_tok, mix_cross, preferred_element_type=f32)
    normed_third = norm_apply(after_cross, gain_third).astype(bf16)
    normed_group = gather(normed_third)
    gate = jnp.einsum("td,fd->tf", normed_group, gate_t, preferred_element_type=f32)
    up = jnp.einsum("td,fd->tf", normed_group, up_t, preferred_element_type=f32)
    hidden = gate_mix(gate, up).astype(bf16)

    grad_hidden = jnp.einsum("td,fd->tf", grad_group, ff_out, preferred_element_type=f32)
    _, pull_mix = jax.vjp(gate_mix, gate, up)
    grad_gate, grad_up = (g.astype(bf16) for g in pull_mix(grad_hidden))
    grad_third_in = jnp.dot(grad_gate, gate_t, preferred_element_type=f32) + jnp.dot(
        grad_up, up_t, preferred_element_type=f32
    )
    grad_third_in = scatter(grad_third_in.astype(bf16))
    outer_part = jnp.dot(hidden, ff_out, preferred_element_type=f32).astype(bf16)
    grad_units = [
        jnp.einsum("tf,td->fd", g, y, preferred_element_type=f32).astype(bf16)
        for g, y in ((grad_gate, normed_group), (grad_up, normed_group), (hidden, grad_group))
    ]
    grad_third_in, outer_part, grad_units = lax.optimization_barrier((grad_third_in, outer_part, grad_units))
    if by_kernel:
        grad_units = jnp.stack([g.reshape(parts, units // parts, width) for g in grad_units], axis=1)
        part_units = lax.psum_scatter(
            grad_units.reshape(3 * units, width), "seq", scatter_dimension=0, tiled=True
        )
    grad_third_in = grad_third_in.astype(f32)
    grad_from_third, grad_gain_third = norm_back(after_cross, gain_third, grad_third_in)
    grad_middle = grad_low.astype(f32) + grad_from_third
    middle_low = grad_middle.astype(bf16)
    grad_mix_cross = jnp.einsum("gtc,td->gcd", cross_tok, middle_low, preferred_element_type=f32)
    grad_cross_tok = jnp.einsum("td,gcd->gtc", middle_low, mix_cross, preferred_element_type=f32).astype(bf16)
    (grad_cross,) = swap([grad_cross_tok], 11)
    grad_cross = grad_cross.reshape(length, own * dh)
    grad_query, grad_pairs = cross_backward(
        cross_limits, cross_rows, query_cross, pairs, grad_cross, cross_t, cross_lse
    )
    grad_query_tok, grad_pairs_tok = swap(
        [grad_query.reshape(parts, local, own * dh), grad_pairs.reshape(parts, enc_local, own * 2 * dh)], 12
    )
    grad_query_tok, grad_pairs_tok = flat(grad_query_tok), flat(grad_pairs_tok)
    grad_query_w = jnp.einsum("td,te->de", normed_second, grad_query_tok, preferred_element_type=f32)
    grad_second_in = jnp.einsum("te,de->td", grad_query_tok, query_w, preferred_element_type=f32)
    grad_pairs_w = jnp.einsum("td,te->de", enc_flat, grad_pairs_tok, preferred_element_type=f32)
    grad_encoder = jnp.dot(grad_pairs_tok, pairs_t.reshape(-1, width), preferred_element_type=f32)
    grad_from_second, grad_gain_second = norm_back(after_self, gain_second, grad_second_in)
    grad_upper = grad_middle + grad_from_second
    upper_low = grad_upper.astype(bf16)
    grad_mix_self = jnp.einsum("gtc,td->gcd", self_tok, upper_low, preferred_element_type=f32)
    grad_self_tok = jnp.einsum("td,gcd->gtc", upper_low, mix_self, preferred_element_type=f32).astype(bf16)
    grad_mid = jnp.concatenate(
        [
            grad_query_w.astype(bf16),
            grad_pairs_w.astype(bf16),
            grad_mix_cross.reshape(width, width).astype(bf16),
            grad_mix_self.reshape(width, width).astype(bf16),
        ],
        axis=1,
    )
    grad_self_tok, grad_mid = lax.optimization_barrier((grad_self_tok, grad_mid))
    part_mid = scatter(grad_mid)
    (grad_self,) = swap([grad_self_tok], 11)
    grad_self = grad_self.reshape(length, own * dh)
    grad_qkv, tile_sums = self_backward(self_limits, self_rows, ext, qkv, grad_self, self_t, self_lse)
    (grad_qkv_tok,) = swap([grad_qkv.reshape(parts, local, own * 3 * dh)], 10)
    grad_qkv_tok = flat(grad_qkv_tok)
    grad_qkv_w = jnp.einsum("td,te->de", normed_first, grad_qkv_tok, preferred_element_type=f32)
    grad_first_in = jnp.einsum("te,de->td", grad_qkv_tok, qkv_w.reshape(width, -1), preferred_element_type=f32)
    grad_from_first, grad_gain_first = norm_back(stream, gain_first, grad_first_in)
    grad_layer_in = (grad_upper + grad_from_first).astype(bf16)
    if not by_kernel:
        part_units = grad_units
    bucket_line = jnp.concatenate(
        [jnp.full((BQ,), -1, jnp.int32), near, jnp.full((BQ + bk,), -1, jnp.int32)]
    )
    by_tile = jnp.stack([bucket_line[t * bk + 1 : t * bk + 1 + BQ + bk] for t in range(tile_count(bk))])
    in_bucket = (by_tile[:, :, None] == jnp.arange(buckets, dtype=jnp.int32)).astype(f32)
    by_bucket = jnp.einsum("twn,gtw->ng", in_bucket, tile_sums, precision=HIGH)
    grad_table = lax.dynamic_update_slice_in_dim(jnp.zeros((buckets, heads), f32), by_bucket, first_head, 1)

    gains = jnp.concatenate(
        [g.reshape(-1, part) for g in (grad_gain_first, grad_gain_second, grad_gain_third)], axis=1
    )
    tables = jnp.transpose(grad_table.reshape(buckets, -1, table_own), (1, 0, 2)).reshape(-1, buckets * table_own)
    small_grads = lax.psum(jnp.concatenate([gains, tables], axis=1).astype(bf16), "fsdp")
    small_grads = lax.dynamic_index_in_dim(small_grads, lax.axis_index("fsdp"), 0, False)
    small_size = small_grads.shape[0]
    small_grads = jnp.pad(small_grads, (0, parts * 1024 - small_size)).reshape(parts * 8, 128)
    going_home = jnp.concatenate([grad_layer_in, grad_encoder.astype(bf16)])
    going_home, small_grads, grad_qkv_w, part_units = lax.optimization_barrier(
        (going_home, small_grads, grad_qkv_w.astype(bf16), part_units)
    )
    part_last = scatter(grad_qkv_w)
    going_home = change_home(going_home)
    if by_kernel:
        total_inner, total_outer, outer_sum = units_total(part_units, outer_part, 0)
    else:
        grad_units = [lax.psum(g, "seq") for g in grad_units]
        total_inner = spread(jnp.transpose(jnp.stack(grad_units[:2]).reshape(2, units, fan, -1), (2, 0, 1, 3)))
        total_outer, outer_sum = grad_units[2], scatter(outer_part).astype(f32)
    total_mid, total_qkv, small_total = over_seq([part_mid, part_last, small_grads], (2, 2, 1), 1)
    layer_out = (after_cross + outer_sum).astype(bf16)
    layer_out, total_inner, total_outer, total_mid, total_qkv, going_home = lax.optimization_barrier(
        (layer_out, total_inner, total_outer, total_mid, total_qkv, going_home)
    )
    layer_out = change_home(layer_out).reshape(seqs, local, width)
    grad_layer_in = going_home[:rows].astype(f32).reshape(seqs, local, width)
    grad_encoder = going_home[rows:].astype(f32).reshape(seqs, enc_local, width)
    if by_kernel:
        total_inner = jnp.transpose(total_inner.reshape(parts, fan, 2, units // parts, -1), (4, 2, 1, 0, 3))
    else:
        total_inner = jnp.transpose(total_inner, (3, 1, 0, 2))
    total_inner = total_inner.reshape(-1, 2 * fan * units).astype(f32)
    total_outer, total_mid, total_qkv = (v.astype(f32) for v in (total_outer, total_mid, total_qkv))
    total_query, total_mix_cross = total_mid[:, :width], total_mid[:, 3 * width : 4 * width]
    total_pairs = total_mid[:, width : 3 * width].reshape(-1, heads, 2 * dh)
    total_mix_self, total_qkv = total_mid[:, 4 * width :], total_qkv.reshape(-1, heads, 3 * dh)
    mine = small_total.reshape(-1)[:small_size].astype(f32)
    total_gain_first, total_gain_second, total_gain_third = (mine[i * part : (i + 1) * part] for i in range(3))
    total_table = mine[3 * part :].reshape(buckets, table_own)
    return (
        layer_out, grad_layer_in, grad_encoder, total_gain_first, total_qkv, total_mix_self, total_table,
        total_gain_second, total_query, total_pairs, total_mix_cross, total_gain_third, total_inner, total_outer,
    )


def solution(mesh):
    in_specs = (
        P("fsdp", "seq", None), P("fsdp", "seq", None), P("fsdp", "seq"), P("fsdp", "seq"), P(),
        P("fsdp"), P("fsdp", None, None), P("fsdp", None), P(None, "fsdp"), P("fsdp"), P("fsdp", None),
        P("fsdp", None, None), P("fsdp", None), P("fsdp"), P("fsdp", None), P("fsdp", None),
        P("fsdp", "seq", None),
    )
    out_specs = (
        P("fsdp", "seq", None), P("fsdp", "seq", None), P("fsdp", "seq", None), P("fsdp"), P("fsdp", None, None),
        P("fsdp", None), P(None, "fsdp"), P("fsdp"), P("fsdp", None), P("fsdp", None, None), P("fsdp", None),
        P("fsdp"), P("fsdp", None), P("fsdp", None),
    )
    return jax.shard_map(shards, mesh=mesh, in_specs=in_specs, out_specs=out_specs, check_vma=False)
```

```python
import functools

import jax
import jax.numpy as jnp
from jax import lax
from jax.experimental import pallas as pl
from jax.experimental.layout import Layout, with_layout_constraint
from jax.experimental.pallas import tpu as pltpu
from jax.sharding import PartitionSpec as P

EPS = 1e-06
HIGH = lax.Precision.HIGHEST
MASKED = -1e30
DOCS = 4

BQ = 256
REACH = 1024


def blk(index, size):
    return pl.ds(pl.multiple_of(index * size, size), size)


def turn(value):
    return jnp.transpose(value.astype(jnp.float32), (1, 0))


def bias_tiles(ext_ref, tile_ref, own, bk):
    span = BQ + bk
    for h in range(own):
        for t in range(tile_ref.shape[1]):
            first = t * bk
            line = jnp.broadcast_to(ext_ref[h : h + 1, first : first + span], (bk, span))
            tile_ref[h, t] = pltpu.roll(line, 0, 1, stride=1, stride_axis=0)[:, bk:]


def tile_count(bk):
    return BQ // bk + REACH // bk


def unpack(ref, own, width, picks, flips, base):
    block = 256

    def one(b, _):
        rows = blk(b, block)
        value = ref[rows, :]
        if flips:
            flat = turn(value).astype(jnp.bfloat16)
            for target, piece in flips:
                for h in range(own):
                    at = h * width + piece * 64
                    target[base + h, :, rows] = flat[at : at + 64]
        for target, piece in picks:
            for h in range(own):
                at = h * width + piece * 64
                target[base + h, rows, :] = value[:, at : at + 64]
        return 0

    lax.fori_loop(0, ref.shape[0] // block, one, 0)


def dot(a, b):
    return jnp.dot(a, b, preferred_element_type=jnp.float32)


def score(own_index, key_tile, query_t, tile_ref, t, low, high, first_key):
    value = dot(key_tile, query_t)
    place = lax.broadcasted_iota(jnp.int32, value.shape, 0)
    keep = place >= low - first_key
    if high is not None:
        keep = keep & (place < high - first_key)
    else:
        value = value + tile_ref[own_index, t]
    return jnp.where(keep, value, MASKED)


def forward_body(own, bk, causal, lim_ref, rows_ref, q_t, k_rows, v_t, tile_ref, o_ref, ot_ref, lse_ref):
    length = o_ref.shape[0]

    def q_block(i, _):
        cols = blk(i, BQ)
        queries = [q_t[h, :, cols] for h in range(own)]
        low = rows_ref[0:1, cols]
        high = None if causal else rows_ref[1:2, cols]

        def k_block(j, carry):
            keys = blk(j, bk)
            t = i * (BQ // bk) - j + (BQ // bk - 1)
            out = []
            for h in range(own):
                top, total, acc = carry[h]
                s = score(h, k_rows[h, keys, :], queries[h], tile_ref, t, low, high, j * bk)
                new_top = jnp.maximum(top, jnp.max(s, axis=0, keepdims=True))
                p = jnp.exp(s - new_top)
                scale = jnp.exp(top - new_top)
                total = total * scale + jnp.sum(p, axis=0, keepdims=True)
                acc = acc * scale + dot(v_t[h, :, keys], p.astype(jnp.bfloat16))
                out.append((new_top, total, acc))
            return tuple(out)

        start = tuple(
            (
                jnp.full((1, BQ), MASKED, jnp.float32),
                jnp.zeros((1, BQ), jnp.float32),
                jnp.zeros((64, BQ), jnp.float32),
            )
            for _ in range(own)
        )
        ends = lax.fori_loop(lim_ref[0, i], lim_ref[1, i], k_block, start)
        for h in range(own):
            top, total, acc = ends[h]
            ot_ref[h * 64 : h * 64 + 64, cols] = acc / total
            lse_ref[h : h + 1, cols] = top + jnp.log(total)
        o_ref[cols, :] = turn(ot_ref[:, cols]).astype(jnp.bfloat16)
        return 0

    lax.fori_loop(0, length // BQ, q_block, 0)


def self_forward_kernel(own, bk, lim_ref, rows_ref, ext_ref, x_ref, o_ref, ot_ref, lse_ref, q_t, k_rows, v_t, tile_ref):
    bias_tiles(ext_ref, tile_ref, own, bk)
    unpack(x_ref, own, 192, [(k_rows, 1)], [(q_t, 0), (v_t, 2)], 0)
    forward_body(own, bk, True, lim_ref, rows_ref, q_t, k_rows, v_t, tile_ref, o_ref, ot_ref, lse_ref)


def cross_forward_kernel(own, bk, lim_ref, rows_ref, q_ref, kv_ref, o_ref, ot_ref, lse_ref, q_t, k_rows, v_t):
    unpack(q_ref, own, 64, [], [(q_t, 0)], 0)
    unpack(kv_ref, own, 128, [(k_rows, 0)], [(v_t, 1)], 0)
    forward_body(own, bk, False, lim_ref, rows_ref, q_t, k_rows, v_t, None, o_ref, ot_ref, lse_ref)


def backward_body(
    own, bk, causal, lim_ref, rows_ref, do_ref, ot_ref, lse_ref,
    q_t, q_rows, k_t, k_rows, v_rows, do_t, do_rows, tile_ref, sum_ref, dq_t, dk, dv,
):
    length = do_ref.shape[0]
    dk[...] = jnp.zeros_like(dk)
    dv[...] = jnp.zeros_like(dv)
    if causal:
        sum_ref[...] = jnp.zeros_like(sum_ref)

    def q_block(i, _):
        cols = blk(i, BQ)
        low = rows_ref[0:1, cols]
        high = None if causal else rows_ref[1:2, cols]
        per_head = []
        for h in range(own):
            grad_t = do_t[h, :, cols]
            delta = jnp.sum(
                grad_t.astype(jnp.float32) * ot_ref[h * 64 : h * 64 + 64, cols], axis=0, keepdims=True
            )
            per_head.append((q_t[h, :, cols], grad_t, delta, lse_ref[h : h + 1, cols]))

        def k_block(j, carry):
            keys = blk(j, bk)
            t = i * (BQ // bk) - j + (BQ // bk - 1)
            out = []
            for h in range(own):
                query_t, grad_t, delta, lse = per_head[h]
                s = score(h, k_rows[h, keys, :], query_t, tile_ref, t, low, high, j * bk)
                p = jnp.exp(s - lse)
                dp = dot(v_rows[h, keys, :], grad_t)
                ds = (p * (dp - delta)).astype(jnp.bfloat16)
                dv[h, keys, :] += dot(p.astype(jnp.bfloat16), do_rows[h, cols, :])
                dk[h, keys, :] += dot(ds, q_rows[h, cols, :])
                if causal:
                    sum_ref[h, t] += ds.astype(jnp.float32)
                out.append(carry[h] + dot(k_t[h, :, keys], ds))
            return tuple(out)

        ends = lax.fori_loop(
            lim_ref[0, i],
            lim_ref[1, i],
            k_block,
            tuple(jnp.zeros((64, BQ), jnp.float32) for _ in range(own)),
        )
        for h in range(own):
            dq_t[h * 64 : h * 64 + 64, cols] = ends[h]
        return 0

    lax.fori_loop(0, length // BQ, q_block, 0)


def diagonal_sums(sum_ref, u_ref, own, bk):
    flip = (
        lax.broadcasted_iota(jnp.int32, (bk, bk), 0) + lax.broadcasted_iota(jnp.int32, (bk, bk), 1) == bk - 1
    ).astype(jnp.float32)
    for h in range(own):
        for t in range(sum_ref.shape[1]):
            upside = jnp.dot(flip, sum_ref[h, t], precision=HIGH, preferred_element_type=jnp.float32)
            wide = jnp.concatenate([upside, jnp.zeros((bk, bk), jnp.float32)], axis=1)
            aligned = pltpu.roll(wide, 0, 1, stride=1, stride_axis=0)
            u_ref[h, t : t + 1, :] = jnp.sum(aligned, axis=0, keepdims=True)


def self_backward_kernel(
    own, bk, lim_ref, rows_ref, ext_ref, x_ref, do_ref, ot_ref, lse_ref, dx_ref, u_ref,
    q_t, q_rows, k_t, k_rows, v_rows, do_t, do_rows, tile_ref, sum_ref, dq_t, dk, dv,
):
    bias_tiles(ext_ref, tile_ref, own, bk)
    unpack(x_ref, own, 192, [(q_rows, 0), (k_rows, 1), (v_rows, 2)], [(q_t, 0), (k_t, 1)], 0)
    unpack(do_ref, own, 64, [(do_rows, 0)], [(do_t, 0)], 0)
    backward_body(
        own, bk, True, lim_ref, rows_ref, do_ref, ot_ref, lse_ref,
        q_t, q_rows, k_t, k_rows, v_rows, do_t, do_rows, tile_ref, sum_ref, dq_t, dk, dv,
    )
    diagonal_sums(sum_ref, u_ref, own, bk)

    def pack(b, _):
        rows = blk(b, 256)
        dq = turn(dq_t[:, rows])
        pieces = []
        for h in range(own):
            pieces += [dq[:, h * 64 : h * 64 + 64], dk[h, rows, :], dv[h, rows, :]]
        dx_ref[rows, :] = jnp.concatenate(pieces, axis=1).astype(jnp.bfloat16)
        return 0

    lax.fori_loop(0, x_ref.shape[0] // 256, pack, 0)


def cross_backward_kernel(
    own, bk, lim_ref, rows_ref, q_ref, kv_ref, do_ref, ot_ref, lse_ref, dq_ref, dkv_ref,
    q_t, q_rows, k_t, k_rows, v_rows, do_t, do_rows, dq_t, dk, dv,
):
    unpack(q_ref, own, 64, [(q_rows, 0)], [(q_t, 0)], 0)
    unpack(kv_ref, own, 128, [(k_rows, 0), (v_rows, 1)], [(k_t, 0)], 0)
    unpack(do_ref, own, 64, [(do_rows, 0)], [(do_t, 0)], 0)
    backward_body(
        own, bk, False, lim_ref, rows_ref, do_ref, ot_ref, lse_ref,
        q_t, q_rows, k_t, k_rows, v_rows, do_t, do_rows, None, None, dq_t, dk, dv,
    )

    def pack_q(b, _):
        rows = blk(b, 256)
        dq_ref[rows, :] = turn(dq_t[:, rows]).astype(jnp.bfloat16)
        return 0

    def pack_kv(b, _):
        rows = blk(b, 256)
        pieces = []
        for h in range(own):
            pieces += [dk[h, rows, :], dv[h, rows, :]]
        dkv_ref[rows, :] = jnp.concatenate(pieces, axis=1).astype(jnp.bfloat16)
        return 0

    lax.fori_loop(0, q_ref.shape[0] // 256, pack_q, 0)
    lax.fori_loop(0, kv_ref.shape[0] // 256, pack_kv, 0)


SMEM = pl.BlockSpec(memory_space=pltpu.SMEM)
VMEM = pl.BlockSpec(memory_space=pltpu.VMEM)
bf16, f32 = jnp.bfloat16, jnp.float32


def call(body, name, operands, outs, scratch, flops):
    size = sum(v.size * v.dtype.itemsize for v in operands)
    return pl.pallas_call(
        body,
        name=name,
        out_shape=[jax.ShapeDtypeStruct(s, d) for s, d in outs],
        in_specs=[SMEM] + [VMEM] * (len(operands) - 1),
        out_specs=[VMEM] * len(outs),
        scratch_shapes=[pltpu.VMEM(s, d) for s, d in scratch],
        compiler_params=pltpu.CompilerParams(vmem_limit_bytes=40 << 20),
        cost_estimate=pl.CostEstimate(flops=0, bytes_accessed=size, transcendentals=0),
    )(*operands)


def self_forward(limits, rows, ext, x, bk=256):
    length, own = x.shape[0], x.shape[1] // 192
    return call(
        functools.partial(self_forward_kernel, own, bk),
        "self_forward",
        [limits, rows, ext, x],
        [((length, own * 64), bf16), ((own * 64, length), f32), ((own, length), f32)],
        [
            ((own, 64, length), bf16),
            ((own, length, 64), bf16),
            ((own, 64, length), bf16),
            ((own, tile_count(bk), bk, BQ), f32),
        ],
        length * length * own * 64,
    )


def cross_forward(limits, rows, q, kv, bk=256):
    length, own, keys = q.shape[0], q.shape[1] // 64, kv.shape[0]
    return call(
        functools.partial(cross_forward_kernel, own, bk),
        "cross_forward",
        [limits, rows, q, kv],
        [((length, own * 64), bf16), ((own * 64, length), f32), ((own, length), f32)],
        [((own, 64, length), bf16), ((own, keys, 64), bf16), ((own, 64, keys), bf16)],
        length * keys * own * 128,
    )


def self_backward(limits, rows, ext, x, grad, o_t, lse, bk=256):
    length, own = x.shape[0], x.shape[1] // 192
    return call(
        functools.partial(self_backward_kernel, own, bk),
        "self_backward",
        [limits, rows, ext, x, grad, o_t, lse],
        [((length, own * 192), bf16), ((own, tile_count(bk), BQ + bk), f32)],
        [
            ((own, 64, length), bf16),
            ((own, length, 64), bf16),
            ((own, 64, length), bf16),
            ((own, length, 64), bf16),
            ((own, length, 64), bf16),
            ((own, 64, length), bf16),
            ((own, length, 64), bf16),
            ((own, tile_count(bk), bk, BQ), f32),
            ((own, tile_count(bk), bk, BQ), f32),
            ((own * 64, length), f32),
            ((own, length, 64), f32),
            ((own, length, 64), f32),
        ],
        length * length * own * 160,
    )


def cross_backward(limits, rows, q, kv, grad, o_t, lse, bk=256):
    length, own, keys = q.shape[0], q.shape[1] // 64, kv.shape[0]
    return call(
        functools.partial(cross_backward_kernel, own, bk),
        "cross_backward",
        [limits, rows, q, kv, grad, o_t, lse],
        [((length, own * 64), bf16), ((keys, own * 128), bf16)],
        [
            ((own, 64, length), bf16),
            ((own, length, 64), bf16),
            ((own, 64, keys), bf16),
            ((own, keys, 64), bf16),
            ((own, keys, 64), bf16),
            ((own, 64, length), bf16),
            ((own, length, 64), bf16),
            ((own * 64, length), f32),
            ((own, keys, 64), f32),
            ((own, keys, 64), f32),
        ],
        length * keys * own * 320,
    )


MESH = pl.DeviceIdType.MESH


def ring_place(index, n):
    z, x = index // 2, index % 2
    return z + x * (n - 1 - 2 * z)


def ring_index(place, n):
    x = place // (n // 2)
    z = place + x * (n - 1 - 2 * place)
    return 2 * z + x


def ring_greet(n, others):
    place = ring_place(lax.axis_index("seq"), n)
    right = ring_index((place + 1) % n, n)
    left = ring_index((place + n - 1) % n, n)
    barrier = pltpu.get_barrier_semaphore()
    for neighbour in (left, right):
        pl.semaphore_signal(barrier, inc=1, device_id={"seq": neighbour}, device_id_type=MESH)
    for other in others:
        pl.semaphore_signal(barrier, inc=1, device_id={"fsdp": other}, device_id_type=MESH)
    pl.semaphore_wait(barrier, 2 + len(others))
    return place, right, left


def ring_cut(shape, split, n):
    rows, cols = shape[0] // n, shape[1]
    return (rows, cols // split) if split > 0 else (rows // -split, cols)


def ring_window(ref, shape, split, n, piece, chunk):
    whole = shape[0] // n
    rows, cols = ring_cut(shape, split, n)
    if split > 0:
        return ref.at[pl.ds(chunk * whole, rows), pl.ds(piece * cols, cols)]
    return ref.at[pl.ds(chunk * whole + piece * rows, rows), :]


def ring_kernel(n, splits, *refs):
    count = len(splits)
    x_refs, y_refs, slots = refs[:count], refs[count : 2 * count], refs[2 * count : 3 * count]
    send_sem, recv_sem = refs[3 * count :]
    place, right, left = ring_greet(n, [])
    streams = [(k, piece, piece % 2) for k in range(count) for piece in range(abs(splits[k]))]

    def window(ref, k, piece, chunk):
        return ring_window(ref, x_refs[k].shape, splits[k], n, piece, chunk)

    def chunk_at(down, step):
        return (place + 1 + step) % n if down else (place + 2 * n - 1 - step) % n

    copies = {}

    def start(number, step, src, dst, down):
        copies[number, step] = pltpu.make_async_remote_copy(
            src_ref=src,
            dst_ref=dst,
            send_sem=send_sem.at[number, step],
            recv_sem=recv_sem.at[number, step],
            device_id={"seq": left if down else right},
            device_id_type=MESH,
        )
        copies[number, step].start()

    for number, (k, piece, down) in enumerate(streams):
        start(number, 0, window(x_refs[k], k, piece, place), window(slots[k], k, piece, 0), down)
    for step in range(n - 1):
        for number, (k, piece, down) in enumerate(streams):
            copies[number, step].wait_recv()
            chunk = chunk_at(down, step)
            mine = window(x_refs[k], k, piece, chunk)
            landed = window(slots[k], k, piece, step)
            total = landed[...].astype(jnp.float32) + mine[...].astype(jnp.float32)
            if step < n - 2:
                landed[...] = total.astype(jnp.bfloat16)
                start(number, step + 1, landed, window(slots[k], k, piece, step + 1), down)
            else:
                done = window(y_refs[k], k, piece, chunk)
                done[...] = total.astype(jnp.bfloat16)
                start(number, n - 1, done, done, down)
    for step in range(n - 1):
        for number, (k, piece, down) in enumerate(streams):
            copies[number, n - 1 + step].wait_recv()
            if step < n - 2:
                done = window(y_refs[k], k, piece, chunk_at(down, n - 1 + step))
                start(number, n + step, done, done, down)
    for one in copies.values():
        one.wait_send()


def ring_call(body, name, arrays, outs, scratch, ident):
    size = sum(v.size * 2 for v in arrays)
    return pl.pallas_call(
        body,
        name=name,
        out_shape=[jax.ShapeDtypeStruct(s, d) for s, d in outs],
        in_specs=[pl.BlockSpec(memory_space=pltpu.VMEM)] * len(arrays),
        out_specs=[pl.BlockSpec(memory_space=pltpu.VMEM)] * len(outs),
        scratch_shapes=scratch,
        compiler_params=pltpu.CompilerParams(
            collective_id=ident, has_side_effects=True, vmem_limit_bytes=48 << 20
        ),
        cost_estimate=pl.CostEstimate(flops=0, bytes_accessed=60 * size, transcendentals=0),
    )(*arrays)


def ring_total(arrays, splits, ident):
    n = lax.axis_size("seq")
    streams = sum(abs(s) for s in splits)
    return ring_call(
        functools.partial(ring_kernel, n, splits),
        "ring_total",
        arrays,
        [(v.shape, jnp.bfloat16) for v in arrays],
        [pltpu.VMEM((v.shape[0] // n * (n - 1), v.shape[1]), jnp.bfloat16) for v in arrays]
        + [pltpu.SemaphoreType.DMA((streams, 2 * n - 2))] * 2,
        ident,
    )


def units_kernel(
    n, fan, x_ref, part_ref, inner_ref, outer_ref, sum_ref, slots, acc, landed,
    down_send, down_recv, swap_send, swap_recv, own_sem, send_sem, recv_sem, part_send, part_recv,
):
    s, me = lax.axis_index("seq"), lax.axis_index("fsdp")
    rows, width = acc.shape[0] // 3, x_ref.shape[1]
    cols = width // fan
    block = 2 * fan * rows
    place, right, left = ring_greet(n, [(me + far) % fan for far in range(1, fan)])
    tokens = sum_ref.shape[0]
    parts = []
    for far in range(1, fan):
        target = (me + far) % fan
        one = pltpu.make_async_remote_copy(
            src_ref=part_ref.at[pl.ds(target * tokens, tokens), :],
            dst_ref=landed.at[far],
            send_sem=part_send.at[far],
            recv_sem=part_recv.at[far],
            device_id={"fsdp": target},
            device_id_type=MESH,
        )
        one.start()
        parts.append(one)

    sums = {}

    def piece_of(ref, at, piece):
        return ref.at[pl.ds(at * 3 * rows, 3 * rows), pl.ds(piece * cols, cols)]

    def send_sum(piece, step, src):
        to = left if piece >= fan // 2 else right
        sums[piece, step] = pltpu.make_async_remote_copy(
            src_ref=src,
            dst_ref=piece_of(slots, step, piece),
            send_sem=down_send.at[piece, step],
            recv_sem=down_recv.at[piece, step],
            device_id={"seq": to},
            device_id_type=MESH,
        )
        sums[piece, step].start()

    def chunk(piece, step):
        return ring_index((place + 1 + step) % n if piece >= fan // 2 else (place + 2 * n - 1 - step) % n, n)

    for piece in range(fan):
        send_sum(piece, 0, piece_of(x_ref, chunk(piece, 0), piece))
    for step in range(n - 1):
        for piece in range(fan):
            sums[piece, step].wait_recv()
            arrived = piece_of(slots, step, piece)
            mine = piece_of(x_ref, chunk(piece, step + 1), piece)
            total = (arrived[...].astype(jnp.float32) + mine[...].astype(jnp.float32)).astype(jnp.bfloat16)
            if step < n - 2:
                arrived[...] = total
                send_sum(piece, step + 1, arrived)
            else:
                acc[:, piece * cols : (piece + 1) * cols] = total
    moves = []
    for far in range(fan):
        target = (me + far) % fan
        for half in range(2):
            src = acc.at[pl.ds(half * rows, rows), pl.ds(pl.multiple_of(target * cols, 128), cols)]
            dst = inner_ref.at[pl.ds(s * block + (me * 2 + half) * rows, rows), :]
            if far:
                one = pltpu.make_async_remote_copy(
                    src_ref=src,
                    dst_ref=dst,
                    send_sem=swap_send.at[far, half],
                    recv_sem=swap_recv.at[far, half],
                    device_id={"fsdp": target},
                    device_id_type=MESH,
                )
            else:
                one = pltpu.make_async_copy(src, dst, own_sem.at[half])
            one.start()
            moves.append(one)
    mine = pltpu.make_async_copy(
        acc.at[pl.ds(2 * rows, rows), :], outer_ref.at[pl.ds(s * rows, rows), :], own_sem.at[2]
    )
    mine.start()
    copies = {}
    outs = ((outer_ref, (n * rows, width), 2), (inner_ref, (n * block, cols), -2))

    def start(k, piece, step):
        ref, shape, split = outs[k]
        chunk = ring_index((place + step) % n if piece else (place + n - step) % n, n)
        view = ring_window(ref, shape, split, n, piece, chunk)
        copies[k, piece, step] = pltpu.make_async_remote_copy(
            src_ref=view,
            dst_ref=view,
            send_sem=send_sem.at[2 * k + piece, step],
            recv_sem=recv_sem.at[2 * k + piece, step],
            device_id={"seq": left if piece else right},
            device_id_type=MESH,
        )
        copies[k, piece, step].start()

    mine.wait()
    start(0, 0, 0)
    start(0, 1, 0)
    for one in moves:
        one.wait()
    start(1, 0, 0)
    start(1, 1, 0)
    for step in range(n - 1):
        for k in range(2):
            for piece in range(2):
                copies[k, piece, step].wait_recv()
                if step < n - 2:
                    start(k, piece, step + 1)
    total = part_ref[pl.ds(pl.multiple_of(me * tokens, tokens), tokens), :].astype(jnp.float32)
    for far in range(1, fan):
        parts[far - 1].wait()
        total = total + landed[far].astype(jnp.float32)
    sum_ref[...] = total
    for one in [*copies.values(), *sums.values()]:
        one.wait_send()


def units_total(grads, part, ident):
    n, fan = lax.axis_size("seq"), lax.axis_size("fsdp")
    rows, width = grads.shape[0] // (3 * n), grads.shape[1]
    tokens = part.shape[0] // fan
    sems = lambda *shape: pltpu.SemaphoreType.DMA(shape)
    return ring_call(
        functools.partial(units_kernel, n, fan),
        "units_total",
        [grads, part],
        [
            ((n * 2 * fan * rows, width // fan), jnp.bfloat16),
            ((n * rows, width), jnp.bfloat16),
            ((tokens, part.shape[1]), jnp.float32),
        ],
        [
            pltpu.VMEM(((n - 1) * 3 * rows, width), jnp.bfloat16),
            pltpu.VMEM((3 * rows, width), jnp.bfloat16),
            pltpu.VMEM((fan, tokens, part.shape[1]), jnp.bfloat16),
        ]
        + [sems(fan, n - 1), sems(fan, n - 1), sems(fan, 2), sems(fan, 2), sems(3)]
        + [sems(4, n - 1), sems(4, n - 1), sems(fan), sems(fan)],
        ident,
    )


def team(n):
    s, f = lax.axis_index("seq"), lax.axis_index("fsdp")
    half = s // (n // 2)
    away = (half + f) % 2
    return f // 2, half, (s + away * (n // 2)) % n


def swap_kernel(n, fan, count, fars, fresh, *refs):
    given = count + (len(fars) > 0) + (0 if fresh else 2)
    x_refs, y_refs = refs[:count], refs[given : given + count]
    sems = refs[given + count + (2 if fars else 0) :]
    send_sem, recv_sem, own_sem = sems[:3]
    pair, half, rank = team(n)
    me = lax.axis_index("fsdp")

    def device(other):
        away = (other // (n // 2) + half) % 2
        return {"seq": (other + away * (n // 2)) % n, "fsdp": 2 * pair + (half + away) % 2}

    barrier = pltpu.get_barrier_semaphore()
    for j in range(1, n):
        pl.semaphore_signal(barrier, inc=1, device_id=device((rank + j) % n), device_id_type=MESH)
    travel = [far for far in fars if far]
    for far in travel:
        pl.semaphore_signal(barrier, inc=1, device_id={"fsdp": (me + fan - far) % fan}, device_id_type=MESH)
    pl.semaphore_wait(barrier, n - 1 + len(travel))
    copies = []
    for k in range(count):
        for j in range(1, n):
            other = (rank + j) % n
            one = pltpu.make_async_remote_copy(
                src_ref=x_refs[k].at[other],
                dst_ref=y_refs[k].at[rank],
                send_sem=send_sem.at[k, j],
                recv_sem=recv_sem.at[k, j],
                device_id=device(other),
                device_id_type=MESH,
            )
            one.start()
            copies.append(one)
    for k in range(count):
        one = pltpu.make_async_copy(x_refs[k].at[rank], y_refs[k].at[rank], own_sem.at[k])
        one.start()
        copies.append(one)
    if fars:
        w_ref, halves = refs[count], refs[given + count : given + count + 2]
        far_send, far_recv, far_own, stage = sems[3:]
        rest = []
        units, cols = halves[0].shape[0], w_ref.shape[1]
        for i, far in enumerate(fars):
            target = (me + far) % fan
            for part in range(2):
                src = w_ref.at[pl.ds((part * fan + target) * units, units), :]
                dst = halves[part].at[:, pl.ds(pl.multiple_of(me * cols, 128), cols)]
                if far:
                    one = pltpu.make_async_remote_copy(
                        src_ref=src,
                        dst_ref=dst,
                        send_sem=far_send.at[i, part],
                        recv_sem=far_recv.at[i, part],
                        device_id={"fsdp": target},
                        device_id_type=MESH,
                    )
                else:
                    one = pltpu.make_async_copy(src, stage.at[part], far_own.at[0, part])
                    rest.append((one, pltpu.make_async_copy(stage.at[part], dst, far_own.at[1, part])))
                one.start()
                if far:
                    copies.append(one)
        for inward, outward in rest:
            inward.wait()
            outward.start()
            copies.append(outward)
    for one in copies:
        one.wait()


def swap(arrays, ident, fars=(), given=None, halves=None):
    n, fan = lax.axis_size("seq"), lax.axis_size("fsdp")
    count = len(arrays)
    size = sum(v.size * 2 for v in arrays)
    operands, outs, alias = list(arrays), [jax.ShapeDtypeStruct(v.shape, v.dtype) for v in arrays], {}
    scratch = [
        pltpu.SemaphoreType.DMA((count, n)),
        pltpu.SemaphoreType.DMA((count, n)),
        pltpu.SemaphoreType.DMA((count,)),
    ]
    if fars:
        operands.append(given)
        shape = (given.shape[0] // (2 * fan), given.shape[1] * fan)
        outs += [jax.ShapeDtypeStruct(shape, given.dtype)] * 2
        scratch += [pltpu.SemaphoreType.DMA((len(fars), 2))] * 2 + [
            pltpu.SemaphoreType.DMA((2, 2)),
            pltpu.VMEM((2, given.shape[0] // (2 * fan), given.shape[1]), given.dtype),
        ]
        if halves is not None:
            operands += list(halves)
            alias = {count + 1: count, count + 2: count + 1}
    return pl.pallas_call(
        functools.partial(swap_kernel, n, fan, count, fars, not fars or halves is None),
        name="swap",
        out_shape=outs,
        in_specs=[pl.BlockSpec(memory_space=pl.ANY)] * len(operands),
        out_specs=[pl.BlockSpec(memory_space=pl.ANY)] * len(outs),
        scratch_shapes=scratch,
        input_output_aliases=alias,
        compiler_params=pltpu.CompilerParams(collective_id=ident, has_side_effects=True),
        cost_estimate=pl.CostEstimate(flops=0, bytes_accessed=size, transcendentals=0),
    )(*operands)


def norm_apply(value, gain):
    return value * lax.rsqrt(jnp.mean(value * value, axis=-1, keepdims=True) + EPS) * gain


def norm_back(value, gain, grad):
    _, pull = jax.vjp(norm_apply, value, gain)
    return pull(grad)


def gate_mix(gate, up):
    return jax.nn.gelu(gate, approximate=True) * up


def counts_below(ids, values):
    total = jnp.zeros_like(values)
    for doc in range(DOCS):
        total = total + jnp.where(values > doc, jnp.sum((ids == doc).astype(jnp.int32)), 0)
    return total


def change_home(value):
    n, fan = lax.axis_size("seq"), lax.axis_size("fsdp")
    pairs = []
    for s in range(n):
        for f in range(fan):
            away = (s // (n // 2) + f) % 2
            target = ((s + n // 2) % n, f ^ 1) if away else (s, f)
            pairs.append((s * fan + f, target[0] * fan + target[1]))
    return lax.ppermute(value, ("seq", "fsdp"), pairs)


def spread(blocks):
    fan, me = lax.axis_size("fsdp"), lax.axis_index("fsdp")
    result = blocks
    for far in range(1, fan):
        block = lax.dynamic_index_in_dim(blocks, (me + far) % fan, 0, True)
        block = lax.ppermute(block, "fsdp", [(f, (f + far) % fan) for f in range(fan)])
        result = lax.dynamic_update_slice_in_dim(result, block, (me - far) % fan, 0)
    return result


def flat(blocks):
    return jnp.transpose(blocks, (1, 0, 2)).reshape(blocks.shape[1], -1)


def by_rows(value):
    return with_layout_constraint(value, Layout(major_to_minor=tuple(range(value.ndim))))


def scatter(grad):
    return lax.psum_scatter(grad, "fsdp", scatter_dimension=0, tiled=True)


def over_seq(arrays, splits, ident):
    n = lax.axis_size("seq")
    if all(
        v.shape[0] % (8 * n) == 0
        and ring_cut(v.shape, s, n)[0] % 8 == 0
        and v.shape[1] % (128 * max(s, 1)) == 0
        for v, s in zip(arrays, splits)
    ):
        return ring_total(arrays, splits, ident)
    return [lax.psum(v, "seq") for v in arrays]


def shards(
    layer_in, encoder, decoder_ids, encoder_ids, rel_buckets,
    norm_self, self_qkv, self_out, rel_table, norm_cross, cross_q, cross_kv, cross_out, norm_ff, ff_in, ff_out,
    cotangent,
):
    seqs, local, width = layer_in.shape
    enc_local = encoder.shape[1]
    parts = lax.axis_size("seq")
    heads = self_qkv.shape[1]
    dh = self_qkv.shape[2] // 3
    own = heads // parts
    rows = seqs * local
    buckets, table_own = rel_table.shape
    length, keys = local * parts, enc_local * parts
    gather = lambda v: lax.all_gather(v, "fsdp", axis=0, tiled=True)

    fan = lax.axis_size("fsdp")
    units = ff_in.shape[1] // (2 * fan)
    part = norm_self.shape[0]
    pair, half, rank = team(parts)

    qkv_w = gather(self_qkv)
    small = jnp.concatenate([norm_self, norm_cross, norm_ff, rel_table.reshape(-1)])
    small = lax.all_gather(small, "fsdp", axis=0, tiled=False)
    early = by_rows(jnp.stack([self_out, cross_q, *jnp.split(cross_kv.reshape(-1, 2 * width), 2, axis=1)]))
    small, early = lax.optimization_barrier((small, early))
    early = lax.all_gather(early, "fsdp", axis=1, tiled=True)
    both_ids = jnp.concatenate([decoder_ids.reshape(-1), encoder_ids.reshape(-1)])
    both_ids = change_home(jnp.pad(both_ids, (0, 1024 - local - enc_local)).reshape(8, 128))
    inner_t = ff_in.T
    by_kernel = (width // fan) % 128 == 0
    both_ids, *halves = swap(
        [jnp.broadcast_to(both_ids[None], (parts, 8, 128))], 13, tuple(range(fan)) if by_kernel else (), inner_t
    )
    if not by_kernel:
        halves = spread(jnp.transpose(inner_t.reshape(2, fan, units, -1), (1, 0, 2, 3)))
        halves = [jnp.transpose(halves[:, i], (1, 0, 2)).reshape(units, width) for i in range(2)]
    gate_t, up_t = halves
    home = change_home(layer_in.reshape(rows, width))
    early = by_rows(early)
    mix_self = early[0].reshape(parts, own * dh, width)
    query_w = early[1].reshape(width, parts, own * dh)
    pairs_w = early[2:]

    gain_first, gain_second, gain_third = (
        small[:, i * part : (i + 1) * part].reshape(width).astype(f32) for i in range(3)
    )
    table = jnp.transpose(small[:, 3 * part :].reshape(-1, buckets, table_own), (1, 0, 2)).reshape(buckets, heads)
    both_ids = both_ids.reshape(parts, 1024)
    ids = both_ids[:, :local].reshape(length)
    enc_ids = both_ids[:, local : local + enc_local].reshape(keys)

    first_seen = counts_below(ids, ids)
    enc_first = counts_below(enc_ids, ids)
    enc_last = counts_below(enc_ids, ids + 1)
    blocks = length // BQ
    bk = 256
    self_rows = jnp.broadcast_to(first_seen[None], (8, length))
    cross_rows = jnp.concatenate([enc_first[None], enc_last[None], jnp.zeros((6, length), jnp.int32)])
    self_limits = jnp.stack(
        [first_seen[::BQ] // bk, (jnp.arange(blocks, dtype=jnp.int32) + 1) * (BQ // bk)]
    )
    cross_limits = jnp.stack([enc_first[::BQ] // bk, (enc_last[BQ - 1 :: BQ] + bk - 1) // bk])

    first_head = rank * own
    table_mine = lax.dynamic_slice_in_dim(table.astype(f32), first_head, own, 1)
    near = rel_buckets[:REACH]
    onehot = (near[:, None] == jnp.arange(buckets, dtype=jnp.int32)[None, :]).astype(f32)
    bias = jnp.einsum("ln,ng->gl", onehot, table_mine, precision=HIGH)
    ext = jnp.concatenate(
        [jnp.full((own, BQ), MASKED, f32), bias, jnp.zeros((own, BQ), f32)], axis=1
    )

    qkv_w, home, gate_t, ext, self_rows, cross_rows, self_limits, cross_limits = lax.optimization_barrier(
        (qkv_w, home, gate_t, ext, self_rows, cross_rows, self_limits, cross_limits)
    )
    qkv_w = qkv_w.reshape(width, parts, own * 3 * dh)

    stream = home.astype(f32)
    normed_first = norm_apply(stream, gain_first).astype(bf16)
    qkv_tok = jnp.einsum("td,dge->gte", normed_first, qkv_w, preferred_element_type=f32).astype(bf16)
    others = change_home(jnp.concatenate([cotangent.reshape(rows, width), encoder.reshape(-1, width)]))
    grad_low, enc_flat = others[:rows], others[rows:]
    (qkv,) = swap([qkv_tok], 10)
    qkv, cross_out, grad_low = lax.optimization_barrier((qkv, cross_out, grad_low))
    if rows == cross_out.shape[0]:
        mix_cross, grad_group = lax.all_gather(jnp.stack([cross_out, grad_low]), "fsdp", axis=1, tiled=True)
    else:
        mix_cross, grad_group = gather(cross_out), gather(grad_low)
    mix_cross = mix_cross.reshape(parts, own * dh, width)
    qkv = qkv.reshape(length, own * 3 * dh)
    out_self, self_t, self_lse = self_forward(self_limits, self_rows, ext, qkv)
    (self_tok,) = swap([out_self.reshape(parts, local, own * dh)], 11)
    after_self = stream + jnp.einsum("gtc,gcd->td", self_tok, mix_self, preferred_element_type=f32)
    normed_second = norm_apply(after_self, gain_second).astype(bf16)
    query_tok = jnp.einsum("td,dgc->gtc", normed_second, query_w, preferred_element_type=f32).astype(bf16)
    pairs_tok = jnp.einsum(
        "td,sdge->sgte", enc_flat, pairs_w.reshape(2, width, parts // 2, -1), preferred_element_type=f32
    )
    pairs_tok = pairs_tok.astype(bf16).reshape(parts, enc_local, -1)
    query_cross, pairs = swap([query_tok, pairs_tok], 12)
    query_cross, pairs = query_cross.reshape(length, own * dh), pairs.reshape(keys, own * 2 * dh)
    out_cross, cross_t, cross_lse = cross_forward(cross_limits, cross_rows, query_cross, pairs)
    (cross_tok,) = swap([out_cross.reshape(parts, local, own * dh)], 11)
    after_cross = after_self + jnp.einsum("gtc,gcd->td", cross_tok, mix_cross, preferred_element_type=f32)
    normed_third = norm_apply(after_cross, gain_third).astype(bf16)
    normed_group = gather(normed_third)
    gate = jnp.einsum("td,fd->tf", normed_group, gate_t, preferred_element_type=f32)
    up = jnp.einsum("td,fd->tf", normed_group, up_t, preferred_element_type=f32)
    hidden = gate_mix(gate, up).astype(bf16)

    grad_hidden = jnp.einsum("td,fd->tf", grad_group, ff_out, preferred_element_type=f32)
    _, pull_mix = jax.vjp(gate_mix, gate, up)
    grad_gate, grad_up = (g.astype(bf16) for g in pull_mix(grad_hidden))
    grad_third_in = jnp.dot(grad_gate, gate_t, preferred_element_type=f32) + jnp.dot(
        grad_up, up_t, preferred_element_type=f32
    )
    grad_third_in = scatter(grad_third_in.astype(bf16))
    outer_part = jnp.dot(hidden, ff_out, preferred_element_type=f32).astype(bf16)
    grad_units = [
        jnp.einsum("tf,td->fd", g, y, preferred_element_type=f32).astype(bf16)
        for g, y in ((grad_gate, normed_group), (grad_up, normed_group), (hidden, grad_group))
    ]
    grad_third_in, outer_part, grad_units = lax.optimization_barrier((grad_third_in, outer_part, grad_units))
    if by_kernel:
        grad_units = jnp.stack([g.reshape(parts, units // parts, width) for g in grad_units], axis=1)
        part_units = grad_units.reshape(3 * units, width)
    grad_third_in = grad_third_in.astype(f32)
    grad_from_third, grad_gain_third = norm_back(after_cross, gain_third, grad_third_in)
    grad_middle = grad_low.astype(f32) + grad_from_third
    middle_low = grad_middle.astype(bf16)
    grad_mix_cross = jnp.einsum("gtc,td->gcd", cross_tok, middle_low, preferred_element_type=f32)
    grad_cross_tok = jnp.einsum("td,gcd->gtc", middle_low, mix_cross, preferred_element_type=f32).astype(bf16)
    (grad_cross,) = swap([grad_cross_tok], 11)
    grad_cross = grad_cross.reshape(length, own * dh)
    grad_query, grad_pairs = cross_backward(
        cross_limits, cross_rows, query_cross, pairs, grad_cross, cross_t, cross_lse
    )
    grad_query_tok, grad_pairs_tok = swap(
        [grad_query.reshape(parts, local, own * dh), grad_pairs.reshape(parts, enc_local, own * 2 * dh)], 12
    )
    grad_query_tok, grad_pairs_tok = flat(grad_query_tok), flat(grad_pairs_tok)
    grad_query_w = jnp.einsum("td,te->de", normed_second, grad_query_tok, preferred_element_type=f32)
    grad_second_in = jnp.einsum("te,de->td", grad_query_tok, query_w.reshape(width, -1), preferred_element_type=f32)
    grad_pairs_w = jnp.einsum("td,te->de", enc_flat, grad_pairs_tok, preferred_element_type=f32)
    grad_encoder = sum(
        jnp.einsum("te,de->td", grad_pairs_tok[:, i * width : (i + 1) * width], pairs_w[i], preferred_element_type=f32)
        for i in range(2)
    )
    grad_from_second, grad_gain_second = norm_back(after_self, gain_second, grad_second_in)
    grad_upper = grad_middle + grad_from_second
    upper_low = grad_upper.astype(bf16)
    grad_mix_self = jnp.einsum("gtc,td->gcd", self_tok, upper_low, preferred_element_type=f32)
    grad_self_tok = jnp.einsum("td,gcd->gtc", upper_low, mix_self, preferred_element_type=f32).astype(bf16)
    grad_mid = jnp.concatenate(
        [
            grad_query_w.astype(bf16),
            grad_pairs_w.astype(bf16),
            grad_mix_cross.reshape(width, width).astype(bf16),
            grad_mix_self.reshape(width, width).astype(bf16),
        ],
        axis=1,
    )
    grad_self_tok, grad_mid = lax.optimization_barrier((grad_self_tok, grad_mid))
    part_mid = scatter(grad_mid)
    (grad_self,) = swap([grad_self_tok], 11)
    grad_self = grad_self.reshape(length, own * dh)
    grad_qkv, tile_sums = self_backward(self_limits, self_rows, ext, qkv, grad_self, self_t, self_lse)
    (grad_qkv_tok,) = swap([grad_qkv.reshape(parts, local, own * 3 * dh)], 10)
    grad_qkv_tok = flat(grad_qkv_tok)
    grad_qkv_w = jnp.einsum("td,te->de", normed_first, grad_qkv_tok, preferred_element_type=f32)
    grad_first_in = jnp.einsum("te,de->td", grad_qkv_tok, qkv_w.reshape(width, -1), preferred_element_type=f32)
    grad_from_first, grad_gain_first = norm_back(stream, gain_first, grad_first_in)
    grad_layer_in = (grad_upper + grad_from_first).astype(bf16)
    if not by_kernel:
        part_units = grad_units
    bucket_line = jnp.concatenate(
        [jnp.full((BQ,), -1, jnp.int32), near, jnp.full((BQ + bk,), -1, jnp.int32)]
    )
    by_tile = jnp.stack([bucket_line[t * bk + 1 : t * bk + 1 + BQ + bk] for t in range(tile_count(bk))])
    in_bucket = (by_tile[:, :, None] == jnp.arange(buckets, dtype=jnp.int32)).astype(f32)
    by_bucket = jnp.einsum("twn,gtw->ng", in_bucket, tile_sums, precision=HIGH)
    grad_table = lax.dynamic_update_slice_in_dim(jnp.zeros((buckets, heads), f32), by_bucket, first_head, 1)

    gains = jnp.concatenate(
        [g.reshape(-1, part) for g in (grad_gain_first, grad_gain_second, grad_gain_third)], axis=1
    )
    tables = jnp.transpose(grad_table.reshape(buckets, -1, table_own), (1, 0, 2)).reshape(-1, buckets * table_own)
    small_grads = lax.psum(jnp.concatenate([gains, tables], axis=1).astype(bf16), "fsdp")
    small_grads = lax.dynamic_index_in_dim(small_grads, lax.axis_index("fsdp"), 0, False)
    small_size = small_grads.shape[0]
    small_grads = jnp.pad(small_grads, (0, parts * 1024 - small_size)).reshape(parts * 8, 128)
    going_home = jnp.concatenate([grad_layer_in, grad_encoder.astype(bf16)])
    going_home, small_grads, grad_qkv_w, part_units, part_mid = lax.optimization_barrier(
        (going_home, small_grads, grad_qkv_w.astype(bf16), part_units, part_mid)
    )
    part_last = scatter(grad_qkv_w)
    going_home = change_home(going_home)
    if by_kernel:
        total_inner, total_outer, outer_sum = units_total(part_units, outer_part, 0)
    else:
        grad_units = [lax.psum(g, "seq") for g in grad_units]
        total_inner = spread(jnp.transpose(jnp.stack(grad_units[:2]).reshape(2, units, fan, -1), (2, 0, 1, 3)))
        total_outer, outer_sum = grad_units[2], scatter(outer_part).astype(f32)
    total_mid, total_qkv, small_total = over_seq([part_mid, part_last, small_grads], (2, 2, 1), 1)
    layer_out = (after_cross + outer_sum).astype(bf16)
    layer_out, total_inner, total_outer, total_mid, total_qkv, going_home = lax.optimization_barrier(
        (layer_out, total_inner, total_outer, total_mid, total_qkv, going_home)
    )
    layer_out = change_home(layer_out).reshape(seqs, local, width)
    grad_layer_in = going_home[:rows].astype(f32).reshape(seqs, local, width)
    grad_encoder = going_home[rows:].astype(f32).reshape(seqs, enc_local, width)
    if by_kernel:
        total_inner = jnp.transpose(total_inner.reshape(parts, fan, 2, units // parts, -1), (4, 2, 1, 0, 3))
    else:
        total_inner = jnp.transpose(total_inner, (3, 1, 0, 2))
    total_inner = total_inner.reshape(-1, 2 * fan * units).astype(f32)
    total_outer, total_mid, total_qkv = (v.astype(f32) for v in (total_outer, total_mid, total_qkv))
    total_query, total_mix_cross = total_mid[:, :width], total_mid[:, 3 * width : 4 * width]
    total_pairs = total_mid[:, width : 3 * width].reshape(-1, heads, 2 * dh)
    total_mix_self, total_qkv = total_mid[:, 4 * width :], total_qkv.reshape(-1, heads, 3 * dh)
    mine = small_total.reshape(-1)[:small_size].astype(f32)
    total_gain_first, total_gain_second, total_gain_third = (mine[i * part : (i + 1) * part] for i in range(3))
    total_table = mine[3 * part :].reshape(buckets, table_own)
    return (
        layer_out, grad_layer_in, grad_encoder, total_gain_first, total_qkv, total_mix_self, total_table,
        total_gain_second, total_query, total_pairs, total_mix_cross, total_gain_third, total_inner, total_outer,
    )


def solution(mesh):
    in_specs = (
        P("fsdp", "seq", None), P("fsdp", "seq", None), P("fsdp", "seq"), P("fsdp", "seq"), P(),
        P("fsdp"), P("fsdp", None, None), P("fsdp", None), P(None, "fsdp"), P("fsdp"), P("fsdp", None),
        P("fsdp", None, None), P("fsdp", None), P("fsdp"), P("fsdp", None), P("fsdp", None),
        P("fsdp", "seq", None),
    )
    out_specs = (
        P("fsdp", "seq", None), P("fsdp", "seq", None), P("fsdp", "seq", None), P("fsdp"), P("fsdp", None, None),
        P("fsdp", None), P(None, "fsdp"), P("fsdp"), P("fsdp", None), P("fsdp", None, None), P("fsdp", None),
        P("fsdp"), P("fsdp", None), P("fsdp", None),
    )
    return jax.shard_map(shards, mesh=mesh, in_specs=in_specs, out_specs=out_specs, check_vma=False)
```

```python
import functools

import jax
import jax.numpy as jnp
from jax import lax
from jax.experimental import pallas as pl
from jax.experimental.layout import Layout, with_layout_constraint
from jax.experimental.pallas import tpu as pltpu
from jax.sharding import PartitionSpec as P

EPS = 1e-06
HIGH = lax.Precision.HIGHEST
MASKED = -1e30
DOCS = 4

BQ = 256
REACH = 1024


def blk(index, size):
    return pl.ds(pl.multiple_of(index * size, size), size)


def turn(value):
    return jnp.transpose(value.astype(jnp.float32), (1, 0))


def bias_tiles(ext_ref, tile_ref, own):
    for h in range(own):
        line = jnp.broadcast_to(ext_ref[h : h + 1, :], tile_ref.shape[1:])
        tile_ref[h] = pltpu.roll(line, 0, 1, stride=1, stride_axis=0)


def unpack(ref, own, width, picks, flips, base):
    block = 256

    def one(b, _):
        rows = blk(b, block)
        value = ref[rows, :]
        if flips:
            flat = turn(value).astype(jnp.bfloat16)
            for target, piece in flips:
                for h in range(own):
                    at = h * width + piece * 64
                    target[base + h, :, rows] = flat[at : at + 64]
        for target, piece in picks:
            for h in range(own):
                at = h * width + piece * 64
                target[base + h, rows, :] = value[:, at : at + 64]
        return 0

    lax.fori_loop(0, ref.shape[0] // block, one, 0)


def dot(a, b):
    return jnp.dot(a, b, preferred_element_type=jnp.float32)


def score(own_index, key_tile, query_t, tile_ref, t, low, high, first_key):
    value = dot(key_tile, query_t)
    place = lax.broadcasted_iota(jnp.int32, value.shape, 0)
    keep = place >= low - first_key
    if high is not None:
        keep = keep & (place < high - first_key)
    else:
        value = value + tile_ref[own_index, :, blk(t + 1, BQ)]
    return jnp.where(keep, value, MASKED)


def forward_body(own, bk, causal, lim_ref, rows_ref, q_t, k_rows, v_t, tile_ref, o_ref, ot_ref, lse_ref):
    length = o_ref.shape[0]

    def q_block(i, _):
        cols = blk(i, BQ)
        queries = [q_t[h, :, cols] for h in range(own)]
        low = rows_ref[0:1, cols]
        high = None if causal else rows_ref[1:2, cols]

        def k_block(j, carry):
            keys = blk(j, bk)
            t = i - j
            out = []
            for h in range(own):
                top, total, acc = carry[h]
                s = score(h, k_rows[h, keys, :], queries[h], tile_ref, t, low, high, j * bk)
                new_top = jnp.maximum(top, jnp.max(s, axis=0, keepdims=True))
                p = jnp.exp(s - new_top)
                scale = jnp.exp(top - new_top)
                total = total * scale + jnp.sum(p, axis=0, keepdims=True)
                acc = acc * scale + dot(v_t[h, :, keys], p.astype(jnp.bfloat16))
                out.append((new_top, total, acc))
            return tuple(out)

        start = tuple(
            (
                jnp.full((1, BQ), MASKED, jnp.float32),
                jnp.zeros((1, BQ), jnp.float32),
                jnp.zeros((64, BQ), jnp.float32),
            )
            for _ in range(own)
        )
        ends = lax.fori_loop(lim_ref[0, i], lim_ref[1, i], k_block, start)
        for h in range(own):
            top, total, acc = ends[h]
            ot_ref[h * 64 : h * 64 + 64, cols] = acc / total
            lse_ref[h : h + 1, cols] = top + jnp.log(total)
        o_ref[cols, :] = turn(ot_ref[:, cols]).astype(jnp.bfloat16)
        return 0

    lax.fori_loop(0, length // BQ, q_block, 0)


def self_forward_kernel(own, bk, lim_ref, rows_ref, ext_ref, x_ref, o_ref, ot_ref, lse_ref, q_t, k_rows, v_t, tile_ref):
    bias_tiles(ext_ref, tile_ref, own)
    unpack(x_ref, own, 192, [(k_rows, 1)], [(q_t, 0), (v_t, 2)], 0)
    forward_body(own, bk, True, lim_ref, rows_ref, q_t, k_rows, v_t, tile_ref, o_ref, ot_ref, lse_ref)


def cross_forward_kernel(own, bk, lim_ref, rows_ref, q_ref, kv_ref, o_ref, ot_ref, lse_ref, q_t, k_rows, v_t):
    unpack(q_ref, own, 64, [], [(q_t, 0)], 0)
    unpack(kv_ref, own, 128, [(k_rows, 0)], [(v_t, 1)], 0)
    forward_body(own, bk, False, lim_ref, rows_ref, q_t, k_rows, v_t, None, o_ref, ot_ref, lse_ref)


def backward_body(
    own, bk, causal, lim_ref, rows_ref, do_ref, ot_ref, lse_ref,
    q_t, q_rows, k_t, k_rows, v_rows, do_t, do_rows, tile_ref, sum_ref, dq_t, dk, dv,
):
    length = do_ref.shape[0]
    dk[...] = jnp.zeros_like(dk)
    dv[...] = jnp.zeros_like(dv)
    if causal:
        sum_ref[...] = jnp.zeros_like(sum_ref)

    def q_block(i, _):
        cols = blk(i, BQ)
        low = rows_ref[0:1, cols]
        high = None if causal else rows_ref[1:2, cols]
        per_head = []
        for h in range(own):
            grad_t = do_t[h, :, cols]
            delta = jnp.sum(
                grad_t.astype(jnp.float32) * ot_ref[h * 64 : h * 64 + 64, cols], axis=0, keepdims=True
            )
            per_head.append((q_t[h, :, cols], grad_t, delta, lse_ref[h : h + 1, cols]))

        def k_block(j, carry):
            keys = blk(j, bk)
            t = i - j
            out = []
            for h in range(own):
                query_t, grad_t, delta, lse = per_head[h]
                s = score(h, k_rows[h, keys, :], query_t, tile_ref, t, low, high, j * bk)
                p = jnp.exp(s - lse)
                dp = dot(v_rows[h, keys, :], grad_t)
                ds = (p * (dp - delta)).astype(jnp.bfloat16)
                dv[h, keys, :] += dot(p.astype(jnp.bfloat16), do_rows[h, cols, :])
                dk[h, keys, :] += dot(ds, q_rows[h, cols, :])
                if causal:
                    sum_ref[h, :, blk(t, BQ)] += ds.astype(jnp.float32)
                out.append(carry[h] + dot(k_t[h, :, keys], ds))
            return tuple(out)

        ends = lax.fori_loop(
            lim_ref[0, i],
            lim_ref[1, i],
            k_block,
            tuple(jnp.zeros((64, BQ), jnp.float32) for _ in range(own)),
        )
        for h in range(own):
            dq_t[h * 64 : h * 64 + 64, cols] = ends[h]
        return 0

    lax.fori_loop(0, length // BQ, q_block, 0)


def diagonal_sums(sum_ref, u_ref, own):
    flip = lax.broadcasted_iota(jnp.int32, (BQ, BQ), 0) + lax.broadcasted_iota(jnp.int32, (BQ, BQ), 1) == BQ - 1
    flip = jnp.where(flip, 1.0, 0.0).astype(jnp.bfloat16)
    for h in range(own):
        grid = sum_ref[h]
        high = grid.astype(jnp.bfloat16)
        low = (grid - high.astype(jnp.float32)).astype(jnp.bfloat16)
        upside = dot(flip, high) + dot(flip, low)
        wide = jnp.concatenate([upside, jnp.zeros((BQ, BQ), jnp.float32)], axis=1)
        aligned = pltpu.roll(wide, 0, 1, stride=1, stride_axis=0)
        u_ref[h : h + 1, :] = jnp.sum(aligned, axis=0, keepdims=True)


def self_backward_kernel(
    own, bk, lim_ref, rows_ref, ext_ref, x_ref, do_ref, ot_ref, lse_ref, dx_ref, u_ref,
    q_t, q_rows, k_t, k_rows, v_rows, do_t, do_rows, tile_ref, sum_ref, dq_t, dk, dv,
):
    bias_tiles(ext_ref, tile_ref, own)
    unpack(x_ref, own, 192, [(q_rows, 0), (k_rows, 1), (v_rows, 2)], [(q_t, 0), (k_t, 1)], 0)
    unpack(do_ref, own, 64, [(do_rows, 0)], [(do_t, 0)], 0)
    backward_body(
        own, bk, True, lim_ref, rows_ref, do_ref, ot_ref, lse_ref,
        q_t, q_rows, k_t, k_rows, v_rows, do_t, do_rows, tile_ref, sum_ref, dq_t, dk, dv,
    )
    diagonal_sums(sum_ref, u_ref, own)

    def pack(b, _):
        rows = blk(b, 256)
        dq = turn(dq_t[:, rows])
        pieces = []
        for h in range(own):
            pieces += [dq[:, h * 64 : h * 64 + 64], dk[h, rows, :], dv[h, rows, :]]
        dx_ref[rows, :] = jnp.concatenate(pieces, axis=1).astype(jnp.bfloat16)
        return 0

    lax.fori_loop(0, x_ref.shape[0] // 256, pack, 0)


def cross_backward_kernel(
    own, bk, lim_ref, rows_ref, q_ref, kv_ref, do_ref, ot_ref, lse_ref, dq_ref, dkv_ref,
    q_t, q_rows, k_t, k_rows, v_rows, do_t, do_rows, dq_t, dk, dv,
):
    unpack(q_ref, own, 64, [(q_rows, 0)], [(q_t, 0)], 0)
    unpack(kv_ref, own, 128, [(k_rows, 0), (v_rows, 1)], [(k_t, 0)], 0)
    unpack(do_ref, own, 64, [(do_rows, 0)], [(do_t, 0)], 0)
    backward_body(
        own, bk, False, lim_ref, rows_ref, do_ref, ot_ref, lse_ref,
        q_t, q_rows, k_t, k_rows, v_rows, do_t, do_rows, None, None, dq_t, dk, dv,
    )

    def pack_q(b, _):
        rows = blk(b, 256)
        dq_ref[rows, :] = turn(dq_t[:, rows]).astype(jnp.bfloat16)
        return 0

    def pack_kv(b, _):
        rows = blk(b, 256)
        pieces = []
        for h in range(own):
            pieces += [dk[h, rows, :], dv[h, rows, :]]
        dkv_ref[rows, :] = jnp.concatenate(pieces, axis=1).astype(jnp.bfloat16)
        return 0

    lax.fori_loop(0, q_ref.shape[0] // 256, pack_q, 0)
    lax.fori_loop(0, kv_ref.shape[0] // 256, pack_kv, 0)


SMEM = pl.BlockSpec(memory_space=pltpu.SMEM)
VMEM = pl.BlockSpec(memory_space=pltpu.VMEM)
bf16, f32 = jnp.bfloat16, jnp.float32


def call(body, name, operands, outs, scratch, flops):
    size = sum(v.size * v.dtype.itemsize for v in operands)
    return pl.pallas_call(
        body,
        name=name,
        out_shape=[jax.ShapeDtypeStruct(s, d) for s, d in outs],
        in_specs=[SMEM] + [VMEM] * (len(operands) - 1),
        out_specs=[VMEM] * len(outs),
        scratch_shapes=[pltpu.VMEM(s, d) for s, d in scratch],
        compiler_params=pltpu.CompilerParams(vmem_limit_bytes=40 << 20),
        cost_estimate=pl.CostEstimate(flops=0, bytes_accessed=size, transcendentals=0),
    )(*operands)


def self_forward(limits, rows, ext, x, bk=BQ):
    length, own = x.shape[0], x.shape[1] // 192
    return call(
        functools.partial(self_forward_kernel, own, bk),
        "self_forward",
        [limits, rows, ext, x],
        [((length, own * 64), bf16), ((own * 64, length), f32), ((own, length), f32)],
        [
            ((own, 64, length), bf16),
            ((own, length, 64), bf16),
            ((own, 64, length), bf16),
            ((own, BQ, REACH + 2 * BQ), f32),
        ],
        length * length * own * 64,
    )


def cross_forward(limits, rows, q, kv, bk=BQ):
    length, own, keys = q.shape[0], q.shape[1] // 64, kv.shape[0]
    return call(
        functools.partial(cross_forward_kernel, own, bk),
        "cross_forward",
        [limits, rows, q, kv],
        [((length, own * 64), bf16), ((own * 64, length), f32), ((own, length), f32)],
        [((own, 64, length), bf16), ((own, keys, 64), bf16), ((own, 64, keys), bf16)],
        length * keys * own * 128,
    )


def self_backward(limits, rows, ext, x, grad, o_t, lse, bk=BQ):
    length, own = x.shape[0], x.shape[1] // 192
    return call(
        functools.partial(self_backward_kernel, own, bk),
        "self_backward",
        [limits, rows, ext, x, grad, o_t, lse],
        [((length, own * 192), bf16), ((own, REACH + 2 * BQ), f32)],
        [
            ((own, 64, length), bf16),
            ((own, length, 64), bf16),
            ((own, 64, length), bf16),
            ((own, length, 64), bf16),
            ((own, length, 64), bf16),
            ((own, 64, length), bf16),
            ((own, length, 64), bf16),
            ((own, BQ, REACH + 2 * BQ), f32),
            ((own, BQ, REACH + BQ), f32),
            ((own * 64, length), f32),
            ((own, length, 64), f32),
            ((own, length, 64), f32),
        ],
        length * length * own * 160,
    )


def cross_backward(limits, rows, q, kv, grad, o_t, lse, bk=BQ):
    length, own, keys = q.shape[0], q.shape[1] // 64, kv.shape[0]
    return call(
        functools.partial(cross_backward_kernel, own, bk),
        "cross_backward",
        [limits, rows, q, kv, grad, o_t, lse],
        [((length, own * 64), bf16), ((keys, own * 128), bf16)],
        [
            ((own, 64, length), bf16),
            ((own, length, 64), bf16),
            ((own, 64, keys), bf16),
            ((own, keys, 64), bf16),
            ((own, keys, 64), bf16),
            ((own, 64, length), bf16),
            ((own, length, 64), bf16),
            ((own * 64, length), f32),
            ((own, keys, 64), f32),
            ((own, keys, 64), f32),
        ],
        length * keys * own * 320,
    )


MESH = pl.DeviceIdType.MESH


def ring_place(index, n):
    z, x = index // 2, index % 2
    return z + x * (n - 1 - 2 * z)


def ring_index(place, n):
    x = place // (n // 2)
    z = place + x * (n - 1 - 2 * place)
    return 2 * z + x


def ring_greet(n, others):
    place = ring_place(lax.axis_index("seq"), n)
    right = ring_index((place + 1) % n, n)
    left = ring_index((place + n - 1) % n, n)
    barrier = pltpu.get_barrier_semaphore()
    for neighbour in (left, right):
        pl.semaphore_signal(barrier, inc=1, device_id={"seq": neighbour}, device_id_type=MESH)
    for other in others:
        pl.semaphore_signal(barrier, inc=1, device_id={"fsdp": other}, device_id_type=MESH)
    pl.semaphore_wait(barrier, 2 + len(others))
    return place, right, left


def ring_cut(shape, split, n):
    rows, cols = shape[0] // n, shape[1]
    return (rows, cols // split) if split > 0 else (rows // -split, cols)


def ring_window(ref, shape, split, n, piece, chunk):
    whole = shape[0] // n
    rows, cols = ring_cut(shape, split, n)
    if split > 0:
        return ref.at[pl.ds(chunk * whole, rows), pl.ds(piece * cols, cols)]
    return ref.at[pl.ds(chunk * whole + piece * rows, rows), :]


def ring_kernel(n, splits, *refs):
    count = len(splits)
    x_refs, y_refs, slots = refs[:count], refs[count : 2 * count], refs[2 * count : 3 * count]
    send_sem, recv_sem = refs[3 * count :]
    place, right, left = ring_greet(n, [])
    streams = [(k, piece, piece % 2) for k in range(count) for piece in range(abs(splits[k]))]

    def window(ref, k, piece, chunk):
        return ring_window(ref, x_refs[k].shape, splits[k], n, piece, chunk)

    def chunk_at(down, step):
        return (place + 1 + step) % n if down else (place + 2 * n - 1 - step) % n

    copies = {}

    def start(number, step, src, dst, down):
        copies[number, step] = pltpu.make_async_remote_copy(
            src_ref=src,
            dst_ref=dst,
            send_sem=send_sem.at[number, step],
            recv_sem=recv_sem.at[number, step],
            device_id={"seq": left if down else right},
            device_id_type=MESH,
        )
        copies[number, step].start()

    for number, (k, piece, down) in enumerate(streams):
        start(number, 0, window(x_refs[k], k, piece, place), window(slots[k], k, piece, 0), down)
    for step in range(n - 1):
        for number, (k, piece, down) in enumerate(streams):
            copies[number, step].wait_recv()
            chunk = chunk_at(down, step)
            mine = window(x_refs[k], k, piece, chunk)
            landed = window(slots[k], k, piece, step)
            total = landed[...].astype(jnp.float32) + mine[...].astype(jnp.float32)
            if step < n - 2:
                landed[...] = total.astype(jnp.bfloat16)
                start(number, step + 1, landed, window(slots[k], k, piece, step + 1), down)
            else:
                done = window(y_refs[k], k, piece, chunk)
                done[...] = total.astype(jnp.bfloat16)
                start(number, n - 1, done, done, down)
    for step in range(n - 1):
        for number, (k, piece, down) in enumerate(streams):
            copies[number, n - 1 + step].wait_recv()
            if step < n - 2:
                done = window(y_refs[k], k, piece, chunk_at(down, n - 1 + step))
                start(number, n + step, done, done, down)
    for one in copies.values():
        one.wait_send()


def ring_call(body, name, arrays, outs, scratch, ident):
    size = sum(v.size * 2 for v in arrays)
    return pl.pallas_call(
        body,
        name=name,
        out_shape=[jax.ShapeDtypeStruct(s, d) for s, d in outs],
        in_specs=[pl.BlockSpec(memory_space=pltpu.VMEM)] * len(arrays),
        out_specs=[pl.BlockSpec(memory_space=pltpu.VMEM)] * len(outs),
        scratch_shapes=scratch,
        compiler_params=pltpu.CompilerParams(
            collective_id=ident, has_side_effects=True, vmem_limit_bytes=48 << 20
        ),
        cost_estimate=pl.CostEstimate(flops=0, bytes_accessed=60 * size, transcendentals=0),
    )(*arrays)


def ring_total(arrays, splits, ident):
    n = lax.axis_size("seq")
    streams = sum(abs(s) for s in splits)
    return ring_call(
        functools.partial(ring_kernel, n, splits),
        "ring_total",
        arrays,
        [(v.shape, jnp.bfloat16) for v in arrays],
        [pltpu.VMEM((v.shape[0] // n * (n - 1), v.shape[1]), jnp.bfloat16) for v in arrays]
        + [pltpu.SemaphoreType.DMA((streams, 2 * n - 2))] * 2,
        ident,
    )


def units_kernel(
    n, fan, x_ref, part_ref, inner_ref, outer_ref, sum_ref, slots, acc, landed,
    down_send, down_recv, swap_send, swap_recv, own_sem, send_sem, recv_sem, part_send, part_recv,
):
    s, me = lax.axis_index("seq"), lax.axis_index("fsdp")
    rows, width = acc.shape[0] // 3, x_ref.shape[1]
    cols = width // fan
    block = 2 * fan * rows
    place, right, left = ring_greet(n, [(me + far) % fan for far in range(1, fan)])
    tokens = sum_ref.shape[0]
    parts = []
    for far in range(1, fan):
        target = (me + far) % fan
        one = pltpu.make_async_remote_copy(
            src_ref=part_ref.at[pl.ds(target * tokens, tokens), :],
            dst_ref=landed.at[far],
            send_sem=part_send.at[far],
            recv_sem=part_recv.at[far],
            device_id={"fsdp": target},
            device_id_type=MESH,
        )
        one.start()
        parts.append(one)

    sums = {}

    def piece_of(ref, at, piece):
        return ref.at[pl.ds(at * 3 * rows, 3 * rows), pl.ds(piece * cols, cols)]

    def send_sum(piece, step, src):
        to = left if piece >= fan // 2 else right
        sums[piece, step] = pltpu.make_async_remote_copy(
            src_ref=src,
            dst_ref=piece_of(slots, step, piece),
            send_sem=down_send.at[piece, step],
            recv_sem=down_recv.at[piece, step],
            device_id={"seq": to},
            device_id_type=MESH,
        )
        sums[piece, step].start()

    def chunk(piece, step):
        return ring_index((place + 1 + step) % n if piece >= fan // 2 else (place + 2 * n - 1 - step) % n, n)

    for piece in range(fan):
        send_sum(piece, 0, piece_of(x_ref, chunk(piece, 0), piece))
    for step in range(n - 1):
        for piece in range(fan):
            sums[piece, step].wait_recv()
            arrived = piece_of(slots, step, piece)
            mine = piece_of(x_ref, chunk(piece, step + 1), piece)
            total = (arrived[...].astype(jnp.float32) + mine[...].astype(jnp.float32)).astype(jnp.bfloat16)
            if step < n - 2:
                arrived[...] = total
                send_sum(piece, step + 1, arrived)
            else:
                acc[:, piece * cols : (piece + 1) * cols] = total
    moves = []
    for far in range(fan):
        target = (me + far) % fan
        for half in range(2):
            src = acc.at[pl.ds(half * rows, rows), pl.ds(pl.multiple_of(target * cols, 128), cols)]
            dst = inner_ref.at[pl.ds(s * block + (me * 2 + half) * rows, rows), :]
            if far:
                one = pltpu.make_async_remote_copy(
                    src_ref=src,
                    dst_ref=dst,
                    send_sem=swap_send.at[far, half],
                    recv_sem=swap_recv.at[far, half],
                    device_id={"fsdp": target},
                    device_id_type=MESH,
                )
            else:
                one = pltpu.make_async_copy(src, dst, own_sem.at[half])
            one.start()
            moves.append(one)
    mine = pltpu.make_async_copy(
        acc.at[pl.ds(2 * rows, rows), :], outer_ref.at[pl.ds(s * rows, rows), :], own_sem.at[2]
    )
    mine.start()
    copies = {}
    outs = ((outer_ref, (n * rows, width), 2), (inner_ref, (n * block, cols), -2))

    def start(k, piece, step):
        ref, shape, split = outs[k]
        chunk = ring_index((place + step) % n if piece else (place + n - step) % n, n)
        view = ring_window(ref, shape, split, n, piece, chunk)
        copies[k, piece, step] = pltpu.make_async_remote_copy(
            src_ref=view,
            dst_ref=view,
            send_sem=send_sem.at[2 * k + piece, step],
            recv_sem=recv_sem.at[2 * k + piece, step],
            device_id={"seq": left if piece else right},
            device_id_type=MESH,
        )
        copies[k, piece, step].start()

    mine.wait()
    start(0, 0, 0)
    start(0, 1, 0)
    for one in moves:
        one.wait()
    start(1, 0, 0)
    start(1, 1, 0)
    for step in range(n - 1):
        for k in range(2):
            for piece in range(2):
                copies[k, piece, step].wait_recv()
                if step < n - 2:
                    start(k, piece, step + 1)
    total = part_ref[pl.ds(pl.multiple_of(me * tokens, tokens), tokens), :].astype(jnp.float32)
    for far in range(1, fan):
        parts[far - 1].wait()
        total = total + landed[far].astype(jnp.float32)
    sum_ref[...] = total
    for one in [*copies.values(), *sums.values()]:
        one.wait_send()


def units_total(grads, part, ident):
    n, fan = lax.axis_size("seq"), lax.axis_size("fsdp")
    rows, width = grads.shape[0] // (3 * n), grads.shape[1]
    tokens = part.shape[0] // fan
    sems = lambda *shape: pltpu.SemaphoreType.DMA(shape)
    return ring_call(
        functools.partial(units_kernel, n, fan),
        "units_total",
        [grads, part],
        [
            ((n * 2 * fan * rows, width // fan), jnp.bfloat16),
            ((n * rows, width), jnp.bfloat16),
            ((tokens, part.shape[1]), jnp.float32),
        ],
        [
            pltpu.VMEM(((n - 1) * 3 * rows, width), jnp.bfloat16),
            pltpu.VMEM((3 * rows, width), jnp.bfloat16),
            pltpu.VMEM((fan, tokens, part.shape[1]), jnp.bfloat16),
        ]
        + [sems(fan, n - 1), sems(fan, n - 1), sems(fan, 2), sems(fan, 2), sems(3)]
        + [sems(4, n - 1), sems(4, n - 1), sems(fan), sems(fan)],
        ident,
    )


def team(n):
    s, f = lax.axis_index("seq"), lax.axis_index("fsdp")
    half = s // (n // 2)
    away = (half + f) % 2
    return f // 2, half, (s + away * (n // 2)) % n


def swap_kernel(n, fan, count, fars, fresh, *refs):
    given = count + (len(fars) > 0) + (0 if fresh else 2)
    x_refs, y_refs = refs[:count], refs[given : given + count]
    sems = refs[given + count + (2 if fars else 0) :]
    send_sem, recv_sem, own_sem = sems[:3]
    pair, half, rank = team(n)
    me = lax.axis_index("fsdp")

    def device(other):
        away = (other // (n // 2) + half) % 2
        return {"seq": (other + away * (n // 2)) % n, "fsdp": 2 * pair + (half + away) % 2}

    barrier = pltpu.get_barrier_semaphore()
    for j in range(1, n):
        pl.semaphore_signal(barrier, inc=1, device_id=device((rank + j) % n), device_id_type=MESH)
    travel = [far for far in fars if far]
    for far in travel:
        pl.semaphore_signal(barrier, inc=1, device_id={"fsdp": (me + fan - far) % fan}, device_id_type=MESH)
    pl.semaphore_wait(barrier, n - 1 + len(travel))
    copies = []
    for k in range(count):
        for j in range(1, n):
            other = (rank + j) % n
            one = pltpu.make_async_remote_copy(
                src_ref=x_refs[k].at[other],
                dst_ref=y_refs[k].at[rank],
                send_sem=send_sem.at[k, j],
                recv_sem=recv_sem.at[k, j],
                device_id=device(other),
                device_id_type=MESH,
            )
            one.start()
            copies.append(one)
    for k in range(count):
        one = pltpu.make_async_copy(x_refs[k].at[rank], y_refs[k].at[rank], own_sem.at[k])
        one.start()
        copies.append(one)
    if fars:
        w_ref, halves = refs[count], refs[given + count : given + count + 2]
        far_send, far_recv, far_own, stage = sems[3:]
        rest = []
        units, cols = halves[0].shape[0], w_ref.shape[1]
        for i, far in enumerate(fars):
            target = (me + far) % fan
            for part in range(2):
                src = w_ref.at[pl.ds((part * fan + target) * units, units), :]
                dst = halves[part].at[:, pl.ds(pl.multiple_of(me * cols, 128), cols)]
                if far:
                    one = pltpu.make_async_remote_copy(
                        src_ref=src,
                        dst_ref=dst,
                        send_sem=far_send.at[i, part],
                        recv_sem=far_recv.at[i, part],
                        device_id={"fsdp": target},
                        device_id_type=MESH,
                    )
                else:
                    one = pltpu.make_async_copy(src, stage.at[part], far_own.at[0, part])
                    rest.append((one, pltpu.make_async_copy(stage.at[part], dst, far_own.at[1, part])))
                one.start()
                if far:
                    copies.append(one)
        for inward, outward in rest:
            inward.wait()
            outward.start()
            copies.append(outward)
    for one in copies:
        one.wait()


def swap(arrays, ident, fars=(), given=None, halves=None):
    n, fan = lax.axis_size("seq"), lax.axis_size("fsdp")
    count = len(arrays)
    size = sum(v.size * 2 for v in arrays)
    operands, outs, alias = list(arrays), [jax.ShapeDtypeStruct(v.shape, v.dtype) for v in arrays], {}
    scratch = [
        pltpu.SemaphoreType.DMA((count, n)),
        pltpu.SemaphoreType.DMA((count, n)),
        pltpu.SemaphoreType.DMA((count,)),
    ]
    if fars:
        operands.append(given)
        shape = (given.shape[0] // (2 * fan), given.shape[1] * fan)
        outs += [jax.ShapeDtypeStruct(shape, given.dtype)] * 2
        scratch += [pltpu.SemaphoreType.DMA((len(fars), 2))] * 2 + [
            pltpu.SemaphoreType.DMA((2, 2)),
            pltpu.VMEM((2, given.shape[0] // (2 * fan), given.shape[1]), given.dtype),
        ]
        if halves is not None:
            operands += list(halves)
            alias = {count + 1: count, count + 2: count + 1}
    return pl.pallas_call(
        functools.partial(swap_kernel, n, fan, count, fars, not fars or halves is None),
        name="swap",
        out_shape=outs,
        in_specs=[pl.BlockSpec(memory_space=pl.ANY)] * len(operands),
        out_specs=[pl.BlockSpec(memory_space=pl.ANY)] * len(outs),
        scratch_shapes=scratch,
        input_output_aliases=alias,
        compiler_params=pltpu.CompilerParams(collective_id=ident, has_side_effects=True),
        cost_estimate=pl.CostEstimate(flops=0, bytes_accessed=size, transcendentals=0),
    )(*operands)


def norm_apply(value, gain):
    return value * lax.rsqrt(jnp.mean(value * value, axis=-1, keepdims=True) + EPS) * gain


def norm_back(value, gain, grad):
    _, pull = jax.vjp(norm_apply, value, gain)
    return pull(grad)


def gate_mix(gate, up):
    return jax.nn.gelu(gate, approximate=True) * up


def counts_below(ids, values):
    total = jnp.zeros_like(values)
    for doc in range(DOCS):
        total = total + jnp.where(values > doc, jnp.sum((ids == doc).astype(jnp.int32)), 0)
    return total


def change_home(value):
    n, fan = lax.axis_size("seq"), lax.axis_size("fsdp")
    pairs = []
    for s in range(n):
        for f in range(fan):
            away = (s // (n // 2) + f) % 2
            target = ((s + n // 2) % n, f ^ 1) if away else (s, f)
            pairs.append((s * fan + f, target[0] * fan + target[1]))
    return lax.ppermute(value, ("seq", "fsdp"), pairs)


def spread(blocks):
    fan, me = lax.axis_size("fsdp"), lax.axis_index("fsdp")
    result = blocks
    for far in range(1, fan):
        block = lax.dynamic_index_in_dim(blocks, (me + far) % fan, 0, True)
        block = lax.ppermute(block, "fsdp", [(f, (f + far) % fan) for f in range(fan)])
        result = lax.dynamic_update_slice_in_dim(result, block, (me - far) % fan, 0)
    return result


def flat(blocks):
    return jnp.transpose(blocks, (1, 0, 2)).reshape(blocks.shape[1], -1)


def by_rows(value):
    return with_layout_constraint(value, Layout(major_to_minor=tuple(range(value.ndim))))


def scatter(grad):
    return lax.psum_scatter(grad, "fsdp", scatter_dimension=0, tiled=True)


def over_seq(arrays, splits, ident):
    n = lax.axis_size("seq")
    if all(
        v.shape[0] % (8 * n) == 0
        and ring_cut(v.shape, s, n)[0] % 8 == 0
        and v.shape[1] % (128 * max(s, 1)) == 0
        for v, s in zip(arrays, splits)
    ):
        return ring_total(arrays, splits, ident)
    return [lax.psum(v, "seq") for v in arrays]


def shards(
    layer_in, encoder, decoder_ids, encoder_ids, rel_buckets,
    norm_self, self_qkv, self_out, rel_table, norm_cross, cross_q, cross_kv, cross_out, norm_ff, ff_in, ff_out,
    cotangent,
):
    seqs, local, width = layer_in.shape
    enc_local = encoder.shape[1]
    parts = lax.axis_size("seq")
    heads = self_qkv.shape[1]
    dh = self_qkv.shape[2] // 3
    own = heads // parts
    rows = seqs * local
    buckets, table_own = rel_table.shape
    length, keys = local * parts, enc_local * parts
    gather = lambda v: lax.all_gather(v, "fsdp", axis=0, tiled=True)

    fan = lax.axis_size("fsdp")
    units = ff_in.shape[1] // (2 * fan)
    part = norm_self.shape[0]
    pair, half, rank = team(parts)

    qkv_w = gather(self_qkv)
    small = jnp.concatenate([norm_self, norm_cross, norm_ff, rel_table.reshape(-1)])
    small = lax.all_gather(small, "fsdp", axis=0, tiled=False)
    early = by_rows(jnp.stack([self_out, cross_q, *jnp.split(cross_kv.reshape(-1, 2 * width), 2, axis=1)]))
    small, early = lax.optimization_barrier((small, early))
    early = lax.all_gather(early, "fsdp", axis=1, tiled=True)
    both_ids = jnp.concatenate([decoder_ids.reshape(-1), encoder_ids.reshape(-1)])
    both_ids = change_home(jnp.pad(both_ids, (0, 1024 - local - enc_local)).reshape(8, 128))
    inner_t = ff_in.T
    by_kernel = (width // fan) % 128 == 0
    (both_ids,) = swap([jnp.broadcast_to(both_ids[None], (parts, 8, 128))], 13)
    home = change_home(layer_in.reshape(rows, width))
    early = by_rows(early)
    mix_self = early[0].reshape(parts, own * dh, width)
    query_w = early[1].reshape(width, parts, own * dh)
    pairs_w = early[2:]

    gain_first, gain_second, gain_third = (
        small[:, i * part : (i + 1) * part].reshape(width).astype(f32) for i in range(3)
    )
    table = jnp.transpose(small[:, 3 * part :].reshape(-1, buckets, table_own), (1, 0, 2)).reshape(buckets, heads)
    both_ids = both_ids.reshape(parts, 1024)
    ids = both_ids[:, :local].reshape(length)
    enc_ids = both_ids[:, local : local + enc_local].reshape(keys)

    first_seen = counts_below(ids, ids)
    enc_first = counts_below(enc_ids, ids)
    enc_last = counts_below(enc_ids, ids + 1)
    blocks = length // BQ
    bk = BQ
    self_rows = jnp.broadcast_to(first_seen[None], (8, length))
    cross_rows = jnp.concatenate([enc_first[None], enc_last[None], jnp.zeros((6, length), jnp.int32)])
    self_limits = jnp.stack(
        [first_seen[::BQ] // bk, (jnp.arange(blocks, dtype=jnp.int32) + 1) * (BQ // bk)]
    )
    cross_limits = jnp.stack([enc_first[::BQ] // bk, (enc_last[BQ - 1 :: BQ] + bk - 1) // bk])

    first_head = rank * own
    table_mine = lax.dynamic_slice_in_dim(table.astype(f32), first_head, own, 1)
    near = rel_buckets[:REACH]
    onehot = (near[:, None] == jnp.arange(buckets, dtype=jnp.int32)[None, :]).astype(f32)
    bias = jnp.einsum("ln,ng->gl", onehot, table_mine, precision=HIGH)
    ext = jnp.concatenate(
        [jnp.full((own, BQ), MASKED, f32), bias, jnp.zeros((own, BQ), f32)], axis=1
    )

    qkv_w, home, inner_t, ext, self_rows, cross_rows, self_limits, cross_limits = lax.optimization_barrier(
        (qkv_w, home, inner_t, ext, self_rows, cross_rows, self_limits, cross_limits)
    )
    qkv_w = qkv_w.reshape(width, parts, own * 3 * dh)

    stream = home.astype(f32)
    normed_first = norm_apply(stream, gain_first).astype(bf16)
    qkv_tok = jnp.einsum("td,dge->gte", normed_first, qkv_w, preferred_element_type=f32).astype(bf16)
    others = change_home(jnp.concatenate([cotangent.reshape(rows, width), encoder.reshape(-1, width)]))
    grad_low, enc_flat = others[:rows], others[rows:]
    fars = [tuple(far for far in range(fan) if by_kernel and min(far, 3) in some) for some in ((2,), (0, 1), (3,))]
    qkv, *halves = swap([qkv_tok], 17, fars[0], inner_t)
    qkv, cross_out, grad_low = lax.optimization_barrier((qkv, cross_out, grad_low))
    if rows == cross_out.shape[0]:
        mix_cross, grad_group = lax.all_gather(jnp.stack([cross_out, grad_low]), "fsdp", axis=1, tiled=True)
    else:
        mix_cross, grad_group = gather(cross_out), gather(grad_low)
    mix_cross = mix_cross.reshape(parts, own * dh, width)
    qkv = qkv.reshape(length, own * 3 * dh)
    out_self, self_t, self_lse = self_forward(self_limits, self_rows, ext, qkv)
    (self_tok,) = swap([out_self.reshape(parts, local, own * dh)], 11)
    after_self = stream + jnp.einsum("gtc,gcd->td", self_tok, mix_self, preferred_element_type=f32)
    normed_second = norm_apply(after_self, gain_second).astype(bf16)
    query_tok = jnp.einsum("td,dgc->gtc", normed_second, query_w, preferred_element_type=f32).astype(bf16)
    pairs_tok = jnp.einsum(
        "td,sdge->sgte", enc_flat, pairs_w.reshape(2, width, parts // 2, -1), preferred_element_type=f32
    )
    pairs_tok = pairs_tok.astype(bf16).reshape(parts, enc_local, -1)
    query_cross, pairs, *halves = swap([query_tok, pairs_tok], 15, fars[1], inner_t, halves)
    query_cross, pairs = query_cross.reshape(length, own * dh), pairs.reshape(keys, own * 2 * dh)
    out_cross, cross_t, cross_lse = cross_forward(cross_limits, cross_rows, query_cross, pairs)
    cross_tok, *halves = swap([out_cross.reshape(parts, local, own * dh)], 16, fars[2], inner_t, halves)
    if not by_kernel:
        halves = spread(jnp.transpose(inner_t.reshape(2, fan, units, -1), (1, 0, 2, 3)))
        halves = [jnp.transpose(halves[:, i], (1, 0, 2)).reshape(units, width) for i in range(2)]
    gate_t, up_t = halves
    after_cross = after_self + jnp.einsum("gtc,gcd->td", cross_tok, mix_cross, preferred_element_type=f32)
    normed_third = norm_apply(after_cross, gain_third).astype(bf16)
    normed_group = gather(normed_third)
    gate = jnp.einsum("td,fd->tf", normed_group, gate_t, preferred_element_type=f32)
    up = jnp.einsum("td,fd->tf", normed_group, up_t, preferred_element_type=f32)
    hidden = gate_mix(gate, up).astype(bf16)

    grad_hidden = jnp.einsum("td,fd->tf", grad_group, ff_out, preferred_element_type=f32)
    _, pull_mix = jax.vjp(gate_mix, gate, up)
    grad_gate, grad_up = (g.astype(bf16) for g in pull_mix(grad_hidden))
    grad_third_in = jnp.dot(grad_gate, gate_t, preferred_element_type=f32) + jnp.dot(
        grad_up, up_t, preferred_element_type=f32
    )
    grad_third_in = scatter(grad_third_in.astype(bf16))
    outer_part = jnp.dot(hidden, ff_out, preferred_element_type=f32).astype(bf16)
    grad_units = [
        jnp.einsum("tf,td->fd", g, y, preferred_element_type=f32).astype(bf16)
        for g, y in ((grad_gate, normed_group), (grad_up, normed_group), (hidden, grad_group))
    ]
    grad_third_in, outer_part, grad_units = lax.optimization_barrier((grad_third_in, outer_part, grad_units))
    if by_kernel:
        grad_units = jnp.stack([g.reshape(parts, units // parts, width) for g in grad_units], axis=1)
        part_units = grad_units.reshape(3 * units, width)
    grad_third_in = grad_third_in.astype(f32)
    grad_from_third, grad_gain_third = norm_back(after_cross, gain_third, grad_third_in)
    grad_middle = grad_low.astype(f32) + grad_from_third
    middle_low = grad_middle.astype(bf16)
    grad_mix_cross = jnp.einsum("gtc,td->gcd", cross_tok, middle_low, preferred_element_type=f32)
    grad_cross_tok = jnp.einsum("td,gcd->gtc", middle_low, mix_cross, preferred_element_type=f32).astype(bf16)
    (grad_cross,) = swap([grad_cross_tok], 11)
    grad_cross = grad_cross.reshape(length, own * dh)
    grad_query, grad_pairs = cross_backward(
        cross_limits, cross_rows, query_cross, pairs, grad_cross, cross_t, cross_lse
    )
    grad_query_tok, grad_pairs_tok = swap(
        [grad_query.reshape(parts, local, own * dh), grad_pairs.reshape(parts, enc_local, own * 2 * dh)], 12
    )
    grad_query_tok, grad_pairs_tok = flat(grad_query_tok), flat(grad_pairs_tok)
    grad_query_w = jnp.einsum("td,te->de", normed_second, grad_query_tok, preferred_element_type=f32)
    grad_second_in = jnp.einsum("te,de->td", grad_query_tok, query_w.reshape(width, -1), preferred_element_type=f32)
    grad_pairs_w = jnp.einsum("td,te->de", enc_flat, grad_pairs_tok, preferred_element_type=f32)
    grad_encoder = sum(
        jnp.einsum("te,de->td", grad_pairs_tok[:, i * width : (i + 1) * width], pairs_w[i], preferred_element_type=f32)
        for i in range(2)
    )
    grad_from_second, grad_gain_second = norm_back(after_self, gain_second, grad_second_in)
    grad_upper = grad_middle + grad_from_second
    upper_low = grad_upper.astype(bf16)
    grad_mix_self = jnp.einsum("gtc,td->gcd", self_tok, upper_low, preferred_element_type=f32)
    grad_self_tok = jnp.einsum("td,gcd->gtc", upper_low, mix_self, preferred_element_type=f32).astype(bf16)
    grad_mid = jnp.concatenate(
        [
            grad_query_w.astype(bf16),
            grad_pairs_w.astype(bf16),
            grad_mix_cross.reshape(width, width).astype(bf16),
            grad_mix_self.reshape(width, width).astype(bf16),
        ],
        axis=1,
    )
    grad_self_tok, grad_mid = lax.optimization_barrier((grad_self_tok, grad_mid))
    part_mid = scatter(grad_mid)
    (grad_self,) = swap([grad_self_tok], 11)
    grad_self = grad_self.reshape(length, own * dh)
    grad_qkv, diagonals = self_backward(self_limits, self_rows, ext, qkv, grad_self, self_t, self_lse)
    (grad_qkv_tok,) = swap([grad_qkv.reshape(parts, local, own * 3 * dh)], 10)
    grad_qkv_tok = flat(grad_qkv_tok)
    grad_qkv_w = jnp.einsum("td,te->de", normed_first, grad_qkv_tok, preferred_element_type=f32)
    grad_first_in = jnp.einsum("te,de->td", grad_qkv_tok, qkv_w.reshape(width, -1), preferred_element_type=f32)
    grad_from_first, grad_gain_first = norm_back(stream, gain_first, grad_first_in)
    grad_layer_in = (grad_upper + grad_from_first).astype(bf16)
    if not by_kernel:
        part_units = grad_units
    bucket_line = jnp.concatenate([jnp.full((BQ - 1,), -1, jnp.int32), near, jnp.full((BQ + 1,), -1, jnp.int32)])
    in_bucket = (bucket_line[:, None] == jnp.arange(buckets, dtype=jnp.int32)).astype(f32)
    by_bucket = jnp.einsum("xn,gx->ng", in_bucket, diagonals, precision=HIGH)
    grad_table = lax.dynamic_update_slice_in_dim(jnp.zeros((buckets, heads), f32), by_bucket, first_head, 1)

    gains = jnp.concatenate(
        [g.reshape(-1, part) for g in (grad_gain_first, grad_gain_second, grad_gain_third)], axis=1
    )
    tables = jnp.transpose(grad_table.reshape(buckets, -1, table_own), (1, 0, 2)).reshape(-1, buckets * table_own)
    small_grads = lax.psum(jnp.concatenate([gains, tables], axis=1).astype(bf16), "fsdp")
    small_grads = lax.dynamic_index_in_dim(small_grads, lax.axis_index("fsdp"), 0, False)
    small_size = small_grads.shape[0]
    small_grads = jnp.pad(small_grads, (0, parts * 1024 - small_size)).reshape(parts * 8, 128)
    going_home = jnp.concatenate([grad_layer_in, grad_encoder.astype(bf16)])
    going_home, small_grads, grad_qkv_w, part_units, part_mid = lax.optimization_barrier(
        (going_home, small_grads, grad_qkv_w.astype(bf16), part_units, part_mid)
    )
    part_last = scatter(grad_qkv_w)
    going_home = change_home(going_home)
    if by_kernel:
        total_inner, total_outer, outer_sum = units_total(part_units, outer_part, 0)
    else:
        grad_units = [lax.psum(g, "seq") for g in grad_units]
        total_inner = spread(jnp.transpose(jnp.stack(grad_units[:2]).reshape(2, units, fan, -1), (2, 0, 1, 3)))
        total_outer, outer_sum = grad_units[2], scatter(outer_part).astype(f32)
    total_mid, total_qkv, small_total = over_seq([part_mid, part_last, small_grads], (2, 2, 1), 1)
    layer_out = (after_cross + outer_sum).astype(bf16)
    layer_out, total_inner, total_outer, total_mid, total_qkv, going_home = lax.optimization_barrier(
        (layer_out, total_inner, total_outer, total_mid, total_qkv, going_home)
    )
    layer_out = change_home(layer_out).reshape(seqs, local, width)
    grad_layer_in = going_home[:rows].astype(f32).reshape(seqs, local, width)
    grad_encoder = going_home[rows:].astype(f32).reshape(seqs, enc_local, width)
    if by_kernel:
        total_inner = jnp.transpose(total_inner.reshape(parts, fan, 2, units // parts, -1), (4, 2, 1, 0, 3))
    else:
        total_inner = jnp.transpose(total_inner, (3, 1, 0, 2))
    total_inner = total_inner.reshape(-1, 2 * fan * units).astype(f32)
    total_outer, total_mid, total_qkv = (v.astype(f32) for v in (total_outer, total_mid, total_qkv))
    total_query, total_mix_cross = total_mid[:, :width], total_mid[:, 3 * width : 4 * width]
    total_pairs = total_mid[:, width : 3 * width].reshape(-1, heads, 2 * dh)
    total_mix_self, total_qkv = total_mid[:, 4 * width :], total_qkv.reshape(-1, heads, 3 * dh)
    mine = small_total.reshape(-1)[:small_size].astype(f32)
    total_gain_first, total_gain_second, total_gain_third = (mine[i * part : (i + 1) * part] for i in range(3))
    total_table = mine[3 * part :].reshape(buckets, table_own)
    return (
        layer_out, grad_layer_in, grad_encoder, total_gain_first, total_qkv, total_mix_self, total_table,
        total_gain_second, total_query, total_pairs, total_mix_cross, total_gain_third, total_inner, total_outer,
    )


def solution(mesh):
    in_specs = (
        P("fsdp", "seq", None), P("fsdp", "seq", None), P("fsdp", "seq"), P("fsdp", "seq"), P(),
        P("fsdp"), P("fsdp", None, None), P("fsdp", None), P(None, "fsdp"), P("fsdp"), P("fsdp", None),
        P("fsdp", None, None), P("fsdp", None), P("fsdp"), P("fsdp", None), P("fsdp", None),
        P("fsdp", "seq", None),
    )
    out_specs = (
        P("fsdp", "seq", None), P("fsdp", "seq", None), P("fsdp", "seq", None), P("fsdp"), P("fsdp", None, None),
        P("fsdp", None), P(None, "fsdp"), P("fsdp"), P("fsdp", None), P("fsdp", None, None), P("fsdp", None),
        P("fsdp"), P("fsdp", None), P("fsdp", None),
    )
    return jax.shard_map(shards, mesh=mesh, in_specs=in_specs, out_specs=out_specs, check_vma=False)
```

```python
import functools

import jax
import jax.numpy as jnp
from jax import lax
from jax.experimental import pallas as pl
from jax.experimental.layout import Layout, with_layout_constraint
from jax.experimental.pallas import tpu as pltpu
from jax.sharding import PartitionSpec as P

EPS = 1e-06
HIGH = lax.Precision.HIGHEST
MASKED = -1e30
DOCS = 4

BQ = 256
REACH = 1024


def blk(index, size):
    return pl.ds(pl.multiple_of(index * size, size), size)


def turn(value):
    return jnp.transpose(value.astype(jnp.float32), (1, 0))


def bias_tiles(ext_ref, tile_ref, own):
    for h in range(own):
        line = jnp.broadcast_to(ext_ref[h : h + 1, :], tile_ref.shape[1:])
        tile_ref[h] = pltpu.roll(line, 0, 1, stride=1, stride_axis=0)


def unpack(ref, own, width, picks, flips, base):
    block = 256

    def one(b, _):
        rows = blk(b, block)
        value = ref[rows, :]
        if flips:
            flat = turn(value).astype(jnp.bfloat16)
            for target, piece in flips:
                for h in range(own):
                    at = h * width + piece * 64
                    target[base + h, :, rows] = flat[at : at + 64]
        for target, piece in picks:
            for h in range(own):
                at = h * width + piece * 64
                target[base + h, rows, :] = value[:, at : at + 64]
        return 0

    lax.fori_loop(0, ref.shape[0] // block, one, 0)


def dot(a, b):
    return jnp.dot(a, b, preferred_element_type=jnp.float32)


def score(own_index, key_tile, query_t, tile_ref, t, low, high, first_key):
    value = dot(key_tile, query_t)
    place = lax.broadcasted_iota(jnp.int32, value.shape, 0)
    keep = place >= low - first_key
    if high is not None:
        keep = keep & (place < high - first_key)
    else:
        value = value + tile_ref[own_index, :, blk(t + 1, BQ)]
    return jnp.where(keep, value, MASKED)


def forward_body(own, bk, causal, lim_ref, rows_ref, q_t, k_rows, v_t, tile_ref, o_ref, ot_ref, lse_ref):
    length = o_ref.shape[0]

    def q_block(i, _):
        cols = blk(i, BQ)
        queries = [q_t[h, :, cols] for h in range(own)]
        low = rows_ref[0:1, cols]
        high = None if causal else rows_ref[1:2, cols]

        def k_block(j, carry):
            keys = blk(j, bk)
            t = i - j
            out = []
            for h in range(own):
                top, total, acc = carry[h]
                s = score(h, k_rows[h, keys, :], queries[h], tile_ref, t, low, high, j * bk)
                new_top = jnp.maximum(top, jnp.max(s, axis=0, keepdims=True))
                p = jnp.exp(s - new_top)
                scale = jnp.exp(top - new_top)
                total = total * scale + jnp.sum(p, axis=0, keepdims=True)
                acc = acc * scale + dot(v_t[h, :, keys], p.astype(jnp.bfloat16))
                out.append((new_top, total, acc))
            return tuple(out)

        start = tuple(
            (
                jnp.full((1, BQ), MASKED, jnp.float32),
                jnp.zeros((1, BQ), jnp.float32),
                jnp.zeros((64, BQ), jnp.float32),
            )
            for _ in range(own)
        )
        ends = lax.fori_loop(lim_ref[0, i], lim_ref[1, i], k_block, start)
        for h in range(own):
            top, total, acc = ends[h]
            ot_ref[h * 64 : h * 64 + 64, cols] = acc / total
            lse_ref[h : h + 1, cols] = top + jnp.log(total)
        o_ref[cols, :] = turn(ot_ref[:, cols]).astype(jnp.bfloat16)
        return 0

    lax.fori_loop(0, length // BQ, q_block, 0)


def self_forward_kernel(own, bk, lim_ref, rows_ref, ext_ref, x_ref, o_ref, ot_ref, lse_ref, q_t, k_rows, v_t, tile_ref):
    bias_tiles(ext_ref, tile_ref, own)
    unpack(x_ref, own, 192, [(k_rows, 1)], [(q_t, 0), (v_t, 2)], 0)
    forward_body(own, bk, True, lim_ref, rows_ref, q_t, k_rows, v_t, tile_ref, o_ref, ot_ref, lse_ref)


def cross_forward_kernel(own, bk, lim_ref, rows_ref, q_ref, kv_ref, o_ref, ot_ref, lse_ref, q_t, k_rows, v_t):
    unpack(q_ref, own, 64, [], [(q_t, 0)], 0)
    unpack(kv_ref, own, 128, [(k_rows, 0)], [(v_t, 1)], 0)
    forward_body(own, bk, False, lim_ref, rows_ref, q_t, k_rows, v_t, None, o_ref, ot_ref, lse_ref)


def backward_body(
    own, bk, causal, lim_ref, rows_ref, do_ref, ot_ref, lse_ref,
    q_t, q_rows, k_t, k_rows, v_rows, do_t, do_rows, tile_ref, sum_ref, dq_t, dk, dv,
):
    length = do_ref.shape[0]
    dk[...] = jnp.zeros_like(dk)
    dv[...] = jnp.zeros_like(dv)
    if causal:
        sum_ref[...] = jnp.zeros_like(sum_ref)

    def q_block(i, _):
        cols = blk(i, BQ)
        low = rows_ref[0:1, cols]
        high = None if causal else rows_ref[1:2, cols]
        per_head = []
        for h in range(own):
            grad_t = do_t[h, :, cols]
            delta = jnp.sum(
                grad_t.astype(jnp.float32) * ot_ref[h * 64 : h * 64 + 64, cols], axis=0, keepdims=True
            )
            per_head.append((q_t[h, :, cols], grad_t, delta, lse_ref[h : h + 1, cols]))

        def k_block(j, carry):
            keys = blk(j, bk)
            t = i - j
            out = []
            for h in range(own):
                query_t, grad_t, delta, lse = per_head[h]
                s = score(h, k_rows[h, keys, :], query_t, tile_ref, t, low, high, j * bk)
                p = jnp.exp(s - lse)
                dp = dot(v_rows[h, keys, :], grad_t)
                ds = (p * (dp - delta)).astype(jnp.bfloat16)
                dv[h, keys, :] += dot(p.astype(jnp.bfloat16), do_rows[h, cols, :])
                dk[h, keys, :] += dot(ds, q_rows[h, cols, :])
                if causal:
                    sum_ref[h, :, blk(t, BQ)] += ds.astype(jnp.float32)
                out.append(carry[h] + dot(k_t[h, :, keys], ds))
            return tuple(out)

        ends = lax.fori_loop(
            lim_ref[0, i],
            lim_ref[1, i],
            k_block,
            tuple(jnp.zeros((64, BQ), jnp.float32) for _ in range(own)),
        )
        for h in range(own):
            dq_t[h * 64 : h * 64 + 64, cols] = ends[h]
        return 0

    lax.fori_loop(0, length // BQ, q_block, 0)


def diagonal_sums(sum_ref, u_ref, own):
    flip = lax.broadcasted_iota(jnp.int32, (BQ, BQ), 0) + lax.broadcasted_iota(jnp.int32, (BQ, BQ), 1) == BQ - 1
    flip = jnp.where(flip, 1.0, 0.0).astype(jnp.bfloat16)
    for h in range(own):
        grid = sum_ref[h]
        high = grid.astype(jnp.bfloat16)
        low = (grid - high.astype(jnp.float32)).astype(jnp.bfloat16)
        upside = dot(flip, high) + dot(flip, low)
        wide = jnp.concatenate([upside, jnp.zeros((BQ, BQ), jnp.float32)], axis=1)
        aligned = pltpu.roll(wide, 0, 1, stride=1, stride_axis=0)
        u_ref[h : h + 1, :] = jnp.sum(aligned, axis=0, keepdims=True)


def self_backward_kernel(
    own, bk, lim_ref, rows_ref, ext_ref, x_ref, do_ref, ot_ref, lse_ref, dx_ref, u_ref,
    q_t, q_rows, k_t, k_rows, v_rows, do_t, do_rows, tile_ref, sum_ref, dq_t, dk, dv,
):
    bias_tiles(ext_ref, tile_ref, own)
    unpack(x_ref, own, 192, [(q_rows, 0), (k_rows, 1), (v_rows, 2)], [(q_t, 0), (k_t, 1)], 0)
    unpack(do_ref, own, 64, [(do_rows, 0)], [(do_t, 0)], 0)
    backward_body(
        own, bk, True, lim_ref, rows_ref, do_ref, ot_ref, lse_ref,
        q_t, q_rows, k_t, k_rows, v_rows, do_t, do_rows, tile_ref, sum_ref, dq_t, dk, dv,
    )
    diagonal_sums(sum_ref, u_ref, own)

    def pack(b, _):
        rows = blk(b, 256)
        dq = turn(dq_t[:, rows])
        pieces = []
        for h in range(own):
            pieces += [dq[:, h * 64 : h * 64 + 64], dk[h, rows, :], dv[h, rows, :]]
        dx_ref[rows, :] = jnp.concatenate(pieces, axis=1).astype(jnp.bfloat16)
        return 0

    lax.fori_loop(0, x_ref.shape[0] // 256, pack, 0)


def cross_backward_kernel(
    own, bk, lim_ref, rows_ref, q_ref, kv_ref, do_ref, ot_ref, lse_ref, dq_ref, dkv_ref,
    q_t, q_rows, k_t, k_rows, v_rows, do_t, do_rows, dq_t, dk, dv,
):
    unpack(q_ref, own, 64, [(q_rows, 0)], [(q_t, 0)], 0)
    unpack(kv_ref, own, 128, [(k_rows, 0), (v_rows, 1)], [(k_t, 0)], 0)
    unpack(do_ref, own, 64, [(do_rows, 0)], [(do_t, 0)], 0)
    backward_body(
        own, bk, False, lim_ref, rows_ref, do_ref, ot_ref, lse_ref,
        q_t, q_rows, k_t, k_rows, v_rows, do_t, do_rows, None, None, dq_t, dk, dv,
    )

    def pack_q(b, _):
        rows = blk(b, 256)
        dq_ref[rows, :] = turn(dq_t[:, rows]).astype(jnp.bfloat16)
        return 0

    def pack_kv(b, _):
        rows = blk(b, 256)
        pieces = []
        for h in range(own):
            pieces += [dk[h, rows, :], dv[h, rows, :]]
        dkv_ref[rows, :] = jnp.concatenate(pieces, axis=1).astype(jnp.bfloat16)
        return 0

    lax.fori_loop(0, q_ref.shape[0] // 256, pack_q, 0)
    lax.fori_loop(0, kv_ref.shape[0] // 256, pack_kv, 0)


SMEM = pl.BlockSpec(memory_space=pltpu.SMEM)
VMEM = pl.BlockSpec(memory_space=pltpu.VMEM)
bf16, f32 = jnp.bfloat16, jnp.float32


def call(body, name, operands, outs, scratch, flops):
    size = sum(v.size * v.dtype.itemsize for v in operands)
    return pl.pallas_call(
        body,
        name=name,
        out_shape=[jax.ShapeDtypeStruct(s, d) for s, d in outs],
        in_specs=[SMEM] + [VMEM] * (len(operands) - 1),
        out_specs=[VMEM] * len(outs),
        scratch_shapes=[pltpu.VMEM(s, d) for s, d in scratch],
        compiler_params=pltpu.CompilerParams(vmem_limit_bytes=40 << 20),
        cost_estimate=pl.CostEstimate(flops=0, bytes_accessed=size, transcendentals=0),
    )(*operands)


def self_forward(limits, rows, ext, x, bk=BQ):
    length, own = x.shape[0], x.shape[1] // 192
    return call(
        functools.partial(self_forward_kernel, own, bk),
        "self_forward",
        [limits, rows, ext, x],
        [((length, own * 64), bf16), ((own * 64, length), f32), ((own, length), f32)],
        [
            ((own, 64, length), bf16),
            ((own, length, 64), bf16),
            ((own, 64, length), bf16),
            ((own, BQ, REACH + 2 * BQ), f32),
        ],
        length * length * own * 64,
    )


def cross_forward(limits, rows, q, kv, bk=BQ):
    length, own, keys = q.shape[0], q.shape[1] // 64, kv.shape[0]
    return call(
        functools.partial(cross_forward_kernel, own, bk),
        "cross_forward",
        [limits, rows, q, kv],
        [((length, own * 64), bf16), ((own * 64, length), f32), ((own, length), f32)],
        [((own, 64, length), bf16), ((own, keys, 64), bf16), ((own, 64, keys), bf16)],
        length * keys * own * 128,
    )


def self_backward(limits, rows, ext, x, grad, o_t, lse, bk=BQ):
    length, own = x.shape[0], x.shape[1] // 192
    return call(
        functools.partial(self_backward_kernel, own, bk),
        "self_backward",
        [limits, rows, ext, x, grad, o_t, lse],
        [((length, own * 192), bf16), ((own, REACH + 2 * BQ), f32)],
        [
            ((own, 64, length), bf16),
            ((own, length, 64), bf16),
            ((own, 64, length), bf16),
            ((own, length, 64), bf16),
            ((own, length, 64), bf16),
            ((own, 64, length), bf16),
            ((own, length, 64), bf16),
            ((own, BQ, REACH + 2 * BQ), f32),
            ((own, BQ, REACH + BQ), f32),
            ((own * 64, length), f32),
            ((own, length, 64), f32),
            ((own, length, 64), f32),
        ],
        length * length * own * 160,
    )


def cross_backward(limits, rows, q, kv, grad, o_t, lse, bk=BQ):
    length, own, keys = q.shape[0], q.shape[1] // 64, kv.shape[0]
    return call(
        functools.partial(cross_backward_kernel, own, bk),
        "cross_backward",
        [limits, rows, q, kv, grad, o_t, lse],
        [((length, own * 64), bf16), ((keys, own * 128), bf16)],
        [
            ((own, 64, length), bf16),
            ((own, length, 64), bf16),
            ((own, 64, keys), bf16),
            ((own, keys, 64), bf16),
            ((own, keys, 64), bf16),
            ((own, 64, length), bf16),
            ((own, length, 64), bf16),
            ((own * 64, length), f32),
            ((own, keys, 64), f32),
            ((own, keys, 64), f32),
        ],
        length * keys * own * 320,
    )


MESH = pl.DeviceIdType.MESH


def ring_place(index, n):
    z, x = index // 2, index % 2
    return z + x * (n - 1 - 2 * z)


def ring_index(place, n):
    x = place // (n // 2)
    z = place + x * (n - 1 - 2 * place)
    return 2 * z + x


def ring_greet(n, others):
    place = ring_place(lax.axis_index("seq"), n)
    right = ring_index((place + 1) % n, n)
    left = ring_index((place + n - 1) % n, n)
    barrier = pltpu.get_barrier_semaphore()
    for neighbour in (left, right):
        pl.semaphore_signal(barrier, inc=1, device_id={"seq": neighbour}, device_id_type=MESH)
    for other in others:
        pl.semaphore_signal(barrier, inc=1, device_id={"fsdp": other}, device_id_type=MESH)
    pl.semaphore_wait(barrier, 2 + len(others))
    return place, right, left


def ring_cut(shape, split, n):
    rows, cols = shape[0] // n, shape[1]
    return (rows, cols // split) if split > 0 else (rows // -split, cols)


def ring_window(ref, shape, split, n, piece, chunk):
    whole = shape[0] // n
    rows, cols = ring_cut(shape, split, n)
    if split > 0:
        return ref.at[pl.ds(chunk * whole, rows), pl.ds(piece * cols, cols)]
    return ref.at[pl.ds(chunk * whole + piece * rows, rows), :]


def ring_kernel(n, splits, fan, *refs):
    count = len(splits)
    more = 1 if fan else 0
    x_refs, y_refs = refs[:count], refs[count + more : 2 * count + more]
    slots = refs[2 * (count + more) : 3 * count + 2 * more]
    send_sem, recv_sem = refs[3 * count + 2 * more :]
    place, right, left = ring_greet(n, [])
    streams = [(k, piece, piece % 2) for k in range(count) for piece in range(abs(splits[k]))]

    def window(ref, k, piece, chunk):
        return ring_window(ref, x_refs[k].shape, splits[k], n, piece, chunk)

    def chunk_at(down, step):
        return (place + 1 + step) % n if down else (place + 2 * n - 1 - step) % n

    copies = {}

    def start(number, step, src, dst, down):
        copies[number, step] = pltpu.make_async_remote_copy(
            src_ref=src,
            dst_ref=dst,
            send_sem=send_sem.at[number, step],
            recv_sem=recv_sem.at[number, step],
            device_id={"seq": left if down else right},
            device_id_type=MESH,
        )
        copies[number, step].start()

    def turn_block(number):
        inner_ref, turned_ref = refs[count], refs[2 * count + 1]
        rows = inner_ref.shape[0] // (2 * fan * n)
        half, first = number // (fan // 2), number % (fan // 2) * 2
        tall = jnp.concatenate(
            [
                inner_ref[pl.ds(((chunk * fan + group) * 2 + half) * rows, rows), :].astype(jnp.float32)
                for group in (first, first + 1)
                for chunk in range(n)
            ]
        )
        wide = 2 * n * rows
        turned_ref[:, number * wide : (number + 1) * wide] = jnp.transpose(tall, (1, 0))

    for number, (k, piece, down) in enumerate(streams):
        start(number, 0, window(x_refs[k], k, piece, place), window(slots[k], k, piece, 0), down)
    for step in range(n - 1):
        if step < fan:
            turn_block(step)
        for number, (k, piece, down) in enumerate(streams):
            copies[number, step].wait_recv()
            chunk = chunk_at(down, step)
            mine = window(x_refs[k], k, piece, chunk)
            landed = window(slots[k], k, piece, step)
            total = landed[...].astype(jnp.float32) + mine[...].astype(jnp.float32)
            if step < n - 2:
                landed[...] = total.astype(jnp.bfloat16)
                start(number, step + 1, landed, window(slots[k], k, piece, step + 1), down)
            else:
                done = window(y_refs[k], k, piece, chunk)
                done[...] = total.astype(jnp.bfloat16)
                start(number, n - 1, done, done, down)
    for step in range(n - 1):
        for number, (k, piece, down) in enumerate(streams):
            copies[number, n - 1 + step].wait_recv()
            if step < n - 2:
                done = window(y_refs[k], k, piece, chunk_at(down, n - 1 + step))
                start(number, n + step, done, done, down)
    for one in copies.values():
        one.wait_send()


def ring_call(body, name, arrays, outs, scratch, ident):
    size = sum(v.size * 2 for v in arrays)
    return pl.pallas_call(
        body,
        name=name,
        out_shape=[jax.ShapeDtypeStruct(s, d) for s, d in outs],
        in_specs=[pl.BlockSpec(memory_space=pltpu.VMEM)] * len(arrays),
        out_specs=[pl.BlockSpec(memory_space=pltpu.VMEM)] * len(outs),
        scratch_shapes=scratch,
        compiler_params=pltpu.CompilerParams(
            collective_id=ident, has_side_effects=True, vmem_limit_bytes=48 << 20
        ),
        cost_estimate=pl.CostEstimate(flops=0, bytes_accessed=60 * size, transcendentals=0),
    )(*arrays)


def ring_total(arrays, splits, ident, inner=None):
    n, fan = lax.axis_size("seq"), lax.axis_size("fsdp")
    streams = sum(abs(s) for s in splits)
    more = [] if inner is None else [inner]
    return ring_call(
        functools.partial(ring_kernel, n, splits, 0 if inner is None else fan),
        "ring_total",
        arrays + more,
        [(v.shape, jnp.bfloat16) for v in arrays] + [(v.shape[::-1], jnp.float32) for v in more],
        [pltpu.VMEM((v.shape[0] // n * (n - 1), v.shape[1]), jnp.bfloat16) for v in arrays]
        + [pltpu.SemaphoreType.DMA((streams, 2 * n - 2))] * 2,
        ident,
    )


def units_kernel(
    n, fan, x_ref, part_ref, few_ref, inner_ref, outer_ref, sum_ref, few_sum_ref, slots, acc, landed, few_landed,
    down_send, down_recv, swap_send, swap_recv, own_sem, send_sem, recv_sem, part_send, part_recv,
):
    s, me = lax.axis_index("seq"), lax.axis_index("fsdp")
    rows, width = acc.shape[0] // 3, x_ref.shape[1]
    cols = width // fan
    block = 2 * fan * rows
    place, right, left = ring_greet(n, [(me + far) % fan for far in range(1, fan)])
    parts = []
    for far in range(1, fan):
        target = (me + far) % fan
        for which, (src, into) in enumerate(((part_ref, landed), (few_ref, few_landed))):
            rest = src.shape[0] // fan
            one = pltpu.make_async_remote_copy(
                src_ref=src.at[pl.ds(target * rest, rest), :],
                dst_ref=into.at[far],
                send_sem=part_send.at[which, far],
                recv_sem=part_recv.at[which, far],
                device_id={"fsdp": target},
                device_id_type=MESH,
            )
            one.start()
            parts.append(one)

    sums = {}

    def piece_of(ref, at, piece):
        return ref.at[pl.ds(at * 3 * rows, 3 * rows), pl.ds(piece * cols, cols)]

    def send_sum(piece, step, src):
        to = left if piece >= fan // 2 else right
        sums[piece, step] = pltpu.make_async_remote_copy(
            src_ref=src,
            dst_ref=piece_of(slots, step, piece),
            send_sem=down_send.at[piece, step],
            recv_sem=down_recv.at[piece, step],
            device_id={"seq": to},
            device_id_type=MESH,
        )
        sums[piece, step].start()

    def chunk(piece, step):
        return ring_index((place + 1 + step) % n if piece >= fan // 2 else (place + 2 * n - 1 - step) % n, n)

    for piece in range(fan):
        send_sum(piece, 0, piece_of(x_ref, chunk(piece, 0), piece))
    for step in range(n - 1):
        for piece in range(fan):
            sums[piece, step].wait_recv()
            arrived = piece_of(slots, step, piece)
            mine = piece_of(x_ref, chunk(piece, step + 1), piece)
            total = (arrived[...].astype(jnp.float32) + mine[...].astype(jnp.float32)).astype(jnp.bfloat16)
            if step < n - 2:
                arrived[...] = total
                send_sum(piece, step + 1, arrived)
            else:
                acc[:, piece * cols : (piece + 1) * cols] = total
    moves = []
    for far in range(fan):
        target = (me + far) % fan
        for half in range(2):
            src = acc.at[pl.ds(half * rows, rows), pl.ds(pl.multiple_of(target * cols, 128), cols)]
            dst = inner_ref.at[pl.ds(s * block + (me * 2 + half) * rows, rows), :]
            if far:
                one = pltpu.make_async_remote_copy(
                    src_ref=src,
                    dst_ref=dst,
                    send_sem=swap_send.at[far, half],
                    recv_sem=swap_recv.at[far, half],
                    device_id={"fsdp": target},
                    device_id_type=MESH,
                )
            else:
                one = pltpu.make_async_copy(src, dst, own_sem.at[half])
            one.start()
            moves.append(one)
    mine = pltpu.make_async_copy(
        acc.at[pl.ds(2 * rows, rows), :], outer_ref.at[pl.ds(s * rows, rows), :], own_sem.at[2]
    )
    mine.start()
    copies = {}
    outs = ((outer_ref, (n * rows, width), 2), (inner_ref, (n * block, cols), -2))

    def start(k, piece, step):
        ref, shape, split = outs[k]
        chunk = ring_index((place + step) % n if piece else (place + n - step) % n, n)
        view = ring_window(ref, shape, split, n, piece, chunk)
        copies[k, piece, step] = pltpu.make_async_remote_copy(
            src_ref=view,
            dst_ref=view,
            send_sem=send_sem.at[2 * k + piece, step],
            recv_sem=recv_sem.at[2 * k + piece, step],
            device_id={"seq": left if piece else right},
            device_id_type=MESH,
        )
        copies[k, piece, step].start()

    def forward(k, step):
        for piece in range(2):
            copies[k, piece, step].wait_recv()
            if step < n - 2:
                start(k, piece, step + 1)

    mine.wait()
    start(0, 0, 0)
    start(0, 1, 0)
    lead = (n - 1) // 2
    for step in range(lead):
        forward(0, step)
    for one in moves:
        one.wait()
    start(1, 0, 0)
    start(1, 1, 0)
    for step in range(n - 1):
        forward(1, step)
        if lead + step < n - 1:
            forward(0, lead + step)
    for one in parts:
        one.wait()
    for src, into, out in ((part_ref, landed, sum_ref), (few_ref, few_landed, few_sum_ref)):
        rest = src.shape[0] // fan
        total = src[pl.ds(pl.multiple_of(me * rest, rest), rest), :].astype(jnp.float32)
        for far in range(1, fan):
            total = total + into[far].astype(jnp.float32)
        out[...] = total
    for one in [*copies.values(), *sums.values()]:
        one.wait_send()


def units_total(grads, part, few, ident):
    n, fan = lax.axis_size("seq"), lax.axis_size("fsdp")
    rows, width = grads.shape[0] // (3 * n), grads.shape[1]
    tokens = part.shape[0] // fan
    sems = lambda *shape: pltpu.SemaphoreType.DMA(shape)
    return ring_call(
        functools.partial(units_kernel, n, fan),
        "units_total",
        [grads, part, few],
        [
            ((n * 2 * fan * rows, width // fan), jnp.bfloat16),
            ((n * rows, width), jnp.bfloat16),
            ((tokens, part.shape[1]), jnp.float32),
            ((few.shape[0] // fan, few.shape[1]), jnp.float32),
        ],
        [
            pltpu.VMEM(((n - 1) * 3 * rows, width), jnp.bfloat16),
            pltpu.VMEM((3 * rows, width), jnp.bfloat16),
            pltpu.VMEM((fan, tokens, part.shape[1]), jnp.bfloat16),
            pltpu.VMEM((fan, few.shape[0] // fan, few.shape[1]), jnp.bfloat16),
        ]
        + [sems(fan, n - 1), sems(fan, n - 1), sems(fan, 2), sems(fan, 2), sems(3)]
        + [sems(4, n - 1), sems(4, n - 1), sems(2, fan), sems(2, fan)],
        ident,
    )


def team(n):
    s, f = lax.axis_index("seq"), lax.axis_index("fsdp")
    half = s // (n // 2)
    away = (half + f) % 2
    return f // 2, half, (s + away * (n // 2)) % n


def swap_kernel(n, fan, count, fars, fresh, *refs):
    given = count + (len(fars) > 0) + (0 if fresh else 2)
    x_refs, y_refs = refs[:count], refs[given : given + count]
    sems = refs[given + count + (2 if fars else 0) :]
    send_sem, recv_sem, own_sem = sems[:3]
    pair, half, rank = team(n)
    me = lax.axis_index("fsdp")

    def device(other):
        away = (other // (n // 2) + half) % 2
        return {"seq": (other + away * (n // 2)) % n, "fsdp": 2 * pair + (half + away) % 2}

    barrier = pltpu.get_barrier_semaphore()
    for j in range(1, n):
        pl.semaphore_signal(barrier, inc=1, device_id=device((rank + j) % n), device_id_type=MESH)
    travel = [far for far in fars if far]
    for far in travel:
        pl.semaphore_signal(barrier, inc=1, device_id={"fsdp": (me + fan - far) % fan}, device_id_type=MESH)
    pl.semaphore_wait(barrier, n - 1 + len(travel))
    copies = []
    for k in range(count):
        for j in range(1, n):
            other = (rank + j) % n
            one = pltpu.make_async_remote_copy(
                src_ref=x_refs[k].at[other],
                dst_ref=y_refs[k].at[rank],
                send_sem=send_sem.at[k, j],
                recv_sem=recv_sem.at[k, j],
                device_id=device(other),
                device_id_type=MESH,
            )
            one.start()
            copies.append(one)
    for k in range(count):
        one = pltpu.make_async_copy(x_refs[k].at[rank], y_refs[k].at[rank], own_sem.at[k])
        one.start()
        copies.append(one)
    if fars:
        w_ref, halves = refs[count], refs[given + count : given + count + 2]
        far_send, far_recv, far_own, stage = sems[3:]
        rest = []
        units, cols = halves[0].shape[0], w_ref.shape[1]
        for i, far in enumerate(fars):
            target = (me + far) % fan
            for part in range(2):
                src = w_ref.at[pl.ds((part * fan + target) * units, units), :]
                dst = halves[part].at[:, pl.ds(pl.multiple_of(me * cols, 128), cols)]
                if far:
                    one = pltpu.make_async_remote_copy(
                        src_ref=src,
                        dst_ref=dst,
                        send_sem=far_send.at[i, part],
                        recv_sem=far_recv.at[i, part],
                        device_id={"fsdp": target},
                        device_id_type=MESH,
                    )
                else:
                    one = pltpu.make_async_copy(src, stage.at[part], far_own.at[0, part])
                    rest.append((one, pltpu.make_async_copy(stage.at[part], dst, far_own.at[1, part])))
                one.start()
                if far:
                    copies.append(one)
        for inward, outward in rest:
            inward.wait()
            outward.start()
            copies.append(outward)
    for one in copies:
        one.wait()


def swap(arrays, ident, fars=(), given=None, halves=None):
    n, fan = lax.axis_size("seq"), lax.axis_size("fsdp")
    count = len(arrays)
    size = sum(v.size * 2 for v in arrays)
    operands, outs, alias = list(arrays), [jax.ShapeDtypeStruct(v.shape, v.dtype) for v in arrays], {}
    scratch = [
        pltpu.SemaphoreType.DMA((count, n)),
        pltpu.SemaphoreType.DMA((count, n)),
        pltpu.SemaphoreType.DMA((count,)),
    ]
    if fars:
        operands.append(given)
        shape = (given.shape[0] // (2 * fan), given.shape[1] * fan)
        outs += [jax.ShapeDtypeStruct(shape, given.dtype)] * 2
        scratch += [pltpu.SemaphoreType.DMA((len(fars), 2))] * 2 + [
            pltpu.SemaphoreType.DMA((2, 2)),
            pltpu.VMEM((2, given.shape[0] // (2 * fan), given.shape[1]), given.dtype),
        ]
        if halves is not None:
            operands += list(halves)
            alias = {count + 1: count, count + 2: count + 1}
    return pl.pallas_call(
        functools.partial(swap_kernel, n, fan, count, fars, not fars or halves is None),
        name="swap",
        out_shape=outs,
        in_specs=[pl.BlockSpec(memory_space=pl.ANY)] * len(operands),
        out_specs=[pl.BlockSpec(memory_space=pl.ANY)] * len(outs),
        scratch_shapes=scratch,
        input_output_aliases=alias,
        compiler_params=pltpu.CompilerParams(collective_id=ident, has_side_effects=True),
        cost_estimate=pl.CostEstimate(flops=0, bytes_accessed=size, transcendentals=0),
    )(*operands)


def norm_apply(value, gain):
    return value * lax.rsqrt(jnp.mean(value * value, axis=-1, keepdims=True) + EPS) * gain


def norm_back(value, gain, grad):
    _, pull = jax.vjp(norm_apply, value, gain)
    return pull(grad)


def gate_mix(gate, up):
    return jax.nn.gelu(gate, approximate=True) * up


def counts_below(ids, values):
    total = jnp.zeros_like(values)
    for doc in range(DOCS):
        total = total + jnp.where(values > doc, jnp.sum((ids == doc).astype(jnp.int32)), 0)
    return total


def change_home(value):
    n, fan = lax.axis_size("seq"), lax.axis_size("fsdp")
    pairs = []
    for s in range(n):
        for f in range(fan):
            away = (s // (n // 2) + f) % 2
            target = ((s + n // 2) % n, f ^ 1) if away else (s, f)
            pairs.append((s * fan + f, target[0] * fan + target[1]))
    return lax.ppermute(value, ("seq", "fsdp"), pairs)


def spread(blocks):
    fan, me = lax.axis_size("fsdp"), lax.axis_index("fsdp")
    result = blocks
    for far in range(1, fan):
        block = lax.dynamic_index_in_dim(blocks, (me + far) % fan, 0, True)
        block = lax.ppermute(block, "fsdp", [(f, (f + far) % fan) for f in range(fan)])
        result = lax.dynamic_update_slice_in_dim(result, block, (me - far) % fan, 0)
    return result


def flat(blocks):
    return jnp.transpose(blocks, (1, 0, 2)).reshape(blocks.shape[1], -1)


def by_rows(value):
    return with_layout_constraint(value, Layout(major_to_minor=tuple(range(value.ndim))))


def scatter(grad):
    return lax.psum_scatter(grad, "fsdp", scatter_dimension=0, tiled=True)


def shards(
    layer_in, encoder, decoder_ids, encoder_ids, rel_buckets,
    norm_self, self_qkv, self_out, rel_table, norm_cross, cross_q, cross_kv, cross_out, norm_ff, ff_in, ff_out,
    cotangent,
):
    seqs, local, width = layer_in.shape
    enc_local = encoder.shape[1]
    parts = lax.axis_size("seq")
    heads = self_qkv.shape[1]
    dh = self_qkv.shape[2] // 3
    own = heads // parts
    rows = seqs * local
    buckets, table_own = rel_table.shape
    length, keys = local * parts, enc_local * parts
    gather = lambda v: lax.all_gather(v, "fsdp", axis=0, tiled=True)

    fan = lax.axis_size("fsdp")
    units = ff_in.shape[1] // (2 * fan)
    part = norm_self.shape[0]
    pair, half, rank = team(parts)

    qkv_w = gather(self_qkv)
    small = jnp.concatenate([norm_self, norm_cross, norm_ff, rel_table.reshape(-1)])
    small = lax.all_gather(small, "fsdp", axis=0, tiled=False)
    early = by_rows(jnp.stack([self_out, cross_q, *jnp.split(cross_kv.reshape(-1, 2 * width), 2, axis=1)]))
    small, early = lax.optimization_barrier((small, early))
    early = lax.all_gather(early, "fsdp", axis=1, tiled=True)
    both_ids = jnp.concatenate([decoder_ids.reshape(-1), encoder_ids.reshape(-1)])
    both_ids = change_home(jnp.pad(both_ids, (0, 1024 - local - enc_local)).reshape(8, 128))
    inner_t = ff_in.T
    by_kernel = (width // fan) % 128 == 0 and fan % 2 == 0 and (ff_in.shape[0] // parts) % 8 == 0
    (both_ids,) = swap([jnp.broadcast_to(both_ids[None], (parts, 8, 128))], 13)
    home = change_home(layer_in.reshape(rows, width))
    early = by_rows(early)
    mix_self = early[0].reshape(parts, own * dh, width)
    query_w = early[1].reshape(width, parts, own * dh)
    pairs_w = early[2:]

    gain_first, gain_second, gain_third = (
        small[:, i * part : (i + 1) * part].reshape(width).astype(f32) for i in range(3)
    )
    table = jnp.transpose(small[:, 3 * part :].reshape(-1, buckets, table_own), (1, 0, 2)).reshape(buckets, heads)
    both_ids = both_ids.reshape(parts, 1024)
    ids = both_ids[:, :local].reshape(length)
    enc_ids = both_ids[:, local : local + enc_local].reshape(keys)

    first_seen = counts_below(ids, ids)
    enc_first = counts_below(enc_ids, ids)
    enc_last = counts_below(enc_ids, ids + 1)
    blocks = length // BQ
    bk = BQ
    self_rows = jnp.broadcast_to(first_seen[None], (8, length))
    cross_rows = jnp.concatenate([enc_first[None], enc_last[None], jnp.zeros((6, length), jnp.int32)])
    self_limits = jnp.stack(
        [first_seen[::BQ] // bk, (jnp.arange(blocks, dtype=jnp.int32) + 1) * (BQ // bk)]
    )
    cross_limits = jnp.stack([enc_first[::BQ] // bk, (enc_last[BQ - 1 :: BQ] + bk - 1) // bk])

    first_head = rank * own
    table_mine = lax.dynamic_slice_in_dim(table.astype(f32), first_head, own, 1)
    near = rel_buckets[:REACH]
    onehot = (near[:, None] == jnp.arange(buckets, dtype=jnp.int32)[None, :]).astype(f32)
    bias = jnp.einsum("ln,ng->gl", onehot, table_mine, precision=HIGH)
    ext = jnp.concatenate(
        [jnp.full((own, BQ), MASKED, f32), bias, jnp.zeros((own, BQ), f32)], axis=1
    )

    qkv_w, home, inner_t, ext, self_rows, cross_rows, self_limits, cross_limits = lax.optimization_barrier(
        (qkv_w, home, inner_t, ext, self_rows, cross_rows, self_limits, cross_limits)
    )
    qkv_w = qkv_w.reshape(width, parts, own * 3 * dh)

    stream = home.astype(f32)
    normed_first = norm_apply(stream, gain_first).astype(bf16)
    qkv_tok = jnp.einsum("td,dge->gte", normed_first, qkv_w, preferred_element_type=f32).astype(bf16)
    others = change_home(jnp.concatenate([cotangent.reshape(rows, width), encoder.reshape(-1, width)]))
    grad_low, enc_flat = others[:rows], others[rows:]
    fars = [tuple(far for far in range(fan) if by_kernel and min(far, 3) in some) for some in ((2,), (0, 1), (3,))]
    qkv, *halves = swap([qkv_tok], 17, fars[0], inner_t)
    qkv, cross_out, grad_low = lax.optimization_barrier((qkv, cross_out, grad_low))
    if rows == cross_out.shape[0]:
        mix_cross, grad_group = lax.all_gather(jnp.stack([cross_out, grad_low]), "fsdp", axis=1, tiled=True)
    else:
        mix_cross, grad_group = gather(cross_out), gather(grad_low)
    mix_cross = mix_cross.reshape(parts, own * dh, width)
    qkv = qkv.reshape(length, own * 3 * dh)
    out_self, self_t, self_lse = self_forward(self_limits, self_rows, ext, qkv)
    (self_tok,) = swap([out_self.reshape(parts, local, own * dh)], 11)
    after_self = stream + jnp.einsum("gtc,gcd->td", self_tok, mix_self, preferred_element_type=f32)
    normed_second = norm_apply(after_self, gain_second).astype(bf16)
    query_tok = jnp.einsum("td,dgc->gtc", normed_second, query_w, preferred_element_type=f32).astype(bf16)
    pairs_tok = jnp.einsum(
        "td,sdge->sgte", enc_flat, pairs_w.reshape(2, width, parts // 2, -1), preferred_element_type=f32
    )
    pairs_tok = pairs_tok.astype(bf16).reshape(parts, enc_local, -1)
    query_cross, pairs, *halves = swap([query_tok, pairs_tok], 15, fars[1], inner_t, halves)
    query_cross, pairs = query_cross.reshape(length, own * dh), pairs.reshape(keys, own * 2 * dh)
    out_cross, cross_t, cross_lse = cross_forward(cross_limits, cross_rows, query_cross, pairs)
    cross_tok, *halves = swap([out_cross.reshape(parts, local, own * dh)], 16, fars[2], inner_t, halves)
    if not by_kernel:
        halves = spread(jnp.transpose(inner_t.reshape(2, fan, units, -1), (1, 0, 2, 3)))
        halves = [jnp.transpose(halves[:, i], (1, 0, 2)).reshape(units, width) for i in range(2)]
    gate_t, up_t = halves
    after_cross = after_self + jnp.einsum("gtc,gcd->td", cross_tok, mix_cross, preferred_element_type=f32)
    normed_third = norm_apply(after_cross, gain_third).astype(bf16)
    normed_group = gather(normed_third)
    gate = jnp.einsum("td,fd->tf", normed_group, gate_t, preferred_element_type=f32)
    up = jnp.einsum("td,fd->tf", normed_group, up_t, preferred_element_type=f32)
    hidden = gate_mix(gate, up).astype(bf16)

    grad_hidden = jnp.einsum("td,fd->tf", grad_group, ff_out, preferred_element_type=f32)
    _, pull_mix = jax.vjp(gate_mix, gate, up)
    grad_gate, grad_up = (g.astype(bf16) for g in pull_mix(grad_hidden))
    grad_third_in = jnp.dot(grad_gate, gate_t, preferred_element_type=f32) + jnp.dot(
        grad_up, up_t, preferred_element_type=f32
    )
    grad_third_in = scatter(grad_third_in.astype(bf16))
    outer_part = jnp.dot(hidden, ff_out, preferred_element_type=f32).astype(bf16)
    grad_units = [
        jnp.einsum("tf,td->fd", g, y, preferred_element_type=f32).astype(bf16)
        for g, y in ((grad_gate, normed_group), (grad_up, normed_group), (hidden, grad_group))
    ]
    grad_third_in, outer_part, grad_units = lax.optimization_barrier((grad_third_in, outer_part, grad_units))
    if by_kernel:
        grad_units = jnp.stack([g.reshape(parts, units // parts, width) for g in grad_units], axis=1)
        part_units = grad_units.reshape(3 * units, width)
    grad_third_in = grad_third_in.astype(f32)
    grad_from_third, grad_gain_third = norm_back(after_cross, gain_third, grad_third_in)
    grad_middle = grad_low.astype(f32) + grad_from_third
    middle_low = grad_middle.astype(bf16)
    grad_mix_cross = jnp.einsum("gtc,td->gcd", cross_tok, middle_low, preferred_element_type=f32)
    grad_cross_tok = jnp.einsum("td,gcd->gtc", middle_low, mix_cross, preferred_element_type=f32).astype(bf16)
    (grad_cross,) = swap([grad_cross_tok], 11)
    grad_cross = grad_cross.reshape(length, own * dh)
    grad_query, grad_pairs = cross_backward(
        cross_limits, cross_rows, query_cross, pairs, grad_cross, cross_t, cross_lse
    )
    grad_query_tok, grad_pairs_tok = swap(
        [grad_query.reshape(parts, local, own * dh), grad_pairs.reshape(parts, enc_local, own * 2 * dh)], 12
    )
    grad_query_tok, grad_pairs_tok = flat(grad_query_tok), flat(grad_pairs_tok)
    grad_query_w = jnp.einsum("td,te->de", normed_second, grad_query_tok, preferred_element_type=f32)
    grad_second_in = jnp.einsum("te,de->td", grad_query_tok, query_w.reshape(width, -1), preferred_element_type=f32)
    grad_pairs_w = jnp.einsum("td,te->de", enc_flat, grad_pairs_tok, preferred_element_type=f32)
    grad_encoder = sum(
        jnp.einsum("te,de->td", grad_pairs_tok[:, i * width : (i + 1) * width], pairs_w[i], preferred_element_type=f32)
        for i in range(2)
    )
    grad_from_second, grad_gain_second = norm_back(after_self, gain_second, grad_second_in)
    grad_upper = grad_middle + grad_from_second
    upper_low = grad_upper.astype(bf16)
    grad_mix_self = jnp.einsum("gtc,td->gcd", self_tok, upper_low, preferred_element_type=f32)
    grad_self_tok = jnp.einsum("td,gcd->gtc", upper_low, mix_self, preferred_element_type=f32).astype(bf16)
    grad_mid = jnp.concatenate(
        [
            grad_query_w.astype(bf16),
            grad_pairs_w.astype(bf16),
            grad_mix_cross.reshape(width, width).astype(bf16),
            grad_mix_self.reshape(width, width).astype(bf16),
        ],
        axis=1,
    )
    grad_self_tok, grad_mid = lax.optimization_barrier((grad_self_tok, grad_mid))
    part_mid = scatter(grad_mid)
    (grad_self,) = swap([grad_self_tok], 11)
    grad_self = grad_self.reshape(length, own * dh)
    grad_qkv, diagonals = self_backward(self_limits, self_rows, ext, qkv, grad_self, self_t, self_lse)
    (grad_qkv_tok,) = swap([grad_qkv.reshape(parts, local, own * 3 * dh)], 10)
    grad_qkv_tok = flat(grad_qkv_tok)
    grad_qkv_w = jnp.einsum("td,te->de", normed_first, grad_qkv_tok, preferred_element_type=f32)
    grad_first_in = jnp.einsum("te,de->td", grad_qkv_tok, qkv_w.reshape(width, -1), preferred_element_type=f32)
    grad_from_first, grad_gain_first = norm_back(stream, gain_first, grad_first_in)
    grad_layer_in = (grad_upper + grad_from_first).astype(bf16)
    if not by_kernel:
        part_units = grad_units
    bucket_line = jnp.concatenate([jnp.full((BQ - 1,), -1, jnp.int32), near, jnp.full((BQ + 1,), -1, jnp.int32)])
    in_bucket = (bucket_line[:, None] == jnp.arange(buckets, dtype=jnp.int32)).astype(f32)
    by_bucket = jnp.einsum("xn,gx->ng", in_bucket, diagonals, precision=HIGH)
    grad_table = lax.dynamic_update_slice_in_dim(jnp.zeros((buckets, heads), f32), by_bucket, first_head, 1)

    gains = jnp.concatenate(
        [g.reshape(-1, part) for g in (grad_gain_first, grad_gain_second, grad_gain_third)], axis=1
    )
    tables = jnp.transpose(grad_table.reshape(buckets, -1, table_own), (1, 0, 2)).reshape(-1, buckets * table_own)
    small_grads = jnp.concatenate([gains, tables], axis=1).astype(bf16)
    small_size = small_grads.shape[1]
    going_home = jnp.concatenate([grad_layer_in, grad_encoder.astype(bf16)])
    going_home, small_grads, grad_qkv_w, part_units, part_mid = lax.optimization_barrier(
        (going_home, small_grads, grad_qkv_w.astype(bf16), part_units, part_mid)
    )
    part_last = scatter(grad_qkv_w)
    going_home = change_home(going_home)
    if by_kernel:
        few = jnp.pad(small_grads[:, None], ((0, 0), (0, 7), (0, 1024 - small_size))).reshape(fan * 8, 1024)
        total_inner, total_outer, outer_sum, few = units_total(part_units, outer_part, few, 0)
        few = jnp.pad(few[0].astype(bf16).reshape(8, 128), ((0, parts * 8 - 8), (0, 0)))
        total_mid, total_qkv, small_total, total_inner = ring_total(
            [part_mid, part_last, few], (2, 2, 1), 1, total_inner
        )
    else:
        grad_units = [lax.psum(g, "seq") for g in part_units]
        total_inner = spread(jnp.transpose(jnp.stack(grad_units[:2]).reshape(2, units, fan, -1), (2, 0, 1, 3)))
        total_inner = jnp.transpose(total_inner, (3, 1, 0, 2)).reshape(-1, 2 * fan * units).astype(f32)
        total_outer, outer_sum = grad_units[2], scatter(outer_part).astype(f32)
        few = lax.dynamic_index_in_dim(lax.psum(small_grads, "fsdp"), lax.axis_index("fsdp"), 0, False)
        total_mid, total_qkv, small_total = (lax.psum(v, "seq") for v in (part_mid, part_last, few))
    layer_out = (after_cross + outer_sum).astype(bf16)
    layer_out, total_inner, total_outer, total_mid, total_qkv, going_home = lax.optimization_barrier(
        (layer_out, total_inner, total_outer, total_mid, total_qkv, going_home)
    )
    layer_out = change_home(layer_out).reshape(seqs, local, width)
    grad_layer_in = going_home[:rows].astype(f32).reshape(seqs, local, width)
    grad_encoder = going_home[rows:].astype(f32).reshape(seqs, enc_local, width)
    total_outer, total_mid, total_qkv = (v.astype(f32) for v in (total_outer, total_mid, total_qkv))
    total_query, total_mix_cross = total_mid[:, :width], total_mid[:, 3 * width : 4 * width]
    total_pairs = total_mid[:, width : 3 * width].reshape(-1, heads, 2 * dh)
    total_mix_self, total_qkv = total_mid[:, 4 * width :], total_qkv.reshape(-1, heads, 3 * dh)
    mine = small_total.reshape(-1)[:small_size].astype(f32)
    total_gain_first, total_gain_second, total_gain_third = (mine[i * part : (i + 1) * part] for i in range(3))
    total_table = mine[3 * part :].reshape(buckets, table_own)
    return (
        layer_out, grad_layer_in, grad_encoder, total_gain_first, total_qkv, total_mix_self, total_table,
        total_gain_second, total_query, total_pairs, total_mix_cross, total_gain_third, total_inner, total_outer,
    )


def solution(mesh):
    in_specs = (
        P("fsdp", "seq", None), P("fsdp", "seq", None), P("fsdp", "seq"), P("fsdp", "seq"), P(),
        P("fsdp"), P("fsdp", None, None), P("fsdp", None), P(None, "fsdp"), P("fsdp"), P("fsdp", None),
        P("fsdp", None, None), P("fsdp", None), P("fsdp"), P("fsdp", None), P("fsdp", None),
        P("fsdp", "seq", None),
    )
    out_specs = (
        P("fsdp", "seq", None), P("fsdp", "seq", None), P("fsdp", "seq", None), P("fsdp"), P("fsdp", None, None),
        P("fsdp", None), P(None, "fsdp"), P("fsdp"), P("fsdp", None), P("fsdp", None, None), P("fsdp", None),
        P("fsdp"), P("fsdp", None), P("fsdp", None),
    )
    return jax.shard_map(shards, mesh=mesh, in_specs=in_specs, out_specs=out_specs, check_vma=False)
```

```python
import functools

import jax
import jax.numpy as jnp
from jax import lax
from jax.experimental import pallas as pl
from jax.experimental.layout import Layout, with_layout_constraint
from jax.experimental.pallas import tpu as pltpu
from jax.sharding import PartitionSpec as P

EPS = 1e-06
HIGH = lax.Precision.HIGHEST
MASKED = -1e30
DOCS = 4

BQ = 256
REACH = 1024


def blk(index, size):
    return pl.ds(pl.multiple_of(index * size, size), size)


def turn(value):
    return jnp.transpose(value.astype(jnp.float32), (1, 0))


def bias_tiles(ext_ref, tile_ref, own):
    for h in range(own):
        line = jnp.broadcast_to(ext_ref[h : h + 1, :], tile_ref.shape[1:])
        tile_ref[h] = pltpu.roll(line, 0, 1, stride=1, stride_axis=0)


def unpack(ref, own, width, picks, flips, base):
    block = 256

    def one(b, _):
        rows = blk(b, block)
        value = ref[rows, :]
        if flips:
            flat = turn(value).astype(jnp.bfloat16)
            for target, piece in flips:
                for h in range(own):
                    at = h * width + piece * 64
                    target[base + h, :, rows] = flat[at : at + 64]
        for target, piece in picks:
            for h in range(own):
                at = h * width + piece * 64
                target[base + h, rows, :] = value[:, at : at + 64]
        return 0

    lax.fori_loop(0, ref.shape[0] // block, one, 0)


def dot(a, b):
    return jnp.dot(a, b, preferred_element_type=jnp.float32)


def score(own_index, key_tile, query_t, tile_ref, t, low, high, first_key):
    value = dot(key_tile, query_t)
    place = lax.broadcasted_iota(jnp.int32, value.shape, 0)
    keep = place >= low - first_key
    if high is not None:
        keep = keep & (place < high - first_key)
    else:
        value = value + tile_ref[own_index, :, blk(t + 1, BQ)]
    return jnp.where(keep, value, MASKED)


def forward_body(own, bk, causal, lim_ref, rows_ref, q_t, k_rows, v_t, tile_ref, o_ref, ot_ref, lse_ref):
    length = o_ref.shape[0]

    def q_block(i, _):
        cols = blk(i, BQ)
        queries = [q_t[h, :, cols] for h in range(own)]
        low = rows_ref[0:1, cols]
        high = None if causal else rows_ref[1:2, cols]

        def k_block(j, carry):
            keys = blk(j, bk)
            t = i - j
            out = []
            for h in range(own):
                top, total, acc = carry[h]
                s = score(h, k_rows[h, keys, :], queries[h], tile_ref, t, low, high, j * bk)
                new_top = jnp.maximum(top, jnp.max(s, axis=0, keepdims=True))
                p = jnp.exp(s - new_top)
                scale = jnp.exp(top - new_top)
                total = total * scale + jnp.sum(p, axis=0, keepdims=True)
                acc = acc * scale + dot(v_t[h, :, keys], p.astype(jnp.bfloat16))
                out.append((new_top, total, acc))
            return tuple(out)

        start = tuple(
            (
                jnp.full((1, BQ), MASKED, jnp.float32),
                jnp.zeros((1, BQ), jnp.float32),
                jnp.zeros((64, BQ), jnp.float32),
            )
            for _ in range(own)
        )
        ends = lax.fori_loop(lim_ref[0, i], lim_ref[1, i], k_block, start)
        for h in range(own):
            top, total, acc = ends[h]
            ot_ref[h * 64 : h * 64 + 64, cols] = acc / total
            lse_ref[h : h + 1, cols] = top + jnp.log(total)
        o_ref[cols, :] = turn(ot_ref[:, cols]).astype(jnp.bfloat16)
        return 0

    lax.fori_loop(0, length // BQ, q_block, 0)


def self_forward_kernel(own, bk, lim_ref, rows_ref, ext_ref, x_ref, o_ref, ot_ref, lse_ref, q_t, k_rows, v_t, tile_ref):
    bias_tiles(ext_ref, tile_ref, own)
    unpack(x_ref, own, 192, [(k_rows, 1)], [(q_t, 0), (v_t, 2)], 0)
    forward_body(own, bk, True, lim_ref, rows_ref, q_t, k_rows, v_t, tile_ref, o_ref, ot_ref, lse_ref)


def cross_forward_kernel(own, bk, lim_ref, rows_ref, q_ref, kv_ref, o_ref, ot_ref, lse_ref, q_t, k_rows, v_t):
    unpack(q_ref, own, 64, [], [(q_t, 0)], 0)
    unpack(kv_ref, own, 128, [(k_rows, 0)], [(v_t, 1)], 0)
    forward_body(own, bk, False, lim_ref, rows_ref, q_t, k_rows, v_t, None, o_ref, ot_ref, lse_ref)


def backward_body(
    own, bk, causal, lim_ref, rows_ref, do_ref, ot_ref, lse_ref,
    q_t, q_rows, k_t, k_rows, v_rows, do_t, do_rows, tile_ref, sum_ref, dq_t, dk, dv,
):
    length = do_ref.shape[0]
    dk[...] = jnp.zeros_like(dk)
    dv[...] = jnp.zeros_like(dv)
    if causal:
        sum_ref[...] = jnp.zeros_like(sum_ref)

    def q_block(i, _):
        cols = blk(i, BQ)
        low = rows_ref[0:1, cols]
        high = None if causal else rows_ref[1:2, cols]
        per_head = []
        for h in range(own):
            grad_t = do_t[h, :, cols]
            delta = jnp.sum(
                grad_t.astype(jnp.float32) * ot_ref[h * 64 : h * 64 + 64, cols], axis=0, keepdims=True
            )
            per_head.append((q_t[h, :, cols], grad_t, delta, lse_ref[h : h + 1, cols]))

        def k_block(j, carry):
            keys = blk(j, bk)
            t = i - j
            out = []
            for h in range(own):
                query_t, grad_t, delta, lse = per_head[h]
                s = score(h, k_rows[h, keys, :], query_t, tile_ref, t, low, high, j * bk)
                p = jnp.exp(s - lse)
                dp = dot(v_rows[h, keys, :], grad_t)
                ds = (p * (dp - delta)).astype(jnp.bfloat16)
                dv[h, keys, :] += dot(p.astype(jnp.bfloat16), do_rows[h, cols, :])
                dk[h, keys, :] += dot(ds, q_rows[h, cols, :])
                if causal:
                    sum_ref[h, :, blk(t, BQ)] += ds.astype(jnp.float32)
                out.append(carry[h] + dot(k_t[h, :, keys], ds))
            return tuple(out)

        ends = lax.fori_loop(
            lim_ref[0, i],
            lim_ref[1, i],
            k_block,
            tuple(jnp.zeros((64, BQ), jnp.float32) for _ in range(own)),
        )
        for h in range(own):
            dq_t[h * 64 : h * 64 + 64, cols] = ends[h]
        return 0

    lax.fori_loop(0, length // BQ, q_block, 0)


def diagonal_sums(sum_ref, u_ref, own):
    flip = lax.broadcasted_iota(jnp.int32, (BQ, BQ), 0) + lax.broadcasted_iota(jnp.int32, (BQ, BQ), 1) == BQ - 1
    flip = jnp.where(flip, 1.0, 0.0).astype(jnp.bfloat16)
    for h in range(own):
        grid = sum_ref[h]
        high = grid.astype(jnp.bfloat16)
        low = (grid - high.astype(jnp.float32)).astype(jnp.bfloat16)
        upside = dot(flip, high) + dot(flip, low)
        wide = jnp.concatenate([upside, jnp.zeros((BQ, BQ), jnp.float32)], axis=1)
        aligned = pltpu.roll(wide, 0, 1, stride=1, stride_axis=0)
        u_ref[h : h + 1, :] = jnp.sum(aligned, axis=0, keepdims=True)


def self_backward_kernel(
    own, bk, lim_ref, rows_ref, ext_ref, x_ref, do_ref, ot_ref, lse_ref, dx_ref, u_ref,
    q_t, q_rows, k_t, k_rows, v_rows, do_t, do_rows, tile_ref, sum_ref, dq_t, dk, dv,
):
    bias_tiles(ext_ref, tile_ref, own)
    unpack(x_ref, own, 192, [(q_rows, 0), (k_rows, 1), (v_rows, 2)], [(q_t, 0), (k_t, 1)], 0)
    unpack(do_ref, own, 64, [(do_rows, 0)], [(do_t, 0)], 0)
    backward_body(
        own, bk, True, lim_ref, rows_ref, do_ref, ot_ref, lse_ref,
        q_t, q_rows, k_t, k_rows, v_rows, do_t, do_rows, tile_ref, sum_ref, dq_t, dk, dv,
    )
    diagonal_sums(sum_ref, u_ref, own)

    def pack(b, _):
        rows = blk(b, 256)
        dq = turn(dq_t[:, rows])
        pieces = []
        for h in range(own):
            pieces += [dq[:, h * 64 : h * 64 + 64], dk[h, rows, :], dv[h, rows, :]]
        dx_ref[rows, :] = jnp.concatenate(pieces, axis=1).astype(jnp.bfloat16)
        return 0

    lax.fori_loop(0, x_ref.shape[0] // 256, pack, 0)


def cross_backward_kernel(
    own, bk, lim_ref, rows_ref, q_ref, kv_ref, do_ref, ot_ref, lse_ref, dq_ref, dkv_ref,
    q_t, q_rows, k_t, k_rows, v_rows, do_t, do_rows, dq_t, dk, dv,
):
    unpack(q_ref, own, 64, [(q_rows, 0)], [(q_t, 0)], 0)
    unpack(kv_ref, own, 128, [(k_rows, 0), (v_rows, 1)], [(k_t, 0)], 0)
    unpack(do_ref, own, 64, [(do_rows, 0)], [(do_t, 0)], 0)
    backward_body(
        own, bk, False, lim_ref, rows_ref, do_ref, ot_ref, lse_ref,
        q_t, q_rows, k_t, k_rows, v_rows, do_t, do_rows, None, None, dq_t, dk, dv,
    )

    def pack_q(b, _):
        rows = blk(b, 256)
        dq_ref[rows, :] = turn(dq_t[:, rows]).astype(jnp.bfloat16)
        return 0

    def pack_kv(b, _):
        rows = blk(b, 256)
        pieces = []
        for h in range(own):
            pieces += [dk[h, rows, :], dv[h, rows, :]]
        dkv_ref[rows, :] = jnp.concatenate(pieces, axis=1).astype(jnp.bfloat16)
        return 0

    lax.fori_loop(0, q_ref.shape[0] // 256, pack_q, 0)
    lax.fori_loop(0, kv_ref.shape[0] // 256, pack_kv, 0)


SMEM = pl.BlockSpec(memory_space=pltpu.SMEM)
VMEM = pl.BlockSpec(memory_space=pltpu.VMEM)
bf16, f32 = jnp.bfloat16, jnp.float32


def call(body, name, operands, outs, scratch, flops):
    size = sum(v.size * v.dtype.itemsize for v in operands)
    return pl.pallas_call(
        body,
        name=name,
        out_shape=[jax.ShapeDtypeStruct(s, d) for s, d in outs],
        in_specs=[SMEM] + [VMEM] * (len(operands) - 1),
        out_specs=[VMEM] * len(outs),
        scratch_shapes=[pltpu.VMEM(s, d) for s, d in scratch],
        compiler_params=pltpu.CompilerParams(vmem_limit_bytes=40 << 20),
        cost_estimate=pl.CostEstimate(flops=0, bytes_accessed=size, transcendentals=0),
    )(*operands)


def self_forward(limits, rows, ext, x, bk=BQ):
    length, own = x.shape[0], x.shape[1] // 192
    return call(
        functools.partial(self_forward_kernel, own, bk),
        "self_forward",
        [limits, rows, ext, x],
        [((length, own * 64), bf16), ((own * 64, length), f32), ((own, length), f32)],
        [
            ((own, 64, length), bf16),
            ((own, length, 64), bf16),
            ((own, 64, length), bf16),
            ((own, BQ, REACH + 2 * BQ), f32),
        ],
        length * length * own * 64,
    )


def cross_forward(limits, rows, q, kv, bk=BQ):
    length, own, keys = q.shape[0], q.shape[1] // 64, kv.shape[0]
    return call(
        functools.partial(cross_forward_kernel, own, bk),
        "cross_forward",
        [limits, rows, q, kv],
        [((length, own * 64), bf16), ((own * 64, length), f32), ((own, length), f32)],
        [((own, 64, length), bf16), ((own, keys, 64), bf16), ((own, 64, keys), bf16)],
        length * keys * own * 128,
    )


def self_backward(limits, rows, ext, x, grad, o_t, lse, bk=BQ):
    length, own = x.shape[0], x.shape[1] // 192
    return call(
        functools.partial(self_backward_kernel, own, bk),
        "self_backward",
        [limits, rows, ext, x, grad, o_t, lse],
        [((length, own * 192), bf16), ((own, REACH + 2 * BQ), f32)],
        [
            ((own, 64, length), bf16),
            ((own, length, 64), bf16),
            ((own, 64, length), bf16),
            ((own, length, 64), bf16),
            ((own, length, 64), bf16),
            ((own, 64, length), bf16),
            ((own, length, 64), bf16),
            ((own, BQ, REACH + 2 * BQ), f32),
            ((own, BQ, REACH + BQ), f32),
            ((own * 64, length), f32),
            ((own, length, 64), f32),
            ((own, length, 64), f32),
        ],
        length * length * own * 160,
    )


def cross_backward(limits, rows, q, kv, grad, o_t, lse, bk=BQ):
    length, own, keys = q.shape[0], q.shape[1] // 64, kv.shape[0]
    return call(
        functools.partial(cross_backward_kernel, own, bk),
        "cross_backward",
        [limits, rows, q, kv, grad, o_t, lse],
        [((length, own * 64), bf16), ((keys, own * 128), bf16)],
        [
            ((own, 64, length), bf16),
            ((own, length, 64), bf16),
            ((own, 64, keys), bf16),
            ((own, keys, 64), bf16),
            ((own, keys, 64), bf16),
            ((own, 64, length), bf16),
            ((own, length, 64), bf16),
            ((own * 64, length), f32),
            ((own, keys, 64), f32),
            ((own, keys, 64), f32),
        ],
        length * keys * own * 320,
    )


MESH = pl.DeviceIdType.MESH


def ring_place(index, n):
    z, x = index // 2, index % 2
    return z + x * (n - 1 - 2 * z)


def ring_index(place, n):
    x = place // (n // 2)
    z = place + x * (n - 1 - 2 * place)
    return 2 * z + x


def ring_greet(n, others):
    place = ring_place(lax.axis_index("seq"), n)
    right = ring_index((place + 1) % n, n)
    left = ring_index((place + n - 1) % n, n)
    barrier = pltpu.get_barrier_semaphore()
    for neighbour in (left, right):
        pl.semaphore_signal(barrier, inc=1, device_id={"seq": neighbour}, device_id_type=MESH)
    for other in others:
        pl.semaphore_signal(barrier, inc=1, device_id={"fsdp": other}, device_id_type=MESH)
    pl.semaphore_wait(barrier, 2 + len(others))
    return place, right, left


def ring_cut(shape, split, n):
    rows, cols = shape[0] // n, shape[1]
    return (rows, cols // split) if split > 0 else (rows // -split, cols)


def ring_window(ref, shape, split, n, piece, chunk):
    whole = shape[0] // n
    rows, cols = ring_cut(shape, split, n)
    if split > 0:
        return ref.at[pl.ds(chunk * whole, rows), pl.ds(piece * cols, cols)]
    return ref.at[pl.ds(chunk * whole + piece * rows, rows), :]


def ring_kernel(n, splits, fan, *refs):
    count = len(splits)
    more = 1 if fan else 0
    x_refs, y_refs = refs[:count], refs[count + more : 2 * count + more]
    slots = refs[2 * (count + more) : 3 * count + 2 * more]
    send_sem, recv_sem = refs[3 * count + 2 * more :]
    place, right, left = ring_greet(n, [])
    streams = [(k, piece, piece % 2) for k in range(count) for piece in range(abs(splits[k]))]

    def window(ref, k, piece, chunk):
        return ring_window(ref, x_refs[k].shape, splits[k], n, piece, chunk)

    def chunk_at(down, step):
        return (place + 1 + step) % n if down else (place + 2 * n - 1 - step) % n

    copies = {}

    def start(number, step, src, dst, down):
        copies[number, step] = pltpu.make_async_remote_copy(
            src_ref=src,
            dst_ref=dst,
            send_sem=send_sem.at[number, step],
            recv_sem=recv_sem.at[number, step],
            device_id={"seq": left if down else right},
            device_id_type=MESH,
        )
        copies[number, step].start()

    def turn_block(number):
        inner_ref, turned_ref = refs[count], refs[2 * count + 1]
        rows = inner_ref.shape[0] // (2 * fan * n)
        half, first = number // (fan // 2), number % (fan // 2) * 2
        tall = jnp.concatenate(
            [
                inner_ref[pl.ds(((chunk * fan + group) * 2 + half) * rows, rows), :].astype(jnp.float32)
                for group in (first, first + 1)
                for chunk in range(n)
            ]
        )
        wide = 2 * n * rows
        turned_ref[:, number * wide : (number + 1) * wide] = jnp.transpose(tall, (1, 0))

    for number, (k, piece, down) in enumerate(streams):
        start(number, 0, window(x_refs[k], k, piece, place), window(slots[k], k, piece, 0), down)
    for step in range(n - 1):
        if step < fan:
            turn_block(step)
        for number, (k, piece, down) in enumerate(streams):
            copies[number, step].wait_recv()
            chunk = chunk_at(down, step)
            mine = window(x_refs[k], k, piece, chunk)
            landed = window(slots[k], k, piece, step)
            total = landed[...].astype(jnp.float32) + mine[...].astype(jnp.float32)
            if step < n - 2:
                landed[...] = total.astype(jnp.bfloat16)
                start(number, step + 1, landed, window(slots[k], k, piece, step + 1), down)
            else:
                done = window(y_refs[k], k, piece, chunk)
                done[...] = total.astype(jnp.bfloat16)
                start(number, n - 1, done, done, down)
    for step in range(n - 1):
        for number, (k, piece, down) in enumerate(streams):
            copies[number, n - 1 + step].wait_recv()
            if step < n - 2:
                done = window(y_refs[k], k, piece, chunk_at(down, n - 1 + step))
                start(number, n + step, done, done, down)
    for one in copies.values():
        one.wait_send()


def ring_call(body, name, arrays, outs, scratch, ident):
    size = sum(v.size * 2 for v in arrays)
    return pl.pallas_call(
        body,
        name=name,
        out_shape=[jax.ShapeDtypeStruct(s, d) for s, d in outs],
        in_specs=[pl.BlockSpec(memory_space=pltpu.VMEM)] * len(arrays),
        out_specs=[pl.BlockSpec(memory_space=pltpu.VMEM)] * len(outs),
        scratch_shapes=scratch,
        compiler_params=pltpu.CompilerParams(
            collective_id=ident, has_side_effects=True, vmem_limit_bytes=48 << 20
        ),
        cost_estimate=pl.CostEstimate(flops=0, bytes_accessed=60 * size, transcendentals=0),
    )(*arrays)


def ring_total(arrays, splits, ident, inner=None):
    n, fan = lax.axis_size("seq"), lax.axis_size("fsdp")
    streams = sum(abs(s) for s in splits)
    more = [] if inner is None else [inner]
    return ring_call(
        functools.partial(ring_kernel, n, splits, 0 if inner is None else fan),
        "ring_total",
        arrays + more,
        [(v.shape, jnp.bfloat16) for v in arrays] + [(v.shape[::-1], jnp.float32) for v in more],
        [pltpu.VMEM((v.shape[0] // n * (n - 1), v.shape[1]), jnp.bfloat16) for v in arrays]
        + [pltpu.SemaphoreType.DMA((streams, 2 * n - 2))] * 2,
        ident,
    )


def units_kernel(
    n, fan, x_ref, part_ref, few_ref, inner_ref, outer_ref, sum_ref, few_sum_ref, slots, acc, landed, few_landed,
    down_send, down_recv, swap_send, swap_recv, own_sem, send_sem, recv_sem, part_send, part_recv,
):
    s, me = lax.axis_index("seq"), lax.axis_index("fsdp")
    rows, width = acc.shape[0] // 3, x_ref.shape[1]
    cols = width // fan
    block = 2 * fan * rows
    place, right, left = ring_greet(n, [(me + far) % fan for far in range(1, fan)])
    parts = []
    for far in range(1, fan):
        target = (me + far) % fan
        for which, (src, into) in enumerate(((part_ref, landed), (few_ref, few_landed))):
            rest = src.shape[0] // fan
            one = pltpu.make_async_remote_copy(
                src_ref=src.at[pl.ds(target * rest, rest), :],
                dst_ref=into.at[far],
                send_sem=part_send.at[which, far],
                recv_sem=part_recv.at[which, far],
                device_id={"fsdp": target},
                device_id_type=MESH,
            )
            one.start()
            parts.append(one)

    sums = {}

    def piece_of(ref, at, piece):
        return ref.at[pl.ds(at * 3 * rows, 3 * rows), pl.ds(piece * cols, cols)]

    def send_sum(piece, step, src):
        to = left if piece >= fan // 2 else right
        sums[piece, step] = pltpu.make_async_remote_copy(
            src_ref=src,
            dst_ref=piece_of(slots, step, piece),
            send_sem=down_send.at[piece, step],
            recv_sem=down_recv.at[piece, step],
            device_id={"seq": to},
            device_id_type=MESH,
        )
        sums[piece, step].start()

    def chunk(piece, step):
        return ring_index((place + 1 + step) % n if piece >= fan // 2 else (place + 2 * n - 1 - step) % n, n)

    for piece in range(fan):
        send_sum(piece, 0, piece_of(x_ref, chunk(piece, 0), piece))
    for step in range(n - 1):
        for piece in range(fan):
            sums[piece, step].wait_recv()
            arrived = piece_of(slots, step, piece)
            mine = piece_of(x_ref, chunk(piece, step + 1), piece)
            total = (arrived[...].astype(jnp.float32) + mine[...].astype(jnp.float32)).astype(jnp.bfloat16)
            if step < n - 2:
                arrived[...] = total
                send_sum(piece, step + 1, arrived)
            else:
                acc[:, piece * cols : (piece + 1) * cols] = total
    moves = []
    for far in range(fan):
        target = (me + far) % fan
        for half in range(2):
            src = acc.at[pl.ds(half * rows, rows), pl.ds(pl.multiple_of(target * cols, 128), cols)]
            dst = inner_ref.at[pl.ds(s * block + (me * 2 + half) * rows, rows), :]
            if far:
                one = pltpu.make_async_remote_copy(
                    src_ref=src,
                    dst_ref=dst,
                    send_sem=swap_send.at[far, half],
                    recv_sem=swap_recv.at[far, half],
                    device_id={"fsdp": target},
                    device_id_type=MESH,
                )
            else:
                one = pltpu.make_async_copy(src, dst, own_sem.at[half])
            one.start()
            moves.append(one)
    mine = pltpu.make_async_copy(
        acc.at[pl.ds(2 * rows, rows), :], outer_ref.at[pl.ds(s * rows, rows), :], own_sem.at[2]
    )
    mine.start()
    copies = {}
    outs = ((outer_ref, (n * rows, width), 2), (inner_ref, (n * block, cols), -2))

    def start(k, piece, step):
        ref, shape, split = outs[k]
        chunk = ring_index((place + step) % n if piece else (place + n - step) % n, n)
        view = ring_window(ref, shape, split, n, piece, chunk)
        copies[k, piece, step] = pltpu.make_async_remote_copy(
            src_ref=view,
            dst_ref=view,
            send_sem=send_sem.at[2 * k + piece, step],
            recv_sem=recv_sem.at[2 * k + piece, step],
            device_id={"seq": left if piece else right},
            device_id_type=MESH,
        )
        copies[k, piece, step].start()

    def forward(k, step):
        for piece in range(2):
            copies[k, piece, step].wait_recv()
            if step < n - 2:
                start(k, piece, step + 1)

    mine.wait()
    start(0, 0, 0)
    start(0, 1, 0)
    lead = (n - 1) // 2
    for step in range(lead):
        forward(0, step)
    for one in moves:
        one.wait()
    start(1, 0, 0)
    start(1, 1, 0)
    for step in range(n - 1):
        forward(1, step)
        if lead + step < n - 1:
            forward(0, lead + step)
    for one in parts:
        one.wait()
    for src, into, out in ((part_ref, landed, sum_ref), (few_ref, few_landed, few_sum_ref)):
        rest = src.shape[0] // fan
        total = src[pl.ds(pl.multiple_of(me * rest, rest), rest), :].astype(jnp.float32)
        for far in range(1, fan):
            total = total + into[far].astype(jnp.float32)
        out[...] = total
    for one in [*copies.values(), *sums.values()]:
        one.wait_send()


def units_total(grads, part, few, ident):
    n, fan = lax.axis_size("seq"), lax.axis_size("fsdp")
    rows, width = grads.shape[0] // (3 * n), grads.shape[1]
    tokens = part.shape[0] // fan
    sems = lambda *shape: pltpu.SemaphoreType.DMA(shape)
    return ring_call(
        functools.partial(units_kernel, n, fan),
        "units_total",
        [grads, part, few],
        [
            ((n * 2 * fan * rows, width // fan), jnp.bfloat16),
            ((n * rows, width), jnp.bfloat16),
            ((tokens, part.shape[1]), jnp.float32),
            ((few.shape[0] // fan, few.shape[1]), jnp.float32),
        ],
        [
            pltpu.VMEM(((n - 1) * 3 * rows, width), jnp.bfloat16),
            pltpu.VMEM((3 * rows, width), jnp.bfloat16),
            pltpu.VMEM((fan, tokens, part.shape[1]), jnp.bfloat16),
            pltpu.VMEM((fan, few.shape[0] // fan, few.shape[1]), jnp.bfloat16),
        ]
        + [sems(fan, n - 1), sems(fan, n - 1), sems(fan, 2), sems(fan, 2), sems(3)]
        + [sems(4, n - 1), sems(4, n - 1), sems(2, fan), sems(2, fan)],
        ident,
    )


def team(n):
    s, f = lax.axis_index("seq"), lax.axis_index("fsdp")
    half = s // (n // 2)
    away = (half + f) % 2
    return f // 2, half, (s + away * (n // 2)) % n


def swap_kernel(n, fan, count, fars, fresh, *refs):
    given = count + (len(fars) > 0) + (0 if fresh else 2)
    x_refs, y_refs = refs[:count], refs[given : given + count]
    sems = refs[given + count + (2 if fars else 0) :]
    send_sem, recv_sem, own_sem = sems[:3]
    pair, half, rank = team(n)
    me = lax.axis_index("fsdp")

    def device(other):
        away = (other // (n // 2) + half) % 2
        return {"seq": (other + away * (n // 2)) % n, "fsdp": 2 * pair + (half + away) % 2}

    barrier = pltpu.get_barrier_semaphore()
    for j in range(1, n):
        pl.semaphore_signal(barrier, inc=1, device_id=device((rank + j) % n), device_id_type=MESH)
    travel = [far for far in fars if far]
    for far in travel:
        pl.semaphore_signal(barrier, inc=1, device_id={"fsdp": (me + fan - far) % fan}, device_id_type=MESH)
    pl.semaphore_wait(barrier, n - 1 + len(travel))
    copies = []
    for k in range(count):
        for j in range(1, n):
            other = (rank + j) % n
            one = pltpu.make_async_remote_copy(
                src_ref=x_refs[k].at[other],
                dst_ref=y_refs[k].at[rank],
                send_sem=send_sem.at[k, j],
                recv_sem=recv_sem.at[k, j],
                device_id=device(other),
                device_id_type=MESH,
            )
            one.start()
            copies.append(one)
    for k in range(count):
        one = pltpu.make_async_copy(x_refs[k].at[rank], y_refs[k].at[rank], own_sem.at[k])
        one.start()
        copies.append(one)
    if fars:
        w_ref, halves = refs[count], refs[given + count : given + count + 2]
        far_send, far_recv, far_own, stage = sems[3:]
        rest = []
        units, cols = halves[0].shape[0], w_ref.shape[1]
        for i, far in enumerate(fars):
            target = (me + far) % fan
            for part in range(2):
                src = w_ref.at[pl.ds((part * fan + target) * units, units), :]
                dst = halves[part].at[:, pl.ds(pl.multiple_of(me * cols, 128), cols)]
                if far:
                    one = pltpu.make_async_remote_copy(
                        src_ref=src,
                        dst_ref=dst,
                        send_sem=far_send.at[i, part],
                        recv_sem=far_recv.at[i, part],
                        device_id={"fsdp": target},
                        device_id_type=MESH,
                    )
                else:
                    one = pltpu.make_async_copy(src, stage.at[part], far_own.at[0, part])
                    rest.append((one, pltpu.make_async_copy(stage.at[part], dst, far_own.at[1, part])))
                one.start()
                if far:
                    copies.append(one)
        for inward, outward in rest:
            inward.wait()
            outward.start()
            copies.append(outward)
    for one in copies:
        one.wait()


def swap(arrays, ident, fars=(), given=None, halves=None):
    n, fan = lax.axis_size("seq"), lax.axis_size("fsdp")
    count = len(arrays)
    size = sum(v.size * 2 for v in arrays)
    operands, outs, alias = list(arrays), [jax.ShapeDtypeStruct(v.shape, v.dtype) for v in arrays], {}
    scratch = [
        pltpu.SemaphoreType.DMA((count, n)),
        pltpu.SemaphoreType.DMA((count, n)),
        pltpu.SemaphoreType.DMA((count,)),
    ]
    if fars:
        operands.append(given)
        shape = (given.shape[0] // (2 * fan), given.shape[1] * fan)
        outs += [jax.ShapeDtypeStruct(shape, given.dtype)] * 2
        scratch += [pltpu.SemaphoreType.DMA((len(fars), 2))] * 2 + [
            pltpu.SemaphoreType.DMA((2, 2)),
            pltpu.VMEM((2, given.shape[0] // (2 * fan), given.shape[1]), given.dtype),
        ]
        if halves is not None:
            operands += list(halves)
            alias = {count + 1: count, count + 2: count + 1}
    return pl.pallas_call(
        functools.partial(swap_kernel, n, fan, count, fars, not fars or halves is None),
        name="swap",
        out_shape=outs,
        in_specs=[pl.BlockSpec(memory_space=pl.ANY)] * len(operands),
        out_specs=[pl.BlockSpec(memory_space=pl.ANY)] * len(outs),
        scratch_shapes=scratch,
        input_output_aliases=alias,
        compiler_params=pltpu.CompilerParams(collective_id=ident, has_side_effects=True),
        cost_estimate=pl.CostEstimate(flops=0, bytes_accessed=size, transcendentals=0),
    )(*operands)


def norm_apply(value, gain):
    return value * lax.rsqrt(jnp.mean(value * value, axis=-1, keepdims=True) + EPS) * gain


def norm_back(value, gain, grad):
    _, pull = jax.vjp(norm_apply, value, gain)
    return pull(grad)


def gate_mix(gate, up):
    return jax.nn.gelu(gate, approximate=True) * up


def counts_below(ids, values):
    total = jnp.zeros_like(values)
    for doc in range(DOCS):
        total = total + jnp.where(values > doc, jnp.sum((ids == doc).astype(jnp.int32)), 0)
    return total


def change_home(value):
    n, fan = lax.axis_size("seq"), lax.axis_size("fsdp")
    pairs = []
    for s in range(n):
        for f in range(fan):
            away = (s // (n // 2) + f) % 2
            target = ((s + n // 2) % n, f ^ 1) if away else (s, f)
            pairs.append((s * fan + f, target[0] * fan + target[1]))
    return lax.ppermute(value, ("seq", "fsdp"), pairs)


def spread(blocks):
    fan, me = lax.axis_size("fsdp"), lax.axis_index("fsdp")
    result = blocks
    for far in range(1, fan):
        block = lax.dynamic_index_in_dim(blocks, (me + far) % fan, 0, True)
        block = lax.ppermute(block, "fsdp", [(f, (f + far) % fan) for f in range(fan)])
        result = lax.dynamic_update_slice_in_dim(result, block, (me - far) % fan, 0)
    return result


def flat(blocks):
    return jnp.transpose(blocks, (1, 0, 2)).reshape(blocks.shape[1], -1)


def by_rows(value):
    return with_layout_constraint(value, Layout(major_to_minor=tuple(range(value.ndim))))


def scatter(grad):
    return lax.psum_scatter(grad, "fsdp", scatter_dimension=0, tiled=True)


def shards(
    layer_in, encoder, decoder_ids, encoder_ids, rel_buckets,
    norm_self, self_qkv, self_out, rel_table, norm_cross, cross_q, cross_kv, cross_out, norm_ff, ff_in, ff_out,
    cotangent,
):
    seqs, local, width = layer_in.shape
    enc_local = encoder.shape[1]
    parts = lax.axis_size("seq")
    heads = self_qkv.shape[1]
    dh = self_qkv.shape[2] // 3
    own = heads // parts
    rows = seqs * local
    buckets, table_own = rel_table.shape
    length, keys = local * parts, enc_local * parts
    gather = lambda v: lax.all_gather(v, "fsdp", axis=0, tiled=True)

    fan = lax.axis_size("fsdp")
    units = ff_in.shape[1] // (2 * fan)
    part = norm_self.shape[0]
    pair, half, rank = team(parts)

    qkv_w = gather(self_qkv)
    small = jnp.concatenate([norm_self, norm_cross, norm_ff, rel_table.reshape(-1)])
    small = lax.all_gather(small, "fsdp", axis=0, tiled=False)
    early = by_rows(jnp.stack([self_out, cross_q, *jnp.split(cross_kv.reshape(-1, 2 * width), 2, axis=1)]))
    small, early = lax.optimization_barrier((small, early))
    early = lax.all_gather(early, "fsdp", axis=1, tiled=True)
    both_ids = jnp.concatenate([decoder_ids.reshape(-1), encoder_ids.reshape(-1)])
    both_ids = change_home(jnp.pad(both_ids, (0, 1024 - local - enc_local)).reshape(8, 128))
    inner_t = ff_in.T
    by_kernel = (width // fan) % 128 == 0 and fan % 2 == 0 and (ff_in.shape[0] // parts) % 8 == 0
    (both_ids,) = swap([jnp.broadcast_to(both_ids[None], (parts, 8, 128))], 13)
    home = change_home(layer_in.reshape(rows, width))
    early = by_rows(early)
    mix_self = early[0].reshape(parts, own * dh, width)
    query_w = early[1].reshape(width, parts, own * dh)
    pairs_w = early[2:]

    gain_first, gain_second, gain_third = (
        small[:, i * part : (i + 1) * part].reshape(width).astype(f32) for i in range(3)
    )
    table = jnp.transpose(small[:, 3 * part :].reshape(-1, buckets, table_own), (1, 0, 2)).reshape(buckets, heads)
    both_ids = both_ids.reshape(parts, 1024)
    ids = both_ids[:, :local].reshape(length)
    enc_ids = both_ids[:, local : local + enc_local].reshape(keys)

    first_seen = counts_below(ids, ids)
    enc_first = counts_below(enc_ids, ids)
    enc_last = counts_below(enc_ids, ids + 1)
    blocks = length // BQ
    bk = BQ
    self_rows = jnp.broadcast_to(first_seen[None], (8, length))
    cross_rows = jnp.concatenate([enc_first[None], enc_last[None], jnp.zeros((6, length), jnp.int32)])
    self_limits = jnp.stack(
        [first_seen[::BQ] // bk, (jnp.arange(blocks, dtype=jnp.int32) + 1) * (BQ // bk)]
    )
    cross_limits = jnp.stack([enc_first[::BQ] // bk, (enc_last[BQ - 1 :: BQ] + bk - 1) // bk])

    first_head = rank * own
    table_mine = lax.dynamic_slice_in_dim(table.astype(f32), first_head, own, 1)
    near = rel_buckets[:REACH]
    onehot = (near[:, None] == jnp.arange(buckets, dtype=jnp.int32)[None, :]).astype(f32)
    bias = jnp.einsum("ln,ng->gl", onehot, table_mine, precision=HIGH)
    ext = jnp.concatenate(
        [jnp.full((own, BQ), MASKED, f32), bias, jnp.zeros((own, BQ), f32)], axis=1
    )

    qkv_w, home, inner_t, ext, self_rows, cross_rows, self_limits, cross_limits = lax.optimization_barrier(
        (qkv_w, home, inner_t, ext, self_rows, cross_rows, self_limits, cross_limits)
    )
    qkv_w = qkv_w.reshape(width, parts, own * 3 * dh)

    stream = home.astype(f32)
    normed_first = norm_apply(stream, gain_first).astype(bf16)
    qkv_tok = jnp.einsum("td,dge->gte", normed_first, qkv_w, preferred_element_type=f32).astype(bf16)
    others = change_home(jnp.concatenate([cotangent.reshape(rows, width), encoder.reshape(-1, width)]))
    grad_low, enc_flat = others[:rows], others[rows:]
    fars = [tuple(far for far in range(fan) if by_kernel and min(far, 3) in some) for some in ((2,), (0, 1), (3,))]
    qkv, *halves = swap([qkv_tok], 17, fars[0], inner_t)
    qkv, cross_out, grad_low = lax.optimization_barrier((qkv, cross_out, grad_low))
    if rows == cross_out.shape[0]:
        mix_cross, grad_group = lax.all_gather(jnp.stack([cross_out, grad_low]), "fsdp", axis=1, tiled=True)
    else:
        mix_cross, grad_group = gather(cross_out), gather(grad_low)
    mix_cross = mix_cross.reshape(parts, own * dh, width)
    qkv = qkv.reshape(length, own * 3 * dh)
    out_self, self_t, self_lse = self_forward(self_limits, self_rows, ext, qkv)
    (self_tok,) = swap([out_self.reshape(parts, local, own * dh)], 11)
    after_self = stream + jnp.einsum("gtc,gcd->td", self_tok, mix_self, preferred_element_type=f32)
    normed_second = norm_apply(after_self, gain_second).astype(bf16)
    query_tok = jnp.einsum("td,dgc->gtc", normed_second, query_w, preferred_element_type=f32).astype(bf16)
    pairs_tok = jnp.einsum(
        "td,sdge->sgte", enc_flat, pairs_w.reshape(2, width, parts // 2, -1), preferred_element_type=f32
    )
    pairs_tok = pairs_tok.astype(bf16).reshape(parts, enc_local, -1)
    query_cross, pairs, *halves = swap([query_tok, pairs_tok], 15, fars[1], inner_t, halves)
    query_cross, pairs = query_cross.reshape(length, own * dh), pairs.reshape(keys, own * 2 * dh)
    out_cross, cross_t, cross_lse = cross_forward(cross_limits, cross_rows, query_cross, pairs)
    cross_tok, *halves = swap([out_cross.reshape(parts, local, own * dh)], 16, fars[2], inner_t, halves)
    if not by_kernel:
        halves = spread(jnp.transpose(inner_t.reshape(2, fan, units, -1), (1, 0, 2, 3)))
        halves = [jnp.transpose(halves[:, i], (1, 0, 2)).reshape(units, width) for i in range(2)]
    gate_t, up_t = halves
    after_cross = after_self + jnp.einsum("gtc,gcd->td", cross_tok, mix_cross, preferred_element_type=f32)
    normed_third = norm_apply(after_cross, gain_third).astype(bf16)
    normed_group = gather(normed_third)
    gate = jnp.einsum("td,fd->tf", normed_group, gate_t, preferred_element_type=f32)
    up = jnp.einsum("td,fd->tf", normed_group, up_t, preferred_element_type=f32)
    hidden = gate_mix(gate, up).astype(bf16)

    grad_hidden = jnp.einsum("td,fd->tf", grad_group, ff_out, preferred_element_type=f32)
    _, pull_mix = jax.vjp(gate_mix, gate, up)
    grad_gate, grad_up = (g.astype(bf16) for g in pull_mix(grad_hidden))
    grad_third_in = jnp.dot(grad_gate, gate_t, preferred_element_type=f32) + jnp.dot(
        grad_up, up_t, preferred_element_type=f32
    )
    grad_third_in = scatter(grad_third_in.astype(bf16))
    outer_part = jnp.dot(hidden, ff_out, preferred_element_type=f32).astype(bf16)
    grad_units = [
        jnp.einsum("tf,td->fd", g, y, preferred_element_type=f32).astype(bf16)
        for g, y in ((grad_gate, normed_group), (grad_up, normed_group), (hidden, grad_group))
    ]
    grad_third_in, outer_part, grad_units = lax.optimization_barrier((grad_third_in, outer_part, grad_units))
    if by_kernel:
        grad_units = jnp.stack([g.reshape(parts, units // parts, width) for g in grad_units], axis=1)
        part_units = grad_units.reshape(3 * units, width)
    grad_third_in = grad_third_in.astype(f32)
    grad_from_third, grad_gain_third = norm_back(after_cross, gain_third, grad_third_in)
    grad_middle = grad_low.astype(f32) + grad_from_third
    middle_low = grad_middle.astype(bf16)
    grad_mix_cross = jnp.einsum("gtc,td->gcd", cross_tok, middle_low, preferred_element_type=f32)
    part_cross = scatter(grad_mix_cross.reshape(width, width).astype(bf16))
    grad_cross_tok = jnp.einsum("td,gcd->gtc", middle_low, mix_cross, preferred_element_type=f32).astype(bf16)
    (grad_cross,) = swap([grad_cross_tok], 11)
    grad_cross = grad_cross.reshape(length, own * dh)
    grad_query, grad_pairs = cross_backward(
        cross_limits, cross_rows, query_cross, pairs, grad_cross, cross_t, cross_lse
    )
    grad_query_tok, grad_pairs_tok = swap(
        [grad_query.reshape(parts, local, own * dh), grad_pairs.reshape(parts, enc_local, own * 2 * dh)], 12
    )
    grad_query_tok, grad_pairs_tok = flat(grad_query_tok), flat(grad_pairs_tok)
    grad_query_w = jnp.einsum("td,te->de", normed_second, grad_query_tok, preferred_element_type=f32)
    grad_second_in = jnp.einsum("te,de->td", grad_query_tok, query_w.reshape(width, -1), preferred_element_type=f32)
    grad_pairs_w = jnp.einsum("td,te->de", enc_flat, grad_pairs_tok, preferred_element_type=f32)
    grad_encoder = sum(
        jnp.einsum("te,de->td", grad_pairs_tok[:, i * width : (i + 1) * width], pairs_w[i], preferred_element_type=f32)
        for i in range(2)
    )
    grad_from_second, grad_gain_second = norm_back(after_self, gain_second, grad_second_in)
    grad_upper = grad_middle + grad_from_second
    upper_low = grad_upper.astype(bf16)
    grad_mix_self = jnp.einsum("gtc,td->gcd", self_tok, upper_low, preferred_element_type=f32)
    grad_self_tok = jnp.einsum("td,gcd->gtc", upper_low, mix_self, preferred_element_type=f32).astype(bf16)
    grad_mid = jnp.concatenate(
        [
            grad_query_w.astype(bf16),
            grad_pairs_w.astype(bf16),
            grad_mix_self.reshape(width, width).astype(bf16),
        ],
        axis=1,
    )
    grad_self_tok, grad_mid = lax.optimization_barrier((grad_self_tok, grad_mid))
    part_mid = scatter(grad_mid)
    (grad_self,) = swap([grad_self_tok], 11)
    grad_self = grad_self.reshape(length, own * dh)
    grad_qkv, diagonals = self_backward(self_limits, self_rows, ext, qkv, grad_self, self_t, self_lse)
    (grad_qkv_tok,) = swap([grad_qkv.reshape(parts, local, own * 3 * dh)], 10)
    grad_qkv_tok = flat(grad_qkv_tok)
    grad_qkv_w = jnp.einsum("td,te->de", normed_first, grad_qkv_tok, preferred_element_type=f32)
    grad_first_in = jnp.einsum("te,de->td", grad_qkv_tok, qkv_w.reshape(width, -1), preferred_element_type=f32)
    grad_from_first, grad_gain_first = norm_back(stream, gain_first, grad_first_in)
    grad_layer_in = (grad_upper + grad_from_first).astype(bf16)
    if not by_kernel:
        part_units = grad_units
    bucket_line = jnp.concatenate([jnp.full((BQ - 1,), -1, jnp.int32), near, jnp.full((BQ + 1,), -1, jnp.int32)])
    in_bucket = (bucket_line[:, None] == jnp.arange(buckets, dtype=jnp.int32)).astype(f32)
    by_bucket = jnp.einsum("xn,gx->ng", in_bucket, diagonals, precision=HIGH)
    grad_table = lax.dynamic_update_slice_in_dim(jnp.zeros((buckets, heads), f32), by_bucket, first_head, 1)

    gains = jnp.concatenate(
        [g.reshape(-1, part) for g in (grad_gain_first, grad_gain_second, grad_gain_third)], axis=1
    )
    tables = jnp.transpose(grad_table.reshape(buckets, -1, table_own), (1, 0, 2)).reshape(-1, buckets * table_own)
    small_grads = jnp.concatenate([gains, tables], axis=1).astype(bf16)
    small_size = small_grads.shape[1]
    going_home = jnp.concatenate([grad_layer_in, grad_encoder.astype(bf16)])
    going_home, small_grads, grad_qkv_w, part_units, part_cross, part_mid = lax.optimization_barrier(
        (change_home(going_home), small_grads, grad_qkv_w.astype(bf16), part_units, part_cross, part_mid)
    )
    part_last = scatter(grad_qkv_w)
    if by_kernel:
        few = jnp.pad(small_grads[:, None], ((0, 0), (0, 7), (0, 1024 - small_size))).reshape(fan * 8, 1024)
        total_inner, total_outer, outer_sum, few = units_total(part_units, outer_part, few, 0)
        few = jnp.pad(few[0].astype(bf16).reshape(8, 128), ((0, parts * 8 - 8), (0, 0)))
        total_cross, total_mid, total_qkv, small_total, total_inner = ring_total(
            [part_cross, part_mid, part_last, few], (2, 2, 2, 1), 1, total_inner
        )
    else:
        grad_units = [lax.psum(g, "seq") for g in part_units]
        total_inner = spread(jnp.transpose(jnp.stack(grad_units[:2]).reshape(2, units, fan, -1), (2, 0, 1, 3)))
        total_inner = jnp.transpose(total_inner, (3, 1, 0, 2)).reshape(-1, 2 * fan * units).astype(f32)
        total_outer, outer_sum = grad_units[2], scatter(outer_part).astype(f32)
        few = lax.dynamic_index_in_dim(lax.psum(small_grads, "fsdp"), lax.axis_index("fsdp"), 0, False)
        total_cross, total_mid, total_qkv, small_total = (
            lax.psum(v, "seq") for v in (part_cross, part_mid, part_last, few)
        )
    layer_out = (after_cross + outer_sum).astype(bf16)
    layer_out, total_inner, total_outer, total_cross, total_mid, total_qkv, going_home = lax.optimization_barrier(
        (layer_out, total_inner, total_outer, total_cross, total_mid, total_qkv, going_home)
    )
    layer_out = change_home(layer_out).reshape(seqs, local, width)
    grad_layer_in = going_home[:rows].astype(f32).reshape(seqs, local, width)
    grad_encoder = going_home[rows:].astype(f32).reshape(seqs, enc_local, width)
    total_outer, total_mid, total_qkv = (v.astype(f32) for v in (total_outer, total_mid, total_qkv))
    total_query, total_mix_cross = total_mid[:, :width], total_cross.astype(f32)
    total_pairs = total_mid[:, width : 3 * width].reshape(-1, heads, 2 * dh)
    total_mix_self, total_qkv = total_mid[:, 3 * width :], total_qkv.reshape(-1, heads, 3 * dh)
    mine = small_total.reshape(-1)[:small_size].astype(f32)
    total_gain_first, total_gain_second, total_gain_third = (mine[i * part : (i + 1) * part] for i in range(3))
    total_table = mine[3 * part :].reshape(buckets, table_own)
    return (
        layer_out, grad_layer_in, grad_encoder, total_gain_first, total_qkv, total_mix_self, total_table,
        total_gain_second, total_query, total_pairs, total_mix_cross, total_gain_third, total_inner, total_outer,
    )


def solution(mesh):
    in_specs = (
        P("fsdp", "seq", None), P("fsdp", "seq", None), P("fsdp", "seq"), P("fsdp", "seq"), P(),
        P("fsdp"), P("fsdp", None, None), P("fsdp", None), P(None, "fsdp"), P("fsdp"), P("fsdp", None),
        P("fsdp", None, None), P("fsdp", None), P("fsdp"), P("fsdp", None), P("fsdp", None),
        P("fsdp", "seq", None),
    )
    out_specs = (
        P("fsdp", "seq", None), P("fsdp", "seq", None), P("fsdp", "seq", None), P("fsdp"), P("fsdp", None, None),
        P("fsdp", None), P(None, "fsdp"), P("fsdp"), P("fsdp", None), P("fsdp", None, None), P("fsdp", None),
        P("fsdp"), P("fsdp", None), P("fsdp", None),
    )
    return jax.shard_map(shards, mesh=mesh, in_specs=in_specs, out_specs=out_specs, check_vma=False)
```

```python
import functools

import jax
import jax.numpy as jnp
from jax import lax
from jax.experimental import pallas as pl
from jax.experimental.layout import Layout, with_layout_constraint
from jax.experimental.pallas import tpu as pltpu
from jax.sharding import PartitionSpec as P

EPS = 1e-06
HIGH = lax.Precision.HIGHEST
MASKED = -1e30
DOCS = 4

BQ = 256
REACH = 1024


def blk(index, size):
    return pl.ds(pl.multiple_of(index * size, size), size)


def turn(value):
    return jnp.transpose(value.astype(jnp.float32), (1, 0))


def bias_tiles(ext_ref, tile_ref, own):
    for h in range(own):
        line = jnp.broadcast_to(ext_ref[h : h + 1, :], tile_ref.shape[1:])
        tile_ref[h] = pltpu.roll(line, 0, 1, stride=1, stride_axis=0)


def unpack(ref, own, width, picks, flips, base):
    block = 256

    def one(b, _):
        rows = blk(b, block)
        value = ref[rows, :]
        if flips:
            flat = turn(value).astype(jnp.bfloat16)
            for target, piece in flips:
                for h in range(own):
                    at = h * width + piece * 64
                    target[base + h, :, rows] = flat[at : at + 64]
        for target, piece in picks:
            for h in range(own):
                at = h * width + piece * 64
                target[base + h, rows, :] = value[:, at : at + 64]
        return 0

    lax.fori_loop(0, ref.shape[0] // block, one, 0)


def dot(a, b):
    return jnp.dot(a, b, preferred_element_type=jnp.float32)


def score(own_index, key_tile, query_t, tile_ref, t, low, high, first_key):
    value = dot(key_tile, query_t)
    place = lax.broadcasted_iota(jnp.int32, value.shape, 0)
    keep = place >= low - first_key
    if high is not None:
        keep = keep & (place < high - first_key)
    else:
        value = value + tile_ref[own_index, :, blk(t + 1, BQ)]
    return jnp.where(keep, value, MASKED)


def forward_body(own, bk, causal, lim_ref, rows_ref, q_t, k_rows, v_t, tile_ref, o_ref, ot_ref, lse_ref):
    length = o_ref.shape[0]

    def q_block(i, _):
        cols = blk(i, BQ)
        queries = [q_t[h, :, cols] for h in range(own)]
        low = rows_ref[0:1, cols]
        high = None if causal else rows_ref[1:2, cols]

        def k_block(j, carry):
            keys = blk(j, bk)
            t = i - j
            out = []
            for h in range(own):
                top, total, acc = carry[h]
                s = score(h, k_rows[h, keys, :], queries[h], tile_ref, t, low, high, j * bk)
                new_top = jnp.maximum(top, jnp.max(s, axis=0, keepdims=True))
                p = jnp.exp(s - new_top)
                scale = jnp.exp(top - new_top)
                total = total * scale + jnp.sum(p, axis=0, keepdims=True)
                acc = acc * scale + dot(v_t[h, :, keys], p.astype(jnp.bfloat16))
                out.append((new_top, total, acc))
            return tuple(out)

        start = tuple(
            (
                jnp.full((1, BQ), MASKED, jnp.float32),
                jnp.zeros((1, BQ), jnp.float32),
                jnp.zeros((64, BQ), jnp.float32),
            )
            for _ in range(own)
        )
        ends = lax.fori_loop(lim_ref[0, i], lim_ref[1, i], k_block, start)
        for h in range(own):
            top, total, acc = ends[h]
            ot_ref[h * 64 : h * 64 + 64, cols] = acc / total
            lse_ref[h : h + 1, cols] = top + jnp.log(total)
        o_ref[cols, :] = turn(ot_ref[:, cols]).astype(jnp.bfloat16)
        return 0

    lax.fori_loop(0, length // BQ, q_block, 0)


def self_forward_kernel(own, bk, lim_ref, rows_ref, ext_ref, x_ref, o_ref, ot_ref, lse_ref, q_t, k_rows, v_t, tile_ref):
    bias_tiles(ext_ref, tile_ref, own)
    unpack(x_ref, own, 192, [(k_rows, 1)], [(q_t, 0), (v_t, 2)], 0)
    forward_body(own, bk, True, lim_ref, rows_ref, q_t, k_rows, v_t, tile_ref, o_ref, ot_ref, lse_ref)


def cross_forward_kernel(own, bk, lim_ref, rows_ref, q_ref, kv_ref, o_ref, ot_ref, lse_ref, q_t, k_rows, v_t):
    unpack(q_ref, own, 64, [], [(q_t, 0)], 0)
    unpack(kv_ref, own, 128, [(k_rows, 0)], [(v_t, 1)], 0)
    forward_body(own, bk, False, lim_ref, rows_ref, q_t, k_rows, v_t, None, o_ref, ot_ref, lse_ref)


def backward_body(
    own, bk, causal, lim_ref, rows_ref, do_ref, ot_ref, lse_ref,
    q_t, q_rows, k_t, k_rows, v_rows, do_t, do_rows, tile_ref, sum_ref, dq_t, dk, dv,
):
    length = do_ref.shape[0]
    dk[...] = jnp.zeros_like(dk)
    dv[...] = jnp.zeros_like(dv)
    if causal:
        sum_ref[...] = jnp.zeros_like(sum_ref)

    def q_block(i, _):
        cols = blk(i, BQ)
        low = rows_ref[0:1, cols]
        high = None if causal else rows_ref[1:2, cols]
        per_head = []
        for h in range(own):
            grad_t = do_t[h, :, cols]
            delta = jnp.sum(
                grad_t.astype(jnp.float32) * ot_ref[h * 64 : h * 64 + 64, cols], axis=0, keepdims=True
            )
            per_head.append((q_t[h, :, cols], grad_t, delta, lse_ref[h : h + 1, cols]))

        def k_block(j, carry):
            keys = blk(j, bk)
            t = i - j
            out = []
            for h in range(own):
                query_t, grad_t, delta, lse = per_head[h]
                s = score(h, k_rows[h, keys, :], query_t, tile_ref, t, low, high, j * bk)
                p = jnp.exp(s - lse)
                dp = dot(v_rows[h, keys, :], grad_t)
                ds = (p * (dp - delta)).astype(jnp.bfloat16)
                dv[h, keys, :] += dot(p.astype(jnp.bfloat16), do_rows[h, cols, :])
                dk[h, keys, :] += dot(ds, q_rows[h, cols, :])
                if causal:
                    sum_ref[h, :, blk(t, BQ)] += ds.astype(jnp.float32)
                out.append(carry[h] + dot(k_t[h, :, keys], ds))
            return tuple(out)

        ends = lax.fori_loop(
            lim_ref[0, i],
            lim_ref[1, i],
            k_block,
            tuple(jnp.zeros((64, BQ), jnp.float32) for _ in range(own)),
        )
        for h in range(own):
            dq_t[h * 64 : h * 64 + 64, cols] = ends[h]
        return 0

    lax.fori_loop(0, length // BQ, q_block, 0)


def diagonal_sums(sum_ref, u_ref, own):
    flip = lax.broadcasted_iota(jnp.int32, (BQ, BQ), 0) + lax.broadcasted_iota(jnp.int32, (BQ, BQ), 1) == BQ - 1
    flip = jnp.where(flip, 1.0, 0.0).astype(jnp.bfloat16)
    for h in range(own):
        grid = sum_ref[h]
        high = grid.astype(jnp.bfloat16)
        low = (grid - high.astype(jnp.float32)).astype(jnp.bfloat16)
        upside = dot(flip, high) + dot(flip, low)
        wide = jnp.concatenate([upside, jnp.zeros((BQ, BQ), jnp.float32)], axis=1)
        aligned = pltpu.roll(wide, 0, 1, stride=1, stride_axis=0)
        u_ref[h : h + 1, :] = jnp.sum(aligned, axis=0, keepdims=True)


def self_backward_kernel(
    own, bk, lim_ref, rows_ref, ext_ref, x_ref, do_ref, ot_ref, lse_ref, dx_ref, u_ref,
    q_t, q_rows, k_t, k_rows, v_rows, do_t, do_rows, tile_ref, sum_ref, dq_t, dk, dv,
):
    bias_tiles(ext_ref, tile_ref, own)
    unpack(x_ref, own, 192, [(q_rows, 0), (k_rows, 1), (v_rows, 2)], [(q_t, 0), (k_t, 1)], 0)
    unpack(do_ref, own, 64, [(do_rows, 0)], [(do_t, 0)], 0)
    backward_body(
        own, bk, True, lim_ref, rows_ref, do_ref, ot_ref, lse_ref,
        q_t, q_rows, k_t, k_rows, v_rows, do_t, do_rows, tile_ref, sum_ref, dq_t, dk, dv,
    )
    diagonal_sums(sum_ref, u_ref, own)

    def pack(b, _):
        rows = blk(b, 256)
        dq = turn(dq_t[:, rows])
        pieces = []
        for h in range(own):
            pieces += [dq[:, h * 64 : h * 64 + 64], dk[h, rows, :], dv[h, rows, :]]
        dx_ref[rows, :] = jnp.concatenate(pieces, axis=1).astype(jnp.bfloat16)
        return 0

    lax.fori_loop(0, x_ref.shape[0] // 256, pack, 0)


def cross_backward_kernel(
    own, bk, lim_ref, rows_ref, q_ref, kv_ref, do_ref, ot_ref, lse_ref, dq_ref, dkv_ref,
    q_t, q_rows, k_t, k_rows, v_rows, do_t, do_rows, dq_t, dk, dv,
):
    unpack(q_ref, own, 64, [(q_rows, 0)], [(q_t, 0)], 0)
    unpack(kv_ref, own, 128, [(k_rows, 0), (v_rows, 1)], [(k_t, 0)], 0)
    unpack(do_ref, own, 64, [(do_rows, 0)], [(do_t, 0)], 0)
    backward_body(
        own, bk, False, lim_ref, rows_ref, do_ref, ot_ref, lse_ref,
        q_t, q_rows, k_t, k_rows, v_rows, do_t, do_rows, None, None, dq_t, dk, dv,
    )

    def pack_q(b, _):
        rows = blk(b, 256)
        dq_ref[rows, :] = turn(dq_t[:, rows]).astype(jnp.bfloat16)
        return 0

    def pack_kv(b, _):
        rows = blk(b, 256)
        pieces = []
        for h in range(own):
            pieces += [dk[h, rows, :], dv[h, rows, :]]
        dkv_ref[rows, :] = jnp.concatenate(pieces, axis=1).astype(jnp.bfloat16)
        return 0

    lax.fori_loop(0, q_ref.shape[0] // 256, pack_q, 0)
    lax.fori_loop(0, kv_ref.shape[0] // 256, pack_kv, 0)


SMEM = pl.BlockSpec(memory_space=pltpu.SMEM)
VMEM = pl.BlockSpec(memory_space=pltpu.VMEM)
bf16, f32 = jnp.bfloat16, jnp.float32


def call(body, name, operands, outs, scratch, flops):
    size = sum(v.size * v.dtype.itemsize for v in operands)
    return pl.pallas_call(
        body,
        name=name,
        out_shape=[jax.ShapeDtypeStruct(s, d) for s, d in outs],
        in_specs=[SMEM] + [VMEM] * (len(operands) - 1),
        out_specs=[VMEM] * len(outs),
        scratch_shapes=[pltpu.VMEM(s, d) for s, d in scratch],
        compiler_params=pltpu.CompilerParams(vmem_limit_bytes=40 << 20),
        cost_estimate=pl.CostEstimate(flops=0, bytes_accessed=size, transcendentals=0),
    )(*operands)


def self_forward(limits, rows, ext, x, bk=BQ):
    length, own = x.shape[0], x.shape[1] // 192
    return call(
        functools.partial(self_forward_kernel, own, bk),
        "self_forward",
        [limits, rows, ext, x],
        [((length, own * 64), bf16), ((own * 64, length), f32), ((own, length), f32)],
        [
            ((own, 64, length), bf16),
            ((own, length, 64), bf16),
            ((own, 64, length), bf16),
            ((own, BQ, REACH + 2 * BQ), f32),
        ],
        length * length * own * 64,
    )


def cross_forward(limits, rows, q, kv, bk=BQ):
    length, own, keys = q.shape[0], q.shape[1] // 64, kv.shape[0]
    return call(
        functools.partial(cross_forward_kernel, own, bk),
        "cross_forward",
        [limits, rows, q, kv],
        [((length, own * 64), bf16), ((own * 64, length), f32), ((own, length), f32)],
        [((own, 64, length), bf16), ((own, keys, 64), bf16), ((own, 64, keys), bf16)],
        length * keys * own * 128,
    )


def self_backward(limits, rows, ext, x, grad, o_t, lse, bk=BQ):
    length, own = x.shape[0], x.shape[1] // 192
    return call(
        functools.partial(self_backward_kernel, own, bk),
        "self_backward",
        [limits, rows, ext, x, grad, o_t, lse],
        [((length, own * 192), bf16), ((own, REACH + 2 * BQ), f32)],
        [
            ((own, 64, length), bf16),
            ((own, length, 64), bf16),
            ((own, 64, length), bf16),
            ((own, length, 64), bf16),
            ((own, length, 64), bf16),
            ((own, 64, length), bf16),
            ((own, length, 64), bf16),
            ((own, BQ, REACH + 2 * BQ), f32),
            ((own, BQ, REACH + BQ), f32),
            ((own * 64, length), f32),
            ((own, length, 64), f32),
            ((own, length, 64), f32),
        ],
        length * length * own * 160,
    )


def cross_backward(limits, rows, q, kv, grad, o_t, lse, bk=BQ):
    length, own, keys = q.shape[0], q.shape[1] // 64, kv.shape[0]
    return call(
        functools.partial(cross_backward_kernel, own, bk),
        "cross_backward",
        [limits, rows, q, kv, grad, o_t, lse],
        [((length, own * 64), bf16), ((keys, own * 128), bf16)],
        [
            ((own, 64, length), bf16),
            ((own, length, 64), bf16),
            ((own, 64, keys), bf16),
            ((own, keys, 64), bf16),
            ((own, keys, 64), bf16),
            ((own, 64, length), bf16),
            ((own, length, 64), bf16),
            ((own * 64, length), f32),
            ((own, keys, 64), f32),
            ((own, keys, 64), f32),
        ],
        length * keys * own * 320,
    )


def rows_of(blocks_ref):
    return jnp.concatenate([blocks_ref[g] for g in range(blocks_ref.shape[0])], axis=1)


def against(a, b):
    return lax.dot_general(a, b, (((1,), (1,)), ((), ())), preferred_element_type=jnp.float32)


def into_kernel(tok_ref, home_ref, gain_ref, enc_ref, w_ref, after_ref, norm_ref, query_ref, pairs_ref):
    which = pl.program_id(0)

    @pl.when(which == 0)
    def _():
        value = home_ref[...].astype(jnp.float32) + dot(rows_of(tok_ref), w_ref[0])
        after_ref[...] = value
        scale = lax.rsqrt(jnp.mean(value * value, axis=1, keepdims=True) + EPS)
        norm_ref[...] = (value * scale * gain_ref[...]).astype(jnp.bfloat16)

    @pl.when(which == 1)
    def _():
        query = dot(norm_ref[...], w_ref[0]).astype(jnp.bfloat16)
        cols = query_ref.shape[2]
        for g in range(query_ref.shape[0]):
            query_ref[g] = query[:, g * cols : (g + 1) * cols]

    for half in range(2):

        @pl.when(which == 2 + half)
        def _():
            pairs = dot(enc_ref[...], w_ref[0]).astype(jnp.bfloat16)
            groups, cols = pairs_ref.shape[0] // 2, pairs_ref.shape[2]
            for g in range(groups):
                pairs_ref[half * groups + g] = pairs[:, g * cols : (g + 1) * cols]


def outof_kernel(
    dq_ref, dkv_ref, after_ref, gain_ref, middle_ref, w_ref,
    upper_ref, low_ref, out_ref, gain_grad_ref, enc_grad_ref, dq_flat_ref, dkv_flat_ref, enc_sum,
):
    which = pl.program_id(0)

    @pl.when(which == 0)
    def _():
        grad_query = rows_of(dq_ref)
        dq_flat_ref[...] = grad_query
        dkv_flat_ref[...] = rows_of(dkv_ref)
        grad = against(grad_query, w_ref[0])
        value = after_ref[...]
        unit = value * lax.rsqrt(jnp.mean(value * value, axis=1, keepdims=True) + EPS)
        gain_grad_ref[...] = jnp.sum(grad * unit, axis=0, keepdims=True)
        scale = lax.rsqrt(jnp.mean(value * value, axis=1, keepdims=True) + EPS)
        grad = grad * gain_ref[...]
        inner = jnp.mean(grad * unit, axis=1, keepdims=True)
        upper = middle_ref[...] + scale * (grad - unit * inner)
        upper_ref[...] = upper
        low_ref[...] = upper.astype(jnp.bfloat16)

    @pl.when(which == 1)
    def _():
        grad = against(low_ref[...], w_ref[0]).astype(jnp.bfloat16)
        cols = out_ref.shape[2]
        for g in range(out_ref.shape[0]):
            out_ref[g] = grad[:, g * cols : (g + 1) * cols]

    width = w_ref.shape[1]

    @pl.when(which == 2)
    def _():
        enc_sum[...] = against(dkv_flat_ref[:, :width], w_ref[0])

    @pl.when(which == 3)
    def _():
        enc_grad_ref[...] = (enc_sum[...] + against(dkv_flat_ref[:, width:], w_ref[0])).astype(jnp.bfloat16)


def over_weights(body, name, arrays, weights, order, outs, scratch=()):
    count, rows, cols = weights.shape
    whole = lambda shape: pl.BlockSpec(shape, lambda i: (0,) * len(shape))
    return pl.pallas_call(
        body,
        name=name,
        grid=(count,),
        out_shape=[jax.ShapeDtypeStruct(s, d) for s, d in outs],
        in_specs=[whole(v.shape) for v in arrays] + [pl.BlockSpec((1, rows, cols), lambda i: (order(i), 0, 0))],
        out_specs=[whole(s) for s, _ in outs],
        scratch_shapes=[pltpu.VMEM(s, d) for s, d in scratch],
        compiler_params=pltpu.CompilerParams(vmem_limit_bytes=40 << 20, dimension_semantics=("arbitrary",)),
        cost_estimate=pl.CostEstimate(flops=0, bytes_accessed=weights.size * 2, transcendentals=0),
    )(*arrays, weights)


MESH = pl.DeviceIdType.MESH


def ring_place(index, n):
    z, x = index // 2, index % 2
    return z + x * (n - 1 - 2 * z)


def ring_index(place, n):
    x = place // (n // 2)
    z = place + x * (n - 1 - 2 * place)
    return 2 * z + x


def ring_greet(n, others):
    place = ring_place(lax.axis_index("seq"), n)
    right = ring_index((place + 1) % n, n)
    left = ring_index((place + n - 1) % n, n)
    barrier = pltpu.get_barrier_semaphore()
    for neighbour in (left, right):
        pl.semaphore_signal(barrier, inc=1, device_id={"seq": neighbour}, device_id_type=MESH)
    for other in others:
        pl.semaphore_signal(barrier, inc=1, device_id={"fsdp": other}, device_id_type=MESH)
    pl.semaphore_wait(barrier, 2 + len(others))
    return place, right, left


def ring_cut(shape, split, n):
    rows, cols = shape[0] // n, shape[1]
    return (rows, cols // split) if split > 0 else (rows // -split, cols)


def ring_window(ref, shape, split, n, piece, chunk):
    whole = shape[0] // n
    rows, cols = ring_cut(shape, split, n)
    if split > 0:
        return ref.at[pl.ds(chunk * whole, rows), pl.ds(piece * cols, cols)]
    return ref.at[pl.ds(chunk * whole + piece * rows, rows), :]


def ring_kernel(n, splits, fan, *refs):
    count = len(splits)
    more = 1 if fan else 0
    x_refs, y_refs = refs[:count], refs[count + more : 2 * count + more]
    slots = refs[2 * (count + more) : 3 * count + 2 * more]
    send_sem, recv_sem = refs[3 * count + 2 * more :]
    place, right, left = ring_greet(n, [])
    streams = [(k, piece, piece % 2) for k in range(count) for piece in range(abs(splits[k]))]

    def window(ref, k, piece, chunk):
        return ring_window(ref, x_refs[k].shape, splits[k], n, piece, chunk)

    def chunk_at(down, step):
        return (place + 1 + step) % n if down else (place + 2 * n - 1 - step) % n

    copies = {}

    def start(number, step, src, dst, down):
        copies[number, step] = pltpu.make_async_remote_copy(
            src_ref=src,
            dst_ref=dst,
            send_sem=send_sem.at[number, step],
            recv_sem=recv_sem.at[number, step],
            device_id={"seq": left if down else right},
            device_id_type=MESH,
        )
        copies[number, step].start()

    def turn_block(number):
        inner_ref, turned_ref = refs[count], refs[2 * count + 1]
        rows = inner_ref.shape[0] // (2 * fan * n)
        half, first = number // (fan // 2), number % (fan // 2) * 2
        tall = jnp.concatenate(
            [
                inner_ref[pl.ds(((chunk * fan + group) * 2 + half) * rows, rows), :].astype(jnp.float32)
                for group in (first, first + 1)
                for chunk in range(n)
            ]
        )
        wide = 2 * n * rows
        turned_ref[:, number * wide : (number + 1) * wide] = jnp.transpose(tall, (1, 0))

    for number, (k, piece, down) in enumerate(streams):
        start(number, 0, window(x_refs[k], k, piece, place), window(slots[k], k, piece, 0), down)
    for step in range(n - 1):
        if step < fan:
            turn_block(step)
        for number, (k, piece, down) in enumerate(streams):
            copies[number, step].wait_recv()
            chunk = chunk_at(down, step)
            mine = window(x_refs[k], k, piece, chunk)
            landed = window(slots[k], k, piece, step)
            total = landed[...].astype(jnp.float32) + mine[...].astype(jnp.float32)
            if step < n - 2:
                landed[...] = total.astype(jnp.bfloat16)
                start(number, step + 1, landed, window(slots[k], k, piece, step + 1), down)
            else:
                done = window(y_refs[k], k, piece, chunk)
                done[...] = total.astype(jnp.bfloat16)
                start(number, n - 1, done, done, down)
    for step in range(n - 1):
        for number, (k, piece, down) in enumerate(streams):
            copies[number, n - 1 + step].wait_recv()
            if step < n - 2:
                done = window(y_refs[k], k, piece, chunk_at(down, n - 1 + step))
                start(number, n + step, done, done, down)
    for one in copies.values():
        one.wait_send()


def ring_call(body, name, arrays, outs, scratch, ident):
    size = sum(v.size * 2 for v in arrays)
    return pl.pallas_call(
        body,
        name=name,
        out_shape=[jax.ShapeDtypeStruct(s, d) for s, d in outs],
        in_specs=[pl.BlockSpec(memory_space=pltpu.VMEM)] * len(arrays),
        out_specs=[pl.BlockSpec(memory_space=pltpu.VMEM)] * len(outs),
        scratch_shapes=scratch,
        compiler_params=pltpu.CompilerParams(
            collective_id=ident, has_side_effects=True, vmem_limit_bytes=48 << 20
        ),
        cost_estimate=pl.CostEstimate(flops=0, bytes_accessed=60 * size, transcendentals=0),
    )(*arrays)


def ring_total(arrays, splits, ident, inner=None):
    n, fan = lax.axis_size("seq"), lax.axis_size("fsdp")
    streams = sum(abs(s) for s in splits)
    more = [] if inner is None else [inner]
    return ring_call(
        functools.partial(ring_kernel, n, splits, 0 if inner is None else fan),
        "ring_total",
        arrays + more,
        [(v.shape, jnp.bfloat16) for v in arrays] + [(v.shape[::-1], jnp.float32) for v in more],
        [pltpu.VMEM((v.shape[0] // n * (n - 1), v.shape[1]), jnp.bfloat16) for v in arrays]
        + [pltpu.SemaphoreType.DMA((streams, 2 * n - 2))] * 2,
        ident,
    )


def units_kernel(
    n, fan, x_ref, part_ref, few_ref, inner_ref, outer_ref, sum_ref, few_sum_ref, slots, acc, landed, few_landed,
    down_send, down_recv, swap_send, swap_recv, own_sem, send_sem, recv_sem, part_send, part_recv,
):
    s, me = lax.axis_index("seq"), lax.axis_index("fsdp")
    rows, width = acc.shape[0] // 3, x_ref.shape[1]
    cols = width // fan
    block = 2 * fan * rows
    place, right, left = ring_greet(n, [(me + far) % fan for far in range(1, fan)])
    sums = {}

    def piece_of(ref, at, piece):
        return ref.at[pl.ds(at * 3 * rows, 3 * rows), pl.ds(piece * cols, cols)]

    def send_sum(piece, step, src):
        to = left if piece >= fan // 2 else right
        sums[piece, step] = pltpu.make_async_remote_copy(
            src_ref=src,
            dst_ref=piece_of(slots, step, piece),
            send_sem=down_send.at[piece, step],
            recv_sem=down_recv.at[piece, step],
            device_id={"seq": to},
            device_id_type=MESH,
        )
        sums[piece, step].start()

    def chunk(piece, step):
        return ring_index((place + 1 + step) % n if piece >= fan // 2 else (place + 2 * n - 1 - step) % n, n)

    for piece in range(fan):
        send_sum(piece, 0, piece_of(x_ref, chunk(piece, 0), piece))
    for step in range(n - 1):
        for piece in range(fan):
            sums[piece, step].wait_recv()
            arrived = piece_of(slots, step, piece)
            mine = piece_of(x_ref, chunk(piece, step + 1), piece)
            total = (arrived[...].astype(jnp.float32) + mine[...].astype(jnp.float32)).astype(jnp.bfloat16)
            if step < n - 2:
                arrived[...] = total
                send_sum(piece, step + 1, arrived)
            else:
                acc[:, piece * cols : (piece + 1) * cols] = total
    moves = []
    for far in range(fan):
        target = (me + far) % fan
        for half in range(2):
            src = acc.at[pl.ds(half * rows, rows), pl.ds(pl.multiple_of(target * cols, 128), cols)]
            dst = inner_ref.at[pl.ds(s * block + (me * 2 + half) * rows, rows), :]
            if far:
                one = pltpu.make_async_remote_copy(
                    src_ref=src,
                    dst_ref=dst,
                    send_sem=swap_send.at[far, half],
                    recv_sem=swap_recv.at[far, half],
                    device_id={"fsdp": target},
                    device_id_type=MESH,
                )
            else:
                one = pltpu.make_async_copy(src, dst, own_sem.at[half])
            one.start()
            moves.append(one)
    mine = pltpu.make_async_copy(
        acc.at[pl.ds(2 * rows, rows), :], outer_ref.at[pl.ds(s * rows, rows), :], own_sem.at[2]
    )
    mine.start()
    copies = {}
    outs = ((outer_ref, (n * rows, width), 2), (inner_ref, (n * block, cols), -2))

    def start(k, piece, step):
        ref, shape, split = outs[k]
        chunk = ring_index((place + step) % n if piece else (place + n - step) % n, n)
        view = ring_window(ref, shape, split, n, piece, chunk)
        copies[k, piece, step] = pltpu.make_async_remote_copy(
            src_ref=view,
            dst_ref=view,
            send_sem=send_sem.at[2 * k + piece, step],
            recv_sem=recv_sem.at[2 * k + piece, step],
            device_id={"seq": left if piece else right},
            device_id_type=MESH,
        )
        copies[k, piece, step].start()

    def forward(k, step):
        for piece in range(2):
            copies[k, piece, step].wait_recv()
            if step < n - 2:
                start(k, piece, step + 1)

    mine.wait()
    start(0, 0, 0)
    start(0, 1, 0)
    lead = (n - 1) // 2
    for step in range(lead):
        forward(0, step)
    for one in moves:
        one.wait()
    parts = []
    for far in range(1, fan):
        target = (me + far) % fan
        for which, (src, into) in enumerate(((part_ref, landed), (few_ref, few_landed))):
            rest = src.shape[0] // fan
            one = pltpu.make_async_remote_copy(
                src_ref=src.at[pl.ds(target * rest, rest), :],
                dst_ref=into.at[far],
                send_sem=part_send.at[which, far],
                recv_sem=part_recv.at[which, far],
                device_id={"fsdp": target},
                device_id_type=MESH,
            )
            one.start()
            parts.append(one)
    start(1, 0, 0)
    start(1, 1, 0)
    for step in range(n - 1):
        forward(1, step)
        if lead + step < n - 1:
            forward(0, lead + step)
    for one in parts:
        one.wait()
    for src, into, out in ((part_ref, landed, sum_ref), (few_ref, few_landed, few_sum_ref)):
        rest = src.shape[0] // fan
        total = src[pl.ds(pl.multiple_of(me * rest, rest), rest), :].astype(jnp.float32)
        for far in range(1, fan):
            total = total + into[far].astype(jnp.float32)
        out[...] = total
    for one in [*copies.values(), *sums.values()]:
        one.wait_send()


def units_total(grads, part, few, ident):
    n, fan = lax.axis_size("seq"), lax.axis_size("fsdp")
    rows, width = grads.shape[0] // (3 * n), grads.shape[1]
    tokens = part.shape[0] // fan
    sems = lambda *shape: pltpu.SemaphoreType.DMA(shape)
    return ring_call(
        functools.partial(units_kernel, n, fan),
        "units_total",
        [grads, part, few],
        [
            ((n * 2 * fan * rows, width // fan), jnp.bfloat16),
            ((n * rows, width), jnp.bfloat16),
            ((tokens, part.shape[1]), jnp.float32),
            ((few.shape[0] // fan, few.shape[1]), jnp.float32),
        ],
        [
            pltpu.VMEM(((n - 1) * 3 * rows, width), jnp.bfloat16),
            pltpu.VMEM((3 * rows, width), jnp.bfloat16),
            pltpu.VMEM((fan, tokens, part.shape[1]), jnp.bfloat16),
            pltpu.VMEM((fan, few.shape[0] // fan, few.shape[1]), jnp.bfloat16),
        ]
        + [sems(fan, n - 1), sems(fan, n - 1), sems(fan, 2), sems(fan, 2), sems(3)]
        + [sems(4, n - 1), sems(4, n - 1), sems(2, fan), sems(2, fan)],
        ident,
    )


def team(n):
    s, f = lax.axis_index("seq"), lax.axis_index("fsdp")
    half = s // (n // 2)
    away = (half + f) % 2
    return f // 2, half, (s + away * (n // 2)) % n


def swap_kernel(n, fan, count, fars, fresh, *refs):
    given = count + (len(fars) > 0) + (0 if fresh else 2)
    x_refs, y_refs = refs[:count], refs[given : given + count]
    sems = refs[given + count + (2 if fars else 0) :]
    send_sem, recv_sem, own_sem = sems[:3]
    pair, half, rank = team(n)
    me = lax.axis_index("fsdp")

    def device(other):
        away = (other // (n // 2) + half) % 2
        return {"seq": (other + away * (n // 2)) % n, "fsdp": 2 * pair + (half + away) % 2}

    barrier = pltpu.get_barrier_semaphore()
    for j in range(1, n):
        pl.semaphore_signal(barrier, inc=1, device_id=device((rank + j) % n), device_id_type=MESH)
    travel = [far for far in fars if far]
    for far in travel:
        pl.semaphore_signal(barrier, inc=1, device_id={"fsdp": (me + fan - far) % fan}, device_id_type=MESH)
    pl.semaphore_wait(barrier, n - 1 + len(travel))
    copies = []
    for k in range(count):
        for j in range(1, n):
            other = (rank + j) % n
            one = pltpu.make_async_remote_copy(
                src_ref=x_refs[k].at[other],
                dst_ref=y_refs[k].at[rank],
                send_sem=send_sem.at[k, j],
                recv_sem=recv_sem.at[k, j],
                device_id=device(other),
                device_id_type=MESH,
            )
            one.start()
            copies.append(one)
    for k in range(count):
        one = pltpu.make_async_copy(x_refs[k].at[rank], y_refs[k].at[rank], own_sem.at[k])
        one.start()
        copies.append(one)
    if fars:
        w_ref, halves = refs[count], refs[given + count : given + count + 2]
        far_send, far_recv, far_own, stage = sems[3:]
        rest = []
        units, cols = halves[0].shape[0], w_ref.shape[1]
        for i, far in enumerate(fars):
            target = (me + far) % fan
            for part in range(2):
                src = w_ref.at[pl.ds((part * fan + target) * units, units), :]
                dst = halves[part].at[:, pl.ds(pl.multiple_of(me * cols, 128), cols)]
                if far:
                    one = pltpu.make_async_remote_copy(
                        src_ref=src,
                        dst_ref=dst,
                        send_sem=far_send.at[i, part],
                        recv_sem=far_recv.at[i, part],
                        device_id={"fsdp": target},
                        device_id_type=MESH,
                    )
                else:
                    one = pltpu.make_async_copy(src, stage.at[part], far_own.at[0, part])
                    rest.append((one, pltpu.make_async_copy(stage.at[part], dst, far_own.at[1, part])))
                one.start()
                if far:
                    copies.append(one)
        for inward, outward in rest:
            inward.wait()
            outward.start()
            copies.append(outward)
    for one in copies:
        one.wait()


def swap(arrays, ident, fars=(), given=None, halves=None):
    n, fan = lax.axis_size("seq"), lax.axis_size("fsdp")
    count = len(arrays)
    size = sum(v.size * 2 for v in arrays)
    operands, outs, alias = list(arrays), [jax.ShapeDtypeStruct(v.shape, v.dtype) for v in arrays], {}
    scratch = [
        pltpu.SemaphoreType.DMA((count, n)),
        pltpu.SemaphoreType.DMA((count, n)),
        pltpu.SemaphoreType.DMA((count,)),
    ]
    if fars:
        operands.append(given)
        shape = (given.shape[0] // (2 * fan), given.shape[1] * fan)
        outs += [jax.ShapeDtypeStruct(shape, given.dtype)] * 2
        scratch += [pltpu.SemaphoreType.DMA((len(fars), 2))] * 2 + [
            pltpu.SemaphoreType.DMA((2, 2)),
            pltpu.VMEM((2, given.shape[0] // (2 * fan), given.shape[1]), given.dtype),
        ]
        if halves is not None:
            operands += list(halves)
            alias = {count + 1: count, count + 2: count + 1}
    return pl.pallas_call(
        functools.partial(swap_kernel, n, fan, count, fars, not fars or halves is None),
        name="swap",
        out_shape=outs,
        in_specs=[pl.BlockSpec(memory_space=pl.ANY)] * len(operands),
        out_specs=[pl.BlockSpec(memory_space=pl.ANY)] * len(outs),
        scratch_shapes=scratch,
        input_output_aliases=alias,
        compiler_params=pltpu.CompilerParams(collective_id=ident, has_side_effects=True),
        cost_estimate=pl.CostEstimate(flops=0, bytes_accessed=size, transcendentals=0),
    )(*operands)


def norm_apply(value, gain):
    return value * lax.rsqrt(jnp.mean(value * value, axis=-1, keepdims=True) + EPS) * gain


def norm_back(value, gain, grad):
    _, pull = jax.vjp(norm_apply, value, gain)
    return pull(grad)


def gate_mix(gate, up):
    return jax.nn.gelu(gate, approximate=True) * up


def counts_below(ids, values):
    total = jnp.zeros_like(values)
    for doc in range(DOCS):
        total = total + jnp.where(values > doc, jnp.sum((ids == doc).astype(jnp.int32)), 0)
    return total


def change_home(value):
    n, fan = lax.axis_size("seq"), lax.axis_size("fsdp")
    pairs = []
    for s in range(n):
        for f in range(fan):
            away = (s // (n // 2) + f) % 2
            target = ((s + n // 2) % n, f ^ 1) if away else (s, f)
            pairs.append((s * fan + f, target[0] * fan + target[1]))
    return lax.ppermute(value, ("seq", "fsdp"), pairs)


def spread(blocks):
    fan, me = lax.axis_size("fsdp"), lax.axis_index("fsdp")
    result = blocks
    for far in range(1, fan):
        block = lax.dynamic_index_in_dim(blocks, (me + far) % fan, 0, True)
        block = lax.ppermute(block, "fsdp", [(f, (f + far) % fan) for f in range(fan)])
        result = lax.dynamic_update_slice_in_dim(result, block, (me - far) % fan, 0)
    return result


def flat(blocks):
    return jnp.transpose(blocks, (1, 0, 2)).reshape(blocks.shape[1], -1)


def by_rows(value):
    return with_layout_constraint(value, Layout(major_to_minor=tuple(range(value.ndim))))


def scatter(grad):
    return lax.psum_scatter(grad, "fsdp", scatter_dimension=0, tiled=True)


def shards(
    layer_in, encoder, decoder_ids, encoder_ids, rel_buckets,
    norm_self, self_qkv, self_out, rel_table, norm_cross, cross_q, cross_kv, cross_out, norm_ff, ff_in, ff_out,
    cotangent,
):
    seqs, local, width = layer_in.shape
    enc_local = encoder.shape[1]
    parts = lax.axis_size("seq")
    heads = self_qkv.shape[1]
    dh = self_qkv.shape[2] // 3
    own = heads // parts
    rows = seqs * local
    buckets, table_own = rel_table.shape
    length, keys = local * parts, enc_local * parts
    gather = lambda v: lax.all_gather(v, "fsdp", axis=0, tiled=True)

    fan = lax.axis_size("fsdp")
    units = ff_in.shape[1] // (2 * fan)
    part = norm_self.shape[0]
    pair, half, rank = team(parts)

    qkv_w = gather(self_qkv)
    small = jnp.concatenate([norm_self, norm_cross, norm_ff, rel_table.reshape(-1)])
    small = lax.all_gather(small, "fsdp", axis=0, tiled=False)
    early = by_rows(jnp.stack([self_out, cross_q, *jnp.split(cross_kv.reshape(-1, 2 * width), 2, axis=1)]))
    small, early = lax.optimization_barrier((small, early))
    early = lax.all_gather(early, "fsdp", axis=1, tiled=True)
    both_ids = jnp.concatenate([decoder_ids.reshape(-1), encoder_ids.reshape(-1)])
    both_ids = change_home(jnp.pad(both_ids, (0, 1024 - local - enc_local)).reshape(8, 128))
    inner_t = ff_in.T
    by_kernel = (width // fan) % 128 == 0 and fan % 2 == 0 and (ff_in.shape[0] // parts) % 8 == 0
    (both_ids,) = swap([jnp.broadcast_to(both_ids[None], (parts, 8, 128))], 13)
    home = change_home(layer_in.reshape(rows, width))
    early = by_rows(early)
    gain_first, gain_second, gain_third = (
        small[:, i * part : (i + 1) * part].reshape(width).astype(f32) for i in range(3)
    )
    table = jnp.transpose(small[:, 3 * part :].reshape(-1, buckets, table_own), (1, 0, 2)).reshape(buckets, heads)
    both_ids = both_ids.reshape(parts, 1024)
    ids = both_ids[:, :local].reshape(length)
    enc_ids = both_ids[:, local : local + enc_local].reshape(keys)

    first_seen = counts_below(ids, ids)
    enc_first = counts_below(enc_ids, ids)
    enc_last = counts_below(enc_ids, ids + 1)
    blocks = length // BQ
    bk = BQ
    self_rows = jnp.broadcast_to(first_seen[None], (8, length))
    cross_rows = jnp.concatenate([enc_first[None], enc_last[None], jnp.zeros((6, length), jnp.int32)])
    self_limits = jnp.stack(
        [first_seen[::BQ] // bk, (jnp.arange(blocks, dtype=jnp.int32) + 1) * (BQ // bk)]
    )
    cross_limits = jnp.stack([enc_first[::BQ] // bk, (enc_last[BQ - 1 :: BQ] + bk - 1) // bk])

    first_head = rank * own
    table_mine = lax.dynamic_slice_in_dim(table.astype(f32), first_head, own, 1)
    near = rel_buckets[:REACH]
    onehot = (near[:, None] == jnp.arange(buckets, dtype=jnp.int32)[None, :]).astype(f32)
    bias = jnp.einsum("ln,ng->gl", onehot, table_mine, precision=HIGH)
    ext = jnp.concatenate(
        [jnp.full((own, BQ), MASKED, f32), bias, jnp.zeros((own, BQ), f32)], axis=1
    )

    qkv_w, home, inner_t, ext, self_rows, cross_rows, self_limits, cross_limits = lax.optimization_barrier(
        (qkv_w, home, inner_t, ext, self_rows, cross_rows, self_limits, cross_limits)
    )
    qkv_w = qkv_w.reshape(width, parts, own * 3 * dh)

    stream = home.astype(f32)
    normed_first = norm_apply(stream, gain_first).astype(bf16)
    qkv_tok = jnp.einsum("td,dge->gte", normed_first, qkv_w, preferred_element_type=f32).astype(bf16)
    others = change_home(jnp.concatenate([cotangent.reshape(rows, width), encoder.reshape(-1, width)]))
    grad_low, enc_flat = others[:rows], others[rows:]
    fars = [tuple(far for far in range(fan) if by_kernel and min(far, 3) in some) for some in ((2,), (0, 1), (3,))]
    qkv, *halves = swap([qkv_tok], 17, fars[0], inner_t)
    qkv, cross_out, grad_low = lax.optimization_barrier((qkv, cross_out, grad_low))
    if rows == cross_out.shape[0]:
        mix_cross, grad_group = lax.all_gather(jnp.stack([cross_out, grad_low]), "fsdp", axis=1, tiled=True)
    else:
        mix_cross, grad_group = gather(cross_out), gather(grad_low)
    mix_cross = mix_cross.reshape(parts, own * dh, width)
    qkv = qkv.reshape(length, own * 3 * dh)
    out_self, self_t, self_lse = self_forward(self_limits, self_rows, ext, qkv)
    (self_tok,) = swap([out_self.reshape(parts, local, own * dh)], 11)
    after_self, normed_second, query_tok, pairs_tok = over_weights(
        into_kernel,
        "self_out_to_cross",
        [self_tok, home, gain_second.reshape(1, width), enc_flat],
        early,
        lambda i: i,
        [
            ((rows, width), f32),
            ((rows, width), bf16),
            ((parts, rows, own * dh), bf16),
            ((parts, enc_local, own * 2 * dh), bf16),
        ],
    )
    query_cross, pairs, *halves = swap([query_tok, pairs_tok], 15, fars[1], inner_t, halves)
    query_cross, pairs = query_cross.reshape(length, own * dh), pairs.reshape(keys, own * 2 * dh)
    out_cross, cross_t, cross_lse = cross_forward(cross_limits, cross_rows, query_cross, pairs)
    cross_tok, *halves = swap([out_cross.reshape(parts, local, own * dh)], 16, fars[2], inner_t, halves)
    if not by_kernel:
        halves = spread(jnp.transpose(inner_t.reshape(2, fan, units, -1), (1, 0, 2, 3)))
        halves = [jnp.transpose(halves[:, i], (1, 0, 2)).reshape(units, width) for i in range(2)]
    gate_t, up_t = halves
    after_cross = after_self + jnp.einsum("gtc,gcd->td", cross_tok, mix_cross, preferred_element_type=f32)
    normed_third = norm_apply(after_cross, gain_third).astype(bf16)
    normed_group = gather(normed_third)
    gate = jnp.einsum("td,fd->tf", normed_group, gate_t, preferred_element_type=f32)
    up = jnp.einsum("td,fd->tf", normed_group, up_t, preferred_element_type=f32)
    hidden = gate_mix(gate, up).astype(bf16)

    grad_hidden = jnp.einsum("td,fd->tf", grad_group, ff_out, preferred_element_type=f32)
    _, pull_mix = jax.vjp(gate_mix, gate, up)
    grad_gate, grad_up = (g.astype(bf16) for g in pull_mix(grad_hidden))
    grad_third_in = jnp.dot(grad_gate, gate_t, preferred_element_type=f32) + jnp.dot(
        grad_up, up_t, preferred_element_type=f32
    )
    grad_third_in = scatter(grad_third_in.astype(bf16))
    outer_part = jnp.dot(hidden, ff_out, preferred_element_type=f32).astype(bf16)
    grad_units = [
        jnp.einsum("tf,td->fd", g, y, preferred_element_type=f32).astype(bf16)
        for g, y in ((grad_gate, normed_group), (grad_up, normed_group), (hidden, grad_group))
    ]
    grad_third_in, outer_part, grad_units = lax.optimization_barrier((grad_third_in, outer_part, grad_units))
    if by_kernel:
        grad_units = jnp.stack([g.reshape(parts, units // parts, width) for g in grad_units], axis=1)
        part_units = grad_units.reshape(3 * units, width)
    grad_third_in = grad_third_in.astype(f32)
    grad_from_third, grad_gain_third = norm_back(after_cross, gain_third, grad_third_in)
    grad_middle = grad_low.astype(f32) + grad_from_third
    middle_low = grad_middle.astype(bf16)
    grad_mix_cross = jnp.einsum("gtc,td->gcd", cross_tok, middle_low, preferred_element_type=f32)
    part_cross = scatter(grad_mix_cross.reshape(width, width).astype(bf16))
    grad_cross_tok = jnp.einsum("td,gcd->gtc", middle_low, mix_cross, preferred_element_type=f32).astype(bf16)
    (grad_cross,) = swap([grad_cross_tok], 11)
    grad_cross = grad_cross.reshape(length, own * dh)
    grad_query, grad_pairs = cross_backward(
        cross_limits, cross_rows, query_cross, pairs, grad_cross, cross_t, cross_lse
    )
    grad_query_tok, grad_pairs_tok = swap(
        [grad_query.reshape(parts, local, own * dh), grad_pairs.reshape(parts, enc_local, own * 2 * dh)], 12
    )
    (
        grad_upper, upper_low, grad_self_tok, grad_gain_second, grad_encoder, grad_query_tok, grad_pairs_tok
    ) = over_weights(
        outof_kernel,
        "cross_to_self_out",
        [grad_query_tok, grad_pairs_tok, after_self, gain_second.reshape(1, width), grad_middle],
        early,
        lambda i: jnp.where(i < 2, 1 - i, i),
        [
            ((rows, width), f32),
            ((rows, width), bf16),
            ((parts, rows, own * dh), bf16),
            ((1, width), f32),
            ((enc_local, width), bf16),
            ((rows, width), bf16),
            ((enc_local, 2 * width), bf16),
        ],
        [((enc_local, width), f32)],
    )
    grad_query_w = jnp.einsum("td,te->de", normed_second, grad_query_tok, preferred_element_type=f32)
    grad_pairs_w = jnp.einsum("td,te->de", enc_flat, grad_pairs_tok, preferred_element_type=f32)
    grad_mix_self = jnp.einsum("gtc,td->gcd", self_tok, upper_low, preferred_element_type=f32)
    grad_mid = jnp.concatenate(
        [
            grad_query_w.astype(bf16),
            grad_pairs_w.astype(bf16),
            grad_mix_self.reshape(width, width).astype(bf16),
        ],
        axis=1,
    )
    grad_self_tok, grad_mid = lax.optimization_barrier((grad_self_tok, grad_mid))
    part_mid = scatter(grad_mid)
    (grad_self,) = swap([grad_self_tok], 11)
    grad_self = grad_self.reshape(length, own * dh)
    grad_qkv, diagonals = self_backward(self_limits, self_rows, ext, qkv, grad_self, self_t, self_lse)
    (grad_qkv_tok,) = swap([grad_qkv.reshape(parts, local, own * 3 * dh)], 10)
    grad_qkv_tok = flat(grad_qkv_tok)
    grad_qkv_w = jnp.einsum("td,te->de", normed_first, grad_qkv_tok, preferred_element_type=f32)
    grad_first_in = jnp.einsum("te,de->td", grad_qkv_tok, qkv_w.reshape(width, -1), preferred_element_type=f32)
    grad_from_first, grad_gain_first = norm_back(stream, gain_first, grad_first_in)
    grad_layer_in = (grad_upper + grad_from_first).astype(bf16)
    if not by_kernel:
        part_units = grad_units
    bucket_line = jnp.concatenate([jnp.full((BQ - 1,), -1, jnp.int32), near, jnp.full((BQ + 1,), -1, jnp.int32)])
    in_bucket = (bucket_line[:, None] == jnp.arange(buckets, dtype=jnp.int32)).astype(f32)
    by_bucket = jnp.einsum("xn,gx->ng", in_bucket, diagonals, precision=HIGH)
    grad_table = lax.dynamic_update_slice_in_dim(jnp.zeros((buckets, heads), f32), by_bucket, first_head, 1)

    gains = jnp.concatenate(
        [g.reshape(-1, part) for g in (grad_gain_first, grad_gain_second, grad_gain_third)], axis=1
    )
    tables = jnp.transpose(grad_table.reshape(buckets, -1, table_own), (1, 0, 2)).reshape(-1, buckets * table_own)
    small_grads = jnp.concatenate([gains, tables], axis=1).astype(bf16)
    small_size = small_grads.shape[1]
    going_home = jnp.concatenate([grad_layer_in, grad_encoder.astype(bf16)])
    going_home, small_grads, grad_qkv_w, part_units, part_cross, part_mid = lax.optimization_barrier(
        (change_home(going_home), small_grads, grad_qkv_w.astype(bf16), part_units, part_cross, part_mid)
    )
    part_last = scatter(grad_qkv_w)
    if by_kernel:
        few = jnp.pad(small_grads[:, None], ((0, 0), (0, 7), (0, 1024 - small_size))).reshape(fan * 8, 1024)
        total_inner, total_outer, outer_sum, few = units_total(part_units, outer_part, few, 0)
        few = jnp.pad(few[0].astype(bf16).reshape(8, 128), ((0, parts * 8 - 8), (0, 0)))
        total_cross, total_mid, total_qkv, small_total, total_inner = ring_total(
            [part_cross, part_mid, part_last, few], (2, 2, 2, 1), 1, total_inner
        )
    else:
        grad_units = [lax.psum(g, "seq") for g in part_units]
        total_inner = spread(jnp.transpose(jnp.stack(grad_units[:2]).reshape(2, units, fan, -1), (2, 0, 1, 3)))
        total_inner = jnp.transpose(total_inner, (3, 1, 0, 2)).reshape(-1, 2 * fan * units).astype(f32)
        total_outer, outer_sum = grad_units[2], scatter(outer_part).astype(f32)
        few = lax.dynamic_index_in_dim(lax.psum(small_grads, "fsdp"), lax.axis_index("fsdp"), 0, False)
        total_cross, total_mid, total_qkv, small_total = (
            lax.psum(v, "seq") for v in (part_cross, part_mid, part_last, few)
        )
    layer_out = (after_cross + outer_sum).astype(bf16)
    layer_out, total_inner, total_outer, total_cross, total_mid, total_qkv, going_home = lax.optimization_barrier(
        (layer_out, total_inner, total_outer, total_cross, total_mid, total_qkv, going_home)
    )
    layer_out = change_home(layer_out).reshape(seqs, local, width)
    grad_layer_in = going_home[:rows].astype(f32).reshape(seqs, local, width)
    grad_encoder = going_home[rows:].astype(f32).reshape(seqs, enc_local, width)
    total_outer, total_mid, total_qkv = (v.astype(f32) for v in (total_outer, total_mid, total_qkv))
    total_query, total_mix_cross = total_mid[:, :width], total_cross.astype(f32)
    total_pairs = total_mid[:, width : 3 * width].reshape(-1, heads, 2 * dh)
    total_mix_self, total_qkv = total_mid[:, 3 * width :], total_qkv.reshape(-1, heads, 3 * dh)
    mine = small_total.reshape(-1)[:small_size].astype(f32)
    total_gain_first, total_gain_second, total_gain_third = (mine[i * part : (i + 1) * part] for i in range(3))
    total_table = mine[3 * part :].reshape(buckets, table_own)
    return (
        layer_out, grad_layer_in, grad_encoder, total_gain_first, total_qkv, total_mix_self, total_table,
        total_gain_second, total_query, total_pairs, total_mix_cross, total_gain_third, total_inner, total_outer,
    )


def solution(mesh):
    in_specs = (
        P("fsdp", "seq", None), P("fsdp", "seq", None), P("fsdp", "seq"), P("fsdp", "seq"), P(),
        P("fsdp"), P("fsdp", None, None), P("fsdp", None), P(None, "fsdp"), P("fsdp"), P("fsdp", None),
        P("fsdp", None, None), P("fsdp", None), P("fsdp"), P("fsdp", None), P("fsdp", None),
        P("fsdp", "seq", None),
    )
    out_specs = (
        P("fsdp", "seq", None), P("fsdp", "seq", None), P("fsdp", "seq", None), P("fsdp"), P("fsdp", None, None),
        P("fsdp", None), P(None, "fsdp"), P("fsdp"), P("fsdp", None), P("fsdp", None, None), P("fsdp", None),
        P("fsdp"), P("fsdp", None), P("fsdp", None),
    )
    return jax.shard_map(shards, mesh=mesh, in_specs=in_specs, out_specs=out_specs, check_vma=False)
```

```python
import functools

import jax
import jax.numpy as jnp
from jax import lax
from jax.experimental import pallas as pl
from jax.experimental.layout import Layout, with_layout_constraint
from jax.experimental.pallas import tpu as pltpu
from jax.sharding import PartitionSpec as P

EPS = 1e-06
HIGH = lax.Precision.HIGHEST
MASKED = -1e30
DOCS = 4

BQ = 256
REACH = 1024


def blk(index, size):
    return pl.ds(pl.multiple_of(index * size, size), size)


def turn(value):
    return jnp.transpose(value.astype(jnp.float32), (1, 0))


def bias_tiles(ext_ref, tile_ref, own):
    for h in range(own):
        line = jnp.broadcast_to(ext_ref[h : h + 1, :], tile_ref.shape[1:])
        tile_ref[h] = pltpu.roll(line, 0, 1, stride=1, stride_axis=0)


def unpack(ref, own, width, picks, flips, base):
    block = 256

    def one(b, _):
        rows = blk(b, block)
        value = ref[rows, :]
        if flips:
            flat = turn(value).astype(jnp.bfloat16)
            for target, piece in flips:
                for h in range(own):
                    at = h * width + piece * 64
                    target[base + h, :, rows] = flat[at : at + 64]
        for target, piece in picks:
            for h in range(own):
                at = h * width + piece * 64
                target[base + h, rows, :] = value[:, at : at + 64]
        return 0

    lax.fori_loop(0, ref.shape[0] // block, one, 0)


def dot(a, b):
    return jnp.dot(a, b, preferred_element_type=jnp.float32)


def score(own_index, key_tile, query_t, tile_ref, t, low, high, first_key):
    value = dot(key_tile, query_t)
    place = lax.broadcasted_iota(jnp.int32, value.shape, 0)
    keep = place >= low - first_key
    if high is not None:
        keep = keep & (place < high - first_key)
    else:
        value = value + tile_ref[own_index, :, blk(t + 1, BQ)]
    return jnp.where(keep, value, MASKED)


def forward_body(own, bk, causal, lim_ref, rows_ref, q_t, k_rows, v_t, tile_ref, o_ref, ot_ref, lse_ref):
    length = o_ref.shape[0]

    def q_block(i, _):
        cols = blk(i, BQ)
        queries = [q_t[h, :, cols] for h in range(own)]
        low = rows_ref[0:1, cols]
        high = None if causal else rows_ref[1:2, cols]

        def k_block(j, carry):
            keys = blk(j, bk)
            t = i - j
            out = []
            for h in range(own):
                top, total, acc = carry[h]
                s = score(h, k_rows[h, keys, :], queries[h], tile_ref, t, low, high, j * bk)
                new_top = jnp.maximum(top, jnp.max(s, axis=0, keepdims=True))
                p = jnp.exp(s - new_top)
                scale = jnp.exp(top - new_top)
                total = total * scale + jnp.sum(p, axis=0, keepdims=True)
                acc = acc * scale + dot(v_t[h, :, keys], p.astype(jnp.bfloat16))
                out.append((new_top, total, acc))
            return tuple(out)

        start = tuple(
            (
                jnp.full((1, BQ), MASKED, jnp.float32),
                jnp.zeros((1, BQ), jnp.float32),
                jnp.zeros((64, BQ), jnp.float32),
            )
            for _ in range(own)
        )
        ends = lax.fori_loop(lim_ref[0, i], lim_ref[1, i], k_block, start)
        for h in range(own):
            top, total, acc = ends[h]
            ot_ref[h * 64 : h * 64 + 64, cols] = acc / total
            lse_ref[h : h + 1, cols] = top + jnp.log(total)
        o_ref[cols, :] = turn(ot_ref[:, cols]).astype(jnp.bfloat16)
        return 0

    lax.fori_loop(0, length // BQ, q_block, 0)


def self_forward_kernel(own, bk, lim_ref, rows_ref, ext_ref, x_ref, o_ref, ot_ref, lse_ref, q_t, k_rows, v_t, tile_ref):
    bias_tiles(ext_ref, tile_ref, own)
    unpack(x_ref, own, 192, [(k_rows, 1)], [(q_t, 0), (v_t, 2)], 0)
    forward_body(own, bk, True, lim_ref, rows_ref, q_t, k_rows, v_t, tile_ref, o_ref, ot_ref, lse_ref)


def cross_forward_kernel(own, bk, lim_ref, rows_ref, q_ref, kv_ref, o_ref, ot_ref, lse_ref, q_t, k_rows, v_t):
    unpack(q_ref, own, 64, [], [(q_t, 0)], 0)
    unpack(kv_ref, own, 128, [(k_rows, 0)], [(v_t, 1)], 0)
    forward_body(own, bk, False, lim_ref, rows_ref, q_t, k_rows, v_t, None, o_ref, ot_ref, lse_ref)


def backward_body(
    own, bk, causal, lim_ref, rows_ref, do_ref, ot_ref, lse_ref,
    q_t, q_rows, k_t, k_rows, v_rows, do_t, do_rows, tile_ref, sum_ref, dq_t, dk, dv,
):
    length = do_ref.shape[0]
    dk[...] = jnp.zeros_like(dk)
    dv[...] = jnp.zeros_like(dv)
    if causal:
        sum_ref[...] = jnp.zeros_like(sum_ref)

    def q_block(i, _):
        cols = blk(i, BQ)
        low = rows_ref[0:1, cols]
        high = None if causal else rows_ref[1:2, cols]
        per_head = []
        for h in range(own):
            grad_t = do_t[h, :, cols]
            delta = jnp.sum(
                grad_t.astype(jnp.float32) * ot_ref[h * 64 : h * 64 + 64, cols], axis=0, keepdims=True
            )
            per_head.append((q_t[h, :, cols], grad_t, delta, lse_ref[h : h + 1, cols]))

        def k_block(j, carry):
            keys = blk(j, bk)
            t = i - j
            out = []
            for h in range(own):
                query_t, grad_t, delta, lse = per_head[h]
                s = score(h, k_rows[h, keys, :], query_t, tile_ref, t, low, high, j * bk)
                p = jnp.exp(s - lse)
                dp = dot(v_rows[h, keys, :], grad_t)
                ds = (p * (dp - delta)).astype(jnp.bfloat16)
                dv[h, keys, :] += dot(p.astype(jnp.bfloat16), do_rows[h, cols, :])
                dk[h, keys, :] += dot(ds, q_rows[h, cols, :])
                if causal:
                    sum_ref[h, :, blk(t, BQ)] += ds.astype(jnp.float32)
                out.append(carry[h] + dot(k_t[h, :, keys], ds))
            return tuple(out)

        ends = lax.fori_loop(
            lim_ref[0, i],
            lim_ref[1, i],
            k_block,
            tuple(jnp.zeros((64, BQ), jnp.float32) for _ in range(own)),
        )
        for h in range(own):
            dq_t[h * 64 : h * 64 + 64, cols] = ends[h]
        return 0

    lax.fori_loop(0, length // BQ, q_block, 0)


def diagonal_sums(sum_ref, u_ref, own):
    flip = lax.broadcasted_iota(jnp.int32, (BQ, BQ), 0) + lax.broadcasted_iota(jnp.int32, (BQ, BQ), 1) == BQ - 1
    flip = jnp.where(flip, 1.0, 0.0).astype(jnp.bfloat16)
    for h in range(own):
        grid = sum_ref[h]
        high = grid.astype(jnp.bfloat16)
        low = (grid - high.astype(jnp.float32)).astype(jnp.bfloat16)
        upside = dot(flip, high) + dot(flip, low)
        wide = jnp.concatenate([upside, jnp.zeros((BQ, BQ), jnp.float32)], axis=1)
        aligned = pltpu.roll(wide, 0, 1, stride=1, stride_axis=0)
        u_ref[h : h + 1, :] = jnp.sum(aligned, axis=0, keepdims=True)


def self_backward_kernel(
    own, bk, lim_ref, rows_ref, ext_ref, x_ref, do_ref, ot_ref, lse_ref, dx_ref, u_ref,
    q_t, q_rows, k_t, k_rows, v_rows, do_t, do_rows, tile_ref, sum_ref, dq_t, dk, dv,
):
    bias_tiles(ext_ref, tile_ref, own)
    unpack(x_ref, own, 192, [(q_rows, 0), (k_rows, 1), (v_rows, 2)], [(q_t, 0), (k_t, 1)], 0)
    unpack(do_ref, own, 64, [(do_rows, 0)], [(do_t, 0)], 0)
    backward_body(
        own, bk, True, lim_ref, rows_ref, do_ref, ot_ref, lse_ref,
        q_t, q_rows, k_t, k_rows, v_rows, do_t, do_rows, tile_ref, sum_ref, dq_t, dk, dv,
    )
    diagonal_sums(sum_ref, u_ref, own)

    def pack(b, _):
        rows = blk(b, 256)
        dq = turn(dq_t[:, rows])
        pieces = []
        for h in range(own):
            pieces += [dq[:, h * 64 : h * 64 + 64], dk[h, rows, :], dv[h, rows, :]]
        dx_ref[rows, :] = jnp.concatenate(pieces, axis=1).astype(jnp.bfloat16)
        return 0

    lax.fori_loop(0, x_ref.shape[0] // 256, pack, 0)


def cross_backward_kernel(
    own, bk, lim_ref, rows_ref, q_ref, kv_ref, do_ref, ot_ref, lse_ref, dq_ref, dkv_ref,
    q_t, q_rows, k_t, k_rows, v_rows, do_t, do_rows, dq_t, dk, dv,
):
    unpack(q_ref, own, 64, [(q_rows, 0)], [(q_t, 0)], 0)
    unpack(kv_ref, own, 128, [(k_rows, 0), (v_rows, 1)], [(k_t, 0)], 0)
    unpack(do_ref, own, 64, [(do_rows, 0)], [(do_t, 0)], 0)
    backward_body(
        own, bk, False, lim_ref, rows_ref, do_ref, ot_ref, lse_ref,
        q_t, q_rows, k_t, k_rows, v_rows, do_t, do_rows, None, None, dq_t, dk, dv,
    )

    def pack_q(b, _):
        rows = blk(b, 256)
        dq_ref[rows, :] = turn(dq_t[:, rows]).astype(jnp.bfloat16)
        return 0

    def pack_kv(b, _):
        rows = blk(b, 256)
        pieces = []
        for h in range(own):
            pieces += [dk[h, rows, :], dv[h, rows, :]]
        dkv_ref[rows, :] = jnp.concatenate(pieces, axis=1).astype(jnp.bfloat16)
        return 0

    lax.fori_loop(0, q_ref.shape[0] // 256, pack_q, 0)
    lax.fori_loop(0, kv_ref.shape[0] // 256, pack_kv, 0)


SMEM = pl.BlockSpec(memory_space=pltpu.SMEM)
VMEM = pl.BlockSpec(memory_space=pltpu.VMEM)
bf16, f32 = jnp.bfloat16, jnp.float32


def call(body, name, operands, outs, scratch, flops):
    size = sum(v.size * v.dtype.itemsize for v in operands)
    return pl.pallas_call(
        body,
        name=name,
        out_shape=[jax.ShapeDtypeStruct(s, d) for s, d in outs],
        in_specs=[SMEM] + [VMEM] * (len(operands) - 1),
        out_specs=[VMEM] * len(outs),
        scratch_shapes=[pltpu.VMEM(s, d) for s, d in scratch],
        compiler_params=pltpu.CompilerParams(vmem_limit_bytes=40 << 20),
        cost_estimate=pl.CostEstimate(flops=0, bytes_accessed=size, transcendentals=0),
    )(*operands)


def self_forward(limits, rows, ext, x, bk=BQ):
    length, own = x.shape[0], x.shape[1] // 192
    return call(
        functools.partial(self_forward_kernel, own, bk),
        "self_forward",
        [limits, rows, ext, x],
        [((length, own * 64), bf16), ((own * 64, length), f32), ((own, length), f32)],
        [
            ((own, 64, length), bf16),
            ((own, length, 64), bf16),
            ((own, 64, length), bf16),
            ((own, BQ, REACH + 2 * BQ), f32),
        ],
        length * length * own * 64,
    )


def cross_forward(limits, rows, q, kv, bk=BQ):
    length, own, keys = q.shape[0], q.shape[1] // 64, kv.shape[0]
    return call(
        functools.partial(cross_forward_kernel, own, bk),
        "cross_forward",
        [limits, rows, q, kv],
        [((length, own * 64), bf16), ((own * 64, length), f32), ((own, length), f32)],
        [((own, 64, length), bf16), ((own, keys, 64), bf16), ((own, 64, keys), bf16)],
        length * keys * own * 128,
    )


def self_backward(limits, rows, ext, x, grad, o_t, lse, bk=BQ):
    length, own = x.shape[0], x.shape[1] // 192
    return call(
        functools.partial(self_backward_kernel, own, bk),
        "self_backward",
        [limits, rows, ext, x, grad, o_t, lse],
        [((length, own * 192), bf16), ((own, REACH + 2 * BQ), f32)],
        [
            ((own, 64, length), bf16),
            ((own, length, 64), bf16),
            ((own, 64, length), bf16),
            ((own, length, 64), bf16),
            ((own, length, 64), bf16),
            ((own, 64, length), bf16),
            ((own, length, 64), bf16),
            ((own, BQ, REACH + 2 * BQ), f32),
            ((own, BQ, REACH + BQ), f32),
            ((own * 64, length), f32),
            ((own, length, 64), f32),
            ((own, length, 64), f32),
        ],
        length * length * own * 160,
    )


def cross_backward(limits, rows, q, kv, grad, o_t, lse, bk=BQ):
    length, own, keys = q.shape[0], q.shape[1] // 64, kv.shape[0]
    return call(
        functools.partial(cross_backward_kernel, own, bk),
        "cross_backward",
        [limits, rows, q, kv, grad, o_t, lse],
        [((length, own * 64), bf16), ((keys, own * 128), bf16)],
        [
            ((own, 64, length), bf16),
            ((own, length, 64), bf16),
            ((own, 64, keys), bf16),
            ((own, keys, 64), bf16),
            ((own, keys, 64), bf16),
            ((own, 64, length), bf16),
            ((own, length, 64), bf16),
            ((own * 64, length), f32),
            ((own, keys, 64), f32),
            ((own, keys, 64), f32),
        ],
        length * keys * own * 320,
    )


def rows_of(blocks_ref):
    return jnp.concatenate([blocks_ref[g] for g in range(blocks_ref.shape[0])], axis=1)


def against(a, b):
    return lax.dot_general(a, b, (((1,), (1,)), ((), ())), preferred_element_type=jnp.float32)


def into_kernel(tok_ref, home_ref, gain_ref, enc_ref, w_ref, after_ref, norm_ref, query_ref, pairs_ref):
    which = pl.program_id(0)

    @pl.when(which == 0)
    def _():
        value = home_ref[...].astype(jnp.float32) + dot(rows_of(tok_ref), w_ref[0])
        after_ref[...] = value
        scale = lax.rsqrt(jnp.mean(value * value, axis=1, keepdims=True) + EPS)
        norm_ref[...] = (value * scale * gain_ref[...]).astype(jnp.bfloat16)

    @pl.when(which == 1)
    def _():
        query = dot(norm_ref[...], w_ref[0]).astype(jnp.bfloat16)
        cols = query_ref.shape[2]
        for g in range(query_ref.shape[0]):
            query_ref[g] = query[:, g * cols : (g + 1) * cols]

    for half in range(2):

        @pl.when(which == 2 + half)
        def _():
            pairs = dot(enc_ref[...], w_ref[0]).astype(jnp.bfloat16)
            groups, cols = pairs_ref.shape[0] // 2, pairs_ref.shape[2]
            for g in range(groups):
                pairs_ref[half * groups + g] = pairs[:, g * cols : (g + 1) * cols]


def outof_kernel(
    dq_ref, dkv_ref, after_ref, gain_ref, middle_ref, w_ref,
    upper_ref, low_ref, out_ref, gain_grad_ref, enc_grad_ref, dq_flat_ref, dkv_flat_ref, enc_sum,
):
    which = pl.program_id(0)

    @pl.when(which == 0)
    def _():
        grad_query = rows_of(dq_ref)
        dq_flat_ref[...] = grad_query
        dkv_flat_ref[...] = rows_of(dkv_ref)
        grad = against(grad_query, w_ref[0])
        value = after_ref[...]
        unit = value * lax.rsqrt(jnp.mean(value * value, axis=1, keepdims=True) + EPS)
        gain_grad_ref[...] = jnp.sum(grad * unit, axis=0, keepdims=True)
        scale = lax.rsqrt(jnp.mean(value * value, axis=1, keepdims=True) + EPS)
        grad = grad * gain_ref[...]
        inner = jnp.mean(grad * unit, axis=1, keepdims=True)
        upper = middle_ref[...] + scale * (grad - unit * inner)
        upper_ref[...] = upper
        low_ref[...] = upper.astype(jnp.bfloat16)

    @pl.when(which == 1)
    def _():
        grad = against(low_ref[...], w_ref[0]).astype(jnp.bfloat16)
        cols = out_ref.shape[2]
        for g in range(out_ref.shape[0]):
            out_ref[g] = grad[:, g * cols : (g + 1) * cols]

    width = w_ref.shape[1]

    @pl.when(which == 2)
    def _():
        enc_sum[...] = against(dkv_flat_ref[:, :width], w_ref[0])

    @pl.when(which == 3)
    def _():
        enc_grad_ref[...] = (enc_sum[...] + against(dkv_flat_ref[:, width:], w_ref[0])).astype(jnp.bfloat16)


def over_weights(body, name, arrays, weights, order, outs, scratch=()):
    count, rows, cols = weights.shape
    whole = lambda shape: pl.BlockSpec(shape, lambda i: (0,) * len(shape))
    return pl.pallas_call(
        body,
        name=name,
        grid=(count,),
        out_shape=[jax.ShapeDtypeStruct(s, d) for s, d in outs],
        in_specs=[whole(v.shape) for v in arrays] + [pl.BlockSpec((1, rows, cols), lambda i: (order(i), 0, 0))],
        out_specs=[whole(s) for s, _ in outs],
        scratch_shapes=[pltpu.VMEM(s, d) for s, d in scratch],
        compiler_params=pltpu.CompilerParams(vmem_limit_bytes=40 << 20, dimension_semantics=("arbitrary",)),
        cost_estimate=pl.CostEstimate(flops=0, bytes_accessed=weights.size * 2, transcendentals=0),
    )(*arrays, weights)


MESH = pl.DeviceIdType.MESH


def ring_place(index, n):
    z, x = index // 2, index % 2
    return z + x * (n - 1 - 2 * z)


def ring_index(place, n):
    x = place // (n // 2)
    z = place + x * (n - 1 - 2 * place)
    return 2 * z + x


def ring_greet(n, others):
    place = ring_place(lax.axis_index("seq"), n)
    right = ring_index((place + 1) % n, n)
    left = ring_index((place + n - 1) % n, n)
    barrier = pltpu.get_barrier_semaphore()
    for neighbour in (left, right):
        pl.semaphore_signal(barrier, inc=1, device_id={"seq": neighbour}, device_id_type=MESH)
    for other in others:
        pl.semaphore_signal(barrier, inc=1, device_id={"fsdp": other}, device_id_type=MESH)
    pl.semaphore_wait(barrier, 2 + len(others))
    return place, right, left


def ring_cut(shape, split, n):
    rows, cols = shape[0] // n, shape[1]
    return (rows, cols // split) if split > 0 else (rows // -split, cols)


def ring_window(ref, shape, split, n, piece, chunk):
    whole = shape[0] // n
    rows, cols = ring_cut(shape, split, n)
    if split > 0:
        return ref.at[pl.ds(chunk * whole, rows), pl.ds(piece * cols, cols)]
    return ref.at[pl.ds(chunk * whole + piece * rows, rows), :]


def ring_kernel(n, splits, fan, *refs):
    count = len(splits)
    more = 1 if fan else 0
    x_refs, y_refs = refs[:count], refs[count + more : 2 * count + more]
    slots = refs[2 * (count + more) : 3 * count + 2 * more]
    send_sem, recv_sem = refs[3 * count + 2 * more :]
    place, right, left = ring_greet(n, [])
    streams = [(k, piece, piece % 2) for k in range(count) for piece in range(abs(splits[k]))]

    def window(ref, k, piece, chunk):
        return ring_window(ref, x_refs[k].shape, splits[k], n, piece, chunk)

    def chunk_at(down, step):
        return (place + 1 + step) % n if down else (place + 2 * n - 1 - step) % n

    copies = {}

    def start(number, step, src, dst, down):
        copies[number, step] = pltpu.make_async_remote_copy(
            src_ref=src,
            dst_ref=dst,
            send_sem=send_sem.at[number, step],
            recv_sem=recv_sem.at[number, step],
            device_id={"seq": left if down else right},
            device_id_type=MESH,
        )
        copies[number, step].start()

    def turn_block(number):
        inner_ref, turned_ref = refs[count], refs[2 * count + 1]
        rows = inner_ref.shape[0] // (2 * fan * n)
        half, first = number // (fan // 2), number % (fan // 2) * 2
        tall = jnp.concatenate(
            [
                inner_ref[pl.ds(((chunk * fan + group) * 2 + half) * rows, rows), :].astype(jnp.float32)
                for group in (first, first + 1)
                for chunk in range(n)
            ]
        )
        wide = 2 * n * rows
        turned_ref[:, number * wide : (number + 1) * wide] = jnp.transpose(tall, (1, 0))

    for number, (k, piece, down) in enumerate(streams):
        start(number, 0, window(x_refs[k], k, piece, place), window(slots[k], k, piece, 0), down)
    for step in range(n - 1):
        if step < fan:
            turn_block(step)
        for number, (k, piece, down) in enumerate(streams):
            copies[number, step].wait_recv()
            chunk = chunk_at(down, step)
            mine = window(x_refs[k], k, piece, chunk)
            landed = window(slots[k], k, piece, step)
            total = landed[...].astype(jnp.float32) + mine[...].astype(jnp.float32)
            if step < n - 2:
                landed[...] = total.astype(jnp.bfloat16)
                start(number, step + 1, landed, window(slots[k], k, piece, step + 1), down)
            else:
                done = window(y_refs[k], k, piece, chunk)
                done[...] = total.astype(jnp.bfloat16)
                start(number, n - 1, done, done, down)
    for step in range(n - 1):
        for number, (k, piece, down) in enumerate(streams):
            copies[number, n - 1 + step].wait_recv()
            if step < n - 2:
                done = window(y_refs[k], k, piece, chunk_at(down, n - 1 + step))
                start(number, n + step, done, done, down)
    for one in copies.values():
        one.wait_send()


def ring_call(body, name, arrays, outs, scratch, ident):
    size = sum(v.size * 2 for v in arrays)
    return pl.pallas_call(
        body,
        name=name,
        out_shape=[jax.ShapeDtypeStruct(s, d) for s, d in outs],
        in_specs=[pl.BlockSpec(memory_space=pltpu.VMEM)] * len(arrays),
        out_specs=[pl.BlockSpec(memory_space=pltpu.VMEM)] * len(outs),
        scratch_shapes=scratch,
        compiler_params=pltpu.CompilerParams(
            collective_id=ident, has_side_effects=True, vmem_limit_bytes=48 << 20
        ),
        cost_estimate=pl.CostEstimate(flops=0, bytes_accessed=60 * size, transcendentals=0),
    )(*arrays)


def ring_total(arrays, splits, ident, inner=None):
    n, fan = lax.axis_size("seq"), lax.axis_size("fsdp")
    streams = sum(abs(s) for s in splits)
    more = [] if inner is None else [inner]
    return ring_call(
        functools.partial(ring_kernel, n, splits, 0 if inner is None else fan),
        "ring_total",
        arrays + more,
        [(v.shape, jnp.bfloat16) for v in arrays] + [(v.shape[::-1], jnp.float32) for v in more],
        [pltpu.VMEM((v.shape[0] // n * (n - 1), v.shape[1]), jnp.bfloat16) for v in arrays]
        + [pltpu.SemaphoreType.DMA((streams, 2 * n - 2))] * 2,
        ident,
    )


def units_kernel(
    n, fan, x_ref, part_ref, few_ref, inner_ref, outer_ref, sum_ref, few_sum_ref, slots, acc, landed, few_landed,
    down_send, down_recv, swap_send, swap_recv, own_sem, send_sem, recv_sem, part_send, part_recv,
):
    s, me = lax.axis_index("seq"), lax.axis_index("fsdp")
    rows, width = acc.shape[0] // 3, x_ref.shape[1]
    cols = width // fan
    block = 2 * fan * rows
    place, right, left = ring_greet(n, [(me + far) % fan for far in range(1, fan)])
    sums = {}

    def piece_of(ref, at, piece):
        return ref.at[pl.ds(at * 3 * rows, 3 * rows), pl.ds(piece * cols, cols)]

    def send_sum(piece, step, src):
        to = left if piece >= fan // 2 else right
        sums[piece, step] = pltpu.make_async_remote_copy(
            src_ref=src,
            dst_ref=piece_of(slots, step, piece),
            send_sem=down_send.at[piece, step],
            recv_sem=down_recv.at[piece, step],
            device_id={"seq": to},
            device_id_type=MESH,
        )
        sums[piece, step].start()

    def chunk(piece, step):
        return ring_index((place + 1 + step) % n if piece >= fan // 2 else (place + 2 * n - 1 - step) % n, n)

    for piece in range(fan):
        send_sum(piece, 0, piece_of(x_ref, chunk(piece, 0), piece))
    for step in range(n - 1):
        for piece in range(fan):
            sums[piece, step].wait_recv()
            arrived = piece_of(slots, step, piece)
            mine = piece_of(x_ref, chunk(piece, step + 1), piece)
            total = (arrived[...].astype(jnp.float32) + mine[...].astype(jnp.float32)).astype(jnp.bfloat16)
            if step < n - 2:
                arrived[...] = total
                send_sum(piece, step + 1, arrived)
            else:
                acc[:, piece * cols : (piece + 1) * cols] = total
    moves = []
    for far in range(fan):
        target = (me + far) % fan
        for half in range(2):
            src = acc.at[pl.ds(half * rows, rows), pl.ds(pl.multiple_of(target * cols, 128), cols)]
            dst = inner_ref.at[pl.ds(s * block + (me * 2 + half) * rows, rows), :]
            if far:
                one = pltpu.make_async_remote_copy(
                    src_ref=src,
                    dst_ref=dst,
                    send_sem=swap_send.at[far, half],
                    recv_sem=swap_recv.at[far, half],
                    device_id={"fsdp": target},
                    device_id_type=MESH,
                )
            else:
                one = pltpu.make_async_copy(src, dst, own_sem.at[half])
            one.start()
            moves.append(one)
    mine = pltpu.make_async_copy(
        acc.at[pl.ds(2 * rows, rows), :], outer_ref.at[pl.ds(s * rows, rows), :], own_sem.at[2]
    )
    mine.start()
    copies = {}
    outs = ((outer_ref, (n * rows, width), 2), (inner_ref, (n * block, cols), -2))

    def start(k, piece, step):
        ref, shape, split = outs[k]
        chunk = ring_index((place + step) % n if piece else (place + n - step) % n, n)
        view = ring_window(ref, shape, split, n, piece, chunk)
        copies[k, piece, step] = pltpu.make_async_remote_copy(
            src_ref=view,
            dst_ref=view,
            send_sem=send_sem.at[2 * k + piece, step],
            recv_sem=recv_sem.at[2 * k + piece, step],
            device_id={"seq": left if piece else right},
            device_id_type=MESH,
        )
        copies[k, piece, step].start()

    def forward(k, step):
        for piece in range(2):
            copies[k, piece, step].wait_recv()
            if step < n - 2:
                start(k, piece, step + 1)

    mine.wait()
    start(0, 0, 0)
    start(0, 1, 0)
    lead = (n - 1) // 2
    for step in range(lead):
        forward(0, step)
    for one in moves:
        one.wait()
    parts = []
    for far in range(1, fan):
        target = (me + far) % fan
        for which, (src, into) in enumerate(((part_ref, landed), (few_ref, few_landed))):
            rest = src.shape[0] // fan
            one = pltpu.make_async_remote_copy(
                src_ref=src.at[pl.ds(target * rest, rest), :],
                dst_ref=into.at[far],
                send_sem=part_send.at[which, far],
                recv_sem=part_recv.at[which, far],
                device_id={"fsdp": target},
                device_id_type=MESH,
            )
            one.start()
            parts.append(one)
    start(1, 0, 0)
    start(1, 1, 0)
    for step in range(n - 1):
        forward(1, step)
        if lead + step < n - 1:
            forward(0, lead + step)
    for one in parts:
        one.wait()
    for src, into, out in ((part_ref, landed, sum_ref), (few_ref, few_landed, few_sum_ref)):
        rest = src.shape[0] // fan
        total = src[pl.ds(pl.multiple_of(me * rest, rest), rest), :].astype(jnp.float32)
        for far in range(1, fan):
            total = total + into[far].astype(jnp.float32)
        out[...] = total
    for one in [*copies.values(), *sums.values()]:
        one.wait_send()


def units_total(grads, part, few, ident):
    n, fan = lax.axis_size("seq"), lax.axis_size("fsdp")
    rows, width = grads.shape[0] // (3 * n), grads.shape[1]
    tokens = part.shape[0] // fan
    sems = lambda *shape: pltpu.SemaphoreType.DMA(shape)
    return ring_call(
        functools.partial(units_kernel, n, fan),
        "units_total",
        [grads, part, few],
        [
            ((n * 2 * fan * rows, width // fan), jnp.bfloat16),
            ((n * rows, width), jnp.bfloat16),
            ((tokens, part.shape[1]), jnp.float32),
            ((few.shape[0] // fan, few.shape[1]), jnp.float32),
        ],
        [
            pltpu.VMEM(((n - 1) * 3 * rows, width), jnp.bfloat16),
            pltpu.VMEM((3 * rows, width), jnp.bfloat16),
            pltpu.VMEM((fan, tokens, part.shape[1]), jnp.bfloat16),
            pltpu.VMEM((fan, few.shape[0] // fan, few.shape[1]), jnp.bfloat16),
        ]
        + [sems(fan, n - 1), sems(fan, n - 1), sems(fan, 2), sems(fan, 2), sems(3)]
        + [sems(4, n - 1), sems(4, n - 1), sems(2, fan), sems(2, fan)],
        ident,
    )


def team(n):
    s, f = lax.axis_index("seq"), lax.axis_index("fsdp")
    half = s // (n // 2)
    away = (half + f) % 2
    return f // 2, half, (s + away * (n // 2)) % n


def swap_kernel(n, fan, count, fars, fresh, *refs):
    given = count + (len(fars) > 0) + (0 if fresh else 2)
    x_refs, y_refs = refs[:count], refs[given : given + count]
    sems = refs[given + count + (2 if fars else 0) :]
    send_sem, recv_sem, own_sem = sems[:3]
    pair, half, rank = team(n)
    me = lax.axis_index("fsdp")

    def device(other):
        away = (other // (n // 2) + half) % 2
        return {"seq": (other + away * (n // 2)) % n, "fsdp": 2 * pair + (half + away) % 2}

    barrier = pltpu.get_barrier_semaphore()
    for j in range(1, n):
        pl.semaphore_signal(barrier, inc=1, device_id=device((rank + j) % n), device_id_type=MESH)
    travel = [far for far in fars if far]
    for far in travel:
        pl.semaphore_signal(barrier, inc=1, device_id={"fsdp": (me + fan - far) % fan}, device_id_type=MESH)
    pl.semaphore_wait(barrier, n - 1 + len(travel))
    copies = []
    for k in range(count):
        for j in range(1, n):
            other = (rank + j) % n
            one = pltpu.make_async_remote_copy(
                src_ref=x_refs[k].at[other],
                dst_ref=y_refs[k].at[rank],
                send_sem=send_sem.at[k, j],
                recv_sem=recv_sem.at[k, j],
                device_id=device(other),
                device_id_type=MESH,
            )
            one.start()
            copies.append(one)
    for k in range(count):
        one = pltpu.make_async_copy(x_refs[k].at[rank], y_refs[k].at[rank], own_sem.at[k])
        one.start()
        copies.append(one)
    if fars:
        w_ref, halves = refs[count], refs[given + count : given + count + 2]
        far_send, far_recv, far_own, stage = sems[3:]
        rest = []
        units, cols = halves[0].shape[0], w_ref.shape[1]
        for i, far in enumerate(fars):
            target = (me + far) % fan
            for part in range(2):
                src = w_ref.at[pl.ds((part * fan + target) * units, units), :]
                dst = halves[part].at[:, pl.ds(pl.multiple_of(me * cols, 128), cols)]
                if far:
                    one = pltpu.make_async_remote_copy(
                        src_ref=src,
                        dst_ref=dst,
                        send_sem=far_send.at[i, part],
                        recv_sem=far_recv.at[i, part],
                        device_id={"fsdp": target},
                        device_id_type=MESH,
                    )
                else:
                    one = pltpu.make_async_copy(src, stage.at[part], far_own.at[0, part])
                    rest.append((one, pltpu.make_async_copy(stage.at[part], dst, far_own.at[1, part])))
                one.start()
                if far:
                    copies.append(one)
        for inward, outward in rest:
            inward.wait()
            outward.start()
            copies.append(outward)
    for one in copies:
        one.wait()


def swap(arrays, ident, fars=(), given=None, halves=None):
    n, fan = lax.axis_size("seq"), lax.axis_size("fsdp")
    count = len(arrays)
    size = sum(v.size * 2 for v in arrays)
    operands, outs, alias = list(arrays), [jax.ShapeDtypeStruct(v.shape, v.dtype) for v in arrays], {}
    scratch = [
        pltpu.SemaphoreType.DMA((count, n)),
        pltpu.SemaphoreType.DMA((count, n)),
        pltpu.SemaphoreType.DMA((count,)),
    ]
    if fars:
        operands.append(given)
        shape = (given.shape[0] // (2 * fan), given.shape[1] * fan)
        outs += [jax.ShapeDtypeStruct(shape, given.dtype)] * 2
        scratch += [pltpu.SemaphoreType.DMA((len(fars), 2))] * 2 + [
            pltpu.SemaphoreType.DMA((2, 2)),
            pltpu.VMEM((2, given.shape[0] // (2 * fan), given.shape[1]), given.dtype),
        ]
        if halves is not None:
            operands += list(halves)
            alias = {count + 1: count, count + 2: count + 1}
    return pl.pallas_call(
        functools.partial(swap_kernel, n, fan, count, fars, not fars or halves is None),
        name="swap",
        out_shape=outs,
        in_specs=[pl.BlockSpec(memory_space=pl.ANY)] * len(operands),
        out_specs=[pl.BlockSpec(memory_space=pl.ANY)] * len(outs),
        scratch_shapes=scratch,
        input_output_aliases=alias,
        compiler_params=pltpu.CompilerParams(collective_id=ident, has_side_effects=True),
        cost_estimate=pl.CostEstimate(flops=0, bytes_accessed=size, transcendentals=0),
    )(*operands)


def entry_kernel(n, w_ref, few_ref, out_ref, few_out_ref, side_sem, ring_send, ring_recv, pass_send, pass_recv, own_sem, few_sem):
    s, me = lax.axis_index("seq"), lax.axis_index("fsdp")
    core, y = me % 2, me // 2
    partner, across = 2 * y + 1 - core, 2 * (1 - y) + core
    far = 2 * (1 - y) + 1 - core
    rows, cols = w_ref.shape
    chunk_rows = rows // n
    half_rows = chunk_rows // 2
    place, right, left = ring_greet(n, [partner, across, far])

    def columns(of):
        return pl.ds(pl.multiple_of(of * cols, 128), cols)

    def copy(src, dst, send, recv, device):
        one = pltpu.make_async_remote_copy(
            src_ref=src, dst_ref=dst, send_sem=send, recv_sem=recv, device_id=device, device_id_type=MESH
        )
        one.start()
        return one

    def window(chunk, half):
        return out_ref.at[pl.ds(chunk * chunk_rows + half * half_rows, half_rows), columns(across)]

    mine = pl.ds(s * chunk_rows, chunk_rows)
    first = copy(
        w_ref.at[mine, :], out_ref.at[mine, columns(me)], side_sem.at[0], side_sem.at[1], {"fsdp": across}
    )
    others = []
    for i, to in enumerate((partner, across, far)):
        others.append(copy(few_ref, few_out_ref.at[me], few_sem.at[0, i], few_sem.at[1, i], {"fsdp": to}))
    others.append(copy(w_ref, out_ref.at[:, columns(me)], side_sem.at[2], side_sem.at[3], {"fsdp": partner}))
    own = [
        pltpu.make_async_copy(w_ref, out_ref.at[:, columns(me)], own_sem.at[0]),
        pltpu.make_async_copy(few_ref, few_out_ref.at[me], own_sem.at[1]),
    ]
    for one in own:
        one.start()

    travel = {}

    def send(half, step):
        chunk = ring_index((place + step) % n if half else (place + n - step) % n, n)
        view = window(chunk, half)
        if step < n - 1:
            to = left if half else right
            travel[half, step] = copy(view, view, ring_send.at[half, step], ring_recv.at[half, step], {"seq": to})
        others.append(copy(view, view, pass_send.at[half, step], pass_recv.at[half, step], {"fsdp": partner}))

    first.wait()
    for half in range(2):
        send(half, 0)
    for step in range(n - 1):
        for half in range(2):
            travel[half, step].wait_recv()
            send(half, step + 1)
    for one in travel.values():
        one.wait_send()
    for one in others + own:
        one.wait()


def entry(w, few, ident):
    n, fan = lax.axis_size("seq"), lax.axis_size("fsdp")
    rows, cols = w.shape
    sems = lambda *shape: pltpu.SemaphoreType.DMA(shape)
    return pl.pallas_call(
        functools.partial(entry_kernel, n),
        name="entry",
        out_shape=[
            jax.ShapeDtypeStruct((rows, cols * fan), w.dtype),
            jax.ShapeDtypeStruct((fan,) + few.shape, few.dtype),
        ],
        in_specs=[pl.BlockSpec(memory_space=pltpu.VMEM)] * 2,
        out_specs=[pl.BlockSpec(memory_space=pl.ANY)] * 2,
        scratch_shapes=[sems(4), sems(2, n - 1), sems(2, n - 1), sems(2, n), sems(2, n), sems(2), sems(2, 3)],
        compiler_params=pltpu.CompilerParams(
            collective_id=ident, has_side_effects=True, vmem_limit_bytes=24 << 20
        ),
        cost_estimate=pl.CostEstimate(flops=0, bytes_accessed=w.size * 2, transcendentals=0),
    )(w, few)


def norm_apply(value, gain):
    return value * lax.rsqrt(jnp.mean(value * value, axis=-1, keepdims=True) + EPS) * gain


def norm_back(value, gain, grad):
    _, pull = jax.vjp(norm_apply, value, gain)
    return pull(grad)


def gate_mix(gate, up):
    return jax.nn.gelu(gate, approximate=True) * up


def counts_below(ids, values):
    total = jnp.zeros_like(values)
    for doc in range(DOCS):
        total = total + jnp.where(values > doc, jnp.sum((ids == doc).astype(jnp.int32)), 0)
    return total


def change_home(value):
    n, fan = lax.axis_size("seq"), lax.axis_size("fsdp")
    pairs = []
    for s in range(n):
        for f in range(fan):
            away = (s // (n // 2) + f) % 2
            target = ((s + n // 2) % n, f ^ 1) if away else (s, f)
            pairs.append((s * fan + f, target[0] * fan + target[1]))
    return lax.ppermute(value, ("seq", "fsdp"), pairs)


def spread(blocks):
    fan, me = lax.axis_size("fsdp"), lax.axis_index("fsdp")
    result = blocks
    for far in range(1, fan):
        block = lax.dynamic_index_in_dim(blocks, (me + far) % fan, 0, True)
        block = lax.ppermute(block, "fsdp", [(f, (f + far) % fan) for f in range(fan)])
        result = lax.dynamic_update_slice_in_dim(result, block, (me - far) % fan, 0)
    return result


def flat(blocks):
    return jnp.transpose(blocks, (1, 0, 2)).reshape(blocks.shape[1], -1)


def by_rows(value):
    return with_layout_constraint(value, Layout(major_to_minor=tuple(range(value.ndim))))


def scatter(grad):
    return lax.psum_scatter(grad, "fsdp", scatter_dimension=0, tiled=True)


def shards(
    layer_in, encoder, decoder_ids, encoder_ids, rel_buckets,
    norm_self, self_qkv, self_out, rel_table, norm_cross, cross_q, cross_kv, cross_out, norm_ff, ff_in, ff_out,
    cotangent,
):
    seqs, local, width = layer_in.shape
    enc_local = encoder.shape[1]
    parts = lax.axis_size("seq")
    heads = self_qkv.shape[1]
    dh = self_qkv.shape[2] // 3
    own = heads // parts
    rows = seqs * local
    buckets, table_own = rel_table.shape
    length, keys = local * parts, enc_local * parts
    gather = lambda v: lax.all_gather(v, "fsdp", axis=0, tiled=True)

    fan = lax.axis_size("fsdp")
    units = ff_in.shape[1] // (2 * fan)
    part = norm_self.shape[0]
    pair, half, rank = team(parts)

    by_kernel = fan == 4 and (width // fan) % 128 == 0 and (ff_in.shape[0] // parts) % 8 == 0
    small = jnp.concatenate([norm_self, norm_cross, norm_ff, rel_table.reshape(-1)])
    early = by_rows(jnp.stack([self_out, cross_q, *jnp.split(cross_kv.reshape(-1, 2 * width), 2, axis=1)]))
    small, early = lax.optimization_barrier((small, early))
    qkv_t = jnp.transpose(self_qkv, (1, 2, 0)).reshape(heads * 3 * dh, -1)
    if by_kernel:
        few = jnp.pad(small, (0, 1024 - small.shape[0])).reshape(8, 128)
        qkv_t, few = entry(qkv_t, few, 18)
        small = few.reshape(fan, 1024)[:, : small.shape[0]]
    else:
        qkv_t = lax.all_gather(qkv_t, "fsdp", axis=1, tiled=True)
        small = lax.all_gather(small, "fsdp", axis=0, tiled=False)
    early = by_rows(lax.all_gather(early, "fsdp", axis=1, tiled=True))
    both_ids = jnp.concatenate([decoder_ids.reshape(-1), encoder_ids.reshape(-1)])
    both_ids = change_home(jnp.pad(both_ids, (0, 1024 - local - enc_local)).reshape(8, 128))
    inner_t = ff_in.T
    (both_ids,) = swap([jnp.broadcast_to(both_ids[None], (parts, 8, 128))], 13)
    home = change_home(layer_in.reshape(rows, width))
    gain_first, gain_second, gain_third = (
        small[:, i * part : (i + 1) * part].reshape(width).astype(f32) for i in range(3)
    )
    table = jnp.transpose(small[:, 3 * part :].reshape(-1, buckets, table_own), (1, 0, 2)).reshape(buckets, heads)
    both_ids = both_ids.reshape(parts, 1024)
    ids = both_ids[:, :local].reshape(length)
    enc_ids = both_ids[:, local : local + enc_local].reshape(keys)

    first_seen = counts_below(ids, ids)
    enc_first = counts_below(enc_ids, ids)
    enc_last = counts_below(enc_ids, ids + 1)
    blocks = length // BQ
    bk = BQ
    self_rows = jnp.broadcast_to(first_seen[None], (8, length))
    cross_rows = jnp.concatenate([enc_first[None], enc_last[None], jnp.zeros((6, length), jnp.int32)])
    self_limits = jnp.stack(
        [first_seen[::BQ] // bk, (jnp.arange(blocks, dtype=jnp.int32) + 1) * (BQ // bk)]
    )
    cross_limits = jnp.stack([enc_first[::BQ] // bk, (enc_last[BQ - 1 :: BQ] + bk - 1) // bk])

    first_head = rank * own
    table_mine = lax.dynamic_slice_in_dim(table.astype(f32), first_head, own, 1)
    near = rel_buckets[:REACH]
    onehot = (near[:, None] == jnp.arange(buckets, dtype=jnp.int32)[None, :]).astype(f32)
    bias = jnp.einsum("ln,ng->gl", onehot, table_mine, precision=HIGH)
    ext = jnp.concatenate(
        [jnp.full((own, BQ), MASKED, f32), bias, jnp.zeros((own, BQ), f32)], axis=1
    )

    qkv_t, home, inner_t, ext, self_rows, cross_rows, self_limits, cross_limits = lax.optimization_barrier(
        (qkv_t, home, inner_t, ext, self_rows, cross_rows, self_limits, cross_limits)
    )

    stream = home.astype(f32)
    normed_first = norm_apply(stream, gain_first).astype(bf16)
    qkv_tok = jnp.einsum(
        "td,ged->gte", normed_first, qkv_t.reshape(parts, own * 3 * dh, width), preferred_element_type=f32
    ).astype(bf16)
    others = change_home(jnp.concatenate([cotangent.reshape(rows, width), encoder.reshape(-1, width)]))
    grad_low, enc_flat = others[:rows], others[rows:]
    fars = [tuple(far for far in range(fan) if by_kernel and min(far, 3) in some) for some in ((2,), (0, 1), (3,))]
    qkv, *halves = swap([qkv_tok], 17, fars[0], inner_t)
    qkv, cross_out, grad_low = lax.optimization_barrier((qkv, cross_out, grad_low))
    if rows == cross_out.shape[0]:
        apart = lax.all_gather(jnp.stack([cross_out, grad_low]), "fsdp", axis=1, tiled=True)
    else:
        apart = (gather(cross_out), gather(grad_low))
    qkv = qkv.reshape(length, own * 3 * dh)
    out_self, self_t, self_lse = self_forward(self_limits, self_rows, ext, qkv)
    (self_tok,) = swap([out_self.reshape(parts, local, own * dh)], 11)
    after_self, normed_second, query_tok, pairs_tok = over_weights(
        into_kernel,
        "self_out_to_cross",
        [self_tok, home, gain_second.reshape(1, width), enc_flat],
        early,
        lambda i: i,
        [
            ((rows, width), f32),
            ((rows, width), bf16),
            ((parts, rows, own * dh), bf16),
            ((parts, enc_local, own * 2 * dh), bf16),
        ],
    )
    query_cross, pairs, *halves = swap([query_tok, pairs_tok], 15, fars[1], inner_t, halves)
    query_cross, pairs = query_cross.reshape(length, own * dh), pairs.reshape(keys, own * 2 * dh)
    out_cross, cross_t, cross_lse = cross_forward(cross_limits, cross_rows, query_cross, pairs)
    cross_tok, *halves = swap([out_cross.reshape(parts, local, own * dh)], 16, fars[2], inner_t, halves)
    if not by_kernel:
        halves = spread(jnp.transpose(inner_t.reshape(2, fan, units, -1), (1, 0, 2, 3)))
        halves = [jnp.transpose(halves[:, i], (1, 0, 2)).reshape(units, width) for i in range(2)]
    gate_t, up_t = halves
    cross_tok, apart = lax.optimization_barrier((cross_tok, apart))
    mix_cross, grad_group = apart
    mix_cross = mix_cross.reshape(parts, own * dh, width)
    after_cross = after_self + jnp.einsum("gtc,gcd->td", cross_tok, mix_cross, preferred_element_type=f32)
    normed_third = norm_apply(after_cross, gain_third).astype(bf16)
    normed_group = gather(normed_third)
    gate = jnp.einsum("td,fd->tf", normed_group, gate_t, preferred_element_type=f32)
    up = jnp.einsum("td,fd->tf", normed_group, up_t, preferred_element_type=f32)
    hidden = gate_mix(gate, up).astype(bf16)

    grad_hidden = jnp.einsum("td,fd->tf", grad_group, ff_out, preferred_element_type=f32)
    _, pull_mix = jax.vjp(gate_mix, gate, up)
    grad_gate, grad_up = (g.astype(bf16) for g in pull_mix(grad_hidden))
    grad_third_in = jnp.dot(grad_gate, gate_t, preferred_element_type=f32) + jnp.dot(
        grad_up, up_t, preferred_element_type=f32
    )
    grad_third_in = scatter(grad_third_in.astype(bf16))
    outer_part = jnp.dot(hidden, ff_out, preferred_element_type=f32).astype(bf16)
    grad_units = [
        jnp.einsum("tf,td->fd", g, y, preferred_element_type=f32).astype(bf16)
        for g, y in ((grad_gate, normed_group), (grad_up, normed_group), (hidden, grad_group))
    ]
    grad_third_in, outer_part, grad_units = lax.optimization_barrier((grad_third_in, outer_part, grad_units))
    if by_kernel:
        grad_units = jnp.stack([g.reshape(parts, units // parts, width) for g in grad_units], axis=1)
        part_units = grad_units.reshape(3 * units, width)
    grad_third_in = grad_third_in.astype(f32)
    grad_from_third, grad_gain_third = norm_back(after_cross, gain_third, grad_third_in)
    grad_middle = grad_low.astype(f32) + grad_from_third
    middle_low = grad_middle.astype(bf16)
    grad_mix_cross = jnp.einsum("gtc,td->gcd", cross_tok, middle_low, preferred_element_type=f32)
    part_cross = scatter(grad_mix_cross.reshape(width, width).astype(bf16))
    grad_cross_tok = jnp.einsum("td,gcd->gtc", middle_low, mix_cross, preferred_element_type=f32).astype(bf16)
    (grad_cross,) = swap([grad_cross_tok], 11)
    grad_cross = grad_cross.reshape(length, own * dh)
    grad_query, grad_pairs = cross_backward(
        cross_limits, cross_rows, query_cross, pairs, grad_cross, cross_t, cross_lse
    )
    grad_query_tok, grad_pairs_tok = swap(
        [grad_query.reshape(parts, local, own * dh), grad_pairs.reshape(parts, enc_local, own * 2 * dh)], 12
    )
    (
        grad_upper, upper_low, grad_self_tok, grad_gain_second, grad_encoder, grad_query_tok, grad_pairs_tok
    ) = over_weights(
        outof_kernel,
        "cross_to_self_out",
        [grad_query_tok, grad_pairs_tok, after_self, gain_second.reshape(1, width), grad_middle],
        early,
        lambda i: jnp.where(i < 2, 1 - i, i),
        [
            ((rows, width), f32),
            ((rows, width), bf16),
            ((parts, rows, own * dh), bf16),
            ((1, width), f32),
            ((enc_local, width), bf16),
            ((rows, width), bf16),
            ((enc_local, 2 * width), bf16),
        ],
        [((enc_local, width), f32)],
    )
    grad_query_w = jnp.einsum("td,te->de", normed_second, grad_query_tok, preferred_element_type=f32)
    grad_pairs_w = jnp.einsum("td,te->de", enc_flat, grad_pairs_tok, preferred_element_type=f32)
    grad_mix_self = jnp.einsum("gtc,td->gcd", self_tok, upper_low, preferred_element_type=f32)
    grad_mid = jnp.concatenate(
        [
            grad_query_w.astype(bf16),
            grad_pairs_w.astype(bf16),
            grad_mix_self.reshape(width, width).astype(bf16),
        ],
        axis=1,
    )
    grad_self_tok, grad_mid = lax.optimization_barrier((grad_self_tok, grad_mid))
    part_mid = scatter(grad_mid)
    (grad_self,) = swap([grad_self_tok], 11)
    grad_self = grad_self.reshape(length, own * dh)
    grad_qkv, diagonals = self_backward(self_limits, self_rows, ext, qkv, grad_self, self_t, self_lse)
    (grad_qkv_tok,) = swap([grad_qkv.reshape(parts, local, own * 3 * dh)], 10)
    grad_qkv_tok = flat(grad_qkv_tok)
    grad_qkv_w = jnp.einsum("td,te->de", normed_first, grad_qkv_tok, preferred_element_type=f32)
    grad_first_in = jnp.dot(grad_qkv_tok, qkv_t, preferred_element_type=f32)
    grad_from_first, grad_gain_first = norm_back(stream, gain_first, grad_first_in)
    grad_layer_in = (grad_upper + grad_from_first).astype(bf16)
    if not by_kernel:
        part_units = grad_units
    bucket_line = jnp.concatenate([jnp.full((BQ - 1,), -1, jnp.int32), near, jnp.full((BQ + 1,), -1, jnp.int32)])
    in_bucket = (bucket_line[:, None] == jnp.arange(buckets, dtype=jnp.int32)).astype(f32)
    by_bucket = jnp.einsum("xn,gx->ng", in_bucket, diagonals, precision=HIGH)
    grad_table = lax.dynamic_update_slice_in_dim(jnp.zeros((buckets, heads), f32), by_bucket, first_head, 1)

    gains = jnp.concatenate(
        [g.reshape(-1, part) for g in (grad_gain_first, grad_gain_second, grad_gain_third)], axis=1
    )
    tables = jnp.transpose(grad_table.reshape(buckets, -1, table_own), (1, 0, 2)).reshape(-1, buckets * table_own)
    small_grads = jnp.concatenate([gains, tables], axis=1).astype(bf16)
    small_size = small_grads.shape[1]
    going_home = jnp.concatenate([grad_layer_in, grad_encoder.astype(bf16)])
    going_home, small_grads, grad_qkv_w, part_units, part_cross, part_mid = lax.optimization_barrier(
        (change_home(going_home), small_grads, grad_qkv_w.astype(bf16), part_units, part_cross, part_mid)
    )
    part_last = scatter(grad_qkv_w)
    if by_kernel:
        few = jnp.pad(small_grads[:, None], ((0, 0), (0, 7), (0, 1024 - small_size))).reshape(fan * 8, 1024)
        total_inner, total_outer, outer_sum, few = units_total(part_units, outer_part, few, 0)
        few = jnp.pad(few[0].astype(bf16).reshape(8, 128), ((0, parts * 8 - 8), (0, 0)))
        total_cross, total_mid, total_qkv, small_total, total_inner = ring_total(
            [part_cross, part_mid, part_last, few], (2, 2, 2, 1), 1, total_inner
        )
    else:
        grad_units = [lax.psum(g, "seq") for g in part_units]
        total_inner = spread(jnp.transpose(jnp.stack(grad_units[:2]).reshape(2, units, fan, -1), (2, 0, 1, 3)))
        total_inner = jnp.transpose(total_inner, (3, 1, 0, 2)).reshape(-1, 2 * fan * units).astype(f32)
        total_outer, outer_sum = grad_units[2], scatter(outer_part).astype(f32)
        few = lax.dynamic_index_in_dim(lax.psum(small_grads, "fsdp"), lax.axis_index("fsdp"), 0, False)
        total_cross, total_mid, total_qkv, small_total = (
            lax.psum(v, "seq") for v in (part_cross, part_mid, part_last, few)
        )
    layer_out = (after_cross + outer_sum).astype(bf16)
    layer_out, total_inner, total_outer, total_cross, total_mid, total_qkv, going_home = lax.optimization_barrier(
        (layer_out, total_inner, total_outer, total_cross, total_mid, total_qkv, going_home)
    )
    layer_out = change_home(layer_out).reshape(seqs, local, width)
    grad_layer_in = going_home[:rows].astype(f32).reshape(seqs, local, width)
    grad_encoder = going_home[rows:].astype(f32).reshape(seqs, enc_local, width)
    total_outer, total_mid, total_qkv = (v.astype(f32) for v in (total_outer, total_mid, total_qkv))
    total_query, total_mix_cross = total_mid[:, :width], total_cross.astype(f32)
    total_pairs = total_mid[:, width : 3 * width].reshape(-1, heads, 2 * dh)
    total_mix_self, total_qkv = total_mid[:, 3 * width :], total_qkv.reshape(-1, heads, 3 * dh)
    mine = small_total.reshape(-1)[:small_size].astype(f32)
    total_gain_first, total_gain_second, total_gain_third = (mine[i * part : (i + 1) * part] for i in range(3))
    total_table = mine[3 * part :].reshape(buckets, table_own)
    return (
        layer_out, grad_layer_in, grad_encoder, total_gain_first, total_qkv, total_mix_self, total_table,
        total_gain_second, total_query, total_pairs, total_mix_cross, total_gain_third, total_inner, total_outer,
    )


def solution(mesh):
    in_specs = (
        P("fsdp", "seq", None), P("fsdp", "seq", None), P("fsdp", "seq"), P("fsdp", "seq"), P(),
        P("fsdp"), P("fsdp", None, None), P("fsdp", None), P(None, "fsdp"), P("fsdp"), P("fsdp", None),
        P("fsdp", None, None), P("fsdp", None), P("fsdp"), P("fsdp", None), P("fsdp", None),
        P("fsdp", "seq", None),
    )
    out_specs = (
        P("fsdp", "seq", None), P("fsdp", "seq", None), P("fsdp", "seq", None), P("fsdp"), P("fsdp", None, None),
        P("fsdp", None), P(None, "fsdp"), P("fsdp"), P("fsdp", None), P("fsdp", None, None), P("fsdp", None),
        P("fsdp"), P("fsdp", None), P("fsdp", None),
    )
    return jax.shard_map(shards, mesh=mesh, in_specs=in_specs, out_specs=out_specs, check_vma=False)
```

```python
import functools

import jax
import jax.numpy as jnp
from jax import lax
from jax.experimental import pallas as pl
from jax.experimental.layout import Layout, with_layout_constraint
from jax.experimental.pallas import tpu as pltpu
from jax.sharding import PartitionSpec as P

EPS = 1e-06
HIGH = lax.Precision.HIGHEST
MASKED = -1e30
DOCS = 4

BQ = 256
REACH = 1024


def blk(index, size):
    return pl.ds(pl.multiple_of(index * size, size), size)


def turn(value):
    return jnp.transpose(value.astype(jnp.float32), (1, 0))


def bias_tiles(ext_ref, tile_ref, own):
    for h in range(own):
        line = jnp.broadcast_to(ext_ref[h : h + 1, :], tile_ref.shape[1:])
        tile_ref[h] = pltpu.roll(line, 0, 1, stride=1, stride_axis=0)


def unpack(ref, own, width, picks, flips, base):
    block = 256

    def one(b, _):
        rows = blk(b, block)
        value = ref[rows, :]
        if flips:
            flat = turn(value).astype(jnp.bfloat16)
            for target, piece in flips:
                for h in range(own):
                    at = h * width + piece * 64
                    target[base + h, :, rows] = flat[at : at + 64]
        for target, piece in picks:
            for h in range(own):
                at = h * width + piece * 64
                target[base + h, rows, :] = value[:, at : at + 64]
        return 0

    lax.fori_loop(0, ref.shape[0] // block, one, 0)


def dot(a, b):
    return jnp.dot(a, b, preferred_element_type=jnp.float32)


def score(own_index, key_tile, query_t, tile_ref, t, low, high, first_key):
    value = dot(key_tile, query_t)
    place = lax.broadcasted_iota(jnp.int32, value.shape, 0)
    keep = place >= low - first_key
    if high is not None:
        keep = keep & (place < high - first_key)
    else:
        value = value + tile_ref[own_index, :, blk(t + 1, BQ)]
    return jnp.where(keep, value, MASKED)


def forward_body(own, bk, causal, lim_ref, rows_ref, q_t, k_rows, v_t, tile_ref, o_ref, ot_ref, lse_ref):
    length = o_ref.shape[0]

    def q_block(i, _):
        cols = blk(i, BQ)
        queries = [q_t[h, :, cols] for h in range(own)]
        low = rows_ref[0:1, cols]
        high = None if causal else rows_ref[1:2, cols]

        def k_block(j, carry):
            keys = blk(j, bk)
            t = i - j
            out = []
            for h in range(own):
                top, total, acc = carry[h]
                s = score(h, k_rows[h, keys, :], queries[h], tile_ref, t, low, high, j * bk)
                new_top = jnp.maximum(top, jnp.max(s, axis=0, keepdims=True))
                p = jnp.exp(s - new_top)
                scale = jnp.exp(top - new_top)
                total = total * scale + jnp.sum(p, axis=0, keepdims=True)
                acc = acc * scale + dot(v_t[h, :, keys], p.astype(jnp.bfloat16))
                out.append((new_top, total, acc))
            return tuple(out)

        start = tuple(
            (
                jnp.full((1, BQ), MASKED, jnp.float32),
                jnp.zeros((1, BQ), jnp.float32),
                jnp.zeros((64, BQ), jnp.float32),
            )
            for _ in range(own)
        )
        ends = lax.fori_loop(lim_ref[0, i], lim_ref[1, i], k_block, start)
        for h in range(own):
            top, total, acc = ends[h]
            ot_ref[h * 64 : h * 64 + 64, cols] = acc / total
            lse_ref[h : h + 1, cols] = top + jnp.log(total)
        o_ref[cols, :] = turn(ot_ref[:, cols]).astype(jnp.bfloat16)
        return 0

    lax.fori_loop(0, length // BQ, q_block, 0)


def self_forward_kernel(own, bk, lim_ref, rows_ref, ext_ref, x_ref, o_ref, ot_ref, lse_ref, q_t, k_rows, v_t, tile_ref):
    bias_tiles(ext_ref, tile_ref, own)
    unpack(x_ref, own, 192, [(k_rows, 1)], [(q_t, 0), (v_t, 2)], 0)
    forward_body(own, bk, True, lim_ref, rows_ref, q_t, k_rows, v_t, tile_ref, o_ref, ot_ref, lse_ref)


def cross_forward_kernel(own, bk, lim_ref, rows_ref, q_ref, kv_ref, o_ref, ot_ref, lse_ref, q_t, k_rows, v_t):
    unpack(q_ref, own, 64, [], [(q_t, 0)], 0)
    unpack(kv_ref, own, 128, [(k_rows, 0)], [(v_t, 1)], 0)
    forward_body(own, bk, False, lim_ref, rows_ref, q_t, k_rows, v_t, None, o_ref, ot_ref, lse_ref)


def backward_body(
    own, bk, causal, lim_ref, rows_ref, do_ref, ot_ref, lse_ref,
    q_t, q_rows, k_t, k_rows, v_rows, do_t, do_rows, tile_ref, sum_ref, dq_t, dk, dv,
):
    length = do_ref.shape[0]
    dk[...] = jnp.zeros_like(dk)
    dv[...] = jnp.zeros_like(dv)
    if causal:
        sum_ref[...] = jnp.zeros_like(sum_ref)

    def q_block(i, _):
        cols = blk(i, BQ)
        low = rows_ref[0:1, cols]
        high = None if causal else rows_ref[1:2, cols]
        per_head = []
        for h in range(own):
            grad_t = do_t[h, :, cols]
            delta = jnp.sum(
                grad_t.astype(jnp.float32) * ot_ref[h * 64 : h * 64 + 64, cols], axis=0, keepdims=True
            )
            per_head.append((q_t[h, :, cols], grad_t, delta, lse_ref[h : h + 1, cols]))

        def k_block(j, carry):
            keys = blk(j, bk)
            t = i - j
            out = []
            for h in range(own):
                query_t, grad_t, delta, lse = per_head[h]
                s = score(h, k_rows[h, keys, :], query_t, tile_ref, t, low, high, j * bk)
                p = jnp.exp(s - lse)
                dp = dot(v_rows[h, keys, :], grad_t)
                ds = (p * (dp - delta)).astype(jnp.bfloat16)
                dv[h, keys, :] += dot(p.astype(jnp.bfloat16), do_rows[h, cols, :])
                dk[h, keys, :] += dot(ds, q_rows[h, cols, :])
                if causal:
                    sum_ref[h, :, blk(t, BQ)] += ds.astype(jnp.float32)
                out.append(carry[h] + dot(k_t[h, :, keys], ds))
            return tuple(out)

        ends = lax.fori_loop(
            lim_ref[0, i],
            lim_ref[1, i],
            k_block,
            tuple(jnp.zeros((64, BQ), jnp.float32) for _ in range(own)),
        )
        for h in range(own):
            dq_t[h * 64 : h * 64 + 64, cols] = ends[h]
        return 0

    lax.fori_loop(0, length // BQ, q_block, 0)


def diagonal_sums(sum_ref, u_ref, own):
    flip = lax.broadcasted_iota(jnp.int32, (BQ, BQ), 0) + lax.broadcasted_iota(jnp.int32, (BQ, BQ), 1) == BQ - 1
    flip = jnp.where(flip, 1.0, 0.0).astype(jnp.bfloat16)
    for h in range(own):
        grid = sum_ref[h]
        high = grid.astype(jnp.bfloat16)
        low = (grid - high.astype(jnp.float32)).astype(jnp.bfloat16)
        upside = dot(flip, high) + dot(flip, low)
        wide = jnp.concatenate([upside, jnp.zeros((BQ, BQ), jnp.float32)], axis=1)
        aligned = pltpu.roll(wide, 0, 1, stride=1, stride_axis=0)
        u_ref[h : h + 1, :] = jnp.sum(aligned, axis=0, keepdims=True)


def self_backward_kernel(
    own, bk, lim_ref, rows_ref, ext_ref, x_ref, do_ref, ot_ref, lse_ref, dx_ref, u_ref,
    q_t, q_rows, k_t, k_rows, v_rows, do_t, do_rows, tile_ref, sum_ref, dq_t, dk, dv,
):
    bias_tiles(ext_ref, tile_ref, own)
    unpack(x_ref, own, 192, [(q_rows, 0), (k_rows, 1), (v_rows, 2)], [(q_t, 0), (k_t, 1)], 0)
    unpack(do_ref, own, 64, [(do_rows, 0)], [(do_t, 0)], 0)
    backward_body(
        own, bk, True, lim_ref, rows_ref, do_ref, ot_ref, lse_ref,
        q_t, q_rows, k_t, k_rows, v_rows, do_t, do_rows, tile_ref, sum_ref, dq_t, dk, dv,
    )
    diagonal_sums(sum_ref, u_ref, own)

    def pack(b, _):
        rows = blk(b, 256)
        dq = turn(dq_t[:, rows])
        pieces = []
        for h in range(own):
            pieces += [dq[:, h * 64 : h * 64 + 64], dk[h, rows, :], dv[h, rows, :]]
        dx_ref[rows, :] = jnp.concatenate(pieces, axis=1).astype(jnp.bfloat16)
        return 0

    lax.fori_loop(0, x_ref.shape[0] // 256, pack, 0)


def cross_backward_kernel(
    own, bk, lim_ref, rows_ref, q_ref, kv_ref, do_ref, ot_ref, lse_ref, dq_ref, dkv_ref,
    q_t, q_rows, k_t, k_rows, v_rows, do_t, do_rows, dq_t, dk, dv,
):
    unpack(q_ref, own, 64, [(q_rows, 0)], [(q_t, 0)], 0)
    unpack(kv_ref, own, 128, [(k_rows, 0), (v_rows, 1)], [(k_t, 0)], 0)
    unpack(do_ref, own, 64, [(do_rows, 0)], [(do_t, 0)], 0)
    backward_body(
        own, bk, False, lim_ref, rows_ref, do_ref, ot_ref, lse_ref,
        q_t, q_rows, k_t, k_rows, v_rows, do_t, do_rows, None, None, dq_t, dk, dv,
    )

    def pack_q(b, _):
        rows = blk(b, 256)
        dq_ref[rows, :] = turn(dq_t[:, rows]).astype(jnp.bfloat16)
        return 0

    def pack_kv(b, _):
        rows = blk(b, 256)
        pieces = []
        for h in range(own):
            pieces += [dk[h, rows, :], dv[h, rows, :]]
        dkv_ref[rows, :] = jnp.concatenate(pieces, axis=1).astype(jnp.bfloat16)
        return 0

    lax.fori_loop(0, q_ref.shape[0] // 256, pack_q, 0)
    lax.fori_loop(0, kv_ref.shape[0] // 256, pack_kv, 0)


SMEM = pl.BlockSpec(memory_space=pltpu.SMEM)
VMEM = pl.BlockSpec(memory_space=pltpu.VMEM)
bf16, f32 = jnp.bfloat16, jnp.float32


def call(body, name, operands, outs, scratch, flops):
    size = sum(v.size * v.dtype.itemsize for v in operands)
    return pl.pallas_call(
        body,
        name=name,
        out_shape=[jax.ShapeDtypeStruct(s, d) for s, d in outs],
        in_specs=[SMEM] + [VMEM] * (len(operands) - 1),
        out_specs=[VMEM] * len(outs),
        scratch_shapes=[pltpu.VMEM(s, d) for s, d in scratch],
        compiler_params=pltpu.CompilerParams(vmem_limit_bytes=40 << 20),
        cost_estimate=pl.CostEstimate(flops=0, bytes_accessed=size, transcendentals=0),
    )(*operands)


def self_forward(limits, rows, ext, x, bk=BQ):
    length, own = x.shape[0], x.shape[1] // 192
    return call(
        functools.partial(self_forward_kernel, own, bk),
        "self_forward",
        [limits, rows, ext, x],
        [((length, own * 64), bf16), ((own * 64, length), f32), ((own, length), f32)],
        [
            ((own, 64, length), bf16),
            ((own, length, 64), bf16),
            ((own, 64, length), bf16),
            ((own, BQ, REACH + 2 * BQ), f32),
        ],
        length * length * own * 64,
    )


def cross_forward(limits, rows, q, kv, bk=BQ):
    length, own, keys = q.shape[0], q.shape[1] // 64, kv.shape[0]
    return call(
        functools.partial(cross_forward_kernel, own, bk),
        "cross_forward",
        [limits, rows, q, kv],
        [((length, own * 64), bf16), ((own * 64, length), f32), ((own, length), f32)],
        [((own, 64, length), bf16), ((own, keys, 64), bf16), ((own, 64, keys), bf16)],
        length * keys * own * 128,
    )


def self_backward(limits, rows, ext, x, grad, o_t, lse, bk=BQ):
    length, own = x.shape[0], x.shape[1] // 192
    return call(
        functools.partial(self_backward_kernel, own, bk),
        "self_backward",
        [limits, rows, ext, x, grad, o_t, lse],
        [((length, own * 192), bf16), ((own, REACH + 2 * BQ), f32)],
        [
            ((own, 64, length), bf16),
            ((own, length, 64), bf16),
            ((own, 64, length), bf16),
            ((own, length, 64), bf16),
            ((own, length, 64), bf16),
            ((own, 64, length), bf16),
            ((own, length, 64), bf16),
            ((own, BQ, REACH + 2 * BQ), f32),
            ((own, BQ, REACH + BQ), f32),
            ((own * 64, length), f32),
            ((own, length, 64), f32),
            ((own, length, 64), f32),
        ],
        length * length * own * 160,
    )


def cross_backward(limits, rows, q, kv, grad, o_t, lse, bk=BQ):
    length, own, keys = q.shape[0], q.shape[1] // 64, kv.shape[0]
    return call(
        functools.partial(cross_backward_kernel, own, bk),
        "cross_backward",
        [limits, rows, q, kv, grad, o_t, lse],
        [((length, own * 64), bf16), ((keys, own * 128), bf16)],
        [
            ((own, 64, length), bf16),
            ((own, length, 64), bf16),
            ((own, 64, keys), bf16),
            ((own, keys, 64), bf16),
            ((own, keys, 64), bf16),
            ((own, 64, length), bf16),
            ((own, length, 64), bf16),
            ((own * 64, length), f32),
            ((own, keys, 64), f32),
            ((own, keys, 64), f32),
        ],
        length * keys * own * 320,
    )


def rows_of(blocks_ref):
    return jnp.concatenate([blocks_ref[g] for g in range(blocks_ref.shape[0])], axis=1)


def against(a, b):
    return lax.dot_general(a, b, (((1,), (1,)), ((), ())), preferred_element_type=jnp.float32)


def into_kernel(tok_ref, home_ref, gain_ref, enc_ref, w_ref, after_ref, norm_ref, query_ref, pairs_ref):
    which = pl.program_id(0)

    @pl.when(which == 0)
    def _():
        value = home_ref[...].astype(jnp.float32) + dot(rows_of(tok_ref), w_ref[0])
        after_ref[...] = value
        scale = lax.rsqrt(jnp.mean(value * value, axis=1, keepdims=True) + EPS)
        norm_ref[...] = (value * scale * gain_ref[...]).astype(jnp.bfloat16)

    @pl.when(which == 1)
    def _():
        query = dot(norm_ref[...], w_ref[0]).astype(jnp.bfloat16)
        cols = query_ref.shape[2]
        for g in range(query_ref.shape[0]):
            query_ref[g] = query[:, g * cols : (g + 1) * cols]

    for half in range(2):

        @pl.when(which == 2 + half)
        def _():
            pairs = dot(enc_ref[...], w_ref[0]).astype(jnp.bfloat16)
            groups, cols = pairs_ref.shape[0] // 2, pairs_ref.shape[2]
            for g in range(groups):
                pairs_ref[half * groups + g] = pairs[:, g * cols : (g + 1) * cols]


def outof_kernel(
    dq_ref, dkv_ref, after_ref, gain_ref, middle_ref, w_ref,
    upper_ref, low_ref, out_ref, gain_grad_ref, enc_grad_ref, dq_flat_ref, dkv_flat_ref, enc_sum,
):
    which = pl.program_id(0)

    @pl.when(which == 0)
    def _():
        grad_query = rows_of(dq_ref)
        dq_flat_ref[...] = grad_query
        dkv_flat_ref[...] = rows_of(dkv_ref)
        grad = against(grad_query, w_ref[0])
        value = after_ref[...]
        unit = value * lax.rsqrt(jnp.mean(value * value, axis=1, keepdims=True) + EPS)
        gain_grad_ref[...] = jnp.sum(grad * unit, axis=0, keepdims=True)
        scale = lax.rsqrt(jnp.mean(value * value, axis=1, keepdims=True) + EPS)
        grad = grad * gain_ref[...]
        inner = jnp.mean(grad * unit, axis=1, keepdims=True)
        upper = middle_ref[...] + scale * (grad - unit * inner)
        upper_ref[...] = upper
        low_ref[...] = upper.astype(jnp.bfloat16)

    @pl.when(which == 1)
    def _():
        grad = against(low_ref[...], w_ref[0]).astype(jnp.bfloat16)
        cols = out_ref.shape[2]
        for g in range(out_ref.shape[0]):
            out_ref[g] = grad[:, g * cols : (g + 1) * cols]

    width = w_ref.shape[1]

    @pl.when(which == 2)
    def _():
        enc_sum[...] = against(dkv_flat_ref[:, :width], w_ref[0])

    @pl.when(which == 3)
    def _():
        enc_grad_ref[...] = (enc_sum[...] + against(dkv_flat_ref[:, width:], w_ref[0])).astype(jnp.bfloat16)


def over_weights(body, name, arrays, weights, order, outs, scratch=()):
    count, rows, cols = weights.shape
    whole = lambda shape: pl.BlockSpec(shape, lambda i: (0,) * len(shape))
    return pl.pallas_call(
        body,
        name=name,
        grid=(count,),
        out_shape=[jax.ShapeDtypeStruct(s, d) for s, d in outs],
        in_specs=[whole(v.shape) for v in arrays] + [pl.BlockSpec((1, rows, cols), lambda i: (order(i), 0, 0))],
        out_specs=[whole(s) for s, _ in outs],
        scratch_shapes=[pltpu.VMEM(s, d) for s, d in scratch],
        compiler_params=pltpu.CompilerParams(vmem_limit_bytes=40 << 20, dimension_semantics=("arbitrary",)),
        cost_estimate=pl.CostEstimate(flops=0, bytes_accessed=weights.size * 2, transcendentals=0),
    )(*arrays, weights)


MESH = pl.DeviceIdType.MESH


def ring_place(index, n):
    z, x = index // 2, index % 2
    return z + x * (n - 1 - 2 * z)


def ring_index(place, n):
    x = place // (n // 2)
    z = place + x * (n - 1 - 2 * place)
    return 2 * z + x


def ring_greet(n, others):
    place = ring_place(lax.axis_index("seq"), n)
    right = ring_index((place + 1) % n, n)
    left = ring_index((place + n - 1) % n, n)
    barrier = pltpu.get_barrier_semaphore()
    for neighbour in (left, right):
        pl.semaphore_signal(barrier, inc=1, device_id={"seq": neighbour}, device_id_type=MESH)
    for other in others:
        pl.semaphore_signal(barrier, inc=1, device_id={"fsdp": other}, device_id_type=MESH)
    pl.semaphore_wait(barrier, 2 + len(others))
    return place, right, left


def ring_cut(shape, split, n):
    rows, cols = shape[0] // n, shape[1]
    return (rows, cols // split) if split > 0 else (rows // -split, cols)


def ring_window(ref, shape, split, n, piece, chunk):
    whole = shape[0] // n
    rows, cols = ring_cut(shape, split, n)
    if split > 0:
        return ref.at[pl.ds(chunk * whole, rows), pl.ds(piece * cols, cols)]
    return ref.at[pl.ds(chunk * whole + piece * rows, rows), :]


def ring_kernel(n, splits, fan, *refs):
    count = len(splits)
    more = 1 if fan else 0
    x_refs, y_refs = refs[:count], refs[count + more : 2 * count + more]
    slots = refs[2 * (count + more) : 3 * count + 2 * more]
    send_sem, recv_sem = refs[3 * count + 2 * more :]
    place, right, left = ring_greet(n, [])
    streams = [(k, piece, piece % 2) for k in range(count) for piece in range(abs(splits[k]))]

    def window(ref, k, piece, chunk):
        return ring_window(ref, x_refs[k].shape, splits[k], n, piece, chunk)

    def chunk_at(down, step):
        return (place + 1 + step) % n if down else (place + 2 * n - 1 - step) % n

    copies = {}

    def start(number, step, src, dst, down):
        copies[number, step] = pltpu.make_async_remote_copy(
            src_ref=src,
            dst_ref=dst,
            send_sem=send_sem.at[number, step],
            recv_sem=recv_sem.at[number, step],
            device_id={"seq": left if down else right},
            device_id_type=MESH,
        )
        copies[number, step].start()

    def turn_block(number):
        inner_ref, turned_ref = refs[count], refs[2 * count + 1]
        rows = inner_ref.shape[0] // (2 * fan * n)
        half, first = number // (fan // 2), number % (fan // 2) * 2
        tall = jnp.concatenate(
            [
                inner_ref[pl.ds(((chunk * fan + group) * 2 + half) * rows, rows), :].astype(jnp.float32)
                for group in (first, first + 1)
                for chunk in range(n)
            ]
        )
        wide = 2 * n * rows
        turned_ref[:, number * wide : (number + 1) * wide] = jnp.transpose(tall, (1, 0)).astype(jnp.bfloat16)

    for number, (k, piece, down) in enumerate(streams):
        start(number, 0, window(x_refs[k], k, piece, place), window(slots[k], k, piece, 0), down)
    for step in range(n - 1):
        if step < fan:
            turn_block(step)
        for number, (k, piece, down) in enumerate(streams):
            copies[number, step].wait_recv()
            chunk = chunk_at(down, step)
            mine = window(x_refs[k], k, piece, chunk)
            landed = window(slots[k], k, piece, step)
            total = landed[...].astype(jnp.float32) + mine[...].astype(jnp.float32)
            if step < n - 2:
                landed[...] = total.astype(jnp.bfloat16)
                start(number, step + 1, landed, window(slots[k], k, piece, step + 1), down)
            else:
                done = window(y_refs[k], k, piece, chunk)
                done[...] = total.astype(jnp.bfloat16)
                start(number, n - 1, done, done, down)
    for step in range(n - 1):
        for number, (k, piece, down) in enumerate(streams):
            copies[number, n - 1 + step].wait_recv()
            if step < n - 2:
                done = window(y_refs[k], k, piece, chunk_at(down, n - 1 + step))
                start(number, n + step, done, done, down)
    for one in copies.values():
        one.wait_send()


def ring_call(body, name, arrays, outs, scratch, ident):
    size = sum(v.size * 2 for v in arrays)
    return pl.pallas_call(
        body,
        name=name,
        out_shape=[jax.ShapeDtypeStruct(s, d) for s, d in outs],
        in_specs=[pl.BlockSpec(memory_space=pltpu.VMEM)] * len(arrays),
        out_specs=[pl.BlockSpec(memory_space=pltpu.VMEM)] * len(outs),
        scratch_shapes=scratch,
        compiler_params=pltpu.CompilerParams(
            collective_id=ident, has_side_effects=True, vmem_limit_bytes=48 << 20
        ),
        cost_estimate=pl.CostEstimate(flops=0, bytes_accessed=60 * size, transcendentals=0),
    )(*arrays)


def ring_total(arrays, splits, ident, inner=None):
    n, fan = lax.axis_size("seq"), lax.axis_size("fsdp")
    streams = sum(abs(s) for s in splits)
    more = [] if inner is None else [inner]
    return ring_call(
        functools.partial(ring_kernel, n, splits, 0 if inner is None else fan),
        "ring_total",
        arrays + more,
        [(v.shape, jnp.bfloat16) for v in arrays] + [(v.shape[::-1], jnp.bfloat16) for v in more],
        [pltpu.VMEM((v.shape[0] // n * (n - 1), v.shape[1]), jnp.bfloat16) for v in arrays]
        + [pltpu.SemaphoreType.DMA((streams, 2 * n - 2))] * 2,
        ident,
    )


def units_kernel(
    n, fan, x_ref, part_ref, few_ref, inner_ref, outer_ref, sum_ref, few_sum_ref, slots, acc, landed, few_landed,
    down_send, down_recv, swap_send, swap_recv, own_sem, send_sem, recv_sem, part_send, part_recv,
):
    s, me = lax.axis_index("seq"), lax.axis_index("fsdp")
    rows, width = acc.shape[0] // 3, x_ref.shape[1]
    cols = width // fan
    block = 2 * fan * rows
    place, right, left = ring_greet(n, [(me + far) % fan for far in range(1, fan)])
    sums = {}

    def piece_of(ref, at, piece):
        return ref.at[pl.ds(at * 3 * rows, 3 * rows), pl.ds(piece * cols, cols)]

    def send_sum(piece, step, src):
        to = left if piece >= fan // 2 else right
        sums[piece, step] = pltpu.make_async_remote_copy(
            src_ref=src,
            dst_ref=piece_of(slots, step, piece),
            send_sem=down_send.at[piece, step],
            recv_sem=down_recv.at[piece, step],
            device_id={"seq": to},
            device_id_type=MESH,
        )
        sums[piece, step].start()

    def chunk(piece, step):
        return ring_index((place + 1 + step) % n if piece >= fan // 2 else (place + 2 * n - 1 - step) % n, n)

    for piece in range(fan):
        send_sum(piece, 0, piece_of(x_ref, chunk(piece, 0), piece))
    for step in range(n - 1):
        for piece in range(fan):
            sums[piece, step].wait_recv()
            arrived = piece_of(slots, step, piece)
            mine = piece_of(x_ref, chunk(piece, step + 1), piece)
            total = (arrived[...].astype(jnp.float32) + mine[...].astype(jnp.float32)).astype(jnp.bfloat16)
            if step < n - 2:
                arrived[...] = total
                send_sum(piece, step + 1, arrived)
            else:
                acc[:, piece * cols : (piece + 1) * cols] = total
    moves = []
    for far in range(fan):
        target = (me + far) % fan
        for half in range(2):
            src = acc.at[pl.ds(half * rows, rows), pl.ds(pl.multiple_of(target * cols, 128), cols)]
            dst = inner_ref.at[pl.ds(s * block + (me * 2 + half) * rows, rows), :]
            if far:
                one = pltpu.make_async_remote_copy(
                    src_ref=src,
                    dst_ref=dst,
                    send_sem=swap_send.at[far, half],
                    recv_sem=swap_recv.at[far, half],
                    device_id={"fsdp": target},
                    device_id_type=MESH,
                )
            else:
                one = pltpu.make_async_copy(src, dst, own_sem.at[half])
            one.start()
            moves.append(one)
    mine = pltpu.make_async_copy(
        acc.at[pl.ds(2 * rows, rows), :], outer_ref.at[pl.ds(s * rows, rows), :], own_sem.at[2]
    )
    mine.start()
    copies = {}
    outs = ((outer_ref, (n * rows, width), 2), (inner_ref, (n * block, cols), -2))

    def start(k, piece, step):
        ref, shape, split = outs[k]
        chunk = ring_index((place + step) % n if piece else (place + n - step) % n, n)
        view = ring_window(ref, shape, split, n, piece, chunk)
        copies[k, piece, step] = pltpu.make_async_remote_copy(
            src_ref=view,
            dst_ref=view,
            send_sem=send_sem.at[2 * k + piece, step],
            recv_sem=recv_sem.at[2 * k + piece, step],
            device_id={"seq": left if piece else right},
            device_id_type=MESH,
        )
        copies[k, piece, step].start()

    def forward(k, step):
        for piece in range(2):
            copies[k, piece, step].wait_recv()
            if step < n - 2:
                start(k, piece, step + 1)

    mine.wait()
    start(0, 0, 0)
    start(0, 1, 0)
    lead = (n - 1) // 2
    for step in range(lead):
        forward(0, step)
    for one in moves:
        one.wait()
    parts = []
    for far in range(1, fan):
        target = (me + far) % fan
        for which, (src, into) in enumerate(((part_ref, landed), (few_ref, few_landed))):
            rest = src.shape[0] // fan
            one = pltpu.make_async_remote_copy(
                src_ref=src.at[pl.ds(target * rest, rest), :],
                dst_ref=into.at[far],
                send_sem=part_send.at[which, far],
                recv_sem=part_recv.at[which, far],
                device_id={"fsdp": target},
                device_id_type=MESH,
            )
            one.start()
            parts.append(one)
    start(1, 0, 0)
    start(1, 1, 0)
    for step in range(n - 1):
        forward(1, step)
        if lead + step < n - 1:
            forward(0, lead + step)
    for one in parts:
        one.wait()
    for src, into, out in ((part_ref, landed, sum_ref), (few_ref, few_landed, few_sum_ref)):
        rest = src.shape[0] // fan
        total = src[pl.ds(pl.multiple_of(me * rest, rest), rest), :].astype(jnp.float32)
        for far in range(1, fan):
            total = total + into[far].astype(jnp.float32)
        out[...] = total
    for one in [*copies.values(), *sums.values()]:
        one.wait_send()


def units_total(grads, part, few, ident):
    n, fan = lax.axis_size("seq"), lax.axis_size("fsdp")
    rows, width = grads.shape[0] // (3 * n), grads.shape[1]
    tokens = part.shape[0] // fan
    sems = lambda *shape: pltpu.SemaphoreType.DMA(shape)
    return ring_call(
        functools.partial(units_kernel, n, fan),
        "units_total",
        [grads, part, few],
        [
            ((n * 2 * fan * rows, width // fan), jnp.bfloat16),
            ((n * rows, width), jnp.bfloat16),
            ((tokens, part.shape[1]), jnp.float32),
            ((few.shape[0] // fan, few.shape[1]), jnp.float32),
        ],
        [
            pltpu.VMEM(((n - 1) * 3 * rows, width), jnp.bfloat16),
            pltpu.VMEM((3 * rows, width), jnp.bfloat16),
            pltpu.VMEM((fan, tokens, part.shape[1]), jnp.bfloat16),
            pltpu.VMEM((fan, few.shape[0] // fan, few.shape[1]), jnp.bfloat16),
        ]
        + [sems(fan, n - 1), sems(fan, n - 1), sems(fan, 2), sems(fan, 2), sems(3)]
        + [sems(4, n - 1), sems(4, n - 1), sems(2, fan), sems(2, fan)],
        ident,
    )


def team(n):
    s, f = lax.axis_index("seq"), lax.axis_index("fsdp")
    half = s // (n // 2)
    away = (half + f) % 2
    return f // 2, half, (s + away * (n // 2)) % n


def swap_kernel(n, fan, count, fars, fresh, *refs):
    given = count + (len(fars) > 0) + (0 if fresh else 2)
    x_refs, y_refs = refs[:count], refs[given : given + count]
    sems = refs[given + count + (2 if fars else 0) :]
    send_sem, recv_sem, own_sem = sems[:3]
    pair, half, rank = team(n)
    me = lax.axis_index("fsdp")

    def device(other):
        away = (other // (n // 2) + half) % 2
        return {"seq": (other + away * (n // 2)) % n, "fsdp": 2 * pair + (half + away) % 2}

    barrier = pltpu.get_barrier_semaphore()
    for j in range(1, n):
        pl.semaphore_signal(barrier, inc=1, device_id=device((rank + j) % n), device_id_type=MESH)
    travel = [far for far in fars if far]
    for far in travel:
        pl.semaphore_signal(barrier, inc=1, device_id={"fsdp": (me + fan - far) % fan}, device_id_type=MESH)
    pl.semaphore_wait(barrier, n - 1 + len(travel))
    copies = []
    for k in range(count):
        for j in range(1, n):
            other = (rank + j) % n
            one = pltpu.make_async_remote_copy(
                src_ref=x_refs[k].at[other],
                dst_ref=y_refs[k].at[rank],
                send_sem=send_sem.at[k, j],
                recv_sem=recv_sem.at[k, j],
                device_id=device(other),
                device_id_type=MESH,
            )
            one.start()
            copies.append(one)
    for k in range(count):
        one = pltpu.make_async_copy(x_refs[k].at[rank], y_refs[k].at[rank], own_sem.at[k])
        one.start()
        copies.append(one)
    if fars:
        w_ref, halves = refs[count], refs[given + count : given + count + 2]
        far_send, far_recv, far_own, stage = sems[3:]
        rest = []
        units, cols = halves[0].shape[0], w_ref.shape[1]
        for i, far in enumerate(fars):
            target = (me + far) % fan
            for part in range(2):
                src = w_ref.at[pl.ds((part * fan + target) * units, units), :]
                dst = halves[part].at[:, pl.ds(pl.multiple_of(me * cols, 128), cols)]
                if far:
                    one = pltpu.make_async_remote_copy(
                        src_ref=src,
                        dst_ref=dst,
                        send_sem=far_send.at[i, part],
                        recv_sem=far_recv.at[i, part],
                        device_id={"fsdp": target},
                        device_id_type=MESH,
                    )
                else:
                    one = pltpu.make_async_copy(src, stage.at[part], far_own.at[0, part])
                    rest.append((one, pltpu.make_async_copy(stage.at[part], dst, far_own.at[1, part])))
                one.start()
                if far:
                    copies.append(one)
        for inward, outward in rest:
            inward.wait()
            outward.start()
            copies.append(outward)
    for one in copies:
        one.wait()


def swap(arrays, ident, fars=(), given=None, halves=None):
    n, fan = lax.axis_size("seq"), lax.axis_size("fsdp")
    count = len(arrays)
    size = sum(v.size * 2 for v in arrays)
    operands, outs, alias = list(arrays), [jax.ShapeDtypeStruct(v.shape, v.dtype) for v in arrays], {}
    scratch = [
        pltpu.SemaphoreType.DMA((count, n)),
        pltpu.SemaphoreType.DMA((count, n)),
        pltpu.SemaphoreType.DMA((count,)),
    ]
    if fars:
        operands.append(given)
        shape = (given.shape[0] // (2 * fan), given.shape[1] * fan)
        outs += [jax.ShapeDtypeStruct(shape, given.dtype)] * 2
        scratch += [pltpu.SemaphoreType.DMA((len(fars), 2))] * 2 + [
            pltpu.SemaphoreType.DMA((2, 2)),
            pltpu.VMEM((2, given.shape[0] // (2 * fan), given.shape[1]), given.dtype),
        ]
        if halves is not None:
            operands += list(halves)
            alias = {count + 1: count, count + 2: count + 1}
    return pl.pallas_call(
        functools.partial(swap_kernel, n, fan, count, fars, not fars or halves is None),
        name="swap",
        out_shape=outs,
        in_specs=[pl.BlockSpec(memory_space=pl.ANY)] * len(operands),
        out_specs=[pl.BlockSpec(memory_space=pl.ANY)] * len(outs),
        scratch_shapes=scratch,
        input_output_aliases=alias,
        compiler_params=pltpu.CompilerParams(collective_id=ident, has_side_effects=True),
        cost_estimate=pl.CostEstimate(flops=0, bytes_accessed=size, transcendentals=0),
    )(*operands)


def norm_apply(value, gain):
    return value * lax.rsqrt(jnp.mean(value * value, axis=-1, keepdims=True) + EPS) * gain


def norm_back(value, gain, grad):
    _, pull = jax.vjp(norm_apply, value, gain)
    return pull(grad)


def gate_mix(gate, up):
    return jax.nn.gelu(gate, approximate=True) * up


def counts_below(ids, values):
    total = jnp.zeros_like(values)
    for doc in range(DOCS):
        total = total + jnp.where(values > doc, jnp.sum((ids == doc).astype(jnp.int32)), 0)
    return total


def change_home(value):
    n, fan = lax.axis_size("seq"), lax.axis_size("fsdp")
    pairs = []
    for s in range(n):
        for f in range(fan):
            away = (s // (n // 2) + f) % 2
            target = ((s + n // 2) % n, f ^ 1) if away else (s, f)
            pairs.append((s * fan + f, target[0] * fan + target[1]))
    return lax.ppermute(value, ("seq", "fsdp"), pairs)


def spread(blocks):
    fan, me = lax.axis_size("fsdp"), lax.axis_index("fsdp")
    result = blocks
    for far in range(1, fan):
        block = lax.dynamic_index_in_dim(blocks, (me + far) % fan, 0, True)
        block = lax.ppermute(block, "fsdp", [(f, (f + far) % fan) for f in range(fan)])
        result = lax.dynamic_update_slice_in_dim(result, block, (me - far) % fan, 0)
    return result


def flat(blocks):
    return jnp.transpose(blocks, (1, 0, 2)).reshape(blocks.shape[1], -1)


def by_rows(value):
    return with_layout_constraint(value, Layout(major_to_minor=tuple(range(value.ndim))))


def scatter(grad):
    return lax.psum_scatter(grad, "fsdp", scatter_dimension=0, tiled=True)


def shards(
    layer_in, encoder, decoder_ids, encoder_ids, rel_buckets,
    norm_self, self_qkv, self_out, rel_table, norm_cross, cross_q, cross_kv, cross_out, norm_ff, ff_in, ff_out,
    cotangent,
):
    seqs, local, width = layer_in.shape
    enc_local = encoder.shape[1]
    parts = lax.axis_size("seq")
    heads = self_qkv.shape[1]
    dh = self_qkv.shape[2] // 3
    own = heads // parts
    rows = seqs * local
    buckets, table_own = rel_table.shape
    length, keys = local * parts, enc_local * parts
    gather = lambda v: lax.all_gather(v, "fsdp", axis=0, tiled=True)

    fan = lax.axis_size("fsdp")
    units = ff_in.shape[1] // (2 * fan)
    part = norm_self.shape[0]
    pair, half, rank = team(parts)

    qkv_w = gather(self_qkv)
    small = jnp.concatenate([norm_self, norm_cross, norm_ff, rel_table.reshape(-1)])
    small = lax.all_gather(small, "fsdp", axis=0, tiled=False)
    early = by_rows(jnp.stack([self_out, cross_q, *jnp.split(cross_kv.reshape(-1, 2 * width), 2, axis=1)]))
    small, early = lax.optimization_barrier((small, early))
    early = lax.all_gather(early, "fsdp", axis=1, tiled=True)
    both_ids = jnp.concatenate([decoder_ids.reshape(-1), encoder_ids.reshape(-1)])
    both_ids = change_home(jnp.pad(both_ids, (0, 1024 - local - enc_local)).reshape(8, 128))
    inner_t = ff_in.T
    by_kernel = (width // fan) % 128 == 0 and fan % 2 == 0 and (ff_in.shape[0] // parts) % 8 == 0
    (both_ids,) = swap([jnp.broadcast_to(both_ids[None], (parts, 8, 128))], 13)
    home = change_home(layer_in.reshape(rows, width))
    early = by_rows(early)
    gain_first, gain_second, gain_third = (
        small[:, i * part : (i + 1) * part].reshape(width).astype(f32) for i in range(3)
    )
    table = jnp.transpose(small[:, 3 * part :].reshape(-1, buckets, table_own), (1, 0, 2)).reshape(buckets, heads)
    both_ids = both_ids.reshape(parts, 1024)
    ids = both_ids[:, :local].reshape(length)
    enc_ids = both_ids[:, local : local + enc_local].reshape(keys)

    first_seen = counts_below(ids, ids)
    enc_first = counts_below(enc_ids, ids)
    enc_last = counts_below(enc_ids, ids + 1)
    blocks = length // BQ
    bk = BQ
    self_rows = jnp.broadcast_to(first_seen[None], (8, length))
    cross_rows = jnp.concatenate([enc_first[None], enc_last[None], jnp.zeros((6, length), jnp.int32)])
    self_limits = jnp.stack(
        [first_seen[::BQ] // bk, (jnp.arange(blocks, dtype=jnp.int32) + 1) * (BQ // bk)]
    )
    cross_limits = jnp.stack([enc_first[::BQ] // bk, (enc_last[BQ - 1 :: BQ] + bk - 1) // bk])

    first_head = rank * own
    table_mine = lax.dynamic_slice_in_dim(table.astype(f32), first_head, own, 1)
    near = rel_buckets[:REACH]
    onehot = (near[:, None] == jnp.arange(buckets, dtype=jnp.int32)[None, :]).astype(f32)
    bias = jnp.einsum("ln,ng->gl", onehot, table_mine, precision=HIGH)
    ext = jnp.concatenate(
        [jnp.full((own, BQ), MASKED, f32), bias, jnp.zeros((own, BQ), f32)], axis=1
    )

    qkv_w, home, inner_t, ext, self_rows, cross_rows, self_limits, cross_limits = lax.optimization_barrier(
        (qkv_w, home, inner_t, ext, self_rows, cross_rows, self_limits, cross_limits)
    )
    qkv_w = qkv_w.reshape(width, parts, own * 3 * dh)

    stream = home.astype(f32)
    normed_first = norm_apply(stream, gain_first).astype(bf16)
    qkv_tok = jnp.einsum("td,dge->gte", normed_first, qkv_w, preferred_element_type=f32).astype(bf16)
    others = change_home(jnp.concatenate([cotangent.reshape(rows, width), encoder.reshape(-1, width)]))
    grad_low, enc_flat = others[:rows], others[rows:]
    fars = [tuple(far for far in range(fan) if by_kernel and min(far, 3) in some) for some in ((2,), (0, 1), (3,))]
    qkv, *halves = swap([qkv_tok], 17, fars[0], inner_t)
    qkv, cross_out, grad_low = lax.optimization_barrier((qkv, cross_out, grad_low))
    if rows == cross_out.shape[0]:
        mix_cross, grad_group = lax.all_gather(jnp.stack([cross_out, grad_low]), "fsdp", axis=1, tiled=True)
    else:
        mix_cross, grad_group = gather(cross_out), gather(grad_low)
    mix_cross = mix_cross.reshape(parts, own * dh, width)
    qkv = qkv.reshape(length, own * 3 * dh)
    out_self, self_t, self_lse = self_forward(self_limits, self_rows, ext, qkv)
    (self_tok,) = swap([out_self.reshape(parts, local, own * dh)], 11)
    after_self, normed_second, query_tok, pairs_tok = over_weights(
        into_kernel,
        "self_out_to_cross",
        [self_tok, home, gain_second.reshape(1, width), enc_flat],
        early,
        lambda i: i,
        [
            ((rows, width), f32),
            ((rows, width), bf16),
            ((parts, rows, own * dh), bf16),
            ((parts, enc_local, own * 2 * dh), bf16),
        ],
    )
    query_cross, pairs, *halves = swap([query_tok, pairs_tok], 15, fars[1], inner_t, halves)
    query_cross, pairs = query_cross.reshape(length, own * dh), pairs.reshape(keys, own * 2 * dh)
    out_cross, cross_t, cross_lse = cross_forward(cross_limits, cross_rows, query_cross, pairs)
    cross_tok, *halves = swap([out_cross.reshape(parts, local, own * dh)], 16, fars[2], inner_t, halves)
    if not by_kernel:
        halves = spread(jnp.transpose(inner_t.reshape(2, fan, units, -1), (1, 0, 2, 3)))
        halves = [jnp.transpose(halves[:, i], (1, 0, 2)).reshape(units, width) for i in range(2)]
    gate_t, up_t = halves
    after_cross = after_self + jnp.einsum("gtc,gcd->td", cross_tok, mix_cross, preferred_element_type=f32)
    normed_third = norm_apply(after_cross, gain_third).astype(bf16)
    normed_group = gather(normed_third)
    gate = jnp.einsum("td,fd->tf", normed_group, gate_t, preferred_element_type=f32)
    up = jnp.einsum("td,fd->tf", normed_group, up_t, preferred_element_type=f32)
    hidden = gate_mix(gate, up).astype(bf16)

    grad_hidden = jnp.einsum("td,fd->tf", grad_group, ff_out, preferred_element_type=f32)
    _, pull_mix = jax.vjp(gate_mix, gate, up)
    grad_gate, grad_up = (g.astype(bf16) for g in pull_mix(grad_hidden))
    grad_third_in = jnp.dot(grad_gate, gate_t, preferred_element_type=f32) + jnp.dot(
        grad_up, up_t, preferred_element_type=f32
    )
    grad_third_in = scatter(grad_third_in.astype(bf16))
    outer_part = jnp.dot(hidden, ff_out, preferred_element_type=f32).astype(bf16)
    grad_units = [
        jnp.einsum("tf,td->fd", g, y, preferred_element_type=f32).astype(bf16)
        for g, y in ((grad_gate, normed_group), (grad_up, normed_group), (hidden, grad_group))
    ]
    if by_kernel:
        grad_units = jnp.stack([g.reshape(parts, units // parts, width) for g in grad_units], axis=1)
        grad_units = grad_units.reshape(3 * units, width)
    grad_third_in, outer_part, part_units = lax.optimization_barrier((grad_third_in, outer_part, grad_units))
    grad_third_in = grad_third_in.astype(f32)
    grad_from_third, grad_gain_third = norm_back(after_cross, gain_third, grad_third_in)
    grad_middle = grad_low.astype(f32) + grad_from_third
    middle_low = grad_middle.astype(bf16)
    grad_mix_cross = jnp.einsum("gtc,td->gcd", cross_tok, middle_low, preferred_element_type=f32)
    part_cross = scatter(grad_mix_cross.reshape(width, width).astype(bf16))
    grad_cross_tok = jnp.einsum("td,gcd->gtc", middle_low, mix_cross, preferred_element_type=f32).astype(bf16)
    (grad_cross,) = swap([grad_cross_tok], 11)
    grad_cross = grad_cross.reshape(length, own * dh)
    grad_query, grad_pairs = cross_backward(
        cross_limits, cross_rows, query_cross, pairs, grad_cross, cross_t, cross_lse
    )
    grad_query_tok, grad_pairs_tok = swap(
        [grad_query.reshape(parts, local, own * dh), grad_pairs.reshape(parts, enc_local, own * 2 * dh)], 12
    )
    (
        grad_upper, upper_low, grad_self_tok, grad_gain_second, grad_encoder, grad_query_tok, grad_pairs_tok
    ) = over_weights(
        outof_kernel,
        "cross_to_self_out",
        [grad_query_tok, grad_pairs_tok, after_self, gain_second.reshape(1, width), grad_middle],
        early,
        lambda i: jnp.where(i < 2, 1 - i, i),
        [
            ((rows, width), f32),
            ((rows, width), bf16),
            ((parts, rows, own * dh), bf16),
            ((1, width), f32),
            ((enc_local, width), bf16),
            ((rows, width), bf16),
            ((enc_local, 2 * width), bf16),
        ],
        [((enc_local, width), f32)],
    )
    grad_query_w = jnp.einsum("td,te->de", normed_second, grad_query_tok, preferred_element_type=f32)
    grad_pairs_w = jnp.einsum("td,te->de", enc_flat, grad_pairs_tok, preferred_element_type=f32)
    grad_mix_self = jnp.einsum("gtc,td->gcd", self_tok, upper_low, preferred_element_type=f32)
    grad_mid = jnp.concatenate(
        [
            grad_query_w.astype(bf16),
            grad_pairs_w.astype(bf16),
            grad_mix_self.reshape(width, width).astype(bf16),
        ],
        axis=1,
    )
    grad_self_tok, grad_mid = lax.optimization_barrier((grad_self_tok, grad_mid))
    part_mid = scatter(grad_mid)
    (grad_self,) = swap([grad_self_tok], 11)
    grad_self = grad_self.reshape(length, own * dh)
    grad_qkv, diagonals = self_backward(self_limits, self_rows, ext, qkv, grad_self, self_t, self_lse)
    (grad_qkv_tok,) = swap([grad_qkv.reshape(parts, local, own * 3 * dh)], 10)
    grad_qkv_tok = flat(grad_qkv_tok)
    grad_qkv_w = jnp.einsum("td,te->de", normed_first, grad_qkv_tok, preferred_element_type=f32)
    grad_qkv_w, grad_qkv_tok = lax.optimization_barrier((grad_qkv_w.astype(bf16), grad_qkv_tok))
    grad_first_in = jnp.einsum("te,de->td", grad_qkv_tok, qkv_w.reshape(width, -1), preferred_element_type=f32)
    grad_from_first, grad_gain_first = norm_back(stream, gain_first, grad_first_in)
    grad_layer_in = (grad_upper + grad_from_first).astype(bf16)
    bucket_line = jnp.concatenate([jnp.full((BQ - 1,), -1, jnp.int32), near, jnp.full((BQ + 1,), -1, jnp.int32)])
    in_bucket = (bucket_line[:, None] == jnp.arange(buckets, dtype=jnp.int32)).astype(f32)
    by_bucket = jnp.einsum("xn,gx->ng", in_bucket, diagonals, precision=HIGH)
    grad_table = lax.dynamic_update_slice_in_dim(jnp.zeros((buckets, heads), f32), by_bucket, first_head, 1)

    gains = jnp.concatenate(
        [g.reshape(-1, part) for g in (grad_gain_first, grad_gain_second, grad_gain_third)], axis=1
    )
    tables = jnp.transpose(grad_table.reshape(buckets, -1, table_own), (1, 0, 2)).reshape(-1, buckets * table_own)
    small_grads = jnp.concatenate([gains, tables], axis=1).astype(bf16)
    small_size = small_grads.shape[1]
    going_home = jnp.concatenate([grad_layer_in, grad_encoder.astype(bf16)])
    part_last = scatter(grad_qkv_w)
    going_home, small_grads, part_units, part_cross, part_mid = lax.optimization_barrier(
        (change_home(going_home), small_grads, part_units, part_cross, part_mid)
    )
    if by_kernel:
        few = jnp.pad(small_grads[:, None], ((0, 0), (0, 7), (0, 1024 - small_size))).reshape(fan * 8, 1024)
        total_inner, total_outer, outer_sum, few = units_total(part_units, outer_part, few, 0)
        few = jnp.pad(few[0].astype(bf16).reshape(8, 128), ((0, parts * 8 - 8), (0, 0)))
        total_cross, total_mid, total_qkv, small_total, total_inner = ring_total(
            [part_cross, part_mid, part_last, few], (2, 2, 2, 1), 1, total_inner
        )
    else:
        grad_units = [lax.psum(g, "seq") for g in part_units]
        total_inner = spread(jnp.transpose(jnp.stack(grad_units[:2]).reshape(2, units, fan, -1), (2, 0, 1, 3)))
        total_inner = jnp.transpose(total_inner, (3, 1, 0, 2)).reshape(-1, 2 * fan * units).astype(f32)
        total_outer, outer_sum = grad_units[2], scatter(outer_part).astype(f32)
        few = lax.dynamic_index_in_dim(lax.psum(small_grads, "fsdp"), lax.axis_index("fsdp"), 0, False)
        total_cross, total_mid, total_qkv, small_total = (
            lax.psum(v, "seq") for v in (part_cross, part_mid, part_last, few)
        )
    layer_out = (after_cross + outer_sum).astype(bf16)
    layer_out, total_inner, total_outer, total_cross, total_mid, total_qkv, going_home = lax.optimization_barrier(
        (layer_out, total_inner, total_outer, total_cross, total_mid, total_qkv, going_home)
    )
    layer_out = change_home(layer_out).reshape(seqs, local, width)
    grad_layer_in = going_home[:rows].astype(f32).reshape(seqs, local, width)
    grad_encoder = going_home[rows:].astype(f32).reshape(seqs, enc_local, width)
    total_inner, total_outer, total_mid, total_qkv = (
        v.astype(f32) for v in (total_inner, total_outer, total_mid, total_qkv)
    )
    total_query, total_mix_cross = total_mid[:, :width], total_cross.astype(f32)
    total_pairs = total_mid[:, width : 3 * width].reshape(-1, heads, 2 * dh)
    total_mix_self, total_qkv = total_mid[:, 3 * width :], total_qkv.reshape(-1, heads, 3 * dh)
    mine = small_total.reshape(-1)[:small_size].astype(f32)
    total_gain_first, total_gain_second, total_gain_third = (mine[i * part : (i + 1) * part] for i in range(3))
    total_table = mine[3 * part :].reshape(buckets, table_own)
    return (
        layer_out, grad_layer_in, grad_encoder, total_gain_first, total_qkv, total_mix_self, total_table,
        total_gain_second, total_query, total_pairs, total_mix_cross, total_gain_third, total_inner, total_outer,
    )


def solution(mesh):
    in_specs = (
        P("fsdp", "seq", None), P("fsdp", "seq", None), P("fsdp", "seq"), P("fsdp", "seq"), P(),
        P("fsdp"), P("fsdp", None, None), P("fsdp", None), P(None, "fsdp"), P("fsdp"), P("fsdp", None),
        P("fsdp", None, None), P("fsdp", None), P("fsdp"), P("fsdp", None), P("fsdp", None),
        P("fsdp", "seq", None),
    )
    out_specs = (
        P("fsdp", "seq", None), P("fsdp", "seq", None), P("fsdp", "seq", None), P("fsdp"), P("fsdp", None, None),
        P("fsdp", None), P(None, "fsdp"), P("fsdp"), P("fsdp", None), P("fsdp", None, None), P("fsdp", None),
        P("fsdp"), P("fsdp", None), P("fsdp", None),
    )
    return jax.shard_map(shards, mesh=mesh, in_specs=in_specs, out_specs=out_specs, check_vma=False)
```

```python
import functools

import jax
import jax.numpy as jnp
from jax import lax
from jax.experimental import pallas as pl
from jax.experimental.layout import Layout, with_layout_constraint
from jax.experimental.pallas import tpu as pltpu
from jax.sharding import PartitionSpec as P

EPS = 1e-06
HIGH = lax.Precision.HIGHEST
MASKED = -1e30
DOCS = 4

BQ = 256
REACH = 1024


def blk(index, size):
    return pl.ds(pl.multiple_of(index * size, size), size)


def turn(value):
    return jnp.transpose(value.astype(jnp.float32), (1, 0))


def bias_tiles(ext_ref, tile_ref, own):
    for h in range(own):
        line = jnp.broadcast_to(ext_ref[h : h + 1, :], tile_ref.shape[1:])
        tile_ref[h] = pltpu.roll(line, 0, 1, stride=1, stride_axis=0)


def unpack(ref, own, width, picks, flips, base):
    block = 256

    def one(b, _):
        rows = blk(b, block)
        value = ref[rows, :]
        if flips:
            flat = turn(value).astype(jnp.bfloat16)
            for target, piece in flips:
                for h in range(own):
                    at = h * width + piece * 64
                    target[base + h, :, rows] = flat[at : at + 64]
        for target, piece in picks:
            for h in range(own):
                at = h * width + piece * 64
                target[base + h, rows, :] = value[:, at : at + 64]
        return 0

    lax.fori_loop(0, ref.shape[0] // block, one, 0)


def dot(a, b):
    return jnp.dot(a, b, preferred_element_type=jnp.float32)


def score(own_index, key_tile, query_t, tile_ref, t, low, high, first_key):
    value = dot(key_tile, query_t)
    place = lax.broadcasted_iota(jnp.int32, value.shape, 0)
    keep = place >= low - first_key
    if high is not None:
        keep = keep & (place < high - first_key)
    else:
        value = value + tile_ref[own_index, :, blk(t + 1, BQ)]
    return jnp.where(keep, value, MASKED)


def forward_body(own, bk, causal, lim_ref, rows_ref, q_t, k_rows, v_t, tile_ref, o_ref, ot_ref, lse_ref):
    length = o_ref.shape[0]

    def q_block(i, _):
        cols = blk(i, BQ)
        queries = [q_t[h, :, cols] for h in range(own)]
        low = rows_ref[0:1, cols]
        high = None if causal else rows_ref[1:2, cols]

        def k_block(j, carry):
            keys = blk(j, bk)
            t = i - j
            out = []
            for h in range(own):
                top, total, acc = carry[h]
                s = score(h, k_rows[h, keys, :], queries[h], tile_ref, t, low, high, j * bk)
                new_top = jnp.maximum(top, jnp.max(s, axis=0, keepdims=True))
                p = jnp.exp(s - new_top)
                scale = jnp.exp(top - new_top)
                total = total * scale + jnp.sum(p, axis=0, keepdims=True)
                acc = acc * scale + dot(v_t[h, :, keys], p.astype(jnp.bfloat16))
                out.append((new_top, total, acc))
            return tuple(out)

        start = tuple(
            (
                jnp.full((1, BQ), MASKED, jnp.float32),
                jnp.zeros((1, BQ), jnp.float32),
                jnp.zeros((64, BQ), jnp.float32),
            )
            for _ in range(own)
        )
        ends = lax.fori_loop(lim_ref[0, i], lim_ref[1, i], k_block, start)
        for h in range(own):
            top, total, acc = ends[h]
            ot_ref[h * 64 : h * 64 + 64, cols] = acc / total
            lse_ref[h : h + 1, cols] = top + jnp.log(total)
        o_ref[cols, :] = turn(ot_ref[:, cols]).astype(jnp.bfloat16)
        return 0

    lax.fori_loop(0, length // BQ, q_block, 0)


def self_forward_kernel(own, bk, lim_ref, rows_ref, ext_ref, x_ref, o_ref, ot_ref, lse_ref, q_t, k_rows, v_t, tile_ref):
    bias_tiles(ext_ref, tile_ref, own)
    unpack(x_ref, own, 192, [(k_rows, 1)], [(q_t, 0), (v_t, 2)], 0)
    forward_body(own, bk, True, lim_ref, rows_ref, q_t, k_rows, v_t, tile_ref, o_ref, ot_ref, lse_ref)


def cross_forward_kernel(own, bk, lim_ref, rows_ref, q_ref, kv_ref, o_ref, ot_ref, lse_ref, q_t, k_rows, v_t):
    unpack(q_ref, own, 64, [], [(q_t, 0)], 0)
    unpack(kv_ref, own, 128, [(k_rows, 0)], [(v_t, 1)], 0)
    forward_body(own, bk, False, lim_ref, rows_ref, q_t, k_rows, v_t, None, o_ref, ot_ref, lse_ref)


def backward_body(
    own, bk, causal, lim_ref, rows_ref, do_ref, ot_ref, lse_ref,
    q_t, q_rows, k_t, k_rows, v_rows, do_t, do_rows, tile_ref, sum_ref, dq_t, dk, dv,
):
    length = do_ref.shape[0]
    dk[...] = jnp.zeros_like(dk)
    dv[...] = jnp.zeros_like(dv)
    if causal:
        sum_ref[...] = jnp.zeros_like(sum_ref)

    def q_block(i, _):
        cols = blk(i, BQ)
        low = rows_ref[0:1, cols]
        high = None if causal else rows_ref[1:2, cols]
        per_head = []
        for h in range(own):
            grad_t = do_t[h, :, cols]
            delta = jnp.sum(
                grad_t.astype(jnp.float32) * ot_ref[h * 64 : h * 64 + 64, cols], axis=0, keepdims=True
            )
            per_head.append((q_t[h, :, cols], grad_t, delta, lse_ref[h : h + 1, cols]))

        def k_block(j, carry):
            keys = blk(j, bk)
            t = i - j
            out = []
            for h in range(own):
                query_t, grad_t, delta, lse = per_head[h]
                s = score(h, k_rows[h, keys, :], query_t, tile_ref, t, low, high, j * bk)
                p = jnp.exp(s - lse)
                dp = dot(v_rows[h, keys, :], grad_t)
                ds = (p * (dp - delta)).astype(jnp.bfloat16)
                dv[h, keys, :] += dot(p.astype(jnp.bfloat16), do_rows[h, cols, :])
                dk[h, keys, :] += dot(ds, q_rows[h, cols, :])
                if causal:
                    sum_ref[h, :, blk(t, BQ)] += ds.astype(jnp.float32)
                out.append(carry[h] + dot(k_t[h, :, keys], ds))
            return tuple(out)

        ends = lax.fori_loop(
            lim_ref[0, i],
            lim_ref[1, i],
            k_block,
            tuple(jnp.zeros((64, BQ), jnp.float32) for _ in range(own)),
        )
        for h in range(own):
            dq_t[h * 64 : h * 64 + 64, cols] = ends[h]
        return 0

    lax.fori_loop(0, length // BQ, q_block, 0)


def diagonal_sums(sum_ref, u_ref, own):
    flip = lax.broadcasted_iota(jnp.int32, (BQ, BQ), 0) + lax.broadcasted_iota(jnp.int32, (BQ, BQ), 1) == BQ - 1
    flip = jnp.where(flip, 1.0, 0.0).astype(jnp.bfloat16)
    for h in range(own):
        grid = sum_ref[h]
        high = grid.astype(jnp.bfloat16)
        low = (grid - high.astype(jnp.float32)).astype(jnp.bfloat16)
        upside = dot(flip, high) + dot(flip, low)
        wide = jnp.concatenate([upside, jnp.zeros((BQ, BQ), jnp.float32)], axis=1)
        aligned = pltpu.roll(wide, 0, 1, stride=1, stride_axis=0)
        u_ref[h : h + 1, :] = jnp.sum(aligned, axis=0, keepdims=True)


def self_backward_kernel(
    own, bk, lim_ref, rows_ref, ext_ref, x_ref, do_ref, ot_ref, lse_ref, dx_ref, u_ref,
    q_t, q_rows, k_t, k_rows, v_rows, do_t, do_rows, tile_ref, sum_ref, dq_t, dk, dv,
):
    bias_tiles(ext_ref, tile_ref, own)
    unpack(x_ref, own, 192, [(q_rows, 0), (k_rows, 1), (v_rows, 2)], [(q_t, 0), (k_t, 1)], 0)
    unpack(do_ref, own, 64, [(do_rows, 0)], [(do_t, 0)], 0)
    backward_body(
        own, bk, True, lim_ref, rows_ref, do_ref, ot_ref, lse_ref,
        q_t, q_rows, k_t, k_rows, v_rows, do_t, do_rows, tile_ref, sum_ref, dq_t, dk, dv,
    )
    diagonal_sums(sum_ref, u_ref, own)

    def pack(b, _):
        rows = blk(b, 256)
        dq = turn(dq_t[:, rows])
        pieces = []
        for h in range(own):
            pieces += [dq[:, h * 64 : h * 64 + 64], dk[h, rows, :], dv[h, rows, :]]
        dx_ref[rows, :] = jnp.concatenate(pieces, axis=1).astype(jnp.bfloat16)
        return 0

    lax.fori_loop(0, x_ref.shape[0] // 256, pack, 0)


def cross_backward_kernel(
    own, bk, lim_ref, rows_ref, q_ref, kv_ref, do_ref, ot_ref, lse_ref, dq_ref, dkv_ref,
    q_t, q_rows, k_t, k_rows, v_rows, do_t, do_rows, dq_t, dk, dv,
):
    unpack(q_ref, own, 64, [(q_rows, 0)], [(q_t, 0)], 0)
    unpack(kv_ref, own, 128, [(k_rows, 0), (v_rows, 1)], [(k_t, 0)], 0)
    unpack(do_ref, own, 64, [(do_rows, 0)], [(do_t, 0)], 0)
    backward_body(
        own, bk, False, lim_ref, rows_ref, do_ref, ot_ref, lse_ref,
        q_t, q_rows, k_t, k_rows, v_rows, do_t, do_rows, None, None, dq_t, dk, dv,
    )

    def pack_q(b, _):
        rows = blk(b, 256)
        dq_ref[rows, :] = turn(dq_t[:, rows]).astype(jnp.bfloat16)
        return 0

    def pack_kv(b, _):
        rows = blk(b, 256)
        pieces = []
        for h in range(own):
            pieces += [dk[h, rows, :], dv[h, rows, :]]
        dkv_ref[rows, :] = jnp.concatenate(pieces, axis=1).astype(jnp.bfloat16)
        return 0

    lax.fori_loop(0, q_ref.shape[0] // 256, pack_q, 0)
    lax.fori_loop(0, kv_ref.shape[0] // 256, pack_kv, 0)


SMEM = pl.BlockSpec(memory_space=pltpu.SMEM)
VMEM = pl.BlockSpec(memory_space=pltpu.VMEM)
bf16, f32 = jnp.bfloat16, jnp.float32


def call(body, name, operands, outs, scratch, flops):
    size = sum(v.size * v.dtype.itemsize for v in operands)
    return pl.pallas_call(
        body,
        name=name,
        out_shape=[jax.ShapeDtypeStruct(s, d) for s, d in outs],
        in_specs=[SMEM] + [VMEM] * (len(operands) - 1),
        out_specs=[VMEM] * len(outs),
        scratch_shapes=[pltpu.VMEM(s, d) for s, d in scratch],
        compiler_params=pltpu.CompilerParams(vmem_limit_bytes=40 << 20),
        cost_estimate=pl.CostEstimate(flops=0, bytes_accessed=size, transcendentals=0),
    )(*operands)


def self_forward(limits, rows, ext, x, bk=BQ):
    length, own = x.shape[0], x.shape[1] // 192
    return call(
        functools.partial(self_forward_kernel, own, bk),
        "self_forward",
        [limits, rows, ext, x],
        [((length, own * 64), bf16), ((own * 64, length), f32), ((own, length), f32)],
        [
            ((own, 64, length), bf16),
            ((own, length, 64), bf16),
            ((own, 64, length), bf16),
            ((own, BQ, REACH + 2 * BQ), f32),
        ],
        length * length * own * 64,
    )


def cross_forward(limits, rows, q, kv, bk=BQ):
    length, own, keys = q.shape[0], q.shape[1] // 64, kv.shape[0]
    return call(
        functools.partial(cross_forward_kernel, own, bk),
        "cross_forward",
        [limits, rows, q, kv],
        [((length, own * 64), bf16), ((own * 64, length), f32), ((own, length), f32)],
        [((own, 64, length), bf16), ((own, keys, 64), bf16), ((own, 64, keys), bf16)],
        length * keys * own * 128,
    )


def self_backward(limits, rows, ext, x, grad, o_t, lse, bk=BQ):
    length, own = x.shape[0], x.shape[1] // 192
    return call(
        functools.partial(self_backward_kernel, own, bk),
        "self_backward",
        [limits, rows, ext, x, grad, o_t, lse],
        [((length, own * 192), bf16), ((own, REACH + 2 * BQ), f32)],
        [
            ((own, 64, length), bf16),
            ((own, length, 64), bf16),
            ((own, 64, length), bf16),
            ((own, length, 64), bf16),
            ((own, length, 64), bf16),
            ((own, 64, length), bf16),
            ((own, length, 64), bf16),
            ((own, BQ, REACH + 2 * BQ), f32),
            ((own, BQ, REACH + BQ), f32),
            ((own * 64, length), f32),
            ((own, length, 64), f32),
            ((own, length, 64), f32),
        ],
        length * length * own * 160,
    )


def cross_backward(limits, rows, q, kv, grad, o_t, lse, bk=BQ):
    length, own, keys = q.shape[0], q.shape[1] // 64, kv.shape[0]
    return call(
        functools.partial(cross_backward_kernel, own, bk),
        "cross_backward",
        [limits, rows, q, kv, grad, o_t, lse],
        [((length, own * 64), bf16), ((keys, own * 128), bf16)],
        [
            ((own, 64, length), bf16),
            ((own, length, 64), bf16),
            ((own, 64, keys), bf16),
            ((own, keys, 64), bf16),
            ((own, keys, 64), bf16),
            ((own, 64, length), bf16),
            ((own, length, 64), bf16),
            ((own * 64, length), f32),
            ((own, keys, 64), f32),
            ((own, keys, 64), f32),
        ],
        length * keys * own * 320,
    )


def rows_of(blocks_ref):
    return jnp.concatenate([blocks_ref[g] for g in range(blocks_ref.shape[0])], axis=1)


def against(a, b):
    return lax.dot_general(a, b, (((1,), (1,)), ((), ())), preferred_element_type=jnp.float32)


def into_kernel(tok_ref, home_ref, gain_ref, enc_ref, w_ref, after_ref, norm_ref, query_ref, pairs_ref):
    which = pl.program_id(0)

    @pl.when(which == 0)
    def _():
        value = home_ref[...].astype(jnp.float32) + dot(rows_of(tok_ref), w_ref[0])
        after_ref[...] = value
        scale = lax.rsqrt(jnp.mean(value * value, axis=1, keepdims=True) + EPS)
        norm_ref[...] = (value * scale * gain_ref[...]).astype(jnp.bfloat16)

    @pl.when(which == 1)
    def _():
        query = dot(norm_ref[...], w_ref[0]).astype(jnp.bfloat16)
        cols = query_ref.shape[2]
        for g in range(query_ref.shape[0]):
            query_ref[g] = query[:, g * cols : (g + 1) * cols]

    for half in range(2):

        @pl.when(which == 2 + half)
        def _():
            pairs = dot(enc_ref[...], w_ref[0]).astype(jnp.bfloat16)
            groups, cols = pairs_ref.shape[0] // 2, pairs_ref.shape[2]
            for g in range(groups):
                pairs_ref[half * groups + g] = pairs[:, g * cols : (g + 1) * cols]


def outof_kernel(
    dq_ref, dkv_ref, after_ref, gain_ref, middle_ref, w_ref,
    upper_ref, low_ref, out_ref, gain_grad_ref, enc_grad_ref, dq_flat_ref, dkv_flat_ref, enc_sum,
):
    which = pl.program_id(0)

    @pl.when(which == 0)
    def _():
        grad_query = rows_of(dq_ref)
        dq_flat_ref[...] = grad_query
        dkv_flat_ref[...] = rows_of(dkv_ref)
        grad = against(grad_query, w_ref[0])
        value = after_ref[...]
        unit = value * lax.rsqrt(jnp.mean(value * value, axis=1, keepdims=True) + EPS)
        gain_grad_ref[...] = jnp.sum(grad * unit, axis=0, keepdims=True)
        scale = lax.rsqrt(jnp.mean(value * value, axis=1, keepdims=True) + EPS)
        grad = grad * gain_ref[...]
        inner = jnp.mean(grad * unit, axis=1, keepdims=True)
        upper = middle_ref[...] + scale * (grad - unit * inner)
        upper_ref[...] = upper
        low_ref[...] = upper.astype(jnp.bfloat16)

    @pl.when(which == 1)
    def _():
        grad = against(low_ref[...], w_ref[0]).astype(jnp.bfloat16)
        cols = out_ref.shape[2]
        for g in range(out_ref.shape[0]):
            out_ref[g] = grad[:, g * cols : (g + 1) * cols]

    width = w_ref.shape[1]

    @pl.when(which == 2)
    def _():
        enc_sum[...] = against(dkv_flat_ref[:, :width], w_ref[0])

    @pl.when(which == 3)
    def _():
        enc_grad_ref[...] = (enc_sum[...] + against(dkv_flat_ref[:, width:], w_ref[0])).astype(jnp.bfloat16)


def over_weights(body, name, arrays, weights, order, outs, scratch=()):
    count, rows, cols = weights.shape
    whole = lambda shape: pl.BlockSpec(shape, lambda i: (0,) * len(shape))
    return pl.pallas_call(
        body,
        name=name,
        grid=(count,),
        out_shape=[jax.ShapeDtypeStruct(s, d) for s, d in outs],
        in_specs=[whole(v.shape) for v in arrays] + [pl.BlockSpec((1, rows, cols), lambda i: (order(i), 0, 0))],
        out_specs=[whole(s) for s, _ in outs],
        scratch_shapes=[pltpu.VMEM(s, d) for s, d in scratch],
        compiler_params=pltpu.CompilerParams(vmem_limit_bytes=40 << 20, dimension_semantics=("arbitrary",)),
        cost_estimate=pl.CostEstimate(flops=0, bytes_accessed=weights.size * 2, transcendentals=0),
    )(*arrays, weights)


MESH = pl.DeviceIdType.MESH


def ring_place(index, n):
    z, x = index // 2, index % 2
    return z + x * (n - 1 - 2 * z)


def ring_index(place, n):
    x = place // (n // 2)
    z = place + x * (n - 1 - 2 * place)
    return 2 * z + x


def ring_greet(n, others):
    place = ring_place(lax.axis_index("seq"), n)
    right = ring_index((place + 1) % n, n)
    left = ring_index((place + n - 1) % n, n)
    barrier = pltpu.get_barrier_semaphore()
    for neighbour in (left, right):
        pl.semaphore_signal(barrier, inc=1, device_id={"seq": neighbour}, device_id_type=MESH)
    for other in others:
        pl.semaphore_signal(barrier, inc=1, device_id={"fsdp": other}, device_id_type=MESH)
    pl.semaphore_wait(barrier, 2 + len(others))
    return place, right, left


def ring_cut(shape, split, n):
    rows, cols = shape[0] // n, shape[1]
    return (rows, cols // split) if split > 0 else (rows // -split, cols)


def ring_window(ref, shape, split, n, piece, chunk):
    whole = shape[0] // n
    rows, cols = ring_cut(shape, split, n)
    if split > 0:
        return ref.at[pl.ds(chunk * whole, rows), pl.ds(piece * cols, cols)]
    return ref.at[pl.ds(chunk * whole + piece * rows, rows), :]


def ring_kernel(n, splits, fan, *refs):
    count = len(splits)
    more = 1 if fan else 0
    x_refs, y_refs = refs[:count], refs[count + more : 2 * count + more]
    slots = refs[2 * (count + more) : 3 * count + 2 * more]
    send_sem, recv_sem = refs[3 * count + 2 * more :]
    place, right, left = ring_greet(n, [])
    streams = [(k, piece, piece % 2) for k in range(count) for piece in range(abs(splits[k]))]

    def window(ref, k, piece, chunk):
        return ring_window(ref, x_refs[k].shape, splits[k], n, piece, chunk)

    def chunk_at(down, step):
        return (place + 1 + step) % n if down else (place + 2 * n - 1 - step) % n

    copies = {}

    def start(number, step, src, dst, down):
        copies[number, step] = pltpu.make_async_remote_copy(
            src_ref=src,
            dst_ref=dst,
            send_sem=send_sem.at[number, step],
            recv_sem=recv_sem.at[number, step],
            device_id={"seq": left if down else right},
            device_id_type=MESH,
        )
        copies[number, step].start()

    def turn_block(number):
        inner_ref, turned_ref = refs[count], refs[2 * count + 1]
        rows = inner_ref.shape[0] // (2 * fan * n)
        half, first = number // (fan // 2), number % (fan // 2) * 2
        tall = jnp.concatenate(
            [
                inner_ref[pl.ds(((chunk * fan + group) * 2 + half) * rows, rows), :].astype(jnp.float32)
                for group in (first, first + 1)
                for chunk in range(n)
            ]
        )
        wide = 2 * n * rows
        turned_ref[:, number * wide : (number + 1) * wide] = jnp.transpose(tall, (1, 0)).astype(jnp.bfloat16)

    for number, (k, piece, down) in enumerate(streams):
        start(number, 0, window(x_refs[k], k, piece, place), window(slots[k], k, piece, 0), down)
    for step in range(n - 1):
        if step < fan:
            turn_block(step)
        for number, (k, piece, down) in enumerate(streams):
            copies[number, step].wait_recv()
            chunk = chunk_at(down, step)
            mine = window(x_refs[k], k, piece, chunk)
            landed = window(slots[k], k, piece, step)
            total = landed[...].astype(jnp.float32) + mine[...].astype(jnp.float32)
            if step < n - 2:
                landed[...] = total.astype(jnp.bfloat16)
                start(number, step + 1, landed, window(slots[k], k, piece, step + 1), down)
            else:
                done = window(y_refs[k], k, piece, chunk)
                done[...] = total.astype(jnp.bfloat16)
                start(number, n - 1, done, done, down)
    for step in range(n - 1):
        for number, (k, piece, down) in enumerate(streams):
            copies[number, n - 1 + step].wait_recv()
            if step < n - 2:
                done = window(y_refs[k], k, piece, chunk_at(down, n - 1 + step))
                start(number, n + step, done, done, down)
    for one in copies.values():
        one.wait_send()


def ring_call(body, name, arrays, outs, scratch, ident):
    size = sum(v.size * 2 for v in arrays)
    return pl.pallas_call(
        body,
        name=name,
        out_shape=[jax.ShapeDtypeStruct(s, d) for s, d in outs],
        in_specs=[pl.BlockSpec(memory_space=pltpu.VMEM)] * len(arrays),
        out_specs=[pl.BlockSpec(memory_space=pltpu.VMEM)] * len(outs),
        scratch_shapes=scratch,
        compiler_params=pltpu.CompilerParams(
            collective_id=ident, has_side_effects=True, vmem_limit_bytes=48 << 20
        ),
        cost_estimate=pl.CostEstimate(flops=0, bytes_accessed=60 * size, transcendentals=0),
    )(*arrays)


def ring_total(arrays, splits, ident, inner=None):
    n, fan = lax.axis_size("seq"), lax.axis_size("fsdp")
    streams = sum(abs(s) for s in splits)
    more = [] if inner is None else [inner]
    return ring_call(
        functools.partial(ring_kernel, n, splits, 0 if inner is None else fan),
        "ring_total",
        arrays + more,
        [(v.shape, jnp.bfloat16) for v in arrays] + [(v.shape[::-1], jnp.bfloat16) for v in more],
        [pltpu.VMEM((v.shape[0] // n * (n - 1), v.shape[1]), jnp.bfloat16) for v in arrays]
        + [pltpu.SemaphoreType.DMA((streams, 2 * n - 2))] * 2,
        ident,
    )


def units_kernel(
    n, fan, x_ref, part_ref, few_ref, inner_ref, outer_ref, sum_ref, few_sum_ref, slots, acc, landed, few_landed,
    down_send, down_recv, swap_send, swap_recv, own_sem, send_sem, recv_sem, part_send, part_recv,
):
    s, me = lax.axis_index("seq"), lax.axis_index("fsdp")
    rows, width = acc.shape[0] // 3, x_ref.shape[1]
    cols = width // fan
    block = 2 * fan * rows
    place, right, left = ring_greet(n, [(me + far) % fan for far in range(1, fan)])
    sums = {}

    def piece_of(ref, at, piece):
        return ref.at[pl.ds(at * 3 * rows, 3 * rows), pl.ds(piece * cols, cols)]

    def send_sum(piece, step, src):
        to = left if piece >= fan // 2 else right
        sums[piece, step] = pltpu.make_async_remote_copy(
            src_ref=src,
            dst_ref=piece_of(slots, step, piece),
            send_sem=down_send.at[piece, step],
            recv_sem=down_recv.at[piece, step],
            device_id={"seq": to},
            device_id_type=MESH,
        )
        sums[piece, step].start()

    def chunk(piece, step):
        return ring_index((place + 1 + step) % n if piece >= fan // 2 else (place + 2 * n - 1 - step) % n, n)

    for piece in range(fan):
        send_sum(piece, 0, piece_of(x_ref, chunk(piece, 0), piece))
    for step in range(n - 1):
        for piece in range(fan):
            sums[piece, step].wait_recv()
            arrived = piece_of(slots, step, piece)
            mine = piece_of(x_ref, chunk(piece, step + 1), piece)
            total = (arrived[...].astype(jnp.float32) + mine[...].astype(jnp.float32)).astype(jnp.bfloat16)
            if step < n - 2:
                arrived[...] = total
                send_sum(piece, step + 1, arrived)
            else:
                acc[:, piece * cols : (piece + 1) * cols] = total
    moves = []
    for far in range(fan):
        target = (me + far) % fan
        for half in range(2):
            src = acc.at[pl.ds(half * rows, rows), pl.ds(pl.multiple_of(target * cols, 128), cols)]
            dst = inner_ref.at[pl.ds(s * block + (me * 2 + half) * rows, rows), :]
            if far:
                one = pltpu.make_async_remote_copy(
                    src_ref=src,
                    dst_ref=dst,
                    send_sem=swap_send.at[far, half],
                    recv_sem=swap_recv.at[far, half],
                    device_id={"fsdp": target},
                    device_id_type=MESH,
                )
            else:
                one = pltpu.make_async_copy(src, dst, own_sem.at[half])
            one.start()
            moves.append(one)
    mine = pltpu.make_async_copy(
        acc.at[pl.ds(2 * rows, rows), :], outer_ref.at[pl.ds(s * rows, rows), :], own_sem.at[2]
    )
    mine.start()
    copies = {}
    outs = ((outer_ref, (n * rows, width), 2), (inner_ref, (n * block, cols), -2))

    def start(k, piece, step):
        ref, shape, split = outs[k]
        chunk = ring_index((place + step) % n if piece else (place + n - step) % n, n)
        view = ring_window(ref, shape, split, n, piece, chunk)
        copies[k, piece, step] = pltpu.make_async_remote_copy(
            src_ref=view,
            dst_ref=view,
            send_sem=send_sem.at[2 * k + piece, step],
            recv_sem=recv_sem.at[2 * k + piece, step],
            device_id={"seq": left if piece else right},
            device_id_type=MESH,
        )
        copies[k, piece, step].start()

    def forward(k, step):
        for piece in range(2):
            copies[k, piece, step].wait_recv()
            if step < n - 2:
                start(k, piece, step + 1)

    mine.wait()
    start(0, 0, 0)
    start(0, 1, 0)
    lead = (n - 1) // 2
    for step in range(lead):
        forward(0, step)
    for one in moves:
        one.wait()
    parts = []
    for far in range(1, fan):
        target = (me + far) % fan
        for which, (src, into) in enumerate(((part_ref, landed), (few_ref, few_landed))):
            rest = src.shape[0] // fan
            one = pltpu.make_async_remote_copy(
                src_ref=src.at[pl.ds(target * rest, rest), :],
                dst_ref=into.at[far],
                send_sem=part_send.at[which, far],
                recv_sem=part_recv.at[which, far],
                device_id={"fsdp": target},
                device_id_type=MESH,
            )
            one.start()
            parts.append(one)
    start(1, 0, 0)
    start(1, 1, 0)
    for step in range(n - 1):
        forward(1, step)
        if lead + step < n - 1:
            forward(0, lead + step)
    for one in parts:
        one.wait()
    for src, into, out in ((part_ref, landed, sum_ref), (few_ref, few_landed, few_sum_ref)):
        rest = src.shape[0] // fan
        total = src[pl.ds(pl.multiple_of(me * rest, rest), rest), :].astype(jnp.float32)
        for far in range(1, fan):
            total = total + into[far].astype(jnp.float32)
        out[...] = total
    for one in [*copies.values(), *sums.values()]:
        one.wait_send()


def units_total(grads, part, few, ident):
    n, fan = lax.axis_size("seq"), lax.axis_size("fsdp")
    rows, width = grads.shape[0] // (3 * n), grads.shape[1]
    tokens = part.shape[0] // fan
    sems = lambda *shape: pltpu.SemaphoreType.DMA(shape)
    return ring_call(
        functools.partial(units_kernel, n, fan),
        "units_total",
        [grads, part, few],
        [
            ((n * 2 * fan * rows, width // fan), jnp.bfloat16),
            ((n * rows, width), jnp.bfloat16),
            ((tokens, part.shape[1]), jnp.float32),
            ((few.shape[0] // fan, few.shape[1]), jnp.float32),
        ],
        [
            pltpu.VMEM(((n - 1) * 3 * rows, width), jnp.bfloat16),
            pltpu.VMEM((3 * rows, width), jnp.bfloat16),
            pltpu.VMEM((fan, tokens, part.shape[1]), jnp.bfloat16),
            pltpu.VMEM((fan, few.shape[0] // fan, few.shape[1]), jnp.bfloat16),
        ]
        + [sems(fan, n - 1), sems(fan, n - 1), sems(fan, 2), sems(fan, 2), sems(3)]
        + [sems(4, n - 1), sems(4, n - 1), sems(2, fan), sems(2, fan)],
        ident,
    )


def team(n):
    s, f = lax.axis_index("seq"), lax.axis_index("fsdp")
    half = s // (n // 2)
    away = (half + f) % 2
    return f // 2, half, (s + away * (n // 2)) % n


def swap_kernel(n, fan, count, fars, fresh, *refs):
    given = count + (len(fars) > 0) + (0 if fresh else 2)
    x_refs, y_refs = refs[:count], refs[given : given + count]
    sems = refs[given + count + (2 if fars else 0) :]
    send_sem, recv_sem, own_sem = sems[:3]
    pair, half, rank = team(n)
    me = lax.axis_index("fsdp")

    def device(other):
        away = (other // (n // 2) + half) % 2
        return {"seq": (other + away * (n // 2)) % n, "fsdp": 2 * pair + (half + away) % 2}

    barrier = pltpu.get_barrier_semaphore()
    for j in range(1, n):
        pl.semaphore_signal(barrier, inc=1, device_id=device((rank + j) % n), device_id_type=MESH)
    travel = [far for far in fars if far]
    for far in travel:
        pl.semaphore_signal(barrier, inc=1, device_id={"fsdp": (me + fan - far) % fan}, device_id_type=MESH)
    pl.semaphore_wait(barrier, n - 1 + len(travel))
    copies = []
    for k in range(count):
        for j in range(1, n):
            other = (rank + j) % n
            one = pltpu.make_async_remote_copy(
                src_ref=x_refs[k].at[other],
                dst_ref=y_refs[k].at[rank],
                send_sem=send_sem.at[k, j],
                recv_sem=recv_sem.at[k, j],
                device_id=device(other),
                device_id_type=MESH,
            )
            one.start()
            copies.append(one)
    for k in range(count):
        one = pltpu.make_async_copy(x_refs[k].at[rank], y_refs[k].at[rank], own_sem.at[k])
        one.start()
        copies.append(one)
    if fars:
        w_ref, halves = refs[count], refs[given + count : given + count + 2]
        far_send, far_recv, far_own, stage = sems[3:]
        rest = []
        units, cols = halves[0].shape[0], w_ref.shape[1]
        for i, far in enumerate(fars):
            target = (me + far) % fan
            for part in range(2):
                src = w_ref.at[pl.ds((part * fan + target) * units, units), :]
                dst = halves[part].at[:, pl.ds(pl.multiple_of(me * cols, 128), cols)]
                if far:
                    one = pltpu.make_async_remote_copy(
                        src_ref=src,
                        dst_ref=dst,
                        send_sem=far_send.at[i, part],
                        recv_sem=far_recv.at[i, part],
                        device_id={"fsdp": target},
                        device_id_type=MESH,
                    )
                else:
                    one = pltpu.make_async_copy(src, stage.at[part], far_own.at[0, part])
                    rest.append((one, pltpu.make_async_copy(stage.at[part], dst, far_own.at[1, part])))
                one.start()
                if far:
                    copies.append(one)
        for inward, outward in rest:
            inward.wait()
            outward.start()
            copies.append(outward)
    for one in copies:
        one.wait()


def swap(arrays, ident, fars=(), given=None, halves=None):
    n, fan = lax.axis_size("seq"), lax.axis_size("fsdp")
    count = len(arrays)
    size = sum(v.size * 2 for v in arrays)
    operands, outs, alias = list(arrays), [jax.ShapeDtypeStruct(v.shape, v.dtype) for v in arrays], {}
    scratch = [
        pltpu.SemaphoreType.DMA((count, n)),
        pltpu.SemaphoreType.DMA((count, n)),
        pltpu.SemaphoreType.DMA((count,)),
    ]
    if fars:
        operands.append(given)
        shape = (given.shape[0] // (2 * fan), given.shape[1] * fan)
        outs += [jax.ShapeDtypeStruct(shape, given.dtype)] * 2
        scratch += [pltpu.SemaphoreType.DMA((len(fars), 2))] * 2 + [
            pltpu.SemaphoreType.DMA((2, 2)),
            pltpu.VMEM((2, given.shape[0] // (2 * fan), given.shape[1]), given.dtype),
        ]
        if halves is not None:
            operands += list(halves)
            alias = {count + 1: count, count + 2: count + 1}
    return pl.pallas_call(
        functools.partial(swap_kernel, n, fan, count, fars, not fars or halves is None),
        name="swap",
        out_shape=outs,
        in_specs=[pl.BlockSpec(memory_space=pl.ANY)] * len(operands),
        out_specs=[pl.BlockSpec(memory_space=pl.ANY)] * len(outs),
        scratch_shapes=scratch,
        input_output_aliases=alias,
        compiler_params=pltpu.CompilerParams(collective_id=ident, has_side_effects=True),
        cost_estimate=pl.CostEstimate(flops=0, bytes_accessed=size, transcendentals=0),
    )(*operands)


def norm_apply(value, gain):
    return value * lax.rsqrt(jnp.mean(value * value, axis=-1, keepdims=True) + EPS) * gain


def norm_back(value, gain, grad):
    _, pull = jax.vjp(norm_apply, value, gain)
    return pull(grad)


def gate_mix(gate, up):
    return jax.nn.gelu(gate, approximate=True) * up


def counts_below(ids, values):
    total = jnp.zeros_like(values)
    for doc in range(DOCS):
        total = total + jnp.where(values > doc, jnp.sum((ids == doc).astype(jnp.int32)), 0)
    return total


def change_home(value):
    n, fan = lax.axis_size("seq"), lax.axis_size("fsdp")
    pairs = []
    for s in range(n):
        for f in range(fan):
            away = (s // (n // 2) + f) % 2
            target = ((s + n // 2) % n, f ^ 1) if away else (s, f)
            pairs.append((s * fan + f, target[0] * fan + target[1]))
    return lax.ppermute(value, ("seq", "fsdp"), pairs)


def spread(blocks):
    fan, me = lax.axis_size("fsdp"), lax.axis_index("fsdp")
    result = blocks
    for far in range(1, fan):
        block = lax.dynamic_index_in_dim(blocks, (me + far) % fan, 0, True)
        block = lax.ppermute(block, "fsdp", [(f, (f + far) % fan) for f in range(fan)])
        result = lax.dynamic_update_slice_in_dim(result, block, (me - far) % fan, 0)
    return result


def flat(blocks):
    return jnp.transpose(blocks, (1, 0, 2)).reshape(blocks.shape[1], -1)


def by_rows(value):
    return with_layout_constraint(value, Layout(major_to_minor=tuple(range(value.ndim))))


def scatter(grad):
    return lax.psum_scatter(grad, "fsdp", scatter_dimension=0, tiled=True)


def shards(
    layer_in, encoder, decoder_ids, encoder_ids, rel_buckets,
    norm_self, self_qkv, self_out, rel_table, norm_cross, cross_q, cross_kv, cross_out, norm_ff, ff_in, ff_out,
    cotangent,
):
    seqs, local, width = layer_in.shape
    enc_local = encoder.shape[1]
    parts = lax.axis_size("seq")
    heads = self_qkv.shape[1]
    dh = self_qkv.shape[2] // 3
    own = heads // parts
    rows = seqs * local
    buckets, table_own = rel_table.shape
    length, keys = local * parts, enc_local * parts
    gather = lambda v: lax.all_gather(v, "fsdp", axis=0, tiled=True)

    fan = lax.axis_size("fsdp")
    units = ff_in.shape[1] // (2 * fan)
    part = norm_self.shape[0]
    pair, half, rank = team(parts)

    qkv_w = gather(self_qkv)
    small = jnp.concatenate([norm_self, norm_cross, norm_ff, rel_table.reshape(-1)])
    small = lax.all_gather(small, "fsdp", axis=0, tiled=False)
    early = by_rows(jnp.stack([self_out, cross_q, *jnp.split(cross_kv.reshape(-1, 2 * width), 2, axis=1)]))
    small, early = lax.optimization_barrier((small, early))
    early = lax.all_gather(early, "fsdp", axis=1, tiled=True)
    both_ids = jnp.concatenate([decoder_ids.reshape(-1), encoder_ids.reshape(-1)])
    both_ids = change_home(jnp.pad(both_ids, (0, 1024 - local - enc_local)).reshape(8, 128))
    inner_t = ff_in.T
    by_kernel = (width // fan) % 128 == 0 and fan % 2 == 0 and (ff_in.shape[0] // parts) % 8 == 0
    (both_ids,) = swap([jnp.broadcast_to(both_ids[None], (parts, 8, 128))], 13)
    home = change_home(layer_in.reshape(rows, width))
    early = by_rows(early)
    gain_first, gain_second, gain_third = (
        small[:, i * part : (i + 1) * part].reshape(width).astype(f32) for i in range(3)
    )
    table = jnp.transpose(small[:, 3 * part :].reshape(-1, buckets, table_own), (1, 0, 2)).reshape(buckets, heads)
    both_ids = both_ids.reshape(parts, 1024)
    ids = both_ids[:, :local].reshape(length)
    enc_ids = both_ids[:, local : local + enc_local].reshape(keys)

    first_seen = counts_below(ids, ids)
    enc_first = counts_below(enc_ids, ids)
    enc_last = counts_below(enc_ids, ids + 1)
    blocks = length // BQ
    bk = BQ
    self_rows = jnp.broadcast_to(first_seen[None], (8, length))
    cross_rows = jnp.concatenate([enc_first[None], enc_last[None], jnp.zeros((6, length), jnp.int32)])
    self_limits = jnp.stack(
        [first_seen[::BQ] // bk, (jnp.arange(blocks, dtype=jnp.int32) + 1) * (BQ // bk)]
    )
    cross_limits = jnp.stack([enc_first[::BQ] // bk, (enc_last[BQ - 1 :: BQ] + bk - 1) // bk])

    first_head = rank * own
    table_mine = lax.dynamic_slice_in_dim(table.astype(f32), first_head, own, 1)
    near = rel_buckets[:REACH]
    onehot = (near[:, None] == jnp.arange(buckets, dtype=jnp.int32)[None, :]).astype(f32)
    bias = jnp.einsum("ln,ng->gl", onehot, table_mine, precision=HIGH)
    ext = jnp.concatenate(
        [jnp.full((own, BQ), MASKED, f32), bias, jnp.zeros((own, BQ), f32)], axis=1
    )

    qkv_w, home, inner_t, ext, self_rows, cross_rows, self_limits, cross_limits = lax.optimization_barrier(
        (qkv_w, home, inner_t, ext, self_rows, cross_rows, self_limits, cross_limits)
    )
    qkv_w = qkv_w.reshape(width, parts, own * 3 * dh)

    stream = home.astype(f32)
    normed_first = norm_apply(stream, gain_first).astype(bf16)
    qkv_tok = jnp.einsum("td,dge->gte", normed_first, qkv_w, preferred_element_type=f32).astype(bf16)
    others = change_home(jnp.concatenate([cotangent.reshape(rows, width), encoder.reshape(-1, width)]))
    grad_low, enc_flat = others[:rows], others[rows:]
    fars = [tuple(far for far in range(fan) if by_kernel and (far == 2) == first) for first in (True, False)]
    qkv, *halves = swap([qkv_tok], 17, fars[0], inner_t)
    qkv, cross_out, grad_low = lax.optimization_barrier((qkv, cross_out, grad_low))
    if rows == cross_out.shape[0]:
        mix_cross, grad_group = lax.all_gather(jnp.stack([cross_out, grad_low]), "fsdp", axis=1, tiled=True)
    else:
        mix_cross, grad_group = gather(cross_out), gather(grad_low)
    mix_cross = mix_cross.reshape(parts, own * dh, width)
    qkv = qkv.reshape(length, own * 3 * dh)
    out_self, self_t, self_lse = self_forward(self_limits, self_rows, ext, qkv)
    (self_tok,) = swap([out_self.reshape(parts, local, own * dh)], 11)
    after_self, normed_second, query_tok, pairs_tok = over_weights(
        into_kernel,
        "self_out_to_cross",
        [self_tok, home, gain_second.reshape(1, width), enc_flat],
        early,
        lambda i: i,
        [
            ((rows, width), f32),
            ((rows, width), bf16),
            ((parts, rows, own * dh), bf16),
            ((parts, enc_local, own * 2 * dh), bf16),
        ],
    )
    query_cross, pairs = swap([query_tok, pairs_tok], 12)
    query_cross, pairs = query_cross.reshape(length, own * dh), pairs.reshape(keys, own * 2 * dh)
    out_cross, cross_t, cross_lse = cross_forward(cross_limits, cross_rows, query_cross, pairs)
    cross_tok, *halves = swap([out_cross.reshape(parts, local, own * dh)], 16, fars[1], inner_t, halves)
    if not by_kernel:
        halves = spread(jnp.transpose(inner_t.reshape(2, fan, units, -1), (1, 0, 2, 3)))
        halves = [jnp.transpose(halves[:, i], (1, 0, 2)).reshape(units, width) for i in range(2)]
    gate_t, up_t = halves
    after_cross = after_self + jnp.einsum("gtc,gcd->td", cross_tok, mix_cross, preferred_element_type=f32)
    normed_third = norm_apply(after_cross, gain_third).astype(bf16)
    normed_group = gather(normed_third)
    gate = jnp.einsum("td,fd->tf", normed_group, gate_t, preferred_element_type=f32)
    up = jnp.einsum("td,fd->tf", normed_group, up_t, preferred_element_type=f32)
    hidden = gate_mix(gate, up).astype(bf16)

    grad_hidden = jnp.einsum("td,fd->tf", grad_group, ff_out, preferred_element_type=f32)
    _, pull_mix = jax.vjp(gate_mix, gate, up)
    grad_gate, grad_up = (g.astype(bf16) for g in pull_mix(grad_hidden))
    grad_third_in = jnp.dot(grad_gate, gate_t, preferred_element_type=f32) + jnp.dot(
        grad_up, up_t, preferred_element_type=f32
    )
    grad_third_in = scatter(grad_third_in.astype(bf16))
    outer_part = jnp.dot(hidden, ff_out, preferred_element_type=f32).astype(bf16)
    grad_units = [
        jnp.einsum("tf,td->fd", g, y, preferred_element_type=f32).astype(bf16)
        for g, y in ((grad_gate, normed_group), (grad_up, normed_group), (hidden, grad_group))
    ]
    if by_kernel:
        grad_units = jnp.stack([g.reshape(parts, units // parts, width) for g in grad_units], axis=1)
        grad_units = grad_units.reshape(3 * units, width)
    grad_third_in, outer_part, part_units = lax.optimization_barrier((grad_third_in, outer_part, grad_units))
    grad_third_in = grad_third_in.astype(f32)
    grad_from_third, grad_gain_third = norm_back(after_cross, gain_third, grad_third_in)
    grad_middle = grad_low.astype(f32) + grad_from_third
    middle_low = grad_middle.astype(bf16)
    grad_mix_cross = jnp.einsum("gtc,td->gcd", cross_tok, middle_low, preferred_element_type=f32)
    part_cross = scatter(grad_mix_cross.reshape(width, width).astype(bf16))
    grad_cross_tok = jnp.einsum("td,gcd->gtc", middle_low, mix_cross, preferred_element_type=f32).astype(bf16)
    (grad_cross,) = swap([grad_cross_tok], 11)
    grad_cross = grad_cross.reshape(length, own * dh)
    grad_query, grad_pairs = cross_backward(
        cross_limits, cross_rows, query_cross, pairs, grad_cross, cross_t, cross_lse
    )
    grad_query_tok, grad_pairs_tok = swap(
        [grad_query.reshape(parts, local, own * dh), grad_pairs.reshape(parts, enc_local, own * 2 * dh)], 12
    )
    (
        grad_upper, upper_low, grad_self_tok, grad_gain_second, grad_encoder, grad_query_tok, grad_pairs_tok
    ) = over_weights(
        outof_kernel,
        "cross_to_self_out",
        [grad_query_tok, grad_pairs_tok, after_self, gain_second.reshape(1, width), grad_middle],
        early,
        lambda i: jnp.where(i < 2, 1 - i, i),
        [
            ((rows, width), f32),
            ((rows, width), bf16),
            ((parts, rows, own * dh), bf16),
            ((1, width), f32),
            ((enc_local, width), bf16),
            ((rows, width), bf16),
            ((enc_local, 2 * width), bf16),
        ],
        [((enc_local, width), f32)],
    )
    grad_query_w = jnp.einsum("td,te->de", normed_second, grad_query_tok, preferred_element_type=f32)
    grad_pairs_w = jnp.einsum("td,te->de", enc_flat, grad_pairs_tok, preferred_element_type=f32)
    grad_mix_self = jnp.einsum("gtc,td->gcd", self_tok, upper_low, preferred_element_type=f32)
    grad_mid = jnp.concatenate(
        [
            grad_query_w.astype(bf16),
            grad_pairs_w.astype(bf16),
            grad_mix_self.reshape(width, width).astype(bf16),
        ],
        axis=1,
    )
    grad_self_tok, grad_mid = lax.optimization_barrier((grad_self_tok, grad_mid))
    part_mid = scatter(grad_mid)
    (grad_self,) = swap([grad_self_tok], 11)
    grad_self = grad_self.reshape(length, own * dh)
    grad_qkv, diagonals = self_backward(self_limits, self_rows, ext, qkv, grad_self, self_t, self_lse)
    (grad_qkv_tok,) = swap([grad_qkv.reshape(parts, local, own * 3 * dh)], 10)
    grad_qkv_tok = flat(grad_qkv_tok)
    grad_qkv_w = jnp.einsum("td,te->de", normed_first, grad_qkv_tok, preferred_element_type=f32)
    grad_qkv_w, grad_qkv_tok = lax.optimization_barrier((grad_qkv_w.astype(bf16), grad_qkv_tok))
    grad_first_in = jnp.einsum("te,de->td", grad_qkv_tok, qkv_w.reshape(width, -1), preferred_element_type=f32)
    grad_from_first, grad_gain_first = norm_back(stream, gain_first, grad_first_in)
    grad_layer_in = (grad_upper + grad_from_first).astype(bf16)
    bucket_line = jnp.concatenate([jnp.full((BQ - 1,), -1, jnp.int32), near, jnp.full((BQ + 1,), -1, jnp.int32)])
    in_bucket = (bucket_line[:, None] == jnp.arange(buckets, dtype=jnp.int32)).astype(f32)
    by_bucket = jnp.einsum("xn,gx->ng", in_bucket, diagonals, precision=HIGH)
    grad_table = lax.dynamic_update_slice_in_dim(jnp.zeros((buckets, heads), f32), by_bucket, first_head, 1)

    gains = jnp.concatenate(
        [g.reshape(-1, part) for g in (grad_gain_first, grad_gain_second, grad_gain_third)], axis=1
    )
    tables = jnp.transpose(grad_table.reshape(buckets, -1, table_own), (1, 0, 2)).reshape(-1, buckets * table_own)
    small_grads = jnp.concatenate([gains, tables], axis=1).astype(bf16)
    small_size = small_grads.shape[1]
    going_home = jnp.concatenate([grad_layer_in, grad_encoder.astype(bf16)])
    part_last = scatter(grad_qkv_w)
    going_home, small_grads, part_units, part_cross, part_mid = lax.optimization_barrier(
        (change_home(going_home), small_grads, part_units, part_cross, part_mid)
    )
    if by_kernel:
        few = jnp.pad(small_grads[:, None], ((0, 0), (0, 7), (0, 1024 - small_size))).reshape(fan * 8, 1024)
        total_inner, total_outer, outer_sum, few = units_total(part_units, outer_part, few, 0)
        few = jnp.pad(few[0].astype(bf16).reshape(8, 128), ((0, parts * 8 - 8), (0, 0)))
        total_cross, total_mid, total_qkv, small_total, total_inner = ring_total(
            [part_cross, part_mid, part_last, few], (2, 2, 2, 1), 1, total_inner
        )
    else:
        grad_units = [lax.psum(g, "seq") for g in part_units]
        total_inner = spread(jnp.transpose(jnp.stack(grad_units[:2]).reshape(2, units, fan, -1), (2, 0, 1, 3)))
        total_inner = jnp.transpose(total_inner, (3, 1, 0, 2)).reshape(-1, 2 * fan * units).astype(f32)
        total_outer, outer_sum = grad_units[2], scatter(outer_part).astype(f32)
        few = lax.dynamic_index_in_dim(lax.psum(small_grads, "fsdp"), lax.axis_index("fsdp"), 0, False)
        total_cross, total_mid, total_qkv, small_total = (
            lax.psum(v, "seq") for v in (part_cross, part_mid, part_last, few)
        )
    layer_out = (after_cross + outer_sum).astype(bf16)
    layer_out, total_inner, total_outer, total_cross, total_mid, total_qkv, going_home = lax.optimization_barrier(
        (layer_out, total_inner, total_outer, total_cross, total_mid, total_qkv, going_home)
    )
    layer_out = change_home(layer_out).reshape(seqs, local, width)
    grad_layer_in = going_home[:rows].astype(f32).reshape(seqs, local, width)
    grad_encoder = going_home[rows:].astype(f32).reshape(seqs, enc_local, width)
    total_inner, total_outer, total_mid, total_qkv = (
        v.astype(f32) for v in (total_inner, total_outer, total_mid, total_qkv)
    )
    total_query, total_mix_cross = total_mid[:, :width], total_cross.astype(f32)
    total_pairs = total_mid[:, width : 3 * width].reshape(-1, heads, 2 * dh)
    total_mix_self, total_qkv = total_mid[:, 3 * width :], total_qkv.reshape(-1, heads, 3 * dh)
    mine = small_total.reshape(-1)[:small_size].astype(f32)
    total_gain_first, total_gain_second, total_gain_third = (mine[i * part : (i + 1) * part] for i in range(3))
    total_table = mine[3 * part :].reshape(buckets, table_own)
    return (
        layer_out, grad_layer_in, grad_encoder, total_gain_first, total_qkv, total_mix_self, total_table,
        total_gain_second, total_query, total_pairs, total_mix_cross, total_gain_third, total_inner, total_outer,
    )


def solution(mesh):
    in_specs = (
        P("fsdp", "seq", None), P("fsdp", "seq", None), P("fsdp", "seq"), P("fsdp", "seq"), P(),
        P("fsdp"), P("fsdp", None, None), P("fsdp", None), P(None, "fsdp"), P("fsdp"), P("fsdp", None),
        P("fsdp", None, None), P("fsdp", None), P("fsdp"), P("fsdp", None), P("fsdp", None),
        P("fsdp", "seq", None),
    )
    out_specs = (
        P("fsdp", "seq", None), P("fsdp", "seq", None), P("fsdp", "seq", None), P("fsdp"), P("fsdp", None, None),
        P("fsdp", None), P(None, "fsdp"), P("fsdp"), P("fsdp", None), P("fsdp", None, None), P("fsdp", None),
        P("fsdp"), P("fsdp", None), P("fsdp", None),
    )
    return jax.shard_map(shards, mesh=mesh, in_specs=in_specs, out_specs=out_specs, check_vma=False)
```

```python
import functools

import jax
import jax.numpy as jnp
from jax import lax
from jax.experimental import pallas as pl
from jax.experimental.layout import Layout, with_layout_constraint
from jax.experimental.pallas import tpu as pltpu
from jax.sharding import PartitionSpec as P

EPS = 1e-06
HIGH = lax.Precision.HIGHEST
MASKED = -1e30
DOCS = 4

BQ = 256
REACH = 1024


def blk(index, size):
    return pl.ds(pl.multiple_of(index * size, size), size)


def turn(value):
    return jnp.transpose(value.astype(jnp.float32), (1, 0))


def bias_tiles(ext_ref, tile_ref, own):
    for h in range(own):
        line = jnp.broadcast_to(ext_ref[h : h + 1, :], tile_ref.shape[1:])
        tile_ref[h] = pltpu.roll(line, 0, 1, stride=1, stride_axis=0)


def unpack(ref, own, width, picks, flips, base):
    block = 256

    def one(b, _):
        rows = blk(b, block)
        value = ref[rows, :]
        if flips:
            flat = turn(value).astype(jnp.bfloat16)
            for target, piece in flips:
                for h in range(own):
                    at = h * width + piece * 64
                    target[base + h, :, rows] = flat[at : at + 64]
        for target, piece in picks:
            for h in range(own):
                at = h * width + piece * 64
                target[base + h, rows, :] = value[:, at : at + 64]
        return 0

    lax.fori_loop(0, ref.shape[0] // block, one, 0)


def dot(a, b):
    return jnp.dot(a, b, preferred_element_type=jnp.float32)


def score(own_index, key_tile, query_t, tile_ref, t, low, high, first_key):
    value = dot(key_tile, query_t)
    place = lax.broadcasted_iota(jnp.int32, value.shape, 0)
    keep = place >= low - first_key
    if high is not None:
        keep = keep & (place < high - first_key)
    else:
        value = value + tile_ref[own_index, :, blk(t + 1, BQ)]
    return jnp.where(keep, value, MASKED)


def forward_body(own, bk, causal, lim_ref, rows_ref, q_t, k_rows, v_t, tile_ref, o_ref, ot_ref, lse_ref):
    length = o_ref.shape[0]

    def q_block(i, _):
        cols = blk(i, BQ)
        queries = [q_t[h, :, cols] for h in range(own)]
        low = rows_ref[0:1, cols]
        high = None if causal else rows_ref[1:2, cols]

        def k_block(j, carry):
            keys = blk(j, bk)
            t = i - j
            out = []
            for h in range(own):
                top, total, acc = carry[h]
                s = score(h, k_rows[h, keys, :], queries[h], tile_ref, t, low, high, j * bk)
                new_top = jnp.maximum(top, jnp.max(s, axis=0, keepdims=True))
                p = jnp.exp(s - new_top)
                scale = jnp.exp(top - new_top)
                total = total * scale + jnp.sum(p, axis=0, keepdims=True)
                acc = acc * scale + dot(v_t[h, :, keys], p.astype(jnp.bfloat16))
                out.append((new_top, total, acc))
            return tuple(out)

        start = tuple(
            (
                jnp.full((1, BQ), MASKED, jnp.float32),
                jnp.zeros((1, BQ), jnp.float32),
                jnp.zeros((64, BQ), jnp.float32),
            )
            for _ in range(own)
        )
        ends = lax.fori_loop(lim_ref[0, i], lim_ref[1, i], k_block, start)
        for h in range(own):
            top, total, acc = ends[h]
            ot_ref[h * 64 : h * 64 + 64, cols] = acc / total
            lse_ref[h : h + 1, cols] = top + jnp.log(total)
        o_ref[cols, :] = turn(ot_ref[:, cols]).astype(jnp.bfloat16)
        return 0

    lax.fori_loop(0, length // BQ, q_block, 0)


def self_forward_kernel(own, bk, lim_ref, rows_ref, ext_ref, x_ref, o_ref, ot_ref, lse_ref, q_t, k_rows, v_t, tile_ref):
    bias_tiles(ext_ref, tile_ref, own)
    unpack(x_ref, own, 192, [(k_rows, 1)], [(q_t, 0), (v_t, 2)], 0)
    forward_body(own, bk, True, lim_ref, rows_ref, q_t, k_rows, v_t, tile_ref, o_ref, ot_ref, lse_ref)


def cross_forward_kernel(own, bk, lim_ref, rows_ref, q_ref, kv_ref, o_ref, ot_ref, lse_ref, q_t, k_rows, v_t):
    unpack(q_ref, own, 64, [], [(q_t, 0)], 0)
    unpack(kv_ref, own, 128, [(k_rows, 0)], [(v_t, 1)], 0)
    forward_body(own, bk, False, lim_ref, rows_ref, q_t, k_rows, v_t, None, o_ref, ot_ref, lse_ref)


def backward_body(
    own, bk, causal, lim_ref, rows_ref, do_ref, ot_ref, lse_ref,
    q_t, q_rows, k_t, k_rows, v_rows, do_t, do_rows, tile_ref, sum_ref, dq_t, dk, dv,
):
    length = do_ref.shape[0]
    dk[...] = jnp.zeros_like(dk)
    dv[...] = jnp.zeros_like(dv)
    if causal:
        sum_ref[...] = jnp.zeros_like(sum_ref)

    def q_block(i, _):
        cols = blk(i, BQ)
        low = rows_ref[0:1, cols]
        high = None if causal else rows_ref[1:2, cols]
        per_head = []
        for h in range(own):
            grad_t = do_t[h, :, cols]
            delta = jnp.sum(
                grad_t.astype(jnp.float32) * ot_ref[h * 64 : h * 64 + 64, cols], axis=0, keepdims=True
            )
            per_head.append((q_t[h, :, cols], grad_t, delta, lse_ref[h : h + 1, cols]))

        def k_block(j, carry):
            keys = blk(j, bk)
            t = i - j
            out = []
            for h in range(own):
                query_t, grad_t, delta, lse = per_head[h]
                s = score(h, k_rows[h, keys, :], query_t, tile_ref, t, low, high, j * bk)
                p = jnp.exp(s - lse)
                dp = dot(v_rows[h, keys, :], grad_t)
                ds = (p * (dp - delta)).astype(jnp.bfloat16)
                dv[h, keys, :] += dot(p.astype(jnp.bfloat16), do_rows[h, cols, :])
                dk[h, keys, :] += dot(ds, q_rows[h, cols, :])
                if causal:
                    sum_ref[h, :, blk(t, BQ)] += ds.astype(jnp.float32)
                out.append(carry[h] + dot(k_t[h, :, keys], ds))
            return tuple(out)

        ends = lax.fori_loop(
            lim_ref[0, i],
            lim_ref[1, i],
            k_block,
            tuple(jnp.zeros((64, BQ), jnp.float32) for _ in range(own)),
        )
        for h in range(own):
            dq_t[h * 64 : h * 64 + 64, cols] = ends[h]
        return 0

    lax.fori_loop(0, length // BQ, q_block, 0)


def diagonal_sums(sum_ref, u_ref, own):
    flip = lax.broadcasted_iota(jnp.int32, (BQ, BQ), 0) + lax.broadcasted_iota(jnp.int32, (BQ, BQ), 1) == BQ - 1
    flip = jnp.where(flip, 1.0, 0.0).astype(jnp.bfloat16)
    for h in range(own):
        grid = sum_ref[h]
        high = grid.astype(jnp.bfloat16)
        low = (grid - high.astype(jnp.float32)).astype(jnp.bfloat16)
        upside = dot(flip, high) + dot(flip, low)
        wide = jnp.concatenate([upside, jnp.zeros((BQ, BQ), jnp.float32)], axis=1)
        aligned = pltpu.roll(wide, 0, 1, stride=1, stride_axis=0)
        u_ref[h : h + 1, :] = jnp.sum(aligned, axis=0, keepdims=True)


def self_backward_kernel(
    own, bk, lim_ref, rows_ref, ext_ref, x_ref, do_ref, ot_ref, lse_ref, dx_ref, u_ref,
    q_t, q_rows, k_t, k_rows, v_rows, do_t, do_rows, tile_ref, sum_ref, dq_t, dk, dv,
):
    bias_tiles(ext_ref, tile_ref, own)
    unpack(x_ref, own, 192, [(q_rows, 0), (k_rows, 1), (v_rows, 2)], [(q_t, 0), (k_t, 1)], 0)
    unpack(do_ref, own, 64, [(do_rows, 0)], [(do_t, 0)], 0)
    backward_body(
        own, bk, True, lim_ref, rows_ref, do_ref, ot_ref, lse_ref,
        q_t, q_rows, k_t, k_rows, v_rows, do_t, do_rows, tile_ref, sum_ref, dq_t, dk, dv,
    )
    diagonal_sums(sum_ref, u_ref, own)

    def pack(b, _):
        rows = blk(b, 256)
        dq = turn(dq_t[:, rows])
        pieces = []
        for h in range(own):
            pieces += [dq[:, h * 64 : h * 64 + 64], dk[h, rows, :], dv[h, rows, :]]
        dx_ref[rows, :] = jnp.concatenate(pieces, axis=1).astype(jnp.bfloat16)
        return 0

    lax.fori_loop(0, x_ref.shape[0] // 256, pack, 0)


def cross_backward_kernel(
    own, bk, lim_ref, rows_ref, q_ref, kv_ref, do_ref, ot_ref, lse_ref, dq_ref, dkv_ref,
    q_t, q_rows, k_t, k_rows, v_rows, do_t, do_rows, dq_t, dk, dv,
):
    unpack(q_ref, own, 64, [(q_rows, 0)], [(q_t, 0)], 0)
    unpack(kv_ref, own, 128, [(k_rows, 0), (v_rows, 1)], [(k_t, 0)], 0)
    unpack(do_ref, own, 64, [(do_rows, 0)], [(do_t, 0)], 0)
    backward_body(
        own, bk, False, lim_ref, rows_ref, do_ref, ot_ref, lse_ref,
        q_t, q_rows, k_t, k_rows, v_rows, do_t, do_rows, None, None, dq_t, dk, dv,
    )

    def pack_q(b, _):
        rows = blk(b, 256)
        dq_ref[rows, :] = turn(dq_t[:, rows]).astype(jnp.bfloat16)
        return 0

    def pack_kv(b, _):
        rows = blk(b, 256)
        pieces = []
        for h in range(own):
            pieces += [dk[h, rows, :], dv[h, rows, :]]
        dkv_ref[rows, :] = jnp.concatenate(pieces, axis=1).astype(jnp.bfloat16)
        return 0

    lax.fori_loop(0, q_ref.shape[0] // 256, pack_q, 0)
    lax.fori_loop(0, kv_ref.shape[0] // 256, pack_kv, 0)


SMEM = pl.BlockSpec(memory_space=pltpu.SMEM)
VMEM = pl.BlockSpec(memory_space=pltpu.VMEM)
bf16, f32 = jnp.bfloat16, jnp.float32


def call(body, name, operands, outs, scratch, flops):
    size = sum(v.size * v.dtype.itemsize for v in operands)
    return pl.pallas_call(
        body,
        name=name,
        out_shape=[jax.ShapeDtypeStruct(s, d) for s, d in outs],
        in_specs=[SMEM] + [VMEM] * (len(operands) - 1),
        out_specs=[VMEM] * len(outs),
        scratch_shapes=[pltpu.VMEM(s, d) for s, d in scratch],
        compiler_params=pltpu.CompilerParams(vmem_limit_bytes=40 << 20),
        cost_estimate=pl.CostEstimate(flops=0, bytes_accessed=size, transcendentals=0),
    )(*operands)


def self_forward(limits, rows, ext, x, bk=BQ):
    length, own = x.shape[0], x.shape[1] // 192
    return call(
        functools.partial(self_forward_kernel, own, bk),
        "self_forward",
        [limits, rows, ext, x],
        [((length, own * 64), bf16), ((own * 64, length), f32), ((own, length), f32)],
        [
            ((own, 64, length), bf16),
            ((own, length, 64), bf16),
            ((own, 64, length), bf16),
            ((own, BQ, REACH + 2 * BQ), f32),
        ],
        length * length * own * 64,
    )


def cross_forward(limits, rows, q, kv, bk=BQ):
    length, own, keys = q.shape[0], q.shape[1] // 64, kv.shape[0]
    return call(
        functools.partial(cross_forward_kernel, own, bk),
        "cross_forward",
        [limits, rows, q, kv],
        [((length, own * 64), bf16), ((own * 64, length), f32), ((own, length), f32)],
        [((own, 64, length), bf16), ((own, keys, 64), bf16), ((own, 64, keys), bf16)],
        length * keys * own * 128,
    )


def self_backward(limits, rows, ext, x, grad, o_t, lse, bk=BQ):
    length, own = x.shape[0], x.shape[1] // 192
    return call(
        functools.partial(self_backward_kernel, own, bk),
        "self_backward",
        [limits, rows, ext, x, grad, o_t, lse],
        [((length, own * 192), bf16), ((own, REACH + 2 * BQ), f32)],
        [
            ((own, 64, length), bf16),
            ((own, length, 64), bf16),
            ((own, 64, length), bf16),
            ((own, length, 64), bf16),
            ((own, length, 64), bf16),
            ((own, 64, length), bf16),
            ((own, length, 64), bf16),
            ((own, BQ, REACH + 2 * BQ), f32),
            ((own, BQ, REACH + BQ), f32),
            ((own * 64, length), f32),
            ((own, length, 64), f32),
            ((own, length, 64), f32),
        ],
        length * length * own * 160,
    )


def cross_backward(limits, rows, q, kv, grad, o_t, lse, bk=BQ):
    length, own, keys = q.shape[0], q.shape[1] // 64, kv.shape[0]
    return call(
        functools.partial(cross_backward_kernel, own, bk),
        "cross_backward",
        [limits, rows, q, kv, grad, o_t, lse],
        [((length, own * 64), bf16), ((keys, own * 128), bf16)],
        [
            ((own, 64, length), bf16),
            ((own, length, 64), bf16),
            ((own, 64, keys), bf16),
            ((own, keys, 64), bf16),
            ((own, keys, 64), bf16),
            ((own, 64, length), bf16),
            ((own, length, 64), bf16),
            ((own * 64, length), f32),
            ((own, keys, 64), f32),
            ((own, keys, 64), f32),
        ],
        length * keys * own * 320,
    )


def rows_of(blocks_ref):
    return jnp.concatenate([blocks_ref[g] for g in range(blocks_ref.shape[0])], axis=1)


def against(a, b):
    return lax.dot_general(a, b, (((1,), (1,)), ((), ())), preferred_element_type=jnp.float32)


def into_kernel(tok_ref, home_ref, gain_ref, enc_ref, w_ref, after_ref, norm_ref, query_ref, pairs_ref):
    which = pl.program_id(0)

    @pl.when(which == 0)
    def _():
        value = home_ref[...].astype(jnp.float32) + dot(rows_of(tok_ref), w_ref[0])
        after_ref[...] = value
        scale = lax.rsqrt(jnp.mean(value * value, axis=1, keepdims=True) + EPS)
        norm_ref[...] = (value * scale * gain_ref[...]).astype(jnp.bfloat16)

    @pl.when(which == 1)
    def _():
        query = dot(norm_ref[...], w_ref[0]).astype(jnp.bfloat16)
        cols = query_ref.shape[2]
        for g in range(query_ref.shape[0]):
            query_ref[g] = query[:, g * cols : (g + 1) * cols]

    for half in range(2):

        @pl.when(which == 2 + half)
        def _():
            pairs = dot(enc_ref[...], w_ref[0]).astype(jnp.bfloat16)
            groups, cols = pairs_ref.shape[0] // 2, pairs_ref.shape[2]
            for g in range(groups):
                pairs_ref[half * groups + g] = pairs[:, g * cols : (g + 1) * cols]


def outof_kernel(
    dq_ref, dkv_ref, after_ref, gain_ref, middle_ref, w_ref,
    upper_ref, low_ref, out_ref, gain_grad_ref, enc_grad_ref, dq_flat_ref, dkv_flat_ref, enc_sum,
):
    which = pl.program_id(0)

    @pl.when(which == 0)
    def _():
        grad_query = rows_of(dq_ref)
        dq_flat_ref[...] = grad_query
        dkv_flat_ref[...] = rows_of(dkv_ref)
        grad = against(grad_query, w_ref[0])
        value = after_ref[...]
        unit = value * lax.rsqrt(jnp.mean(value * value, axis=1, keepdims=True) + EPS)
        gain_grad_ref[...] = jnp.sum(grad * unit, axis=0, keepdims=True)
        scale = lax.rsqrt(jnp.mean(value * value, axis=1, keepdims=True) + EPS)
        grad = grad * gain_ref[...]
        inner = jnp.mean(grad * unit, axis=1, keepdims=True)
        upper = middle_ref[...] + scale * (grad - unit * inner)
        upper_ref[...] = upper
        low_ref[...] = upper.astype(jnp.bfloat16)

    @pl.when(which == 1)
    def _():
        grad = against(low_ref[...], w_ref[0]).astype(jnp.bfloat16)
        cols = out_ref.shape[2]
        for g in range(out_ref.shape[0]):
            out_ref[g] = grad[:, g * cols : (g + 1) * cols]

    width = w_ref.shape[1]

    @pl.when(which == 2)
    def _():
        enc_sum[...] = against(dkv_flat_ref[:, :width], w_ref[0])

    @pl.when(which == 3)
    def _():
        enc_grad_ref[...] = (enc_sum[...] + against(dkv_flat_ref[:, width:], w_ref[0])).astype(jnp.bfloat16)


def over_weights(body, name, arrays, weights, order, outs, scratch=()):
    count, rows, cols = weights.shape
    whole = lambda shape: pl.BlockSpec(shape, lambda i: (0,) * len(shape))
    return pl.pallas_call(
        body,
        name=name,
        grid=(count,),
        out_shape=[jax.ShapeDtypeStruct(s, d) for s, d in outs],
        in_specs=[whole(v.shape) for v in arrays] + [pl.BlockSpec((1, rows, cols), lambda i: (order(i), 0, 0))],
        out_specs=[whole(s) for s, _ in outs],
        scratch_shapes=[pltpu.VMEM(s, d) for s, d in scratch],
        compiler_params=pltpu.CompilerParams(vmem_limit_bytes=62 << 20, dimension_semantics=("arbitrary",)),
        cost_estimate=pl.CostEstimate(flops=0, bytes_accessed=weights.size * 2, transcendentals=0),
    )(*arrays, weights)


MESH = pl.DeviceIdType.MESH


def ring_place(index, n):
    z, x = index // 2, index % 2
    return z + x * (n - 1 - 2 * z)


def ring_index(place, n):
    x = place // (n // 2)
    z = place + x * (n - 1 - 2 * place)
    return 2 * z + x


def ring_greet(n, others):
    place = ring_place(lax.axis_index("seq"), n)
    right = ring_index((place + 1) % n, n)
    left = ring_index((place + n - 1) % n, n)
    barrier = pltpu.get_barrier_semaphore()
    for neighbour in (left, right):
        pl.semaphore_signal(barrier, inc=1, device_id={"seq": neighbour}, device_id_type=MESH)
    for other in others:
        pl.semaphore_signal(barrier, inc=1, device_id={"fsdp": other}, device_id_type=MESH)
    pl.semaphore_wait(barrier, 2 + len(others))
    return place, right, left


def ring_cut(shape, split, n):
    rows, cols = shape[0] // n, shape[1]
    return (rows, cols // split) if split > 0 else (rows // -split, cols)


def ring_window(ref, shape, split, n, piece, chunk):
    whole = shape[0] // n
    rows, cols = ring_cut(shape, split, n)
    if split > 0:
        return ref.at[pl.ds(chunk * whole, rows), pl.ds(piece * cols, cols)]
    return ref.at[pl.ds(chunk * whole + piece * rows, rows), :]


def ring_kernel(n, splits, fan, *refs):
    count = len(splits)
    more = 1 if fan else 0
    x_refs, y_refs = refs[:count], refs[count + more : 2 * count + more]
    slots = refs[2 * (count + more) : 3 * count + 2 * more]
    send_sem, recv_sem = refs[3 * count + 2 * more :]
    place, right, left = ring_greet(n, [])
    streams = [
        (k, piece, (piece if abs(splits[k]) > 1 else k) % 2) for k in range(count) for piece in range(abs(splits[k]))
    ]

    def window(ref, k, piece, chunk):
        return ring_window(ref, x_refs[k].shape, splits[k], n, piece, chunk)

    def chunk_at(down, step):
        return (place + 1 + step) % n if down else (place + 2 * n - 1 - step) % n

    copies = {}

    def start(number, step, src, dst, down):
        copies[number, step] = pltpu.make_async_remote_copy(
            src_ref=src,
            dst_ref=dst,
            send_sem=send_sem.at[number, step],
            recv_sem=recv_sem.at[number, step],
            device_id={"seq": left if down else right},
            device_id_type=MESH,
        )
        copies[number, step].start()

    def turn_block(number):
        inner_ref, turned_ref = refs[count], refs[2 * count + 1]
        rows = inner_ref.shape[0] // (2 * fan * n)
        half, first = number // (fan // 2), number % (fan // 2) * 2
        tall = jnp.concatenate(
            [
                inner_ref[pl.ds(((chunk * fan + group) * 2 + half) * rows, rows), :].astype(jnp.float32)
                for group in (first, first + 1)
                for chunk in range(n)
            ]
        )
        wide = 2 * n * rows
        turned_ref[:, number * wide : (number + 1) * wide] = jnp.transpose(tall, (1, 0)).astype(jnp.bfloat16)

    for number, (k, piece, down) in enumerate(streams):
        start(number, 0, window(x_refs[k], k, piece, place), window(slots[k], k, piece, 0), down)
    for step in range(n - 1):
        if step < fan:
            turn_block(step)
        for number, (k, piece, down) in enumerate(streams):
            copies[number, step].wait_recv()
            chunk = chunk_at(down, step)
            mine = window(x_refs[k], k, piece, chunk)
            landed = window(slots[k], k, piece, step)
            total = landed[...].astype(jnp.float32) + mine[...].astype(jnp.float32)
            if step < n - 2:
                landed[...] = total.astype(jnp.bfloat16)
                start(number, step + 1, landed, window(slots[k], k, piece, step + 1), down)
            else:
                done = window(y_refs[k], k, piece, chunk)
                done[...] = total.astype(jnp.bfloat16)
                start(number, n - 1, done, done, down)
    for step in range(n - 1):
        for number, (k, piece, down) in enumerate(streams):
            copies[number, n - 1 + step].wait_recv()
            if step < n - 2:
                done = window(y_refs[k], k, piece, chunk_at(down, n - 1 + step))
                start(number, n + step, done, done, down)
    for one in copies.values():
        one.wait_send()


def ring_call(body, name, arrays, outs, scratch, ident):
    size = sum(v.size * 2 for v in arrays)
    return pl.pallas_call(
        body,
        name=name,
        out_shape=[jax.ShapeDtypeStruct(s, d) for s, d in outs],
        in_specs=[pl.BlockSpec(memory_space=pltpu.VMEM)] * len(arrays),
        out_specs=[pl.BlockSpec(memory_space=pltpu.VMEM)] * len(outs),
        scratch_shapes=scratch,
        compiler_params=pltpu.CompilerParams(
            collective_id=ident, has_side_effects=True, vmem_limit_bytes=48 << 20
        ),
        cost_estimate=pl.CostEstimate(flops=0, bytes_accessed=60 * size, transcendentals=0),
    )(*arrays)


def ring_total(arrays, splits, ident, inner=None):
    n, fan = lax.axis_size("seq"), lax.axis_size("fsdp")
    streams = sum(abs(s) for s in splits)
    more = [] if inner is None else [inner]
    return ring_call(
        functools.partial(ring_kernel, n, splits, 0 if inner is None else fan),
        "ring_total",
        arrays + more,
        [(v.shape, jnp.bfloat16) for v in arrays] + [(v.shape[::-1], jnp.bfloat16) for v in more],
        [pltpu.VMEM((v.shape[0] // n * (n - 1), v.shape[1]), jnp.bfloat16) for v in arrays]
        + [pltpu.SemaphoreType.DMA((streams, 2 * n - 2))] * 2,
        ident,
    )


def units_kernel(
    n, fan, x_ref, part_ref, few_ref, inner_ref, outer_ref, sum_ref, few_sum_ref, slots, acc, landed, few_landed,
    down_send, down_recv, swap_send, swap_recv, own_sem, send_sem, recv_sem, part_send, part_recv,
):
    s, me = lax.axis_index("seq"), lax.axis_index("fsdp")
    rows, width = acc.shape[0] // 3, x_ref.shape[1]
    cols = width // fan
    block = 2 * fan * rows
    place, right, left = ring_greet(n, [(me + far) % fan for far in range(1, fan)])
    sums = {}

    def piece_of(ref, at, piece):
        return ref.at[pl.ds(at * 3 * rows, 3 * rows), pl.ds(piece * cols, cols)]

    def send_sum(piece, step, src):
        to = left if piece >= fan // 2 else right
        sums[piece, step] = pltpu.make_async_remote_copy(
            src_ref=src,
            dst_ref=piece_of(slots, step, piece),
            send_sem=down_send.at[piece, step],
            recv_sem=down_recv.at[piece, step],
            device_id={"seq": to},
            device_id_type=MESH,
        )
        sums[piece, step].start()

    def chunk(piece, step):
        return ring_index((place + 1 + step) % n if piece >= fan // 2 else (place + 2 * n - 1 - step) % n, n)

    for piece in range(fan):
        send_sum(piece, 0, piece_of(x_ref, chunk(piece, 0), piece))
    for step in range(n - 1):
        for piece in range(fan):
            sums[piece, step].wait_recv()
            arrived = piece_of(slots, step, piece)
            mine = piece_of(x_ref, chunk(piece, step + 1), piece)
            total = (arrived[...].astype(jnp.float32) + mine[...].astype(jnp.float32)).astype(jnp.bfloat16)
            if step < n - 2:
                arrived[...] = total
                send_sum(piece, step + 1, arrived)
            else:
                acc[:, piece * cols : (piece + 1) * cols] = total
    moves = []
    for far in range(fan):
        target = (me + far) % fan
        for half in range(2):
            src = acc.at[pl.ds(half * rows, rows), pl.ds(pl.multiple_of(target * cols, 128), cols)]
            dst = inner_ref.at[pl.ds(s * block + (me * 2 + half) * rows, rows), :]
            if far:
                one = pltpu.make_async_remote_copy(
                    src_ref=src,
                    dst_ref=dst,
                    send_sem=swap_send.at[far, half],
                    recv_sem=swap_recv.at[far, half],
                    device_id={"fsdp": target},
                    device_id_type=MESH,
                )
            else:
                one = pltpu.make_async_copy(src, dst, own_sem.at[half])
            one.start()
            moves.append(one)
    mine = pltpu.make_async_copy(
        acc.at[pl.ds(2 * rows, rows), :], outer_ref.at[pl.ds(s * rows, rows), :], own_sem.at[2]
    )
    mine.start()
    copies = {}
    outs = ((outer_ref, (n * rows, width), 2), (inner_ref, (n * block, cols), -2))

    def start(k, piece, step):
        ref, shape, split = outs[k]
        chunk = ring_index((place + step) % n if piece else (place + n - step) % n, n)
        view = ring_window(ref, shape, split, n, piece, chunk)
        copies[k, piece, step] = pltpu.make_async_remote_copy(
            src_ref=view,
            dst_ref=view,
            send_sem=send_sem.at[2 * k + piece, step],
            recv_sem=recv_sem.at[2 * k + piece, step],
            device_id={"seq": left if piece else right},
            device_id_type=MESH,
        )
        copies[k, piece, step].start()

    def forward(k, step):
        for piece in range(2):
            copies[k, piece, step].wait_recv()
            if step < n - 2:
                start(k, piece, step + 1)

    mine.wait()
    start(0, 0, 0)
    start(0, 1, 0)
    lead = (n - 1) // 2
    for step in range(lead):
        forward(0, step)
    for one in moves:
        one.wait()
    parts = []
    for far in range(1, fan):
        target = (me + far) % fan
        for which, (src, into) in enumerate(((part_ref, landed), (few_ref, few_landed))):
            rest = src.shape[0] // fan
            one = pltpu.make_async_remote_copy(
                src_ref=src.at[pl.ds(target * rest, rest), :],
                dst_ref=into.at[far],
                send_sem=part_send.at[which, far],
                recv_sem=part_recv.at[which, far],
                device_id={"fsdp": target},
                device_id_type=MESH,
            )
            one.start()
            parts.append(one)
    start(1, 0, 0)
    start(1, 1, 0)
    for step in range(n - 1):
        forward(1, step)
        if lead + step < n - 1:
            forward(0, lead + step)
    for one in parts:
        one.wait()
    for src, into, out in ((part_ref, landed, sum_ref), (few_ref, few_landed, few_sum_ref)):
        rest = src.shape[0] // fan
        total = src[pl.ds(pl.multiple_of(me * rest, rest), rest), :].astype(jnp.float32)
        for far in range(1, fan):
            total = total + into[far].astype(jnp.float32)
        out[...] = total
    for one in [*copies.values(), *sums.values()]:
        one.wait_send()


def units_total(grads, part, few, ident):
    n, fan = lax.axis_size("seq"), lax.axis_size("fsdp")
    rows, width = grads.shape[0] // (3 * n), grads.shape[1]
    tokens = part.shape[0] // fan
    sems = lambda *shape: pltpu.SemaphoreType.DMA(shape)
    return ring_call(
        functools.partial(units_kernel, n, fan),
        "units_total",
        [grads, part, few],
        [
            ((n * 2 * fan * rows, width // fan), jnp.bfloat16),
            ((n * rows, width), jnp.bfloat16),
            ((tokens, part.shape[1]), jnp.float32),
            ((few.shape[0] // fan, few.shape[1]), jnp.float32),
        ],
        [
            pltpu.VMEM(((n - 1) * 3 * rows, width), jnp.bfloat16),
            pltpu.VMEM((3 * rows, width), jnp.bfloat16),
            pltpu.VMEM((fan, tokens, part.shape[1]), jnp.bfloat16),
            pltpu.VMEM((fan, few.shape[0] // fan, few.shape[1]), jnp.bfloat16),
        ]
        + [sems(fan, n - 1), sems(fan, n - 1), sems(fan, 2), sems(fan, 2), sems(3)]
        + [sems(4, n - 1), sems(4, n - 1), sems(2, fan), sems(2, fan)],
        ident,
    )


def team(n):
    s, f = lax.axis_index("seq"), lax.axis_index("fsdp")
    half = s // (n // 2)
    away = (half + f) % 2
    return f // 2, half, (s + away * (n // 2)) % n


def swap_kernel(n, fan, count, fars, fresh, *refs):
    given = count + (len(fars) > 0) + (0 if fresh else 2)
    x_refs, y_refs = refs[:count], refs[given : given + count]
    sems = refs[given + count + (2 if fars else 0) :]
    send_sem, recv_sem, own_sem = sems[:3]
    pair, half, rank = team(n)
    me = lax.axis_index("fsdp")

    def device(other):
        away = (other // (n // 2) + half) % 2
        return {"seq": (other + away * (n // 2)) % n, "fsdp": 2 * pair + (half + away) % 2}

    barrier = pltpu.get_barrier_semaphore()
    for j in range(1, n):
        pl.semaphore_signal(barrier, inc=1, device_id=device((rank + j) % n), device_id_type=MESH)
    travel = [far for far in fars if far]
    for far in travel:
        pl.semaphore_signal(barrier, inc=1, device_id={"fsdp": (me + fan - far) % fan}, device_id_type=MESH)
    pl.semaphore_wait(barrier, n - 1 + len(travel))
    copies = []
    for k in range(count):
        for j in range(1, n):
            other = (rank + j) % n
            one = pltpu.make_async_remote_copy(
                src_ref=x_refs[k].at[other],
                dst_ref=y_refs[k].at[rank],
                send_sem=send_sem.at[k, j],
                recv_sem=recv_sem.at[k, j],
                device_id=device(other),
                device_id_type=MESH,
            )
            one.start()
            copies.append(one)
    for k in range(count):
        one = pltpu.make_async_copy(x_refs[k].at[rank], y_refs[k].at[rank], own_sem.at[k])
        one.start()
        copies.append(one)
    if fars:
        w_ref, halves = refs[count], refs[given + count : given + count + 2]
        far_send, far_recv, far_own, stage = sems[3:]
        rest = []
        units, cols = halves[0].shape[0], w_ref.shape[1]
        for i, far in enumerate(fars):
            target = (me + far) % fan
            for part in range(2):
                src = w_ref.at[pl.ds((part * fan + target) * units, units), :]
                dst = halves[part].at[:, pl.ds(pl.multiple_of(me * cols, 128), cols)]
                if far:
                    one = pltpu.make_async_remote_copy(
                        src_ref=src,
                        dst_ref=dst,
                        send_sem=far_send.at[i, part],
                        recv_sem=far_recv.at[i, part],
                        device_id={"fsdp": target},
                        device_id_type=MESH,
                    )
                else:
                    one = pltpu.make_async_copy(src, stage.at[part], far_own.at[0, part])
                    rest.append((one, pltpu.make_async_copy(stage.at[part], dst, far_own.at[1, part])))
                one.start()
                if far:
                    copies.append(one)
        for inward, outward in rest:
            inward.wait()
            outward.start()
            copies.append(outward)
    for one in copies:
        one.wait()


def swap(arrays, ident, fars=(), given=None, halves=None):
    n, fan = lax.axis_size("seq"), lax.axis_size("fsdp")
    count = len(arrays)
    size = sum(v.size * 2 for v in arrays)
    operands, outs, alias = list(arrays), [jax.ShapeDtypeStruct(v.shape, v.dtype) for v in arrays], {}
    scratch = [
        pltpu.SemaphoreType.DMA((count, n)),
        pltpu.SemaphoreType.DMA((count, n)),
        pltpu.SemaphoreType.DMA((count,)),
    ]
    if fars:
        operands.append(given)
        shape = (given.shape[0] // (2 * fan), given.shape[1] * fan)
        outs += [jax.ShapeDtypeStruct(shape, given.dtype)] * 2
        scratch += [pltpu.SemaphoreType.DMA((len(fars), 2))] * 2 + [
            pltpu.SemaphoreType.DMA((2, 2)),
            pltpu.VMEM((2, given.shape[0] // (2 * fan), given.shape[1]), given.dtype),
        ]
        if halves is not None:
            operands += list(halves)
            alias = {count + 1: count, count + 2: count + 1}
    return pl.pallas_call(
        functools.partial(swap_kernel, n, fan, count, fars, not fars or halves is None),
        name="swap",
        out_shape=outs,
        in_specs=[pl.BlockSpec(memory_space=pl.ANY)] * len(operands),
        out_specs=[pl.BlockSpec(memory_space=pl.ANY)] * len(outs),
        scratch_shapes=scratch,
        input_output_aliases=alias,
        compiler_params=pltpu.CompilerParams(collective_id=ident, has_side_effects=True),
        cost_estimate=pl.CostEstimate(flops=0, bytes_accessed=size, transcendentals=0),
    )(*operands)


def norm_apply(value, gain):
    return value * lax.rsqrt(jnp.mean(value * value, axis=-1, keepdims=True) + EPS) * gain


def norm_back(value, gain, grad):
    _, pull = jax.vjp(norm_apply, value, gain)
    return pull(grad)


def gate_mix(gate, up):
    return jax.nn.gelu(gate, approximate=True) * up


def counts_below(ids, values):
    total = jnp.zeros_like(values)
    for doc in range(DOCS):
        total = total + jnp.where(values > doc, jnp.sum((ids == doc).astype(jnp.int32)), 0)
    return total


def change_home(value):
    n, fan = lax.axis_size("seq"), lax.axis_size("fsdp")
    pairs = []
    for s in range(n):
        for f in range(fan):
            away = (s // (n // 2) + f) % 2
            target = ((s + n // 2) % n, f ^ 1) if away else (s, f)
            pairs.append((s * fan + f, target[0] * fan + target[1]))
    return lax.ppermute(value, ("seq", "fsdp"), pairs)


def spread(blocks):
    fan, me = lax.axis_size("fsdp"), lax.axis_index("fsdp")
    result = blocks
    for far in range(1, fan):
        block = lax.dynamic_index_in_dim(blocks, (me + far) % fan, 0, True)
        block = lax.ppermute(block, "fsdp", [(f, (f + far) % fan) for f in range(fan)])
        result = lax.dynamic_update_slice_in_dim(result, block, (me - far) % fan, 0)
    return result


def flat(blocks):
    return jnp.transpose(blocks, (1, 0, 2)).reshape(blocks.shape[1], -1)


def by_rows(value):
    return with_layout_constraint(value, Layout(major_to_minor=tuple(range(value.ndim))))


def scatter(grad):
    return lax.psum_scatter(grad, "fsdp", scatter_dimension=0, tiled=True)


def shards(
    layer_in, encoder, decoder_ids, encoder_ids, rel_buckets,
    norm_self, self_qkv, self_out, rel_table, norm_cross, cross_q, cross_kv, cross_out, norm_ff, ff_in, ff_out,
    cotangent,
):
    seqs, local, width = layer_in.shape
    enc_local = encoder.shape[1]
    parts = lax.axis_size("seq")
    heads = self_qkv.shape[1]
    dh = self_qkv.shape[2] // 3
    own = heads // parts
    rows = seqs * local
    buckets, table_own = rel_table.shape
    length, keys = local * parts, enc_local * parts
    gather = lambda v: lax.all_gather(v, "fsdp", axis=0, tiled=True)

    fan = lax.axis_size("fsdp")
    units = ff_in.shape[1] // (2 * fan)
    part = norm_self.shape[0]
    pair, half, rank = team(parts)

    qkv_w = gather(self_qkv)
    small = jnp.concatenate([norm_self, norm_cross, norm_ff, rel_table.reshape(-1)])
    small = lax.all_gather(small, "fsdp", axis=0, tiled=False)
    early = by_rows(jnp.stack([self_out, cross_q, *jnp.split(cross_kv.reshape(-1, 2 * width), 2, axis=1)]))
    small, early = lax.optimization_barrier((small, early))
    early = lax.all_gather(early, "fsdp", axis=1, tiled=True)
    both_ids = jnp.concatenate([decoder_ids.reshape(-1), encoder_ids.reshape(-1)])
    both_ids = change_home(jnp.pad(both_ids, (0, 1024 - local - enc_local)).reshape(8, 128))
    inner_t = ff_in.T
    by_kernel = (width // fan) % 128 == 0 and fan % 2 == 0 and (ff_in.shape[0] // parts) % 8 == 0
    (both_ids,) = swap([jnp.broadcast_to(both_ids[None], (parts, 8, 128))], 13)
    home = change_home(layer_in.reshape(rows, width))
    early = by_rows(early)
    gain_first, gain_second, gain_third = (
        small[:, i * part : (i + 1) * part].reshape(width).astype(f32) for i in range(3)
    )
    table = jnp.transpose(small[:, 3 * part :].reshape(-1, buckets, table_own), (1, 0, 2)).reshape(buckets, heads)
    both_ids = both_ids.reshape(parts, 1024)
    ids = both_ids[:, :local].reshape(length)
    enc_ids = both_ids[:, local : local + enc_local].reshape(keys)

    first_seen = counts_below(ids, ids)
    enc_first = counts_below(enc_ids, ids)
    enc_last = counts_below(enc_ids, ids + 1)
    blocks = length // BQ
    bk = BQ
    self_rows = jnp.broadcast_to(first_seen[None], (8, length))
    cross_rows = jnp.concatenate([enc_first[None], enc_last[None], jnp.zeros((6, length), jnp.int32)])
    self_limits = jnp.stack(
        [first_seen[::BQ] // bk, (jnp.arange(blocks, dtype=jnp.int32) + 1) * (BQ // bk)]
    )
    cross_limits = jnp.stack([enc_first[::BQ] // bk, (enc_last[BQ - 1 :: BQ] + bk - 1) // bk])

    first_head = rank * own
    table_mine = lax.dynamic_slice_in_dim(table.astype(f32), first_head, own, 1)
    near = rel_buckets[:REACH]
    onehot = (near[:, None] == jnp.arange(buckets, dtype=jnp.int32)[None, :]).astype(f32)
    bias = jnp.einsum("ln,ng->gl", onehot, table_mine, precision=HIGH)
    ext = jnp.concatenate(
        [jnp.full((own, BQ), MASKED, f32), bias, jnp.zeros((own, BQ), f32)], axis=1
    )

    qkv_w, home, inner_t, ext, self_rows, cross_rows, self_limits, cross_limits = lax.optimization_barrier(
        (qkv_w, home, inner_t, ext, self_rows, cross_rows, self_limits, cross_limits)
    )
    qkv_w = qkv_w.reshape(width, parts, own * 3 * dh)

    stream = home.astype(f32)
    normed_first = norm_apply(stream, gain_first).astype(bf16)
    qkv_tok = jnp.einsum("td,dge->gte", normed_first, qkv_w, preferred_element_type=f32).astype(bf16)
    others = change_home(jnp.concatenate([cotangent.reshape(rows, width), encoder.reshape(-1, width)]))
    grad_low, enc_flat = others[:rows], others[rows:]
    fars = [tuple(far for far in range(fan) if by_kernel and (far == 2) == first) for first in (True, False)]
    qkv, *halves = swap([qkv_tok], 17, fars[0], inner_t)
    qkv, cross_out, grad_low = lax.optimization_barrier((qkv, cross_out, grad_low))
    if rows == cross_out.shape[0]:
        mix_cross, grad_group = lax.all_gather(jnp.stack([cross_out, grad_low]), "fsdp", axis=1, tiled=True)
    else:
        mix_cross, grad_group = gather(cross_out), gather(grad_low)
    mix_cross = mix_cross.reshape(parts, own * dh, width)
    qkv = qkv.reshape(length, own * 3 * dh)
    out_self, self_t, self_lse = self_forward(self_limits, self_rows, ext, qkv)
    (self_tok,) = swap([out_self.reshape(parts, local, own * dh)], 11)
    after_self, normed_second, query_tok, pairs_tok = over_weights(
        into_kernel,
        "self_out_to_cross",
        [self_tok, home, gain_second.reshape(1, width), enc_flat],
        early,
        lambda i: i,
        [
            ((rows, width), f32),
            ((rows, width), bf16),
            ((parts, rows, own * dh), bf16),
            ((parts, enc_local, own * 2 * dh), bf16),
        ],
    )
    query_cross, pairs = swap([query_tok, pairs_tok], 12)
    query_cross, pairs = query_cross.reshape(length, own * dh), pairs.reshape(keys, own * 2 * dh)
    out_cross, cross_t, cross_lse = cross_forward(cross_limits, cross_rows, query_cross, pairs)
    cross_tok, *halves = swap([out_cross.reshape(parts, local, own * dh)], 16, fars[1], inner_t, halves)
    if not by_kernel:
        halves = spread(jnp.transpose(inner_t.reshape(2, fan, units, -1), (1, 0, 2, 3)))
        halves = [jnp.transpose(halves[:, i], (1, 0, 2)).reshape(units, width) for i in range(2)]
    gate_t, up_t = halves
    after_cross = after_self + jnp.einsum("gtc,gcd->td", cross_tok, mix_cross, preferred_element_type=f32)
    normed_third = norm_apply(after_cross, gain_third).astype(bf16)
    normed_group = gather(normed_third)
    gate = jnp.einsum("td,fd->tf", normed_group, gate_t, preferred_element_type=f32)
    up = jnp.einsum("td,fd->tf", normed_group, up_t, preferred_element_type=f32)
    hidden = gate_mix(gate, up).astype(bf16)

    grad_hidden = jnp.einsum("td,fd->tf", grad_group, ff_out, preferred_element_type=f32)
    _, pull_mix = jax.vjp(gate_mix, gate, up)
    grad_gate, grad_up = (g.astype(bf16) for g in pull_mix(grad_hidden))
    grad_third_in = jnp.dot(grad_gate, gate_t, preferred_element_type=f32) + jnp.dot(
        grad_up, up_t, preferred_element_type=f32
    )
    grad_third_in = scatter(grad_third_in.astype(bf16))
    outer_part = jnp.dot(hidden, ff_out, preferred_element_type=f32).astype(bf16)
    grad_units = [
        jnp.einsum("tf,td->fd", g, y, preferred_element_type=f32).astype(bf16)
        for g, y in ((grad_gate, normed_group), (grad_up, normed_group), (hidden, grad_group))
    ]
    if by_kernel:
        grad_units = jnp.stack([g.reshape(parts, units // parts, width) for g in grad_units], axis=1)
        grad_units = grad_units.reshape(3 * units, width)
    grad_third_in, outer_part, part_units = lax.optimization_barrier((grad_third_in, outer_part, grad_units))
    grad_third_in = grad_third_in.astype(f32)
    grad_from_third, grad_gain_third = norm_back(after_cross, gain_third, grad_third_in)
    grad_middle = grad_low.astype(f32) + grad_from_third
    middle_low = grad_middle.astype(bf16)
    grad_mix_cross = jnp.einsum("gtc,td->gcd", cross_tok, middle_low, preferred_element_type=f32)
    part_cross = scatter(grad_mix_cross.reshape(width, width).astype(bf16))
    grad_cross_tok = jnp.einsum("td,gcd->gtc", middle_low, mix_cross, preferred_element_type=f32).astype(bf16)
    (grad_cross,) = swap([grad_cross_tok], 11)
    grad_cross = grad_cross.reshape(length, own * dh)
    grad_query, grad_pairs = cross_backward(
        cross_limits, cross_rows, query_cross, pairs, grad_cross, cross_t, cross_lse
    )
    grad_query_tok, grad_pairs_tok = swap(
        [grad_query.reshape(parts, local, own * dh), grad_pairs.reshape(parts, enc_local, own * 2 * dh)], 12
    )
    (
        grad_upper, upper_low, grad_self_tok, grad_gain_second, grad_encoder, grad_query_tok, grad_pairs_tok
    ) = over_weights(
        outof_kernel,
        "cross_to_self_out",
        [grad_query_tok, grad_pairs_tok, after_self, gain_second.reshape(1, width), grad_middle],
        early,
        lambda i: jnp.where(i < 2, 1 - i, i),
        [
            ((rows, width), f32),
            ((rows, width), bf16),
            ((parts, rows, own * dh), bf16),
            ((1, width), f32),
            ((enc_local, width), bf16),
            ((rows, width), bf16),
            ((enc_local, 2 * width), bf16),
        ],
        [((enc_local, width), f32)],
    )
    grad_query_w = jnp.einsum("td,te->de", normed_second, grad_query_tok, preferred_element_type=f32)
    grad_pairs_w = jnp.einsum("td,te->de", enc_flat, grad_pairs_tok, preferred_element_type=f32)
    grad_mix_self = jnp.einsum("gtc,td->gcd", self_tok, upper_low, preferred_element_type=f32)
    grad_mid = jnp.concatenate([grad_query_w.astype(bf16), grad_pairs_w.astype(bf16)], axis=1)
    part_self = scatter(grad_mix_self.reshape(width, width).astype(bf16))
    grad_self_tok, grad_mid = lax.optimization_barrier((grad_self_tok, grad_mid))
    part_mid = scatter(grad_mid)
    (grad_self,) = swap([grad_self_tok], 11)
    grad_self = grad_self.reshape(length, own * dh)
    grad_qkv, diagonals = self_backward(self_limits, self_rows, ext, qkv, grad_self, self_t, self_lse)
    (grad_qkv_tok,) = swap([grad_qkv.reshape(parts, local, own * 3 * dh)], 10)
    grad_qkv_tok = flat(grad_qkv_tok)
    grad_qkv_w = jnp.einsum("td,te->de", normed_first, grad_qkv_tok, preferred_element_type=f32)
    grad_qkv_w, grad_qkv_tok = lax.optimization_barrier((grad_qkv_w.astype(bf16), grad_qkv_tok))
    grad_first_in = jnp.einsum("te,de->td", grad_qkv_tok, qkv_w.reshape(width, -1), preferred_element_type=f32)
    grad_from_first, grad_gain_first = norm_back(stream, gain_first, grad_first_in)
    grad_layer_in = (grad_upper + grad_from_first).astype(bf16)
    bucket_line = jnp.concatenate([jnp.full((BQ - 1,), -1, jnp.int32), near, jnp.full((BQ + 1,), -1, jnp.int32)])
    in_bucket = (bucket_line[:, None] == jnp.arange(buckets, dtype=jnp.int32)).astype(f32)
    by_bucket = jnp.einsum("xn,gx->ng", in_bucket, diagonals, precision=HIGH)
    grad_table = lax.dynamic_update_slice_in_dim(jnp.zeros((buckets, heads), f32), by_bucket, first_head, 1)

    gains = jnp.concatenate(
        [g.reshape(-1, part) for g in (grad_gain_first, grad_gain_second, grad_gain_third)], axis=1
    )
    tables = jnp.transpose(grad_table.reshape(buckets, -1, table_own), (1, 0, 2)).reshape(-1, buckets * table_own)
    small_grads = jnp.concatenate([gains, tables], axis=1).astype(bf16)
    small_size = small_grads.shape[1]
    going_home = jnp.concatenate([grad_layer_in, grad_encoder.astype(bf16)])
    part_last = scatter(grad_qkv_w)
    going_home, small_grads, part_units, part_cross, part_mid = lax.optimization_barrier(
        (change_home(going_home), small_grads, part_units, part_cross, part_mid)
    )
    if by_kernel:
        few = jnp.pad(small_grads[:, None], ((0, 0), (0, 7), (0, 1024 - small_size))).reshape(fan * 8, 1024)
        total_inner, total_outer, outer_sum, few = units_total(part_units, outer_part, few, 0)
        few = jnp.pad(few[0].astype(bf16).reshape(8, 128), ((0, parts * 8 - 8), (0, 0)))
        total_cross, total_self, total_mid, total_qkv, small_total, total_inner = ring_total(
            [part_cross, part_self, part_mid, part_last, few], (1, 1, 2, 2, 1), 1, total_inner
        )
    else:
        grad_units = [lax.psum(g, "seq") for g in part_units]
        total_inner = spread(jnp.transpose(jnp.stack(grad_units[:2]).reshape(2, units, fan, -1), (2, 0, 1, 3)))
        total_inner = jnp.transpose(total_inner, (3, 1, 0, 2)).reshape(-1, 2 * fan * units).astype(f32)
        total_outer, outer_sum = grad_units[2], scatter(outer_part).astype(f32)
        few = lax.dynamic_index_in_dim(lax.psum(small_grads, "fsdp"), lax.axis_index("fsdp"), 0, False)
        total_cross, total_self, total_mid, total_qkv, small_total = (
            lax.psum(v, "seq") for v in (part_cross, part_self, part_mid, part_last, few)
        )
    layer_out = (after_cross + outer_sum).astype(bf16)
    layer_out, total_inner, total_outer, total_cross, total_self, total_mid, total_qkv, going_home = (
        lax.optimization_barrier(
            (layer_out, total_inner, total_outer, total_cross, total_self, total_mid, total_qkv, going_home)
        )
    )
    layer_out = change_home(layer_out).reshape(seqs, local, width)
    grad_layer_in = going_home[:rows].astype(f32).reshape(seqs, local, width)
    grad_encoder = going_home[rows:].astype(f32).reshape(seqs, enc_local, width)
    total_inner, total_outer, total_mid, total_qkv = (
        v.astype(f32) for v in (total_inner, total_outer, total_mid, total_qkv)
    )
    total_query, total_mix_cross = total_mid[:, :width], total_cross.astype(f32)
    total_pairs = total_mid[:, width:].reshape(-1, heads, 2 * dh)
    total_mix_self, total_qkv = total_self.astype(f32), total_qkv.reshape(-1, heads, 3 * dh)
    mine = small_total.reshape(-1)[:small_size].astype(f32)
    total_gain_first, total_gain_second, total_gain_third = (mine[i * part : (i + 1) * part] for i in range(3))
    total_table = mine[3 * part :].reshape(buckets, table_own)
    return (
        layer_out, grad_layer_in, grad_encoder, total_gain_first, total_qkv, total_mix_self, total_table,
        total_gain_second, total_query, total_pairs, total_mix_cross, total_gain_third, total_inner, total_outer,
    )


def solution(mesh):
    in_specs = (
        P("fsdp", "seq", None), P("fsdp", "seq", None), P("fsdp", "seq"), P("fsdp", "seq"), P(),
        P("fsdp"), P("fsdp", None, None), P("fsdp", None), P(None, "fsdp"), P("fsdp"), P("fsdp", None),
        P("fsdp", None, None), P("fsdp", None), P("fsdp"), P("fsdp", None), P("fsdp", None),
        P("fsdp", "seq", None),
    )
    out_specs = (
        P("fsdp", "seq", None), P("fsdp", "seq", None), P("fsdp", "seq", None), P("fsdp"), P("fsdp", None, None),
        P("fsdp", None), P(None, "fsdp"), P("fsdp"), P("fsdp", None), P("fsdp", None, None), P("fsdp", None),
        P("fsdp"), P("fsdp", None), P("fsdp", None),
    )
    return jax.shard_map(shards, mesh=mesh, in_specs=in_specs, out_specs=out_specs, check_vma=False)
```

```python
import functools

import jax
import jax.numpy as jnp
from jax import lax
from jax.experimental import pallas as pl
from jax.experimental.layout import Layout, with_layout_constraint
from jax.experimental.pallas import tpu as pltpu
from jax.sharding import PartitionSpec as P

EPS = 1e-06
HIGH = lax.Precision.HIGHEST
MASKED = -1e30
DOCS = 4

BQ = 256
REACH = 1024


def blk(index, size):
    return pl.ds(pl.multiple_of(index * size, size), size)


def turn(value):
    return jnp.transpose(value.astype(jnp.float32), (1, 0))


def bias_tiles(ext_ref, tile_ref, own):
    for h in range(own):
        line = jnp.broadcast_to(ext_ref[h : h + 1, :], tile_ref.shape[1:])
        tile_ref[h] = pltpu.roll(line, 0, 1, stride=1, stride_axis=0)


def unpack(ref, own, width, picks, flips, base):
    block = 256

    def one(b, _):
        rows = blk(b, block)
        value = ref[rows, :]
        if flips:
            flat = turn(value).astype(jnp.bfloat16)
            for target, piece in flips:
                for h in range(own):
                    at = h * width + piece * 64
                    target[base + h, :, rows] = flat[at : at + 64]
        for target, piece in picks:
            for h in range(own):
                at = h * width + piece * 64
                target[base + h, rows, :] = value[:, at : at + 64]
        return 0

    lax.fori_loop(0, ref.shape[0] // block, one, 0)


def dot(a, b):
    return jnp.dot(a, b, preferred_element_type=jnp.float32)


def score(own_index, key_tile, query_t, tile_ref, t, low, high, first_key):
    value = dot(key_tile, query_t)
    place = lax.broadcasted_iota(jnp.int32, value.shape, 0)
    keep = place >= low - first_key
    if high is not None:
        keep = keep & (place < high - first_key)
    else:
        value = value + tile_ref[own_index, :, blk(t + 1, BQ)]
    return jnp.where(keep, value, MASKED)


def forward_body(own, bk, causal, lim_ref, rows_ref, q_t, k_rows, v_t, tile_ref, o_ref, ot_ref, lse_ref):
    length = o_ref.shape[0]

    def q_block(i, _):
        cols = blk(i, BQ)
        queries = [q_t[h, :, cols] for h in range(own)]
        low = rows_ref[0:1, cols]
        high = None if causal else rows_ref[1:2, cols]

        def k_block(j, carry):
            keys = blk(j, bk)
            t = i - j
            out = []
            for h in range(own):
                top, total, acc = carry[h]
                s = score(h, k_rows[h, keys, :], queries[h], tile_ref, t, low, high, j * bk)
                new_top = jnp.maximum(top, jnp.max(s, axis=0, keepdims=True))
                p = jnp.exp(s - new_top)
                scale = jnp.exp(top - new_top)
                total = total * scale + jnp.sum(p, axis=0, keepdims=True)
                acc = acc * scale + dot(v_t[h, :, keys], p.astype(jnp.bfloat16))
                out.append((new_top, total, acc))
            return tuple(out)

        start = tuple(
            (
                jnp.full((1, BQ), MASKED, jnp.float32),
                jnp.zeros((1, BQ), jnp.float32),
                jnp.zeros((64, BQ), jnp.float32),
            )
            for _ in range(own)
        )
        ends = lax.fori_loop(lim_ref[0, i], lim_ref[1, i], k_block, start)
        for h in range(own):
            top, total, acc = ends[h]
            ot_ref[h * 64 : h * 64 + 64, cols] = acc / total
            lse_ref[h : h + 1, cols] = top + jnp.log(total)
        o_ref[cols, :] = turn(ot_ref[:, cols]).astype(jnp.bfloat16)
        return 0

    lax.fori_loop(0, length // BQ, q_block, 0)


def self_forward_kernel(own, bk, lim_ref, rows_ref, ext_ref, x_ref, o_ref, ot_ref, lse_ref, q_t, k_rows, v_t, tile_ref):
    bias_tiles(ext_ref, tile_ref, own)
    unpack(x_ref, own, 192, [(k_rows, 1)], [(q_t, 0), (v_t, 2)], 0)
    forward_body(own, bk, True, lim_ref, rows_ref, q_t, k_rows, v_t, tile_ref, o_ref, ot_ref, lse_ref)


def cross_forward_kernel(own, bk, lim_ref, rows_ref, q_ref, kv_ref, o_ref, ot_ref, lse_ref, q_t, k_rows, v_t):
    unpack(q_ref, own, 64, [], [(q_t, 0)], 0)
    unpack(kv_ref, own, 128, [(k_rows, 0)], [(v_t, 1)], 0)
    forward_body(own, bk, False, lim_ref, rows_ref, q_t, k_rows, v_t, None, o_ref, ot_ref, lse_ref)


def backward_body(
    own, bk, causal, lim_ref, rows_ref, do_ref, ot_ref, lse_ref,
    q_t, q_rows, k_t, k_rows, v_rows, do_t, do_rows, tile_ref, sum_ref, dq_t, dk, dv,
):
    length = do_ref.shape[0]
    dk[...] = jnp.zeros_like(dk)
    dv[...] = jnp.zeros_like(dv)
    if causal:
        sum_ref[...] = jnp.zeros_like(sum_ref)

    def q_block(i, _):
        cols = blk(i, BQ)
        low = rows_ref[0:1, cols]
        high = None if causal else rows_ref[1:2, cols]
        per_head = []
        for h in range(own):
            grad_t = do_t[h, :, cols]
            delta = jnp.sum(
                grad_t.astype(jnp.float32) * ot_ref[h * 64 : h * 64 + 64, cols], axis=0, keepdims=True
            )
            per_head.append((q_t[h, :, cols], grad_t, delta, lse_ref[h : h + 1, cols]))

        def k_block(j, carry):
            keys = blk(j, bk)
            t = i - j
            out = []
            for h in range(own):
                query_t, grad_t, delta, lse = per_head[h]
                s = score(h, k_rows[h, keys, :], query_t, tile_ref, t, low, high, j * bk)
                p = jnp.exp(s - lse)
                dp = dot(v_rows[h, keys, :], grad_t)
                ds = (p * (dp - delta)).astype(jnp.bfloat16)
                dv[h, keys, :] += dot(p.astype(jnp.bfloat16), do_rows[h, cols, :])
                dk[h, keys, :] += dot(ds, q_rows[h, cols, :])
                if causal:
                    sum_ref[h, :, blk(t, BQ)] += ds.astype(jnp.float32)
                out.append(carry[h] + dot(k_t[h, :, keys], ds))
            return tuple(out)

        ends = lax.fori_loop(
            lim_ref[0, i],
            lim_ref[1, i],
            k_block,
            tuple(jnp.zeros((64, BQ), jnp.float32) for _ in range(own)),
        )
        for h in range(own):
            dq_t[h * 64 : h * 64 + 64, cols] = ends[h]
        return 0

    lax.fori_loop(0, length // BQ, q_block, 0)


def diagonal_sums(sum_ref, u_ref, own):
    flip = lax.broadcasted_iota(jnp.int32, (BQ, BQ), 0) + lax.broadcasted_iota(jnp.int32, (BQ, BQ), 1) == BQ - 1
    flip = jnp.where(flip, 1.0, 0.0).astype(jnp.bfloat16)
    for h in range(own):
        grid = sum_ref[h]
        high = grid.astype(jnp.bfloat16)
        low = (grid - high.astype(jnp.float32)).astype(jnp.bfloat16)
        upside = dot(flip, high) + dot(flip, low)
        wide = jnp.concatenate([upside, jnp.zeros((BQ, BQ), jnp.float32)], axis=1)
        aligned = pltpu.roll(wide, 0, 1, stride=1, stride_axis=0)
        u_ref[h : h + 1, :] = jnp.sum(aligned, axis=0, keepdims=True)


def self_backward_kernel(
    own, bk, lim_ref, rows_ref, ext_ref, x_ref, do_ref, ot_ref, lse_ref, dx_ref, u_ref,
    q_t, q_rows, k_t, k_rows, v_rows, do_t, do_rows, tile_ref, sum_ref, dq_t, dk, dv,
):
    bias_tiles(ext_ref, tile_ref, own)
    unpack(x_ref, own, 192, [(q_rows, 0), (k_rows, 1), (v_rows, 2)], [(q_t, 0), (k_t, 1)], 0)
    unpack(do_ref, own, 64, [(do_rows, 0)], [(do_t, 0)], 0)
    backward_body(
        own, bk, True, lim_ref, rows_ref, do_ref, ot_ref, lse_ref,
        q_t, q_rows, k_t, k_rows, v_rows, do_t, do_rows, tile_ref, sum_ref, dq_t, dk, dv,
    )
    diagonal_sums(sum_ref, u_ref, own)

    def pack(b, _):
        rows = blk(b, 256)
        dq = turn(dq_t[:, rows])
        pieces = []
        for h in range(own):
            pieces += [dq[:, h * 64 : h * 64 + 64], dk[h, rows, :], dv[h, rows, :]]
        dx_ref[rows, :] = jnp.concatenate(pieces, axis=1).astype(jnp.bfloat16)
        return 0

    lax.fori_loop(0, x_ref.shape[0] // 256, pack, 0)


def cross_backward_kernel(
    own, bk, lim_ref, rows_ref, q_ref, kv_ref, do_ref, ot_ref, lse_ref, dq_ref, dkv_ref,
    q_t, q_rows, k_t, k_rows, v_rows, do_t, do_rows, dq_t, dk, dv,
):
    unpack(q_ref, own, 64, [(q_rows, 0)], [(q_t, 0)], 0)
    unpack(kv_ref, own, 128, [(k_rows, 0), (v_rows, 1)], [(k_t, 0)], 0)
    unpack(do_ref, own, 64, [(do_rows, 0)], [(do_t, 0)], 0)
    backward_body(
        own, bk, False, lim_ref, rows_ref, do_ref, ot_ref, lse_ref,
        q_t, q_rows, k_t, k_rows, v_rows, do_t, do_rows, None, None, dq_t, dk, dv,
    )

    def pack_q(b, _):
        rows = blk(b, 256)
        dq_ref[rows, :] = turn(dq_t[:, rows]).astype(jnp.bfloat16)
        return 0

    def pack_kv(b, _):
        rows = blk(b, 256)
        pieces = []
        for h in range(own):
            pieces += [dk[h, rows, :], dv[h, rows, :]]
        dkv_ref[rows, :] = jnp.concatenate(pieces, axis=1).astype(jnp.bfloat16)
        return 0

    lax.fori_loop(0, q_ref.shape[0] // 256, pack_q, 0)
    lax.fori_loop(0, kv_ref.shape[0] // 256, pack_kv, 0)


SMEM = pl.BlockSpec(memory_space=pltpu.SMEM)
VMEM = pl.BlockSpec(memory_space=pltpu.VMEM)
bf16, f32 = jnp.bfloat16, jnp.float32


def call(body, name, operands, outs, scratch, flops):
    size = sum(v.size * v.dtype.itemsize for v in operands)
    return pl.pallas_call(
        body,
        name=name,
        out_shape=[jax.ShapeDtypeStruct(s, d) for s, d in outs],
        in_specs=[SMEM] + [VMEM] * (len(operands) - 1),
        out_specs=[VMEM] * len(outs),
        scratch_shapes=[pltpu.VMEM(s, d) for s, d in scratch],
        compiler_params=pltpu.CompilerParams(vmem_limit_bytes=40 << 20),
        cost_estimate=pl.CostEstimate(flops=0, bytes_accessed=size, transcendentals=0),
    )(*operands)


def self_forward(limits, rows, ext, x, bk=BQ):
    length, own = x.shape[0], x.shape[1] // 192
    return call(
        functools.partial(self_forward_kernel, own, bk),
        "self_forward",
        [limits, rows, ext, x],
        [((length, own * 64), bf16), ((own * 64, length), f32), ((own, length), f32)],
        [
            ((own, 64, length), bf16),
            ((own, length, 64), bf16),
            ((own, 64, length), bf16),
            ((own, BQ, REACH + 2 * BQ), f32),
        ],
        length * length * own * 64,
    )


def cross_forward(limits, rows, q, kv, bk=BQ):
    length, own, keys = q.shape[0], q.shape[1] // 64, kv.shape[0]
    return call(
        functools.partial(cross_forward_kernel, own, bk),
        "cross_forward",
        [limits, rows, q, kv],
        [((length, own * 64), bf16), ((own * 64, length), f32), ((own, length), f32)],
        [((own, 64, length), bf16), ((own, keys, 64), bf16), ((own, 64, keys), bf16)],
        length * keys * own * 128,
    )


def self_backward(limits, rows, ext, x, grad, o_t, lse, bk=BQ):
    length, own = x.shape[0], x.shape[1] // 192
    return call(
        functools.partial(self_backward_kernel, own, bk),
        "self_backward",
        [limits, rows, ext, x, grad, o_t, lse],
        [((length, own * 192), bf16), ((own, REACH + 2 * BQ), f32)],
        [
            ((own, 64, length), bf16),
            ((own, length, 64), bf16),
            ((own, 64, length), bf16),
            ((own, length, 64), bf16),
            ((own, length, 64), bf16),
            ((own, 64, length), bf16),
            ((own, length, 64), bf16),
            ((own, BQ, REACH + 2 * BQ), f32),
            ((own, BQ, REACH + BQ), f32),
            ((own * 64, length), f32),
            ((own, length, 64), f32),
            ((own, length, 64), f32),
        ],
        length * length * own * 160,
    )


def cross_backward(limits, rows, q, kv, grad, o_t, lse, bk=BQ):
    length, own, keys = q.shape[0], q.shape[1] // 64, kv.shape[0]
    return call(
        functools.partial(cross_backward_kernel, own, bk),
        "cross_backward",
        [limits, rows, q, kv, grad, o_t, lse],
        [((length, own * 64), bf16), ((keys, own * 128), bf16)],
        [
            ((own, 64, length), bf16),
            ((own, length, 64), bf16),
            ((own, 64, keys), bf16),
            ((own, keys, 64), bf16),
            ((own, keys, 64), bf16),
            ((own, 64, length), bf16),
            ((own, length, 64), bf16),
            ((own * 64, length), f32),
            ((own, keys, 64), f32),
            ((own, keys, 64), f32),
        ],
        length * keys * own * 320,
    )


def rows_of(blocks_ref):
    return jnp.concatenate([blocks_ref[g] for g in range(blocks_ref.shape[0])], axis=1)


def against(a, b):
    return lax.dot_general(a, b, (((1,), (1,)), ((), ())), preferred_element_type=jnp.float32)


def into_kernel(tok_ref, home_ref, gain_ref, enc_ref, w_ref, after_ref, norm_ref, query_ref, pairs_ref):
    which = pl.program_id(0)

    @pl.when(which == 0)
    def _():
        value = home_ref[...].astype(jnp.float32) + dot(rows_of(tok_ref), w_ref[0])
        after_ref[...] = value
        scale = lax.rsqrt(jnp.mean(value * value, axis=1, keepdims=True) + EPS)
        norm_ref[...] = (value * scale * gain_ref[...]).astype(jnp.bfloat16)

    @pl.when(which == 1)
    def _():
        query = dot(norm_ref[...], w_ref[0]).astype(jnp.bfloat16)
        cols = query_ref.shape[2]
        for g in range(query_ref.shape[0]):
            query_ref[g] = query[:, g * cols : (g + 1) * cols]

    for half in range(2):

        @pl.when(which == 2 + half)
        def _():
            pairs = dot(enc_ref[...], w_ref[0]).astype(jnp.bfloat16)
            groups, cols = pairs_ref.shape[0] // 2, pairs_ref.shape[2]
            for g in range(groups):
                pairs_ref[half * groups + g] = pairs[:, g * cols : (g + 1) * cols]


def outof_kernel(
    dq_ref, dkv_ref, after_ref, gain_ref, middle_ref, w_ref,
    upper_ref, low_ref, out_ref, gain_grad_ref, enc_grad_ref, dq_flat_ref, dkv_flat_ref, enc_sum,
):
    which = pl.program_id(0)

    @pl.when(which == 0)
    def _():
        grad_query = rows_of(dq_ref)
        dq_flat_ref[...] = grad_query
        dkv_flat_ref[...] = rows_of(dkv_ref)
        grad = against(grad_query, w_ref[0])
        value = after_ref[...]
        unit = value * lax.rsqrt(jnp.mean(value * value, axis=1, keepdims=True) + EPS)
        gain_grad_ref[...] = jnp.sum(grad * unit, axis=0, keepdims=True)
        scale = lax.rsqrt(jnp.mean(value * value, axis=1, keepdims=True) + EPS)
        grad = grad * gain_ref[...]
        inner = jnp.mean(grad * unit, axis=1, keepdims=True)
        upper = middle_ref[...] + scale * (grad - unit * inner)
        upper_ref[...] = upper
        low_ref[...] = upper.astype(jnp.bfloat16)

    @pl.when(which == 1)
    def _():
        grad = against(low_ref[...], w_ref[0]).astype(jnp.bfloat16)
        cols = out_ref.shape[2]
        for g in range(out_ref.shape[0]):
            out_ref[g] = grad[:, g * cols : (g + 1) * cols]

    width = w_ref.shape[1]

    @pl.when(which == 2)
    def _():
        enc_sum[...] = against(dkv_flat_ref[:, :width], w_ref[0])

    @pl.when(which == 3)
    def _():
        enc_grad_ref[...] = (enc_sum[...] + against(dkv_flat_ref[:, width:], w_ref[0])).astype(jnp.bfloat16)


def over_weights(body, name, arrays, weights, order, outs, scratch=()):
    count, rows, cols = weights.shape
    whole = lambda shape: pl.BlockSpec(shape, lambda i: (0,) * len(shape))
    return pl.pallas_call(
        body,
        name=name,
        grid=(count,),
        out_shape=[jax.ShapeDtypeStruct(s, d) for s, d in outs],
        in_specs=[whole(v.shape) for v in arrays] + [pl.BlockSpec((1, rows, cols), lambda i: (order(i), 0, 0))],
        out_specs=[whole(s) for s, _ in outs],
        scratch_shapes=[pltpu.VMEM(s, d) for s, d in scratch],
        compiler_params=pltpu.CompilerParams(vmem_limit_bytes=62 << 20, dimension_semantics=("arbitrary",)),
        cost_estimate=pl.CostEstimate(flops=0, bytes_accessed=weights.size * 2, transcendentals=0),
    )(*arrays, weights)


MESH = pl.DeviceIdType.MESH


def ring_place(index, n):
    z, x = index // 2, index % 2
    return z + x * (n - 1 - 2 * z)


def ring_index(place, n):
    x = place // (n // 2)
    z = place + x * (n - 1 - 2 * place)
    return 2 * z + x


def ring_greet(n, others):
    place = ring_place(lax.axis_index("seq"), n)
    right = ring_index((place + 1) % n, n)
    left = ring_index((place + n - 1) % n, n)
    barrier = pltpu.get_barrier_semaphore()
    for neighbour in (left, right):
        pl.semaphore_signal(barrier, inc=1, device_id={"seq": neighbour}, device_id_type=MESH)
    for other in others:
        pl.semaphore_signal(barrier, inc=1, device_id={"fsdp": other}, device_id_type=MESH)
    pl.semaphore_wait(barrier, 2 + len(others))
    return place, right, left


def ring_cut(shape, split, n):
    rows, cols = shape[0] // n, shape[1]
    return (rows, cols // split) if split > 0 else (rows // -split, cols)


def ring_window(ref, shape, split, n, piece, chunk):
    whole = shape[0] // n
    rows, cols = ring_cut(shape, split, n)
    if split > 0:
        return ref.at[pl.ds(chunk * whole, rows), pl.ds(piece * cols, cols)]
    return ref.at[pl.ds(chunk * whole + piece * rows, rows), :]


def ring_kernel(n, splits, fan, *refs):
    count = len(splits)
    more = 1 if fan else 0
    x_refs, y_refs = refs[:count], refs[count + more : 2 * count + more]
    slots = refs[2 * (count + more) : 3 * count + 2 * more]
    send_sem, recv_sem = refs[3 * count + 2 * more :]
    place, right, left = ring_greet(n, [])
    streams = [
        (k, piece, (piece if abs(splits[k]) > 1 else k) % 2) for k in range(count) for piece in range(abs(splits[k]))
    ]

    def window(ref, k, piece, chunk):
        return ring_window(ref, x_refs[k].shape, splits[k], n, piece, chunk)

    def chunk_at(down, step):
        return (place + 1 + step) % n if down else (place + 2 * n - 1 - step) % n

    copies = {}

    def start(number, step, src, dst, down):
        copies[number, step] = pltpu.make_async_remote_copy(
            src_ref=src,
            dst_ref=dst,
            send_sem=send_sem.at[number, step],
            recv_sem=recv_sem.at[number, step],
            device_id={"seq": left if down else right},
            device_id_type=MESH,
        )
        copies[number, step].start()

    def turn_block(number):
        inner_ref, turned_ref = refs[count], refs[2 * count + 1]
        rows = inner_ref.shape[0] // (2 * fan * n)
        half, first = number // (fan // 2), number % (fan // 2) * 2
        tall = jnp.concatenate(
            [
                inner_ref[pl.ds(((chunk * fan + group) * 2 + half) * rows, rows), :].astype(jnp.float32)
                for group in (first, first + 1)
                for chunk in range(n)
            ]
        )
        wide = 2 * n * rows
        turned_ref[:, number * wide : (number + 1) * wide] = jnp.transpose(tall, (1, 0)).astype(jnp.bfloat16)

    for number, (k, piece, down) in enumerate(streams):
        start(number, 0, window(x_refs[k], k, piece, place), window(slots[k], k, piece, 0), down)
    for step in range(n - 1):
        if step < fan:
            turn_block(step)
        for number, (k, piece, down) in enumerate(streams):
            copies[number, step].wait_recv()
            chunk = chunk_at(down, step)
            mine = window(x_refs[k], k, piece, chunk)
            landed = window(slots[k], k, piece, step)
            total = landed[...].astype(jnp.float32) + mine[...].astype(jnp.float32)
            if step < n - 2:
                landed[...] = total.astype(jnp.bfloat16)
                start(number, step + 1, landed, window(slots[k], k, piece, step + 1), down)
            else:
                done = window(y_refs[k], k, piece, chunk)
                done[...] = total.astype(jnp.bfloat16)
                start(number, n - 1, done, done, down)
    for step in range(n - 1):
        for number, (k, piece, down) in enumerate(streams):
            copies[number, n - 1 + step].wait_recv()
            if step < n - 2:
                done = window(y_refs[k], k, piece, chunk_at(down, n - 1 + step))
                start(number, n + step, done, done, down)
    for one in copies.values():
        one.wait_send()


def ring_call(body, name, arrays, outs, scratch, ident):
    size = sum(v.size * 2 for v in arrays)
    return pl.pallas_call(
        body,
        name=name,
        out_shape=[jax.ShapeDtypeStruct(s, d) for s, d in outs],
        in_specs=[pl.BlockSpec(memory_space=pltpu.VMEM)] * len(arrays),
        out_specs=[pl.BlockSpec(memory_space=pltpu.VMEM)] * len(outs),
        scratch_shapes=scratch,
        compiler_params=pltpu.CompilerParams(
            collective_id=ident, has_side_effects=True, vmem_limit_bytes=48 << 20
        ),
        cost_estimate=pl.CostEstimate(flops=0, bytes_accessed=60 * size, transcendentals=0),
    )(*arrays)


def ring_total(arrays, splits, ident, inner=None):
    n, fan = lax.axis_size("seq"), lax.axis_size("fsdp")
    streams = sum(abs(s) for s in splits)
    more = [] if inner is None else [inner]
    return ring_call(
        functools.partial(ring_kernel, n, splits, 0 if inner is None else fan),
        "ring_total",
        arrays + more,
        [(v.shape, jnp.bfloat16) for v in arrays] + [(v.shape[::-1], jnp.bfloat16) for v in more],
        [pltpu.VMEM((v.shape[0] // n * (n - 1), v.shape[1]), jnp.bfloat16) for v in arrays]
        + [pltpu.SemaphoreType.DMA((streams, 2 * n - 2))] * 2,
        ident,
    )


def units_kernel(
    n, fan, x_ref, part_ref, few_ref, inner_ref, outer_ref, sum_ref, few_sum_ref, slots, acc, landed, few_landed,
    down_send, down_recv, swap_send, swap_recv, own_sem, send_sem, recv_sem, part_send, part_recv,
):
    s, me = lax.axis_index("seq"), lax.axis_index("fsdp")
    rows, width = acc.shape[0] // 3, x_ref.shape[1]
    cols = width // fan
    block = 2 * fan * rows
    place, right, left = ring_greet(n, [(me + far) % fan for far in range(1, fan)])
    sums = {}

    def piece_of(ref, at, piece):
        return ref.at[pl.ds(at * 3 * rows, 3 * rows), pl.ds(piece * cols, cols)]

    def send_sum(piece, step, src):
        to = left if piece >= fan // 2 else right
        sums[piece, step] = pltpu.make_async_remote_copy(
            src_ref=src,
            dst_ref=piece_of(slots, step, piece),
            send_sem=down_send.at[piece, step],
            recv_sem=down_recv.at[piece, step],
            device_id={"seq": to},
            device_id_type=MESH,
        )
        sums[piece, step].start()

    def chunk(piece, step):
        return ring_index((place + 1 + step) % n if piece >= fan // 2 else (place + 2 * n - 1 - step) % n, n)

    for piece in range(fan):
        send_sum(piece, 0, piece_of(x_ref, chunk(piece, 0), piece))
    for step in range(n - 1):
        for piece in range(fan):
            sums[piece, step].wait_recv()
            arrived = piece_of(slots, step, piece)
            mine = piece_of(x_ref, chunk(piece, step + 1), piece)
            total = (arrived[...].astype(jnp.float32) + mine[...].astype(jnp.float32)).astype(jnp.bfloat16)
            if step < n - 2:
                arrived[...] = total
                send_sum(piece, step + 1, arrived)
            else:
                acc[:, piece * cols : (piece + 1) * cols] = total
    moves = []
    for far in range(fan):
        target = (me + far) % fan
        for half in range(2):
            src = acc.at[pl.ds(half * rows, rows), pl.ds(pl.multiple_of(target * cols, 128), cols)]
            dst = inner_ref.at[pl.ds(s * block + (me * 2 + half) * rows, rows), :]
            if far:
                one = pltpu.make_async_remote_copy(
                    src_ref=src,
                    dst_ref=dst,
                    send_sem=swap_send.at[far, half],
                    recv_sem=swap_recv.at[far, half],
                    device_id={"fsdp": target},
                    device_id_type=MESH,
                )
            else:
                one = pltpu.make_async_copy(src, dst, own_sem.at[half])
            one.start()
            moves.append(one)
    mine = pltpu.make_async_copy(
        acc.at[pl.ds(2 * rows, rows), :], outer_ref.at[pl.ds(s * rows, rows), :], own_sem.at[2]
    )
    mine.start()
    copies = {}
    outs = ((outer_ref, (n * rows, width), 2), (inner_ref, (n * block, cols), -2))

    def start(k, piece, step):
        ref, shape, split = outs[k]
        chunk = ring_index((place + step) % n if piece else (place + n - step) % n, n)
        view = ring_window(ref, shape, split, n, piece, chunk)
        copies[k, piece, step] = pltpu.make_async_remote_copy(
            src_ref=view,
            dst_ref=view,
            send_sem=send_sem.at[2 * k + piece, step],
            recv_sem=recv_sem.at[2 * k + piece, step],
            device_id={"seq": left if piece else right},
            device_id_type=MESH,
        )
        copies[k, piece, step].start()

    def forward(k, step):
        for piece in range(2):
            copies[k, piece, step].wait_recv()
            if step < n - 2:
                start(k, piece, step + 1)

    mine.wait()
    start(0, 0, 0)
    start(0, 1, 0)
    lead = (n - 1) // 2
    for step in range(lead):
        forward(0, step)
    for one in moves:
        one.wait()
    parts = []
    for far in range(1, fan):
        target = (me + far) % fan
        for which, (src, into) in enumerate(((part_ref, landed), (few_ref, few_landed))):
            rest = src.shape[0] // fan
            one = pltpu.make_async_remote_copy(
                src_ref=src.at[pl.ds(target * rest, rest), :],
                dst_ref=into.at[far],
                send_sem=part_send.at[which, far],
                recv_sem=part_recv.at[which, far],
                device_id={"fsdp": target},
                device_id_type=MESH,
            )
            one.start()
            parts.append(one)
    start(1, 0, 0)
    start(1, 1, 0)
    for step in range(n - 1):
        forward(1, step)
        if lead + step < n - 1:
            forward(0, lead + step)
    for one in parts:
        one.wait()
    for src, into, out in ((part_ref, landed, sum_ref), (few_ref, few_landed, few_sum_ref)):
        rest = src.shape[0] // fan
        total = src[pl.ds(pl.multiple_of(me * rest, rest), rest), :].astype(jnp.float32)
        for far in range(1, fan):
            total = total + into[far].astype(jnp.float32)
        out[...] = total
    for one in [*copies.values(), *sums.values()]:
        one.wait_send()


def units_total(grads, part, few, ident):
    n, fan = lax.axis_size("seq"), lax.axis_size("fsdp")
    rows, width = grads.shape[0] // (3 * n), grads.shape[1]
    tokens = part.shape[0] // fan
    sems = lambda *shape: pltpu.SemaphoreType.DMA(shape)
    return ring_call(
        functools.partial(units_kernel, n, fan),
        "units_total",
        [grads, part, few],
        [
            ((n * 2 * fan * rows, width // fan), jnp.bfloat16),
            ((n * rows, width), jnp.bfloat16),
            ((tokens, part.shape[1]), jnp.float32),
            ((few.shape[0] // fan, few.shape[1]), jnp.float32),
        ],
        [
            pltpu.VMEM(((n - 1) * 3 * rows, width), jnp.bfloat16),
            pltpu.VMEM((3 * rows, width), jnp.bfloat16),
            pltpu.VMEM((fan, tokens, part.shape[1]), jnp.bfloat16),
            pltpu.VMEM((fan, few.shape[0] // fan, few.shape[1]), jnp.bfloat16),
        ]
        + [sems(fan, n - 1), sems(fan, n - 1), sems(fan, 2), sems(fan, 2), sems(3)]
        + [sems(4, n - 1), sems(4, n - 1), sems(2, fan), sems(2, fan)],
        ident,
    )


def team(n):
    s, f = lax.axis_index("seq"), lax.axis_index("fsdp")
    half = s // (n // 2)
    away = (half + f) % 2
    return f // 2, half, (s + away * (n // 2)) % n


def swap_kernel(n, fan, count, fars, fresh, *refs):
    given = count + (len(fars) > 0) + (0 if fresh else 2)
    x_refs, y_refs = refs[:count], refs[given : given + count]
    sems = refs[given + count + (2 if fars else 0) :]
    send_sem, recv_sem, own_sem = sems[:3]
    pair, half, rank = team(n)
    me = lax.axis_index("fsdp")

    def device(other):
        away = (other // (n // 2) + half) % 2
        return {"seq": (other + away * (n // 2)) % n, "fsdp": 2 * pair + (half + away) % 2}

    barrier = pltpu.get_barrier_semaphore()
    for j in range(1, n):
        pl.semaphore_signal(barrier, inc=1, device_id=device((rank + j) % n), device_id_type=MESH)
    travel = [far for far in fars if far]
    for far in travel:
        pl.semaphore_signal(barrier, inc=1, device_id={"fsdp": (me + fan - far) % fan}, device_id_type=MESH)
    pl.semaphore_wait(barrier, n - 1 + len(travel))
    copies = []
    for k in range(count):
        for j in range(1, n):
            other = (rank + j) % n
            one = pltpu.make_async_remote_copy(
                src_ref=x_refs[k].at[other],
                dst_ref=y_refs[k].at[rank],
                send_sem=send_sem.at[k, j],
                recv_sem=recv_sem.at[k, j],
                device_id=device(other),
                device_id_type=MESH,
            )
            one.start()
            copies.append(one)
    for k in range(count):
        one = pltpu.make_async_copy(x_refs[k].at[rank], y_refs[k].at[rank], own_sem.at[k])
        one.start()
        copies.append(one)
    if fars:
        w_ref, halves = refs[count], refs[given + count : given + count + 2]
        far_send, far_recv, far_own, stage = sems[3:]
        rest = []
        units, cols = halves[0].shape[0], w_ref.shape[1]
        for i, far in enumerate(fars):
            target = (me + far) % fan
            for part in range(2):
                src = w_ref.at[pl.ds((part * fan + target) * units, units), :]
                dst = halves[part].at[:, pl.ds(pl.multiple_of(me * cols, 128), cols)]
                if far:
                    one = pltpu.make_async_remote_copy(
                        src_ref=src,
                        dst_ref=dst,
                        send_sem=far_send.at[i, part],
                        recv_sem=far_recv.at[i, part],
                        device_id={"fsdp": target},
                        device_id_type=MESH,
                    )
                else:
                    one = pltpu.make_async_copy(src, stage.at[part], far_own.at[0, part])
                    rest.append((one, pltpu.make_async_copy(stage.at[part], dst, far_own.at[1, part])))
                one.start()
                if far:
                    copies.append(one)
        for inward, outward in rest:
            inward.wait()
            outward.start()
            copies.append(outward)
    for one in copies:
        one.wait()


def swap(arrays, ident, fars=(), given=None, halves=None):
    n, fan = lax.axis_size("seq"), lax.axis_size("fsdp")
    count = len(arrays)
    size = sum(v.size * 2 for v in arrays)
    operands, outs, alias = list(arrays), [jax.ShapeDtypeStruct(v.shape, v.dtype) for v in arrays], {}
    scratch = [
        pltpu.SemaphoreType.DMA((count, n)),
        pltpu.SemaphoreType.DMA((count, n)),
        pltpu.SemaphoreType.DMA((count,)),
    ]
    if fars:
        operands.append(given)
        shape = (given.shape[0] // (2 * fan), given.shape[1] * fan)
        outs += [jax.ShapeDtypeStruct(shape, given.dtype)] * 2
        scratch += [pltpu.SemaphoreType.DMA((len(fars), 2))] * 2 + [
            pltpu.SemaphoreType.DMA((2, 2)),
            pltpu.VMEM((2, given.shape[0] // (2 * fan), given.shape[1]), given.dtype),
        ]
        if halves is not None:
            operands += list(halves)
            alias = {count + 1: count, count + 2: count + 1}
    return pl.pallas_call(
        functools.partial(swap_kernel, n, fan, count, fars, not fars or halves is None),
        name="swap",
        out_shape=outs,
        in_specs=[pl.BlockSpec(memory_space=pl.ANY)] * len(operands),
        out_specs=[pl.BlockSpec(memory_space=pl.ANY)] * len(outs),
        scratch_shapes=scratch,
        input_output_aliases=alias,
        compiler_params=pltpu.CompilerParams(collective_id=ident, has_side_effects=True),
        cost_estimate=pl.CostEstimate(flops=0, bytes_accessed=size, transcendentals=0),
    )(*operands)


def norm_apply(value, gain):
    return value * lax.rsqrt(jnp.mean(value * value, axis=-1, keepdims=True) + EPS) * gain


def norm_back(value, gain, grad):
    _, pull = jax.vjp(norm_apply, value, gain)
    return pull(grad)


def gate_mix(gate, up):
    return jax.nn.gelu(gate, approximate=True) * up


def counts_below(ids, values):
    total = jnp.zeros_like(values)
    for doc in range(DOCS):
        total = total + jnp.where(values > doc, jnp.sum((ids == doc).astype(jnp.int32)), 0)
    return total


def change_home(value):
    n, fan = lax.axis_size("seq"), lax.axis_size("fsdp")
    pairs = []
    for s in range(n):
        for f in range(fan):
            away = (s // (n // 2) + f) % 2
            target = ((s + n // 2) % n, f ^ 1) if away else (s, f)
            pairs.append((s * fan + f, target[0] * fan + target[1]))
    return lax.ppermute(value, ("seq", "fsdp"), pairs)


def spread(blocks):
    fan, me = lax.axis_size("fsdp"), lax.axis_index("fsdp")
    result = blocks
    for far in range(1, fan):
        block = lax.dynamic_index_in_dim(blocks, (me + far) % fan, 0, True)
        block = lax.ppermute(block, "fsdp", [(f, (f + far) % fan) for f in range(fan)])
        result = lax.dynamic_update_slice_in_dim(result, block, (me - far) % fan, 0)
    return result


def flat(blocks):
    return jnp.transpose(blocks, (1, 0, 2)).reshape(blocks.shape[1], -1)


def by_rows(value):
    return with_layout_constraint(value, Layout(major_to_minor=tuple(range(value.ndim))))


def scatter(grad):
    return lax.psum_scatter(grad, "fsdp", scatter_dimension=0, tiled=True)


def shards(
    layer_in, encoder, decoder_ids, encoder_ids, rel_buckets,
    norm_self, self_qkv, self_out, rel_table, norm_cross, cross_q, cross_kv, cross_out, norm_ff, ff_in, ff_out,
    cotangent,
):
    seqs, local, width = layer_in.shape
    enc_local = encoder.shape[1]
    parts = lax.axis_size("seq")
    heads = self_qkv.shape[1]
    dh = self_qkv.shape[2] // 3
    own = heads // parts
    rows = seqs * local
    buckets, table_own = rel_table.shape
    length, keys = local * parts, enc_local * parts
    gather = lambda v: lax.all_gather(v, "fsdp", axis=0, tiled=True)

    fan = lax.axis_size("fsdp")
    units = ff_in.shape[1] // (2 * fan)
    part = norm_self.shape[0]
    pair, half, rank = team(parts)

    qkv_w = gather(self_qkv)
    small = jnp.concatenate([norm_self, norm_cross, norm_ff, rel_table.reshape(-1)])
    small = lax.all_gather(small, "fsdp", axis=0, tiled=False)
    early = by_rows(jnp.stack([self_out, cross_q, *jnp.split(cross_kv.reshape(-1, 2 * width), 2, axis=1)]))
    small, early = lax.optimization_barrier((small, early))
    early = lax.all_gather(early, "fsdp", axis=1, tiled=True)
    both_ids = jnp.concatenate([decoder_ids.reshape(-1), encoder_ids.reshape(-1)])
    both_ids = change_home(jnp.pad(both_ids, (0, 1024 - local - enc_local)).reshape(8, 128))
    inner_t = ff_in.T
    by_kernel = (width // fan) % 128 == 0 and fan % 2 == 0 and (ff_in.shape[0] // parts) % 8 == 0
    (both_ids,) = swap([jnp.broadcast_to(both_ids[None], (parts, 8, 128))], 13)
    home = change_home(layer_in.reshape(rows, width))
    early = by_rows(early)
    gain_first, gain_second, gain_third = (
        small[:, i * part : (i + 1) * part].reshape(width).astype(f32) for i in range(3)
    )
    table = jnp.transpose(small[:, 3 * part :].reshape(-1, buckets, table_own), (1, 0, 2)).reshape(buckets, heads)
    both_ids = both_ids.reshape(parts, 1024)
    ids = both_ids[:, :local].reshape(length)
    enc_ids = both_ids[:, local : local + enc_local].reshape(keys)

    first_seen = counts_below(ids, ids)
    enc_first = counts_below(enc_ids, ids)
    enc_last = counts_below(enc_ids, ids + 1)
    blocks = length // BQ
    bk = BQ
    self_rows = jnp.broadcast_to(first_seen[None], (8, length))
    cross_rows = jnp.concatenate([enc_first[None], enc_last[None], jnp.zeros((6, length), jnp.int32)])
    self_limits = jnp.stack(
        [first_seen[::BQ] // bk, (jnp.arange(blocks, dtype=jnp.int32) + 1) * (BQ // bk)]
    )
    cross_limits = jnp.stack([enc_first[::BQ] // bk, (enc_last[BQ - 1 :: BQ] + bk - 1) // bk])

    first_head = rank * own
    table_mine = lax.dynamic_slice_in_dim(table.astype(f32), first_head, own, 1)
    near = rel_buckets[:REACH]
    onehot = (near[:, None] == jnp.arange(buckets, dtype=jnp.int32)[None, :]).astype(f32)
    bias = jnp.einsum("ln,ng->gl", onehot, table_mine, precision=HIGH)
    ext = jnp.concatenate(
        [jnp.full((own, BQ), MASKED, f32), bias, jnp.zeros((own, BQ), f32)], axis=1
    )

    qkv_w, home, inner_t, ext, self_rows, cross_rows, self_limits, cross_limits = lax.optimization_barrier(
        (qkv_w, home, inner_t, ext, self_rows, cross_rows, self_limits, cross_limits)
    )
    qkv_w = qkv_w.reshape(width, parts, own * 3 * dh)

    stream = home.astype(f32)
    normed_first = norm_apply(stream, gain_first).astype(bf16)
    qkv_tok = jnp.einsum("td,dge->gte", normed_first, qkv_w, preferred_element_type=f32).astype(bf16)
    others = change_home(jnp.concatenate([cotangent.reshape(rows, width), encoder.reshape(-1, width)]))
    grad_low, enc_flat = others[:rows], others[rows:]
    fars = [tuple(far for far in range(fan) if by_kernel and (far == 2) == first) for first in (True, False)]
    qkv, *halves = swap([qkv_tok], 17, fars[0], inner_t)
    qkv, cross_out, grad_low = lax.optimization_barrier((qkv, cross_out, grad_low))
    if rows == cross_out.shape[0]:
        mix_cross, grad_group = lax.all_gather(jnp.stack([cross_out, grad_low]), "fsdp", axis=1, tiled=True)
    else:
        mix_cross, grad_group = gather(cross_out), gather(grad_low)
    mix_cross = mix_cross.reshape(parts, own * dh, width)
    qkv = qkv.reshape(length, own * 3 * dh)
    out_self, self_t, self_lse = self_forward(self_limits, self_rows, ext, qkv)
    (self_tok,) = swap([out_self.reshape(parts, local, own * dh)], 11)
    after_self, normed_second, query_tok, pairs_tok = over_weights(
        into_kernel,
        "self_out_to_cross",
        [self_tok, home, gain_second.reshape(1, width), enc_flat],
        early,
        lambda i: i,
        [
            ((rows, width), f32),
            ((rows, width), bf16),
            ((parts, rows, own * dh), bf16),
            ((parts, enc_local, own * 2 * dh), bf16),
        ],
    )
    query_cross, pairs = swap([query_tok, pairs_tok], 12)
    query_cross, pairs = query_cross.reshape(length, own * dh), pairs.reshape(keys, own * 2 * dh)
    out_cross, cross_t, cross_lse = cross_forward(cross_limits, cross_rows, query_cross, pairs)
    cross_tok, *halves = swap([out_cross.reshape(parts, local, own * dh)], 16, fars[1], inner_t, halves)
    if not by_kernel:
        halves = spread(jnp.transpose(inner_t.reshape(2, fan, units, -1), (1, 0, 2, 3)))
        halves = [jnp.transpose(halves[:, i], (1, 0, 2)).reshape(units, width) for i in range(2)]
    gate_t, up_t = halves
    after_cross = after_self + jnp.einsum("gtc,gcd->td", cross_tok, mix_cross, preferred_element_type=f32)
    normed_third = norm_apply(after_cross, gain_third).astype(bf16)
    normed_group = gather(normed_third)
    gate = jnp.einsum("td,fd->tf", normed_group, gate_t, preferred_element_type=f32)
    up = jnp.einsum("td,fd->tf", normed_group, up_t, preferred_element_type=f32)
    hidden = gate_mix(gate, up).astype(bf16)

    grad_hidden = jnp.einsum("td,fd->tf", grad_group, ff_out, preferred_element_type=f32)
    _, pull_mix = jax.vjp(gate_mix, gate, up)
    grad_gate, grad_up = (g.astype(bf16) for g in pull_mix(grad_hidden))
    grad_third_in = jnp.dot(grad_gate, gate_t, preferred_element_type=f32) + jnp.dot(
        grad_up, up_t, preferred_element_type=f32
    )
    grad_third_in = scatter(grad_third_in.astype(bf16))
    outer_part = jnp.dot(hidden, ff_out, preferred_element_type=f32).astype(bf16)
    grad_units = [
        jnp.einsum("tf,td->fd", g, y, preferred_element_type=f32).astype(bf16)
        for g, y in ((grad_gate, normed_group), (grad_up, normed_group), (hidden, grad_group))
    ]
    if by_kernel:
        grad_units = jnp.stack([g.reshape(parts, units // parts, width) for g in grad_units], axis=1)
        grad_units = grad_units.reshape(3 * units, width)
    grad_third_in, outer_part, part_units = lax.optimization_barrier((grad_third_in, outer_part, grad_units))
    grad_third_in = grad_third_in.astype(f32)
    grad_from_third, grad_gain_third = norm_back(after_cross, gain_third, grad_third_in)
    grad_middle = grad_low.astype(f32) + grad_from_third
    middle_low = grad_middle.astype(bf16)
    grad_mix_cross = jnp.einsum("gtc,td->gcd", cross_tok, middle_low, preferred_element_type=f32)
    part_cross = scatter(grad_mix_cross.reshape(width, width).astype(bf16))
    grad_cross_tok = jnp.einsum("td,gcd->gtc", middle_low, mix_cross, preferred_element_type=f32).astype(bf16)
    (grad_cross,) = swap([grad_cross_tok], 11)
    grad_cross = grad_cross.reshape(length, own * dh)
    grad_query, grad_pairs = cross_backward(
        cross_limits, cross_rows, query_cross, pairs, grad_cross, cross_t, cross_lse
    )
    grad_query_tok, grad_pairs_tok = swap(
        [grad_query.reshape(parts, local, own * dh), grad_pairs.reshape(parts, enc_local, own * 2 * dh)], 12
    )
    (
        grad_upper, upper_low, grad_self_tok, grad_gain_second, grad_encoder, grad_query_tok, grad_pairs_tok
    ) = over_weights(
        outof_kernel,
        "cross_to_self_out",
        [grad_query_tok, grad_pairs_tok, after_self, gain_second.reshape(1, width), grad_middle],
        early,
        lambda i: jnp.where(i < 2, 1 - i, i),
        [
            ((rows, width), f32),
            ((rows, width), bf16),
            ((parts, rows, own * dh), bf16),
            ((1, width), f32),
            ((enc_local, width), bf16),
            ((rows, width), bf16),
            ((enc_local, 2 * width), bf16),
        ],
        [((enc_local, width), f32)],
    )
    grad_query_w = jnp.einsum("td,te->de", normed_second, grad_query_tok, preferred_element_type=f32)
    grad_pairs_w = jnp.einsum("td,te->de", enc_flat, grad_pairs_tok, preferred_element_type=f32)
    grad_mix_self = jnp.einsum("gtc,td->gcd", self_tok, upper_low, preferred_element_type=f32)
    grad_mid = jnp.concatenate(
        [
            grad_query_w.astype(bf16),
            grad_pairs_w.astype(bf16),
            grad_mix_self.reshape(width, width).astype(bf16),
        ],
        axis=1,
    )
    grad_self_tok, grad_mid = lax.optimization_barrier((grad_self_tok, grad_mid))
    part_mid = scatter(grad_mid)
    (grad_self,) = swap([grad_self_tok], 11)
    grad_self = grad_self.reshape(length, own * dh)
    grad_qkv, diagonals = self_backward(self_limits, self_rows, ext, qkv, grad_self, self_t, self_lse)
    (grad_qkv_tok,) = swap([grad_qkv.reshape(parts, local, own * 3 * dh)], 10)
    grad_qkv_tok = flat(grad_qkv_tok)
    grad_qkv_w = jnp.einsum("td,te->de", normed_first, grad_qkv_tok, preferred_element_type=f32)
    grad_qkv_w, grad_qkv_tok = lax.optimization_barrier((grad_qkv_w.astype(bf16), grad_qkv_tok))
    grad_first_in = jnp.einsum("te,de->td", grad_qkv_tok, qkv_w.reshape(width, -1), preferred_element_type=f32)
    grad_from_first, grad_gain_first = norm_back(stream, gain_first, grad_first_in)
    grad_layer_in = (grad_upper + grad_from_first).astype(bf16)
    bucket_line = jnp.concatenate([jnp.full((BQ - 1,), -1, jnp.int32), near, jnp.full((BQ + 1,), -1, jnp.int32)])
    in_bucket = (bucket_line[:, None] == jnp.arange(buckets, dtype=jnp.int32)).astype(f32)
    by_bucket = jnp.einsum("xn,gx->ng", in_bucket, diagonals, precision=HIGH)
    grad_table = lax.dynamic_update_slice_in_dim(jnp.zeros((buckets, heads), f32), by_bucket, first_head, 1)

    gains = jnp.concatenate(
        [g.reshape(-1, part) for g in (grad_gain_first, grad_gain_second, grad_gain_third)], axis=1
    )
    tables = jnp.transpose(grad_table.reshape(buckets, -1, table_own), (1, 0, 2)).reshape(-1, buckets * table_own)
    small_grads = jnp.concatenate([gains, tables], axis=1).astype(bf16)
    small_size = small_grads.shape[1]
    going_home = jnp.concatenate([grad_layer_in, grad_encoder.astype(bf16)])
    part_last = scatter(grad_qkv_w)
    going_home, small_grads, part_units, part_cross, part_mid = lax.optimization_barrier(
        (change_home(going_home), small_grads, part_units, part_cross, part_mid)
    )
    if by_kernel:
        few = jnp.pad(small_grads[:, None], ((0, 0), (0, 7), (0, 1024 - small_size))).reshape(fan * 8, 1024)
        total_inner, total_outer, outer_sum, few = units_total(part_units, outer_part, few, 0)
        few = jnp.pad(few[0].astype(bf16).reshape(8, 128), ((0, parts * 8 - 8), (0, 0)))
        total_cross, total_mid, total_qkv, small_total, total_inner = ring_total(
            [part_cross, part_mid, part_last, few], (2, 2, 2, 1), 1, total_inner
        )
    else:
        grad_units = [lax.psum(g, "seq") for g in part_units]
        total_inner = spread(jnp.transpose(jnp.stack(grad_units[:2]).reshape(2, units, fan, -1), (2, 0, 1, 3)))
        total_inner = jnp.transpose(total_inner, (3, 1, 0, 2)).reshape(-1, 2 * fan * units).astype(f32)
        total_outer, outer_sum = grad_units[2], scatter(outer_part).astype(f32)
        few = lax.dynamic_index_in_dim(lax.psum(small_grads, "fsdp"), lax.axis_index("fsdp"), 0, False)
        total_cross, total_mid, total_qkv, small_total = (
            lax.psum(v, "seq") for v in (part_cross, part_mid, part_last, few)
        )
    layer_out = (after_cross + outer_sum).astype(bf16)
    layer_out, total_inner, total_outer, total_cross, total_mid, total_qkv, going_home = lax.optimization_barrier(
        (layer_out, total_inner, total_outer, total_cross, total_mid, total_qkv, going_home)
    )
    layer_out = change_home(layer_out).reshape(seqs, local, width)
    grad_layer_in = going_home[:rows].astype(f32).reshape(seqs, local, width)
    grad_encoder = going_home[rows:].astype(f32).reshape(seqs, enc_local, width)
    total_inner, total_outer, total_mid, total_qkv = (
        v.astype(f32) for v in (total_inner, total_outer, total_mid, total_qkv)
    )
    total_query, total_mix_cross = total_mid[:, :width], total_cross.astype(f32)
    total_pairs = total_mid[:, width : 3 * width].reshape(-1, heads, 2 * dh)
    total_mix_self, total_qkv = total_mid[:, 3 * width :], total_qkv.reshape(-1, heads, 3 * dh)
    mine = small_total.reshape(-1)[:small_size].astype(f32)
    total_gain_first, total_gain_second, total_gain_third = (mine[i * part : (i + 1) * part] for i in range(3))
    total_table = mine[3 * part :].reshape(buckets, table_own)
    return (
        layer_out, grad_layer_in, grad_encoder, total_gain_first, total_qkv, total_mix_self, total_table,
        total_gain_second, total_query, total_pairs, total_mix_cross, total_gain_third, total_inner, total_outer,
    )


def solution(mesh):
    in_specs = (
        P("fsdp", "seq", None), P("fsdp", "seq", None), P("fsdp", "seq"), P("fsdp", "seq"), P(),
        P("fsdp"), P("fsdp", None, None), P("fsdp", None), P(None, "fsdp"), P("fsdp"), P("fsdp", None),
        P("fsdp", None, None), P("fsdp", None), P("fsdp"), P("fsdp", None), P("fsdp", None),
        P("fsdp", "seq", None),
    )
    out_specs = (
        P("fsdp", "seq", None), P("fsdp", "seq", None), P("fsdp", "seq", None), P("fsdp"), P("fsdp", None, None),
        P("fsdp", None), P(None, "fsdp"), P("fsdp"), P("fsdp", None), P("fsdp", None, None), P("fsdp", None),
        P("fsdp"), P("fsdp", None), P("fsdp", None),
    )
    return jax.shard_map(shards, mesh=mesh, in_specs=in_specs, out_specs=out_specs, check_vma=False)
```

```python
import functools

import jax
import jax.numpy as jnp
from jax import lax
from jax.experimental import pallas as pl
from jax.experimental.layout import Layout, with_layout_constraint
from jax.experimental.pallas import tpu as pltpu
from jax.sharding import PartitionSpec as P

EPS = 1e-06
HIGH = lax.Precision.HIGHEST
MASKED = -1e30
DOCS = 4

BQ = 256
REACH = 1024


def blk(index, size):
    return pl.ds(pl.multiple_of(index * size, size), size)


def turn(value):
    return jnp.transpose(value.astype(jnp.float32), (1, 0))


def bias_tiles(ext_ref, tile_ref, own):
    for h in range(own):
        line = jnp.broadcast_to(ext_ref[h : h + 1, :], tile_ref.shape[1:])
        tile_ref[h] = pltpu.roll(line, 0, 1, stride=1, stride_axis=0)


def unpack(ref, own, width, picks, flips, base):
    block = 256

    def one(b, _):
        rows = blk(b, block)
        value = ref[rows, :]
        if flips:
            flat = turn(value).astype(jnp.bfloat16)
            for target, piece in flips:
                for h in range(own):
                    at = h * width + piece * 64
                    target[base + h, :, rows] = flat[at : at + 64]
        for target, piece in picks:
            for h in range(own):
                at = h * width + piece * 64
                target[base + h, rows, :] = value[:, at : at + 64]
        return 0

    lax.fori_loop(0, ref.shape[0] // block, one, 0)


def dot(a, b):
    return jnp.dot(a, b, preferred_element_type=jnp.float32)


def score(own_index, key_tile, query_t, tile_ref, t, low, high, first_key):
    value = dot(key_tile, query_t)
    place = lax.broadcasted_iota(jnp.int32, value.shape, 0)
    keep = place >= low - first_key
    if high is not None:
        keep = keep & (place < high - first_key)
    else:
        value = value + tile_ref[own_index, :, blk(t + 1, BQ)]
    return jnp.where(keep, value, MASKED)


def forward_body(own, bk, causal, lim_ref, rows_ref, q_t, k_rows, v_t, tile_ref, o_ref, ot_ref, lse_ref):
    length = o_ref.shape[0]

    def q_block(i, _):
        cols = blk(i, BQ)
        queries = [q_t[h, :, cols] for h in range(own)]
        low = rows_ref[0:1, cols]
        high = None if causal else rows_ref[1:2, cols]

        def k_block(j, carry):
            keys = blk(j, bk)
            t = i - j
            out = []
            for h in range(own):
                top, total, acc = carry[h]
                s = score(h, k_rows[h, keys, :], queries[h], tile_ref, t, low, high, j * bk)
                new_top = jnp.maximum(top, jnp.max(s, axis=0, keepdims=True))
                p = jnp.exp(s - new_top)
                scale = jnp.exp(top - new_top)
                total = total * scale + jnp.sum(p, axis=0, keepdims=True)
                acc = acc * scale + dot(v_t[h, :, keys], p.astype(jnp.bfloat16))
                out.append((new_top, total, acc))
            return tuple(out)

        start = tuple(
            (
                jnp.full((1, BQ), MASKED, jnp.float32),
                jnp.zeros((1, BQ), jnp.float32),
                jnp.zeros((64, BQ), jnp.float32),
            )
            for _ in range(own)
        )
        ends = lax.fori_loop(lim_ref[0, i], lim_ref[1, i], k_block, start)
        for h in range(own):
            top, total, acc = ends[h]
            ot_ref[h * 64 : h * 64 + 64, cols] = acc / total
            lse_ref[h : h + 1, cols] = top + jnp.log(total)
        o_ref[cols, :] = turn(ot_ref[:, cols]).astype(jnp.bfloat16)
        return 0

    lax.fori_loop(0, length // BQ, q_block, 0)


def self_forward_kernel(own, bk, lim_ref, rows_ref, ext_ref, x_ref, o_ref, ot_ref, lse_ref, q_t, k_rows, v_t, tile_ref):
    bias_tiles(ext_ref, tile_ref, own)
    unpack(x_ref, own, 192, [(k_rows, 1)], [(q_t, 0), (v_t, 2)], 0)
    forward_body(own, bk, True, lim_ref, rows_ref, q_t, k_rows, v_t, tile_ref, o_ref, ot_ref, lse_ref)


def cross_forward_kernel(own, bk, lim_ref, rows_ref, q_ref, kv_ref, o_ref, ot_ref, lse_ref, q_t, k_rows, v_t):
    unpack(q_ref, own, 64, [], [(q_t, 0)], 0)
    unpack(kv_ref, own, 128, [(k_rows, 0)], [(v_t, 1)], 0)
    forward_body(own, bk, False, lim_ref, rows_ref, q_t, k_rows, v_t, None, o_ref, ot_ref, lse_ref)


def backward_body(
    own, bk, causal, lim_ref, rows_ref, do_ref, ot_ref, lse_ref,
    q_t, q_rows, k_t, k_rows, v_rows, do_t, do_rows, tile_ref, sum_ref, dq_t, dk, dv,
):
    length = do_ref.shape[0]
    dk[...] = jnp.zeros_like(dk)
    dv[...] = jnp.zeros_like(dv)
    if causal:
        sum_ref[...] = jnp.zeros_like(sum_ref)

    def q_block(i, _):
        cols = blk(i, BQ)
        low = rows_ref[0:1, cols]
        high = None if causal else rows_ref[1:2, cols]
        per_head = []
        for h in range(own):
            grad_t = do_t[h, :, cols]
            delta = jnp.sum(
                grad_t.astype(jnp.float32) * ot_ref[h * 64 : h * 64 + 64, cols], axis=0, keepdims=True
            )
            per_head.append((q_t[h, :, cols], grad_t, delta, lse_ref[h : h + 1, cols]))

        def k_block(j, carry):
            keys = blk(j, bk)
            t = i - j
            out = []
            for h in range(own):
                query_t, grad_t, delta, lse = per_head[h]
                s = score(h, k_rows[h, keys, :], query_t, tile_ref, t, low, high, j * bk)
                p = jnp.exp(s - lse)
                dp = dot(v_rows[h, keys, :], grad_t)
                ds = (p * (dp - delta)).astype(jnp.bfloat16)
                dv[h, keys, :] += dot(p.astype(jnp.bfloat16), do_rows[h, cols, :])
                dk[h, keys, :] += dot(ds, q_rows[h, cols, :])
                if causal:
                    sum_ref[h, :, blk(t, BQ)] += ds.astype(jnp.float32)
                out.append(carry[h] + dot(k_t[h, :, keys], ds))
            return tuple(out)

        ends = lax.fori_loop(
            lim_ref[0, i],
            lim_ref[1, i],
            k_block,
            tuple(jnp.zeros((64, BQ), jnp.float32) for _ in range(own)),
        )
        for h in range(own):
            dq_t[h * 64 : h * 64 + 64, cols] = ends[h]
        return 0

    lax.fori_loop(0, length // BQ, q_block, 0)


def diagonal_sums(sum_ref, u_ref, own):
    flip = lax.broadcasted_iota(jnp.int32, (BQ, BQ), 0) + lax.broadcasted_iota(jnp.int32, (BQ, BQ), 1) == BQ - 1
    flip = jnp.where(flip, 1.0, 0.0).astype(jnp.bfloat16)
    for h in range(own):
        grid = sum_ref[h]
        high = grid.astype(jnp.bfloat16)
        low = (grid - high.astype(jnp.float32)).astype(jnp.bfloat16)
        upside = dot(flip, high) + dot(flip, low)
        wide = jnp.concatenate([upside, jnp.zeros((BQ, BQ), jnp.float32)], axis=1)
        aligned = pltpu.roll(wide, 0, 1, stride=1, stride_axis=0)
        u_ref[h : h + 1, :] = jnp.sum(aligned, axis=0, keepdims=True)


def self_backward_kernel(
    own, bk, lim_ref, rows_ref, ext_ref, x_ref, do_ref, ot_ref, lse_ref, dx_ref, u_ref,
    q_t, q_rows, k_t, k_rows, v_rows, do_t, do_rows, tile_ref, sum_ref, dq_t, dk, dv,
):
    bias_tiles(ext_ref, tile_ref, own)
    unpack(x_ref, own, 192, [(q_rows, 0), (k_rows, 1), (v_rows, 2)], [(q_t, 0), (k_t, 1)], 0)
    unpack(do_ref, own, 64, [(do_rows, 0)], [(do_t, 0)], 0)
    backward_body(
        own, bk, True, lim_ref, rows_ref, do_ref, ot_ref, lse_ref,
        q_t, q_rows, k_t, k_rows, v_rows, do_t, do_rows, tile_ref, sum_ref, dq_t, dk, dv,
    )
    diagonal_sums(sum_ref, u_ref, own)

    def pack(b, _):
        rows = blk(b, 256)
        dq = turn(dq_t[:, rows])
        pieces = []
        for h in range(own):
            pieces += [dq[:, h * 64 : h * 64 + 64], dk[h, rows, :], dv[h, rows, :]]
        dx_ref[rows, :] = jnp.concatenate(pieces, axis=1).astype(jnp.bfloat16)
        return 0

    lax.fori_loop(0, x_ref.shape[0] // 256, pack, 0)


def cross_backward_kernel(
    own, bk, lim_ref, rows_ref, q_ref, kv_ref, do_ref, ot_ref, lse_ref, dq_ref, dkv_ref,
    q_t, q_rows, k_t, k_rows, v_rows, do_t, do_rows, dq_t, dk, dv,
):
    unpack(q_ref, own, 64, [(q_rows, 0)], [(q_t, 0)], 0)
    unpack(kv_ref, own, 128, [(k_rows, 0), (v_rows, 1)], [(k_t, 0)], 0)
    unpack(do_ref, own, 64, [(do_rows, 0)], [(do_t, 0)], 0)
    backward_body(
        own, bk, False, lim_ref, rows_ref, do_ref, ot_ref, lse_ref,
        q_t, q_rows, k_t, k_rows, v_rows, do_t, do_rows, None, None, dq_t, dk, dv,
    )

    def pack_q(b, _):
        rows = blk(b, 256)
        dq_ref[rows, :] = turn(dq_t[:, rows]).astype(jnp.bfloat16)
        return 0

    def pack_kv(b, _):
        rows = blk(b, 256)
        pieces = []
        for h in range(own):
            pieces += [dk[h, rows, :], dv[h, rows, :]]
        dkv_ref[rows, :] = jnp.concatenate(pieces, axis=1).astype(jnp.bfloat16)
        return 0

    lax.fori_loop(0, q_ref.shape[0] // 256, pack_q, 0)
    lax.fori_loop(0, kv_ref.shape[0] // 256, pack_kv, 0)


SMEM = pl.BlockSpec(memory_space=pltpu.SMEM)
VMEM = pl.BlockSpec(memory_space=pltpu.VMEM)
bf16, f32 = jnp.bfloat16, jnp.float32


def call(body, name, operands, outs, scratch, flops):
    size = sum(v.size * v.dtype.itemsize for v in operands)
    return pl.pallas_call(
        body,
        name=name,
        out_shape=[jax.ShapeDtypeStruct(s, d) for s, d in outs],
        in_specs=[SMEM] + [VMEM] * (len(operands) - 1),
        out_specs=[VMEM] * len(outs),
        scratch_shapes=[pltpu.VMEM(s, d) for s, d in scratch],
        compiler_params=pltpu.CompilerParams(vmem_limit_bytes=62 << 20),
        cost_estimate=pl.CostEstimate(flops=0, bytes_accessed=size, transcendentals=0),
    )(*operands)


def self_forward(limits, rows, ext, x, bk=BQ):
    length, own = x.shape[0], x.shape[1] // 192
    return call(
        functools.partial(self_forward_kernel, own, bk),
        "self_forward",
        [limits, rows, ext, x],
        [((length, own * 64), bf16), ((own * 64, length), f32), ((own, length), f32)],
        [
            ((own, 64, length), bf16),
            ((own, length, 64), bf16),
            ((own, 64, length), bf16),
            ((own, BQ, REACH + 2 * BQ), f32),
        ],
        length * length * own * 64,
    )


def cross_forward(limits, rows, q, kv, bk=BQ):
    length, own, keys = q.shape[0], q.shape[1] // 64, kv.shape[0]
    return call(
        functools.partial(cross_forward_kernel, own, bk),
        "cross_forward",
        [limits, rows, q, kv],
        [((length, own * 64), bf16), ((own * 64, length), f32), ((own, length), f32)],
        [((own, 64, length), bf16), ((own, keys, 64), bf16), ((own, 64, keys), bf16)],
        length * keys * own * 128,
    )


def self_backward(limits, rows, ext, x, grad, o_t, lse, bk=BQ):
    length, own = x.shape[0], x.shape[1] // 192
    return call(
        functools.partial(self_backward_kernel, own, bk),
        "self_backward",
        [limits, rows, ext, x, grad, o_t, lse],
        [((length, own * 192), bf16), ((own, REACH + 2 * BQ), f32)],
        [
            ((own, 64, length), bf16),
            ((own, length, 64), bf16),
            ((own, 64, length), bf16),
            ((own, length, 64), bf16),
            ((own, length, 64), bf16),
            ((own, 64, length), bf16),
            ((own, length, 64), bf16),
            ((own, BQ, REACH + 2 * BQ), f32),
            ((own, BQ, REACH + BQ), f32),
            ((own * 64, length), f32),
            ((own, length, 64), f32),
            ((own, length, 64), f32),
        ],
        length * length * own * 160,
    )


def cross_backward(limits, rows, q, kv, grad, o_t, lse, bk=BQ):
    length, own, keys = q.shape[0], q.shape[1] // 64, kv.shape[0]
    return call(
        functools.partial(cross_backward_kernel, own, bk),
        "cross_backward",
        [limits, rows, q, kv, grad, o_t, lse],
        [((length, own * 64), bf16), ((keys, own * 128), bf16)],
        [
            ((own, 64, length), bf16),
            ((own, length, 64), bf16),
            ((own, 64, keys), bf16),
            ((own, keys, 64), bf16),
            ((own, keys, 64), bf16),
            ((own, 64, length), bf16),
            ((own, length, 64), bf16),
            ((own * 64, length), f32),
            ((own, keys, 64), f32),
            ((own, keys, 64), f32),
        ],
        length * keys * own * 320,
    )


def rows_of(blocks_ref):
    return jnp.concatenate([blocks_ref[g] for g in range(blocks_ref.shape[0])], axis=1)


def against(a, b):
    return lax.dot_general(a, b, (((1,), (1,)), ((), ())), preferred_element_type=jnp.float32)


def into_kernel(tok_ref, home_ref, gain_ref, enc_ref, w_ref, after_ref, norm_ref, query_ref, pairs_ref):
    which = pl.program_id(0)

    @pl.when(which == 0)
    def _():
        value = home_ref[...].astype(jnp.float32) + dot(rows_of(tok_ref), w_ref[0])
        after_ref[...] = value
        scale = lax.rsqrt(jnp.mean(value * value, axis=1, keepdims=True) + EPS)
        norm_ref[...] = (value * scale * gain_ref[...]).astype(jnp.bfloat16)

    @pl.when(which == 1)
    def _():
        query = dot(norm_ref[...], w_ref[0]).astype(jnp.bfloat16)
        cols = query_ref.shape[2]
        for g in range(query_ref.shape[0]):
            query_ref[g] = query[:, g * cols : (g + 1) * cols]

    for half in range(2):

        @pl.when(which == 2 + half)
        def _():
            pairs = dot(enc_ref[...], w_ref[0]).astype(jnp.bfloat16)
            groups, cols = pairs_ref.shape[0] // 2, pairs_ref.shape[2]
            for g in range(groups):
                pairs_ref[half * groups + g] = pairs[:, g * cols : (g + 1) * cols]


def outof_kernel(
    dq_ref, dkv_ref, after_ref, gain_ref, middle_ref, w_ref,
    upper_ref, low_ref, out_ref, gain_grad_ref, enc_grad_ref, dq_flat_ref, dkv_flat_ref, enc_sum,
):
    which = pl.program_id(0)

    @pl.when(which == 0)
    def _():
        grad_query = rows_of(dq_ref)
        dq_flat_ref[...] = grad_query
        dkv_flat_ref[...] = rows_of(dkv_ref)
        grad = against(grad_query, w_ref[0])
        value = after_ref[...]
        unit = value * lax.rsqrt(jnp.mean(value * value, axis=1, keepdims=True) + EPS)
        gain_grad_ref[...] = jnp.sum(grad * unit, axis=0, keepdims=True)
        scale = lax.rsqrt(jnp.mean(value * value, axis=1, keepdims=True) + EPS)
        grad = grad * gain_ref[...]
        inner = jnp.mean(grad * unit, axis=1, keepdims=True)
        upper = middle_ref[...] + scale * (grad - unit * inner)
        upper_ref[...] = upper
        low_ref[...] = upper.astype(jnp.bfloat16)

    @pl.when(which == 1)
    def _():
        grad = against(low_ref[...], w_ref[0]).astype(jnp.bfloat16)
        cols = out_ref.shape[2]
        for g in range(out_ref.shape[0]):
            out_ref[g] = grad[:, g * cols : (g + 1) * cols]

    width = w_ref.shape[1]

    @pl.when(which == 2)
    def _():
        enc_sum[...] = against(dkv_flat_ref[:, :width], w_ref[0])

    @pl.when(which == 3)
    def _():
        enc_grad_ref[...] = (enc_sum[...] + against(dkv_flat_ref[:, width:], w_ref[0])).astype(jnp.bfloat16)


def over_weights(body, name, arrays, weights, order, outs, scratch=()):
    count, rows, cols = weights.shape
    whole = lambda shape: pl.BlockSpec(shape, lambda i: (0,) * len(shape))
    return pl.pallas_call(
        body,
        name=name,
        grid=(count,),
        out_shape=[jax.ShapeDtypeStruct(s, d) for s, d in outs],
        in_specs=[whole(v.shape) for v in arrays] + [pl.BlockSpec((1, rows, cols), lambda i: (order(i), 0, 0))],
        out_specs=[whole(s) for s, _ in outs],
        scratch_shapes=[pltpu.VMEM(s, d) for s, d in scratch],
        compiler_params=pltpu.CompilerParams(vmem_limit_bytes=62 << 20, dimension_semantics=("arbitrary",)),
        cost_estimate=pl.CostEstimate(flops=0, bytes_accessed=weights.size * 2, transcendentals=0),
    )(*arrays, weights)


MESH = pl.DeviceIdType.MESH


def ring_place(index, n):
    z, x = index // 2, index % 2
    return z + x * (n - 1 - 2 * z)


def ring_index(place, n):
    x = place // (n // 2)
    z = place + x * (n - 1 - 2 * place)
    return 2 * z + x


def ring_greet(n, others):
    place = ring_place(lax.axis_index("seq"), n)
    right = ring_index((place + 1) % n, n)
    left = ring_index((place + n - 1) % n, n)
    barrier = pltpu.get_barrier_semaphore()
    for neighbour in (left, right):
        pl.semaphore_signal(barrier, inc=1, device_id={"seq": neighbour}, device_id_type=MESH)
    for other in others:
        pl.semaphore_signal(barrier, inc=1, device_id={"fsdp": other}, device_id_type=MESH)
    pl.semaphore_wait(barrier, 2 + len(others))
    return place, right, left


def ring_cut(shape, split, n):
    rows, cols = shape[0] // n, shape[1]
    return (rows, cols // split) if split > 0 else (rows // -split, cols)


def ring_window(ref, shape, split, n, piece, chunk):
    whole = shape[0] // n
    rows, cols = ring_cut(shape, split, n)
    if split > 0:
        return ref.at[pl.ds(chunk * whole, rows), pl.ds(piece * cols, cols)]
    return ref.at[pl.ds(chunk * whole + piece * rows, rows), :]


def ring_kernel(n, splits, fan, *refs):
    count = len(splits)
    more = 1 if fan else 0
    x_refs, y_refs = refs[:count], refs[count + more : 2 * count + more]
    slots = refs[2 * (count + more) : 3 * count + 2 * more]
    send_sem, recv_sem = refs[3 * count + 2 * more :]
    place, right, left = ring_greet(n, [])
    streams = [
        (k, piece, (piece if abs(splits[k]) > 1 else k) % 2) for k in range(count) for piece in range(abs(splits[k]))
    ]

    def window(ref, k, piece, chunk):
        return ring_window(ref, x_refs[k].shape, splits[k], n, piece, chunk)

    def chunk_at(down, step):
        return (place + 1 + step) % n if down else (place + 2 * n - 1 - step) % n

    copies = {}

    def start(number, step, src, dst, down):
        copies[number, step] = pltpu.make_async_remote_copy(
            src_ref=src,
            dst_ref=dst,
            send_sem=send_sem.at[number, step],
            recv_sem=recv_sem.at[number, step],
            device_id={"seq": left if down else right},
            device_id_type=MESH,
        )
        copies[number, step].start()

    def turn_block(number):
        inner_ref, turned_ref = refs[count], refs[2 * count + 1]
        rows = inner_ref.shape[0] // (2 * fan * n)
        half, first = number // (fan // 2), number % (fan // 2) * 2
        tall = jnp.concatenate(
            [
                inner_ref[pl.ds(((chunk * fan + group) * 2 + half) * rows, rows), :].astype(jnp.float32)
                for group in (first, first + 1)
                for chunk in range(n)
            ]
        )
        wide = 2 * n * rows
        turned_ref[:, number * wide : (number + 1) * wide] = jnp.transpose(tall, (1, 0)).astype(jnp.bfloat16)

    for number, (k, piece, down) in enumerate(streams):
        start(number, 0, window(x_refs[k], k, piece, place), window(slots[k], k, piece, 0), down)
    for step in range(n - 1):
        if step < fan:
            turn_block(step)
        for number, (k, piece, down) in enumerate(streams):
            copies[number, step].wait_recv()
            chunk = chunk_at(down, step)
            mine = window(x_refs[k], k, piece, chunk)
            landed = window(slots[k], k, piece, step)
            total = landed[...].astype(jnp.float32) + mine[...].astype(jnp.float32)
            if step < n - 2:
                landed[...] = total.astype(jnp.bfloat16)
                start(number, step + 1, landed, window(slots[k], k, piece, step + 1), down)
            else:
                done = window(y_refs[k], k, piece, chunk)
                done[...] = total.astype(jnp.bfloat16)
                start(number, n - 1, done, done, down)
    for step in range(n - 1):
        for number, (k, piece, down) in enumerate(streams):
            copies[number, n - 1 + step].wait_recv()
            if step < n - 2:
                done = window(y_refs[k], k, piece, chunk_at(down, n - 1 + step))
                start(number, n + step, done, done, down)
    for one in copies.values():
        one.wait_send()


def ring_call(body, name, arrays, outs, scratch, ident):
    size = sum(v.size * 2 for v in arrays)
    return pl.pallas_call(
        body,
        name=name,
        out_shape=[jax.ShapeDtypeStruct(s, d) for s, d in outs],
        in_specs=[pl.BlockSpec(memory_space=pltpu.VMEM)] * len(arrays),
        out_specs=[pl.BlockSpec(memory_space=pltpu.VMEM)] * len(outs),
        scratch_shapes=scratch,
        compiler_params=pltpu.CompilerParams(
            collective_id=ident, has_side_effects=True, vmem_limit_bytes=48 << 20
        ),
        cost_estimate=pl.CostEstimate(flops=0, bytes_accessed=60 * size, transcendentals=0),
    )(*arrays)


def ring_total(arrays, splits, ident, inner=None):
    n, fan = lax.axis_size("seq"), lax.axis_size("fsdp")
    streams = sum(abs(s) for s in splits)
    more = [] if inner is None else [inner]
    return ring_call(
        functools.partial(ring_kernel, n, splits, 0 if inner is None else fan),
        "ring_total",
        arrays + more,
        [(v.shape, jnp.bfloat16) for v in arrays] + [(v.shape[::-1], jnp.bfloat16) for v in more],
        [pltpu.VMEM((v.shape[0] // n * (n - 1), v.shape[1]), jnp.bfloat16) for v in arrays]
        + [pltpu.SemaphoreType.DMA((streams, 2 * n - 2))] * 2,
        ident,
    )


def units_kernel(
    n, fan, x_ref, part_ref, few_ref, inner_ref, outer_ref, sum_ref, few_sum_ref, slots, acc, landed, few_landed,
    down_send, down_recv, swap_send, swap_recv, own_sem, send_sem, recv_sem, part_send, part_recv,
):
    s, me = lax.axis_index("seq"), lax.axis_index("fsdp")
    rows, width = acc.shape[0] // 3, x_ref.shape[1]
    cols = width // fan
    block = 2 * fan * rows
    place, right, left = ring_greet(n, [(me + far) % fan for far in range(1, fan)])
    sums = {}

    def piece_of(ref, at, piece):
        return ref.at[pl.ds(at * 3 * rows, 3 * rows), pl.ds(piece * cols, cols)]

    def send_sum(piece, step, src):
        to = left if piece >= fan // 2 else right
        sums[piece, step] = pltpu.make_async_remote_copy(
            src_ref=src,
            dst_ref=piece_of(slots, step, piece),
            send_sem=down_send.at[piece, step],
            recv_sem=down_recv.at[piece, step],
            device_id={"seq": to},
            device_id_type=MESH,
        )
        sums[piece, step].start()

    def chunk(piece, step):
        return ring_index((place + 1 + step) % n if piece >= fan // 2 else (place + 2 * n - 1 - step) % n, n)

    for piece in range(fan):
        send_sum(piece, 0, piece_of(x_ref, chunk(piece, 0), piece))
    for step in range(n - 1):
        for piece in range(fan):
            sums[piece, step].wait_recv()
            arrived = piece_of(slots, step, piece)
            mine = piece_of(x_ref, chunk(piece, step + 1), piece)
            total = (arrived[...].astype(jnp.float32) + mine[...].astype(jnp.float32)).astype(jnp.bfloat16)
            if step < n - 2:
                arrived[...] = total
                send_sum(piece, step + 1, arrived)
            else:
                acc[:, piece * cols : (piece + 1) * cols] = total
    moves = []
    for far in range(fan):
        target = (me + far) % fan
        for half in range(2):
            src = acc.at[pl.ds(half * rows, rows), pl.ds(pl.multiple_of(target * cols, 128), cols)]
            dst = inner_ref.at[pl.ds(s * block + (me * 2 + half) * rows, rows), :]
            if far:
                one = pltpu.make_async_remote_copy(
                    src_ref=src,
                    dst_ref=dst,
                    send_sem=swap_send.at[far, half],
                    recv_sem=swap_recv.at[far, half],
                    device_id={"fsdp": target},
                    device_id_type=MESH,
                )
            else:
                one = pltpu.make_async_copy(src, dst, own_sem.at[half])
            one.start()
            moves.append(one)
    mine = pltpu.make_async_copy(
        acc.at[pl.ds(2 * rows, rows), :], outer_ref.at[pl.ds(s * rows, rows), :], own_sem.at[2]
    )
    mine.start()
    copies = {}
    outs = ((outer_ref, (n * rows, width), 2), (inner_ref, (n * block, cols), -2))

    def start(k, piece, step):
        ref, shape, split = outs[k]
        chunk = ring_index((place + step) % n if piece else (place + n - step) % n, n)
        view = ring_window(ref, shape, split, n, piece, chunk)
        copies[k, piece, step] = pltpu.make_async_remote_copy(
            src_ref=view,
            dst_ref=view,
            send_sem=send_sem.at[2 * k + piece, step],
            recv_sem=recv_sem.at[2 * k + piece, step],
            device_id={"seq": left if piece else right},
            device_id_type=MESH,
        )
        copies[k, piece, step].start()

    def forward(k, step):
        for piece in range(2):
            copies[k, piece, step].wait_recv()
            if step < n - 2:
                start(k, piece, step + 1)

    mine.wait()
    start(0, 0, 0)
    start(0, 1, 0)
    lead = (n - 1) // 2
    for step in range(lead):
        forward(0, step)
    for one in moves:
        one.wait()
    parts = []
    for far in range(1, fan):
        target = (me + far) % fan
        for which, (src, into) in enumerate(((part_ref, landed), (few_ref, few_landed))):
            rest = src.shape[0] // fan
            one = pltpu.make_async_remote_copy(
                src_ref=src.at[pl.ds(target * rest, rest), :],
                dst_ref=into.at[far],
                send_sem=part_send.at[which, far],
                recv_sem=part_recv.at[which, far],
                device_id={"fsdp": target},
                device_id_type=MESH,
            )
            one.start()
            parts.append(one)
    start(1, 0, 0)
    start(1, 1, 0)
    for step in range(n - 1):
        forward(1, step)
        if lead + step < n - 1:
            forward(0, lead + step)
    for one in parts:
        one.wait()
    for src, into, out in ((part_ref, landed, sum_ref), (few_ref, few_landed, few_sum_ref)):
        rest = src.shape[0] // fan
        total = src[pl.ds(pl.multiple_of(me * rest, rest), rest), :].astype(jnp.float32)
        for far in range(1, fan):
            total = total + into[far].astype(jnp.float32)
        out[...] = total
    for one in [*copies.values(), *sums.values()]:
        one.wait_send()


def units_total(grads, part, few, ident):
    n, fan = lax.axis_size("seq"), lax.axis_size("fsdp")
    rows, width = grads.shape[0] // (3 * n), grads.shape[1]
    tokens = part.shape[0] // fan
    sems = lambda *shape: pltpu.SemaphoreType.DMA(shape)
    return ring_call(
        functools.partial(units_kernel, n, fan),
        "units_total",
        [grads, part, few],
        [
            ((n * 2 * fan * rows, width // fan), jnp.bfloat16),
            ((n * rows, width), jnp.bfloat16),
            ((tokens, part.shape[1]), jnp.float32),
            ((few.shape[0] // fan, few.shape[1]), jnp.float32),
        ],
        [
            pltpu.VMEM(((n - 1) * 3 * rows, width), jnp.bfloat16),
            pltpu.VMEM((3 * rows, width), jnp.bfloat16),
            pltpu.VMEM((fan, tokens, part.shape[1]), jnp.bfloat16),
            pltpu.VMEM((fan, few.shape[0] // fan, few.shape[1]), jnp.bfloat16),
        ]
        + [sems(fan, n - 1), sems(fan, n - 1), sems(fan, 2), sems(fan, 2), sems(3)]
        + [sems(4, n - 1), sems(4, n - 1), sems(2, fan), sems(2, fan)],
        ident,
    )


def team(n):
    s, f = lax.axis_index("seq"), lax.axis_index("fsdp")
    half = s // (n // 2)
    away = (half + f) % 2
    return f // 2, half, (s + away * (n // 2)) % n


def swap_kernel(n, fan, count, fars, fresh, *refs):
    given = count + (len(fars) > 0) + (0 if fresh else 2)
    x_refs, y_refs = refs[:count], refs[given : given + count]
    sems = refs[given + count + (2 if fars else 0) :]
    send_sem, recv_sem, own_sem = sems[:3]
    pair, half, rank = team(n)
    me = lax.axis_index("fsdp")

    def device(other):
        away = (other // (n // 2) + half) % 2
        return {"seq": (other + away * (n // 2)) % n, "fsdp": 2 * pair + (half + away) % 2}

    barrier = pltpu.get_barrier_semaphore()
    for j in range(1, n):
        pl.semaphore_signal(barrier, inc=1, device_id=device((rank + j) % n), device_id_type=MESH)
    travel = [far for far in fars if far]
    for far in travel:
        pl.semaphore_signal(barrier, inc=1, device_id={"fsdp": (me + fan - far) % fan}, device_id_type=MESH)
    pl.semaphore_wait(barrier, n - 1 + len(travel))
    copies = []
    for k in range(count):
        for j in range(1, n):
            other = (rank + j) % n
            one = pltpu.make_async_remote_copy(
                src_ref=x_refs[k].at[other],
                dst_ref=y_refs[k].at[rank],
                send_sem=send_sem.at[k, j],
                recv_sem=recv_sem.at[k, j],
                device_id=device(other),
                device_id_type=MESH,
            )
            one.start()
            copies.append(one)
    for k in range(count):
        one = pltpu.make_async_copy(x_refs[k].at[rank], y_refs[k].at[rank], own_sem.at[k])
        one.start()
        copies.append(one)
    if fars:
        w_ref, halves = refs[count], refs[given + count : given + count + 2]
        far_send, far_recv, far_own, stage = sems[3:]
        rest = []
        units, cols = halves[0].shape[0], w_ref.shape[1]
        for i, far in enumerate(fars):
            target = (me + far) % fan
            for part in range(2):
                src = w_ref.at[pl.ds((part * fan + target) * units, units), :]
                dst = halves[part].at[:, pl.ds(pl.multiple_of(me * cols, 128), cols)]
                if far:
                    one = pltpu.make_async_remote_copy(
                        src_ref=src,
                        dst_ref=dst,
                        send_sem=far_send.at[i, part],
                        recv_sem=far_recv.at[i, part],
                        device_id={"fsdp": target},
                        device_id_type=MESH,
                    )
                else:
                    one = pltpu.make_async_copy(src, stage.at[part], far_own.at[0, part])
                    rest.append((one, pltpu.make_async_copy(stage.at[part], dst, far_own.at[1, part])))
                one.start()
                if far:
                    copies.append(one)
        for inward, outward in rest:
            inward.wait()
            outward.start()
            copies.append(outward)
    for one in copies:
        one.wait()


def swap(arrays, ident, fars=(), given=None, halves=None):
    n, fan = lax.axis_size("seq"), lax.axis_size("fsdp")
    count = len(arrays)
    size = sum(v.size * 2 for v in arrays)
    operands, outs, alias = list(arrays), [jax.ShapeDtypeStruct(v.shape, v.dtype) for v in arrays], {}
    scratch = [
        pltpu.SemaphoreType.DMA((count, n)),
        pltpu.SemaphoreType.DMA((count, n)),
        pltpu.SemaphoreType.DMA((count,)),
    ]
    if fars:
        operands.append(given)
        shape = (given.shape[0] // (2 * fan), given.shape[1] * fan)
        outs += [jax.ShapeDtypeStruct(shape, given.dtype)] * 2
        scratch += [pltpu.SemaphoreType.DMA((len(fars), 2))] * 2 + [
            pltpu.SemaphoreType.DMA((2, 2)),
            pltpu.VMEM((2, given.shape[0] // (2 * fan), given.shape[1]), given.dtype),
        ]
        if halves is not None:
            operands += list(halves)
            alias = {count + 1: count, count + 2: count + 1}
    return pl.pallas_call(
        functools.partial(swap_kernel, n, fan, count, fars, not fars or halves is None),
        name="swap",
        out_shape=outs,
        in_specs=[pl.BlockSpec(memory_space=pl.ANY)] * len(operands),
        out_specs=[pl.BlockSpec(memory_space=pl.ANY)] * len(outs),
        scratch_shapes=scratch,
        input_output_aliases=alias,
        compiler_params=pltpu.CompilerParams(collective_id=ident, has_side_effects=True),
        cost_estimate=pl.CostEstimate(flops=0, bytes_accessed=size, transcendentals=0),
    )(*operands)


def norm_apply(value, gain):
    return value * lax.rsqrt(jnp.mean(value * value, axis=-1, keepdims=True) + EPS) * gain


def norm_back(value, gain, grad):
    _, pull = jax.vjp(norm_apply, value, gain)
    return pull(grad)


def gate_mix(gate, up):
    return jax.nn.gelu(gate, approximate=True) * up


def counts_below(ids, values):
    total = jnp.zeros_like(values)
    for doc in range(DOCS):
        total = total + jnp.where(values > doc, jnp.sum((ids == doc).astype(jnp.int32)), 0)
    return total


def change_home(value):
    n, fan = lax.axis_size("seq"), lax.axis_size("fsdp")
    pairs = []
    for s in range(n):
        for f in range(fan):
            away = (s // (n // 2) + f) % 2
            target = ((s + n // 2) % n, f ^ 1) if away else (s, f)
            pairs.append((s * fan + f, target[0] * fan + target[1]))
    return lax.ppermute(value, ("seq", "fsdp"), pairs)


def spread(blocks):
    fan, me = lax.axis_size("fsdp"), lax.axis_index("fsdp")
    result = blocks
    for far in range(1, fan):
        block = lax.dynamic_index_in_dim(blocks, (me + far) % fan, 0, True)
        block = lax.ppermute(block, "fsdp", [(f, (f + far) % fan) for f in range(fan)])
        result = lax.dynamic_update_slice_in_dim(result, block, (me - far) % fan, 0)
    return result


def flat(blocks):
    return jnp.transpose(blocks, (1, 0, 2)).reshape(blocks.shape[1], -1)


def by_rows(value):
    return with_layout_constraint(value, Layout(major_to_minor=tuple(range(value.ndim))))


def scatter(grad):
    return lax.psum_scatter(grad, "fsdp", scatter_dimension=0, tiled=True)


def shards(
    layer_in, encoder, decoder_ids, encoder_ids, rel_buckets,
    norm_self, self_qkv, self_out, rel_table, norm_cross, cross_q, cross_kv, cross_out, norm_ff, ff_in, ff_out,
    cotangent,
):
    seqs, local, width = layer_in.shape
    enc_local = encoder.shape[1]
    parts = lax.axis_size("seq")
    heads = self_qkv.shape[1]
    dh = self_qkv.shape[2] // 3
    own = heads // parts
    rows = seqs * local
    buckets, table_own = rel_table.shape
    length, keys = local * parts, enc_local * parts
    gather = lambda v: lax.all_gather(v, "fsdp", axis=0, tiled=True)

    fan = lax.axis_size("fsdp")
    units = ff_in.shape[1] // (2 * fan)
    part = norm_self.shape[0]
    pair, half, rank = team(parts)

    qkv_w = gather(self_qkv)
    small = jnp.concatenate([norm_self, norm_cross, norm_ff, rel_table.reshape(-1)])
    small = lax.all_gather(small, "fsdp", axis=0, tiled=False)
    early = by_rows(jnp.stack([self_out, cross_q, *jnp.split(cross_kv.reshape(-1, 2 * width), 2, axis=1)]))
    small, early = lax.optimization_barrier((small, early))
    early = lax.all_gather(early, "fsdp", axis=1, tiled=True)
    both_ids = jnp.concatenate([decoder_ids.reshape(-1), encoder_ids.reshape(-1)])
    both_ids = change_home(jnp.pad(both_ids, (0, 1024 - local - enc_local)).reshape(8, 128))
    inner_t = ff_in.T
    by_kernel = (width // fan) % 128 == 0 and fan % 2 == 0 and (ff_in.shape[0] // parts) % 8 == 0
    (both_ids,) = swap([jnp.broadcast_to(both_ids[None], (parts, 8, 128))], 13)
    home = change_home(layer_in.reshape(rows, width))
    early = by_rows(early)
    gain_first, gain_second, gain_third = (
        small[:, i * part : (i + 1) * part].reshape(width).astype(f32) for i in range(3)
    )
    table = jnp.transpose(small[:, 3 * part :].reshape(-1, buckets, table_own), (1, 0, 2)).reshape(buckets, heads)
    both_ids = both_ids.reshape(parts, 1024)
    ids = both_ids[:, :local].reshape(length)
    enc_ids = both_ids[:, local : local + enc_local].reshape(keys)

    first_seen = counts_below(ids, ids)
    enc_first = counts_below(enc_ids, ids)
    enc_last = counts_below(enc_ids, ids + 1)
    blocks = length // BQ
    bk = BQ
    self_rows = jnp.broadcast_to(first_seen[None], (8, length))
    cross_rows = jnp.concatenate([enc_first[None], enc_last[None], jnp.zeros((6, length), jnp.int32)])
    self_limits = jnp.stack(
        [first_seen[::BQ] // bk, (jnp.arange(blocks, dtype=jnp.int32) + 1) * (BQ // bk)]
    )
    cross_limits = jnp.stack([enc_first[::BQ] // bk, (enc_last[BQ - 1 :: BQ] + bk - 1) // bk])

    first_head = rank * own
    table_mine = lax.dynamic_slice_in_dim(table.astype(f32), first_head, own, 1)
    near = rel_buckets[:REACH]
    onehot = (near[:, None] == jnp.arange(buckets, dtype=jnp.int32)[None, :]).astype(f32)
    bias = jnp.einsum("ln,ng->gl", onehot, table_mine, precision=HIGH)
    ext = jnp.concatenate(
        [jnp.full((own, BQ), MASKED, f32), bias, jnp.zeros((own, BQ), f32)], axis=1
    )

    qkv_w, home, inner_t, ext, self_rows, cross_rows, self_limits, cross_limits = lax.optimization_barrier(
        (qkv_w, home, inner_t, ext, self_rows, cross_rows, self_limits, cross_limits)
    )
    qkv_w = qkv_w.reshape(width, parts, own * 3 * dh)

    stream = home.astype(f32)
    normed_first = norm_apply(stream, gain_first).astype(bf16)
    qkv_tok = jnp.einsum("td,dge->gte", normed_first, qkv_w, preferred_element_type=f32).astype(bf16)
    others = change_home(jnp.concatenate([cotangent.reshape(rows, width), encoder.reshape(-1, width)]))
    grad_low, enc_flat = others[:rows], others[rows:]
    fars = [tuple(far for far in range(fan) if by_kernel and (far == 2) == first) for first in (True, False)]
    qkv, *halves = swap([qkv_tok], 17, fars[0], inner_t)
    qkv, cross_out, grad_low = lax.optimization_barrier((qkv, cross_out, grad_low))
    if rows == cross_out.shape[0]:
        mix_cross, grad_group = lax.all_gather(jnp.stack([cross_out, grad_low]), "fsdp", axis=1, tiled=True)
    else:
        mix_cross, grad_group = gather(cross_out), gather(grad_low)
    mix_cross = mix_cross.reshape(parts, own * dh, width)
    qkv = qkv.reshape(length, own * 3 * dh)
    out_self, self_t, self_lse = self_forward(self_limits, self_rows, ext, qkv)
    (self_tok,) = swap([out_self.reshape(parts, local, own * dh)], 11)
    after_self, normed_second, query_tok, pairs_tok = over_weights(
        into_kernel,
        "self_out_to_cross",
        [self_tok, home, gain_second.reshape(1, width), enc_flat],
        early,
        lambda i: i,
        [
            ((rows, width), f32),
            ((rows, width), bf16),
            ((parts, rows, own * dh), bf16),
            ((parts, enc_local, own * 2 * dh), bf16),
        ],
    )
    query_cross, pairs = swap([query_tok, pairs_tok], 12)
    query_cross, pairs = query_cross.reshape(length, own * dh), pairs.reshape(keys, own * 2 * dh)
    out_cross, cross_t, cross_lse = cross_forward(cross_limits, cross_rows, query_cross, pairs)
    cross_tok, *halves = swap([out_cross.reshape(parts, local, own * dh)], 16, fars[1], inner_t, halves)
    if not by_kernel:
        halves = spread(jnp.transpose(inner_t.reshape(2, fan, units, -1), (1, 0, 2, 3)))
        halves = [jnp.transpose(halves[:, i], (1, 0, 2)).reshape(units, width) for i in range(2)]
    gate_t, up_t = halves
    after_cross = after_self + jnp.einsum("gtc,gcd->td", cross_tok, mix_cross, preferred_element_type=f32)
    normed_third = norm_apply(after_cross, gain_third).astype(bf16)
    normed_group = gather(normed_third)
    gate = jnp.einsum("td,fd->tf", normed_group, gate_t, preferred_element_type=f32)
    up = jnp.einsum("td,fd->tf", normed_group, up_t, preferred_element_type=f32)
    hidden = gate_mix(gate, up).astype(bf16)

    grad_hidden = jnp.einsum("td,fd->tf", grad_group, ff_out, preferred_element_type=f32)
    _, pull_mix = jax.vjp(gate_mix, gate, up)
    grad_gate, grad_up = (g.astype(bf16) for g in pull_mix(grad_hidden))
    grad_third_in = jnp.dot(grad_gate, gate_t, preferred_element_type=f32) + jnp.dot(
        grad_up, up_t, preferred_element_type=f32
    )
    grad_third_in = scatter(grad_third_in.astype(bf16))
    outer_part = jnp.dot(hidden, ff_out, preferred_element_type=f32).astype(bf16)
    grad_units = [
        jnp.einsum("tf,td->fd", g, y, preferred_element_type=f32).astype(bf16)
        for g, y in ((grad_gate, normed_group), (grad_up, normed_group), (hidden, grad_group))
    ]
    if by_kernel:
        grad_units = jnp.stack([g.reshape(parts, units // parts, width) for g in grad_units], axis=1)
        grad_units = grad_units.reshape(3 * units, width)
    grad_third_in, outer_part, part_units = lax.optimization_barrier((grad_third_in, outer_part, grad_units))
    grad_third_in = grad_third_in.astype(f32)
    grad_from_third, grad_gain_third = norm_back(after_cross, gain_third, grad_third_in)
    grad_middle = grad_low.astype(f32) + grad_from_third
    middle_low = grad_middle.astype(bf16)
    grad_mix_cross = jnp.einsum("gtc,td->gcd", cross_tok, middle_low, preferred_element_type=f32)
    part_cross = scatter(grad_mix_cross.reshape(width, width).astype(bf16))
    grad_cross_tok = jnp.einsum("td,gcd->gtc", middle_low, mix_cross, preferred_element_type=f32).astype(bf16)
    (grad_cross,) = swap([grad_cross_tok], 11)
    grad_cross = grad_cross.reshape(length, own * dh)
    grad_query, grad_pairs = cross_backward(
        cross_limits, cross_rows, query_cross, pairs, grad_cross, cross_t, cross_lse
    )
    grad_query_tok, grad_pairs_tok = swap(
        [grad_query.reshape(parts, local, own * dh), grad_pairs.reshape(parts, enc_local, own * 2 * dh)], 12
    )
    (
        grad_upper, upper_low, grad_self_tok, grad_gain_second, grad_encoder, grad_query_tok, grad_pairs_tok
    ) = over_weights(
        outof_kernel,
        "cross_to_self_out",
        [grad_query_tok, grad_pairs_tok, after_self, gain_second.reshape(1, width), grad_middle],
        early,
        lambda i: jnp.where(i < 2, 1 - i, i),
        [
            ((rows, width), f32),
            ((rows, width), bf16),
            ((parts, rows, own * dh), bf16),
            ((1, width), f32),
            ((enc_local, width), bf16),
            ((rows, width), bf16),
            ((enc_local, 2 * width), bf16),
        ],
        [((enc_local, width), f32)],
    )
    grad_query_w = jnp.einsum("td,te->de", normed_second, grad_query_tok, preferred_element_type=f32)
    grad_pairs_w = jnp.einsum("td,te->de", enc_flat, grad_pairs_tok, preferred_element_type=f32)
    grad_mix_self = jnp.einsum("gtc,td->gcd", self_tok, upper_low, preferred_element_type=f32)
    grad_mid = jnp.concatenate([grad_query_w.astype(bf16), grad_pairs_w.astype(bf16)], axis=1)
    part_self = scatter(grad_mix_self.reshape(width, width).astype(bf16))
    grad_self_tok, grad_mid = lax.optimization_barrier((grad_self_tok, grad_mid))
    part_mid = scatter(grad_mid)
    (grad_self,) = swap([grad_self_tok], 11)
    grad_self = grad_self.reshape(length, own * dh)
    grad_qkv, diagonals = self_backward(self_limits, self_rows, ext, qkv, grad_self, self_t, self_lse)
    (grad_qkv_tok,) = swap([grad_qkv.reshape(parts, local, own * 3 * dh)], 10)
    grad_qkv_tok = flat(grad_qkv_tok)
    grad_qkv_w = jnp.einsum("td,te->de", normed_first, grad_qkv_tok, preferred_element_type=f32)
    grad_qkv_w, grad_qkv_tok = lax.optimization_barrier((grad_qkv_w.astype(bf16), grad_qkv_tok))
    grad_first_in = jnp.einsum("te,de->td", grad_qkv_tok, qkv_w.reshape(width, -1), preferred_element_type=f32)
    grad_from_first, grad_gain_first = norm_back(stream, gain_first, grad_first_in)
    grad_layer_in = (grad_upper + grad_from_first).astype(bf16)
    bucket_line = jnp.concatenate([jnp.full((BQ - 1,), -1, jnp.int32), near, jnp.full((BQ + 1,), -1, jnp.int32)])
    in_bucket = (bucket_line[:, None] == jnp.arange(buckets, dtype=jnp.int32)).astype(f32)
    by_bucket = jnp.einsum("xn,gx->ng", in_bucket, diagonals, precision=HIGH)
    grad_table = lax.dynamic_update_slice_in_dim(jnp.zeros((buckets, heads), f32), by_bucket, first_head, 1)

    gains = jnp.concatenate(
        [g.reshape(-1, part) for g in (grad_gain_first, grad_gain_second, grad_gain_third)], axis=1
    )
    tables = jnp.transpose(grad_table.reshape(buckets, -1, table_own), (1, 0, 2)).reshape(-1, buckets * table_own)
    small_grads = jnp.concatenate([gains, tables], axis=1).astype(bf16)
    small_size = small_grads.shape[1]
    going_home = jnp.concatenate([grad_layer_in, grad_encoder.astype(bf16)])
    part_last = scatter(grad_qkv_w)
    going_home, small_grads, part_units, part_cross, part_mid = lax.optimization_barrier(
        (change_home(going_home), small_grads, part_units, part_cross, part_mid)
    )
    if by_kernel:
        few = jnp.pad(small_grads[:, None], ((0, 0), (0, 7), (0, 1024 - small_size))).reshape(fan * 8, 1024)
        total_inner, total_outer, outer_sum, few = units_total(part_units, outer_part, few, 0)
        few = jnp.pad(few[0].astype(bf16).reshape(8, 128), ((0, parts * 8 - 8), (0, 0)))
        total_cross, total_self, total_mid, total_qkv, small_total, total_inner = ring_total(
            [part_cross, part_self, part_mid, part_last, few], (1, 1, 2, 2, 1), 1, total_inner
        )
    else:
        grad_units = [lax.psum(g, "seq") for g in part_units]
        total_inner = spread(jnp.transpose(jnp.stack(grad_units[:2]).reshape(2, units, fan, -1), (2, 0, 1, 3)))
        total_inner = jnp.transpose(total_inner, (3, 1, 0, 2)).reshape(-1, 2 * fan * units).astype(f32)
        total_outer, outer_sum = grad_units[2], scatter(outer_part).astype(f32)
        few = lax.dynamic_index_in_dim(lax.psum(small_grads, "fsdp"), lax.axis_index("fsdp"), 0, False)
        total_cross, total_self, total_mid, total_qkv, small_total = (
            lax.psum(v, "seq") for v in (part_cross, part_self, part_mid, part_last, few)
        )
    layer_out = (after_cross + outer_sum).astype(bf16)
    layer_out, total_inner, total_outer, total_cross, total_self, total_mid, total_qkv, going_home = (
        lax.optimization_barrier(
            (layer_out, total_inner, total_outer, total_cross, total_self, total_mid, total_qkv, going_home)
        )
    )
    layer_out = change_home(layer_out).reshape(seqs, local, width)
    grad_layer_in = going_home[:rows].astype(f32).reshape(seqs, local, width)
    grad_encoder = going_home[rows:].astype(f32).reshape(seqs, enc_local, width)
    total_inner, total_outer, total_mid, total_qkv = (
        v.astype(f32) for v in (total_inner, total_outer, total_mid, total_qkv)
    )
    total_query, total_mix_cross = total_mid[:, :width], total_cross.astype(f32)
    total_pairs = total_mid[:, width:].reshape(-1, heads, 2 * dh)
    total_mix_self, total_qkv = total_self.astype(f32), total_qkv.reshape(-1, heads, 3 * dh)
    mine = small_total.reshape(-1)[:small_size].astype(f32)
    total_gain_first, total_gain_second, total_gain_third = (mine[i * part : (i + 1) * part] for i in range(3))
    total_table = mine[3 * part :].reshape(buckets, table_own)
    return (
        layer_out, grad_layer_in, grad_encoder, total_gain_first, total_qkv, total_mix_self, total_table,
        total_gain_second, total_query, total_pairs, total_mix_cross, total_gain_third, total_inner, total_outer,
    )


def solution(mesh):
    in_specs = (
        P("fsdp", "seq", None), P("fsdp", "seq", None), P("fsdp", "seq"), P("fsdp", "seq"), P(),
        P("fsdp"), P("fsdp", None, None), P("fsdp", None), P(None, "fsdp"), P("fsdp"), P("fsdp", None),
        P("fsdp", None, None), P("fsdp", None), P("fsdp"), P("fsdp", None), P("fsdp", None),
        P("fsdp", "seq", None),
    )
    out_specs = (
        P("fsdp", "seq", None), P("fsdp", "seq", None), P("fsdp", "seq", None), P("fsdp"), P("fsdp", None, None),
        P("fsdp", None), P(None, "fsdp"), P("fsdp"), P("fsdp", None), P("fsdp", None, None), P("fsdp", None),
        P("fsdp"), P("fsdp", None), P("fsdp", None),
    )
    return jax.shard_map(shards, mesh=mesh, in_specs=in_specs, out_specs=out_specs, check_vma=False)
```

```python
import functools

import jax
import jax.numpy as jnp
from jax import lax
from jax.experimental import pallas as pl
from jax.experimental.layout import Layout, with_layout_constraint
from jax.experimental.pallas import tpu as pltpu
from jax.sharding import PartitionSpec as P

EPS = 1e-06
HIGH = lax.Precision.HIGHEST
MASKED = -1e30
DOCS = 4

BQ = 256
REACH = 1024


def blk(index, size):
    return pl.ds(pl.multiple_of(index * size, size), size)


def turn(value):
    return jnp.transpose(value.astype(jnp.float32), (1, 0))


def bias_tiles(ext_ref, tile_ref, own):
    for h in range(own):
        line = jnp.broadcast_to(ext_ref[h : h + 1, :], tile_ref.shape[1:])
        tile_ref[h] = pltpu.roll(line, 0, 1, stride=1, stride_axis=0)


def unpack(ref, own, width, picks, flips, base):
    block = 256

    def one(b, _):
        rows = blk(b, block)
        value = ref[rows, :]
        if flips:
            flat = turn(value).astype(jnp.bfloat16)
            for target, piece in flips:
                for h in range(own):
                    at = h * width + piece * 64
                    target[base + h, :, rows] = flat[at : at + 64]
        for target, piece in picks:
            for h in range(own):
                at = h * width + piece * 64
                target[base + h, rows, :] = value[:, at : at + 64]
        return 0

    lax.fori_loop(0, ref.shape[0] // block, one, 0)


def dot(a, b):
    return jnp.dot(a, b, preferred_element_type=jnp.float32)


def score(own_index, key_tile, query_t, tile_ref, t, low, high, first_key):
    value = dot(key_tile, query_t)
    place = lax.broadcasted_iota(jnp.int32, value.shape, 0)
    keep = place >= low - first_key
    if high is not None:
        keep = keep & (place < high - first_key)
    else:
        value = value + tile_ref[own_index, :, blk(t + 1, BQ)]
    return jnp.where(keep, value, MASKED)


def forward_body(own, bk, causal, lim_ref, rows_ref, q_t, k_rows, v_t, tile_ref, o_ref, ot_ref, lse_ref):
    length = o_ref.shape[0]

    def q_block(i, _):
        cols = blk(i, BQ)
        queries = [q_t[h, :, cols] for h in range(own)]
        low = rows_ref[0:1, cols]
        high = None if causal else rows_ref[1:2, cols]

        def k_block(j, carry):
            keys = blk(j, bk)
            t = i - j
            out = []
            for h in range(own):
                top, total, acc = carry[h]
                s = score(h, k_rows[h, keys, :], queries[h], tile_ref, t, low, high, j * bk)
                new_top = jnp.maximum(top, jnp.max(s, axis=0, keepdims=True))
                p = jnp.exp(s - new_top)
                scale = jnp.exp(top - new_top)
                total = total * scale + jnp.sum(p, axis=0, keepdims=True)
                acc = acc * scale + dot(v_t[h, :, keys], p.astype(jnp.bfloat16))
                out.append((new_top, total, acc))
            return tuple(out)

        start = tuple(
            (
                jnp.full((1, BQ), MASKED, jnp.float32),
                jnp.zeros((1, BQ), jnp.float32),
                jnp.zeros((64, BQ), jnp.float32),
            )
            for _ in range(own)
        )
        ends = lax.fori_loop(lim_ref[0, i], lim_ref[1, i], k_block, start)
        for h in range(own):
            top, total, acc = ends[h]
            ot_ref[h * 64 : h * 64 + 64, cols] = acc / total
            lse_ref[h : h + 1, cols] = top + jnp.log(total)
        o_ref[cols, :] = turn(ot_ref[:, cols]).astype(jnp.bfloat16)
        return 0

    lax.fori_loop(0, length // BQ, q_block, 0)


def self_forward_kernel(own, bk, lim_ref, rows_ref, ext_ref, x_ref, o_ref, ot_ref, lse_ref, q_t, k_rows, v_t, tile_ref):
    bias_tiles(ext_ref, tile_ref, own)
    unpack(x_ref, own, 192, [(k_rows, 1)], [(q_t, 0), (v_t, 2)], 0)
    forward_body(own, bk, True, lim_ref, rows_ref, q_t, k_rows, v_t, tile_ref, o_ref, ot_ref, lse_ref)


def cross_forward_kernel(own, bk, lim_ref, rows_ref, q_ref, kv_ref, o_ref, ot_ref, lse_ref, q_t, k_rows, v_t):
    unpack(q_ref, own, 64, [], [(q_t, 0)], 0)
    unpack(kv_ref, own, 128, [(k_rows, 0)], [(v_t, 1)], 0)
    forward_body(own, bk, False, lim_ref, rows_ref, q_t, k_rows, v_t, None, o_ref, ot_ref, lse_ref)


def backward_body(
    own, bk, causal, lim_ref, rows_ref, do_ref, ot_ref, lse_ref,
    q_t, q_rows, k_t, k_rows, v_rows, do_t, do_rows, tile_ref, sum_ref, dq_t, dk, dv,
):
    length = do_ref.shape[0]
    dk[...] = jnp.zeros_like(dk)
    dv[...] = jnp.zeros_like(dv)
    if causal:
        sum_ref[...] = jnp.zeros_like(sum_ref)

    def q_block(i, _):
        cols = blk(i, BQ)
        low = rows_ref[0:1, cols]
        high = None if causal else rows_ref[1:2, cols]
        per_head = []
        for h in range(own):
            grad_t = do_t[h, :, cols]
            delta = jnp.sum(
                grad_t.astype(jnp.float32) * ot_ref[h * 64 : h * 64 + 64, cols], axis=0, keepdims=True
            )
            per_head.append((q_t[h, :, cols], grad_t, delta, lse_ref[h : h + 1, cols]))

        def k_block(j, carry):
            keys = blk(j, bk)
            t = i - j
            out = []
            for h in range(own):
                query_t, grad_t, delta, lse = per_head[h]
                s = score(h, k_rows[h, keys, :], query_t, tile_ref, t, low, high, j * bk)
                p = jnp.exp(s - lse)
                dp = dot(v_rows[h, keys, :], grad_t)
                ds = (p * (dp - delta)).astype(jnp.bfloat16)
                dv[h, keys, :] += dot(p.astype(jnp.bfloat16), do_rows[h, cols, :])
                dk[h, keys, :] += dot(ds, q_rows[h, cols, :])
                if causal:
                    sum_ref[h, :, blk(t, BQ)] += ds.astype(jnp.float32)
                out.append(carry[h] + dot(k_t[h, :, keys], ds))
            return tuple(out)

        ends = lax.fori_loop(
            lim_ref[0, i],
            lim_ref[1, i],
            k_block,
            tuple(jnp.zeros((64, BQ), jnp.float32) for _ in range(own)),
        )
        for h in range(own):
            dq_t[h * 64 : h * 64 + 64, cols] = ends[h]
        return 0

    lax.fori_loop(0, length // BQ, q_block, 0)


def diagonal_sums(sum_ref, u_ref, own):
    flip = lax.broadcasted_iota(jnp.int32, (BQ, BQ), 0) + lax.broadcasted_iota(jnp.int32, (BQ, BQ), 1) == BQ - 1
    flip = jnp.where(flip, 1.0, 0.0).astype(jnp.bfloat16)
    for h in range(own):
        grid = sum_ref[h]
        high = grid.astype(jnp.bfloat16)
        low = (grid - high.astype(jnp.float32)).astype(jnp.bfloat16)
        upside = dot(flip, high) + dot(flip, low)
        wide = jnp.concatenate([upside, jnp.zeros((BQ, BQ), jnp.float32)], axis=1)
        aligned = pltpu.roll(wide, 0, 1, stride=1, stride_axis=0)
        u_ref[h : h + 1, :] = jnp.sum(aligned, axis=0, keepdims=True)


def self_backward_kernel(
    own, bk, lim_ref, rows_ref, ext_ref, x_ref, do_ref, ot_ref, lse_ref, dx_ref, u_ref,
    q_t, q_rows, k_t, k_rows, v_rows, do_t, do_rows, tile_ref, sum_ref, dq_t, dk, dv,
):
    bias_tiles(ext_ref, tile_ref, own)
    unpack(x_ref, own, 192, [(q_rows, 0), (k_rows, 1), (v_rows, 2)], [(q_t, 0), (k_t, 1)], 0)
    unpack(do_ref, own, 64, [(do_rows, 0)], [(do_t, 0)], 0)
    backward_body(
        own, bk, True, lim_ref, rows_ref, do_ref, ot_ref, lse_ref,
        q_t, q_rows, k_t, k_rows, v_rows, do_t, do_rows, tile_ref, sum_ref, dq_t, dk, dv,
    )
    diagonal_sums(sum_ref, u_ref, own)

    def pack(b, _):
        rows = blk(b, 256)
        dq = turn(dq_t[:, rows])
        pieces = []
        for h in range(own):
            pieces += [dq[:, h * 64 : h * 64 + 64], dk[h, rows, :], dv[h, rows, :]]
        dx_ref[rows, :] = jnp.concatenate(pieces, axis=1).astype(jnp.bfloat16)
        return 0

    lax.fori_loop(0, x_ref.shape[0] // 256, pack, 0)


def cross_backward_kernel(
    own, bk, lim_ref, rows_ref, q_ref, kv_ref, do_ref, ot_ref, lse_ref, dq_ref, dkv_ref,
    q_t, q_rows, k_t, k_rows, v_rows, do_t, do_rows, dq_t, dk, dv,
):
    unpack(q_ref, own, 64, [(q_rows, 0)], [(q_t, 0)], 0)
    unpack(kv_ref, own, 128, [(k_rows, 0), (v_rows, 1)], [(k_t, 0)], 0)
    unpack(do_ref, own, 64, [(do_rows, 0)], [(do_t, 0)], 0)
    backward_body(
        own, bk, False, lim_ref, rows_ref, do_ref, ot_ref, lse_ref,
        q_t, q_rows, k_t, k_rows, v_rows, do_t, do_rows, None, None, dq_t, dk, dv,
    )

    def pack_q(b, _):
        rows = blk(b, 256)
        dq_ref[rows, :] = turn(dq_t[:, rows]).astype(jnp.bfloat16)
        return 0

    def pack_kv(b, _):
        rows = blk(b, 256)
        pieces = []
        for h in range(own):
            pieces += [dk[h, rows, :], dv[h, rows, :]]
        dkv_ref[rows, :] = jnp.concatenate(pieces, axis=1).astype(jnp.bfloat16)
        return 0

    lax.fori_loop(0, q_ref.shape[0] // 256, pack_q, 0)
    lax.fori_loop(0, kv_ref.shape[0] // 256, pack_kv, 0)


SMEM = pl.BlockSpec(memory_space=pltpu.SMEM)
VMEM = pl.BlockSpec(memory_space=pltpu.VMEM)
bf16, f32 = jnp.bfloat16, jnp.float32


def call(body, name, operands, outs, scratch, flops):
    size = sum(v.size * v.dtype.itemsize for v in operands)
    return pl.pallas_call(
        body,
        name=name,
        out_shape=[jax.ShapeDtypeStruct(s, d) for s, d in outs],
        in_specs=[SMEM] + [VMEM] * (len(operands) - 1),
        out_specs=[VMEM] * len(outs),
        scratch_shapes=[pltpu.VMEM(s, d) for s, d in scratch],
        compiler_params=pltpu.CompilerParams(vmem_limit_bytes=62 << 20),
        cost_estimate=pl.CostEstimate(flops=0, bytes_accessed=size, transcendentals=0),
    )(*operands)


def self_forward(limits, rows, ext, x, bk=BQ):
    length, own = x.shape[0], x.shape[1] // 192
    return call(
        functools.partial(self_forward_kernel, own, bk),
        "self_forward",
        [limits, rows, ext, x],
        [((length, own * 64), bf16), ((own * 64, length), f32), ((own, length), f32)],
        [
            ((own, 64, length), bf16),
            ((own, length, 64), bf16),
            ((own, 64, length), bf16),
            ((own, BQ, REACH + 2 * BQ), f32),
        ],
        length * length * own * 64,
    )


def cross_forward(limits, rows, q, kv, bk=BQ):
    length, own, keys = q.shape[0], q.shape[1] // 64, kv.shape[0]
    return call(
        functools.partial(cross_forward_kernel, own, bk),
        "cross_forward",
        [limits, rows, q, kv],
        [((length, own * 64), bf16), ((own * 64, length), f32), ((own, length), f32)],
        [((own, 64, length), bf16), ((own, keys, 64), bf16), ((own, 64, keys), bf16)],
        length * keys * own * 128,
    )


def self_backward(limits, rows, ext, x, grad, o_t, lse, bk=BQ):
    length, own = x.shape[0], x.shape[1] // 192
    return call(
        functools.partial(self_backward_kernel, own, bk),
        "self_backward",
        [limits, rows, ext, x, grad, o_t, lse],
        [((length, own * 192), bf16), ((own, REACH + 2 * BQ), f32)],
        [
            ((own, 64, length), bf16),
            ((own, length, 64), bf16),
            ((own, 64, length), bf16),
            ((own, length, 64), bf16),
            ((own, length, 64), bf16),
            ((own, 64, length), bf16),
            ((own, length, 64), bf16),
            ((own, BQ, REACH + 2 * BQ), f32),
            ((own, BQ, REACH + BQ), f32),
            ((own * 64, length), f32),
            ((own, length, 64), f32),
            ((own, length, 64), f32),
        ],
        length * length * own * 160,
    )


def cross_backward(limits, rows, q, kv, grad, o_t, lse, bk=BQ):
    length, own, keys = q.shape[0], q.shape[1] // 64, kv.shape[0]
    return call(
        functools.partial(cross_backward_kernel, own, bk),
        "cross_backward",
        [limits, rows, q, kv, grad, o_t, lse],
        [((length, own * 64), bf16), ((keys, own * 128), bf16)],
        [
            ((own, 64, length), bf16),
            ((own, length, 64), bf16),
            ((own, 64, keys), bf16),
            ((own, keys, 64), bf16),
            ((own, keys, 64), bf16),
            ((own, 64, length), bf16),
            ((own, length, 64), bf16),
            ((own * 64, length), f32),
            ((own, keys, 64), f32),
            ((own, keys, 64), f32),
        ],
        length * keys * own * 320,
    )


def rows_of(blocks_ref):
    return jnp.concatenate([blocks_ref[g] for g in range(blocks_ref.shape[0])], axis=1)


def against(a, b):
    return lax.dot_general(a, b, (((1,), (1,)), ((), ())), preferred_element_type=jnp.float32)


def into_kernel(tok_ref, home_ref, gain_ref, enc_ref, w_ref, after_ref, norm_ref, query_ref, pairs_ref):
    which = pl.program_id(0)

    @pl.when(which == 0)
    def _():
        value = home_ref[...].astype(jnp.float32) + dot(rows_of(tok_ref), w_ref[0])
        after_ref[...] = value
        scale = lax.rsqrt(jnp.mean(value * value, axis=1, keepdims=True) + EPS)
        norm_ref[...] = (value * scale * gain_ref[...]).astype(jnp.bfloat16)

    @pl.when(which == 1)
    def _():
        query = dot(norm_ref[...], w_ref[0]).astype(jnp.bfloat16)
        cols = query_ref.shape[2]
        for g in range(query_ref.shape[0]):
            query_ref[g] = query[:, g * cols : (g + 1) * cols]

    for half in range(2):

        @pl.when(which == 2 + half)
        def _():
            pairs = dot(enc_ref[...], w_ref[0]).astype(jnp.bfloat16)
            groups, cols = pairs_ref.shape[0] // 2, pairs_ref.shape[2]
            for g in range(groups):
                pairs_ref[half * groups + g] = pairs[:, g * cols : (g + 1) * cols]


def outof_kernel(
    dq_ref, dkv_ref, after_ref, gain_ref, middle_ref, w_ref,
    upper_ref, low_ref, out_ref, gain_grad_ref, enc_grad_ref, dq_flat_ref, dkv_flat_ref, enc_sum,
):
    which = pl.program_id(0)

    @pl.when(which == 0)
    def _():
        grad_query = rows_of(dq_ref)
        dq_flat_ref[...] = grad_query
        dkv_flat_ref[...] = rows_of(dkv_ref)
        grad = against(grad_query, w_ref[0])
        value = after_ref[...]
        unit = value * lax.rsqrt(jnp.mean(value * value, axis=1, keepdims=True) + EPS)
        gain_grad_ref[...] = jnp.sum(grad * unit, axis=0, keepdims=True)
        scale = lax.rsqrt(jnp.mean(value * value, axis=1, keepdims=True) + EPS)
        grad = grad * gain_ref[...]
        inner = jnp.mean(grad * unit, axis=1, keepdims=True)
        upper = middle_ref[...] + scale * (grad - unit * inner)
        upper_ref[...] = upper
        low_ref[...] = upper.astype(jnp.bfloat16)

    @pl.when(which == 1)
    def _():
        grad = against(low_ref[...], w_ref[0]).astype(jnp.bfloat16)
        cols = out_ref.shape[2]
        for g in range(out_ref.shape[0]):
            out_ref[g] = grad[:, g * cols : (g + 1) * cols]

    width = w_ref.shape[1]

    @pl.when(which == 2)
    def _():
        enc_sum[...] = against(dkv_flat_ref[:, :width], w_ref[0])

    @pl.when(which == 3)
    def _():
        enc_grad_ref[...] = (enc_sum[...] + against(dkv_flat_ref[:, width:], w_ref[0])).astype(jnp.bfloat16)


def over_weights(body, name, arrays, weights, order, outs, scratch=()):
    count, rows, cols = weights.shape
    whole = lambda shape: pl.BlockSpec(shape, lambda i: (0,) * len(shape))
    return pl.pallas_call(
        body,
        name=name,
        grid=(count,),
        out_shape=[jax.ShapeDtypeStruct(s, d) for s, d in outs],
        in_specs=[whole(v.shape) for v in arrays] + [pl.BlockSpec((1, rows, cols), lambda i: (order(i), 0, 0))],
        out_specs=[whole(s) for s, _ in outs],
        scratch_shapes=[pltpu.VMEM(s, d) for s, d in scratch],
        compiler_params=pltpu.CompilerParams(vmem_limit_bytes=62 << 20, dimension_semantics=("arbitrary",)),
        cost_estimate=pl.CostEstimate(flops=0, bytes_accessed=weights.size * 2, transcendentals=0),
    )(*arrays, weights)


MESH = pl.DeviceIdType.MESH


def ring_place(index, n):
    z, x = index // 2, index % 2
    return z + x * (n - 1 - 2 * z)


def ring_index(place, n):
    x = place // (n // 2)
    z = place + x * (n - 1 - 2 * place)
    return 2 * z + x


def ring_greet(n, others):
    place = ring_place(lax.axis_index("seq"), n)
    right = ring_index((place + 1) % n, n)
    left = ring_index((place + n - 1) % n, n)
    barrier = pltpu.get_barrier_semaphore()
    for neighbour in (left, right):
        pl.semaphore_signal(barrier, inc=1, device_id={"seq": neighbour}, device_id_type=MESH)
    for other in others:
        pl.semaphore_signal(barrier, inc=1, device_id={"fsdp": other}, device_id_type=MESH)
    pl.semaphore_wait(barrier, 2 + len(others))
    return place, right, left


def ring_cut(shape, split, n):
    rows, cols = shape[0] // n, shape[1]
    return (rows, cols // split) if split > 0 else (rows // -split, cols)


def ring_window(ref, shape, split, n, piece, chunk):
    whole = shape[0] // n
    rows, cols = ring_cut(shape, split, n)
    if split > 0:
        return ref.at[pl.ds(chunk * whole, rows), pl.ds(piece * cols, cols)]
    return ref.at[pl.ds(chunk * whole + piece * rows, rows), :]


def ring_kernel(n, splits, fan, *refs):
    count = len(splits)
    more = 1 if fan else 0
    x_refs, y_refs = refs[:count], refs[count + more : 2 * count + more]
    slots = refs[2 * (count + more) : 3 * count + 2 * more]
    send_sem, recv_sem = refs[3 * count + 2 * more :]
    place, right, left = ring_greet(n, [])
    streams = [
        (k, piece, (piece if abs(splits[k]) > 1 else k) % 2) for k in range(count) for piece in range(abs(splits[k]))
    ]

    def window(ref, k, piece, chunk):
        return ring_window(ref, x_refs[k].shape, splits[k], n, piece, chunk)

    def chunk_at(down, step):
        return (place + 1 + step) % n if down else (place + 2 * n - 1 - step) % n

    copies = {}

    def start(number, step, src, dst, down):
        copies[number, step] = pltpu.make_async_remote_copy(
            src_ref=src,
            dst_ref=dst,
            send_sem=send_sem.at[number, step],
            recv_sem=recv_sem.at[number, step],
            device_id={"seq": left if down else right},
            device_id_type=MESH,
        )
        copies[number, step].start()

    def turn_block(number):
        inner_ref, turned_ref = refs[count], refs[2 * count + 1]
        rows = inner_ref.shape[0] // (2 * fan * n)
        half, first = number // (fan // 2), number % (fan // 2) * 2
        tall = jnp.concatenate(
            [
                inner_ref[pl.ds(((chunk * fan + group) * 2 + half) * rows, rows), :].astype(jnp.float32)
                for group in (first, first + 1)
                for chunk in range(n)
            ]
        )
        wide = 2 * n * rows
        turned_ref[:, number * wide : (number + 1) * wide] = jnp.transpose(tall, (1, 0)).astype(jnp.bfloat16)

    for number, (k, piece, down) in enumerate(streams):
        start(number, 0, window(x_refs[k], k, piece, place), window(slots[k], k, piece, 0), down)
    for step in range(n - 1):
        if step < fan:
            turn_block(step)
        for number, (k, piece, down) in enumerate(streams):
            copies[number, step].wait_recv()
            chunk = chunk_at(down, step)
            mine = window(x_refs[k], k, piece, chunk)
            landed = window(slots[k], k, piece, step)
            total = landed[...].astype(jnp.float32) + mine[...].astype(jnp.float32)
            if step < n - 2:
                landed[...] = total.astype(jnp.bfloat16)
                start(number, step + 1, landed, window(slots[k], k, piece, step + 1), down)
            else:
                done = window(y_refs[k], k, piece, chunk)
                done[...] = total.astype(jnp.bfloat16)
                start(number, n - 1, done, done, down)
    for step in range(n - 1):
        for number, (k, piece, down) in enumerate(streams):
            copies[number, n - 1 + step].wait_recv()
            if step < n - 2:
                done = window(y_refs[k], k, piece, chunk_at(down, n - 1 + step))
                start(number, n + step, done, done, down)
    for one in copies.values():
        one.wait_send()


def ring_call(body, name, arrays, outs, scratch, ident):
    size = sum(v.size * 2 for v in arrays)
    return pl.pallas_call(
        body,
        name=name,
        out_shape=[jax.ShapeDtypeStruct(s, d) for s, d in outs],
        in_specs=[pl.BlockSpec(memory_space=pltpu.VMEM)] * len(arrays),
        out_specs=[pl.BlockSpec(memory_space=pltpu.VMEM)] * len(outs),
        scratch_shapes=scratch,
        compiler_params=pltpu.CompilerParams(
            collective_id=ident, has_side_effects=True, vmem_limit_bytes=62 << 20
        ),
        cost_estimate=pl.CostEstimate(flops=0, bytes_accessed=60 * size, transcendentals=0),
    )(*arrays)


def ring_total(arrays, splits, ident, inner=None):
    n, fan = lax.axis_size("seq"), lax.axis_size("fsdp")
    streams = sum(abs(s) for s in splits)
    more = [] if inner is None else [inner]
    return ring_call(
        functools.partial(ring_kernel, n, splits, 0 if inner is None else fan),
        "ring_total",
        arrays + more,
        [(v.shape, jnp.bfloat16) for v in arrays] + [(v.shape[::-1], jnp.bfloat16) for v in more],
        [pltpu.VMEM((v.shape[0] // n * (n - 1), v.shape[1]), jnp.bfloat16) for v in arrays]
        + [pltpu.SemaphoreType.DMA((streams, 2 * n - 2))] * 2,
        ident,
    )


def units_kernel(
    n, fan, x_ref, part_ref, few_ref, inner_ref, outer_ref, sum_ref, few_sum_ref, slots, acc, landed, few_landed,
    down_send, down_recv, swap_send, swap_recv, own_sem, send_sem, recv_sem, part_send, part_recv,
):
    s, me = lax.axis_index("seq"), lax.axis_index("fsdp")
    rows, width = acc.shape[0] // 3, x_ref.shape[1]
    cols = width // fan
    block = 2 * fan * rows
    place, right, left = ring_greet(n, [(me + far) % fan for far in range(1, fan)])
    sums = {}

    def piece_of(ref, at, piece):
        return ref.at[pl.ds(at * 3 * rows, 3 * rows), pl.ds(piece * cols, cols)]

    def send_sum(piece, step, src):
        to = left if piece >= fan // 2 else right
        sums[piece, step] = pltpu.make_async_remote_copy(
            src_ref=src,
            dst_ref=piece_of(slots, step, piece),
            send_sem=down_send.at[piece, step],
            recv_sem=down_recv.at[piece, step],
            device_id={"seq": to},
            device_id_type=MESH,
        )
        sums[piece, step].start()

    def chunk(piece, step):
        return ring_index((place + 1 + step) % n if piece >= fan // 2 else (place + 2 * n - 1 - step) % n, n)

    for piece in range(fan):
        send_sum(piece, 0, piece_of(x_ref, chunk(piece, 0), piece))
    for step in range(n - 1):
        for piece in range(fan):
            sums[piece, step].wait_recv()
            arrived = piece_of(slots, step, piece)
            mine = piece_of(x_ref, chunk(piece, step + 1), piece)
            total = (arrived[...].astype(jnp.float32) + mine[...].astype(jnp.float32)).astype(jnp.bfloat16)
            if step < n - 2:
                arrived[...] = total
                send_sum(piece, step + 1, arrived)
            else:
                acc[:, piece * cols : (piece + 1) * cols] = total
    moves = []
    for far in range(fan):
        target = (me + far) % fan
        for half in range(2):
            src = acc.at[pl.ds(half * rows, rows), pl.ds(pl.multiple_of(target * cols, 128), cols)]
            dst = inner_ref.at[pl.ds(s * block + (me * 2 + half) * rows, rows), :]
            if far:
                one = pltpu.make_async_remote_copy(
                    src_ref=src,
                    dst_ref=dst,
                    send_sem=swap_send.at[far, half],
                    recv_sem=swap_recv.at[far, half],
                    device_id={"fsdp": target},
                    device_id_type=MESH,
                )
            else:
                one = pltpu.make_async_copy(src, dst, own_sem.at[half])
            one.start()
            moves.append(one)
    mine = pltpu.make_async_copy(
        acc.at[pl.ds(2 * rows, rows), :], outer_ref.at[pl.ds(s * rows, rows), :], own_sem.at[2]
    )
    mine.start()
    copies = {}
    outs = ((outer_ref, (n * rows, width), 2), (inner_ref, (n * block, cols), -2))

    def start(k, piece, step):
        ref, shape, split = outs[k]
        chunk = ring_index((place + step) % n if piece else (place + n - step) % n, n)
        view = ring_window(ref, shape, split, n, piece, chunk)
        copies[k, piece, step] = pltpu.make_async_remote_copy(
            src_ref=view,
            dst_ref=view,
            send_sem=send_sem.at[2 * k + piece, step],
            recv_sem=recv_sem.at[2 * k + piece, step],
            device_id={"seq": left if piece else right},
            device_id_type=MESH,
        )
        copies[k, piece, step].start()

    def forward(k, step):
        for piece in range(2):
            copies[k, piece, step].wait_recv()
            if step < n - 2:
                start(k, piece, step + 1)

    mine.wait()
    start(0, 0, 0)
    start(0, 1, 0)
    lead = (n - 1) // 2
    for step in range(lead):
        forward(0, step)
    for one in moves:
        one.wait()
    parts = []
    for far in range(1, fan):
        target = (me + far) % fan
        for which, (src, into) in enumerate(((part_ref, landed), (few_ref, few_landed))):
            rest = src.shape[0] // fan
            one = pltpu.make_async_remote_copy(
                src_ref=src.at[pl.ds(target * rest, rest), :],
                dst_ref=into.at[far],
                send_sem=part_send.at[which, far],
                recv_sem=part_recv.at[which, far],
                device_id={"fsdp": target},
                device_id_type=MESH,
            )
            one.start()
            parts.append(one)
    start(1, 0, 0)
    start(1, 1, 0)
    for step in range(n - 1):
        forward(1, step)
        if lead + step < n - 1:
            forward(0, lead + step)
    for one in parts:
        one.wait()
    for src, into, out in ((part_ref, landed, sum_ref), (few_ref, few_landed, few_sum_ref)):
        rest = src.shape[0] // fan
        total = src[pl.ds(pl.multiple_of(me * rest, rest), rest), :].astype(jnp.float32)
        for far in range(1, fan):
            total = total + into[far].astype(jnp.float32)
        out[...] = total
    for one in [*copies.values(), *sums.values()]:
        one.wait_send()


def units_total(grads, part, few, ident):
    n, fan = lax.axis_size("seq"), lax.axis_size("fsdp")
    rows, width = grads.shape[0] // (3 * n), grads.shape[1]
    tokens = part.shape[0] // fan
    sems = lambda *shape: pltpu.SemaphoreType.DMA(shape)
    return ring_call(
        functools.partial(units_kernel, n, fan),
        "units_total",
        [grads, part, few],
        [
            ((n * 2 * fan * rows, width // fan), jnp.bfloat16),
            ((n * rows, width), jnp.bfloat16),
            ((tokens, part.shape[1]), jnp.float32),
            ((few.shape[0] // fan, few.shape[1]), jnp.float32),
        ],
        [
            pltpu.VMEM(((n - 1) * 3 * rows, width), jnp.bfloat16),
            pltpu.VMEM((3 * rows, width), jnp.bfloat16),
            pltpu.VMEM((fan, tokens, part.shape[1]), jnp.bfloat16),
            pltpu.VMEM((fan, few.shape[0] // fan, few.shape[1]), jnp.bfloat16),
        ]
        + [sems(fan, n - 1), sems(fan, n - 1), sems(fan, 2), sems(fan, 2), sems(3)]
        + [sems(4, n - 1), sems(4, n - 1), sems(2, fan), sems(2, fan)],
        ident,
    )


def team(n):
    s, f = lax.axis_index("seq"), lax.axis_index("fsdp")
    half = s // (n // 2)
    away = (half + f) % 2
    return f // 2, half, (s + away * (n // 2)) % n


def swap_kernel(n, fan, count, fars, fresh, *refs):
    given = count + (len(fars) > 0) + (0 if fresh else 2)
    x_refs, y_refs = refs[:count], refs[given : given + count]
    sems = refs[given + count + (2 if fars else 0) :]
    send_sem, recv_sem, own_sem = sems[:3]
    pair, half, rank = team(n)
    me = lax.axis_index("fsdp")

    def device(other):
        away = (other // (n // 2) + half) % 2
        return {"seq": (other + away * (n // 2)) % n, "fsdp": 2 * pair + (half + away) % 2}

    barrier = pltpu.get_barrier_semaphore()
    for j in range(1, n):
        pl.semaphore_signal(barrier, inc=1, device_id=device((rank + j) % n), device_id_type=MESH)
    travel = [far for far in fars if far]
    for far in travel:
        pl.semaphore_signal(barrier, inc=1, device_id={"fsdp": (me + fan - far) % fan}, device_id_type=MESH)
    pl.semaphore_wait(barrier, n - 1 + len(travel))
    copies = []
    for k in range(count):
        for j in range(1, n):
            other = (rank + j) % n
            one = pltpu.make_async_remote_copy(
                src_ref=x_refs[k].at[other],
                dst_ref=y_refs[k].at[rank],
                send_sem=send_sem.at[k, j],
                recv_sem=recv_sem.at[k, j],
                device_id=device(other),
                device_id_type=MESH,
            )
            one.start()
            copies.append(one)
    for k in range(count):
        one = pltpu.make_async_copy(x_refs[k].at[rank], y_refs[k].at[rank], own_sem.at[k])
        one.start()
        copies.append(one)
    if fars:
        w_ref, halves = refs[count], refs[given + count : given + count + 2]
        far_send, far_recv, far_own, stage = sems[3:]
        rest = []
        units, cols = halves[0].shape[0], w_ref.shape[1]
        for i, far in enumerate(fars):
            target = (me + far) % fan
            for part in range(2):
                src = w_ref.at[pl.ds((part * fan + target) * units, units), :]
                dst = halves[part].at[:, pl.ds(pl.multiple_of(me * cols, 128), cols)]
                if far:
                    one = pltpu.make_async_remote_copy(
                        src_ref=src,
                        dst_ref=dst,
                        send_sem=far_send.at[i, part],
                        recv_sem=far_recv.at[i, part],
                        device_id={"fsdp": target},
                        device_id_type=MESH,
                    )
                else:
                    one = pltpu.make_async_copy(src, stage.at[part], far_own.at[0, part])
                    rest.append((one, pltpu.make_async_copy(stage.at[part], dst, far_own.at[1, part])))
                one.start()
                if far:
                    copies.append(one)
        for inward, outward in rest:
            inward.wait()
            outward.start()
            copies.append(outward)
    for one in copies:
        one.wait()


def swap(arrays, ident, fars=(), given=None, halves=None):
    n, fan = lax.axis_size("seq"), lax.axis_size("fsdp")
    count = len(arrays)
    size = sum(v.size * 2 for v in arrays)
    operands, outs, alias = list(arrays), [jax.ShapeDtypeStruct(v.shape, v.dtype) for v in arrays], {}
    scratch = [
        pltpu.SemaphoreType.DMA((count, n)),
        pltpu.SemaphoreType.DMA((count, n)),
        pltpu.SemaphoreType.DMA((count,)),
    ]
    if fars:
        operands.append(given)
        shape = (given.shape[0] // (2 * fan), given.shape[1] * fan)
        outs += [jax.ShapeDtypeStruct(shape, given.dtype)] * 2
        scratch += [pltpu.SemaphoreType.DMA((len(fars), 2))] * 2 + [
            pltpu.SemaphoreType.DMA((2, 2)),
            pltpu.VMEM((2, given.shape[0] // (2 * fan), given.shape[1]), given.dtype),
        ]
        if halves is not None:
            operands += list(halves)
            alias = {count + 1: count, count + 2: count + 1}
    return pl.pallas_call(
        functools.partial(swap_kernel, n, fan, count, fars, not fars or halves is None),
        name="swap",
        out_shape=outs,
        in_specs=[pl.BlockSpec(memory_space=pl.ANY)] * len(operands),
        out_specs=[pl.BlockSpec(memory_space=pl.ANY)] * len(outs),
        scratch_shapes=scratch,
        input_output_aliases=alias,
        compiler_params=pltpu.CompilerParams(collective_id=ident, has_side_effects=True),
        cost_estimate=pl.CostEstimate(flops=0, bytes_accessed=size, transcendentals=0),
    )(*operands)


def norm_apply(value, gain):
    return value * lax.rsqrt(jnp.mean(value * value, axis=-1, keepdims=True) + EPS) * gain


def norm_back(value, gain, grad):
    _, pull = jax.vjp(norm_apply, value, gain)
    return pull(grad)


def gate_mix(gate, up):
    return jax.nn.gelu(gate, approximate=True) * up


def counts_below(ids, values):
    total = jnp.zeros_like(values)
    for doc in range(DOCS):
        total = total + jnp.where(values > doc, jnp.sum((ids == doc).astype(jnp.int32)), 0)
    return total


def change_home(value):
    n, fan = lax.axis_size("seq"), lax.axis_size("fsdp")
    pairs = []
    for s in range(n):
        for f in range(fan):
            away = (s // (n // 2) + f) % 2
            target = ((s + n // 2) % n, f ^ 1) if away else (s, f)
            pairs.append((s * fan + f, target[0] * fan + target[1]))
    return lax.ppermute(value, ("seq", "fsdp"), pairs)


def spread(blocks):
    fan, me = lax.axis_size("fsdp"), lax.axis_index("fsdp")
    result = blocks
    for far in range(1, fan):
        block = lax.dynamic_index_in_dim(blocks, (me + far) % fan, 0, True)
        block = lax.ppermute(block, "fsdp", [(f, (f + far) % fan) for f in range(fan)])
        result = lax.dynamic_update_slice_in_dim(result, block, (me - far) % fan, 0)
    return result


def flat(blocks):
    return jnp.transpose(blocks, (1, 0, 2)).reshape(blocks.shape[1], -1)


def by_rows(value):
    return with_layout_constraint(value, Layout(major_to_minor=tuple(range(value.ndim))))


def scatter(grad):
    return lax.psum_scatter(grad, "fsdp", scatter_dimension=0, tiled=True)


def shards(
    layer_in, encoder, decoder_ids, encoder_ids, rel_buckets,
    norm_self, self_qkv, self_out, rel_table, norm_cross, cross_q, cross_kv, cross_out, norm_ff, ff_in, ff_out,
    cotangent,
):
    seqs, local, width = layer_in.shape
    enc_local = encoder.shape[1]
    parts = lax.axis_size("seq")
    heads = self_qkv.shape[1]
    dh = self_qkv.shape[2] // 3
    own = heads // parts
    rows = seqs * local
    buckets, table_own = rel_table.shape
    length, keys = local * parts, enc_local * parts
    gather = lambda v: lax.all_gather(v, "fsdp", axis=0, tiled=True)

    fan = lax.axis_size("fsdp")
    units = ff_in.shape[1] // (2 * fan)
    part = norm_self.shape[0]
    pair, half, rank = team(parts)

    qkv_w = gather(self_qkv)
    small = jnp.concatenate([norm_self, norm_cross, norm_ff, rel_table.reshape(-1)])
    small = lax.all_gather(small, "fsdp", axis=0, tiled=False)
    early = by_rows(jnp.stack([self_out, cross_q, *jnp.split(cross_kv.reshape(-1, 2 * width), 2, axis=1)]))
    small, early = lax.optimization_barrier((small, early))
    early = lax.all_gather(early, "fsdp", axis=1, tiled=True)
    both_ids = jnp.concatenate([decoder_ids.reshape(-1), encoder_ids.reshape(-1)])
    both_ids = change_home(jnp.pad(both_ids, (0, 1024 - local - enc_local)).reshape(8, 128))
    inner_t = ff_in.T
    by_kernel = (width // fan) % 128 == 0 and fan % 2 == 0 and (ff_in.shape[0] // parts) % 8 == 0
    (both_ids,) = swap([jnp.broadcast_to(both_ids[None], (parts, 8, 128))], 13)
    home = change_home(layer_in.reshape(rows, width))
    early = by_rows(early)
    gain_first, gain_second, gain_third = (
        small[:, i * part : (i + 1) * part].reshape(width).astype(f32) for i in range(3)
    )
    table = jnp.transpose(small[:, 3 * part :].reshape(-1, buckets, table_own), (1, 0, 2)).reshape(buckets, heads)
    both_ids = both_ids.reshape(parts, 1024)
    ids = both_ids[:, :local].reshape(length)
    enc_ids = both_ids[:, local : local + enc_local].reshape(keys)

    first_seen = counts_below(ids, ids)
    enc_first = counts_below(enc_ids, ids)
    enc_last = counts_below(enc_ids, ids + 1)
    blocks = length // BQ
    bk = BQ
    self_rows = jnp.broadcast_to(first_seen[None], (8, length))
    cross_rows = jnp.concatenate([enc_first[None], enc_last[None], jnp.zeros((6, length), jnp.int32)])
    self_limits = jnp.stack(
        [first_seen[::BQ] // bk, (jnp.arange(blocks, dtype=jnp.int32) + 1) * (BQ // bk)]
    )
    cross_limits = jnp.stack([enc_first[::BQ] // bk, (enc_last[BQ - 1 :: BQ] + bk - 1) // bk])

    first_head = rank * own
    table_mine = lax.dynamic_slice_in_dim(table.astype(f32), first_head, own, 1)
    near = rel_buckets[:REACH]
    onehot = (near[:, None] == jnp.arange(buckets, dtype=jnp.int32)[None, :]).astype(f32)
    bias = jnp.einsum("ln,ng->gl", onehot, table_mine, precision=HIGH)
    ext = jnp.concatenate(
        [jnp.full((own, BQ), MASKED, f32), bias, jnp.zeros((own, BQ), f32)], axis=1
    )

    qkv_w, home, inner_t, ext, self_rows, cross_rows, self_limits, cross_limits = lax.optimization_barrier(
        (qkv_w, home, inner_t, ext, self_rows, cross_rows, self_limits, cross_limits)
    )
    qkv_w = qkv_w.reshape(width, parts, own * 3 * dh)

    stream = home.astype(f32)
    normed_first = norm_apply(stream, gain_first).astype(bf16)
    qkv_tok = jnp.einsum("td,dge->gte", normed_first, qkv_w, preferred_element_type=f32).astype(bf16)
    others = change_home(jnp.concatenate([cotangent.reshape(rows, width), encoder.reshape(-1, width)]))
    grad_low, enc_flat = others[:rows], others[rows:]
    fars = [tuple(far for far in range(fan) if by_kernel and (far == 2) == first) for first in (True, False)]
    qkv, *halves = swap([qkv_tok], 17, fars[0], inner_t)
    qkv, cross_out, grad_low = lax.optimization_barrier((qkv, cross_out, grad_low))
    if rows == cross_out.shape[0]:
        mix_cross, grad_group = lax.all_gather(jnp.stack([cross_out, grad_low]), "fsdp", axis=1, tiled=True)
    else:
        mix_cross, grad_group = gather(cross_out), gather(grad_low)
    mix_cross = mix_cross.reshape(parts, own * dh, width)
    qkv = qkv.reshape(length, own * 3 * dh)
    out_self, self_t, self_lse = self_forward(self_limits, self_rows, ext, qkv)
    (self_tok,) = swap([out_self.reshape(parts, local, own * dh)], 11)
    after_self, normed_second, query_tok, pairs_tok = over_weights(
        into_kernel,
        "self_out_to_cross",
        [self_tok, home, gain_second.reshape(1, width), enc_flat],
        early,
        lambda i: i,
        [
            ((rows, width), f32),
            ((rows, width), bf16),
            ((parts, rows, own * dh), bf16),
            ((parts, enc_local, own * 2 * dh), bf16),
        ],
    )
    query_cross, pairs = swap([query_tok, pairs_tok], 12)
    query_cross, pairs = query_cross.reshape(length, own * dh), pairs.reshape(keys, own * 2 * dh)
    out_cross, cross_t, cross_lse = cross_forward(cross_limits, cross_rows, query_cross, pairs)
    cross_tok, *halves = swap([out_cross.reshape(parts, local, own * dh)], 16, fars[1], inner_t, halves)
    if not by_kernel:
        halves = spread(jnp.transpose(inner_t.reshape(2, fan, units, -1), (1, 0, 2, 3)))
        halves = [jnp.transpose(halves[:, i], (1, 0, 2)).reshape(units, width) for i in range(2)]
    gate_t, up_t = halves
    after_cross = after_self + jnp.einsum("gtc,gcd->td", cross_tok, mix_cross, preferred_element_type=f32)
    normed_third = norm_apply(after_cross, gain_third).astype(bf16)
    normed_group = gather(normed_third)
    gate = jnp.einsum("td,fd->tf", normed_group, gate_t, preferred_element_type=f32)
    up = jnp.einsum("td,fd->tf", normed_group, up_t, preferred_element_type=f32)
    hidden = gate_mix(gate, up).astype(bf16)

    grad_hidden = jnp.einsum("td,fd->tf", grad_group, ff_out, preferred_element_type=f32)
    _, pull_mix = jax.vjp(gate_mix, gate, up)
    grad_gate, grad_up = (g.astype(bf16) for g in pull_mix(grad_hidden))
    grad_third_in = jnp.dot(grad_gate, gate_t, preferred_element_type=f32) + jnp.dot(
        grad_up, up_t, preferred_element_type=f32
    )
    grad_third_in = scatter(grad_third_in.astype(bf16))
    outer_part = jnp.dot(hidden, ff_out, preferred_element_type=f32).astype(bf16)
    grad_units = [
        jnp.einsum("tf,td->fd", g, y, preferred_element_type=f32).astype(bf16)
        for g, y in ((grad_gate, normed_group), (grad_up, normed_group), (hidden, grad_group))
    ]
    if by_kernel:
        grad_units = jnp.stack([g.reshape(parts, units // parts, width) for g in grad_units], axis=1)
        grad_units = grad_units.reshape(3 * units, width)
    grad_third_in, outer_part, part_units = lax.optimization_barrier((grad_third_in, outer_part, grad_units))
    grad_third_in = grad_third_in.astype(f32)
    grad_from_third, grad_gain_third = norm_back(after_cross, gain_third, grad_third_in)
    grad_middle = grad_low.astype(f32) + grad_from_third
    middle_low = grad_middle.astype(bf16)
    grad_mix_cross = jnp.einsum("gtc,td->gcd", cross_tok, middle_low, preferred_element_type=f32)
    part_cross = scatter(grad_mix_cross.reshape(width, width).astype(bf16))
    grad_cross_tok = jnp.einsum("td,gcd->gtc", middle_low, mix_cross, preferred_element_type=f32).astype(bf16)
    (grad_cross,) = swap([grad_cross_tok], 11)
    grad_cross = grad_cross.reshape(length, own * dh)
    grad_query, grad_pairs = cross_backward(
        cross_limits, cross_rows, query_cross, pairs, grad_cross, cross_t, cross_lse
    )
    grad_query_tok, grad_pairs_tok = swap(
        [grad_query.reshape(parts, local, own * dh), grad_pairs.reshape(parts, enc_local, own * 2 * dh)], 12
    )
    (
        grad_upper, upper_low, grad_self_tok, grad_gain_second, grad_encoder, grad_query_tok, grad_pairs_tok
    ) = over_weights(
        outof_kernel,
        "cross_to_self_out",
        [grad_query_tok, grad_pairs_tok, after_self, gain_second.reshape(1, width), grad_middle],
        early,
        lambda i: jnp.where(i < 2, 1 - i, i),
        [
            ((rows, width), f32),
            ((rows, width), bf16),
            ((parts, rows, own * dh), bf16),
            ((1, width), f32),
            ((enc_local, width), bf16),
            ((rows, width), bf16),
            ((enc_local, 2 * width), bf16),
        ],
        [((enc_local, width), f32)],
    )
    grad_query_w = jnp.einsum("td,te->de", normed_second, grad_query_tok, preferred_element_type=f32)
    grad_pairs_w = jnp.einsum("td,te->de", enc_flat, grad_pairs_tok, preferred_element_type=f32)
    grad_mix_self = jnp.einsum("gtc,td->gcd", self_tok, upper_low, preferred_element_type=f32)
    grad_mid = jnp.concatenate([grad_query_w.astype(bf16), grad_pairs_w.astype(bf16)], axis=1)
    part_self = scatter(grad_mix_self.reshape(width, width).astype(bf16))
    grad_self_tok, grad_mid = lax.optimization_barrier((grad_self_tok, grad_mid))
    part_mid = scatter(grad_mid)
    (grad_self,) = swap([grad_self_tok], 11)
    grad_self = grad_self.reshape(length, own * dh)
    grad_qkv, diagonals = self_backward(self_limits, self_rows, ext, qkv, grad_self, self_t, self_lse)
    (grad_qkv_tok,) = swap([grad_qkv.reshape(parts, local, own * 3 * dh)], 10)
    grad_qkv_tok = flat(grad_qkv_tok)
    grad_qkv_w = jnp.einsum("td,te->de", normed_first, grad_qkv_tok, preferred_element_type=f32)
    grad_qkv_w, grad_qkv_tok = lax.optimization_barrier((grad_qkv_w.astype(bf16), grad_qkv_tok))
    grad_first_in = jnp.einsum("te,de->td", grad_qkv_tok, qkv_w.reshape(width, -1), preferred_element_type=f32)
    grad_from_first, grad_gain_first = norm_back(stream, gain_first, grad_first_in)
    grad_layer_in = (grad_upper + grad_from_first).astype(bf16)
    bucket_line = jnp.concatenate([jnp.full((BQ - 1,), -1, jnp.int32), near, jnp.full((BQ + 1,), -1, jnp.int32)])
    in_bucket = (bucket_line[:, None] == jnp.arange(buckets, dtype=jnp.int32)).astype(f32)
    by_bucket = jnp.einsum("xn,gx->ng", in_bucket, diagonals, precision=HIGH)
    grad_table = lax.dynamic_update_slice_in_dim(jnp.zeros((buckets, heads), f32), by_bucket, first_head, 1)

    gains = jnp.concatenate(
        [g.reshape(-1, part) for g in (grad_gain_first, grad_gain_second, grad_gain_third)], axis=1
    )
    tables = jnp.transpose(grad_table.reshape(buckets, -1, table_own), (1, 0, 2)).reshape(-1, buckets * table_own)
    small_grads = jnp.concatenate([gains, tables], axis=1).astype(bf16)
    small_size = small_grads.shape[1]
    going_home = jnp.concatenate([grad_layer_in, grad_encoder.astype(bf16)])
    part_last = scatter(grad_qkv_w)
    going_home, small_grads, part_units, part_cross, part_mid = lax.optimization_barrier(
        (change_home(going_home), small_grads, part_units, part_cross, part_mid)
    )
    if by_kernel:
        few = jnp.pad(small_grads[:, None], ((0, 0), (0, 7), (0, 1024 - small_size))).reshape(fan * 8, 1024)
        total_inner, total_outer, outer_sum, few = units_total(part_units, outer_part, few, 0)
        few = jnp.pad(few[0].astype(bf16).reshape(8, 128), ((0, parts * 8 - 8), (0, 0)))
        total_cross, total_self, total_mid, total_qkv, small_total, total_inner = ring_total(
            [part_cross, part_self, part_mid, part_last, few], (1, 1, 2, 2, 1), 1, total_inner
        )
    else:
        grad_units = [lax.psum(g, "seq") for g in part_units]
        total_inner = spread(jnp.transpose(jnp.stack(grad_units[:2]).reshape(2, units, fan, -1), (2, 0, 1, 3)))
        total_inner = jnp.transpose(total_inner, (3, 1, 0, 2)).reshape(-1, 2 * fan * units).astype(f32)
        total_outer, outer_sum = grad_units[2], scatter(outer_part).astype(f32)
        few = lax.dynamic_index_in_dim(lax.psum(small_grads, "fsdp"), lax.axis_index("fsdp"), 0, False)
        total_cross, total_self, total_mid, total_qkv, small_total = (
            lax.psum(v, "seq") for v in (part_cross, part_self, part_mid, part_last, few)
        )
    layer_out = (after_cross + outer_sum).astype(bf16)
    layer_out, total_inner, total_outer, total_cross, total_self, total_mid, total_qkv, going_home = (
        lax.optimization_barrier(
            (layer_out, total_inner, total_outer, total_cross, total_self, total_mid, total_qkv, going_home)
        )
    )
    layer_out = change_home(layer_out).reshape(seqs, local, width)
    grad_layer_in = going_home[:rows].astype(f32).reshape(seqs, local, width)
    grad_encoder = going_home[rows:].astype(f32).reshape(seqs, enc_local, width)
    total_inner, total_outer, total_mid, total_qkv = (
        v.astype(f32) for v in (total_inner, total_outer, total_mid, total_qkv)
    )
    total_query, total_mix_cross = total_mid[:, :width], total_cross.astype(f32)
    total_pairs = total_mid[:, width:].reshape(-1, heads, 2 * dh)
    total_mix_self, total_qkv = total_self.astype(f32), total_qkv.reshape(-1, heads, 3 * dh)
    mine = small_total.reshape(-1)[:small_size].astype(f32)
    total_gain_first, total_gain_second, total_gain_third = (mine[i * part : (i + 1) * part] for i in range(3))
    total_table = mine[3 * part :].reshape(buckets, table_own)
    return (
        layer_out, grad_layer_in, grad_encoder, total_gain_first, total_qkv, total_mix_self, total_table,
        total_gain_second, total_query, total_pairs, total_mix_cross, total_gain_third, total_inner, total_outer,
    )


def solution(mesh):
    in_specs = (
        P("fsdp", "seq", None), P("fsdp", "seq", None), P("fsdp", "seq"), P("fsdp", "seq"), P(),
        P("fsdp"), P("fsdp", None, None), P("fsdp", None), P(None, "fsdp"), P("fsdp"), P("fsdp", None),
        P("fsdp", None, None), P("fsdp", None), P("fsdp"), P("fsdp", None), P("fsdp", None),
        P("fsdp", "seq", None),
    )
    out_specs = (
        P("fsdp", "seq", None), P("fsdp", "seq", None), P("fsdp", "seq", None), P("fsdp"), P("fsdp", None, None),
        P("fsdp", None), P(None, "fsdp"), P("fsdp"), P("fsdp", None), P("fsdp", None, None), P("fsdp", None),
        P("fsdp"), P("fsdp", None), P("fsdp", None),
    )
    return jax.shard_map(shards, mesh=mesh, in_specs=in_specs, out_specs=out_specs, check_vma=False)
```
